32 devices in a mesh: dp: 8 (over z, y), fsdp: 4 (over x, core).
Axes of the slice: x: 2, y: 2, z: 4, core: 2. Of those that a mesh axis runs over, the one named last changes fastest.
Arguments:
- layer_input: bfloat16 [16, 4, 256, 768], P(None, 'fsdp', 'dp'), may hold values from -6 to 6
- teacher: bfloat16 [16, 4, 256, 768], P('dp', 'fsdp'), may hold values from -6 to 6
- lengths: int32 [16], replicated, may hold values from 1 to 1024, 14336 in all
- dealing: int32 [16], replicated, may hold values from 0 to 15, each once
- attn_routes: int32 [16, 128], replicated, may hold values from 0 to 1023, as said below
- ffn_routes: int32 [16, 128], replicated, may hold values from 0 to 1023, as said below
- ffn_scores: float32 [16, 128], replicated, may hold values from 0.25 to 1
- gain_attn: bfloat16 [768], P(('dp', 'fsdp')), may hold values from 0.5 to 1.5
- gain_ffn: bfloat16 [768], P(('dp', 'fsdp')), may hold values from 0.5 to 1.5
- light_qkv: bfloat16 [768, 1536], P(('dp', 'fsdp')), may hold values from -0.21875 to 0.21875
- light_out: bfloat16 [512, 768], P(('dp', 'fsdp')), may hold values from -3 to 3
- heavy_qkv: bfloat16 [768, 2304], P(('dp', 'fsdp')), may hold values from -0.21875 to 0.21875
- heavy_out: bfloat16 [768, 768], P(('dp', 'fsdp')), may hold values from -2.5 to 2.5
- light_in: bfloat16 [768, 2048], P(('dp', 'fsdp')), may hold values from -0.21875 to 0.21875
- light_down: bfloat16 [1024, 768], P(('dp', 'fsdp')), may hold values from -0.1875 to 0.1875
- heavy_in: bfloat16 [768, 8192], P(('dp', 'fsdp')), may hold values from -0.21875 to 0.21875
- heavy_down: bfloat16 [4096, 768], P(('dp', 'fsdp')), may hold values from -0.09375 to 0.09375
Outputs:
- loss: float32 [], replicated
- input_grad: float32 [16, 4, 256, 768], P(None, 'fsdp', 'dp')
- gain_attn_grad: float32 [768], P(('dp', 'fsdp'))
- gain_ffn_grad: float32 [768], P(('dp', 'fsdp'))
- light_qkv_grad: float32 [768, 1536], P(('dp', 'fsdp'))
- light_out_grad: float32 [512, 768], P(('dp', 'fsdp'))
- heavy_qkv_grad: float32 [768, 2304], P(('dp', 'fsdp'))
- heavy_out_grad: float32 [768, 768], P(('dp', 'fsdp'))
- light_in_grad: float32 [768, 2048], P(('dp', 'fsdp'))
- light_down_grad: float32 [1024, 768], P(('dp', 'fsdp'))
- heavy_in_grad: float32 [768, 8192], P(('dp', 'fsdp'))
- heavy_down_grad: float32 [4096, 768], P(('dp', 'fsdp'))
The draws below stay inside these ranges and needn't reach their ends.
Inputs may be any that keep to these rules, and one draw needn't show every extreme that they name: `attn_routes`: each row names 128 different positions of its sequence; at most 64 of them lie in one of the aligned blocks of 256 positions, and exactly 64 in one such block. `ffn_routes`: each row names 128 different positions of its sequence; at most 64 of them lie in one of the aligned blocks of 256 positions, and exactly 64 in one such block. `dealing`: each sequence once.
All inputs are finite; a program needn't handle non-finite values.
Results may differ from the reference program's by a relative error of at most 0.01.
The reference program's roundings to bfloat16 on the way count: a program that leaves them out, or rounds other values in their place, can miss the bound.
Values may be sent and summed in bfloat16 or wider, within the bound.
A program may use at most 256 MiB of HBM per device.

```python
import math
import jax
import jax.numpy as jnp
import numpy as np
from jax import lax

D = 768
HL = 8
HH = 12
DH = 64
FL = 1024
FH = 4096
L = 1024
WIN = 128
QLEN = 256
KR = 128
CAP = 64
SEQS = 16
N_FSDP = 4


def route_row(row_key):
    pieces = L // QLEN
    key_piece, key_first, key_rest, key_order = jax.random.split(row_key, 4)
    heavy_piece = jax.random.randint(key_piece, (), 0, pieces)
    first_part = jax.random.permutation(key_first, QLEN)[:CAP] + heavy_piece * QLEN
    rest_part = jax.random.permutation(key_rest, L - QLEN)[:KR - CAP]
    rest_part = rest_part + jnp.where(rest_part >= heavy_piece * QLEN, QLEN, 0)
    joined = jnp.concatenate([first_part, rest_part])
    return jax.random.permutation(key_order, joined).astype(jnp.int32)


def route_table(table_key):
    return jax.vmap(route_row)(jax.random.split(table_key, SEQS))


def draw_attn_routes(key, part):
    return route_table(jax.random.fold_in(key, 17))


def draw_ffn_routes(key, part):
    return route_table(jax.random.fold_in(key, 29))


def block_levels(own_key, dims, cuts, low, high):
    level, own = 1.0, jax.random.fold_in(own_key, 6)
    for dim, blocks in cuts:
        heights = jnp.exp(jax.random.uniform(jax.random.fold_in(own, dim), (blocks,), jnp.float32, low / len(cuts), high / len(cuts)))
        level = level * jnp.repeat(heights, dims[dim] // blocks).reshape([-1 if axis == dim else 1 for axis in range(len(dims))])
    return level


def split_up(count, total, bound, slope):
    weights = [(1 << 20) // math.isqrt(standing ** slope) + 1 for standing in range(2, count + 1)]
    surplus, given = total - bound - (count - 1), [1] * (count - 1)
    while surplus > 0:
        candidates = [i for i in range(count - 1) if given[i] < bound]
        whole, left = sum([weights[i] for i in candidates]), surplus
        for i in candidates:
            extra = min(bound - given[i], max(1, left * weights[i] // whole), surplus)
            given[i] = given[i] + extra
            surplus = surplus - extra
    return np.array([bound] + given)


def ragged_sizes(key, amount, total, limit, skew):
    if amount == 2:
        one = jax.random.randint(key, (), max(1, total - limit), min(limit, total - 1) + 1)
        return jnp.stack([one, total - one])
    sizes = jnp.asarray(split_up(amount, total, limit, skew), jnp.int32)
    twos = (amount - 1) // 2
    source_of, taker = sizes[1:1 + 2 * twos:2], sizes[2:2 + 2 * twos:2]
    room = jnp.minimum(source_of - 1, limit - taker)
    shifted = jax.random.randint(jax.random.fold_in(key, 1), (twos,), 0, 1 << 20) % (room + 1)
    sizes = sizes.at[1:1 + 2 * twos:2].set(source_of - shifted).at[2:2 + 2 * twos:2].set(taker + shifted)
    return sizes[jax.random.permutation(jax.random.fold_in(key, 2), amount)]


def gaussian(rng, extent, deviation, most, cuts=(), held_as=jnp.bfloat16):
    drawn = deviation * jax.random.normal(rng, extent, jnp.float32)
    if cuts:
        drawn = drawn * block_levels(rng, extent, cuts, -0.22, 0.18)
    return jnp.clip(drawn, -most, most).astype(held_as)


def setup_inputs(seed: int = 0) -> dict:
    streams_of = jax.random.split(jax.random.key(seed), 18)
    return {
        "layer_input": gaussian(streams_of[0], (SEQS, N_FSDP, QLEN, D), 1.0, 6.0, ((1, 4), (2, 8))),
        "teacher": gaussian(streams_of[1], (SEQS, N_FSDP, QLEN, D), 1.0, 6.0, ((0, 8), (1, 4))),
        "lengths": ragged_sizes(streams_of[2], SEQS, SEQS * L * 7 // 8, L, 1).astype(jnp.int32),
        "dealing": jax.random.permutation(streams_of[3], SEQS).astype(jnp.int32),
        "attn_routes": draw_attn_routes(jax.random.fold_in(streams_of[17], 71), 0),
        "ffn_routes": draw_ffn_routes(jax.random.fold_in(streams_of[17], 71), 0),
        "ffn_scores": jnp.clip(jax.random.uniform(streams_of[6], (SEQS, KR), jnp.float32, 0.25, 1.0), 0.25, 1.0),
        "gain_attn": jnp.clip(1.0 + 0.1 * jax.random.normal(streams_of[7], (D,), jnp.float32), 0.5, 1.5).astype(jnp.bfloat16),
        "gain_ffn": jnp.clip(1.0 + 0.1 * jax.random.normal(streams_of[8], (D,), jnp.float32), 0.5, 1.5).astype(jnp.bfloat16),
        "light_qkv": gaussian(streams_of[9], (D, 3 * HL * DH), D ** -0.5, 0.21875, ((0, 32),)),
        "light_out": gaussian(streams_of[10], (HL * DH, D), (HL * DH // WIN) ** -0.5, 3.0, ((0, 32),)),
        "heavy_qkv": gaussian(streams_of[11], (D, 3 * HH * DH), D ** -0.5, 0.21875, ((0, 32),)),
        "heavy_out": gaussian(streams_of[12], (HH * DH, D), (HH * DH // KR) ** -0.5, 2.5, ((0, 32),)),
        "light_in": gaussian(streams_of[13], (D, 2 * FL), D ** -0.5, 0.21875, ((0, 32),)),
        "light_down": gaussian(streams_of[14], (FL, D), FL ** -0.5, 0.1875, ((0, 32),)),
        "heavy_in": gaussian(streams_of[15], (D, 2 * FH), D ** -0.5, 0.21875, ((0, 32),)),
        "heavy_down": gaussian(streams_of[16], (FH, D), FH ** -0.5, 0.09375, ((0, 32),)),
    }


EPSILON = 1e-06
MASKED = -1000000000.0
SCORE_SCALE = 0.125
PRECISE = lax.Precision.HIGHEST

@jax.custom_vjp
def low(v):
    return lax.optimization_barrier(v.astype(jnp.bfloat16)).astype(jnp.float32)

@jax.custom_vjp
def low_back(v):
    return v

def low_keep(v):
    return (low(v), None)

def low_pass(kept, grad):
    return (grad,)

def back_keep(v):
    return (v, None)

def back_low(kept, grad):
    return (low(grad),)
low.defvjp(low_keep, low_pass)
low_back.defvjp(back_keep, back_low)

def both_ways(value):
    return low_back(low(value))

def matmul(left, right):
    return jnp.dot(left, right, precision=PRECISE, preferred_element_type=jnp.float32)

def rms_norm(value, gain):
    return value * lax.rsqrt(lax.optimization_barrier(jnp.mean(value * value, axis=-1, keepdims=True)) + EPSILON) * gain

def geglu(gate, upper):
    return jax.nn.gelu(gate, approximate=True) * upper

def attend(queries, key_rows, value_rows, allowed, heads):
    query_heads = queries.reshape(queries.shape[0], heads, -1)
    key_heads = key_rows.reshape(key_rows.shape[0], heads, -1)
    value_heads = value_rows.reshape(value_rows.shape[0], heads, -1)
    scores = jnp.einsum('qhd,khd->hqk', query_heads, key_heads, precision=PRECISE) * SCORE_SCALE
    scores = low_back(scores)
    scores = jnp.where(allowed[None], scores, MASKED)
    attn_prob = low(jax.nn.softmax(scores, axis=-1))
    attended = jnp.einsum('hqk,khd->qhd', attn_prob, value_heads, precision=PRECISE)
    return both_ways(attended.reshape(queries.shape[0], -1))

def seq_loss(params, seq_inputs, seq_targets, length, attn_index, ffn_index, seq_scores):
    g_one, g_two, w_lqkv, w_lout, w_hqkv, w_hout, w_lin, w_ldown, w_hin, w_hdown = params
    places = jnp.arange(L)
    valid_mask = places < length
    width_light = HL * DH
    width_heavy = HH * DH
    normed = low(rms_norm(seq_inputs, g_one))
    projected = matmul(normed, w_lqkv)
    queries = both_ways(projected[:, :width_light])
    key_rows = both_ways(projected[:, width_light:2 * width_light])
    value_rows = both_ways(projected[:, 2 * width_light:])
    within_reach = jnp.abs(places[:, None] - places[None, :]) <= WIN
    light_allowed = within_reach & (valid_mask[None, :] | (places[:, None] == places[None, :]))
    light_branch = low_back(matmul(attend(queries, key_rows, value_rows, light_allowed, HL), w_lout))
    routed_rows = normed[attn_index]
    heavy_proj = matmul(routed_rows, w_hqkv)
    heavy_queries = both_ways(heavy_proj[:, :width_heavy])
    heavy_keys = both_ways(heavy_proj[:, width_heavy:2 * width_heavy])
    heavy_values = both_ways(heavy_proj[:, 2 * width_heavy:])
    heavy_allowed = valid_mask[attn_index][None, :] | (attn_index[:, None] == attn_index[None, :])
    heavy_branch = low_back(matmul(attend(heavy_queries, heavy_keys, heavy_values, heavy_allowed, HH), w_hout))
    hidden = seq_inputs + light_branch + jnp.zeros_like(seq_inputs).at[attn_index].add(heavy_branch)
    normed_two = low(rms_norm(hidden, g_two))
    up_proj = low_back(matmul(normed_two, w_lin))
    activated = low(geglu(up_proj[:, :FL], up_proj[:, FL:]))
    light_ffn = low_back(matmul(activated, w_ldown))
    ffn_rows = normed_two[ffn_index]
    heavy_up = low_back(matmul(ffn_rows, w_hin))
    heavy_act = low(geglu(heavy_up[:, :FH], heavy_up[:, FH:]))
    heavy_ffn = low_back(matmul(heavy_act, w_hdown)) * seq_scores[:, None]
    output = hidden + light_ffn + jnp.zeros_like(hidden).at[ffn_index].add(heavy_ffn)
    misfit = output - seq_targets
    return jnp.sum(valid_mask.astype(jnp.float32)[:, None] * misfit * misfit)

def reference(layer_input, teacher, lengths, dealing, attn_routes, ffn_routes, ffn_scores, gain_attn, gain_ffn, light_qkv, light_out, heavy_qkv, heavy_out, light_in, light_down, heavy_in, heavy_down):
    inputs = layer_input.astype(jnp.float32).reshape(SEQS, L, D)
    targets = teacher.astype(jnp.float32).reshape(SEQS, L, D)
    params = (gain_attn.astype(jnp.float32), gain_ffn.astype(jnp.float32), light_qkv.astype(jnp.float32), light_out.astype(jnp.float32), heavy_qkv.astype(jnp.float32), heavy_out.astype(jnp.float32), light_in.astype(jnp.float32), light_down.astype(jnp.float32), heavy_in.astype(jnp.float32), heavy_down.astype(jnp.float32))
    token_count = jnp.sum(lengths).astype(jnp.float32)
    checked = jax.checkpoint(seq_loss)

    def loss_of(inputs_all, weights_all):
        dealt_inputs = jnp.take(inputs_all, dealing, axis=0)

        def scan_step(running, seq_item):
            seq_inputs, seq_targets, length, attn_index, ffn_index, seq_scores = seq_item
            return (running + checked(weights_all, seq_inputs, seq_targets, length, attn_index, ffn_index, seq_scores), None)
        summed, _ = lax.scan(scan_step, jnp.zeros((), jnp.float32), (dealt_inputs, targets, jnp.take(lengths, dealing), jnp.take(attn_routes, dealing, axis=0), jnp.take(ffn_routes, dealing, axis=0), jnp.take(ffn_scores, dealing, axis=0)))
        return summed / (D * token_count)
    loss_value, pullback = jax.vjp(loss_of, inputs, params)
    d_inputs, d_params = pullback(jnp.ones((), jnp.float32))
    return (loss_value, d_inputs.reshape(SEQS, N_FSDP, QLEN, D), d_params[0], d_params[1], d_params[2], d_params[3], d_params[4], d_params[5], d_params[6], d_params[7], d_params[8], d_params[9])
```

```python
import functools
import jax
import jax.numpy as jnp
from jax import lax
from jax.experimental import pallas as pl
from jax.experimental.pallas import tpu as pltpu
from jax.sharding import PartitionSpec as P

D = 768
HL = 8
HH = 12
DH = 64
FL = 1024
FH = 4096
WIN = 128
CAP = 64

EPSILON = 1e-06
MASKED = -1000000000.0
SCORE_SCALE = 0.125
MESH = pl.DeviceIdType.MESH
BF = jnp.bfloat16
F32 = jnp.float32
ANY = pl.BlockSpec(memory_space=pl.ANY)
VM = pl.BlockSpec(memory_space=pltpu.VMEM)
DMA = pltpu.SemaphoreType.DMA
VMEM_BYTES = 60 * 1024 * 1024


def place():
    d = lax.axis_index("dp")
    f = lax.axis_index("fsdp")
    return d // 2, d % 2, f // 2, f % 2


def at(hi, lo, x, c):
    return (hi * 2 + lo, x * 2 + c)


def meet(peers):
    barrier = pltpu.get_barrier_semaphore()
    for peer in peers:
        pl.semaphore_signal(barrier, inc=1, device_id=peer, device_id_type=MESH)
    pl.semaphore_wait(barrier, len(peers))


def send(src, dst, send_sem, recv_sem, peer):
    copy = pltpu.make_async_remote_copy(
        src_ref=src,
        dst_ref=dst,
        send_sem=send_sem,
        recv_sem=recv_sem,
        device_id=peer,
        device_id_type=MESH,
    )
    copy.start()
    return copy


def keep(src, dst, sem):
    copy = pltpu.make_async_copy(src, dst, sem)
    copy.start()
    return copy


def quad_peers():
    hi, lo, x, c = place()
    return [(lo, 1 - x), (1 - lo, x), (1 - lo, 1 - x)]


def call(kernel, out_shape, operands, in_specs, out_specs, scratch, collective_id):
    return pl.pallas_call(
        kernel,
        out_shape=out_shape,
        in_specs=in_specs,
        out_specs=out_specs,
        scratch_shapes=scratch,
        compiler_params=pltpu.CompilerParams(
            collective_id=collective_id, has_side_effects=True, vmem_limit_bytes=VMEM_BYTES
        ),
    )(*operands)


def deal_kernel(deal_ref, x_ref, o_ref, sem):
    count = o_ref.shape[0]

    def begin(i, carry):
        pltpu.make_async_copy(x_ref.at[deal_ref[i]], o_ref.at[i], sem.at[i]).start()
        return carry

    def finish(i, carry):
        pltpu.make_async_copy(x_ref.at[deal_ref[i]], o_ref.at[i], sem.at[i]).wait()
        return carry

    lax.fori_loop(0, count, begin, 0)
    lax.fori_loop(0, count, finish, 0)


def deal_rows(dealing, rows):
    return pl.pallas_call(
        deal_kernel,
        out_shape=jax.ShapeDtypeStruct(rows.shape, rows.dtype),
        in_specs=[pl.BlockSpec(memory_space=pltpu.SMEM), ANY],
        out_specs=ANY,
        scratch_shapes=[DMA((rows.shape[0],))],
    )(dealing, rows)


def undeal_kernel(deal_ref, x_ref, o_ref):
    def body(i, carry):
        o_ref[deal_ref[i]] = x_ref[i].astype(F32)
        return carry

    lax.fori_loop(0, x_ref.shape[0], body, 0)


def undeal_rows(dealing, rows):
    return pl.pallas_call(
        undeal_kernel,
        out_shape=jax.ShapeDtypeStruct(rows.shape, F32),
        in_specs=[pl.BlockSpec(memory_space=pltpu.SMEM), VM],
        out_specs=VM,
        compiler_params=pltpu.CompilerParams(vmem_limit_bytes=VMEM_BYTES),
    )(dealing, rows)


def packed(matrix):
    rows, columns = matrix.shape
    if rows % 8 == 0:
        return matrix
    return matrix.reshape(rows * columns // 128, 128)


def unpacked(gathered, rows, columns):
    return gathered.reshape(-1, rows, columns).reshape(-1, columns)


def gather_kernel(dp, nw, *refs):
    nz = dp // 2
    xin, ws, hin, hdn = refs[0], refs[1 : 1 + nw], refs[1 + nw], refs[2 + nw]
    outs = refs[3 + nw :]
    xo, wos, hin_o, hdn_o = outs[0], outs[1 : 1 + nw], outs[1 + nw], outs[2 + nw]
    loc, xs, xr, zs, zr, ps, pr, cs, cr, hs, hr = outs[3 + nw :]
    hi, lo, x, c = place()
    d = hi * 2 + lo
    f = x * 2 + c
    plane = (lo * 2 + x) * 2 + c
    group = xin.shape[0] // dp
    dp_peers = [(lax.rem(d + k, dp), f) for k in range(1, dp)]
    rest = [(a, b, e) for a in (0, 1) for b in (0, 1) for e in (0, 1) if a or b or e]
    flat8 = []
    for a, b, e in rest:
        l2 = 1 - lo if a else lo
        x2 = 1 - x if b else x
        c2 = 1 - c if e else c
        flat8.append((l2, x2, c2))
    meet(dp_peers + [at(hi, *p) for (a, b, e), p in zip(rest, flat8) if b or e])
    locals_ = [keep(ws[w], wos[w].at[hi, lo, x, c], loc.at[w]) for w in range(nw)]
    locals_.append(keep(xin.at[pl.ds(d * group, group)], xo.at[:, d], loc.at[nw]))
    locals_.append(keep(hin.at[plane], hin_o.at[hi, plane], loc.at[nw + 1]))
    locals_.append(keep(hdn, hdn_o.at[hi], loc.at[nw + 2]))
    x_sends = []
    for k, peer in enumerate(dp_peers):
        x_sends.append(
            send(xin.at[pl.ds(peer[0] * group, group)], xo.at[:, d], xs.at[k], xr.at[k], peer)
        )
    z_peers = [at(lax.rem(hi + k, nz), lo, x, c) for k in range(1, nz)]
    z_sends = [
        [
            send(ws[w], wos[w].at[hi, lo, x, c], zs.at[w, k], zr.at[w, k], peer)
            for k, peer in enumerate(z_peers)
        ]
        for w in range(nw)
    ]
    h_sends = []
    for k, (l2, x2, c2) in enumerate(flat8):
        h_sends.append(
            send(
                hin.at[(l2 * 2 + x2) * 2 + c2],
                hin_o.at[hi, plane],
                hs.at[0, k],
                hr.at[0, k],
                at(hi, l2, x2, c2),
            )
        )
    quad = quad_peers()
    partner = at(hi, lo, x, 1 - c)
    p_sends, c_sends = [], []

    def forward_plane(w):
        locals_[w].wait()
        for copy in z_sends[w]:
            copy.wait()
        column = wos[w].at[:, lo, x, c]
        p_sends.append(
            [
                send(column, column, ps.at[w, k], pr.at[w, k], at(hi, l2, x2, c))
                for k, (l2, x2) in enumerate(quad)
            ]
        )
        c_sends.append([send(column, column, cs.at[w, 0], cr.at[w, 0], partner)])

    def forward_core(w):
        for k, (l2, x2) in enumerate(quad):
            p_sends[w][k].wait()
            column = wos[w].at[:, l2, x2, c]
            c_sends[w].append(send(column, column, cs.at[w, k + 1], cr.at[w, k + 1], partner))

    for w in range(nw):
        forward_plane(w)
        if w >= 1:
            forward_core(w - 1)
    for copy in h_sends:
        copy.wait()
    locals_[nw + 1].wait()
    late = []
    for k, peer in enumerate(z_peers):
        late.append(send(hin_o.at[hi], hin_o.at[hi], hs.at[1, k], hr.at[1, k], peer))
        late.append(send(hdn, hdn_o.at[hi], hs.at[2, k], hr.at[2, k], peer))
    forward_core(nw - 1)
    locals_[nw].wait()
    locals_[nw + 2].wait()
    for copy in x_sends + late:
        copy.wait()
    for copies in c_sends:
        for copy in copies:
            copy.wait()


def gather_all(dp, xin, weights, hin, hdn):
    nz = dp // 2
    nw = len(weights)
    seqs, rows, _ = xin.shape
    shapes = [jax.ShapeDtypeStruct((seqs // dp, dp, rows, D), BF)]
    shapes += [jax.ShapeDtypeStruct((nz, 2, 2, 2) + w.shape, BF) for w in weights]
    shapes.append(jax.ShapeDtypeStruct((nz,) + hin.shape, BF))
    shapes.append(jax.ShapeDtypeStruct((nz,) + hdn.shape, BF))
    most = max(7, nz)
    scratch = [
        DMA((nw + 3,)),
        DMA((dp,)),
        DMA((dp,)),
        DMA((nw, nz)),
        DMA((nw, nz)),
        DMA((nw, 3)),
        DMA((nw, 3)),
        DMA((nw, 4)),
        DMA((nw, 4)),
        DMA((3, most)),
        DMA((3, most)),
    ]
    return call(
        functools.partial(gather_kernel, dp, nw),
        shapes,
        [xin, *weights, hin, hdn],
        [ANY] * (3 + nw),
        [ANY] * (3 + nw),
        scratch,
        1,
    )


def rim_exchange(left, right, from_left, from_right, ls, lr, rs, rr):
    d = lax.axis_index("dp")
    f = lax.axis_index("fsdp")
    last = lax.axis_size("fsdp") - 1

    def down():
        return pltpu.make_async_remote_copy(
            src_ref=left,
            dst_ref=from_right,
            send_sem=ls,
            recv_sem=lr,
            device_id=(d, lax.max(f - 1, 0)),
            device_id_type=MESH,
        )

    def up():
        return pltpu.make_async_remote_copy(
            src_ref=right,
            dst_ref=from_left,
            send_sem=rs,
            recv_sem=rr,
            device_id=(d, lax.min(f + 1, last)),
            device_id_type=MESH,
        )

    @pl.when(f > 0)
    def _():
        down().start()

    @pl.when(f < last)
    def _():
        up().start()

    @pl.when(f == 0)
    def _():
        from_left[...] = jnp.zeros(from_left.shape, from_left.dtype)

    @pl.when(f == last)
    def _():
        from_right[...] = jnp.zeros(from_right.shape, from_right.dtype)

    def finish():
        @pl.when(f > 0)
        def _():
            down().wait_send()
            up().wait_recv()

        @pl.when(f < last)
        def _():
            up().wait_send()
            down().wait_recv()

    return finish


def line_peers():
    hi, lo, x, c = place()
    return [at(hi, lo, x, 1 - c), at(hi, lo, 1 - x, c), at(hi, lo, 1 - x, 1 - c)]


def keys_kernel(left, right, kv, from_left, from_right, every, own, ls, lr, rs, rr, ss, sr):
    hi, lo, x, c = place()
    f = x * 2 + c
    meet(line_peers())
    finish = rim_exchange(left, right, from_left, from_right, ls, lr, rs, rr)
    mine = keep(kv, every.at[:, f], own)
    across = send(kv, every.at[:, f], ss.at[0], sr.at[0], at(hi, lo, 1 - x, c))
    beside = send(kv, every.at[:, f], ss.at[1], sr.at[1], at(hi, lo, x, 1 - c))
    across.wait()
    other = every.at[:, (1 - x) * 2 + c]
    relay = send(other, other, ss.at[2], sr.at[2], at(hi, lo, x, 1 - c))
    mine.wait()
    beside.wait()
    relay.wait()
    finish()


def exchange_keys(left, right, kv):
    group, cap, width = kv.shape
    return call(
        keys_kernel,
        [
            jax.ShapeDtypeStruct(left.shape, BF),
            jax.ShapeDtypeStruct(right.shape, BF),
            jax.ShapeDtypeStruct((group, 4, cap, width), BF),
        ],
        [left, right, kv],
        [VM] * 3,
        [VM] * 3,
        [DMA, DMA, DMA, DMA, DMA, DMA((3,)), DMA((3,))],
        2,
    )


def key_grads_kernel(left, right, part, from_left, from_right, total, got, far, ls, lr, rs, rr, ss, sr):
    hi, lo, x, c = place()
    meet(line_peers())
    finish = rim_exchange(left, right, from_left, from_right, ls, lr, rs, rr)
    beside = [
        send(
            part.at[:, b * 2 + 1 - c], got.at[b], ss.at[b], sr.at[b], at(hi, lo, x, 1 - c)
        )
        for b in (0, 1)
    ]
    for copy in beside:
        copy.wait()
    for b in (0, 1):
        got[b] = (got[b].astype(F32) + part[:, b * 2 + c].astype(F32)).astype(BF)
    across = send(got.at[1 - x], far, ss.at[2], sr.at[2], at(hi, lo, 1 - x, c))
    across.wait()
    total[...] = got[x].astype(F32) + far[...].astype(F32)
    finish()


def exchange_key_grads(left, right, part):
    group, _, cap, width = part.shape
    return call(
        key_grads_kernel,
        [
            jax.ShapeDtypeStruct(left.shape, BF),
            jax.ShapeDtypeStruct(right.shape, BF),
            jax.ShapeDtypeStruct((group, cap, width), F32),
        ],
        [left, right, part],
        [VM] * 3,
        [VM] * 3,
        [
            pltpu.VMEM((2, group, cap, width), BF),
            pltpu.VMEM((group, cap, width), BF),
            DMA,
            DMA,
            DMA,
            DMA,
            DMA((3,)),
            DMA((3,)),
        ],
        3,
    )


def plane_meet():
    hi, lo, x, c = place()
    meet([at(hi, l2, x2, c) for l2, x2 in quad_peers()] + [at(hi, lo, x, 1 - c)])


def plane_gather_kernel(rows, every, own, ss, sr, cs, cr):
    hi, lo, x, c = place()
    quad = quad_peers()
    partner = at(hi, lo, x, 1 - c)
    plane_meet()
    spot = every.at[lo, x, c]
    mine = keep(rows, spot, own)
    out = [
        send(rows, spot, ss.at[k], sr.at[k], at(hi, l2, x2, c)) for k, (l2, x2) in enumerate(quad)
    ]
    back = [send(rows, spot, cs.at[3], cr.at[3], partner)]
    for k, (l2, x2) in enumerate(quad):
        out[k].wait()
        other = every.at[l2, x2, c]
        back.append(send(other, other, cs.at[k], cr.at[k], partner))
    mine.wait()
    for copy in back:
        copy.wait()


def plane_gather(rows, collective_id):
    return call(
        plane_gather_kernel,
        jax.ShapeDtypeStruct((2, 2, 2) + rows.shape, BF),
        [rows],
        [ANY],
        ANY,
        [DMA, DMA((3,)), DMA((3,)), DMA((4,)), DMA((4,))],
        collective_id,
    )


def plane_sum_kernel(part, total, near, far, ss, sr, cs, cr):
    hi, lo, x, c = place()
    quad = quad_peers()
    partner = at(hi, lo, x, 1 - c)
    plane_meet()
    spots = quad + [(lo, x)]
    back = [
        send(part.at[l2, x2, 1 - c], near.at[l2, x2], cs.at[k], cr.at[k], partner)
        for k, (l2, x2) in enumerate(spots)
    ]
    out = []
    for k, (l2, x2) in enumerate(spots):
        back[k].wait()
        near[l2, x2] = (near[l2, x2].astype(F32) + part[l2, x2, c].astype(F32)).astype(BF)
        if k < 3:
            out.append(
                send(near.at[l2, x2], far.at[k], ss.at[k], sr.at[k], at(hi, l2, x2, c))
            )
    for copy in out:
        copy.wait()
    total[...] = (
        near[lo, x].astype(F32)
        + far[0].astype(F32)
        + far[1].astype(F32)
        + far[2].astype(F32)
    )


def plane_sum(part, collective_id):
    shape = part.shape[3:]
    return call(
        plane_sum_kernel,
        jax.ShapeDtypeStruct(shape, F32),
        [part],
        [VM],
        VM,
        [
            pltpu.VMEM((2, 2) + shape, BF),
            pltpu.VMEM((3,) + shape, BF),
            DMA((3,)),
            DMA((3,)),
            DMA((4,)),
            DMA((4,)),
        ],
        collective_id,
    )


def scatter_kernel(dp, nw, *refs):
    nz = dp // 2
    dx, stats, gs, hin, hdn = refs[0], refs[1], refs[2 : 2 + nw], refs[2 + nw], refs[3 + nw]
    outs = refs[4 + nw :]
    dxo, total, gos, hin_o, hdn_o = outs[0], outs[1], outs[2 : 2 + nw], outs[2 + nw], outs[3 + nw]
    scr = outs[4 + nw :]
    nears, fars, sums, ends = (scr[i * nw : (i + 1) * nw] for i in range(4))
    hin_r, hin_s, hdn_r, sc, sp, sz, acc, acc2 = scr[4 * nw : 4 * nw + 8]
    own, xs, xr, cs, cr, ps, pr, zs, zr, hs, hr, ts, tr = scr[4 * nw + 8 :]
    hi, lo, x, c = place()
    d = hi * 2 + lo
    f = x * 2 + c
    plane = (lo * 2 + x) * 2 + c
    dp_peers = [(lax.rem(d + k, dp), f) for k in range(1, dp)]
    rest = [(a, b, e) for a in (0, 1) for b in (0, 1) for e in (0, 1) if a or b or e]
    flat8 = []
    for a, b, e in rest:
        l2 = 1 - lo if a else lo
        x2 = 1 - x if b else x
        c2 = 1 - c if e else c
        flat8.append((l2, x2, c2))
    meet(dp_peers + [at(hi, *p) for (a, b, e), p in zip(rest, flat8) if b or e])
    partner = at(hi, lo, x, 1 - c)
    quad = quad_peers()
    z_index = [lax.rem(hi + k, nz) for k in range(1, nz)]
    z_peers = [at(z, lo, x, c) for z in z_index]
    c_sends = [
        send(gs[w].at[:, :, :, 1 - c], nears[w], cs.at[w], cr.at[w], partner) for w in range(nw)
    ]
    t_c = send(stats, sc, ts.at[0], tr.at[0], partner)
    mine = keep(dx.at[:, d], dxo.at[d], own)
    x_sends = [
        send(dx.at[:, peer[0]], dxo.at[d], xs.at[k], xr.at[k], peer)
        for k, peer in enumerate(dp_peers)
    ]
    h_sends = []
    for k, z in enumerate(z_index):
        h_sends.append(send(hin.at[z], hin_r.at[k], hs.at[1, k], hr.at[1, k], z_peers[k]))
        h_sends.append(send(hdn.at[z], hdn_r.at[k], hs.at[2, k], hr.at[2, k], z_peers[k]))
    p_sends, z_sends = [], []
    t_c.wait()
    acc[...] = stats[...] + sc[...]
    t_p = [
        send(acc, sp.at[k], ts.at[1 + k], tr.at[1 + k], at(hi, l2, x2, c))
        for k, (l2, x2) in enumerate(quad)
    ]

    def add_core(w):
        c_sends[w].wait()
        near, g = nears[w], gs[w]

        def body(i, carry):
            z, a, b = i // 4, (i // 2) % 2, i % 2
            near[z, a, b] = (near[z, a, b].astype(F32) + g[z, a, b, c].astype(F32)).astype(BF)
            return carry

        lax.fori_loop(0, nz * 4, body, 0)
        p_sends.append(
            [
                send(near.at[:, l2, x2], fars[w].at[k], ps.at[w, k], pr.at[w, k], at(hi, l2, x2, c))
                for k, (l2, x2) in enumerate(quad)
            ]
        )

    def add_plane(w):
        for copy in p_sends[w]:
            copy.wait()
        near, far, part = nears[w], fars[w], sums[w]

        def body(z, carry):
            part[z] = (
                near[z, lo, x].astype(F32)
                + far[0, z].astype(F32)
                + far[1, z].astype(F32)
                + far[2, z].astype(F32)
            ).astype(BF)
            return carry

        lax.fori_loop(0, nz, body, 0)
        z_sends.append(
            [
                send(part.at[z], ends[w].at[k], zs.at[w, k], zr.at[w, k], z_peers[k])
                for k, z in enumerate(z_index)
            ]
        )

    def add_line(w):
        for copy in z_sends[w]:
            copy.wait()
        gos[w][...] = sums[w][hi].astype(F32)
        for k in range(nz - 1):
            gos[w][...] += ends[w][k].astype(F32)

    for w in range(nw):
        add_core(w)
        if w >= 2:
            add_plane(w - 2)
    for copy in t_p:
        copy.wait()
    acc2[...] = acc[...] + sp[0] + sp[1] + sp[2]
    t_z = [send(acc2, sz.at[k], ts.at[4 + k], tr.at[4 + k], z_peers[k]) for k in range(nz - 1)]
    for copy in h_sends:
        copy.wait()

    def body(i, carry):
        value = hin[hi, i].astype(F32)
        for k in range(nz - 1):
            value += hin_r[k, i].astype(F32)
        hin_s[i] = value.astype(BF)
        return carry

    lax.fori_loop(0, 8, body, 0)
    hin_o[plane] = hin_s[plane]
    a_sends = [
        send(
            hin_s.at[(l2 * 2 + x2) * 2 + c2],
            hin_o.at[plane],
            hs.at[0, k],
            hr.at[0, k],
            at(hi, l2, x2, c2),
        )
        for k, (l2, x2, c2) in enumerate(flat8)
    ]
    hdn_o[...] = hdn[hi].astype(F32)
    for k in range(nz - 1):
        hdn_o[...] += hdn_r[k].astype(F32)
    for w in range(max(nw - 2, 0), nw):
        add_plane(w)
    for copy in t_z:
        copy.wait()
    total[...] = acc2[...]
    for k in range(nz - 1):
        total[...] += sz[k]
    for w in range(nw):
        add_line(w)
    mine.wait()
    for copy in x_sends + a_sends:
        copy.wait()


def scatter_all(dp, dx, stats, grads, hin, hdn):
    nz = dp // 2
    nw = len(grads)
    group, _, rows, _ = dx.shape
    tiles = [g.shape[4:] for g in grads]
    most = max(7, nz)
    scratch = [pltpu.VMEM((nz, 2, 2) + t, BF) for t in tiles]
    scratch += [pltpu.VMEM((3, nz) + t, BF) for t in tiles]
    scratch += [pltpu.VMEM((nz,) + t, BF) for t in tiles]
    scratch += [pltpu.VMEM((nz - 1,) + t, BF) for t in tiles]
    scratch += [
        pltpu.VMEM((nz - 1,) + hin.shape[1:], BF),
        pltpu.VMEM(hin.shape[1:], BF),
        pltpu.VMEM((nz - 1,) + hdn.shape[1:], BF),
        pltpu.VMEM(stats.shape, F32),
        pltpu.VMEM((3,) + stats.shape, F32),
        pltpu.VMEM((nz - 1,) + stats.shape, F32),
        pltpu.VMEM(stats.shape, F32),
        pltpu.VMEM(stats.shape, F32),
        DMA,
        DMA((dp,)),
        DMA((dp,)),
        DMA((nw,)),
        DMA((nw,)),
        DMA((nw, 3)),
        DMA((nw, 3)),
        DMA((nw, nz)),
        DMA((nw, nz)),
        DMA((3, most)),
        DMA((3, most)),
        DMA((4 + nz,)),
        DMA((4 + nz,)),
    ]
    shapes = [jax.ShapeDtypeStruct((dp, group, rows, D), BF), jax.ShapeDtypeStruct(stats.shape, F32)]
    shapes += [jax.ShapeDtypeStruct(t, F32) for t in tiles]
    shapes.append(jax.ShapeDtypeStruct(hin.shape[1:], BF))
    shapes.append(jax.ShapeDtypeStruct(hdn.shape[1:], F32))
    return call(
        functools.partial(scatter_kernel, dp, nw),
        shapes,
        [dx, stats, *grads, hin, hdn],
        [ANY] + [VM] * (3 + nw),
        [ANY] + [VM] * (3 + nw),
        scratch,
        4,
    )


def rms_norm(value, gain):
    return value * lax.rsqrt(jnp.mean(value * value, axis=-1, keepdims=True) + EPSILON) * gain


def geglu(gate, upper):
    return jax.nn.gelu(gate, approximate=True) * upper


def geglu_back(up_proj, d_act):
    half_width = up_proj.shape[-1] // 2
    _, pullback = jax.vjp(geglu, up_proj[..., :half_width], up_proj[..., half_width:])
    d_gate, d_upper = pullback(d_act)
    return jnp.concatenate([d_gate, d_upper], axis=-1).astype(BF)


def split_heads(rows, heads):
    return rows.reshape(rows.shape[0], rows.shape[1], heads, -1)


def head_scores(queries, key_rows, allowed, heads):
    scores = (
        jnp.einsum(
            "sqhd,skhd->shqk",
            split_heads(queries, heads),
            split_heads(key_rows, heads),
            preferred_element_type=F32,
        )
        * SCORE_SCALE
    )
    return jnp.where(allowed[:, None], scores, MASKED)


def attend_forward(queries, key_rows, value_rows, allowed, heads):
    scores = head_scores(queries, key_rows, allowed, heads)
    row_max = jnp.max(scores, axis=-1, keepdims=True)
    shifted = jnp.exp(scores - row_max)
    row_sum = jnp.sum(shifted, axis=-1, keepdims=True)
    attn_prob = (shifted / row_sum).astype(BF)
    attended = jnp.einsum(
        "shqk,skhd->sqhd", attn_prob, split_heads(value_rows, heads), preferred_element_type=F32
    )
    return (attended.reshape(queries.shape).astype(BF), row_max + jnp.log(row_sum))


def attend_backward(queries, key_rows, value_rows, allowed, log_sum, d_attended, heads):
    scores = head_scores(queries, key_rows, allowed, heads)
    attn_prob = jnp.exp(scores - log_sum)
    d_heads = split_heads(d_attended, heads)
    d_prob = jnp.einsum(
        "sqhd,skhd->shqk", d_heads, split_heads(value_rows, heads), preferred_element_type=F32
    )
    row_dot = jnp.sum(attn_prob * d_prob, axis=-1, keepdims=True)
    d_scores = (attn_prob * (d_prob - row_dot)).astype(BF)
    d_query = (
        jnp.einsum(
            "shqk,skhd->sqhd", d_scores, split_heads(key_rows, heads), preferred_element_type=F32
        )
        * SCORE_SCALE
    )
    d_key = (
        jnp.einsum(
            "shqk,sqhd->skhd", d_scores, split_heads(queries, heads), preferred_element_type=F32
        )
        * SCORE_SCALE
    )
    d_value = jnp.einsum(
        "shqk,sqhd->skhd", attn_prob.astype(BF), d_heads, preferred_element_type=F32
    )
    return (
        d_query.reshape(queries.shape),
        d_key.reshape(key_rows.shape),
        d_value.reshape(value_rows.shape),
    )


def mul(left, right):
    return jnp.einsum("...d,de->...e", left, right, preferred_element_type=F32)


def mul_back(left, right):
    return jnp.einsum("...e,de->...d", left, right, preferred_element_type=F32)


def weight_grad(left, right):
    a = left.reshape(-1, left.shape[-1])
    b = right.reshape(-1, right.shape[-1])
    return jnp.einsum("pd,pe->de", a, b, preferred_element_type=F32)


def pick(spec, hot, value):
    high = value.astype(BF)
    rest = (value - high.astype(F32)).astype(BF)
    return jnp.einsum(spec, hot, high, preferred_element_type=F32) + jnp.einsum(
        spec, hot, rest, preferred_element_type=F32
    )


def routing(routes, pieces, piece_len):
    places = jnp.arange(pieces * piece_len)
    routed = jnp.any(routes[:, None, :] == places[None, :, None], axis=-1)
    routed = routed.reshape(-1, pieces, piece_len)
    before = jnp.arange(piece_len)[:, None] < jnp.arange(piece_len)[None, :]
    rank = jnp.einsum(
        "skp,pq->skq", routed.astype(BF), before.astype(BF), preferred_element_type=F32
    )
    slots = jnp.arange(CAP, dtype=F32)
    hot = routed[:, :, None, :] & (rank[:, :, None, :] == slots[None, None, :, None])
    filled = jnp.any(hot, axis=-1)
    spots = jnp.sum(jnp.where(hot, places.reshape(1, pieces, 1, piece_len), 0), axis=-1)
    return hot, jnp.where(filled, spots, -1)


def local(
    layer_input,
    teacher,
    lengths,
    dealing,
    attn_routes,
    ffn_routes,
    ffn_scores,
    gain_attn,
    gain_ffn,
    light_qkv,
    light_out,
    heavy_qkv,
    heavy_out,
    light_in,
    light_down,
    heavy_in,
    heavy_down,
):
    dp = lax.axis_size("dp")
    pieces = lax.axis_size("fsdp")
    data_index = lax.axis_index("dp")
    piece = lax.axis_index("fsdp")
    nz = dp // 2
    n = dp * pieces
    seqs = dealing.shape[0]
    group = seqs // dp
    gain_len = gain_attn.shape[0]
    hidden_units = heavy_in.shape[1] // 2 // n
    xin = deal_rows(dealing, layer_input[:, 0])
    gains = jnp.pad(
        jnp.stack([gain_attn, gain_ffn]), ((0, 6), (0, 128 - gain_len))
    )
    matrices = (light_qkv, heavy_qkv, light_out, heavy_out, light_in, light_down)
    hin_rows = heavy_in.shape[0]
    hin_src = (
        heavy_in.reshape(hin_rows, 2, nz, 8, hidden_units)
        .transpose(3, 0, 1, 2, 4)
        .reshape(8, hin_rows, 2 * nz * hidden_units)
    )
    if hin_rows % 8:
        hin_src = hin_src.reshape(8, -1, 128)
    got = gather_all(dp, xin, [gains] + [packed(m) for m in matrices], hin_src, heavy_down)
    tokens = layer_input.shape[2] * dp
    inputs = got[0].reshape(group, tokens, D).astype(F32)
    gain_rows = got[1].reshape(n, 8, 128)
    gain_one = gain_rows[:, 0, :gain_len].reshape(-1).astype(F32)
    gain_two = gain_rows[:, 1, :gain_len].reshape(-1).astype(F32)
    w_lqkv, w_hqkv, w_lout, w_hout, w_lin, w_ldown = (
        unpacked(full, *m.shape) for full, m in zip(got[2:8], matrices)
    )
    w_hin = unpacked(got[8], hin_rows, 2 * nz * hidden_units)
    w_hdown = got[9].reshape(-1, D)
    chosen = lax.dynamic_slice_in_dim(dealing, data_index * group, group)
    one = (chosen[:, None] == jnp.arange(seqs)[None, :])
    seq_lengths = jnp.sum(jnp.where(one, lengths[None, :], 0), axis=1)
    attn_pick = jnp.sum(jnp.where(one[:, :, None], attn_routes[None], 0), axis=1)
    ffn_pick = jnp.sum(jnp.where(one[:, :, None], ffn_routes[None], 0), axis=1)
    score_pick = jnp.sum(jnp.where(one[:, :, None], ffn_scores[None], 0.0), axis=1)
    token_count = jnp.sum(lengths).astype(F32)
    positions = piece * tokens + jnp.arange(tokens)
    valid_mask = positions[None, :] < seq_lengths[:, None]
    a_hot, a_spots = routing(attn_pick, pieces, tokens)
    f_hot, f_spots = routing(ffn_pick, pieces, tokens)
    a_select = lax.dynamic_index_in_dim(a_hot, piece, 1, False).astype(BF)
    f_select = lax.dynamic_index_in_dim(f_hot, piece, 1, False).astype(BF)
    a_spot = lax.dynamic_index_in_dim(a_spots, piece, 1, False)
    f_spot = lax.dynamic_index_in_dim(f_spots, piece, 1, False)
    slot_score = jnp.sum(
        jnp.where(f_spot[:, :, None] == ffn_pick[:, None, :], score_pick[:, None, :], 0.0), axis=-1
    )
    targets = teacher[:, 0].astype(F32)
    width_light = HL * DH
    width_heavy = HH * DH
    normed = rms_norm(inputs, gain_one).astype(BF)
    light_proj = mul(normed, w_lqkv).astype(BF)
    l_query = light_proj[..., :width_light]
    own_pair = light_proj[..., width_light:]
    a_rows = jnp.einsum("scp,spd->scd", a_select, normed, preferred_element_type=F32).astype(BF)
    heavy_proj = mul(a_rows, w_hqkv).astype(BF)
    h_query = heavy_proj[..., :width_heavy]
    from_left, from_right, kv_every = exchange_keys(
        own_pair[:, :WIN], own_pair[:, tokens - WIN :], heavy_proj[..., width_heavy:]
    )
    rim_pair = jnp.concatenate([from_left, own_pair, from_right], axis=1)
    rim_keys = rim_pair[..., :width_light]
    rim_values = rim_pair[..., width_light:]
    key_pos = piece * tokens - WIN + jnp.arange(tokens + 2 * WIN)
    within_reach = (jnp.abs(positions[:, None] - key_pos[None, :]) <= WIN) & (key_pos >= 0)[None, :]
    live_key = key_pos[None, :] < seq_lengths[:, None]
    light_allowed = within_reach[None] & (
        live_key[:, None, :] | (positions[:, None] == key_pos[None, :])[None]
    )
    l_att, l_lse = attend_forward(l_query, rim_keys, rim_values, light_allowed, HL)
    light_branch = mul(l_att, w_lout)
    kv_every = kv_every.reshape(group, pieces * CAP, 2 * width_heavy)
    all_spots = a_spots.reshape(group, pieces * CAP)
    heavy_allowed = ((all_spots >= 0) & (all_spots < seq_lengths[:, None]))[:, None, :] | (
        a_spot[:, :, None] == all_spots[:, None, :]
    )
    hv_keys = kv_every[..., :width_heavy]
    hv_values = kv_every[..., width_heavy:]
    h_att, h_lse = attend_forward(h_query, hv_keys, hv_values, heavy_allowed, HH)
    heavy_branch = mul(h_att, w_hout)
    hidden = inputs + light_branch + pick("scp,scd->spd", a_select, heavy_branch)
    normed_two = rms_norm(hidden, gain_two).astype(BF)
    f_rows = jnp.einsum("scp,spd->scd", f_select, normed_two, preferred_element_type=F32).astype(BF)
    t_rows = plane_gather(f_rows.reshape(group * CAP, D), 5).reshape(-1, D)
    heavy_up = mul(t_rows, w_hin)
    half = heavy_up.shape[-1] // 2
    heavy_mid = geglu(heavy_up[..., :half], heavy_up[..., half:]).astype(BF)
    heavy_part = mul(heavy_mid, w_hdown).astype(BF)
    heavy_ffn = plane_sum(heavy_part.reshape(2, 2, 2, group * CAP, D), 6).reshape(group, CAP, D)
    light_up = mul(normed_two, w_lin)
    light_mid = geglu(light_up[..., :FL], light_up[..., FL:]).astype(BF)
    light_ffn = mul(light_mid, w_ldown)
    output = hidden + light_ffn + pick("scp,scd->spd", f_select, heavy_ffn * slot_score[..., None])
    misfit = output - targets
    weight_mask = valid_mask[..., None].astype(F32)
    partial_loss = jnp.sum(weight_mask * misfit * misfit)
    d_out = 2.0 * weight_mask * misfit / (D * token_count)
    d_heavy_ffn = (pick("scp,spd->scd", f_select, d_out) * slot_score[..., None]).astype(BF)
    t_grad = plane_gather(d_heavy_ffn.reshape(group * CAP, D), 7).reshape(-1, D)
    grad_hdown = weight_grad(heavy_mid, t_grad)
    d_heavy_mid = mul_back(t_grad, w_hdown)
    d_heavy_up = geglu_back(heavy_up, d_heavy_mid)
    grad_hin = weight_grad(t_rows, d_heavy_up)
    d_f_part = mul_back(d_heavy_up, w_hin).astype(BF)
    d_f_rows = plane_sum(d_f_part.reshape(2, 2, 2, group * CAP, D), 8).reshape(group, CAP, D)
    d_light = d_out.astype(BF)
    grad_ldown = weight_grad(light_mid, d_light)
    d_light_mid = mul_back(d_light, w_ldown)
    d_light_up = geglu_back(light_up, d_light_mid)
    grad_lin = weight_grad(normed_two, d_light_up)
    d_norm_two = pick("scp,scd->spd", f_select, d_f_rows) + mul_back(d_light_up, w_lin)
    _, second_pull = jax.vjp(rms_norm, hidden, gain_two)
    d_hidden_norm, grad_gain_two = second_pull(d_norm_two)
    d_hidden = d_out + d_hidden_norm
    d_heavy_attn = pick("scp,spd->scd", a_select, d_hidden).astype(BF)
    grad_hout = weight_grad(h_att, d_heavy_attn)
    d_h_att = mul_back(d_heavy_attn, w_hout).astype(BF)
    dq_heavy, dk_heavy, dv_heavy = attend_backward(
        h_query, hv_keys, hv_values, heavy_allowed, h_lse, d_h_att, HH
    )
    kv_part = jnp.concatenate([dk_heavy, dv_heavy], axis=-1).astype(BF)
    d_light_attn = d_hidden.astype(BF)
    grad_lout = weight_grad(l_att, d_light_attn)
    d_l_att = mul_back(d_light_attn, w_lout).astype(BF)
    dq_light, dk_light, dv_light = attend_backward(
        l_query, rim_keys, rim_values, light_allowed, l_lse, d_l_att, HL
    )
    rim_grads = jnp.concatenate([dk_light, dv_light], axis=-1)
    back_left, back_right, kv_grads = exchange_key_grads(
        rim_grads[:, :WIN].astype(BF),
        rim_grads[:, tokens + WIN :].astype(BF),
        kv_part.reshape(group, pieces, CAP, 2 * width_heavy),
    )
    d_h_proj = jnp.concatenate([dq_heavy.astype(BF), kv_grads.astype(BF)], axis=-1)
    grad_hqkv = weight_grad(a_rows, d_h_proj)
    d_a_rows = mul_back(d_h_proj, w_hqkv)
    own_grads = rim_grads[:, WIN : WIN + tokens]
    own_grads = jnp.concatenate(
        [
            own_grads[:, :WIN] + back_left.astype(F32),
            own_grads[:, WIN : tokens - WIN],
            own_grads[:, tokens - WIN :] + back_right.astype(F32),
        ],
        axis=1,
    )
    d_l_proj = jnp.concatenate([dq_light.astype(BF), own_grads.astype(BF)], axis=-1)
    grad_lqkv = weight_grad(normed, d_l_proj)
    d_normed = pick("scp,scd->spd", a_select, d_a_rows) + mul_back(d_l_proj, w_lqkv)
    _, first_pull = jax.vjp(rms_norm, inputs, gain_one)
    d_inputs_norm, grad_gain_one = first_pull(d_normed)
    d_inputs = d_hidden + d_inputs_norm
    rows = tokens // dp
    stats = jnp.concatenate(
        [
            grad_gain_one.reshape(-1, 128),
            grad_gain_two.reshape(-1, 128),
            jnp.broadcast_to(partial_loss, (4, 128)),
        ]
    )
    grads = (grad_lin, grad_ldown, grad_hout, grad_lout, grad_hqkv, grad_lqkv)
    shards = (light_in, light_down, heavy_out, light_out, heavy_qkv, light_qkv)
    sent = [
        packed_full(grad.astype(BF), shard.shape, nz) for grad, shard in zip(grads, shards)
    ]
    hin_tile = hin_src.shape[1:]
    done = scatter_all(
        dp,
        d_inputs.astype(BF).reshape(group, dp, rows, D),
        stats,
        sent,
        grad_hin.astype(BF).reshape((nz, 8) + hin_tile),
        grad_hdown.astype(BF).reshape(nz, -1, D),
    )
    d_layer = undeal_rows(dealing, done[0].reshape(seqs, rows, D))[:, None]
    summed = done[1]
    mine = data_index * pieces + piece
    loss_value = summed[12, 0] / (D * token_count)
    own_one = lax.dynamic_slice_in_dim(summed[:6].reshape(-1), mine * gain_len, gain_len)
    own_two = lax.dynamic_slice_in_dim(summed[6:12].reshape(-1), mine * gain_len, gain_len)
    g_lin, g_ldown, g_hout, g_lout, g_hqkv, g_lqkv = (
        full.reshape(shard.shape) for full, shard in zip(done[2:8], shards)
    )
    g_hin = (
        done[8]
        .astype(F32)
        .reshape(8, hin_rows, 2, nz, hidden_units)
        .transpose(1, 2, 3, 0, 4)
        .reshape(heavy_in.shape)
    )
    return (
        loss_value,
        d_layer,
        own_one,
        own_two,
        g_lqkv,
        g_lout,
        g_hqkv,
        g_hout,
        g_lin,
        g_ldown,
        g_hin,
        done[9].reshape(heavy_down.shape),
    )


def packed_full(grad, shard_shape, nz):
    rows, columns = shard_shape
    if rows % 8 == 0:
        return grad.reshape(nz, 2, 2, 2, rows, columns)
    return grad.reshape(nz, 2, 2, 2, rows * columns // 128, 128)


def solution(mesh):
    split = P(("dp", "fsdp"))
    matrix = P(("dp", "fsdp"), None)
    placed = (
        P(None, "fsdp", "dp", None),
        P("dp", "fsdp", None, None),
        P(),
        P(),
        P(),
        P(),
        P(),
        split,
        split,
    ) + (matrix,) * 8
    return jax.shard_map(
        local,
        mesh=mesh,
        in_specs=placed,
        out_specs=(P(), P(None, "fsdp", "dp", None), split, split) + (matrix,) * 8,
        check_vma=False,
    )
```

```python
import functools
import jax
import jax.numpy as jnp
from jax import lax
from jax.experimental import pallas as pl
from jax.experimental.pallas import tpu as pltpu
from jax.sharding import PartitionSpec as P

D = 768
HL = 8
HH = 12
DH = 64
FL = 1024
FH = 4096
WIN = 128
CAP = 64

EPSILON = 1e-06
MASKED = -1000000000.0
SCORE_SCALE = 0.125
MESH = pl.DeviceIdType.MESH
BF = jnp.bfloat16
F32 = jnp.float32
ANY = pl.BlockSpec(memory_space=pl.ANY)
VM = pl.BlockSpec(memory_space=pltpu.VMEM)
DMA = pltpu.SemaphoreType.DMA
VMEM_BYTES = 60 * 1024 * 1024


def place():
    d = lax.axis_index("dp")
    f = lax.axis_index("fsdp")
    return d // 2, d % 2, f // 2, f % 2


def at(hi, lo, x, c):
    return (hi * 2 + lo, x * 2 + c)


def meet(peers):
    barrier = pltpu.get_barrier_semaphore()
    for peer in peers:
        pl.semaphore_signal(barrier, inc=1, device_id=peer, device_id_type=MESH)
    pl.semaphore_wait(barrier, len(peers))


def send(src, dst, send_sem, recv_sem, peer):
    copy = pltpu.make_async_remote_copy(
        src_ref=src,
        dst_ref=dst,
        send_sem=send_sem,
        recv_sem=recv_sem,
        device_id=peer,
        device_id_type=MESH,
    )
    copy.start()
    return copy


def keep(src, dst, sem):
    copy = pltpu.make_async_copy(src, dst, sem)
    copy.start()
    return copy


def quad_peers():
    hi, lo, x, c = place()
    return [(lo, 1 - x), (1 - lo, x), (1 - lo, 1 - x)]


def call(kernel, out_shape, operands, in_specs, out_specs, scratch, collective_id):
    return pl.pallas_call(
        kernel,
        out_shape=out_shape,
        in_specs=in_specs,
        out_specs=out_specs,
        scratch_shapes=scratch,
        compiler_params=pltpu.CompilerParams(
            collective_id=collective_id, has_side_effects=True, vmem_limit_bytes=VMEM_BYTES
        ),
    )(*operands)


def deal_kernel(deal_ref, x_ref, o_ref):
    def body(i, carry):
        o_ref[i] = x_ref[deal_ref[i]]
        return carry

    lax.fori_loop(0, o_ref.shape[0], body, 0)


def deal_rows(dealing, rows):
    return pl.pallas_call(
        deal_kernel,
        out_shape=jax.ShapeDtypeStruct(rows.shape, rows.dtype),
        in_specs=[pl.BlockSpec(memory_space=pltpu.SMEM), VM],
        out_specs=VM,
        compiler_params=pltpu.CompilerParams(vmem_limit_bytes=VMEM_BYTES),
    )(dealing, rows)


def undeal_kernel(deal_ref, x_ref, o_ref):
    def body(i, carry):
        o_ref[deal_ref[i]] = x_ref[i].astype(F32)
        return carry

    lax.fori_loop(0, x_ref.shape[0], body, 0)


def undeal_rows(dealing, rows):
    return pl.pallas_call(
        undeal_kernel,
        out_shape=jax.ShapeDtypeStruct(rows.shape, F32),
        in_specs=[pl.BlockSpec(memory_space=pltpu.SMEM), VM],
        out_specs=VM,
        compiler_params=pltpu.CompilerParams(vmem_limit_bytes=VMEM_BYTES),
    )(dealing, rows)


def packed(matrix):
    rows, columns = matrix.shape
    if rows % 8 == 0:
        return matrix
    return matrix.reshape(rows * columns // 128, 128)


def unpacked(gathered, rows, columns):
    return gathered.reshape(-1, rows, columns).reshape(-1, columns)


def gather_kernel(dp, nw, *refs):
    nz = dp // 2
    xin, ws, hin, hdn = refs[0], refs[1 : 1 + nw], refs[1 + nw], refs[2 + nw]
    outs = refs[3 + nw :]
    xo, wos, hin_o, hdn_o = outs[0], outs[1 : 1 + nw], outs[1 + nw], outs[2 + nw]
    loc, xs, xr, zs, zr, ps, pr, cs, cr, hs, hr = outs[3 + nw :]
    hi, lo, x, c = place()
    d = hi * 2 + lo
    f = x * 2 + c
    plane = (lo * 2 + x) * 2 + c
    group = xin.shape[0] // dp
    dp_peers = [(lax.rem(d + k, dp), f) for k in range(1, dp)]
    rest = [(a, b, e) for a in (0, 1) for b in (0, 1) for e in (0, 1) if a or b or e]
    flat8 = []
    for a, b, e in rest:
        l2 = 1 - lo if a else lo
        x2 = 1 - x if b else x
        c2 = 1 - c if e else c
        flat8.append((l2, x2, c2))
    meet(dp_peers + [at(hi, *p) for (a, b, e), p in zip(rest, flat8) if b or e])
    locals_ = [keep(ws[w], wos[w].at[hi, lo, x, c], loc.at[w]) for w in range(nw)]
    locals_.append(keep(xin.at[pl.ds(d * group, group)], xo.at[:, d], loc.at[nw]))
    locals_.append(keep(hin.at[plane], hin_o.at[hi, plane], loc.at[nw + 1]))
    locals_.append(keep(hdn, hdn_o.at[hi], loc.at[nw + 2]))
    x_sends = []
    for k, peer in enumerate(dp_peers):
        x_sends.append(
            send(xin.at[pl.ds(peer[0] * group, group)], xo.at[:, d], xs.at[k], xr.at[k], peer)
        )
    z_peers = [at(lax.rem(hi + k, nz), lo, x, c) for k in range(1, nz)]
    z_sends = [
        [
            send(ws[w], wos[w].at[hi, lo, x, c], zs.at[w, k], zr.at[w, k], peer)
            for k, peer in enumerate(z_peers)
        ]
        for w in range(nw)
    ]
    h_sends = []
    for k, (l2, x2, c2) in enumerate(flat8):
        h_sends.append(
            send(
                hin.at[(l2 * 2 + x2) * 2 + c2],
                hin_o.at[hi, plane],
                hs.at[0, k],
                hr.at[0, k],
                at(hi, l2, x2, c2),
            )
        )
    quad = quad_peers()
    partner = at(hi, lo, x, 1 - c)
    p_sends, c_sends = [], []

    def forward_plane(w):
        locals_[w].wait()
        for copy in z_sends[w]:
            copy.wait()
        column = wos[w].at[:, lo, x, c]
        p_sends.append(
            [
                send(column, column, ps.at[w, k], pr.at[w, k], at(hi, l2, x2, c))
                for k, (l2, x2) in enumerate(quad)
            ]
        )
        c_sends.append([send(column, column, cs.at[w, 0], cr.at[w, 0], partner)])

    def forward_core(w):
        for k, (l2, x2) in enumerate(quad):
            p_sends[w][k].wait()
            column = wos[w].at[:, l2, x2, c]
            c_sends[w].append(send(column, column, cs.at[w, k + 1], cr.at[w, k + 1], partner))

    for w in range(nw):
        forward_plane(w)
        if w >= 1:
            forward_core(w - 1)
    for copy in h_sends:
        copy.wait()
    locals_[nw + 1].wait()
    late = []
    for k, peer in enumerate(z_peers):
        late.append(send(hin_o.at[hi], hin_o.at[hi], hs.at[1, k], hr.at[1, k], peer))
        late.append(send(hdn, hdn_o.at[hi], hs.at[2, k], hr.at[2, k], peer))
    forward_core(nw - 1)
    locals_[nw].wait()
    locals_[nw + 2].wait()
    for copy in x_sends + late:
        copy.wait()
    for copies in c_sends:
        for copy in copies:
            copy.wait()


def gather_all(dp, xin, weights, hin, hdn):
    nz = dp // 2
    nw = len(weights)
    seqs, rows, _ = xin.shape
    shapes = [jax.ShapeDtypeStruct((seqs // dp, dp, rows, D), BF)]
    shapes += [jax.ShapeDtypeStruct((nz, 2, 2, 2) + w.shape, BF) for w in weights]
    shapes.append(jax.ShapeDtypeStruct((nz,) + hin.shape, BF))
    shapes.append(jax.ShapeDtypeStruct((nz,) + hdn.shape, BF))
    most = max(7, nz)
    scratch = [
        DMA((nw + 3,)),
        DMA((dp,)),
        DMA((dp,)),
        DMA((nw, nz)),
        DMA((nw, nz)),
        DMA((nw, 3)),
        DMA((nw, 3)),
        DMA((nw, 4)),
        DMA((nw, 4)),
        DMA((3, most)),
        DMA((3, most)),
    ]
    return call(
        functools.partial(gather_kernel, dp, nw),
        shapes,
        [xin, *weights, hin, hdn],
        [ANY] * (3 + nw),
        [ANY] * (3 + nw),
        scratch,
        1,
    )


def rim_exchange(left, right, from_left, from_right, ls, lr, rs, rr):
    d = lax.axis_index("dp")
    f = lax.axis_index("fsdp")
    last = lax.axis_size("fsdp") - 1

    def down():
        return pltpu.make_async_remote_copy(
            src_ref=left,
            dst_ref=from_right,
            send_sem=ls,
            recv_sem=lr,
            device_id=(d, lax.max(f - 1, 0)),
            device_id_type=MESH,
        )

    def up():
        return pltpu.make_async_remote_copy(
            src_ref=right,
            dst_ref=from_left,
            send_sem=rs,
            recv_sem=rr,
            device_id=(d, lax.min(f + 1, last)),
            device_id_type=MESH,
        )

    @pl.when(f > 0)
    def _():
        down().start()

    @pl.when(f < last)
    def _():
        up().start()

    @pl.when(f == 0)
    def _():
        from_left[...] = jnp.zeros(from_left.shape, from_left.dtype)

    @pl.when(f == last)
    def _():
        from_right[...] = jnp.zeros(from_right.shape, from_right.dtype)

    def finish():
        @pl.when(f > 0)
        def _():
            down().wait_send()
            up().wait_recv()

        @pl.when(f < last)
        def _():
            up().wait_send()
            down().wait_recv()

    return finish


def line_peers():
    hi, lo, x, c = place()
    return [at(hi, lo, x, 1 - c), at(hi, lo, 1 - x, c), at(hi, lo, 1 - x, 1 - c)]


def keys_kernel(left, right, kv, from_left, from_right, every, own, ls, lr, rs, rr, ss, sr):
    hi, lo, x, c = place()
    f = x * 2 + c
    meet(line_peers())
    finish = rim_exchange(left, right, from_left, from_right, ls, lr, rs, rr)
    mine = keep(kv, every.at[:, f], own)
    across = send(kv, every.at[:, f], ss.at[0], sr.at[0], at(hi, lo, 1 - x, c))
    beside = send(kv, every.at[:, f], ss.at[1], sr.at[1], at(hi, lo, x, 1 - c))
    across.wait()
    other = every.at[:, (1 - x) * 2 + c]
    relay = send(other, other, ss.at[2], sr.at[2], at(hi, lo, x, 1 - c))
    mine.wait()
    beside.wait()
    relay.wait()
    finish()


def exchange_keys(left, right, kv):
    group, cap, width = kv.shape
    return call(
        keys_kernel,
        [
            jax.ShapeDtypeStruct(left.shape, BF),
            jax.ShapeDtypeStruct(right.shape, BF),
            jax.ShapeDtypeStruct((group, 4, cap, width), BF),
        ],
        [left, right, kv],
        [VM] * 3,
        [VM] * 3,
        [DMA, DMA, DMA, DMA, DMA, DMA((3,)), DMA((3,))],
        2,
    )


def key_grads_kernel(left, right, part, from_left, from_right, total, got, far, ls, lr, rs, rr, ss, sr):
    hi, lo, x, c = place()
    meet(line_peers())
    finish = rim_exchange(left, right, from_left, from_right, ls, lr, rs, rr)
    beside = [
        send(
            part.at[:, b * 2 + 1 - c], got.at[b], ss.at[b], sr.at[b], at(hi, lo, x, 1 - c)
        )
        for b in (0, 1)
    ]
    for copy in beside:
        copy.wait()
    for b in (0, 1):
        got[b] = (got[b].astype(F32) + part[:, b * 2 + c].astype(F32)).astype(BF)
    across = send(got.at[1 - x], far, ss.at[2], sr.at[2], at(hi, lo, 1 - x, c))
    across.wait()
    total[...] = got[x].astype(F32) + far[...].astype(F32)
    finish()


def exchange_key_grads(left, right, part):
    group, _, cap, width = part.shape
    return call(
        key_grads_kernel,
        [
            jax.ShapeDtypeStruct(left.shape, BF),
            jax.ShapeDtypeStruct(right.shape, BF),
            jax.ShapeDtypeStruct((group, cap, width), F32),
        ],
        [left, right, part],
        [VM] * 3,
        [VM] * 3,
        [
            pltpu.VMEM((2, group, cap, width), BF),
            pltpu.VMEM((group, cap, width), BF),
            DMA,
            DMA,
            DMA,
            DMA,
            DMA((3,)),
            DMA((3,)),
        ],
        3,
    )


def dot(left, right):
    return jnp.dot(left, right, preferred_element_type=F32)


def dot_back(left, right):
    return lax.dot_general(left, right, (((1,), (1,)), ((), ())), preferred_element_type=F32)


def dot_grad(left, right):
    return lax.dot_general(left, right, (((0,), (0,)), ((), ())), preferred_element_type=F32)


def halves(value):
    high = value.astype(BF)
    return high, (value - high.astype(F32)).astype(BF)


def tiles(extent, step, body):
    def run(i, carry):
        body(pl.ds(pl.multiple_of(i * step, step), step))
        return carry

    lax.fori_loop(0, extent // step, run, 0)


GELU_A = 0.7978845608028654
GELU_B = 0.044715


def gelu_parts(v):
    square = v * v
    t = jnp.tanh(GELU_A * v * (1.0 + GELU_B * square))
    value = 0.5 * v * (1.0 + t)
    slope = 0.5 * (1.0 + t) + 0.5 * v * (1.0 - t * t) * GELU_A * (1.0 + 3.0 * GELU_B * square)
    return value, slope


def gelu_value(v):
    return 0.5 * v * (1.0 + jnp.tanh(GELU_A * v * (1.0 + GELU_B * v * v)))


def ffn_kernel(
    hidden,
    select,
    select_t,
    score,
    gain,
    teach,
    mask,
    scale,
    w_in,
    w_dn,
    w_hin,
    w_hdn,
    g_in,
    g_dn,
    g_hin,
    g_hdn,
    d_hidden,
    stats,
    hn,
    every,
    d_every,
    up_l,
    z,
    up_h,
    zh,
    part,
    near,
    far,
    near2,
    far2,
    out,
    dl,
    dup_l,
    dup_h,
    dhn,
    ps,
    pr,
    cs,
    cr,
    qs,
    qr,
    es,
    er,
):
    hi, lo, x, c = place()
    quad = quad_peers()
    partner = at(hi, lo, x, 1 - c)
    spots = [l2 * 2 + x2 for l2, x2 in quad]
    home = lo * 2 + x
    tokens = hidden.shape[0]
    group, cap, width = select.shape
    fl = z.shape[1]
    fh = zh.shape[2]
    rows_h = part.shape[1] * part.shape[2]
    meet([at(hi, l2, x2, c) for l2, x2 in quad] + [partner])

    def spread(buffer, i):
        spot = buffer.at[c, home]
        there = [
            send(spot, spot, ps.at[i, k], pr.at[i, k], at(hi, l2, x2, c))
            for k, (l2, x2) in enumerate(quad)
        ]
        return there, [send(spot, spot, cs.at[i, 3], cr.at[i, 3], partner)]

    def relay(buffer, i, there, back):
        for k, q in enumerate(spots):
            there[k].wait()
            other = buffer.at[c, q]
            back.append(send(other, other, cs.at[i, k], cr.at[i, k], partner))

    def fold(near_ref, far_ref, i, copy):
        copy.wait()
        there = []
        for k, q in enumerate(spots):
            near_ref[q] = (near_ref[q].astype(F32) + part[c, q].astype(F32)).astype(BF)
            l2, x2 = quad[k]
            there.append(
                send(near_ref.at[q], far_ref.at[k], qs.at[i, k], qr.at[i, k], at(hi, l2, x2, c))
            )
        return there

    def folded(near_ref, far_ref, there):
        for copy in there:
            copy.wait()
        return (
            near_ref[home].astype(F32)
            + part[c, home].astype(F32)
            + far_ref[0].astype(F32)
            + far_ref[1].astype(F32)
            + far_ref[2].astype(F32)
        )

    def norm(r):
        h = hidden[r, :]
        inv = lax.rsqrt(jnp.mean(h * h, axis=-1, keepdims=True) + EPSILON)
        hn[r, :] = (h * inv * gain[...]).astype(BF)

    tiles(tokens, 128, norm)
    for s in range(group):
        every[c, home, s * cap : (s + 1) * cap, :] = dot(
            select[s], hn[s * width : (s + 1) * width, :]
        ).astype(BF)
    there, back = spread(every, 0)

    def light_up(r):
        a = hn[r, :]

        def inner(j):
            k = pl.ds(pl.multiple_of(j.start + fl, 256), 256)
            g = dot(a, w_in[:, j])
            u = dot(a, w_in[:, k])
            up_l[r, j] = g
            up_l[r, k] = u
            z[r, j] = (gelu_value(g) * u).astype(BF)

        tiles(fl, 256, inner)

    tiles(tokens, 256, light_up)
    relay(every, 0, there, back)

    def light_down(r):
        out[r, :] = hidden[r, :] + dot(z[r, :], w_dn[...])

    tiles(tokens, 256, light_down)
    for copy in back:
        copy.wait()

    def heavy(e):
        def up(i, carry):
            a = every[e, pl.ds(2 * i, 2)].reshape(2 * group * cap, D)
            r = pl.ds(pl.multiple_of(i * 256, 256), 256)
            for j in range(0, fh, 256):
                g = dot(a, w_hin[:, j : j + 256])
                u = dot(a, w_hin[:, fh + j : fh + j + 256])
                up_h[e, r, j : j + 256] = g
                up_h[e, r, fh + j : fh + j + 256] = u
                zh[e, r, j : j + 256] = (gelu_value(g) * u).astype(BF)
            v = dot(zh[e, r, :], w_hdn[...]).astype(BF)
            part[e, pl.ds(2 * i, 2)] = v.reshape(2, group * cap, D)
            return carry

        lax.fori_loop(0, 2, up, 0)

    heavy(1 - c)
    first = send(part.at[1 - c], near, es.at[0], er.at[0], partner)
    heavy(c)
    there = fold(near, far, 0, first)
    hf = folded(near, far, there) * score[...]
    hf_high, hf_low = halves(hf)
    for s in range(group):
        r = slice(s * width, (s + 1) * width)
        q = slice(s * cap, (s + 1) * cap)
        out[r, :] += dot(select_t[s], hf_high[q]) + dot(select_t[s], hf_low[q])
    stats[...] = jnp.zeros(stats.shape, F32)

    def misfit(r):
        m = out[r, :] - teach[r, :].astype(F32)
        stats[1:2, :] += jnp.sum(mask[r, :] * m * m, axis=0, keepdims=True)
        d = scale[r, :] * m
        out[r, :] = d
        dl[r, :] = d.astype(BF)

    tiles(tokens, 128, misfit)
    for s in range(group):
        high, low = halves(out[s * width : (s + 1) * width, :])
        picked = dot(select[s], high) + dot(select[s], low)
        q = slice(s * cap, (s + 1) * cap)
        d_every[c, home, q, :] = (picked * score[q, :]).astype(BF)
    there, back = spread(d_every, 1)

    def light_back(r):
        d = dl[r, :]

        def inner(j):
            k = pl.ds(pl.multiple_of(j.start + fl, 256), 256)
            dz = dot_back(d, w_dn[j, :])
            value, slope = gelu_parts(up_l[r, j])
            dup_l[r, j] = (dz * up_l[r, k] * slope).astype(BF)
            dup_l[r, k] = (dz * value).astype(BF)

        tiles(fl, 256, inner)

    tiles(tokens, 256, light_back)
    relay(d_every, 1, there, back)

    def light_grad(j):
        g_dn[j, :] = dot_grad(z[:, j], dl[...]).astype(BF)

    tiles(fl, 256, light_grad)
    for copy in back:
        copy.wait()

    def heavy_back(e):
        def run(i, carry):
            d = d_every[e, pl.ds(2 * i, 2)].reshape(2 * group * cap, D)
            r = pl.ds(pl.multiple_of(i * 256, 256), 256)
            for j in range(0, fh, 256):
                dz = dot_back(d, w_hdn[j : j + 256, :])
                value, slope = gelu_parts(up_h[e, r, j : j + 256])
                dup_h[e, r, j : j + 256] = (
                    dz * up_h[e, r, fh + j : fh + j + 256] * slope
                ).astype(BF)
                dup_h[e, r, fh + j : fh + j + 256] = (dz * value).astype(BF)
            v = dot_back(dup_h[e, r, :], w_hin[...]).astype(BF)
            part[e, pl.ds(2 * i, 2)] = v.reshape(2, group * cap, D)
            return carry

        lax.fori_loop(0, 2, run, 0)

    heavy_back(1 - c)
    second = send(part.at[1 - c], near2, es.at[1], er.at[1], partner)
    heavy_back(c)
    there = fold(near2, far2, 1, second)

    def light_in_grad(j):
        g_in[:, j] = dot_grad(hn[...], dup_l[:, j]).astype(BF)

    tiles(2 * fl, 256, light_in_grad)

    def light_in_back(r):
        dhn[r, :] = dot_back(dup_l[r, :], w_in[...])

    tiles(tokens, 256, light_in_back)
    every_rows = every[...].reshape(2 * rows_h, D)

    def heavy_grad(j):
        g_hin[:, j] = dot_grad(every_rows, dup_h[:, :, j].reshape(2 * rows_h, 256)).astype(BF)

    tiles(2 * fh, 256, heavy_grad)
    d_rows = d_every[...].reshape(2 * rows_h, D)

    def heavy_down_grad(j):
        g_hdn[j, :] = dot_grad(zh[:, :, j].reshape(2 * rows_h, 256), d_rows).astype(BF)

    tiles(fh, 256, heavy_down_grad)
    d_high, d_low = halves(folded(near2, far2, there))
    for s in range(group):
        r = slice(s * width, (s + 1) * width)
        q = slice(s * cap, (s + 1) * cap)
        dhn[r, :] += dot(select_t[s], d_high[q]) + dot(select_t[s], d_low[q])

    def norm_back(r):
        h = hidden[r, :]
        inv = lax.rsqrt(jnp.mean(h * h, axis=-1, keepdims=True) + EPSILON)
        d = dhn[r, :]
        dh = d * h
        stats[0:1, :] += jnp.sum(dh * inv, axis=0, keepdims=True)
        mean = jnp.mean(gain[...] * dh, axis=-1, keepdims=True)
        d_hidden[r, :] = out[r, :] + inv * gain[...] * d - h * (inv * inv * inv * mean)

    tiles(tokens, 128, norm_back)


def feed_forward(hidden, select, select_t, score, gain, teach, mask, scale, w_in, w_dn, w_hin, w_hdn):
    tokens = hidden.shape[0]
    group, cap, _ = select.shape
    rows = group * cap
    fl, fh = w_dn.shape[0], w_hdn.shape[0]
    block = (2, 4, rows, D)
    operands = [hidden, select, select_t, score, gain, teach, mask, scale, w_in, w_dn, w_hin, w_hdn]
    return call(
        ffn_kernel,
        [
            jax.ShapeDtypeStruct((D, 2 * fl), BF),
            jax.ShapeDtypeStruct((fl, D), BF),
            jax.ShapeDtypeStruct((D, 2 * fh), BF),
            jax.ShapeDtypeStruct((fh, D), BF),
            jax.ShapeDtypeStruct((tokens, D), F32),
            jax.ShapeDtypeStruct((8, D), F32),
        ],
        operands,
        [VM] * len(operands),
        [VM] * 6,
        [
            pltpu.VMEM((tokens, D), BF),
            pltpu.VMEM(block, BF),
            pltpu.VMEM(block, BF),
            pltpu.VMEM((tokens, 2 * fl), F32),
            pltpu.VMEM((tokens, fl), BF),
            pltpu.VMEM((2, 4 * rows, 2 * fh), F32),
            pltpu.VMEM((2, 4 * rows, fh), BF),
            pltpu.VMEM(block, BF),
            pltpu.VMEM(block[1:], BF),
            pltpu.VMEM((3, rows, D), BF),
            pltpu.VMEM(block[1:], BF),
            pltpu.VMEM((3, rows, D), BF),
            pltpu.VMEM((tokens, D), F32),
            pltpu.VMEM((tokens, D), BF),
            pltpu.VMEM((tokens, 2 * fl), BF),
            pltpu.VMEM((2, 4 * rows, 2 * fh), BF),
            pltpu.VMEM((tokens, D), F32),
            DMA((2, 3)),
            DMA((2, 3)),
            DMA((2, 4)),
            DMA((2, 4)),
            DMA((2, 3)),
            DMA((2, 3)),
            DMA((2,)),
            DMA((2,)),
        ],
        5,
    )


def scatter_kernel(dp, nw, *refs):
    nz = dp // 2
    dx, stats, gs, hin, hdn = refs[0], refs[1], refs[2 : 2 + nw], refs[2 + nw], refs[3 + nw]
    outs = refs[4 + nw :]
    dxo, total, gos, hin_o, hdn_o = outs[0], outs[1], outs[2 : 2 + nw], outs[2 + nw], outs[3 + nw]
    scr = outs[4 + nw :]
    nears, fars, sums, ends = (scr[i * nw : (i + 1) * nw] for i in range(4))
    hin_r, hin_s, hdn_r, sc, sp, sz, acc, acc2 = scr[4 * nw : 4 * nw + 8]
    own, xs, xr, cs, cr, ps, pr, zs, zr, hs, hr, ts, tr = scr[4 * nw + 8 :]
    hi, lo, x, c = place()
    d = hi * 2 + lo
    f = x * 2 + c
    plane = (lo * 2 + x) * 2 + c
    dp_peers = [(lax.rem(d + k, dp), f) for k in range(1, dp)]
    rest = [(a, b, e) for a in (0, 1) for b in (0, 1) for e in (0, 1) if a or b or e]
    flat8 = []
    for a, b, e in rest:
        l2 = 1 - lo if a else lo
        x2 = 1 - x if b else x
        c2 = 1 - c if e else c
        flat8.append((l2, x2, c2))
    meet(dp_peers + [at(hi, *p) for (a, b, e), p in zip(rest, flat8) if b or e])
    partner = at(hi, lo, x, 1 - c)
    quad = quad_peers()
    z_index = [lax.rem(hi + k, nz) for k in range(1, nz)]
    z_peers = [at(z, lo, x, c) for z in z_index]
    c_sends = [
        send(gs[w].at[:, :, :, 1 - c], nears[w], cs.at[w], cr.at[w], partner) for w in range(nw)
    ]
    t_c = send(stats, sc, ts.at[0], tr.at[0], partner)
    mine = keep(dx.at[:, d], dxo.at[d], own)
    x_sends = [
        send(dx.at[:, peer[0]], dxo.at[d], xs.at[k], xr.at[k], peer)
        for k, peer in enumerate(dp_peers)
    ]
    h_sends = []
    for k, z in enumerate(z_index):
        h_sends.append(send(hin.at[z], hin_r.at[k], hs.at[1, k], hr.at[1, k], z_peers[k]))
        h_sends.append(send(hdn.at[z], hdn_r.at[k], hs.at[2, k], hr.at[2, k], z_peers[k]))
    p_sends, z_sends = [], []
    t_c.wait()
    acc[...] = stats[...] + sc[...]
    t_p = [
        send(acc, sp.at[k], ts.at[1 + k], tr.at[1 + k], at(hi, l2, x2, c))
        for k, (l2, x2) in enumerate(quad)
    ]

    def add_core(w):
        c_sends[w].wait()
        near, g = nears[w], gs[w]

        def body(i, carry):
            z, a, b = i // 4, (i // 2) % 2, i % 2
            near[z, a, b] = (near[z, a, b].astype(F32) + g[z, a, b, c].astype(F32)).astype(BF)
            return carry

        lax.fori_loop(0, nz * 4, body, 0)
        p_sends.append(
            [
                send(near.at[:, l2, x2], fars[w].at[k], ps.at[w, k], pr.at[w, k], at(hi, l2, x2, c))
                for k, (l2, x2) in enumerate(quad)
            ]
        )

    def add_plane(w):
        for copy in p_sends[w]:
            copy.wait()
        near, far, part = nears[w], fars[w], sums[w]

        def body(z, carry):
            part[z] = (
                near[z, lo, x].astype(F32)
                + far[0, z].astype(F32)
                + far[1, z].astype(F32)
                + far[2, z].astype(F32)
            ).astype(BF)
            return carry

        lax.fori_loop(0, nz, body, 0)
        z_sends.append(
            [
                send(part.at[z], ends[w].at[k], zs.at[w, k], zr.at[w, k], z_peers[k])
                for k, z in enumerate(z_index)
            ]
        )

    def add_line(w):
        for copy in z_sends[w]:
            copy.wait()
        gos[w][...] = sums[w][hi].astype(F32)
        for k in range(nz - 1):
            gos[w][...] += ends[w][k].astype(F32)

    for w in range(nw):
        add_core(w)
        if w >= 2:
            add_plane(w - 2)
    for copy in t_p:
        copy.wait()
    acc2[...] = acc[...] + sp[0] + sp[1] + sp[2]
    t_z = [send(acc2, sz.at[k], ts.at[4 + k], tr.at[4 + k], z_peers[k]) for k in range(nz - 1)]
    for copy in h_sends:
        copy.wait()

    def body(i, carry):
        value = hin[hi, i].astype(F32)
        for k in range(nz - 1):
            value += hin_r[k, i].astype(F32)
        hin_s[i] = value.astype(BF)
        return carry

    lax.fori_loop(0, 8, body, 0)
    hin_o[plane] = hin_s[plane]
    a_sends = [
        send(
            hin_s.at[(l2 * 2 + x2) * 2 + c2],
            hin_o.at[plane],
            hs.at[0, k],
            hr.at[0, k],
            at(hi, l2, x2, c2),
        )
        for k, (l2, x2, c2) in enumerate(flat8)
    ]
    hdn_o[...] = hdn[hi].astype(F32)
    for k in range(nz - 1):
        hdn_o[...] += hdn_r[k].astype(F32)
    for w in range(max(nw - 2, 0), nw):
        add_plane(w)
    for copy in t_z:
        copy.wait()
    total[...] = acc2[...]
    for k in range(nz - 1):
        total[...] += sz[k]
    for w in range(nw):
        add_line(w)
    mine.wait()
    for copy in x_sends + a_sends:
        copy.wait()


def scatter_all(dp, dx, stats, grads, hin, hdn):
    nz = dp // 2
    nw = len(grads)
    group, _, rows, _ = dx.shape
    tiles = [g.shape[4:] for g in grads]
    most = max(7, nz)
    scratch = [pltpu.VMEM((nz, 2, 2) + t, BF) for t in tiles]
    scratch += [pltpu.VMEM((3, nz) + t, BF) for t in tiles]
    scratch += [pltpu.VMEM((nz,) + t, BF) for t in tiles]
    scratch += [pltpu.VMEM((nz - 1,) + t, BF) for t in tiles]
    scratch += [
        pltpu.VMEM((nz - 1,) + hin.shape[1:], BF),
        pltpu.VMEM(hin.shape[1:], BF),
        pltpu.VMEM((nz - 1,) + hdn.shape[1:], BF),
        pltpu.VMEM(stats.shape, F32),
        pltpu.VMEM((3,) + stats.shape, F32),
        pltpu.VMEM((nz - 1,) + stats.shape, F32),
        pltpu.VMEM(stats.shape, F32),
        pltpu.VMEM(stats.shape, F32),
        DMA,
        DMA((dp,)),
        DMA((dp,)),
        DMA((nw,)),
        DMA((nw,)),
        DMA((nw, 3)),
        DMA((nw, 3)),
        DMA((nw, nz)),
        DMA((nw, nz)),
        DMA((3, most)),
        DMA((3, most)),
        DMA((4 + nz,)),
        DMA((4 + nz,)),
    ]
    shapes = [jax.ShapeDtypeStruct((dp, group, rows, D), BF), jax.ShapeDtypeStruct(stats.shape, F32)]
    shapes += [jax.ShapeDtypeStruct(t, F32) for t in tiles]
    shapes.append(jax.ShapeDtypeStruct(hin.shape[1:], BF))
    shapes.append(jax.ShapeDtypeStruct(hdn.shape[1:], F32))
    return call(
        functools.partial(scatter_kernel, dp, nw),
        shapes,
        [dx, stats, *grads, hin, hdn],
        [ANY] + [VM] * (3 + nw),
        [ANY] + [VM] * (3 + nw),
        scratch,
        4,
    )


def rms_norm(value, gain):
    return value * lax.rsqrt(jnp.mean(value * value, axis=-1, keepdims=True) + EPSILON) * gain


def split_heads(rows, heads):
    return rows.reshape(rows.shape[0], rows.shape[1], heads, -1)


def head_scores(queries, key_rows, allowed, heads):
    scores = (
        jnp.einsum(
            "sqhd,skhd->shqk",
            split_heads(queries, heads),
            split_heads(key_rows, heads),
            preferred_element_type=F32,
        )
        * SCORE_SCALE
    )
    return jnp.where(allowed[:, None], scores, MASKED)


def attend_forward(queries, key_rows, value_rows, allowed, heads):
    scores = head_scores(queries, key_rows, allowed, heads)
    row_max = jnp.max(scores, axis=-1, keepdims=True)
    shifted = jnp.exp(scores - row_max)
    row_sum = jnp.sum(shifted, axis=-1, keepdims=True)
    attn_prob = (shifted / row_sum).astype(BF)
    attended = jnp.einsum(
        "shqk,skhd->sqhd", attn_prob, split_heads(value_rows, heads), preferred_element_type=F32
    )
    return (attended.reshape(queries.shape).astype(BF), row_max + jnp.log(row_sum))


def attend_backward(queries, key_rows, value_rows, allowed, log_sum, d_attended, heads):
    scores = head_scores(queries, key_rows, allowed, heads)
    attn_prob = jnp.exp(scores - log_sum)
    d_heads = split_heads(d_attended, heads)
    d_prob = jnp.einsum(
        "sqhd,skhd->shqk", d_heads, split_heads(value_rows, heads), preferred_element_type=F32
    )
    row_dot = jnp.sum(attn_prob * d_prob, axis=-1, keepdims=True)
    d_scores = (attn_prob * (d_prob - row_dot)).astype(BF)
    d_query = (
        jnp.einsum(
            "shqk,skhd->sqhd", d_scores, split_heads(key_rows, heads), preferred_element_type=F32
        )
        * SCORE_SCALE
    )
    d_key = (
        jnp.einsum(
            "shqk,sqhd->skhd", d_scores, split_heads(queries, heads), preferred_element_type=F32
        )
        * SCORE_SCALE
    )
    d_value = jnp.einsum(
        "shqk,sqhd->skhd", attn_prob.astype(BF), d_heads, preferred_element_type=F32
    )
    return (
        d_query.reshape(queries.shape),
        d_key.reshape(key_rows.shape),
        d_value.reshape(value_rows.shape),
    )


def mul(left, right):
    return jnp.einsum("...d,de->...e", left, right, preferred_element_type=F32)


def mul_back(left, right):
    return jnp.einsum("...e,de->...d", left, right, preferred_element_type=F32)


def weight_grad(left, right):
    a = left.reshape(-1, left.shape[-1])
    b = right.reshape(-1, right.shape[-1])
    return jnp.einsum("pd,pe->de", a, b, preferred_element_type=F32)


def pick(spec, hot, value):
    high = value.astype(BF)
    rest = (value - high.astype(F32)).astype(BF)
    return jnp.einsum(spec, hot, high, preferred_element_type=F32) + jnp.einsum(
        spec, hot, rest, preferred_element_type=F32
    )


def routing(routes, pieces, piece_len):
    places = jnp.arange(pieces * piece_len)
    routed = jnp.any(routes[:, None, :] == places[None, :, None], axis=-1)
    routed = routed.reshape(-1, pieces, piece_len)
    before = jnp.arange(piece_len)[:, None] < jnp.arange(piece_len)[None, :]
    rank = jnp.einsum(
        "skp,pq->skq", routed.astype(BF), before.astype(BF), preferred_element_type=F32
    )
    slots = jnp.arange(CAP, dtype=F32)
    hot = routed[:, :, None, :] & (rank[:, :, None, :] == slots[None, None, :, None])
    filled = jnp.any(hot, axis=-1)
    spots = jnp.sum(jnp.where(hot, places.reshape(1, pieces, 1, piece_len), 0), axis=-1)
    return hot, jnp.where(filled, spots, -1)


def local(
    layer_input,
    teacher,
    lengths,
    dealing,
    attn_routes,
    ffn_routes,
    ffn_scores,
    gain_attn,
    gain_ffn,
    light_qkv,
    light_out,
    heavy_qkv,
    heavy_out,
    light_in,
    light_down,
    heavy_in,
    heavy_down,
):
    dp = lax.axis_size("dp")
    pieces = lax.axis_size("fsdp")
    data_index = lax.axis_index("dp")
    piece = lax.axis_index("fsdp")
    nz = dp // 2
    n = dp * pieces
    seqs = dealing.shape[0]
    group = seqs // dp
    gain_len = gain_attn.shape[0]
    hidden_units = heavy_in.shape[1] // 2 // n
    xin = deal_rows(dealing, layer_input[:, 0])
    gains = jnp.pad(
        jnp.stack([gain_attn, gain_ffn]), ((0, 6), (0, 128 - gain_len))
    )
    matrices = (light_qkv, heavy_qkv, light_out, heavy_out, light_in, light_down)
    hin_rows = heavy_in.shape[0]
    hin_src = (
        heavy_in.reshape(hin_rows, 2, nz, 8, hidden_units)
        .transpose(3, 0, 1, 2, 4)
        .reshape(8, hin_rows, 2 * nz * hidden_units)
    )
    if hin_rows % 8:
        hin_src = hin_src.reshape(8, -1, 128)
    got = gather_all(dp, xin, [gains] + [packed(m) for m in matrices], hin_src, heavy_down)
    tokens = layer_input.shape[2] * dp
    inputs = got[0].reshape(group, tokens, D).astype(F32)
    gain_rows = got[1].reshape(n, 8, 128)
    gain_one = gain_rows[:, 0, :gain_len].reshape(-1).astype(F32)
    gain_two = gain_rows[:, 1, :gain_len].reshape(-1).astype(F32)
    w_lqkv, w_hqkv, w_lout, w_hout, w_lin, w_ldown = (
        unpacked(full, *m.shape) for full, m in zip(got[2:8], matrices)
    )
    w_hin = unpacked(got[8], hin_rows, 2 * nz * hidden_units)
    w_hdown = got[9].reshape(-1, D)
    chosen = lax.dynamic_slice_in_dim(dealing, data_index * group, group)
    one = (chosen[:, None] == jnp.arange(seqs)[None, :])
    seq_lengths = jnp.sum(jnp.where(one, lengths[None, :], 0), axis=1)
    attn_pick = jnp.sum(jnp.where(one[:, :, None], attn_routes[None], 0), axis=1)
    ffn_pick = jnp.sum(jnp.where(one[:, :, None], ffn_routes[None], 0), axis=1)
    score_pick = jnp.sum(jnp.where(one[:, :, None], ffn_scores[None], 0.0), axis=1)
    token_count = jnp.sum(lengths).astype(F32)
    positions = piece * tokens + jnp.arange(tokens)
    valid_mask = positions[None, :] < seq_lengths[:, None]
    a_hot, a_spots = routing(attn_pick, pieces, tokens)
    f_hot, f_spots = routing(ffn_pick, pieces, tokens)
    a_select = lax.dynamic_index_in_dim(a_hot, piece, 1, False).astype(BF)
    f_select = lax.dynamic_index_in_dim(f_hot, piece, 1, False).astype(BF)
    a_spot = lax.dynamic_index_in_dim(a_spots, piece, 1, False)
    f_spot = lax.dynamic_index_in_dim(f_spots, piece, 1, False)
    slot_score = jnp.sum(
        jnp.where(f_spot[:, :, None] == ffn_pick[:, None, :], score_pick[:, None, :], 0.0), axis=-1
    )
    width_light = HL * DH
    width_heavy = HH * DH
    normed = rms_norm(inputs, gain_one).astype(BF)
    light_proj = mul(normed, w_lqkv).astype(BF)
    l_query = light_proj[..., :width_light]
    own_pair = light_proj[..., width_light:]
    a_rows = jnp.einsum("scp,spd->scd", a_select, normed, preferred_element_type=F32).astype(BF)
    heavy_proj = mul(a_rows, w_hqkv).astype(BF)
    h_query = heavy_proj[..., :width_heavy]
    from_left, from_right, kv_every = exchange_keys(
        own_pair[:, :WIN], own_pair[:, tokens - WIN :], heavy_proj[..., width_heavy:]
    )
    rim_pair = jnp.concatenate([from_left, own_pair, from_right], axis=1)
    rim_keys = rim_pair[..., :width_light]
    rim_values = rim_pair[..., width_light:]
    key_pos = piece * tokens - WIN + jnp.arange(tokens + 2 * WIN)
    within_reach = (jnp.abs(positions[:, None] - key_pos[None, :]) <= WIN) & (key_pos >= 0)[None, :]
    live_key = key_pos[None, :] < seq_lengths[:, None]
    light_allowed = within_reach[None] & (
        live_key[:, None, :] | (positions[:, None] == key_pos[None, :])[None]
    )
    l_att, l_lse = attend_forward(l_query, rim_keys, rim_values, light_allowed, HL)
    light_branch = mul(l_att, w_lout)
    kv_every = kv_every.reshape(group, pieces * CAP, 2 * width_heavy)
    all_spots = a_spots.reshape(group, pieces * CAP)
    heavy_allowed = ((all_spots >= 0) & (all_spots < seq_lengths[:, None]))[:, None, :] | (
        a_spot[:, :, None] == all_spots[:, None, :]
    )
    hv_keys = kv_every[..., :width_heavy]
    hv_values = kv_every[..., width_heavy:]
    h_att, h_lse = attend_forward(h_query, hv_keys, hv_values, heavy_allowed, HH)
    heavy_branch = mul(h_att, w_hout)
    hidden = inputs + light_branch + pick("scp,scd->spd", a_select, heavy_branch)
    weight_mask = valid_mask.reshape(-1, 1).astype(F32)
    grad_lin, grad_ldown, grad_hin, grad_hdown, d_hidden, ffn_stats = feed_forward(
        hidden.reshape(-1, D),
        f_select,
        f_select.swapaxes(1, 2),
        slot_score.reshape(-1, 1),
        gain_two.reshape(1, D),
        teacher.reshape(-1, D),
        weight_mask,
        2.0 * weight_mask / (D * token_count),
        w_lin,
        w_ldown,
        w_hin,
        w_hdown,
    )
    d_hidden = d_hidden.reshape(group, tokens, D)
    d_heavy_attn = pick("scp,spd->scd", a_select, d_hidden).astype(BF)
    grad_hout = weight_grad(h_att, d_heavy_attn)
    d_h_att = mul_back(d_heavy_attn, w_hout).astype(BF)
    dq_heavy, dk_heavy, dv_heavy = attend_backward(
        h_query, hv_keys, hv_values, heavy_allowed, h_lse, d_h_att, HH
    )
    kv_part = jnp.concatenate([dk_heavy, dv_heavy], axis=-1).astype(BF)
    d_light_attn = d_hidden.astype(BF)
    grad_lout = weight_grad(l_att, d_light_attn)
    d_l_att = mul_back(d_light_attn, w_lout).astype(BF)
    dq_light, dk_light, dv_light = attend_backward(
        l_query, rim_keys, rim_values, light_allowed, l_lse, d_l_att, HL
    )
    rim_grads = jnp.concatenate([dk_light, dv_light], axis=-1)
    back_left, back_right, kv_grads = exchange_key_grads(
        rim_grads[:, :WIN].astype(BF),
        rim_grads[:, tokens + WIN :].astype(BF),
        kv_part.reshape(group, pieces, CAP, 2 * width_heavy),
    )
    d_h_proj = jnp.concatenate([dq_heavy.astype(BF), kv_grads.astype(BF)], axis=-1)
    grad_hqkv = weight_grad(a_rows, d_h_proj)
    d_a_rows = mul_back(d_h_proj, w_hqkv)
    own_grads = rim_grads[:, WIN : WIN + tokens]
    own_grads = jnp.concatenate(
        [
            own_grads[:, :WIN] + back_left.astype(F32),
            own_grads[:, WIN : tokens - WIN],
            own_grads[:, tokens - WIN :] + back_right.astype(F32),
        ],
        axis=1,
    )
    d_l_proj = jnp.concatenate([dq_light.astype(BF), own_grads.astype(BF)], axis=-1)
    grad_lqkv = weight_grad(normed, d_l_proj)
    d_normed = pick("scp,scd->spd", a_select, d_a_rows) + mul_back(d_l_proj, w_lqkv)
    _, first_pull = jax.vjp(rms_norm, inputs, gain_one)
    d_inputs_norm, grad_gain_one = first_pull(d_normed)
    d_inputs = d_hidden + d_inputs_norm
    rows = tokens // dp
    stats = jnp.concatenate(
        [
            grad_gain_one.reshape(-1, 128),
            ffn_stats[0].reshape(-1, 128),
            jnp.broadcast_to(jnp.sum(ffn_stats[1]), (4, 128)),
        ]
    )
    grads = (grad_lin, grad_ldown, grad_hout, grad_lout, grad_hqkv, grad_lqkv)
    shards = (light_in, light_down, heavy_out, light_out, heavy_qkv, light_qkv)
    sent = [
        packed_full(grad.astype(BF), shard.shape, nz) for grad, shard in zip(grads, shards)
    ]
    hin_tile = hin_src.shape[1:]
    done = scatter_all(
        dp,
        d_inputs.astype(BF).reshape(group, dp, rows, D),
        stats,
        sent,
        grad_hin.astype(BF).reshape((nz, 8) + hin_tile),
        grad_hdown.astype(BF).reshape(nz, -1, D),
    )
    d_layer = undeal_rows(dealing, done[0].reshape(seqs, rows, D))[:, None]
    summed = done[1]
    mine = data_index * pieces + piece
    loss_value = summed[12, 0] / (D * token_count)
    own_one = lax.dynamic_slice_in_dim(summed[:6].reshape(-1), mine * gain_len, gain_len)
    own_two = lax.dynamic_slice_in_dim(summed[6:12].reshape(-1), mine * gain_len, gain_len)
    g_lin, g_ldown, g_hout, g_lout, g_hqkv, g_lqkv = (
        full.reshape(shard.shape) for full, shard in zip(done[2:8], shards)
    )
    g_hin = (
        done[8]
        .astype(F32)
        .reshape(8, hin_rows, 2, nz, hidden_units)
        .transpose(1, 2, 3, 0, 4)
        .reshape(heavy_in.shape)
    )
    return (
        loss_value,
        d_layer,
        own_one,
        own_two,
        g_lqkv,
        g_lout,
        g_hqkv,
        g_hout,
        g_lin,
        g_ldown,
        g_hin,
        done[9].reshape(heavy_down.shape),
    )


def packed_full(grad, shard_shape, nz):
    rows, columns = shard_shape
    if rows % 8 == 0:
        return grad.reshape(nz, 2, 2, 2, rows, columns)
    return grad.reshape(nz, 2, 2, 2, rows * columns // 128, 128)


def solution(mesh):
    split = P(("dp", "fsdp"))
    matrix = P(("dp", "fsdp"), None)
    placed = (
        P(None, "fsdp", "dp", None),
        P("dp", "fsdp", None, None),
        P(),
        P(),
        P(),
        P(),
        P(),
        split,
        split,
    ) + (matrix,) * 8
    return jax.shard_map(
        local,
        mesh=mesh,
        in_specs=placed,
        out_specs=(P(), P(None, "fsdp", "dp", None), split, split) + (matrix,) * 8,
        check_vma=False,
    )
```

```python
import functools
import jax
import jax.numpy as jnp
from jax import lax
from jax.experimental import pallas as pl
from jax.experimental.pallas import tpu as pltpu
from jax.sharding import PartitionSpec as P

D = 768
HL = 8
HH = 12
DH = 64
FL = 1024
FH = 4096
WIN = 128
CAP = 64

EPSILON = 1e-06
MASKED = -1000000000.0
SCORE_SCALE = 0.125
MESH = pl.DeviceIdType.MESH
BF = jnp.bfloat16
F32 = jnp.float32
ANY = pl.BlockSpec(memory_space=pl.ANY)
VM = pl.BlockSpec(memory_space=pltpu.VMEM)
DMA = pltpu.SemaphoreType.DMA
VMEM_BYTES = 60 * 1024 * 1024


def place():
    d = lax.axis_index("dp")
    f = lax.axis_index("fsdp")
    return d // 2, d % 2, f // 2, f % 2


def at(hi, lo, x, c):
    return (hi * 2 + lo, x * 2 + c)


def meet(peers):
    barrier = pltpu.get_barrier_semaphore()
    for peer in peers:
        pl.semaphore_signal(barrier, inc=1, device_id=peer, device_id_type=MESH)
    pl.semaphore_wait(barrier, len(peers))


def send(src, dst, send_sem, recv_sem, peer):
    copy = pltpu.make_async_remote_copy(
        src_ref=src,
        dst_ref=dst,
        send_sem=send_sem,
        recv_sem=recv_sem,
        device_id=peer,
        device_id_type=MESH,
    )
    copy.start()
    return copy


def keep(src, dst, sem):
    copy = pltpu.make_async_copy(src, dst, sem)
    copy.start()
    return copy


def quad_peers():
    hi, lo, x, c = place()
    return [(lo, 1 - x), (1 - lo, x), (1 - lo, 1 - x)]


def call(kernel, out_shape, operands, in_specs, out_specs, scratch, collective_id):
    return pl.pallas_call(
        kernel,
        out_shape=out_shape,
        in_specs=in_specs,
        out_specs=out_specs,
        scratch_shapes=scratch,
        compiler_params=pltpu.CompilerParams(
            collective_id=collective_id, has_side_effects=True, vmem_limit_bytes=VMEM_BYTES
        ),
    )(*operands)


def deal_kernel(deal_ref, x_ref, o_ref):
    def body(i, carry):
        o_ref[i] = x_ref[deal_ref[i]]
        return carry

    lax.fori_loop(0, o_ref.shape[0], body, 0)


def deal_rows(dealing, rows):
    return pl.pallas_call(
        deal_kernel,
        out_shape=jax.ShapeDtypeStruct(rows.shape, rows.dtype),
        in_specs=[pl.BlockSpec(memory_space=pltpu.SMEM), VM],
        out_specs=VM,
        compiler_params=pltpu.CompilerParams(vmem_limit_bytes=VMEM_BYTES),
    )(dealing, rows)


def undeal_kernel(deal_ref, x_ref, o_ref):
    def body(i, carry):
        o_ref[deal_ref[i]] = x_ref[i].astype(F32)
        return carry

    lax.fori_loop(0, x_ref.shape[0], body, 0)


def undeal_rows(dealing, rows):
    return pl.pallas_call(
        undeal_kernel,
        out_shape=jax.ShapeDtypeStruct(rows.shape, F32),
        in_specs=[pl.BlockSpec(memory_space=pltpu.SMEM), VM],
        out_specs=VM,
        compiler_params=pltpu.CompilerParams(vmem_limit_bytes=VMEM_BYTES),
    )(dealing, rows)


def packed(matrix):
    rows, columns = matrix.shape
    if rows % 8 == 0:
        return matrix
    return matrix.reshape(rows * columns // 128, 128)


def unpacked(gathered, rows, columns):
    return gathered.reshape(-1, rows, columns).reshape(-1, columns)


def gather_kernel(dp, nw, *refs):
    nz = dp // 2
    xin, ws, hin, hdn = refs[0], refs[1 : 1 + nw], refs[1 + nw], refs[2 + nw]
    outs = refs[3 + nw :]
    xo, wos, hin_o, hdn_o = outs[0], outs[1 : 1 + nw], outs[1 + nw], outs[2 + nw]
    loc, xs, xr, zs, zr, ps, pr, cs, cr, hs, hr = outs[3 + nw :]
    hi, lo, x, c = place()
    d = hi * 2 + lo
    f = x * 2 + c
    plane = (lo * 2 + x) * 2 + c
    group = xin.shape[0] // dp
    dp_peers = [(lax.rem(d + k, dp), f) for k in range(1, dp)]
    rest = [(a, b, e) for a in (0, 1) for b in (0, 1) for e in (0, 1) if a or b or e]
    flat8 = []
    for a, b, e in rest:
        l2 = 1 - lo if a else lo
        x2 = 1 - x if b else x
        c2 = 1 - c if e else c
        flat8.append((l2, x2, c2))
    meet(dp_peers + [at(hi, *p) for (a, b, e), p in zip(rest, flat8) if b or e])
    locals_ = [keep(ws[w], wos[w].at[hi, lo, x, c], loc.at[w]) for w in range(nw)]
    locals_.append(keep(xin.at[pl.ds(d * group, group)], xo.at[:, d], loc.at[nw]))
    locals_.append(keep(hin.at[plane], hin_o.at[hi, plane], loc.at[nw + 1]))
    locals_.append(keep(hdn, hdn_o.at[hi], loc.at[nw + 2]))
    x_sends = []
    for k, peer in enumerate(dp_peers):
        x_sends.append(
            send(xin.at[pl.ds(peer[0] * group, group)], xo.at[:, d], xs.at[k], xr.at[k], peer)
        )
    z_peers = [at(lax.rem(hi + k, nz), lo, x, c) for k in range(1, nz)]
    z_sends = [
        [
            send(ws[w], wos[w].at[hi, lo, x, c], zs.at[w, k], zr.at[w, k], peer)
            for k, peer in enumerate(z_peers)
        ]
        for w in range(nw)
    ]
    h_sends = []
    for k, (l2, x2, c2) in enumerate(flat8):
        h_sends.append(
            send(
                hin.at[(l2 * 2 + x2) * 2 + c2],
                hin_o.at[hi, plane],
                hs.at[0, k],
                hr.at[0, k],
                at(hi, l2, x2, c2),
            )
        )
    quad = quad_peers()
    partner = at(hi, lo, x, 1 - c)
    p_sends, c_sends = [], []

    def forward_plane(w):
        locals_[w].wait()
        for copy in z_sends[w]:
            copy.wait()
        column = wos[w].at[:, lo, x, c]
        p_sends.append(
            [
                send(column, column, ps.at[w, k], pr.at[w, k], at(hi, l2, x2, c))
                for k, (l2, x2) in enumerate(quad)
            ]
        )
        c_sends.append([send(column, column, cs.at[w, 0], cr.at[w, 0], partner)])

    def forward_core(w):
        for k, (l2, x2) in enumerate(quad):
            p_sends[w][k].wait()
            column = wos[w].at[:, l2, x2, c]
            c_sends[w].append(send(column, column, cs.at[w, k + 1], cr.at[w, k + 1], partner))

    for w in range(nw):
        forward_plane(w)
        if w >= 1:
            forward_core(w - 1)
    for copy in h_sends:
        copy.wait()
    locals_[nw + 1].wait()
    late = []
    for k, peer in enumerate(z_peers):
        late.append(send(hin_o.at[hi], hin_o.at[hi], hs.at[1, k], hr.at[1, k], peer))
        late.append(send(hdn, hdn_o.at[hi], hs.at[2, k], hr.at[2, k], peer))
    forward_core(nw - 1)
    locals_[nw].wait()
    locals_[nw + 2].wait()
    for copy in x_sends + late:
        copy.wait()
    for copies in c_sends:
        for copy in copies:
            copy.wait()


def gather_all(dp, xin, weights, hin, hdn):
    nz = dp // 2
    nw = len(weights)
    seqs, rows, _ = xin.shape
    shapes = [jax.ShapeDtypeStruct((seqs // dp, dp, rows, D), BF)]
    shapes += [jax.ShapeDtypeStruct((nz, 2, 2, 2) + w.shape, BF) for w in weights]
    shapes.append(jax.ShapeDtypeStruct((nz,) + hin.shape, BF))
    shapes.append(jax.ShapeDtypeStruct((nz,) + hdn.shape, BF))
    most = max(7, nz)
    scratch = [
        DMA((nw + 3,)),
        DMA((dp,)),
        DMA((dp,)),
        DMA((nw, nz)),
        DMA((nw, nz)),
        DMA((nw, 3)),
        DMA((nw, 3)),
        DMA((nw, 4)),
        DMA((nw, 4)),
        DMA((3, most)),
        DMA((3, most)),
    ]
    return call(
        functools.partial(gather_kernel, dp, nw),
        shapes,
        [xin, *weights, hin, hdn],
        [ANY] * (3 + nw),
        [ANY] * (3 + nw),
        scratch,
        1,
    )


def rim_exchange(left, right, from_left, from_right, ls, lr, rs, rr):
    d = lax.axis_index("dp")
    f = lax.axis_index("fsdp")
    last = lax.axis_size("fsdp") - 1

    def down():
        return pltpu.make_async_remote_copy(
            src_ref=left,
            dst_ref=from_right,
            send_sem=ls,
            recv_sem=lr,
            device_id=(d, lax.max(f - 1, 0)),
            device_id_type=MESH,
        )

    def up():
        return pltpu.make_async_remote_copy(
            src_ref=right,
            dst_ref=from_left,
            send_sem=rs,
            recv_sem=rr,
            device_id=(d, lax.min(f + 1, last)),
            device_id_type=MESH,
        )

    @pl.when(f > 0)
    def _():
        down().start()

    @pl.when(f < last)
    def _():
        up().start()

    @pl.when(f == 0)
    def _():
        from_left[...] = jnp.zeros(from_left.shape, from_left.dtype)

    @pl.when(f == last)
    def _():
        from_right[...] = jnp.zeros(from_right.shape, from_right.dtype)

    def finish():
        @pl.when(f > 0)
        def _():
            down().wait_send()
            up().wait_recv()

        @pl.when(f < last)
        def _():
            up().wait_send()
            down().wait_recv()

    return finish


def line_peers():
    hi, lo, x, c = place()
    return [at(hi, lo, x, 1 - c), at(hi, lo, 1 - x, c), at(hi, lo, 1 - x, 1 - c)]


def dot(left, right):
    return jnp.dot(left, right, preferred_element_type=F32)


def dot_back(left, right):
    return lax.dot_general(left, right, (((1,), (1,)), ((), ())), preferred_element_type=F32)


def dot_grad(left, right):
    return lax.dot_general(left, right, (((0,), (0,)), ((), ())), preferred_element_type=F32)


def halves(value):
    high = value.astype(BF)
    return high, (value - high.astype(F32)).astype(BF)


def tiles(extent, step, body):
    def run(i, carry):
        body(pl.ds(pl.multiple_of(i * step, step), step))
        return carry

    lax.fori_loop(0, extent // step, run, 0)


GELU_A = 0.7978845608028654
GELU_B = 0.044715


def gelu_parts(v):
    square = v * v
    t = jnp.tanh(GELU_A * v * (1.0 + GELU_B * square))
    value = 0.5 * v * (1.0 + t)
    slope = 0.5 * (1.0 + t) + 0.5 * v * (1.0 - t * t) * GELU_A * (1.0 + 3.0 * GELU_B * square)
    return value, slope


def gelu_value(v):
    return 0.5 * v * (1.0 + jnp.tanh(GELU_A * v * (1.0 + GELU_B * v * v)))


def ffn_kernel(
    hidden,
    select,
    select_t,
    score,
    gain,
    teach,
    mask,
    scale,
    w_in,
    w_dn,
    w_hin,
    w_hdn,
    g_in,
    g_dn,
    g_hin,
    g_hdn,
    d_hidden,
    stats,
    hn,
    every,
    d_every,
    up_l,
    z,
    up_h,
    zh,
    part,
    near,
    far,
    near2,
    far2,
    out,
    dl,
    dup_l,
    dup_h,
    dhn,
    ps,
    pr,
    cs,
    cr,
    qs,
    qr,
    es,
    er,
):
    hi, lo, x, c = place()
    quad = quad_peers()
    partner = at(hi, lo, x, 1 - c)
    spots = [l2 * 2 + x2 for l2, x2 in quad]
    home = lo * 2 + x
    tokens = hidden.shape[0]
    group, cap, width = select.shape
    fl = z.shape[1]
    fh = zh.shape[2]
    rows_h = part.shape[1] * part.shape[2]
    meet([at(hi, l2, x2, c) for l2, x2 in quad] + [partner])

    def spread(buffer, i):
        spot = buffer.at[c, home]
        there = [
            send(spot, spot, ps.at[i, k], pr.at[i, k], at(hi, l2, x2, c))
            for k, (l2, x2) in enumerate(quad)
        ]
        return there, [send(spot, spot, cs.at[i, 3], cr.at[i, 3], partner)]

    def relay(buffer, i, there, back):
        for k, q in enumerate(spots):
            there[k].wait()
            other = buffer.at[c, q]
            back.append(send(other, other, cs.at[i, k], cr.at[i, k], partner))

    def fold(near_ref, far_ref, i, copy):
        copy.wait()
        there = []
        for k, q in enumerate(spots):
            near_ref[q] = (near_ref[q].astype(F32) + part[c, q].astype(F32)).astype(BF)
            l2, x2 = quad[k]
            there.append(
                send(near_ref.at[q], far_ref.at[k], qs.at[i, k], qr.at[i, k], at(hi, l2, x2, c))
            )
        return there

    def folded(near_ref, far_ref, there):
        for copy in there:
            copy.wait()
        return (
            near_ref[home].astype(F32)
            + part[c, home].astype(F32)
            + far_ref[0].astype(F32)
            + far_ref[1].astype(F32)
            + far_ref[2].astype(F32)
        )

    def norm(r):
        h = hidden[r, :]
        inv = lax.rsqrt(jnp.mean(h * h, axis=-1, keepdims=True) + EPSILON)
        hn[r, :] = (h * inv * gain[...]).astype(BF)

    tiles(tokens, 128, norm)
    for s in range(group):
        every[c, home, s * cap : (s + 1) * cap, :] = dot(
            select[s], hn[s * width : (s + 1) * width, :]
        ).astype(BF)
    there, back = spread(every, 0)

    def light_up(r):
        up_l[r, :] = dot(hn[r, :], w_in[...])
        z[r, :] = (gelu_value(up_l[r, :fl]) * up_l[r, fl:]).astype(BF)

    tiles(tokens, 256, light_up)
    relay(every, 0, there, back)

    def light_down(r):
        out[r, :] = hidden[r, :] + dot(z[r, :], w_dn[...])

    tiles(tokens, 256, light_down)
    for copy in back:
        copy.wait()

    def heavy(e):
        def up(i, carry):
            a = every[e, pl.ds(2 * i, 2)].reshape(2 * group * cap, D)
            r = pl.ds(pl.multiple_of(i * 256, 256), 256)
            up_h[e, r, :] = dot(a, w_hin[...])
            zh[e, r, :] = (gelu_value(up_h[e, r, :fh]) * up_h[e, r, fh:]).astype(BF)
            v = dot(zh[e, r, :], w_hdn[...]).astype(BF)
            part[e, pl.ds(2 * i, 2)] = v.reshape(2, group * cap, D)
            return carry

        lax.fori_loop(0, 2, up, 0)

    heavy(1 - c)
    first = send(part.at[1 - c], near, es.at[0], er.at[0], partner)
    heavy(c)
    there = fold(near, far, 0, first)
    hf = folded(near, far, there) * score[...]
    hf_high, hf_low = halves(hf)
    for s in range(group):
        r = slice(s * width, (s + 1) * width)
        q = slice(s * cap, (s + 1) * cap)
        out[r, :] += dot(select_t[s], hf_high[q]) + dot(select_t[s], hf_low[q])
    stats[...] = jnp.zeros(stats.shape, F32)

    def misfit(r):
        m = out[r, :] - teach[r, :].astype(F32)
        stats[1:2, :] += jnp.sum(mask[r, :] * m * m, axis=0, keepdims=True)
        d = scale[r, :] * m
        out[r, :] = d
        dl[r, :] = d.astype(BF)

    tiles(tokens, 128, misfit)
    for s in range(group):
        high, low = halves(out[s * width : (s + 1) * width, :])
        picked = dot(select[s], high) + dot(select[s], low)
        q = slice(s * cap, (s + 1) * cap)
        d_every[c, home, q, :] = (picked * score[q, :]).astype(BF)
    there, back = spread(d_every, 1)

    def light_back(r):
        dz = dot_back(dl[r, :], w_dn[...])
        value, slope = gelu_parts(up_l[r, :fl])
        dup_l[r, :fl] = (dz * up_l[r, fl:] * slope).astype(BF)
        dup_l[r, fl:] = (dz * value).astype(BF)

    tiles(tokens, 256, light_back)
    relay(d_every, 1, there, back)

    def light_grad(j):
        g_dn[j, :] = dot_grad(z[:, j], dl[...]).astype(BF)

    tiles(fl, 512, light_grad)
    for copy in back:
        copy.wait()

    def heavy_back(e):
        def run(i, carry):
            d = d_every[e, pl.ds(2 * i, 2)].reshape(2 * group * cap, D)
            r = pl.ds(pl.multiple_of(i * 256, 256), 256)
            dz = dot_back(d, w_hdn[...])
            value, slope = gelu_parts(up_h[e, r, :fh])
            dup_h[e, r, :fh] = (dz * up_h[e, r, fh:] * slope).astype(BF)
            dup_h[e, r, fh:] = (dz * value).astype(BF)
            v = dot_back(dup_h[e, r, :], w_hin[...]).astype(BF)
            part[e, pl.ds(2 * i, 2)] = v.reshape(2, group * cap, D)
            return carry

        lax.fori_loop(0, 2, run, 0)

    heavy_back(1 - c)
    second = send(part.at[1 - c], near2, es.at[1], er.at[1], partner)
    heavy_back(c)
    there = fold(near2, far2, 1, second)

    def light_in_grad(j):
        g_in[:, j] = dot_grad(hn[...], dup_l[:, j]).astype(BF)

    tiles(2 * fl, 1024, light_in_grad)

    def light_in_back(r):
        dhn[r, :] = dot_back(dup_l[r, :], w_in[...])

    tiles(tokens, 256, light_in_back)
    every_rows = every[...].reshape(2 * rows_h, D)

    def heavy_grad(j):
        g_hin[:, j] = dot_grad(every_rows, dup_h[:, :, j].reshape(2 * rows_h, 512)).astype(BF)

    tiles(2 * fh, 512, heavy_grad)
    d_rows = d_every[...].reshape(2 * rows_h, D)

    def heavy_down_grad(j):
        g_hdn[j, :] = dot_grad(zh[:, :, j].reshape(2 * rows_h, 512), d_rows).astype(BF)

    tiles(fh, 512, heavy_down_grad)
    d_high, d_low = halves(folded(near2, far2, there))
    for s in range(group):
        r = slice(s * width, (s + 1) * width)
        q = slice(s * cap, (s + 1) * cap)
        dhn[r, :] += dot(select_t[s], d_high[q]) + dot(select_t[s], d_low[q])

    def norm_back(r):
        h = hidden[r, :]
        inv = lax.rsqrt(jnp.mean(h * h, axis=-1, keepdims=True) + EPSILON)
        d = dhn[r, :]
        dh = d * h
        stats[0:1, :] += jnp.sum(dh * inv, axis=0, keepdims=True)
        mean = jnp.mean(gain[...] * dh, axis=-1, keepdims=True)
        d_hidden[r, :] = out[r, :] + inv * gain[...] * d - h * (inv * inv * inv * mean)

    tiles(tokens, 128, norm_back)


def feed_forward(hidden, select, select_t, score, gain, teach, mask, scale, w_in, w_dn, w_hin, w_hdn):
    tokens = hidden.shape[0]
    group, cap, _ = select.shape
    rows = group * cap
    fl, fh = w_dn.shape[0], w_hdn.shape[0]
    block = (2, 4, rows, D)
    operands = [hidden, select, select_t, score, gain, teach, mask, scale, w_in, w_dn, w_hin, w_hdn]
    return call(
        ffn_kernel,
        [
            jax.ShapeDtypeStruct((D, 2 * fl), BF),
            jax.ShapeDtypeStruct((fl, D), BF),
            jax.ShapeDtypeStruct((D, 2 * fh), BF),
            jax.ShapeDtypeStruct((fh, D), BF),
            jax.ShapeDtypeStruct((tokens, D), F32),
            jax.ShapeDtypeStruct((8, D), F32),
        ],
        operands,
        [VM] * len(operands),
        [VM] * 6,
        [
            pltpu.VMEM((tokens, D), BF),
            pltpu.VMEM(block, BF),
            pltpu.VMEM(block, BF),
            pltpu.VMEM((tokens, 2 * fl), F32),
            pltpu.VMEM((tokens, fl), BF),
            pltpu.VMEM((2, 4 * rows, 2 * fh), F32),
            pltpu.VMEM((2, 4 * rows, fh), BF),
            pltpu.VMEM(block, BF),
            pltpu.VMEM(block[1:], BF),
            pltpu.VMEM((3, rows, D), BF),
            pltpu.VMEM(block[1:], BF),
            pltpu.VMEM((3, rows, D), BF),
            pltpu.VMEM((tokens, D), F32),
            pltpu.VMEM((tokens, D), BF),
            pltpu.VMEM((tokens, 2 * fl), BF),
            pltpu.VMEM((2, 4 * rows, 2 * fh), BF),
            pltpu.VMEM((tokens, D), F32),
            DMA((2, 3)),
            DMA((2, 3)),
            DMA((2, 4)),
            DMA((2, 4)),
            DMA((2, 3)),
            DMA((2, 3)),
            DMA((2,)),
            DMA((2,)),
        ],
        5,
    )


def pair_masks(scale):
    lane = lax.broadcasted_iota(jnp.int32, (1, 2 * DH), 1)
    left = jnp.where(lane < DH, scale, 0.0).astype(BF)
    right = jnp.where(lane < DH, 0.0, scale).astype(BF)
    return left, right


def both(value, masks):
    return jnp.concatenate([value * masks[0], value * masks[1]], axis=0)


def side(stacked):
    rows = stacked.shape[0] // 2
    return jnp.concatenate([stacked[:rows], stacked[rows:]], axis=1)


def pair_forward(q, k, v, bias, ones, scaled):
    scores = dot_back(both(q, scaled), k) + bias
    top = jnp.max(scores, axis=-1, keepdims=True)
    shifted = jnp.exp(scores - top)
    total = jnp.sum(shifted, axis=-1, keepdims=True)
    prob = (shifted / total).astype(BF)
    return dot(side(prob), both(v, ones)).astype(BF), top + jnp.log(total)


def pair_backward(q, k, v, bias, lse, d_out, ones, scaled):
    q2 = both(q, scaled)
    d2 = both(d_out, ones)
    prob = jnp.exp(dot_back(q2, k) + bias - lse)
    d_prob = dot_back(d2, v)
    row = jnp.sum(prob * d_prob, axis=-1, keepdims=True)
    d_scores = (prob * (d_prob - row)).astype(BF)
    dq = dot(side(d_scores), both(k, scaled))
    return dq, dot_grad(d_scores, q2), dot_grad(prob.astype(BF), d2)


def reach_bias(key_bias):
    shape = (WIN, 3 * WIN)
    offset = lax.broadcasted_iota(jnp.int32, shape, 1) - lax.broadcasted_iota(jnp.int32, shape, 0) - WIN
    near = (offset >= -WIN) & (offset <= WIN)
    inner = jnp.where(offset == 0, 0.0, jnp.broadcast_to(key_bias, shape))
    bias = jnp.where(near, inner, MASKED)
    return jnp.concatenate([bias, bias], axis=0)


def put_lse(lse, pair, column):
    lane = lax.broadcasted_iota(jnp.int32, lse.shape, 1)
    rows = lse.shape[0]
    lse = jnp.where(lane == 2 * pair, column[:rows], lse)
    return jnp.where(lane == 2 * pair + 1, column[rows:], lse)


def get_lse(lse, pair):
    return jnp.concatenate([lse[:, 2 * pair : 2 * pair + 1], lse[:, 2 * pair + 1 : 2 * pair + 2]], axis=0)


def attend_kernel(
    x,
    gain,
    select,
    select_t,
    key_bias,
    heavy_bias,
    w_lqkv,
    w_hqkv,
    w_lout,
    w_hout,
    hidden,
    xn,
    lq,
    rim,
    lo_out,
    l_lse,
    a_rows,
    hq,
    kvh,
    ho,
    h_lse,
    ls,
    lr,
    rs,
    rr,
    ss,
    sr,
):
    hi, lo, x_, c = place()
    f = x_ * 2 + c
    meet(line_peers())
    tokens = x.shape[0]
    group, cap, width = select.shape
    wl, wh = HL * DH, HH * DH
    ones, scaled = pair_masks(1.0), pair_masks(SCORE_SCALE)
    across, partner = at(hi, lo, 1 - x_, c), at(hi, lo, x_, 1 - c)

    def norm(r):
        h = x[r, :].astype(F32)
        inv = lax.rsqrt(jnp.mean(h * h, axis=-1, keepdims=True) + EPSILON)
        xn[r, :] = (h * inv * gain[...]).astype(BF)

    tiles(tokens, 128, norm)
    for s in range(group):
        rows = dot(select[s], xn[s * width : (s + 1) * width, :]).astype(BF)
        a_rows[s * cap : (s + 1) * cap, :] = rows
    kv = dot(a_rows[...], w_hqkv[:, wh:]).astype(BF)
    for s in range(group):
        kvh[s, f] = kv[s * cap : (s + 1) * cap]
    mine = kvh.at[:, f]
    first = send(mine, mine, ss.at[0], sr.at[0], across)
    beside = send(mine, mine, ss.at[1], sr.at[1], partner)
    for s in range(group):
        rows = xn[s * width : (s + 1) * width, :]
        rim[s, WIN : WIN + width, :] = dot(rows, w_lqkv[:, wl:]).astype(BF)
    finish = rim_exchange(
        rim.at[:, pl.ds(WIN, WIN)],
        rim.at[:, pl.ds(width, WIN)],
        rim.at[:, pl.ds(0, WIN)],
        rim.at[:, pl.ds(width + WIN, WIN)],
        ls,
        lr,
        rs,
        rr,
    )
    hq[...] = dot(a_rows[...], w_hqkv[:, :wh]).astype(BF)
    for s in range(group):
        rows = slice(s * width, (s + 1) * width)
        lq[rows, :] = dot(xn[rows, :], w_lqkv[:, :wl]).astype(BF)
    first.wait()
    other = kvh.at[:, (1 - x_) * 2 + c]
    relay = send(other, other, ss.at[2], sr.at[2], partner)
    finish()
    blocks = width // WIN

    def light(i, carry):
        s, b = i // blocks, i % blocks
        r = pl.ds(pl.multiple_of(i * WIN, WIN), WIN)
        keys = pl.ds(pl.multiple_of(b * WIN, WIN), 3 * WIN)
        bias = reach_bias(key_bias[i])
        lse = jnp.zeros((WIN, 128), F32)
        for pair in range(HL // 2):
            at_k = slice(pair * 128, (pair + 1) * 128)
            at_v = slice(wl + pair * 128, wl + (pair + 1) * 128)
            o, column = pair_forward(
                lq[r, at_k], rim[s, keys, at_k], rim[s, keys, at_v], bias, ones, scaled
            )
            lo_out[r, at_k] = o
            lse = put_lse(lse, pair, column)
        l_lse[r, :] = lse
        return carry

    lax.fori_loop(0, group * blocks, light, 0)
    beside.wait()
    relay.wait()
    heavy_kv = kvh.reshape(group, 4 * cap, 2 * wh)

    def heavy(s, carry):
        r = pl.ds(pl.multiple_of(s * cap, cap), cap)
        bias = heavy_bias[s]
        bias = jnp.concatenate([bias, bias], axis=0)
        lse = jnp.zeros((cap, 128), F32)
        for pair in range(HH // 2):
            at_k = slice(pair * 128, (pair + 1) * 128)
            at_v = slice(wh + pair * 128, wh + (pair + 1) * 128)
            o, column = pair_forward(
                hq[r, at_k], heavy_kv[s, :, at_k], heavy_kv[s, :, at_v], bias, ones, scaled
            )
            ho[r, at_k] = o
            lse = put_lse(lse, pair, column)
        h_lse[r, :] = lse
        return carry

    lax.fori_loop(0, group, heavy, 0)
    high, low = halves(dot(ho[...], w_hout[...]))
    for s in range(group):
        r = slice(s * width, (s + 1) * width)
        q = slice(s * cap, (s + 1) * cap)
        hidden[r, :] = (
            x[r, :].astype(F32)
            + dot(lo_out[r, :], w_lout[...])
            + (dot(select_t[s], high[q]) + dot(select_t[s], low[q]))
        )


def attend(x, gain, select, select_t, key_bias, heavy_bias, w_lqkv, w_hqkv, w_lout, w_hout):
    tokens = x.shape[0]
    group, cap, width = select.shape
    wl, wh = HL * DH, HH * DH
    rows = group * cap
    operands = [x, gain, select, select_t, key_bias, heavy_bias, w_lqkv, w_hqkv, w_lout, w_hout]
    shapes = [
        jax.ShapeDtypeStruct((tokens, D), F32),
        jax.ShapeDtypeStruct((tokens, D), BF),
        jax.ShapeDtypeStruct((tokens, wl), BF),
        jax.ShapeDtypeStruct((group, width + 2 * WIN, 2 * wl), BF),
        jax.ShapeDtypeStruct((tokens, wl), BF),
        jax.ShapeDtypeStruct((tokens, 128), F32),
        jax.ShapeDtypeStruct((rows, D), BF),
        jax.ShapeDtypeStruct((rows, wh), BF),
        jax.ShapeDtypeStruct((group, 4, cap, 2 * wh), BF),
        jax.ShapeDtypeStruct((rows, wh), BF),
        jax.ShapeDtypeStruct((rows, 128), F32),
    ]
    return call(
        attend_kernel,
        shapes,
        operands,
        [VM] * len(operands),
        [VM] * len(shapes),
        [DMA, DMA, DMA, DMA, DMA((3,)), DMA((3,))],
        2,
    )


def attend_back_kernel(
    d_hidden,
    x,
    gain,
    select,
    select_t,
    key_bias,
    heavy_bias,
    w_lqkv,
    w_hqkv,
    w_lout,
    w_hout,
    xn,
    lq,
    rim,
    lo_out,
    l_lse,
    a_rows,
    hq,
    kvh,
    ho,
    h_lse,
    g_lqkv,
    g_hqkv,
    g_lout,
    g_hout,
    dx,
    stats,
    d_ho,
    d_hproj,
    part,
    got,
    far,
    d_la,
    d_lo,
    d_rim,
    edge,
    edge_in,
    d_lproj,
    d_xn,
    ls,
    lr,
    rs,
    rr,
    ss,
    sr,
):
    hi, lo, x_, c = place()
    meet(line_peers())
    tokens = x.shape[0]
    group, cap, width = select.shape
    wl, wh = HL * DH, HH * DH
    ones, scaled = pair_masks(1.0), pair_masks(SCORE_SCALE)
    across, partner = at(hi, lo, 1 - x_, c), at(hi, lo, x_, 1 - c)
    picked = []
    for s in range(group):
        high, low = halves(d_hidden[s * width : (s + 1) * width, :])
        picked.append((dot(select[s], high) + dot(select[s], low)).astype(BF))
    d_ha = jnp.concatenate(picked, axis=0)
    d_ho[...] = dot_back(d_ha, w_hout[...]).astype(BF)
    heavy_kv = kvh.reshape(group, 4 * cap, 2 * wh)
    part_kv = part.reshape(group, 4 * cap, 2 * wh)

    def heavy(s, carry):
        r = pl.ds(pl.multiple_of(s * cap, cap), cap)
        bias = heavy_bias[s]
        bias = jnp.concatenate([bias, bias], axis=0)
        lse = h_lse[r, :]
        for pair in range(HH // 2):
            at_k = slice(pair * 128, (pair + 1) * 128)
            at_v = slice(wh + pair * 128, wh + (pair + 1) * 128)
            dq, dk, dv = pair_backward(
                hq[r, at_k],
                heavy_kv[s, :, at_k],
                heavy_kv[s, :, at_v],
                bias,
                get_lse(lse, pair),
                d_ho[r, at_k],
                ones,
                scaled,
            )
            d_hproj[r, at_k] = dq.astype(BF)
            part_kv[s, :, at_k] = dk.astype(BF)
            part_kv[s, :, at_v] = dv.astype(BF)
        return carry

    lax.fori_loop(0, group, heavy, 0)
    beside = [
        send(part.at[:, b * 2 + 1 - c], got.at[b], ss.at[b], sr.at[b], partner) for b in (0, 1)
    ]
    g_hout[...] = dot_grad(ho[...], d_ha).astype(BF)

    def light_out_back(r):
        d = d_hidden[r, :].astype(BF)
        d_la[r, :] = d
        d_lo[r, :] = dot_back(d, w_lout[...]).astype(BF)

    tiles(tokens, 256, light_out_back)
    for copy in beside:
        copy.wait()
    for b in (0, 1):
        got[b] = (got[b].astype(F32) + part[:, b * 2 + c].astype(F32)).astype(BF)
    third = send(got.at[1 - x_], far, ss.at[2], sr.at[2], across)
    d_rim[...] = jnp.zeros(d_rim.shape, F32)
    blocks = width // WIN

    def light(i, carry):
        s, b = i // blocks, i % blocks
        r = pl.ds(pl.multiple_of(i * WIN, WIN), WIN)
        keys = pl.ds(pl.multiple_of(b * WIN, WIN), 3 * WIN)
        bias = reach_bias(key_bias[i])
        lse = l_lse[r, :]
        for pair in range(HL // 2):
            at_k = slice(pair * 128, (pair + 1) * 128)
            at_v = slice(wl + pair * 128, wl + (pair + 1) * 128)
            dq, dk, dv = pair_backward(
                lq[r, at_k],
                rim[s, keys, at_k],
                rim[s, keys, at_v],
                bias,
                get_lse(lse, pair),
                d_lo[r, at_k],
                ones,
                scaled,
            )
            d_lproj[r, at_k] = dq.astype(BF)
            d_rim[s, keys, at_k] += dk
            d_rim[s, keys, at_v] += dv
        return carry

    lax.fori_loop(0, group * blocks, light, 0)
    edge[0] = d_rim[:, :WIN, :].astype(BF)
    edge[1] = d_rim[:, WIN + width :, :].astype(BF)
    finish = rim_exchange(
        edge.at[0], edge.at[1], edge_in.at[0], edge_in.at[1], ls, lr, rs, rr
    )
    g_lout[...] = dot_grad(lo_out[...], d_la[...]).astype(BF)
    third.wait()
    total = (got[x_].astype(F32) + far[...].astype(F32)).astype(BF)
    for s in range(group):
        d_hproj[s * cap : (s + 1) * cap, wh:] = total[s]

    def heavy_grad(j):
        g_hqkv[:, j] = dot_grad(a_rows[...], d_hproj[:, j]).astype(BF)

    tiles(3 * wh, 768, heavy_grad)
    d_high, d_low = halves(dot_back(d_hproj[...], w_hqkv[...]))
    finish()
    for s in range(group):
        d_rim[s, WIN : 2 * WIN, :] += edge_in[0, s].astype(F32)
        d_rim[s, width : width + WIN, :] += edge_in[1, s].astype(F32)
        d_lproj[s * width : (s + 1) * width, wl:] = d_rim[s, WIN : WIN + width, :].astype(BF)

    def light_grad(j):
        g_lqkv[:, j] = dot_grad(xn[...], d_lproj[:, j]).astype(BF)

    tiles(3 * wl, 768, light_grad)
    for s in range(group):
        r = slice(s * width, (s + 1) * width)
        q = slice(s * cap, (s + 1) * cap)
        d_xn[r, :] = dot_back(d_lproj[r, :], w_lqkv[...]) + (
            dot(select_t[s], d_high[q]) + dot(select_t[s], d_low[q])
        )
    stats[...] = jnp.zeros(stats.shape, F32)

    def norm_back(r):
        h = x[r, :].astype(F32)
        inv = lax.rsqrt(jnp.mean(h * h, axis=-1, keepdims=True) + EPSILON)
        d = d_xn[r, :]
        dh = d * h
        stats[0:1, :] += jnp.sum(dh * inv, axis=0, keepdims=True)
        mean = jnp.mean(gain[...] * dh, axis=-1, keepdims=True)
        dx[r, :] = (
            d_hidden[r, :] + inv * gain[...] * d - h * (inv * inv * inv * mean)
        ).astype(BF)

    tiles(tokens, 128, norm_back)


def attend_back(d_hidden, x, gain, select, select_t, key_bias, heavy_bias, weights, saved):
    tokens = x.shape[0]
    group, cap, width = select.shape
    wl, wh = HL * DH, HH * DH
    rows = group * cap
    operands = [d_hidden, x, gain, select, select_t, key_bias, heavy_bias, *weights, *saved]
    shapes = [
        jax.ShapeDtypeStruct((D, 3 * wl), BF),
        jax.ShapeDtypeStruct((D, 3 * wh), BF),
        jax.ShapeDtypeStruct((wl, D), BF),
        jax.ShapeDtypeStruct((wh, D), BF),
        jax.ShapeDtypeStruct((tokens, D), BF),
        jax.ShapeDtypeStruct((8, D), F32),
    ]
    return call(
        attend_back_kernel,
        shapes,
        operands,
        [VM] * len(operands),
        [VM] * len(shapes),
        [
            pltpu.VMEM((rows, wh), BF),
            pltpu.VMEM((rows, 3 * wh), BF),
            pltpu.VMEM((group, 4, cap, 2 * wh), BF),
            pltpu.VMEM((2, group, cap, 2 * wh), BF),
            pltpu.VMEM((group, cap, 2 * wh), BF),
            pltpu.VMEM((tokens, D), BF),
            pltpu.VMEM((tokens, wl), BF),
            pltpu.VMEM((group, width + 2 * WIN, 2 * wl), F32),
            pltpu.VMEM((2, group, WIN, 2 * wl), BF),
            pltpu.VMEM((2, group, WIN, 2 * wl), BF),
            pltpu.VMEM((tokens, 3 * wl), BF),
            pltpu.VMEM((tokens, D), F32),
            DMA,
            DMA,
            DMA,
            DMA,
            DMA((3,)),
            DMA((3,)),
        ],
        3,
    )


def scatter_kernel(dp, nw, *refs):
    nz = dp // 2
    dx, stats, gs, hin, hdn = refs[0], refs[1], refs[2 : 2 + nw], refs[2 + nw], refs[3 + nw]
    outs = refs[4 + nw :]
    dxo, total, gos, hin_o, hdn_o = outs[0], outs[1], outs[2 : 2 + nw], outs[2 + nw], outs[3 + nw]
    scr = outs[4 + nw :]
    nears, fars, sums, ends = (scr[i * nw : (i + 1) * nw] for i in range(4))
    hin_r, hin_s, hdn_r, sc, sp, sz, acc, acc2 = scr[4 * nw : 4 * nw + 8]
    own, xs, xr, cs, cr, ps, pr, zs, zr, hs, hr, ts, tr = scr[4 * nw + 8 :]
    hi, lo, x, c = place()
    d = hi * 2 + lo
    f = x * 2 + c
    plane = (lo * 2 + x) * 2 + c
    dp_peers = [(lax.rem(d + k, dp), f) for k in range(1, dp)]
    rest = [(a, b, e) for a in (0, 1) for b in (0, 1) for e in (0, 1) if a or b or e]
    flat8 = []
    for a, b, e in rest:
        l2 = 1 - lo if a else lo
        x2 = 1 - x if b else x
        c2 = 1 - c if e else c
        flat8.append((l2, x2, c2))
    meet(dp_peers + [at(hi, *p) for (a, b, e), p in zip(rest, flat8) if b or e])
    partner = at(hi, lo, x, 1 - c)
    quad = quad_peers()
    z_index = [lax.rem(hi + k, nz) for k in range(1, nz)]
    z_peers = [at(z, lo, x, c) for z in z_index]
    c_sends = [
        send(gs[w].at[:, :, :, 1 - c], nears[w], cs.at[w], cr.at[w], partner) for w in range(nw)
    ]
    t_c = send(stats, sc, ts.at[0], tr.at[0], partner)
    mine = keep(dx.at[:, d], dxo.at[d], own)
    x_sends = [
        send(dx.at[:, peer[0]], dxo.at[d], xs.at[k], xr.at[k], peer)
        for k, peer in enumerate(dp_peers)
    ]
    h_sends = []
    for k, z in enumerate(z_index):
        h_sends.append(send(hin.at[z], hin_r.at[k], hs.at[1, k], hr.at[1, k], z_peers[k]))
        h_sends.append(send(hdn.at[z], hdn_r.at[k], hs.at[2, k], hr.at[2, k], z_peers[k]))
    p_sends, z_sends = [], []
    t_c.wait()
    acc[...] = stats[...] + sc[...]
    t_p = [
        send(acc, sp.at[k], ts.at[1 + k], tr.at[1 + k], at(hi, l2, x2, c))
        for k, (l2, x2) in enumerate(quad)
    ]

    def add_core(w):
        c_sends[w].wait()
        near, g = nears[w], gs[w]

        def body(i, carry):
            z, a, b = i // 4, (i // 2) % 2, i % 2
            near[z, a, b] = (near[z, a, b].astype(F32) + g[z, a, b, c].astype(F32)).astype(BF)
            return carry

        lax.fori_loop(0, nz * 4, body, 0)
        p_sends.append(
            [
                send(near.at[:, l2, x2], fars[w].at[k], ps.at[w, k], pr.at[w, k], at(hi, l2, x2, c))
                for k, (l2, x2) in enumerate(quad)
            ]
        )

    def add_plane(w):
        for copy in p_sends[w]:
            copy.wait()
        near, far, part = nears[w], fars[w], sums[w]

        def body(z, carry):
            part[z] = (
                near[z, lo, x].astype(F32)
                + far[0, z].astype(F32)
                + far[1, z].astype(F32)
                + far[2, z].astype(F32)
            ).astype(BF)
            return carry

        lax.fori_loop(0, nz, body, 0)
        z_sends.append(
            [
                send(part.at[z], ends[w].at[k], zs.at[w, k], zr.at[w, k], z_peers[k])
                for k, z in enumerate(z_index)
            ]
        )

    def add_line(w):
        for copy in z_sends[w]:
            copy.wait()
        gos[w][...] = sums[w][hi].astype(F32)
        for k in range(nz - 1):
            gos[w][...] += ends[w][k].astype(F32)

    for w in range(nw):
        add_core(w)
        if w >= 2:
            add_plane(w - 2)
    for copy in t_p:
        copy.wait()
    acc2[...] = acc[...] + sp[0] + sp[1] + sp[2]
    t_z = [send(acc2, sz.at[k], ts.at[4 + k], tr.at[4 + k], z_peers[k]) for k in range(nz - 1)]
    for copy in h_sends:
        copy.wait()

    def body(i, carry):
        value = hin[hi, i].astype(F32)
        for k in range(nz - 1):
            value += hin_r[k, i].astype(F32)
        hin_s[i] = value.astype(BF)
        return carry

    lax.fori_loop(0, 8, body, 0)
    hin_o[plane] = hin_s[plane]
    a_sends = [
        send(
            hin_s.at[(l2 * 2 + x2) * 2 + c2],
            hin_o.at[plane],
            hs.at[0, k],
            hr.at[0, k],
            at(hi, l2, x2, c2),
        )
        for k, (l2, x2, c2) in enumerate(flat8)
    ]
    hdn_o[...] = hdn[hi].astype(F32)
    for k in range(nz - 1):
        hdn_o[...] += hdn_r[k].astype(F32)
    for w in range(max(nw - 2, 0), nw):
        add_plane(w)
    for copy in t_z:
        copy.wait()
    total[...] = acc2[...]
    for k in range(nz - 1):
        total[...] += sz[k]
    for w in range(nw):
        add_line(w)
    mine.wait()
    for copy in x_sends + a_sends:
        copy.wait()


def scatter_all(dp, dx, stats, grads, hin, hdn):
    nz = dp // 2
    nw = len(grads)
    group, _, rows, _ = dx.shape
    tiles = [g.shape[4:] for g in grads]
    most = max(7, nz)
    scratch = [pltpu.VMEM((nz, 2, 2) + t, BF) for t in tiles]
    scratch += [pltpu.VMEM((3, nz) + t, BF) for t in tiles]
    scratch += [pltpu.VMEM((nz,) + t, BF) for t in tiles]
    scratch += [pltpu.VMEM((nz - 1,) + t, BF) for t in tiles]
    scratch += [
        pltpu.VMEM((nz - 1,) + hin.shape[1:], BF),
        pltpu.VMEM(hin.shape[1:], BF),
        pltpu.VMEM((nz - 1,) + hdn.shape[1:], BF),
        pltpu.VMEM(stats.shape, F32),
        pltpu.VMEM((3,) + stats.shape, F32),
        pltpu.VMEM((nz - 1,) + stats.shape, F32),
        pltpu.VMEM(stats.shape, F32),
        pltpu.VMEM(stats.shape, F32),
        DMA,
        DMA((dp,)),
        DMA((dp,)),
        DMA((nw,)),
        DMA((nw,)),
        DMA((nw, 3)),
        DMA((nw, 3)),
        DMA((nw, nz)),
        DMA((nw, nz)),
        DMA((3, most)),
        DMA((3, most)),
        DMA((4 + nz,)),
        DMA((4 + nz,)),
    ]
    shapes = [jax.ShapeDtypeStruct((dp, group, rows, D), BF), jax.ShapeDtypeStruct(stats.shape, F32)]
    shapes += [jax.ShapeDtypeStruct(t, F32) for t in tiles]
    shapes.append(jax.ShapeDtypeStruct(hin.shape[1:], BF))
    shapes.append(jax.ShapeDtypeStruct(hdn.shape[1:], F32))
    return call(
        functools.partial(scatter_kernel, dp, nw),
        shapes,
        [dx, stats, *grads, hin, hdn],
        [ANY] + [VM] * (3 + nw),
        [ANY] + [VM] * (3 + nw),
        scratch,
        4,
    )


def routing(routes, pieces, piece_len):
    places = jnp.arange(pieces * piece_len)
    routed = jnp.any(routes[:, None, :] == places[None, :, None], axis=-1)
    routed = routed.reshape(-1, pieces, piece_len)
    before = jnp.arange(piece_len)[:, None] < jnp.arange(piece_len)[None, :]
    rank = jnp.einsum(
        "skp,pq->skq", routed.astype(BF), before.astype(BF), preferred_element_type=F32
    )
    slots = jnp.arange(CAP, dtype=F32)
    hot = routed[:, :, None, :] & (rank[:, :, None, :] == slots[None, None, :, None])
    filled = jnp.any(hot, axis=-1)
    spots = jnp.sum(jnp.where(hot, places.reshape(1, pieces, 1, piece_len), 0), axis=-1)
    return hot, jnp.where(filled, spots, -1)


def local(
    layer_input,
    teacher,
    lengths,
    dealing,
    attn_routes,
    ffn_routes,
    ffn_scores,
    gain_attn,
    gain_ffn,
    light_qkv,
    light_out,
    heavy_qkv,
    heavy_out,
    light_in,
    light_down,
    heavy_in,
    heavy_down,
):
    dp = lax.axis_size("dp")
    pieces = lax.axis_size("fsdp")
    data_index = lax.axis_index("dp")
    piece = lax.axis_index("fsdp")
    nz = dp // 2
    n = dp * pieces
    seqs = dealing.shape[0]
    group = seqs // dp
    gain_len = gain_attn.shape[0]
    hidden_units = heavy_in.shape[1] // 2 // n
    xin = deal_rows(dealing, layer_input[:, 0])
    gains = jnp.pad(
        jnp.stack([gain_attn, gain_ffn]), ((0, 6), (0, 128 - gain_len))
    )
    matrices = (light_qkv, heavy_qkv, light_out, heavy_out, light_in, light_down)
    hin_rows = heavy_in.shape[0]
    hin_src = (
        heavy_in.reshape(hin_rows, 2, nz, 8, hidden_units)
        .transpose(3, 0, 1, 2, 4)
        .reshape(8, hin_rows, 2 * nz * hidden_units)
    )
    if hin_rows % 8:
        hin_src = hin_src.reshape(8, -1, 128)
    got = gather_all(dp, xin, [gains] + [packed(m) for m in matrices], hin_src, heavy_down)
    tokens = layer_input.shape[2] * dp
    gain_rows = got[1].reshape(n, 8, 128)
    gain_one = gain_rows[:, 0, :gain_len].reshape(-1).astype(F32)
    gain_two = gain_rows[:, 1, :gain_len].reshape(-1).astype(F32)
    w_lqkv, w_hqkv, w_lout, w_hout, w_lin, w_ldown = (
        unpacked(full, *m.shape) for full, m in zip(got[2:8], matrices)
    )
    w_hin = unpacked(got[8], hin_rows, 2 * nz * hidden_units)
    w_hdown = got[9].reshape(-1, D)
    chosen = lax.dynamic_slice_in_dim(dealing, data_index * group, group)
    one = (chosen[:, None] == jnp.arange(seqs)[None, :])
    seq_lengths = jnp.sum(jnp.where(one, lengths[None, :], 0), axis=1)
    attn_pick = jnp.sum(jnp.where(one[:, :, None], attn_routes[None], 0), axis=1)
    ffn_pick = jnp.sum(jnp.where(one[:, :, None], ffn_routes[None], 0), axis=1)
    score_pick = jnp.sum(jnp.where(one[:, :, None], ffn_scores[None], 0.0), axis=1)
    token_count = jnp.sum(lengths).astype(F32)
    positions = piece * tokens + jnp.arange(tokens)
    valid_mask = positions[None, :] < seq_lengths[:, None]
    a_hot, a_spots = routing(attn_pick, pieces, tokens)
    f_hot, f_spots = routing(ffn_pick, pieces, tokens)
    a_select = lax.dynamic_index_in_dim(a_hot, piece, 1, False).astype(BF)
    f_select = lax.dynamic_index_in_dim(f_hot, piece, 1, False).astype(BF)
    a_spot = lax.dynamic_index_in_dim(a_spots, piece, 1, False)
    f_spot = lax.dynamic_index_in_dim(f_spots, piece, 1, False)
    slot_score = jnp.sum(
        jnp.where(f_spot[:, :, None] == ffn_pick[:, None, :], score_pick[:, None, :], 0.0), axis=-1
    )
    key_pos = piece * tokens - WIN + jnp.arange(tokens + 2 * WIN)
    live_key = (key_pos >= 0)[None, :] & (key_pos[None, :] < seq_lengths[:, None])
    key_line = jnp.where(live_key, 0.0, MASKED)
    key_bias = jnp.stack(
        [key_line[:, b : b + 3 * WIN] for b in range(0, tokens, WIN)], axis=1
    ).reshape(-1, 1, 3 * WIN)
    all_spots = a_spots.reshape(group, pieces * CAP)
    heavy_allowed = ((all_spots >= 0) & (all_spots < seq_lengths[:, None]))[:, None, :] | (
        a_spot[:, :, None] == all_spots[:, None, :]
    )
    heavy_bias = jnp.where(heavy_allowed, 0.0, MASKED)
    flat_x = got[0].reshape(-1, D)
    masks = (a_select, a_select.swapaxes(1, 2), key_bias, heavy_bias)
    attn_weights = (w_lqkv, w_hqkv, w_lout, w_hout)
    hidden, *saved = attend(flat_x, gain_one.reshape(1, D), *masks, *attn_weights)
    weight_mask = valid_mask.reshape(-1, 1).astype(F32)
    grad_lin, grad_ldown, grad_hin, grad_hdown, d_hidden, ffn_stats = feed_forward(
        hidden,
        f_select,
        f_select.swapaxes(1, 2),
        slot_score.reshape(-1, 1),
        gain_two.reshape(1, D),
        teacher.reshape(-1, D),
        weight_mask,
        2.0 * weight_mask / (D * token_count),
        w_lin,
        w_ldown,
        w_hin,
        w_hdown,
    )
    grad_lqkv, grad_hqkv, grad_lout, grad_hout, d_inputs, attn_stats = attend_back(
        d_hidden, flat_x, gain_one.reshape(1, D), *masks, attn_weights, saved
    )
    rows = tokens // dp
    stats = jnp.concatenate(
        [
            attn_stats[0].reshape(-1, 128),
            ffn_stats[0].reshape(-1, 128),
            jnp.broadcast_to(jnp.sum(ffn_stats[1]), (4, 128)),
        ]
    )
    grads = (grad_lin, grad_ldown, grad_hout, grad_lout, grad_hqkv, grad_lqkv)
    shards = (light_in, light_down, heavy_out, light_out, heavy_qkv, light_qkv)
    sent = [
        packed_full(grad.astype(BF), shard.shape, nz) for grad, shard in zip(grads, shards)
    ]
    hin_tile = hin_src.shape[1:]
    done = scatter_all(
        dp,
        d_inputs.reshape(group, dp, rows, D),
        stats,
        sent,
        grad_hin.astype(BF).reshape((nz, 8) + hin_tile),
        grad_hdown.astype(BF).reshape(nz, -1, D),
    )
    d_layer = undeal_rows(dealing, done[0].reshape(seqs, rows, D))[:, None]
    summed = done[1]
    mine = data_index * pieces + piece
    loss_value = summed[12, 0] / (D * token_count)
    own_one = lax.dynamic_slice_in_dim(summed[:6].reshape(-1), mine * gain_len, gain_len)
    own_two = lax.dynamic_slice_in_dim(summed[6:12].reshape(-1), mine * gain_len, gain_len)
    g_lin, g_ldown, g_hout, g_lout, g_hqkv, g_lqkv = (
        full.reshape(shard.shape) for full, shard in zip(done[2:8], shards)
    )
    g_hin = (
        done[8]
        .astype(F32)
        .reshape(8, hin_rows, 2, nz, hidden_units)
        .transpose(1, 2, 3, 0, 4)
        .reshape(heavy_in.shape)
    )
    return (
        loss_value,
        d_layer,
        own_one,
        own_two,
        g_lqkv,
        g_lout,
        g_hqkv,
        g_hout,
        g_lin,
        g_ldown,
        g_hin,
        done[9].reshape(heavy_down.shape),
    )


def packed_full(grad, shard_shape, nz):
    rows, columns = shard_shape
    if rows % 8 == 0:
        return grad.reshape(nz, 2, 2, 2, rows, columns)
    return grad.reshape(nz, 2, 2, 2, rows * columns // 128, 128)


def solution(mesh):
    split = P(("dp", "fsdp"))
    matrix = P(("dp", "fsdp"), None)
    placed = (
        P(None, "fsdp", "dp", None),
        P("dp", "fsdp", None, None),
        P(),
        P(),
        P(),
        P(),
        P(),
        split,
        split,
    ) + (matrix,) * 8
    return jax.shard_map(
        local,
        mesh=mesh,
        in_specs=placed,
        out_specs=(P(), P(None, "fsdp", "dp", None), split, split) + (matrix,) * 8,
        check_vma=False,
    )
```

```python
import functools
import jax
import jax.numpy as jnp
from jax import lax
from jax.experimental import pallas as pl
from jax.experimental.pallas import tpu as pltpu
from jax.sharding import PartitionSpec as P

D = 768
HL = 8
HH = 12
DH = 64
FL = 1024
FH = 4096
WIN = 128
CAP = 64

EPSILON = 1e-06
MASKED = -1000000000.0
SCORE_SCALE = 0.125
MESH = pl.DeviceIdType.MESH
BF = jnp.bfloat16
F32 = jnp.float32
ANY = pl.BlockSpec(memory_space=pl.ANY)
VM = pl.BlockSpec(memory_space=pltpu.VMEM)
DMA = pltpu.SemaphoreType.DMA
VMEM_BYTES = 60 * 1024 * 1024


def place():
    d = lax.axis_index("dp")
    f = lax.axis_index("fsdp")
    return d // 2, d % 2, f // 2, f % 2


def at(hi, lo, x, c):
    return (hi * 2 + lo, x * 2 + c)


def meet(peers):
    barrier = pltpu.get_barrier_semaphore()
    for peer in peers:
        pl.semaphore_signal(barrier, inc=1, device_id=peer, device_id_type=MESH)
    pl.semaphore_wait(barrier, len(peers))


def send(src, dst, send_sem, recv_sem, peer):
    copy = pltpu.make_async_remote_copy(
        src_ref=src,
        dst_ref=dst,
        send_sem=send_sem,
        recv_sem=recv_sem,
        device_id=peer,
        device_id_type=MESH,
    )
    copy.start()
    return copy


def keep(src, dst, sem):
    copy = pltpu.make_async_copy(src, dst, sem)
    copy.start()
    return copy


def quad_peers():
    hi, lo, x, c = place()
    return [(lo, 1 - x), (1 - lo, x), (1 - lo, 1 - x)]


def call(kernel, out_shape, operands, in_specs, out_specs, scratch, collective_id):
    return pl.pallas_call(
        kernel,
        out_shape=out_shape,
        in_specs=in_specs,
        out_specs=out_specs,
        scratch_shapes=scratch,
        compiler_params=pltpu.CompilerParams(
            collective_id=collective_id, has_side_effects=True, vmem_limit_bytes=VMEM_BYTES
        ),
    )(*operands)


def deal_kernel(deal_ref, x_ref, o_ref):
    def body(i, carry):
        o_ref[i] = x_ref[deal_ref[i]]
        return carry

    lax.fori_loop(0, o_ref.shape[0], body, 0)


def deal_rows(dealing, rows):
    return pl.pallas_call(
        deal_kernel,
        out_shape=jax.ShapeDtypeStruct(rows.shape, rows.dtype),
        in_specs=[pl.BlockSpec(memory_space=pltpu.SMEM), VM],
        out_specs=VM,
        compiler_params=pltpu.CompilerParams(vmem_limit_bytes=VMEM_BYTES),
    )(dealing, rows)


def undeal_kernel(deal_ref, x_ref, o_ref):
    def body(i, carry):
        o_ref[deal_ref[i]] = x_ref[i].astype(F32)
        return carry

    lax.fori_loop(0, x_ref.shape[0], body, 0)


def undeal_rows(dealing, rows):
    return pl.pallas_call(
        undeal_kernel,
        out_shape=jax.ShapeDtypeStruct(rows.shape, F32),
        in_specs=[pl.BlockSpec(memory_space=pltpu.SMEM), VM],
        out_specs=VM,
        compiler_params=pltpu.CompilerParams(vmem_limit_bytes=VMEM_BYTES),
    )(dealing, rows)


def packed(matrix):
    rows, columns = matrix.shape
    if rows % 8 == 0:
        return matrix
    return matrix.reshape(rows * columns // 128, 128)


def unpacked(gathered, rows, columns):
    return gathered.reshape(-1, rows, columns).reshape(-1, columns)


def plane_others():
    hi, lo, x, c = place()
    others = []
    for a in (0, 1):
        for b in (0, 1):
            for e in (0, 1):
                if a or b or e:
                    others.append(
                        (1 - lo if a else lo, 1 - x if b else x, 1 - c if e else c, b or e)
                    )
    return others


class Gather:
    def __init__(self, dp, xin, ws, hin, hdn, xo, wos, hin_o, hdn_o, sems):
        self.dp, self.nz = dp, dp // 2
        self.xin, self.ws, self.hin, self.hdn = xin, ws, hin, hdn
        self.xo, self.wos, self.hin_o, self.hdn_o = xo, wos, hin_o, hdn_o
        self.loc, self.xs, self.xr, self.zs, self.zr = sems[:5]
        self.ps, self.pr, self.cs, self.cr, self.hs, self.hr = sems[5:]
        self.hi, self.lo, self.x, self.c = place()
        hi, lo, x, c = place()
        self.d = hi * 2 + lo
        self.home = (lo * 2 + x) * 2 + c
        self.rows_to = [(lax.rem(self.d + k, dp), x * 2 + c) for k in range(1, dp)]
        self.z_to = [at(lax.rem(hi + k, self.nz), lo, x, c) for k in range(1, self.nz)]
        self.others = plane_others()
        nw = len(ws)
        self.kept, self.z, self.p, self.f, self.k = ([None] * nw for _ in range(5))

    def shard(self, w, z, lo, x):
        full, rows = self.wos[w], self.ws[w].shape[0]
        if len(full.shape) == 6:
            return full.at[z, lo, x, self.c]
        return full.at[z, lo, x, pl.ds(pl.multiple_of(self.c * rows, 8), rows)]

    def meet(self):
        peers = self.rows_to + [at(self.hi, *q[:3]) for q in self.others if q[3]]
        meet(peers)

    def rows(self):
        group = self.xin.shape[0] // self.dp
        nw = len(self.ws)
        spot = self.xo.at[:, self.d]
        self.own = keep(self.xin.at[pl.ds(self.d * group, group)], spot, self.loc.at[nw])
        self.moved = [
            send(self.xin.at[pl.ds(to[0] * group, group)], spot, self.xs.at[k], self.xr.at[k], to)
            for k, to in enumerate(self.rows_to)
        ]

    def rows_ready(self):
        self.own.wait()
        for copy in self.moved:
            copy.wait()

    def line(self, w):
        spot = self.shard(w, self.hi, self.lo, self.x)
        self.kept[w] = keep(self.ws[w], spot, self.loc.at[w])
        self.z[w] = [
            send(self.ws[w], spot, self.zs.at[w, k], self.zr.at[w, k], to)
            for k, to in enumerate(self.z_to)
        ]

    def onward(self, part, w, k, to, sems):
        return send(part, part, sems[0].at[w, k], sems[1].at[w, k], to)

    def plane(self, w):
        self.kept[w].wait()
        for copy in self.z[w]:
            copy.wait()
        hi, lo, x, c = self.hi, self.lo, self.x, self.c
        column = self.shard(w, slice(None), lo, x)
        plane = (self.ps, self.pr)
        self.p[w] = [
            self.onward(column, w, 0, at(hi, lo, 1 - x, c), plane),
            self.onward(column, w, 1, at(hi, 1 - lo, x, c), plane),
        ]
        self.k[w] = [self.onward(column, w, 0, at(hi, lo, x, 1 - c), (self.cs, self.cr))]

    def cross(self, w):
        hi, lo, x, c = self.hi, self.lo, self.x, self.c
        plane, core, half = (self.ps, self.pr), (self.cs, self.cr), self.nz // 2
        partner = at(hi, lo, x, 1 - c)
        self.p[w][1].wait()
        part = self.shard(w, pl.ds(0, half), 1 - lo, x)
        first = self.onward(part, w, 2, at(hi, lo, 1 - x, c), plane)
        self.p[w][0].wait()
        part = self.shard(w, pl.ds(half, self.nz - half), lo, 1 - x)
        self.f[w] = [first, self.onward(part, w, 3, at(hi, 1 - lo, x, c), plane)]
        for k, part in ((1, (1 - lo, x)), (2, (lo, 1 - x))):
            self.k[w].append(
                self.onward(self.shard(w, slice(None), *part), w, k, partner, core)
            )

    def core(self, w):
        for copy in self.f[w]:
            copy.wait()
        part = self.shard(w, slice(None), 1 - self.lo, 1 - self.x)
        partner = at(self.hi, self.lo, self.x, 1 - self.c)
        self.k[w].append(self.onward(part, w, 3, partner, (self.cs, self.cr)))

    def ready(self, w):
        for copy in self.k[w]:
            copy.wait()

    def heavy_plane(self):
        nw, hi = len(self.ws), self.hi
        spot = self.hin_o.at[hi, self.home]
        self.h_own = [
            keep(self.hin.at[self.home], spot, self.loc.at[nw + 1]),
            keep(self.hdn, self.hdn_o.at[hi], self.loc.at[nw + 2]),
        ]
        self.h_near = [
            send(
                self.hin.at[(q[0] * 2 + q[1]) * 2 + q[2]],
                spot,
                self.hs.at[0, k],
                self.hr.at[0, k],
                at(hi, *q[:3]),
            )
            for k, q in enumerate(self.others)
        ]

    def heavy_line(self):
        for copy in self.h_own + self.h_near:
            copy.wait()
        part = self.hin_o.at[self.hi]
        self.h_far = []
        for k, to in enumerate(self.z_to):
            self.h_far.append(send(part, part, self.hs.at[1, k], self.hr.at[1, k], to))
            self.h_far.append(
                send(self.hdn, self.hdn_o.at[self.hi], self.hs.at[2, k], self.hr.at[2, k], to)
            )

    def heavy_ready(self):
        for copy in self.h_far:
            copy.wait()


def gather_sems(dp, nw):
    nz, most = dp // 2, max(7, dp // 2)
    return [
        DMA((nw + 3,)),
        DMA((dp,)),
        DMA((dp,)),
        DMA((nw, nz)),
        DMA((nw, nz)),
        DMA((nw, 4)),
        DMA((nw, 4)),
        DMA((nw, 4)),
        DMA((nw, 4)),
        DMA((3, most)),
        DMA((3, most)),
    ]


def gather_kernel(dp, nw, *refs):
    ins, outs, sems = refs[: 3 + nw], refs[3 + nw : 6 + 2 * nw], refs[6 + 2 * nw :]
    g = Gather(
        dp, ins[0], ins[1:-2], ins[-2], ins[-1], outs[0], outs[1:-2], outs[-2], outs[-1], sems
    )
    g.meet()
    g.rows()
    for w in range(nw):
        g.line(w)
    g.heavy_plane()
    for w in range(nw):
        g.plane(w)
        if w == 1:
            g.heavy_line()
        if w >= 1:
            g.cross(w - 1)
        if w >= 2:
            g.core(w - 2)
    g.cross(nw - 1)
    for w in range(nw - 2, nw):
        g.core(w)
    g.rows_ready()
    for w in range(nw):
        g.ready(w)
    g.heavy_ready()


def gather_shapes(dp, xin, weights, hin, hdn, paired):
    nz = dp // 2
    seqs, rows, _ = xin.shape
    shapes = [jax.ShapeDtypeStruct((seqs // dp, dp, rows, D), BF)]
    if paired:
        shapes += [jax.ShapeDtypeStruct((nz, 2, 2, 2 * w.shape[0], w.shape[1]), BF) for w in weights]
    else:
        shapes += [jax.ShapeDtypeStruct((nz, 2, 2, 2) + w.shape, BF) for w in weights]
    shapes.append(jax.ShapeDtypeStruct((nz,) + hin.shape, BF))
    shapes.append(jax.ShapeDtypeStruct((nz,) + hdn.shape, BF))
    return shapes


def gather_all(dp, xin, weights, hin, hdn):
    nw = len(weights)
    return call(
        functools.partial(gather_kernel, dp, nw),
        gather_shapes(dp, xin, weights, hin, hdn, False),
        [xin, *weights, hin, hdn],
        [ANY] * (3 + nw),
        [ANY] * (3 + nw),
        gather_sems(dp, nw),
        1,
    )


def rim_exchange(left, right, from_left, from_right, ls, lr, rs, rr):
    d = lax.axis_index("dp")
    f = lax.axis_index("fsdp")
    last = lax.axis_size("fsdp") - 1

    def down():
        return pltpu.make_async_remote_copy(
            src_ref=left,
            dst_ref=from_right,
            send_sem=ls,
            recv_sem=lr,
            device_id=(d, lax.max(f - 1, 0)),
            device_id_type=MESH,
        )

    def up():
        return pltpu.make_async_remote_copy(
            src_ref=right,
            dst_ref=from_left,
            send_sem=rs,
            recv_sem=rr,
            device_id=(d, lax.min(f + 1, last)),
            device_id_type=MESH,
        )

    @pl.when(f > 0)
    def _():
        down().start()

    @pl.when(f < last)
    def _():
        up().start()

    @pl.when(f == 0)
    def _():
        from_left[...] = jnp.zeros(from_left.shape, from_left.dtype)

    @pl.when(f == last)
    def _():
        from_right[...] = jnp.zeros(from_right.shape, from_right.dtype)

    def finish():
        @pl.when(f > 0)
        def _():
            down().wait_send()
            up().wait_recv()

        @pl.when(f < last)
        def _():
            up().wait_send()
            down().wait_recv()

    return finish


def line_peers():
    hi, lo, x, c = place()
    return [at(hi, lo, x, 1 - c), at(hi, lo, 1 - x, c), at(hi, lo, 1 - x, 1 - c)]


def dot(left, right):
    return jnp.dot(left, right, preferred_element_type=F32)


def dot_back(left, right):
    return lax.dot_general(left, right, (((1,), (1,)), ((), ())), preferred_element_type=F32)


def dot_grad(left, right):
    return lax.dot_general(left, right, (((0,), (0,)), ((), ())), preferred_element_type=F32)


def halves(value):
    high = value.astype(BF)
    return high, (value - high.astype(F32)).astype(BF)


def tiles(extent, step, body):
    def run(i, carry):
        body(pl.ds(pl.multiple_of(i * step, step), step))
        return carry

    lax.fori_loop(0, extent // step, run, 0)


GELU_A = 0.7978845608028654
GELU_B = 0.044715


def gelu_parts(v):
    square = v * v
    t = jnp.tanh(GELU_A * v * (1.0 + GELU_B * square))
    value = 0.5 * v * (1.0 + t)
    slope = 0.5 * (1.0 + t) + 0.5 * v * (1.0 - t * t) * GELU_A * (1.0 + 3.0 * GELU_B * square)
    return value, slope


def gelu_value(v):
    return 0.5 * v * (1.0 + jnp.tanh(GELU_A * v * (1.0 + GELU_B * v * v)))


def ffn_kernel(
    hidden,
    select,
    select_t,
    score,
    gain,
    teach,
    mask,
    scale,
    w_in,
    w_dn,
    w_hin,
    w_hdn,
    g_in,
    g_dn,
    g_hin,
    g_hdn,
    d_hidden,
    stats,
    hn,
    every,
    d_every,
    up_l,
    z,
    up_h,
    zh,
    part,
    near,
    far,
    near2,
    far2,
    out,
    dl,
    dup_l,
    dup_h,
    dhn,
    ps,
    pr,
    cs,
    cr,
    qs,
    qr,
    es,
    er,
):
    hi, lo, x, c = place()
    quad = quad_peers()
    partner = at(hi, lo, x, 1 - c)
    spots = [l2 * 2 + x2 for l2, x2 in quad]
    home = lo * 2 + x
    tokens = hidden.shape[0]
    group, cap, width = select.shape
    fl = z.shape[1]
    fh = zh.shape[2]
    rows_h = part.shape[1] * part.shape[2]
    meet([at(hi, l2, x2, c) for l2, x2 in quad] + [partner])

    def spread(buffer, i):
        spot = buffer.at[c, home]
        there = [
            send(spot, spot, ps.at[i, k], pr.at[i, k], at(hi, l2, x2, c))
            for k, (l2, x2) in enumerate(quad)
        ]
        return there, [send(spot, spot, cs.at[i, 3], cr.at[i, 3], partner)]

    def relay(buffer, i, there, back):
        for k, q in enumerate(spots):
            there[k].wait()
            other = buffer.at[c, q]
            back.append(send(other, other, cs.at[i, k], cr.at[i, k], partner))

    def fold(near_ref, far_ref, i, copy):
        copy.wait()
        there = []
        for k, q in enumerate(spots):
            near_ref[q] = (near_ref[q].astype(F32) + part[c, q].astype(F32)).astype(BF)
            l2, x2 = quad[k]
            there.append(
                send(near_ref.at[q], far_ref.at[k], qs.at[i, k], qr.at[i, k], at(hi, l2, x2, c))
            )
        return there

    def folded(near_ref, far_ref, there):
        for copy in there:
            copy.wait()
        return (
            near_ref[home].astype(F32)
            + part[c, home].astype(F32)
            + far_ref[0].astype(F32)
            + far_ref[1].astype(F32)
            + far_ref[2].astype(F32)
        )

    def norm(r):
        h = hidden[r, :]
        inv = lax.rsqrt(jnp.mean(h * h, axis=-1, keepdims=True) + EPSILON)
        hn[r, :] = (h * inv * gain[1:2, :]).astype(BF)

    tiles(tokens, 128, norm)
    for s in range(group):
        every[c, home, s * cap : (s + 1) * cap, :] = dot(
            select[s], hn[s * width : (s + 1) * width, :]
        ).astype(BF)
    there, back = spread(every, 0)

    def light_up(r):
        up_l[r, :] = dot(hn[r, :], w_in[...])
        z[r, :] = (gelu_value(up_l[r, :fl]) * up_l[r, fl:]).astype(BF)

    tiles(tokens, 256, light_up)
    relay(every, 0, there, back)

    def light_down(r):
        out[r, :] = hidden[r, :] + dot(z[r, :], w_dn[...])

    tiles(tokens, 256, light_down)
    for copy in back:
        copy.wait()

    def heavy(e):
        def up(i, carry):
            a = every[e, pl.ds(2 * i, 2)].reshape(2 * group * cap, D)
            r = pl.ds(pl.multiple_of(i * 256, 256), 256)
            up_h[e, r, :] = dot(a, w_hin[...])
            zh[e, r, :] = (gelu_value(up_h[e, r, :fh]) * up_h[e, r, fh:]).astype(BF)
            v = dot(zh[e, r, :], w_hdn[...]).astype(BF)
            part[e, pl.ds(2 * i, 2)] = v.reshape(2, group * cap, D)
            return carry

        lax.fori_loop(0, 2, up, 0)

    heavy(1 - c)
    first = send(part.at[1 - c], near, es.at[0], er.at[0], partner)
    heavy(c)
    there = fold(near, far, 0, first)
    hf = folded(near, far, there) * score[...]
    hf_high, hf_low = halves(hf)
    for s in range(group):
        r = slice(s * width, (s + 1) * width)
        q = slice(s * cap, (s + 1) * cap)
        out[r, :] += dot(select_t[s], hf_high[q]) + dot(select_t[s], hf_low[q])
    stats[...] = jnp.zeros(stats.shape, F32)

    def misfit(r):
        m = out[r, :] - teach[r, :].astype(F32)
        stats[1:2, :] += jnp.sum(mask[r, :] * m * m, axis=0, keepdims=True)
        d = scale[r, :] * m
        out[r, :] = d
        dl[r, :] = d.astype(BF)

    tiles(tokens, 128, misfit)
    for s in range(group):
        high, low = halves(out[s * width : (s + 1) * width, :])
        picked = dot(select[s], high) + dot(select[s], low)
        q = slice(s * cap, (s + 1) * cap)
        d_every[c, home, q, :] = (picked * score[q, :]).astype(BF)
    there, back = spread(d_every, 1)

    def light_back(r):
        dz = dot_back(dl[r, :], w_dn[...])
        value, slope = gelu_parts(up_l[r, :fl])
        dup_l[r, :fl] = (dz * up_l[r, fl:] * slope).astype(BF)
        dup_l[r, fl:] = (dz * value).astype(BF)

    tiles(tokens, 256, light_back)
    relay(d_every, 1, there, back)

    def light_grad(j):
        g_dn[j, :] = dot_grad(z[:, j], dl[...]).astype(BF)

    tiles(fl, 512, light_grad)
    for copy in back:
        copy.wait()

    def heavy_back(e):
        def run(i, carry):
            d = d_every[e, pl.ds(2 * i, 2)].reshape(2 * group * cap, D)
            r = pl.ds(pl.multiple_of(i * 256, 256), 256)
            dz = dot_back(d, w_hdn[...])
            value, slope = gelu_parts(up_h[e, r, :fh])
            dup_h[e, r, :fh] = (dz * up_h[e, r, fh:] * slope).astype(BF)
            dup_h[e, r, fh:] = (dz * value).astype(BF)
            v = dot_back(dup_h[e, r, :], w_hin[...]).astype(BF)
            part[e, pl.ds(2 * i, 2)] = v.reshape(2, group * cap, D)
            return carry

        lax.fori_loop(0, 2, run, 0)

    heavy_back(1 - c)
    second = send(part.at[1 - c], near2, es.at[1], er.at[1], partner)
    heavy_back(c)
    there = fold(near2, far2, 1, second)

    def light_in_grad(j):
        g_in[:, j] = dot_grad(hn[...], dup_l[:, j]).astype(BF)

    tiles(2 * fl, 1024, light_in_grad)

    def light_in_back(r):
        dhn[r, :] = dot_back(dup_l[r, :], w_in[...])

    tiles(tokens, 256, light_in_back)
    every_rows = every[...].reshape(2 * rows_h, D)

    def heavy_grad(j):
        g_hin[:, j] = dot_grad(every_rows, dup_h[:, :, j].reshape(2 * rows_h, 512)).astype(BF)

    tiles(2 * fh, 512, heavy_grad)
    d_rows = d_every[...].reshape(2 * rows_h, D)

    def heavy_down_grad(j):
        g_hdn[j, :] = dot_grad(zh[:, :, j].reshape(2 * rows_h, 512), d_rows).astype(BF)

    tiles(fh, 512, heavy_down_grad)
    d_high, d_low = halves(folded(near2, far2, there))
    for s in range(group):
        r = slice(s * width, (s + 1) * width)
        q = slice(s * cap, (s + 1) * cap)
        dhn[r, :] += dot(select_t[s], d_high[q]) + dot(select_t[s], d_low[q])

    def norm_back(r):
        h = hidden[r, :]
        inv = lax.rsqrt(jnp.mean(h * h, axis=-1, keepdims=True) + EPSILON)
        d = dhn[r, :]
        dh = d * h
        stats[0:1, :] += jnp.sum(dh * inv, axis=0, keepdims=True)
        mean = jnp.mean(gain[1:2, :] * dh, axis=-1, keepdims=True)
        d_hidden[r, :] = out[r, :] + inv * gain[1:2, :] * d - h * (inv * inv * inv * mean)

    tiles(tokens, 128, norm_back)


def feed_forward(hidden, select, select_t, score, gain, teach, mask, scale, w_in, w_dn, w_hin, w_hdn):
    tokens = hidden.shape[0]
    group, cap, _ = select.shape
    rows = group * cap
    fl, fh = w_dn.shape[0], w_hdn.shape[0]
    block = (2, 4, rows, D)
    operands = [hidden, select, select_t, score, gain, teach, mask, scale, w_in, w_dn, w_hin, w_hdn]
    return call(
        ffn_kernel,
        [
            jax.ShapeDtypeStruct((D, 2 * fl), BF),
            jax.ShapeDtypeStruct((fl, D), BF),
            jax.ShapeDtypeStruct((D, 2 * fh), BF),
            jax.ShapeDtypeStruct((fh, D), BF),
            jax.ShapeDtypeStruct((tokens, D), F32),
            jax.ShapeDtypeStruct((8, D), F32),
        ],
        operands,
        [VM] * len(operands),
        [VM] * 6,
        [
            pltpu.VMEM((tokens, D), BF),
            pltpu.VMEM(block, BF),
            pltpu.VMEM(block, BF),
            pltpu.VMEM((tokens, 2 * fl), F32),
            pltpu.VMEM((tokens, fl), BF),
            pltpu.VMEM((2, 4 * rows, 2 * fh), F32),
            pltpu.VMEM((2, 4 * rows, fh), BF),
            pltpu.VMEM(block, BF),
            pltpu.VMEM(block[1:], BF),
            pltpu.VMEM((3, rows, D), BF),
            pltpu.VMEM(block[1:], BF),
            pltpu.VMEM((3, rows, D), BF),
            pltpu.VMEM((tokens, D), F32),
            pltpu.VMEM((tokens, D), BF),
            pltpu.VMEM((tokens, 2 * fl), BF),
            pltpu.VMEM((2, 4 * rows, 2 * fh), BF),
            pltpu.VMEM((tokens, D), F32),
            DMA((2, 3)),
            DMA((2, 3)),
            DMA((2, 4)),
            DMA((2, 4)),
            DMA((2, 3)),
            DMA((2, 3)),
            DMA((2,)),
            DMA((2,)),
        ],
        5,
    )


def pair_masks(scale):
    lane = lax.broadcasted_iota(jnp.int32, (1, 2 * DH), 1)
    left = jnp.where(lane < DH, scale, 0.0).astype(BF)
    right = jnp.where(lane < DH, 0.0, scale).astype(BF)
    return left, right


def both(value, masks):
    return jnp.concatenate([value * masks[0], value * masks[1]], axis=0)


def side(stacked):
    rows = stacked.shape[0] // 2
    return jnp.concatenate([stacked[:rows], stacked[rows:]], axis=1)


def pair_forward(q, k, v, bias, ones, scaled):
    scores = dot_back(both(q, scaled), k) + bias
    top = jnp.max(scores, axis=-1, keepdims=True)
    shifted = jnp.exp(scores - top)
    total = jnp.sum(shifted, axis=-1, keepdims=True)
    prob = (shifted / total).astype(BF)
    return dot(side(prob), both(v, ones)).astype(BF), top + jnp.log(total)


def pair_backward(q, k, v, bias, lse, d_out, ones, scaled):
    q2 = both(q, scaled)
    d2 = both(d_out, ones)
    prob = jnp.exp(dot_back(q2, k) + bias - lse)
    d_prob = dot_back(d2, v)
    row = jnp.sum(prob * d_prob, axis=-1, keepdims=True)
    d_scores = (prob * (d_prob - row)).astype(BF)
    dq = dot(side(d_scores), both(k, scaled))
    return dq, dot_grad(d_scores, q2), dot_grad(prob.astype(BF), d2)


def reach_bias(key_bias):
    shape = (WIN, 3 * WIN)
    offset = lax.broadcasted_iota(jnp.int32, shape, 1) - lax.broadcasted_iota(jnp.int32, shape, 0) - WIN
    near = (offset >= -WIN) & (offset <= WIN)
    inner = jnp.where(offset == 0, 0.0, jnp.broadcast_to(key_bias, shape))
    bias = jnp.where(near, inner, MASKED)
    return jnp.concatenate([bias, bias], axis=0)


def put_lse(lse, pair, column):
    lane = lax.broadcasted_iota(jnp.int32, lse.shape, 1)
    rows = lse.shape[0]
    lse = jnp.where(lane == 2 * pair, column[:rows], lse)
    return jnp.where(lane == 2 * pair + 1, column[rows:], lse)


def get_lse(lse, pair):
    return jnp.concatenate([lse[:, 2 * pair : 2 * pair + 1], lse[:, 2 * pair + 1 : 2 * pair + 2]], axis=0)


def attend_body(
    stages,
    x,
    gain,
    select,
    select_t,
    key_bias,
    heavy_bias,
    w_lqkv,
    w_hqkv,
    w_lout,
    w_hout,
    hidden,
    xn,
    lq,
    rim,
    lo_out,
    l_lse,
    a_rows,
    hq,
    kvh,
    ho,
    h_lse,
    ls,
    lr,
    rs,
    rr,
    ss,
    sr,
):
    hi, lo, x_, c = place()
    f = x_ * 2 + c
    tokens = x.shape[0]
    group, cap, width = select.shape
    wl, wh = HL * DH, HH * DH
    ones, scaled = pair_masks(1.0), pair_masks(SCORE_SCALE)
    across, partner = at(hi, lo, 1 - x_, c), at(hi, lo, x_, 1 - c)

    def norm(r):
        h = x[r, :].astype(F32)
        inv = lax.rsqrt(jnp.mean(h * h, axis=-1, keepdims=True) + EPSILON)
        xn[r, :] = (h * inv * gain[0:1, :]).astype(BF)

    tiles(tokens, 128, norm)
    for s in range(group):
        rows = dot(select[s], xn[s * width : (s + 1) * width, :]).astype(BF)
        a_rows[s * cap : (s + 1) * cap, :] = rows
    stages[0]()
    kv = dot(a_rows[...], w_hqkv[:, wh:]).astype(BF)
    for s in range(group):
        kvh[s, f] = kv[s * cap : (s + 1) * cap]
    mine = kvh.at[:, f]
    first = send(mine, mine, ss.at[0], sr.at[0], across)
    beside = send(mine, mine, ss.at[1], sr.at[1], partner)
    stages[1]()
    for s in range(group):
        rows = xn[s * width : (s + 1) * width, :]
        rim[s, WIN : WIN + width, :] = dot(rows, w_lqkv[:, wl:]).astype(BF)
    finish = rim_exchange(
        rim.at[:, pl.ds(WIN, WIN)],
        rim.at[:, pl.ds(width, WIN)],
        rim.at[:, pl.ds(0, WIN)],
        rim.at[:, pl.ds(width + WIN, WIN)],
        ls,
        lr,
        rs,
        rr,
    )
    hq[...] = dot(a_rows[...], w_hqkv[:, :wh]).astype(BF)
    for s in range(group):
        rows = slice(s * width, (s + 1) * width)
        lq[rows, :] = dot(xn[rows, :], w_lqkv[:, :wl]).astype(BF)
    stages[2]()
    first.wait()
    other = kvh.at[:, (1 - x_) * 2 + c]
    relay = send(other, other, ss.at[2], sr.at[2], partner)
    finish()
    blocks = width // WIN

    def light(i, carry):
        s, b = i // blocks, i % blocks
        r = pl.ds(pl.multiple_of(i * WIN, WIN), WIN)
        keys = pl.ds(pl.multiple_of(b * WIN, WIN), 3 * WIN)
        bias = reach_bias(key_bias[i])
        lse = jnp.zeros((WIN, 128), F32)
        for pair in range(HL // 2):
            at_k = slice(pair * 128, (pair + 1) * 128)
            at_v = slice(wl + pair * 128, wl + (pair + 1) * 128)
            o, column = pair_forward(
                lq[r, at_k], rim[s, keys, at_k], rim[s, keys, at_v], bias, ones, scaled
            )
            lo_out[r, at_k] = o
            lse = put_lse(lse, pair, column)
        l_lse[r, :] = lse
        return carry

    lax.fori_loop(0, group * blocks // 2, light, 0)
    stages[3]()
    lax.fori_loop(group * blocks // 2, group * blocks, light, 0)
    stages[4]()
    beside.wait()
    relay.wait()
    heavy_kv = kvh.reshape(group, 4 * cap, 2 * wh)

    def heavy(s, carry):
        r = pl.ds(pl.multiple_of(s * cap, cap), cap)
        bias = heavy_bias[s]
        bias = jnp.concatenate([bias, bias], axis=0)
        lse = jnp.zeros((cap, 128), F32)
        for pair in range(HH // 2):
            at_k = slice(pair * 128, (pair + 1) * 128)
            at_v = slice(wh + pair * 128, wh + (pair + 1) * 128)
            o, column = pair_forward(
                hq[r, at_k], heavy_kv[s, :, at_k], heavy_kv[s, :, at_v], bias, ones, scaled
            )
            ho[r, at_k] = o
            lse = put_lse(lse, pair, column)
        h_lse[r, :] = lse
        return carry

    lax.fori_loop(0, group, heavy, 0)
    stages[5]()
    high, low = halves(dot(ho[...], w_hout[...]))
    for s in range(group):
        r = slice(s * width, (s + 1) * width)
        q = slice(s * cap, (s + 1) * cap)
        hidden[r, :] = (
            x[r, :].astype(F32)
            + dot(lo_out[r, :], w_lout[...])
            + (dot(select_t[s], high[q]) + dot(select_t[s], low[q]))
        )


def attend_kernel(*refs):
    meet(line_peers())
    attend_body([lambda: None] * 6, *refs)


def attend_shapes(tokens, select):
    group, cap, width = select.shape
    wl, wh = HL * DH, HH * DH
    rows = group * cap
    return [
        jax.ShapeDtypeStruct((tokens, D), F32),
        jax.ShapeDtypeStruct((tokens, D), BF),
        jax.ShapeDtypeStruct((tokens, wl), BF),
        jax.ShapeDtypeStruct((group, width + 2 * WIN, 2 * wl), BF),
        jax.ShapeDtypeStruct((tokens, wl), BF),
        jax.ShapeDtypeStruct((tokens, 128), F32),
        jax.ShapeDtypeStruct((rows, D), BF),
        jax.ShapeDtypeStruct((rows, wh), BF),
        jax.ShapeDtypeStruct((group, 4, cap, 2 * wh), BF),
        jax.ShapeDtypeStruct((rows, wh), BF),
        jax.ShapeDtypeStruct((rows, 128), F32),
    ]


ATTEND_SEMS = [DMA, DMA, DMA, DMA, DMA((3,)), DMA((3,))]


def attend(x, gain, select, select_t, key_bias, heavy_bias, w_lqkv, w_hqkv, w_lout, w_hout):
    operands = [x, gain, select, select_t, key_bias, heavy_bias, w_lqkv, w_hqkv, w_lout, w_hout]
    shapes = attend_shapes(x.shape[0], select)
    return call(
        attend_kernel,
        shapes,
        operands,
        [VM] * len(operands),
        [VM] * len(shapes),
        ATTEND_SEMS,
        2,
    )


def gather_attend_kernel(dp, nw, *refs):
    n_in, n_out = 7 + nw, 3 + nw + 12
    ins, outs, rest = refs[:n_in], refs[n_in : n_in + n_out], refs[n_in + n_out :]
    xin, ws, hin, hdn = ins[0], ins[1 : 1 + nw], ins[1 + nw], ins[2 + nw]
    masks = ins[3 + nw :]
    xo, wos, hin_o, hdn_o = outs[0], outs[1 : 1 + nw], outs[1 + nw], outs[2 + nw]
    gain, saved = outs[3 + nw], outs[4 + nw :]
    g = Gather(dp, xin, ws, hin, hdn, xo, wos, hin_o, hdn_o, rest[:11])
    g.meet()
    g.rows()
    for w in (0, 1, 2):
        g.line(w)
    g.heavy_plane()
    for w in (0, 1, 2):
        g.plane(w)
    for w in (3, 4, 5, 6):
        g.line(w)
    g.heavy_line()
    g.cross(0)
    g.core(0)
    g.cross(1)
    g.cross(2)
    g.ready(0)
    total = jnp.zeros(gain.shape, F32)
    for z in range(dp // 2):
        for l2, x2 in ((0, 0), (0, 1), (1, 0), (1, 1)):
            pair = wos[0][z, l2, x2].astype(F32)
            total += pair[:8] + pair[8:]
    gain[...] = total
    g.rows_ready()

    def heavy_projection():
        g.core(1)
        g.core(2)
        g.ready(2)

    def keys_travel():
        g.plane(3)
        g.plane(4)

    def half_way():
        g.cross(3)
        g.cross(4)
        g.plane(5)

    def light_done():
        g.core(3)
        g.core(4)
        g.cross(5)
        g.plane(6)

    def heavy_done():
        g.ready(3)
        g.ready(4)
        g.core(5)
        g.cross(6)

    full = [wos[w].reshape(-1, wos[w].shape[-1]) for w in range(nw)]
    stages = [heavy_projection, lambda: g.ready(1), keys_travel, half_way, light_done, heavy_done]
    attend_body(
        stages,
        xo.reshape(-1, D),
        gain,
        *masks,
        full[1],
        full[2],
        full[3],
        full[4],
        *saved,
        *rest[11:],
    )
    g.core(6)
    g.ready(5)
    g.ready(6)
    g.heavy_ready()


def gather_attend(dp, xin, weights, hin, hdn, masks):
    nw = len(weights)
    shapes = gather_shapes(dp, xin, weights, hin, hdn, True)
    tokens = shapes[0].shape[0] * dp * xin.shape[1]
    shapes.append(jax.ShapeDtypeStruct((8, D), F32))
    shapes += attend_shapes(tokens, masks[0])
    return call(
        functools.partial(gather_attend_kernel, dp, nw),
        shapes,
        [xin, *weights, hin, hdn, *masks],
        [ANY] * (3 + nw) + [VM] * 4,
        [VM] * 6 + [ANY] * 4 + [VM] * 12,
        gather_sems(dp, nw) + ATTEND_SEMS,
        1,
    )


def attend_back_kernel(
    d_hidden,
    x,
    gain,
    select,
    select_t,
    key_bias,
    heavy_bias,
    w_lqkv,
    w_hqkv,
    w_lout,
    w_hout,
    xn,
    lq,
    rim,
    lo_out,
    l_lse,
    a_rows,
    hq,
    kvh,
    ho,
    h_lse,
    g_lqkv,
    g_hqkv,
    g_lout,
    g_hout,
    dx,
    stats,
    d_ho,
    d_hproj,
    part,
    got,
    far,
    d_la,
    d_lo,
    d_rim,
    edge,
    edge_in,
    d_lproj,
    d_xn,
    ls,
    lr,
    rs,
    rr,
    ss,
    sr,
):
    hi, lo, x_, c = place()
    meet(line_peers())
    tokens = x.shape[0]
    group, cap, width = select.shape
    wl, wh = HL * DH, HH * DH
    ones, scaled = pair_masks(1.0), pair_masks(SCORE_SCALE)
    across, partner = at(hi, lo, 1 - x_, c), at(hi, lo, x_, 1 - c)
    picked = []
    for s in range(group):
        high, low = halves(d_hidden[s * width : (s + 1) * width, :])
        picked.append((dot(select[s], high) + dot(select[s], low)).astype(BF))
    d_ha = jnp.concatenate(picked, axis=0)
    d_ho[...] = dot_back(d_ha, w_hout[...]).astype(BF)
    heavy_kv = kvh.reshape(group, 4 * cap, 2 * wh)
    part_kv = part.reshape(group, 4 * cap, 2 * wh)

    def heavy(s, carry):
        r = pl.ds(pl.multiple_of(s * cap, cap), cap)
        bias = heavy_bias[s]
        bias = jnp.concatenate([bias, bias], axis=0)
        lse = h_lse[r, :]
        for pair in range(HH // 2):
            at_k = slice(pair * 128, (pair + 1) * 128)
            at_v = slice(wh + pair * 128, wh + (pair + 1) * 128)
            dq, dk, dv = pair_backward(
                hq[r, at_k],
                heavy_kv[s, :, at_k],
                heavy_kv[s, :, at_v],
                bias,
                get_lse(lse, pair),
                d_ho[r, at_k],
                ones,
                scaled,
            )
            d_hproj[r, at_k] = dq.astype(BF)
            part_kv[s, :, at_k] = dk.astype(BF)
            part_kv[s, :, at_v] = dv.astype(BF)
        return carry

    lax.fori_loop(0, group, heavy, 0)
    beside = [
        send(part.at[:, b * 2 + 1 - c], got.at[b], ss.at[b], sr.at[b], partner) for b in (0, 1)
    ]
    g_hout[...] = dot_grad(ho[...], d_ha).astype(BF)

    def light_out_back(r):
        d = d_hidden[r, :].astype(BF)
        d_la[r, :] = d
        d_lo[r, :] = dot_back(d, w_lout[...]).astype(BF)

    tiles(tokens, 256, light_out_back)
    for copy in beside:
        copy.wait()
    for b in (0, 1):
        got[b] = (got[b].astype(F32) + part[:, b * 2 + c].astype(F32)).astype(BF)
    third = send(got.at[1 - x_], far, ss.at[2], sr.at[2], across)
    d_rim[...] = jnp.zeros(d_rim.shape, F32)
    blocks = width // WIN

    def light(i, carry):
        s, b = i // blocks, i % blocks
        r = pl.ds(pl.multiple_of(i * WIN, WIN), WIN)
        keys = pl.ds(pl.multiple_of(b * WIN, WIN), 3 * WIN)
        bias = reach_bias(key_bias[i])
        lse = l_lse[r, :]
        for pair in range(HL // 2):
            at_k = slice(pair * 128, (pair + 1) * 128)
            at_v = slice(wl + pair * 128, wl + (pair + 1) * 128)
            dq, dk, dv = pair_backward(
                lq[r, at_k],
                rim[s, keys, at_k],
                rim[s, keys, at_v],
                bias,
                get_lse(lse, pair),
                d_lo[r, at_k],
                ones,
                scaled,
            )
            d_lproj[r, at_k] = dq.astype(BF)
            d_rim[s, keys, at_k] += dk
            d_rim[s, keys, at_v] += dv
        return carry

    lax.fori_loop(0, group * blocks, light, 0)
    edge[0] = d_rim[:, :WIN, :].astype(BF)
    edge[1] = d_rim[:, WIN + width :, :].astype(BF)
    finish = rim_exchange(
        edge.at[0], edge.at[1], edge_in.at[0], edge_in.at[1], ls, lr, rs, rr
    )
    g_lout[...] = dot_grad(lo_out[...], d_la[...]).astype(BF)
    third.wait()
    total = (got[x_].astype(F32) + far[...].astype(F32)).astype(BF)
    for s in range(group):
        d_hproj[s * cap : (s + 1) * cap, wh:] = total[s]

    def heavy_grad(j):
        g_hqkv[:, j] = dot_grad(a_rows[...], d_hproj[:, j]).astype(BF)

    tiles(3 * wh, 768, heavy_grad)
    d_high, d_low = halves(dot_back(d_hproj[...], w_hqkv[...]))
    finish()
    for s in range(group):
        d_rim[s, WIN : 2 * WIN, :] += edge_in[0, s].astype(F32)
        d_rim[s, width : width + WIN, :] += edge_in[1, s].astype(F32)
        d_lproj[s * width : (s + 1) * width, wl:] = d_rim[s, WIN : WIN + width, :].astype(BF)

    def light_grad(j):
        g_lqkv[:, j] = dot_grad(xn[...], d_lproj[:, j]).astype(BF)

    tiles(3 * wl, 768, light_grad)
    for s in range(group):
        r = slice(s * width, (s + 1) * width)
        q = slice(s * cap, (s + 1) * cap)
        d_xn[r, :] = dot_back(d_lproj[r, :], w_lqkv[...]) + (
            dot(select_t[s], d_high[q]) + dot(select_t[s], d_low[q])
        )
    stats[...] = jnp.zeros(stats.shape, F32)

    def norm_back(r):
        h = x[r, :].astype(F32)
        inv = lax.rsqrt(jnp.mean(h * h, axis=-1, keepdims=True) + EPSILON)
        d = d_xn[r, :]
        dh = d * h
        stats[0:1, :] += jnp.sum(dh * inv, axis=0, keepdims=True)
        mean = jnp.mean(gain[0:1, :] * dh, axis=-1, keepdims=True)
        dx[r, :] = (
            d_hidden[r, :] + inv * gain[0:1, :] * d - h * (inv * inv * inv * mean)
        ).astype(BF)

    tiles(tokens, 128, norm_back)


def attend_back(d_hidden, x, gain, select, select_t, key_bias, heavy_bias, weights, saved):
    tokens = x.shape[0]
    group, cap, width = select.shape
    wl, wh = HL * DH, HH * DH
    rows = group * cap
    operands = [d_hidden, x, gain, select, select_t, key_bias, heavy_bias, *weights, *saved]
    shapes = [
        jax.ShapeDtypeStruct((D, 3 * wl), BF),
        jax.ShapeDtypeStruct((D, 3 * wh), BF),
        jax.ShapeDtypeStruct((wl, D), BF),
        jax.ShapeDtypeStruct((wh, D), BF),
        jax.ShapeDtypeStruct((tokens, D), BF),
        jax.ShapeDtypeStruct((8, D), F32),
    ]
    return call(
        attend_back_kernel,
        shapes,
        operands,
        [VM] * len(operands),
        [VM] * len(shapes),
        [
            pltpu.VMEM((rows, wh), BF),
            pltpu.VMEM((rows, 3 * wh), BF),
            pltpu.VMEM((group, 4, cap, 2 * wh), BF),
            pltpu.VMEM((2, group, cap, 2 * wh), BF),
            pltpu.VMEM((group, cap, 2 * wh), BF),
            pltpu.VMEM((tokens, D), BF),
            pltpu.VMEM((tokens, wl), BF),
            pltpu.VMEM((group, width + 2 * WIN, 2 * wl), F32),
            pltpu.VMEM((2, group, WIN, 2 * wl), BF),
            pltpu.VMEM((2, group, WIN, 2 * wl), BF),
            pltpu.VMEM((tokens, 3 * wl), BF),
            pltpu.VMEM((tokens, D), F32),
            DMA,
            DMA,
            DMA,
            DMA,
            DMA((3,)),
            DMA((3,)),
        ],
        3,
    )


def scatter_kernel(dp, nw, *refs):
    nz = dp // 2
    dx, stats, gs, hin, hdn = refs[0], refs[1], refs[2 : 2 + nw], refs[2 + nw], refs[3 + nw]
    outs = refs[4 + nw :]
    dxo, total, gos, hin_o, hdn_o = outs[0], outs[1], outs[2 : 2 + nw], outs[2 + nw], outs[3 + nw]
    scr = outs[4 + nw :]
    nears, fars, sums, ends = (scr[i * nw : (i + 1) * nw] for i in range(4))
    hin_r, hin_s, hdn_r, sc, sp, sz, acc, acc2 = scr[4 * nw : 4 * nw + 8]
    own, xs, xr, cs, cr, ps, pr, zs, zr, hs, hr, ts, tr = scr[4 * nw + 8 :]
    hi, lo, x, c = place()
    d = hi * 2 + lo
    f = x * 2 + c
    plane = (lo * 2 + x) * 2 + c
    dp_peers = [(lax.rem(d + k, dp), f) for k in range(1, dp)]
    rest = [(a, b, e) for a in (0, 1) for b in (0, 1) for e in (0, 1) if a or b or e]
    flat8 = []
    for a, b, e in rest:
        l2 = 1 - lo if a else lo
        x2 = 1 - x if b else x
        c2 = 1 - c if e else c
        flat8.append((l2, x2, c2))
    meet(dp_peers + [at(hi, *p) for (a, b, e), p in zip(rest, flat8) if b or e])
    partner = at(hi, lo, x, 1 - c)
    quad = quad_peers()
    z_index = [lax.rem(hi + k, nz) for k in range(1, nz)]
    z_peers = [at(z, lo, x, c) for z in z_index]
    c_sends = [
        send(gs[w].at[:, :, :, 1 - c], nears[w], cs.at[w], cr.at[w], partner) for w in range(nw)
    ]
    t_c = send(stats, sc, ts.at[0], tr.at[0], partner)
    mine = keep(dx.at[:, d], dxo.at[d], own)
    x_sends = [
        send(dx.at[:, peer[0]], dxo.at[d], xs.at[k], xr.at[k], peer)
        for k, peer in enumerate(dp_peers)
    ]
    h_sends = []
    for k, z in enumerate(z_index):
        h_sends.append(send(hin.at[z], hin_r.at[k], hs.at[1, k], hr.at[1, k], z_peers[k]))
        h_sends.append(send(hdn.at[z], hdn_r.at[k], hs.at[2, k], hr.at[2, k], z_peers[k]))
    p_sends, z_sends = [], []
    t_c.wait()
    acc[...] = stats[...] + sc[...]
    t_p = [
        send(acc, sp.at[k], ts.at[1 + k], tr.at[1 + k], at(hi, l2, x2, c))
        for k, (l2, x2) in enumerate(quad)
    ]

    def add_core(w):
        c_sends[w].wait()
        near, g = nears[w], gs[w]

        def body(i, carry):
            z, a, b = i // 4, (i // 2) % 2, i % 2
            near[z, a, b] = (near[z, a, b].astype(F32) + g[z, a, b, c].astype(F32)).astype(BF)
            return carry

        lax.fori_loop(0, nz * 4, body, 0)
        p_sends.append(
            [
                send(near.at[:, l2, x2], fars[w].at[k], ps.at[w, k], pr.at[w, k], at(hi, l2, x2, c))
                for k, (l2, x2) in enumerate(quad)
            ]
        )

    def add_plane(w):
        for copy in p_sends[w]:
            copy.wait()
        near, far, part = nears[w], fars[w], sums[w]

        def body(z, carry):
            part[z] = (
                near[z, lo, x].astype(F32)
                + far[0, z].astype(F32)
                + far[1, z].astype(F32)
                + far[2, z].astype(F32)
            ).astype(BF)
            return carry

        lax.fori_loop(0, nz, body, 0)
        z_sends.append(
            [
                send(part.at[z], ends[w].at[k], zs.at[w, k], zr.at[w, k], z_peers[k])
                for k, z in enumerate(z_index)
            ]
        )

    def add_line(w):
        for copy in z_sends[w]:
            copy.wait()
        gos[w][...] = sums[w][hi].astype(F32)
        for k in range(nz - 1):
            gos[w][...] += ends[w][k].astype(F32)

    for w in range(nw):
        add_core(w)
        if w >= 2:
            add_plane(w - 2)
    for copy in t_p:
        copy.wait()
    acc2[...] = acc[...] + sp[0] + sp[1] + sp[2]
    t_z = [send(acc2, sz.at[k], ts.at[4 + k], tr.at[4 + k], z_peers[k]) for k in range(nz - 1)]
    for copy in h_sends:
        copy.wait()

    def body(i, carry):
        value = hin[hi, i].astype(F32)
        for k in range(nz - 1):
            value += hin_r[k, i].astype(F32)
        hin_s[i] = value.astype(BF)
        return carry

    lax.fori_loop(0, 8, body, 0)
    hin_o[plane] = hin_s[plane]
    a_sends = [
        send(
            hin_s.at[(l2 * 2 + x2) * 2 + c2],
            hin_o.at[plane],
            hs.at[0, k],
            hr.at[0, k],
            at(hi, l2, x2, c2),
        )
        for k, (l2, x2, c2) in enumerate(flat8)
    ]
    hdn_o[...] = hdn[hi].astype(F32)
    for k in range(nz - 1):
        hdn_o[...] += hdn_r[k].astype(F32)
    for w in range(max(nw - 2, 0), nw):
        add_plane(w)
    for copy in t_z:
        copy.wait()
    total[...] = acc2[...]
    for k in range(nz - 1):
        total[...] += sz[k]
    for w in range(nw):
        add_line(w)
    mine.wait()
    for copy in x_sends + a_sends:
        copy.wait()


def scatter_all(dp, dx, stats, grads, hin, hdn):
    nz = dp // 2
    nw = len(grads)
    group, _, rows, _ = dx.shape
    tiles = [g.shape[4:] for g in grads]
    most = max(7, nz)
    scratch = [pltpu.VMEM((nz, 2, 2) + t, BF) for t in tiles]
    scratch += [pltpu.VMEM((3, nz) + t, BF) for t in tiles]
    scratch += [pltpu.VMEM((nz,) + t, BF) for t in tiles]
    scratch += [pltpu.VMEM((nz - 1,) + t, BF) for t in tiles]
    scratch += [
        pltpu.VMEM((nz - 1,) + hin.shape[1:], BF),
        pltpu.VMEM(hin.shape[1:], BF),
        pltpu.VMEM((nz - 1,) + hdn.shape[1:], BF),
        pltpu.VMEM(stats.shape, F32),
        pltpu.VMEM((3,) + stats.shape, F32),
        pltpu.VMEM((nz - 1,) + stats.shape, F32),
        pltpu.VMEM(stats.shape, F32),
        pltpu.VMEM(stats.shape, F32),
        DMA,
        DMA((dp,)),
        DMA((dp,)),
        DMA((nw,)),
        DMA((nw,)),
        DMA((nw, 3)),
        DMA((nw, 3)),
        DMA((nw, nz)),
        DMA((nw, nz)),
        DMA((3, most)),
        DMA((3, most)),
        DMA((4 + nz,)),
        DMA((4 + nz,)),
    ]
    shapes = [jax.ShapeDtypeStruct((dp, group, rows, D), BF), jax.ShapeDtypeStruct(stats.shape, F32)]
    shapes += [jax.ShapeDtypeStruct(t, F32) for t in tiles]
    shapes.append(jax.ShapeDtypeStruct(hin.shape[1:], BF))
    shapes.append(jax.ShapeDtypeStruct(hdn.shape[1:], F32))
    return call(
        functools.partial(scatter_kernel, dp, nw),
        shapes,
        [dx, stats, *grads, hin, hdn],
        [ANY] + [VM] * (3 + nw),
        [ANY] + [VM] * (3 + nw),
        scratch,
        4,
    )


def routing(routes, pieces, piece_len):
    places = jnp.arange(pieces * piece_len)
    routed = jnp.any(routes[:, None, :] == places[None, :, None], axis=-1)
    routed = routed.reshape(-1, pieces, piece_len)
    before = jnp.arange(piece_len)[:, None] < jnp.arange(piece_len)[None, :]
    rank = jnp.einsum(
        "skp,pq->skq", routed.astype(BF), before.astype(BF), preferred_element_type=F32
    )
    slots = jnp.arange(CAP, dtype=F32)
    hot = routed[:, :, None, :] & (rank[:, :, None, :] == slots[None, None, :, None])
    filled = jnp.any(hot, axis=-1)
    spots = jnp.sum(jnp.where(hot, places.reshape(1, pieces, 1, piece_len), 0), axis=-1)
    return hot, jnp.where(filled, spots, -1)


def local(
    layer_input,
    teacher,
    lengths,
    dealing,
    attn_routes,
    ffn_routes,
    ffn_scores,
    gain_attn,
    gain_ffn,
    light_qkv,
    light_out,
    heavy_qkv,
    heavy_out,
    light_in,
    light_down,
    heavy_in,
    heavy_down,
):
    dp = lax.axis_size("dp")
    pieces = lax.axis_size("fsdp")
    data_index = lax.axis_index("dp")
    piece = lax.axis_index("fsdp")
    nz = dp // 2
    n = dp * pieces
    seqs = dealing.shape[0]
    group = seqs // dp
    gain_len = gain_attn.shape[0]
    hidden_units = heavy_in.shape[1] // 2 // n
    xin = deal_rows(dealing, layer_input[:, 0])
    mine = data_index * pieces + piece
    owned = jnp.arange(D)[None, :] // gain_len == mine
    spread_out = jnp.broadcast_to(
        jnp.stack([gain_attn, gain_ffn])[:, None, :], (2, D // gain_len, gain_len)
    ).reshape(2, D)
    gains = jnp.pad(jnp.where(owned, spread_out, 0.0).astype(BF), ((0, 6), (0, 0)))
    matrices = (light_qkv, heavy_qkv, light_out, heavy_out, light_in, light_down)
    hin_rows = heavy_in.shape[0]
    hin_src = (
        heavy_in.reshape(hin_rows, 2, nz, 8, hidden_units)
        .transpose(3, 0, 1, 2, 4)
        .reshape(8, hin_rows, 2 * nz * hidden_units)
    )
    if hin_rows % 8:
        hin_src = hin_src.reshape(8, -1, 128)
    tokens = layer_input.shape[2] * dp
    chosen = lax.dynamic_slice_in_dim(dealing, data_index * group, group)
    one = (chosen[:, None] == jnp.arange(seqs)[None, :])
    seq_lengths = jnp.sum(jnp.where(one, lengths[None, :], 0), axis=1)
    attn_pick = jnp.sum(jnp.where(one[:, :, None], attn_routes[None], 0), axis=1)
    ffn_pick = jnp.sum(jnp.where(one[:, :, None], ffn_routes[None], 0), axis=1)
    score_pick = jnp.sum(jnp.where(one[:, :, None], ffn_scores[None], 0.0), axis=1)
    token_count = jnp.sum(lengths).astype(F32)
    positions = piece * tokens + jnp.arange(tokens)
    valid_mask = positions[None, :] < seq_lengths[:, None]
    a_hot, a_spots = routing(attn_pick, pieces, tokens)
    f_hot, f_spots = routing(ffn_pick, pieces, tokens)
    a_select = lax.dynamic_index_in_dim(a_hot, piece, 1, False).astype(BF)
    f_select = lax.dynamic_index_in_dim(f_hot, piece, 1, False).astype(BF)
    a_spot = lax.dynamic_index_in_dim(a_spots, piece, 1, False)
    f_spot = lax.dynamic_index_in_dim(f_spots, piece, 1, False)
    slot_score = jnp.sum(
        jnp.where(f_spot[:, :, None] == ffn_pick[:, None, :], score_pick[:, None, :], 0.0), axis=-1
    )
    key_pos = piece * tokens - WIN + jnp.arange(tokens + 2 * WIN)
    live_key = (key_pos >= 0)[None, :] & (key_pos[None, :] < seq_lengths[:, None])
    key_line = jnp.where(live_key, 0.0, MASKED)
    key_bias = jnp.stack(
        [key_line[:, b : b + 3 * WIN] for b in range(0, tokens, WIN)], axis=1
    ).reshape(-1, 1, 3 * WIN)
    all_spots = a_spots.reshape(group, pieces * CAP)
    heavy_allowed = ((all_spots >= 0) & (all_spots < seq_lengths[:, None]))[:, None, :] | (
        a_spot[:, :, None] == all_spots[:, None, :]
    )
    heavy_bias = jnp.where(heavy_allowed, 0.0, MASKED)
    masks = (a_select, a_select.swapaxes(1, 2), key_bias, heavy_bias)
    sources = (xin, [gains] + [packed(m) for m in matrices], hin_src, heavy_down)
    merged = all(m.shape[0] % 8 == 0 for m in (*matrices, heavy_in, heavy_down, layer_input[0, 0]))
    if merged:
        got = gather_attend(dp, *sources, masks)
    else:
        got = gather_all(dp, *sources)
    flat_x = got[0].reshape(-1, D)
    w_lqkv, w_hqkv, w_lout, w_hout, w_lin, w_ldown = (
        unpacked(full, *m.shape) for full, m in zip(got[2:8], matrices)
    )
    w_hin = unpacked(got[8], hin_rows, 2 * nz * hidden_units)
    w_hdown = got[9].reshape(-1, D)
    attn_weights = (w_lqkv, w_hqkv, w_lout, w_hout)
    if merged:
        gain, hidden, *saved = got[10:]
    else:
        gain = jnp.sum(got[1].reshape(n, 8, D).astype(F32), axis=0)
        hidden, *saved = attend(flat_x, gain, *masks, *attn_weights)
    weight_mask = valid_mask.reshape(-1, 1).astype(F32)
    grad_lin, grad_ldown, grad_hin, grad_hdown, d_hidden, ffn_stats = feed_forward(
        hidden,
        f_select,
        f_select.swapaxes(1, 2),
        slot_score.reshape(-1, 1),
        gain,
        teacher.reshape(-1, D),
        weight_mask,
        2.0 * weight_mask / (D * token_count),
        w_lin,
        w_ldown,
        w_hin,
        w_hdown,
    )
    grad_lqkv, grad_hqkv, grad_lout, grad_hout, d_inputs, attn_stats = attend_back(
        d_hidden, flat_x, gain, *masks, attn_weights, saved
    )
    rows = tokens // dp
    stats = jnp.concatenate(
        [
            attn_stats[0].reshape(-1, 128),
            ffn_stats[0].reshape(-1, 128),
            jnp.broadcast_to(jnp.sum(ffn_stats[1]), (4, 128)),
        ]
    )
    grads = (grad_lin, grad_ldown, grad_hout, grad_lout, grad_hqkv, grad_lqkv)
    shards = (light_in, light_down, heavy_out, light_out, heavy_qkv, light_qkv)
    sent = [
        packed_full(grad.astype(BF), shard.shape, nz) for grad, shard in zip(grads, shards)
    ]
    hin_tile = hin_src.shape[1:]
    done = scatter_all(
        dp,
        d_inputs.reshape(group, dp, rows, D),
        stats,
        sent,
        grad_hin.astype(BF).reshape((nz, 8) + hin_tile),
        grad_hdown.astype(BF).reshape(nz, -1, D),
    )
    d_layer = undeal_rows(dealing, done[0].reshape(seqs, rows, D))[:, None]
    summed = done[1]
    loss_value = summed[12, 0] / (D * token_count)
    own_one = lax.dynamic_slice_in_dim(summed[:6].reshape(-1), mine * gain_len, gain_len)
    own_two = lax.dynamic_slice_in_dim(summed[6:12].reshape(-1), mine * gain_len, gain_len)
    g_lin, g_ldown, g_hout, g_lout, g_hqkv, g_lqkv = (
        full.reshape(shard.shape) for full, shard in zip(done[2:8], shards)
    )
    g_hin = (
        done[8]
        .astype(F32)
        .reshape(8, hin_rows, 2, nz, hidden_units)
        .transpose(1, 2, 3, 0, 4)
        .reshape(heavy_in.shape)
    )
    return (
        loss_value,
        d_layer,
        own_one,
        own_two,
        g_lqkv,
        g_lout,
        g_hqkv,
        g_hout,
        g_lin,
        g_ldown,
        g_hin,
        done[9].reshape(heavy_down.shape),
    )


def packed_full(grad, shard_shape, nz):
    rows, columns = shard_shape
    if rows % 8 == 0:
        return grad.reshape(nz, 2, 2, 2, rows, columns)
    return grad.reshape(nz, 2, 2, 2, rows * columns // 128, 128)


def solution(mesh):
    split = P(("dp", "fsdp"))
    matrix = P(("dp", "fsdp"), None)
    placed = (
        P(None, "fsdp", "dp", None),
        P("dp", "fsdp", None, None),
        P(),
        P(),
        P(),
        P(),
        P(),
        split,
        split,
    ) + (matrix,) * 8
    return jax.shard_map(
        local,
        mesh=mesh,
        in_specs=placed,
        out_specs=(P(), P(None, "fsdp", "dp", None), split, split) + (matrix,) * 8,
        check_vma=False,
    )
```

```python
import functools
import jax
import jax.numpy as jnp
from jax import lax
from jax.experimental import pallas as pl
from jax.experimental.pallas import tpu as pltpu
from jax.sharding import PartitionSpec as P

D = 768
HL = 8
HH = 12
DH = 64
FL = 1024
FH = 4096
WIN = 128
CAP = 64

EPSILON = 1e-06
MASKED = -1000000000.0
SCORE_SCALE = 0.125
MESH = pl.DeviceIdType.MESH
BF = jnp.bfloat16
F32 = jnp.float32
ANY = pl.BlockSpec(memory_space=pl.ANY)
VM = pl.BlockSpec(memory_space=pltpu.VMEM)
DMA = pltpu.SemaphoreType.DMA
VMEM_BYTES = 60 * 1024 * 1024


def place():
    d = lax.axis_index("dp")
    f = lax.axis_index("fsdp")
    return d // 2, d % 2, f // 2, f % 2


def at(hi, lo, x, c):
    return (hi * 2 + lo, x * 2 + c)


def meet(peers):
    barrier = pltpu.get_barrier_semaphore()
    for peer in peers:
        pl.semaphore_signal(barrier, inc=1, device_id=peer, device_id_type=MESH)
    pl.semaphore_wait(barrier, len(peers))


def send(src, dst, send_sem, recv_sem, peer):
    copy = pltpu.make_async_remote_copy(
        src_ref=src,
        dst_ref=dst,
        send_sem=send_sem,
        recv_sem=recv_sem,
        device_id=peer,
        device_id_type=MESH,
    )
    copy.start()
    return copy


def keep(src, dst, sem):
    copy = pltpu.make_async_copy(src, dst, sem)
    copy.start()
    return copy


def quad_peers():
    hi, lo, x, c = place()
    return [(lo, 1 - x), (1 - lo, x), (1 - lo, 1 - x)]


def call(kernel, out_shape, operands, in_specs, out_specs, scratch, collective_id):
    return pl.pallas_call(
        kernel,
        out_shape=out_shape,
        in_specs=in_specs,
        out_specs=out_specs,
        scratch_shapes=scratch,
        compiler_params=pltpu.CompilerParams(
            collective_id=collective_id, has_side_effects=True, vmem_limit_bytes=VMEM_BYTES
        ),
    )(*operands)


def deal_kernel(deal_ref, x_ref, o_ref):
    def body(i, carry):
        o_ref[i] = x_ref[deal_ref[i]]
        return carry

    lax.fori_loop(0, o_ref.shape[0], body, 0)


def deal_rows(dealing, rows):
    return pl.pallas_call(
        deal_kernel,
        out_shape=jax.ShapeDtypeStruct(rows.shape, rows.dtype),
        in_specs=[pl.BlockSpec(memory_space=pltpu.SMEM), VM],
        out_specs=VM,
        compiler_params=pltpu.CompilerParams(vmem_limit_bytes=VMEM_BYTES),
    )(dealing, rows)


def undeal_kernel(deal_ref, x_ref, o_ref):
    def body(i, carry):
        o_ref[deal_ref[i]] = x_ref[i].astype(F32)
        return carry

    lax.fori_loop(0, x_ref.shape[0], body, 0)


def undeal_rows(dealing, rows):
    return pl.pallas_call(
        undeal_kernel,
        out_shape=jax.ShapeDtypeStruct(rows.shape, F32),
        in_specs=[pl.BlockSpec(memory_space=pltpu.SMEM), VM],
        out_specs=VM,
        compiler_params=pltpu.CompilerParams(vmem_limit_bytes=VMEM_BYTES),
    )(dealing, rows)


def packed(matrix):
    rows, columns = matrix.shape
    if rows % 8 == 0:
        return matrix
    return matrix.reshape(rows * columns // 128, 128)


def unpacked(gathered, rows, columns):
    return gathered.reshape(-1, rows, columns).reshape(-1, columns)


def plane_others():
    hi, lo, x, c = place()
    others = []
    for a in (0, 1):
        for b in (0, 1):
            for e in (0, 1):
                if a or b or e:
                    others.append(
                        (1 - lo if a else lo, 1 - x if b else x, 1 - c if e else c, b or e)
                    )
    return others


class Gather:
    def __init__(self, dp, xin, ws, hin, hdn, xo, wos, hin_o, hdn_o, sems, halves=None):
        self.dp, self.nz = dp, dp // 2
        self.xin, self.ws, self.hin, self.hdn = xin, ws, hin, hdn
        self.xo, self.wos, self.hin_o, self.hdn_o = xo, wos, hin_o, hdn_o
        self.loc, self.xs, self.xr, self.zs, self.zr = sems[:5]
        self.ps, self.pr, self.cs, self.cr, self.hs, self.hr = sems[5:]
        self.hi, self.lo, self.x, self.c = place()
        hi, lo, x, c = place()
        self.d = hi * 2 + lo
        self.home = (lo * 2 + x) * 2 + c
        self.rows_to = [(lax.rem(self.d + k, dp), x * 2 + c) for k in range(1, dp)]
        self.z_to = [at(lax.rem(hi + k, self.nz), lo, x, c) for k in range(1, self.nz)]
        self.others = plane_others()
        nw = len(ws)
        self.kept, self.z, self.p, self.f, self.k = ([None] * nw for _ in range(5))

        self.halves = halves

    def lanes(self, w, c):
        half = self.ws[w].shape[1] // 2
        return pl.ds(pl.multiple_of(c * half, 128), half)

    def shard(self, w, z, lo, x):
        if self.halves is None:
            return self.wos[w].at[z, lo, x, self.c]
        return self.wos[w].at[z, lo, x, :, self.lanes(w, self.c)]

    def swap(self, w):
        mine, mate, _, sems = self.halves
        partner = at(self.hi, self.lo, self.x, 1 - self.c)
        self.kept[w] = keep(self.ws[w].at[:, self.lanes(w, self.c)], mine[w], sems[0].at[w])
        out = self.ws[w].at[:, self.lanes(w, 1 - self.c)]
        self.z[w] = send(out, mate[w], sems[1].at[w], sems[2].at[w], partner)

    def join(self, w):
        mine, mate, base, _ = self.halves
        self.kept[w].wait()
        self.z[w].wait()
        a, b = mine[w][...].astype(F32), mate[w][...].astype(F32)
        first = self.c == 0
        rows = [jnp.where(first, a, b), jnp.where(first, b, a)]
        base[w][...] = jnp.concatenate(rows, axis=0).astype(BF)
        self.line(w)

    def meet(self):
        peers = self.rows_to + [at(self.hi, *q[:3]) for q in self.others if q[3]]
        meet(peers)

    def rows(self):
        group = self.xin.shape[0] // self.dp
        nw = len(self.ws)
        spot = self.xo.at[:, self.d]
        self.own = keep(self.xin.at[pl.ds(self.d * group, group)], spot, self.loc.at[nw])
        self.moved = [
            send(self.xin.at[pl.ds(to[0] * group, group)], spot, self.xs.at[k], self.xr.at[k], to)
            for k, to in enumerate(self.rows_to)
        ]

    def rows_ready(self):
        self.own.wait()
        for copy in self.moved:
            copy.wait()

    def line(self, w):
        spot = self.shard(w, self.hi, self.lo, self.x)
        own = self.ws[w] if self.halves is None else self.halves[2][w]
        self.kept[w] = keep(own, spot, self.loc.at[w])
        self.z[w] = [
            send(own, spot, self.zs.at[w, k], self.zr.at[w, k], to)
            for k, to in enumerate(self.z_to)
        ]

    def onward(self, part, w, k, to, sems):
        return send(part, part, sems[0].at[w, k], sems[1].at[w, k], to)

    def plane(self, w):
        self.kept[w].wait()
        for copy in self.z[w]:
            copy.wait()
        hi, lo, x, c = self.hi, self.lo, self.x, self.c
        column = self.shard(w, slice(None), lo, x)
        plane = (self.ps, self.pr)
        self.p[w] = [
            self.onward(column, w, 0, at(hi, lo, 1 - x, c), plane),
            self.onward(column, w, 1, at(hi, 1 - lo, x, c), plane),
        ]
        self.k[w] = [self.onward(column, w, 0, at(hi, lo, x, 1 - c), (self.cs, self.cr))]

    def cross(self, w):
        hi, lo, x, c = self.hi, self.lo, self.x, self.c
        plane, core, half = (self.ps, self.pr), (self.cs, self.cr), self.nz // 2
        partner = at(hi, lo, x, 1 - c)
        self.p[w][1].wait()
        part = self.shard(w, pl.ds(0, half), 1 - lo, x)
        first = self.onward(part, w, 2, at(hi, lo, 1 - x, c), plane)
        self.p[w][0].wait()
        part = self.shard(w, pl.ds(half, self.nz - half), lo, 1 - x)
        self.f[w] = [first, self.onward(part, w, 3, at(hi, 1 - lo, x, c), plane)]
        for k, part in ((1, (1 - lo, x)), (2, (lo, 1 - x))):
            self.k[w].append(
                self.onward(self.shard(w, slice(None), *part), w, k, partner, core)
            )

    def core(self, w):
        for copy in self.f[w]:
            copy.wait()
        part = self.shard(w, slice(None), 1 - self.lo, 1 - self.x)
        partner = at(self.hi, self.lo, self.x, 1 - self.c)
        self.k[w].append(self.onward(part, w, 3, partner, (self.cs, self.cr)))

    def ready(self, w):
        for copy in self.k[w]:
            copy.wait()

    def heavy_plane(self):
        nw, hi = len(self.ws), self.hi
        spot = self.hin_o.at[hi, self.home]
        self.h_own = [
            keep(self.hin.at[self.home], spot, self.loc.at[nw + 1]),
            keep(self.hdn, self.hdn_o.at[hi], self.loc.at[nw + 2]),
        ]
        self.h_near = [
            send(
                self.hin.at[(q[0] * 2 + q[1]) * 2 + q[2]],
                spot,
                self.hs.at[0, k],
                self.hr.at[0, k],
                at(hi, *q[:3]),
            )
            for k, q in enumerate(self.others)
        ]

    def heavy_line(self):
        for copy in self.h_own + self.h_near:
            copy.wait()
        part = self.hin_o.at[self.hi]
        self.h_far = []
        for k, to in enumerate(self.z_to):
            self.h_far.append(send(part, part, self.hs.at[1, k], self.hr.at[1, k], to))
            self.h_far.append(
                send(self.hdn, self.hdn_o.at[self.hi], self.hs.at[2, k], self.hr.at[2, k], to)
            )

    def heavy_ready(self):
        for copy in self.h_far:
            copy.wait()


def gather_sems(dp, nw):
    nz, most = dp // 2, max(7, dp // 2)
    return [
        DMA((nw + 3,)),
        DMA((dp,)),
        DMA((dp,)),
        DMA((nw, nz)),
        DMA((nw, nz)),
        DMA((nw, 4)),
        DMA((nw, 4)),
        DMA((nw, 4)),
        DMA((nw, 4)),
        DMA((3, most)),
        DMA((3, most)),
    ]


def gather_kernel(dp, nw, *refs):
    ins, outs, sems = refs[: 3 + nw], refs[3 + nw : 6 + 2 * nw], refs[6 + 2 * nw :]
    g = Gather(
        dp, ins[0], ins[1:-2], ins[-2], ins[-1], outs[0], outs[1:-2], outs[-2], outs[-1], sems
    )
    g.meet()
    g.rows()
    for w in range(nw):
        g.line(w)
    g.heavy_plane()
    for w in range(nw):
        g.plane(w)
        if w == 1:
            g.heavy_line()
        if w >= 1:
            g.cross(w - 1)
        if w >= 2:
            g.core(w - 2)
    g.cross(nw - 1)
    for w in range(nw - 2, nw):
        g.core(w)
    g.rows_ready()
    for w in range(nw):
        g.ready(w)
    g.heavy_ready()


def gather_shapes(dp, xin, weights, hin, hdn, paired):
    nz = dp // 2
    seqs, rows, _ = xin.shape
    shapes = [jax.ShapeDtypeStruct((seqs // dp, dp, rows, D), BF)]
    if paired:
        shapes += [jax.ShapeDtypeStruct((nz, 2, 2, 2 * w.shape[0], w.shape[1]), BF) for w in weights]
    else:
        shapes += [jax.ShapeDtypeStruct((nz, 2, 2, 2) + w.shape, BF) for w in weights]
    shapes.append(jax.ShapeDtypeStruct((nz,) + hin.shape, BF))
    shapes.append(jax.ShapeDtypeStruct((nz,) + hdn.shape, BF))
    return shapes


def gather_all(dp, xin, weights, hin, hdn):
    nw = len(weights)
    return call(
        functools.partial(gather_kernel, dp, nw),
        gather_shapes(dp, xin, weights, hin, hdn, False),
        [xin, *weights, hin, hdn],
        [ANY] * (3 + nw),
        [ANY] * (3 + nw),
        gather_sems(dp, nw),
        1,
    )


def rim_exchange(left, right, from_left, from_right, ls, lr, rs, rr):
    d = lax.axis_index("dp")
    f = lax.axis_index("fsdp")
    last = lax.axis_size("fsdp") - 1

    def down():
        return pltpu.make_async_remote_copy(
            src_ref=left,
            dst_ref=from_right,
            send_sem=ls,
            recv_sem=lr,
            device_id=(d, lax.max(f - 1, 0)),
            device_id_type=MESH,
        )

    def up():
        return pltpu.make_async_remote_copy(
            src_ref=right,
            dst_ref=from_left,
            send_sem=rs,
            recv_sem=rr,
            device_id=(d, lax.min(f + 1, last)),
            device_id_type=MESH,
        )

    @pl.when(f > 0)
    def _():
        down().start()

    @pl.when(f < last)
    def _():
        up().start()

    @pl.when(f == 0)
    def _():
        from_left[...] = jnp.zeros(from_left.shape, from_left.dtype)

    @pl.when(f == last)
    def _():
        from_right[...] = jnp.zeros(from_right.shape, from_right.dtype)

    def finish():
        @pl.when(f > 0)
        def _():
            down().wait_send()
            up().wait_recv()

        @pl.when(f < last)
        def _():
            up().wait_send()
            down().wait_recv()

    return finish


def line_peers():
    hi, lo, x, c = place()
    return [at(hi, lo, x, 1 - c), at(hi, lo, 1 - x, c), at(hi, lo, 1 - x, 1 - c)]


def dot(left, right):
    return jnp.dot(left, right, preferred_element_type=F32)


def dot_back(left, right):
    return lax.dot_general(left, right, (((1,), (1,)), ((), ())), preferred_element_type=F32)


def dot_grad(left, right):
    return lax.dot_general(left, right, (((0,), (0,)), ((), ())), preferred_element_type=F32)


def halves(value):
    high = value.astype(BF)
    return high, (value - high.astype(F32)).astype(BF)


def tiles(extent, step, body):
    def run(i, carry):
        body(pl.ds(pl.multiple_of(i * step, step), step))
        return carry

    lax.fori_loop(0, extent // step, run, 0)


GELU_A = 0.7978845608028654
GELU_B = 0.044715


def gelu_parts(v):
    square = v * v
    t = jnp.tanh(GELU_A * v * (1.0 + GELU_B * square))
    value = 0.5 * v * (1.0 + t)
    slope = 0.5 * (1.0 + t) + 0.5 * v * (1.0 - t * t) * GELU_A * (1.0 + 3.0 * GELU_B * square)
    return value, slope


def gelu_value(v):
    return 0.5 * v * (1.0 + jnp.tanh(GELU_A * v * (1.0 + GELU_B * v * v)))


def ffn_kernel(
    hidden,
    select,
    select_t,
    score,
    gain,
    teach,
    mask,
    scale,
    w_in,
    w_dn,
    w_hin,
    w_hdn,
    g_in,
    g_dn,
    g_hin,
    g_hdn,
    d_hidden,
    stats,
    hn,
    every,
    d_every,
    up_l,
    z,
    up_h,
    zh,
    part,
    near,
    far,
    near2,
    far2,
    out,
    dl,
    dup_l,
    dup_h,
    dhn,
    ps,
    pr,
    cs,
    cr,
    qs,
    qr,
    es,
    er,
):
    hi, lo, x, c = place()
    quad = quad_peers()
    partner = at(hi, lo, x, 1 - c)
    spots = [l2 * 2 + x2 for l2, x2 in quad]
    home = lo * 2 + x
    tokens = hidden.shape[0]
    group, cap, width = select.shape
    fl = z.shape[1]
    fh = zh.shape[2]
    rows_h = part.shape[1] * part.shape[2]
    meet([at(hi, l2, x2, c) for l2, x2 in quad] + [partner])

    def spread(buffer, i):
        spot = buffer.at[c, home]
        there = [
            send(spot, spot, ps.at[i, k], pr.at[i, k], at(hi, l2, x2, c))
            for k, (l2, x2) in enumerate(quad)
        ]
        return there, [send(spot, spot, cs.at[i, 3], cr.at[i, 3], partner)]

    def relay(buffer, i, there, back):
        for k, q in enumerate(spots):
            there[k].wait()
            other = buffer.at[c, q]
            back.append(send(other, other, cs.at[i, k], cr.at[i, k], partner))

    def fold(near_ref, far_ref, i, copy):
        copy.wait()
        there = []
        for k, q in enumerate(spots):
            near_ref[q] = (near_ref[q].astype(F32) + part[c, q].astype(F32)).astype(BF)
            l2, x2 = quad[k]
            there.append(
                send(near_ref.at[q], far_ref.at[k], qs.at[i, k], qr.at[i, k], at(hi, l2, x2, c))
            )
        return there

    def folded(near_ref, far_ref, there):
        for copy in there:
            copy.wait()
        return (
            near_ref[home].astype(F32)
            + part[c, home].astype(F32)
            + far_ref[0].astype(F32)
            + far_ref[1].astype(F32)
            + far_ref[2].astype(F32)
        )

    def norm(r):
        h = hidden[r, :]
        inv = lax.rsqrt(jnp.mean(h * h, axis=-1, keepdims=True) + EPSILON)
        hn[r, :] = (h * inv * gain[1:2, :]).astype(BF)

    tiles(tokens, 128, norm)
    for s in range(group):
        every[c, home, s * cap : (s + 1) * cap, :] = dot(
            select[s], hn[s * width : (s + 1) * width, :]
        ).astype(BF)
    there, back = spread(every, 0)

    def light_up(r):
        up_l[r, :] = dot(hn[r, :], w_in[...])
        z[r, :] = (gelu_value(up_l[r, :fl]) * up_l[r, fl:]).astype(BF)

    tiles(tokens, 256, light_up)
    relay(every, 0, there, back)

    def light_down(r):
        out[r, :] = hidden[r, :] + dot(z[r, :], w_dn[...])

    tiles(tokens, 256, light_down)
    for copy in back:
        copy.wait()

    def heavy(e):
        def up(i, carry):
            a = every[e, pl.ds(2 * i, 2)].reshape(2 * group * cap, D)
            r = pl.ds(pl.multiple_of(i * 256, 256), 256)
            up_h[e, r, :] = dot(a, w_hin[...])
            zh[e, r, :] = (gelu_value(up_h[e, r, :fh]) * up_h[e, r, fh:]).astype(BF)
            v = dot(zh[e, r, :], w_hdn[...]).astype(BF)
            part[e, pl.ds(2 * i, 2)] = v.reshape(2, group * cap, D)
            return carry

        lax.fori_loop(0, 2, up, 0)

    heavy(1 - c)
    first = send(part.at[1 - c], near, es.at[0], er.at[0], partner)
    heavy(c)
    there = fold(near, far, 0, first)
    hf = folded(near, far, there) * score[...]
    hf_high, hf_low = halves(hf)
    for s in range(group):
        r = slice(s * width, (s + 1) * width)
        q = slice(s * cap, (s + 1) * cap)
        out[r, :] += dot(select_t[s], hf_high[q]) + dot(select_t[s], hf_low[q])
    stats[...] = jnp.zeros(stats.shape, F32)

    def misfit(r):
        m = out[r, :] - teach[r, :].astype(F32)
        stats[1:2, :] += jnp.sum(mask[r, :] * m * m, axis=0, keepdims=True)
        d = scale[r, :] * m
        out[r, :] = d
        dl[r, :] = d.astype(BF)

    tiles(tokens, 128, misfit)
    for s in range(group):
        high, low = halves(out[s * width : (s + 1) * width, :])
        picked = dot(select[s], high) + dot(select[s], low)
        q = slice(s * cap, (s + 1) * cap)
        d_every[c, home, q, :] = (picked * score[q, :]).astype(BF)
    there, back = spread(d_every, 1)

    def light_back(r):
        dz = dot_back(dl[r, :], w_dn[...])
        value, slope = gelu_parts(up_l[r, :fl])
        dup_l[r, :fl] = (dz * up_l[r, fl:] * slope).astype(BF)
        dup_l[r, fl:] = (dz * value).astype(BF)

    tiles(tokens, 256, light_back)
    relay(d_every, 1, there, back)

    def light_grad(j):
        g_dn[j, :] = dot_grad(z[:, j], dl[...]).astype(BF)

    tiles(fl, 512, light_grad)
    for copy in back:
        copy.wait()

    def heavy_back(e):
        def run(i, carry):
            d = d_every[e, pl.ds(2 * i, 2)].reshape(2 * group * cap, D)
            r = pl.ds(pl.multiple_of(i * 256, 256), 256)
            dz = dot_back(d, w_hdn[...])
            value, slope = gelu_parts(up_h[e, r, :fh])
            dup_h[e, r, :fh] = (dz * up_h[e, r, fh:] * slope).astype(BF)
            dup_h[e, r, fh:] = (dz * value).astype(BF)
            v = dot_back(dup_h[e, r, :], w_hin[...]).astype(BF)
            part[e, pl.ds(2 * i, 2)] = v.reshape(2, group * cap, D)
            return carry

        lax.fori_loop(0, 2, run, 0)

    heavy_back(1 - c)
    second = send(part.at[1 - c], near2, es.at[1], er.at[1], partner)
    heavy_back(c)
    there = fold(near2, far2, 1, second)

    def light_in_grad(j):
        g_in[:, j] = dot_grad(hn[...], dup_l[:, j]).astype(BF)

    tiles(2 * fl, 1024, light_in_grad)

    def light_in_back(r):
        dhn[r, :] = dot_back(dup_l[r, :], w_in[...])

    tiles(tokens, 256, light_in_back)
    every_rows = every[...].reshape(2 * rows_h, D)

    def heavy_grad(j):
        g_hin[:, j] = dot_grad(every_rows, dup_h[:, :, j].reshape(2 * rows_h, 512)).astype(BF)

    tiles(2 * fh, 512, heavy_grad)
    d_rows = d_every[...].reshape(2 * rows_h, D)

    def heavy_down_grad(j):
        g_hdn[j, :] = dot_grad(zh[:, :, j].reshape(2 * rows_h, 512), d_rows).astype(BF)

    tiles(fh, 512, heavy_down_grad)
    d_high, d_low = halves(folded(near2, far2, there))
    for s in range(group):
        r = slice(s * width, (s + 1) * width)
        q = slice(s * cap, (s + 1) * cap)
        dhn[r, :] += dot(select_t[s], d_high[q]) + dot(select_t[s], d_low[q])

    def norm_back(r):
        h = hidden[r, :]
        inv = lax.rsqrt(jnp.mean(h * h, axis=-1, keepdims=True) + EPSILON)
        d = dhn[r, :]
        dh = d * h
        stats[0:1, :] += jnp.sum(dh * inv, axis=0, keepdims=True)
        mean = jnp.mean(gain[1:2, :] * dh, axis=-1, keepdims=True)
        d_hidden[r, :] = out[r, :] + inv * gain[1:2, :] * d - h * (inv * inv * inv * mean)

    tiles(tokens, 128, norm_back)


def feed_forward(hidden, select, select_t, score, gain, teach, mask, scale, w_in, w_dn, w_hin, w_hdn):
    tokens = hidden.shape[0]
    group, cap, _ = select.shape
    rows = group * cap
    fl, fh = w_dn.shape[0], w_hdn.shape[0]
    block = (2, 4, rows, D)
    operands = [hidden, select, select_t, score, gain, teach, mask, scale, w_in, w_dn, w_hin, w_hdn]
    return call(
        ffn_kernel,
        [
            jax.ShapeDtypeStruct((D, 2 * fl), BF),
            jax.ShapeDtypeStruct((fl, D), BF),
            jax.ShapeDtypeStruct((D, 2 * fh), BF),
            jax.ShapeDtypeStruct((fh, D), BF),
            jax.ShapeDtypeStruct((tokens, D), F32),
            jax.ShapeDtypeStruct((8, D), F32),
        ],
        operands,
        [VM] * len(operands),
        [VM] * 6,
        [
            pltpu.VMEM((tokens, D), BF),
            pltpu.VMEM(block, BF),
            pltpu.VMEM(block, BF),
            pltpu.VMEM((tokens, 2 * fl), F32),
            pltpu.VMEM((tokens, fl), BF),
            pltpu.VMEM((2, 4 * rows, 2 * fh), F32),
            pltpu.VMEM((2, 4 * rows, fh), BF),
            pltpu.VMEM(block, BF),
            pltpu.VMEM(block[1:], BF),
            pltpu.VMEM((3, rows, D), BF),
            pltpu.VMEM(block[1:], BF),
            pltpu.VMEM((3, rows, D), BF),
            pltpu.VMEM((tokens, D), F32),
            pltpu.VMEM((tokens, D), BF),
            pltpu.VMEM((tokens, 2 * fl), BF),
            pltpu.VMEM((2, 4 * rows, 2 * fh), BF),
            pltpu.VMEM((tokens, D), F32),
            DMA((2, 3)),
            DMA((2, 3)),
            DMA((2, 4)),
            DMA((2, 4)),
            DMA((2, 3)),
            DMA((2, 3)),
            DMA((2,)),
            DMA((2,)),
        ],
        5,
    )


def pair_masks(scale):
    lane = lax.broadcasted_iota(jnp.int32, (1, 2 * DH), 1)
    left = jnp.where(lane < DH, scale, 0.0).astype(BF)
    right = jnp.where(lane < DH, 0.0, scale).astype(BF)
    return left, right


def both(value, masks):
    return jnp.concatenate([value * masks[0], value * masks[1]], axis=0)


def side(stacked):
    rows = stacked.shape[0] // 2
    return jnp.concatenate([stacked[:rows], stacked[rows:]], axis=1)


def pair_forward(q, k, v, bias, ones, scaled):
    scores = dot_back(both(q, scaled), k) + bias
    top = jnp.max(scores, axis=-1, keepdims=True)
    shifted = jnp.exp(scores - top)
    total = jnp.sum(shifted, axis=-1, keepdims=True)
    prob = (shifted / total).astype(BF)
    return dot(side(prob), both(v, ones)).astype(BF), top + jnp.log(total)


def pair_backward(q, k, v, bias, lse, d_out, ones, scaled):
    q2 = both(q, scaled)
    d2 = both(d_out, ones)
    prob = jnp.exp(dot_back(q2, k) + bias - lse)
    d_prob = dot_back(d2, v)
    row = jnp.sum(prob * d_prob, axis=-1, keepdims=True)
    d_scores = (prob * (d_prob - row)).astype(BF)
    dq = dot(side(d_scores), both(k, scaled))
    return dq, dot_grad(d_scores, q2), dot_grad(prob.astype(BF), d2)


def reach_bias(key_bias):
    shape = (WIN, 3 * WIN)
    offset = lax.broadcasted_iota(jnp.int32, shape, 1) - lax.broadcasted_iota(jnp.int32, shape, 0) - WIN
    near = (offset >= -WIN) & (offset <= WIN)
    inner = jnp.where(offset == 0, 0.0, jnp.broadcast_to(key_bias, shape))
    bias = jnp.where(near, inner, MASKED)
    return jnp.concatenate([bias, bias], axis=0)


def put_lse(lse, pair, column):
    lane = lax.broadcasted_iota(jnp.int32, lse.shape, 1)
    rows = lse.shape[0]
    lse = jnp.where(lane == 2 * pair, column[:rows], lse)
    return jnp.where(lane == 2 * pair + 1, column[rows:], lse)


def get_lse(lse, pair):
    return jnp.concatenate([lse[:, 2 * pair : 2 * pair + 1], lse[:, 2 * pair + 1 : 2 * pair + 2]], axis=0)


def attend_body(
    stages,
    x,
    gain,
    select,
    select_t,
    key_bias,
    heavy_bias,
    w_lqkv,
    w_hqkv,
    w_lout,
    w_hout,
    hidden,
    xn,
    lq,
    rim,
    lo_out,
    l_lse,
    a_rows,
    hq,
    kvh,
    ho,
    h_lse,
    ls,
    lr,
    rs,
    rr,
    ss,
    sr,
):
    hi, lo, x_, c = place()
    f = x_ * 2 + c
    tokens = x.shape[0]
    group, cap, width = select.shape
    wl, wh = HL * DH, HH * DH
    ones, scaled = pair_masks(1.0), pair_masks(SCORE_SCALE)
    across, partner = at(hi, lo, 1 - x_, c), at(hi, lo, x_, 1 - c)

    def norm(r):
        h = x[r, :].astype(F32)
        inv = lax.rsqrt(jnp.mean(h * h, axis=-1, keepdims=True) + EPSILON)
        xn[r, :] = (h * inv * gain[0:1, :]).astype(BF)

    tiles(tokens, 128, norm)
    for s in range(group):
        rows = dot(select[s], xn[s * width : (s + 1) * width, :]).astype(BF)
        a_rows[s * cap : (s + 1) * cap, :] = rows
    stages[0]()
    kv = dot(a_rows[...], w_hqkv[:, wh:]).astype(BF)
    for s in range(group):
        kvh[s, f] = kv[s * cap : (s + 1) * cap]
    mine = kvh.at[:, f]
    first = send(mine, mine, ss.at[0], sr.at[0], across)
    beside = send(mine, mine, ss.at[1], sr.at[1], partner)
    stages[1]()
    for s in range(group):
        rows = xn[s * width : (s + 1) * width, :]
        rim[s, WIN : WIN + width, :] = dot(rows, w_lqkv[:, wl:]).astype(BF)
    finish = rim_exchange(
        rim.at[:, pl.ds(WIN, WIN)],
        rim.at[:, pl.ds(width, WIN)],
        rim.at[:, pl.ds(0, WIN)],
        rim.at[:, pl.ds(width + WIN, WIN)],
        ls,
        lr,
        rs,
        rr,
    )
    hq[...] = dot(a_rows[...], w_hqkv[:, :wh]).astype(BF)
    for s in range(group):
        rows = slice(s * width, (s + 1) * width)
        lq[rows, :] = dot(xn[rows, :], w_lqkv[:, :wl]).astype(BF)
    stages[2]()
    first.wait()
    other = kvh.at[:, (1 - x_) * 2 + c]
    relay = send(other, other, ss.at[2], sr.at[2], partner)
    finish()
    blocks = width // WIN

    def light(i, carry):
        s, b = i // blocks, i % blocks
        r = pl.ds(pl.multiple_of(i * WIN, WIN), WIN)
        keys = pl.ds(pl.multiple_of(b * WIN, WIN), 3 * WIN)
        bias = reach_bias(key_bias[i])
        lse = jnp.zeros((WIN, 128), F32)
        for pair in range(HL // 2):
            at_k = slice(pair * 128, (pair + 1) * 128)
            at_v = slice(wl + pair * 128, wl + (pair + 1) * 128)
            o, column = pair_forward(
                lq[r, at_k], rim[s, keys, at_k], rim[s, keys, at_v], bias, ones, scaled
            )
            lo_out[r, at_k] = o
            lse = put_lse(lse, pair, column)
        l_lse[r, :] = lse
        return carry

    lax.fori_loop(0, group * blocks // 2, light, 0)
    stages[3]()
    lax.fori_loop(group * blocks // 2, group * blocks, light, 0)
    stages[4]()
    beside.wait()
    relay.wait()
    heavy_kv = kvh.reshape(group, 4 * cap, 2 * wh)

    def heavy(s, carry):
        r = pl.ds(pl.multiple_of(s * cap, cap), cap)
        bias = heavy_bias[s]
        bias = jnp.concatenate([bias, bias], axis=0)
        lse = jnp.zeros((cap, 128), F32)
        for pair in range(HH // 2):
            at_k = slice(pair * 128, (pair + 1) * 128)
            at_v = slice(wh + pair * 128, wh + (pair + 1) * 128)
            o, column = pair_forward(
                hq[r, at_k], heavy_kv[s, :, at_k], heavy_kv[s, :, at_v], bias, ones, scaled
            )
            ho[r, at_k] = o
            lse = put_lse(lse, pair, column)
        h_lse[r, :] = lse
        return carry

    lax.fori_loop(0, group, heavy, 0)
    stages[5]()
    high, low = halves(dot(ho[...], w_hout[...]))
    for s in range(group):
        r = slice(s * width, (s + 1) * width)
        q = slice(s * cap, (s + 1) * cap)
        hidden[r, :] = (
            x[r, :].astype(F32)
            + dot(lo_out[r, :], w_lout[...])
            + (dot(select_t[s], high[q]) + dot(select_t[s], low[q]))
        )


def attend_kernel(*refs):
    meet(line_peers())
    attend_body([lambda: None] * 6, *refs)


def attend_shapes(tokens, select):
    group, cap, width = select.shape
    wl, wh = HL * DH, HH * DH
    rows = group * cap
    return [
        jax.ShapeDtypeStruct((tokens, D), F32),
        jax.ShapeDtypeStruct((tokens, D), BF),
        jax.ShapeDtypeStruct((tokens, wl), BF),
        jax.ShapeDtypeStruct((group, width + 2 * WIN, 2 * wl), BF),
        jax.ShapeDtypeStruct((tokens, wl), BF),
        jax.ShapeDtypeStruct((tokens, 128), F32),
        jax.ShapeDtypeStruct((rows, D), BF),
        jax.ShapeDtypeStruct((rows, wh), BF),
        jax.ShapeDtypeStruct((group, 4, cap, 2 * wh), BF),
        jax.ShapeDtypeStruct((rows, wh), BF),
        jax.ShapeDtypeStruct((rows, 128), F32),
    ]


ATTEND_SEMS = [DMA, DMA, DMA, DMA, DMA((3,)), DMA((3,))]


def attend(x, gain, select, select_t, key_bias, heavy_bias, w_lqkv, w_hqkv, w_lout, w_hout):
    operands = [x, gain, select, select_t, key_bias, heavy_bias, w_lqkv, w_hqkv, w_lout, w_hout]
    shapes = attend_shapes(x.shape[0], select)
    return call(
        attend_kernel,
        shapes,
        operands,
        [VM] * len(operands),
        [VM] * len(shapes),
        ATTEND_SEMS,
        2,
    )


def gather_attend_kernel(dp, nw, *refs):
    n_in, n_out = 7 + nw, 3 + nw + 12
    ins, outs, rest = refs[:n_in], refs[n_in : n_in + n_out], refs[n_in + n_out :]
    xin, ws, hin, hdn = ins[0], ins[1 : 1 + nw], ins[1 + nw], ins[2 + nw]
    masks = ins[3 + nw :]
    xo, wos, hin_o, hdn_o = outs[0], outs[1 : 1 + nw], outs[1 + nw], outs[2 + nw]
    gain, saved = outs[3 + nw], outs[4 + nw :]
    parts, rest = rest[: 3 * nw + 3], rest[3 * nw + 3 :]
    halves = (parts[:nw], parts[nw : 2 * nw], parts[2 * nw : 3 * nw], parts[3 * nw :])
    g = Gather(dp, xin, ws, hin, hdn, xo, wos, hin_o, hdn_o, rest[:11], halves)
    g.meet()
    for w in range(nw):
        g.swap(w)
    g.rows()
    for w in (0, 1, 2):
        g.join(w)
    g.heavy_plane()
    for w in (0, 1, 2):
        g.plane(w)
    for w in (3, 4, 5, 6):
        g.join(w)
    g.heavy_line()
    g.cross(0)
    g.core(0)
    g.cross(1)
    g.cross(2)
    g.ready(0)
    total = jnp.zeros(gain.shape, F32)
    for z in range(dp // 2):
        for l2, x2 in ((0, 0), (0, 1), (1, 0), (1, 1)):
            pair = wos[0][z, l2, x2].astype(F32)
            total += pair[:8] + pair[8:]
    gain[...] = total
    g.rows_ready()

    def heavy_projection():
        g.core(1)
        g.core(2)
        g.ready(2)

    def keys_travel():
        g.plane(3)
        g.plane(4)

    def half_way():
        g.cross(3)
        g.cross(4)
        g.plane(5)

    def light_done():
        g.core(3)
        g.core(4)
        g.cross(5)
        g.plane(6)

    def heavy_done():
        g.ready(3)
        g.ready(4)
        g.core(5)
        g.cross(6)

    full = [wos[w].reshape(-1, wos[w].shape[-1]) for w in range(nw)]
    stages = [heavy_projection, lambda: g.ready(1), keys_travel, half_way, light_done, heavy_done]
    attend_body(
        stages,
        xo.reshape(-1, D),
        gain,
        *masks,
        full[1],
        full[2],
        full[3],
        full[4],
        *saved,
        *rest[11:],
    )
    g.core(6)
    g.ready(5)
    g.ready(6)
    g.heavy_ready()


def gather_attend(dp, xin, weights, hin, hdn, masks):
    nw = len(weights)
    shapes = gather_shapes(dp, xin, weights, hin, hdn, True)
    tokens = shapes[0].shape[0] * dp * xin.shape[1]
    shapes.append(jax.ShapeDtypeStruct((8, D), F32))
    shapes += attend_shapes(tokens, masks[0])
    return call(
        functools.partial(gather_attend_kernel, dp, nw),
        shapes,
        [xin, *weights, hin, hdn, *masks],
        [ANY] * (3 + nw) + [VM] * 4,
        [VM] * 6 + [ANY] * 4 + [VM] * 12,
        [pltpu.VMEM((w.shape[0], w.shape[1] // 2), BF) for w in weights] * 2
        + [pltpu.VMEM((2 * w.shape[0], w.shape[1] // 2), BF) for w in weights]
        + [DMA((nw,))] * 3
        + gather_sems(dp, nw)
        + ATTEND_SEMS,
        1,
    )


def attend_back_body(
    stages,
    d_hidden,
    x,
    gain,
    select,
    select_t,
    key_bias,
    heavy_bias,
    w_lqkv,
    w_hqkv,
    w_lout,
    w_hout,
    xn,
    lq,
    rim,
    lo_out,
    l_lse,
    a_rows,
    hq,
    kvh,
    ho,
    h_lse,
    g_lqkv,
    g_hqkv,
    g_lout,
    g_hout,
    dx,
    stats,
    d_ho,
    d_hproj,
    part,
    got,
    far,
    d_la,
    d_lo,
    d_rim,
    edge,
    edge_in,
    d_lproj,
    ls,
    lr,
    rs,
    rr,
    ss,
    sr,
):
    hi, lo, x_, c = place()
    tokens = x.shape[0]
    group, cap, width = select.shape
    wl, wh = HL * DH, HH * DH
    ones, scaled = pair_masks(1.0), pair_masks(SCORE_SCALE)
    across, partner = at(hi, lo, 1 - x_, c), at(hi, lo, x_, 1 - c)
    picked = []
    for s in range(group):
        high, low = halves(d_hidden[s * width : (s + 1) * width, :])
        picked.append((dot(select[s], high) + dot(select[s], low)).astype(BF))
    d_ha = jnp.concatenate(picked, axis=0)
    d_ho[...] = dot_back(d_ha, w_hout[...]).astype(BF)
    heavy_kv = kvh.reshape(group, 4 * cap, 2 * wh)
    part_kv = part.reshape(group, 4 * cap, 2 * wh)

    def heavy(s, carry):
        r = pl.ds(pl.multiple_of(s * cap, cap), cap)
        bias = heavy_bias[s]
        bias = jnp.concatenate([bias, bias], axis=0)
        lse = h_lse[r, :]
        for pair in range(HH // 2):
            at_k = slice(pair * 128, (pair + 1) * 128)
            at_v = slice(wh + pair * 128, wh + (pair + 1) * 128)
            dq, dk, dv = pair_backward(
                hq[r, at_k],
                heavy_kv[s, :, at_k],
                heavy_kv[s, :, at_v],
                bias,
                get_lse(lse, pair),
                d_ho[r, at_k],
                ones,
                scaled,
            )
            d_hproj[r, at_k] = dq.astype(BF)
            part_kv[s, :, at_k] = dk.astype(BF)
            part_kv[s, :, at_v] = dv.astype(BF)
        return carry

    lax.fori_loop(0, group, heavy, 0)
    beside = [
        send(part.at[:, b * 2 + 1 - c], got.at[b], ss.at[b], sr.at[b], partner) for b in (0, 1)
    ]
    g_hout[...] = dot_grad(ho[...], d_ha).astype(BF)
    stages[0]()

    def light_out_back(r):
        d = d_hidden[r, :].astype(BF)
        d_la[r, :] = d
        d_lo[r, :] = dot_back(d, w_lout[...]).astype(BF)

    tiles(tokens, 256, light_out_back)
    g_lout[...] = dot_grad(lo_out[...], d_la[...]).astype(BF)
    stages[1]()
    for copy in beside:
        copy.wait()
    for b in (0, 1):
        got[b] = (got[b].astype(F32) + part[:, b * 2 + c].astype(F32)).astype(BF)
    third = send(got.at[1 - x_], far, ss.at[2], sr.at[2], across)
    stages[2]()
    d_rim[...] = jnp.zeros(d_rim.shape, F32)
    blocks = width // WIN

    def light(i, carry):
        s, b = i // blocks, i % blocks
        r = pl.ds(pl.multiple_of(i * WIN, WIN), WIN)
        keys = pl.ds(pl.multiple_of(b * WIN, WIN), 3 * WIN)
        bias = reach_bias(key_bias[i])
        lse = l_lse[r, :]
        for pair in range(HL // 2):
            at_k = slice(pair * 128, (pair + 1) * 128)
            at_v = slice(wl + pair * 128, wl + (pair + 1) * 128)
            dq, dk, dv = pair_backward(
                lq[r, at_k],
                rim[s, keys, at_k],
                rim[s, keys, at_v],
                bias,
                get_lse(lse, pair),
                d_lo[r, at_k],
                ones,
                scaled,
            )
            d_lproj[r, at_k] = dq.astype(BF)
            d_rim[s, keys, at_k] += dk
            d_rim[s, keys, at_v] += dv
        return carry

    lax.fori_loop(0, group * blocks // 2, light, 0)
    stages[3]()
    lax.fori_loop(group * blocks // 2, group * blocks, light, 0)
    edge[0] = d_rim[:, :WIN, :].astype(BF)
    edge[1] = d_rim[:, WIN + width :, :].astype(BF)
    finish = rim_exchange(
        edge.at[0], edge.at[1], edge_in.at[0], edge_in.at[1], ls, lr, rs, rr
    )
    stages[4]()
    third.wait()
    total = (got[x_].astype(F32) + far[...].astype(F32)).astype(BF)
    for s in range(group):
        d_hproj[s * cap : (s + 1) * cap, wh:] = total[s]

    def heavy_grad(j):
        g_hqkv[:, j] = dot_grad(a_rows[...], d_hproj[:, j]).astype(BF)

    tiles(3 * wh, 768, heavy_grad)
    stages[5]()
    d_high, d_low = halves(dot_back(d_hproj[...], w_hqkv[...]))
    finish()
    for s in range(group):
        d_rim[s, WIN : 2 * WIN, :] += edge_in[0, s].astype(F32)
        d_rim[s, width : width + WIN, :] += edge_in[1, s].astype(F32)
        d_lproj[s * width : (s + 1) * width, wl:] = d_rim[s, WIN : WIN + width, :].astype(BF)

    def light_grad(j):
        g_lqkv[:, j] = dot_grad(xn[...], d_lproj[:, j]).astype(BF)

    tiles(3 * wl, 768, light_grad)
    stages[6]()
    stats[...] = jnp.zeros(stats.shape, F32)
    for s in range(group):
        r = slice(s * width, (s + 1) * width)
        q = slice(s * cap, (s + 1) * cap)
        d = dot_back(d_lproj[r, :], w_lqkv[...]) + (
            dot(select_t[s], d_high[q]) + dot(select_t[s], d_low[q])
        )
        h = x[r, :].astype(F32)
        inv = lax.rsqrt(jnp.mean(h * h, axis=-1, keepdims=True) + EPSILON)
        dh = d * h
        stats[0:1, :] += jnp.sum(dh * inv, axis=0, keepdims=True)
        mean = jnp.mean(gain[0:1, :] * dh, axis=-1, keepdims=True)
        dx[r, :] = (
            d_hidden[r, :] + inv * gain[0:1, :] * d - h * (inv * inv * inv * mean)
        ).astype(BF)
    stages[7]()


def attend_back_kernel(*refs):
    meet(line_peers())
    attend_back_body([lambda: None] * 8, *refs)


def attend_back_scratch(tokens, select):
    group, cap, width = select.shape
    wl, wh = HL * DH, HH * DH
    rows = group * cap
    return [
        pltpu.VMEM((rows, wh), BF),
        pltpu.VMEM((rows, 3 * wh), BF),
        pltpu.VMEM((group, 4, cap, 2 * wh), BF),
        pltpu.VMEM((2, group, cap, 2 * wh), BF),
        pltpu.VMEM((group, cap, 2 * wh), BF),
        pltpu.VMEM((tokens, D), BF),
        pltpu.VMEM((tokens, wl), BF),
        pltpu.VMEM((group, width + 2 * WIN, 2 * wl), F32),
        pltpu.VMEM((2, group, WIN, 2 * wl), BF),
        pltpu.VMEM((2, group, WIN, 2 * wl), BF),
        pltpu.VMEM((tokens, 3 * wl), BF),
    ] + ATTEND_SEMS


def attend_back(d_hidden, x, gain, select, select_t, key_bias, heavy_bias, weights, saved):
    tokens = x.shape[0]
    wl, wh = HL * DH, HH * DH
    operands = [d_hidden, x, gain, select, select_t, key_bias, heavy_bias, *weights, *saved]
    shapes = [
        jax.ShapeDtypeStruct((D, 3 * wl), BF),
        jax.ShapeDtypeStruct((D, 3 * wh), BF),
        jax.ShapeDtypeStruct((wl, D), BF),
        jax.ShapeDtypeStruct((wh, D), BF),
        jax.ShapeDtypeStruct((tokens, D), BF),
        jax.ShapeDtypeStruct((8, D), F32),
    ]
    return call(
        attend_back_kernel,
        shapes,
        operands,
        [VM] * len(operands),
        [VM] * len(shapes),
        attend_back_scratch(tokens, select),
        3,
    )


def scatter_kernel(dp, nw, *refs):
    nz = dp // 2
    dx, stats, gs, hin, hdn = refs[0], refs[1], refs[2 : 2 + nw], refs[2 + nw], refs[3 + nw]
    outs = refs[4 + nw :]
    dxo, total, gos, hin_o, hdn_o = outs[0], outs[1], outs[2 : 2 + nw], outs[2 + nw], outs[3 + nw]
    scr = outs[4 + nw :]
    nears, fars, sums, ends = (scr[i * nw : (i + 1) * nw] for i in range(4))
    hin_r, hin_s, hdn_r, sc, sp, sz, acc, acc2 = scr[4 * nw : 4 * nw + 8]
    own, xs, xr, cs, cr, ps, pr, zs, zr, hs, hr, ts, tr = scr[4 * nw + 8 :]
    hi, lo, x, c = place()
    d = hi * 2 + lo
    f = x * 2 + c
    plane = (lo * 2 + x) * 2 + c
    dp_peers = [(lax.rem(d + k, dp), f) for k in range(1, dp)]
    rest = [(a, b, e) for a in (0, 1) for b in (0, 1) for e in (0, 1) if a or b or e]
    flat8 = []
    for a, b, e in rest:
        l2 = 1 - lo if a else lo
        x2 = 1 - x if b else x
        c2 = 1 - c if e else c
        flat8.append((l2, x2, c2))
    meet(dp_peers + [at(hi, *p) for (a, b, e), p in zip(rest, flat8) if b or e])
    partner = at(hi, lo, x, 1 - c)
    quad = quad_peers()
    z_index = [lax.rem(hi + k, nz) for k in range(1, nz)]
    z_peers = [at(z, lo, x, c) for z in z_index]
    c_sends = [
        send(gs[w].at[:, :, :, 1 - c], nears[w], cs.at[w], cr.at[w], partner) for w in range(nw)
    ]
    t_c = send(stats, sc, ts.at[0], tr.at[0], partner)
    mine = keep(dx.at[:, d], dxo.at[d], own)
    x_sends = [
        send(dx.at[:, peer[0]], dxo.at[d], xs.at[k], xr.at[k], peer)
        for k, peer in enumerate(dp_peers)
    ]
    h_sends = []
    for k, z in enumerate(z_index):
        h_sends.append(send(hin.at[z], hin_r.at[k], hs.at[1, k], hr.at[1, k], z_peers[k]))
        h_sends.append(send(hdn.at[z], hdn_r.at[k], hs.at[2, k], hr.at[2, k], z_peers[k]))
    p_sends, z_sends = [], []
    t_c.wait()
    acc[...] = stats[...] + sc[...]
    t_p = [
        send(acc, sp.at[k], ts.at[1 + k], tr.at[1 + k], at(hi, l2, x2, c))
        for k, (l2, x2) in enumerate(quad)
    ]

    def add_core(w):
        c_sends[w].wait()
        near, g = nears[w], gs[w]

        def body(i, carry):
            z, a, b = i // 4, (i // 2) % 2, i % 2
            near[z, a, b] = (near[z, a, b].astype(F32) + g[z, a, b, c].astype(F32)).astype(BF)
            return carry

        lax.fori_loop(0, nz * 4, body, 0)
        p_sends.append(
            [
                send(near.at[:, l2, x2], fars[w].at[k], ps.at[w, k], pr.at[w, k], at(hi, l2, x2, c))
                for k, (l2, x2) in enumerate(quad)
            ]
        )

    def add_plane(w):
        for copy in p_sends[w]:
            copy.wait()
        near, far, part = nears[w], fars[w], sums[w]

        def body(z, carry):
            part[z] = (
                near[z, lo, x].astype(F32)
                + far[0, z].astype(F32)
                + far[1, z].astype(F32)
                + far[2, z].astype(F32)
            ).astype(BF)
            return carry

        lax.fori_loop(0, nz, body, 0)
        z_sends.append(
            [
                send(part.at[z], ends[w].at[k], zs.at[w, k], zr.at[w, k], z_peers[k])
                for k, z in enumerate(z_index)
            ]
        )

    def add_line(w):
        for copy in z_sends[w]:
            copy.wait()
        gos[w][...] = sums[w][hi].astype(F32)
        for k in range(nz - 1):
            gos[w][...] += ends[w][k].astype(F32)

    for w in range(nw):
        add_core(w)
        if w >= 2:
            add_plane(w - 2)
    for copy in t_p:
        copy.wait()
    acc2[...] = acc[...] + sp[0] + sp[1] + sp[2]
    t_z = [send(acc2, sz.at[k], ts.at[4 + k], tr.at[4 + k], z_peers[k]) for k in range(nz - 1)]
    for copy in h_sends:
        copy.wait()

    def body(i, carry):
        value = hin[hi, i].astype(F32)
        for k in range(nz - 1):
            value += hin_r[k, i].astype(F32)
        hin_s[i] = value.astype(BF)
        return carry

    lax.fori_loop(0, 8, body, 0)
    hin_o[plane] = hin_s[plane]
    a_sends = [
        send(
            hin_s.at[(l2 * 2 + x2) * 2 + c2],
            hin_o.at[plane],
            hs.at[0, k],
            hr.at[0, k],
            at(hi, l2, x2, c2),
        )
        for k, (l2, x2, c2) in enumerate(flat8)
    ]
    hdn_o[...] = hdn[hi].astype(F32)
    for k in range(nz - 1):
        hdn_o[...] += hdn_r[k].astype(F32)
    for w in range(max(nw - 2, 0), nw):
        add_plane(w)
    for copy in t_z:
        copy.wait()
    total[...] = acc2[...]
    for k in range(nz - 1):
        total[...] += sz[k]
    for w in range(nw):
        add_line(w)
    mine.wait()
    for copy in x_sends + a_sends:
        copy.wait()


def scatter_all(dp, dx, stats, grads, hin, hdn):
    nz = dp // 2
    nw = len(grads)
    group, _, rows, _ = dx.shape
    tiles = [g.shape[4:] for g in grads]
    most = max(7, nz)
    scratch = [pltpu.VMEM((nz, 2, 2) + t, BF) for t in tiles]
    scratch += [pltpu.VMEM((3, nz) + t, BF) for t in tiles]
    scratch += [pltpu.VMEM((nz,) + t, BF) for t in tiles]
    scratch += [pltpu.VMEM((nz - 1,) + t, BF) for t in tiles]
    scratch += [
        pltpu.VMEM((nz - 1,) + hin.shape[1:], BF),
        pltpu.VMEM(hin.shape[1:], BF),
        pltpu.VMEM((nz - 1,) + hdn.shape[1:], BF),
        pltpu.VMEM(stats.shape, F32),
        pltpu.VMEM((3,) + stats.shape, F32),
        pltpu.VMEM((nz - 1,) + stats.shape, F32),
        pltpu.VMEM(stats.shape, F32),
        pltpu.VMEM(stats.shape, F32),
        DMA,
        DMA((dp,)),
        DMA((dp,)),
        DMA((nw,)),
        DMA((nw,)),
        DMA((nw, 3)),
        DMA((nw, 3)),
        DMA((nw, nz)),
        DMA((nw, nz)),
        DMA((3, most)),
        DMA((3, most)),
        DMA((4 + nz,)),
        DMA((4 + nz,)),
    ]
    shapes = [jax.ShapeDtypeStruct((dp, group, rows, D), BF), jax.ShapeDtypeStruct(stats.shape, F32)]
    shapes += [jax.ShapeDtypeStruct(t, F32) for t in tiles]
    shapes.append(jax.ShapeDtypeStruct(hin.shape[1:], BF))
    shapes.append(jax.ShapeDtypeStruct(hdn.shape[1:], F32))
    return call(
        functools.partial(scatter_kernel, dp, nw),
        shapes,
        [dx, stats, *grads, hin, hdn],
        [ANY] + [VM] * (3 + nw),
        [ANY] + [VM] * (3 + nw),
        scratch,
        4,
    )


class Scatter:
    def __init__(self, nz, shards, gs, near, one, two, end, sems):
        self.nz, self.shards, self.gs = nz, shards, gs
        self.near, self.one, self.two, self.end = near, one, two, end
        self.cs, self.cr, self.ps, self.pr, self.zs, self.zr = sems
        self.hi, self.lo, self.x, self.c = hi, lo, x, c = place()
        self.partner = at(hi, lo, x, 1 - c)
        self.by_x, self.by_y = at(hi, lo, 1 - x, c), at(hi, 1 - lo, x, c)
        self.z_index = [lax.rem(hi + k, nz) for k in range(1, nz)]
        self.copies = {}

    def lanes(self, w, c):
        half = self.shards[w][1] // 2
        return pl.ds(pl.multiple_of(c * half, 128), half)

    def core(self, w):
        out = self.gs[w].at[:, :, :, :, self.lanes(w, 1 - self.c)]
        self.copies[w, 0] = [send(out, self.near[w], self.cs.at[w], self.cr.at[w], self.partner)]

    def wait(self, w, stage):
        for copy in self.copies[w, stage]:
            copy.wait()

    def plane(self, w):
        g, own = self.gs[w], self.lanes(w, self.c)
        self.add_plane(w, lambda z, a, b: g[z, a, b, :, own])

    def own_plane(self, w, kept):
        self.add_plane(w, lambda z, a, b: kept[z, a, b])

    def add_plane(self, w, own):
        self.wait(w, 0)
        near = self.near[w]
        lo, x, half = self.lo, self.x, self.nz // 2

        def body(i, carry):
            z, a, b = i // 4, (i // 2) % 2, i % 2
            near[z, a, b] = (near[z, a, b].astype(F32) + own(z, a, b).astype(F32)).astype(BF)
            return carry

        lax.fori_loop(0, self.nz * 4, body, 0)
        low, high = pl.ds(0, half), pl.ds(half, self.nz - half)
        self.copies[w, 1] = [
            send(near.at[low, :, 1 - x], self.one[w].at[low], self.ps.at[w, 0], self.pr.at[w, 0], self.by_x),
            send(near.at[high, 1 - lo], self.one[w].at[high], self.ps.at[w, 1], self.pr.at[w, 1], self.by_y),
        ]

    def cross(self, w):
        self.wait(w, 1)
        near, one, lo, x, half = self.near[w], self.one[w], self.lo, self.x, self.nz // 2

        def low_body(i, carry):
            z, a = i // 2, i % 2
            near[z, a, x] = (near[z, a, x].astype(F32) + one[z, a].astype(F32)).astype(BF)
            return carry

        def high_body(i, carry):
            z, b = half + i // 2, i % 2
            near[z, lo, b] = (near[z, lo, b].astype(F32) + one[z, b].astype(F32)).astype(BF)
            return carry

        lax.fori_loop(0, half * 2, low_body, 0)
        lax.fori_loop(0, (self.nz - half) * 2, high_body, 0)
        low, high = pl.ds(0, half), pl.ds(half, self.nz - half)
        two = self.two[w]
        self.copies[w, 2] = [
            send(near.at[low, 1 - lo, x], two.at[low], self.ps.at[w, 2], self.pr.at[w, 2], self.by_y),
            send(near.at[high, lo, 1 - x], two.at[high], self.ps.at[w, 3], self.pr.at[w, 3], self.by_x),
        ]

    def line(self, w):
        self.wait(w, 2)
        near, part, lo, x = self.near[w], self.two[w], self.lo, self.x

        def body(z, carry):
            part[z] = (near[z, lo, x].astype(F32) + part[z].astype(F32)).astype(BF)
            return carry

        lax.fori_loop(0, self.nz, body, 0)
        self.copies[w, 3] = [
            send(
                part.at[z],
                self.end[w].at[k],
                self.zs.at[w, k],
                self.zr.at[w, k],
                at(z, lo, x, self.c),
            )
            for k, z in enumerate(self.z_index)
        ]

    def last(self, w, fin, out, sems):
        self.wait(w, 3)
        value = self.two[w][self.hi].astype(F32)
        for k in range(self.nz - 1):
            value += self.end[w][k].astype(F32)
        fin[...] = value
        count = self.shards[w][0]
        own = pl.ds(pl.multiple_of(self.c * count, 8), count)
        mate = pl.ds(pl.multiple_of((1 - self.c) * count, 8), count)
        spot = out.at[:, self.lanes(w, self.c)]
        return [
            keep(fin.at[own], spot, sems[0].at[w]),
            send(fin.at[mate], spot, sems[1].at[w], sems[2].at[w], self.partner),
        ]


def back_scatter_kernel(dp, shards, *refs):
    nz, nw = dp // 2, len(shards)
    n_ops = 7 + 4 + 10
    ops, (g_lin, g_ldn, hin, hdn, ffn_stats) = refs[:n_ops], refs[n_ops : n_ops + 5]
    outs, rest = refs[n_ops + 5 : n_ops + 9 + nw], refs[n_ops + 9 + nw :]
    dxo, total, gos, hin_o, hdn_o = outs[0], outs[1], outs[2 : 2 + nw], outs[2 + nw], outs[3 + nw]
    full, rest = rest[:4], rest[4:]
    own_lin, own_ldn, stats, rest = rest[0], rest[1], rest[2], rest[3:]
    back, rest = rest[:17], rest[17:]
    dx = back[5]
    near, one, two, end, fin = (rest[k * nw : (k + 1) * nw] for k in range(5))
    hin_own, hdn_own, hin_r, hdn_r, acc, sc, sp, sz, acc2 = rest[5 * nw : 5 * nw + 9]
    own, xs, xr, cs, cr, ps, pr, zs, zr, hs, hr, ts, tr, *fsem = rest[5 * nw + 9 :]
    hi, lo, x, c = place()
    d = hi * 2 + lo
    plane = (lo * 2 + x) * 2 + c
    others = plane_others()
    rows_to = [(lax.rem(d + k, dp), x * 2 + c) for k in range(1, dp)]
    z_index = [lax.rem(hi + k, nz) for k in range(1, nz)]
    z_to = [at(z, lo, x, c) for z in z_index]
    quad = quad_peers()
    g_views = [g_lin, g_ldn]
    for k, w in enumerate((2, 3, 4, 5)):
        rows, columns = shards[w]
        g_views.append(full[k].reshape(nz, 2, 2, 2 * rows, columns))
    t = Scatter(nz, shards, g_views, near, one, two, end, (cs, cr, ps, pr, zs, zr))
    meet(rows_to + [at(hi, *q[:3]) for q in others if q[3]])
    h_sends = []
    for k, z in enumerate(z_index):
        h_sends.append(send(hin.at[z], hin_r.at[k], hs.at[1, k], hr.at[1, k], z_to[k]))
        h_sends.append(send(hdn.at[z], hdn_r.at[k], hs.at[2, k], hr.at[2, k], z_to[k]))
    t.core(0)
    t.core(1)
    kept = [
        keep(g_lin.at[:, :, :, :, t.lanes(0, c)], own_lin, own.at[0]),
        keep(g_ldn.at[:, :, :, :, t.lanes(1, c)], own_ldn, own.at[1]),
        keep(hin.at[hi], hin_own, own.at[2]),
        keep(hdn.at[hi], hdn_own, own.at[3]),
    ]
    late = []

    def first_plane():
        kept[0].wait()
        kept[1].wait()
        t.own_plane(0, own_lin)
        t.own_plane(1, own_ldn)
        t.core(2)

    def out_core():
        t.core(3)

    def before_light():
        t.cross(0)
        t.cross(1)

    def half_way():
        t.line(0)
        t.line(1)
        t.plane(2)
        t.plane(3)

    def rims_left():
        t.cross(2)
        t.cross(3)

    def heavy_grad_done():
        t.core(4)
        t.line(2)
        t.line(3)

    def light_grad_done():
        t.core(5)
        t.plane(4)

    def rows_done():
        rows = dx.reshape(dxo.shape[1], dp, dxo.shape[2], D)
        late.append(keep(rows.at[:, d], dxo.at[d], own.at[4]))
        for k, to in enumerate(rows_to):
            late.append(send(rows.at[:, to[0]], dxo.at[d], xs.at[k], xr.at[k], to))

    stages = [
        first_plane,
        out_core,
        before_light,
        half_way,
        rims_left,
        heavy_grad_done,
        light_grad_done,
        rows_done,
    ]
    attend_back_body(
        stages, *ops, full[3], full[2], full[1], full[0], dx, stats, *back
    )
    partner = at(hi, lo, x, 1 - c)
    for k in range(6):
        lanes = slice(k * 128, (k + 1) * 128)
        acc[k : k + 1, :] = stats[0:1, lanes]
        acc[6 + k : 7 + k, :] = ffn_stats[0:1, lanes]
    loss = jnp.sum(ffn_stats[1:2, :], axis=-1, keepdims=True)
    acc[12:16, :] = jnp.broadcast_to(loss, (4, 128))
    t_c = send(acc, sc, ts.at[0], tr.at[0], partner)
    t.plane(5)
    t.cross(4)
    t_c.wait()
    acc2[...] = acc[...] + sc[...]
    t_p = [
        send(acc2, sp.at[k], ts.at[1 + k], tr.at[1 + k], at(hi, l2, x2, c))
        for k, (l2, x2) in enumerate(quad)
    ]
    for copy in h_sends + kept[2:]:
        copy.wait()

    def body(i, carry):
        value = hin_own[i].astype(F32)
        for k in range(nz - 1):
            value += hin_r[k, i].astype(F32)
        hin_own[i] = value.astype(BF)
        return carry

    lax.fori_loop(0, 8, body, 0)
    hin_o[plane] = hin_own[plane]
    late += [
        send(
            hin_own.at[(q[0] * 2 + q[1]) * 2 + q[2]],
            hin_o.at[plane],
            hs.at[0, k],
            hr.at[0, k],
            at(hi, *q[:3]),
        )
        for k, q in enumerate(others)
    ]
    value = hdn_own[...].astype(F32)
    for k in range(nz - 1):
        value += hdn_r[k].astype(F32)
    hdn_o[...] = value
    t.cross(5)
    t.line(4)
    for copy in t_p:
        copy.wait()
    acc[...] = acc2[...] + sp[0] + sp[1] + sp[2]
    t_z = [send(acc, sz.at[k], ts.at[4 + k], tr.at[4 + k], z_to[k]) for k in range(nz - 1)]
    t.line(5)
    for w in range(nw):
        late += t.last(w, fin[w], gos[w], fsem)
    for copy in t_z:
        copy.wait()
    value = acc[...]
    for k in range(nz - 1):
        value += sz[k]
    total[...] = value
    for copy in late:
        copy.wait()


def back_scatter(dp, rows, d_hidden, x, gain, masks, weights, saved, ffn_grads, ffn_stats, shards, hin, hdn):
    nz, nw = dp // 2, len(shards)
    tokens = x.shape[0]
    group = masks[0].shape[0]
    most = max(7, nz)
    stat_shape = (16, 128)
    paired = [
        g.reshape(nz, 2, 2, 2 * s[0], s[1]) for g, s in zip(ffn_grads, shards)
    ]
    operands = [d_hidden, x, gain, *masks, *weights, *saved, *paired, hin, hdn, ffn_stats]
    shapes = [jax.ShapeDtypeStruct((dp, group, rows, D), BF), jax.ShapeDtypeStruct(stat_shape, F32)]
    shapes += [jax.ShapeDtypeStruct(s, F32) for s in shards]
    shapes.append(jax.ShapeDtypeStruct(hin.shape[1:], BF))
    shapes.append(jax.ShapeDtypeStruct(hdn.shape[1:], F32))
    scratch = [pltpu.VMEM((s[0] * 8 * nz, s[1]), BF) for s in shards[2:]]
    split = [(2 * s[0], s[1] // 2) for s in shards]
    scratch += [pltpu.VMEM((nz, 2, 2) + s, BF) for s in split[:2]]
    scratch += [pltpu.VMEM((8, D), F32)]
    scratch += attend_back_scratch(tokens, masks[0])
    scratch += [pltpu.VMEM((nz, 2, 2) + s, BF) for s in split]
    scratch += [pltpu.VMEM((nz, 2) + s, BF) for s in split]
    scratch += [pltpu.VMEM((nz,) + s, BF) for s in split]
    scratch += [pltpu.VMEM((nz - 1,) + s, BF) for s in split]
    scratch += [pltpu.VMEM(s, F32) for s in split]
    scratch += [
        pltpu.VMEM(hin.shape[1:], BF),
        pltpu.VMEM(hdn.shape[1:], BF),
        pltpu.VMEM((nz - 1,) + hin.shape[1:], BF),
        pltpu.VMEM((nz - 1,) + hdn.shape[1:], BF),
        pltpu.VMEM(stat_shape, F32),
        pltpu.VMEM(stat_shape, F32),
        pltpu.VMEM((3,) + stat_shape, F32),
        pltpu.VMEM((nz - 1,) + stat_shape, F32),
        pltpu.VMEM(stat_shape, F32),
        DMA((5,)),
        DMA((dp,)),
        DMA((dp,)),
        DMA((nw,)),
        DMA((nw,)),
        DMA((nw, 4)),
        DMA((nw, 4)),
        DMA((nw, nz)),
        DMA((nw, nz)),
        DMA((3, most)),
        DMA((3, most)),
        DMA((4 + nz,)),
        DMA((4 + nz,)),
        DMA((nw,)),
        DMA((nw,)),
        DMA((nw,)),
    ]
    return call(
        functools.partial(back_scatter_kernel, dp, shards),
        shapes,
        operands,
        [VM] * (len(operands) - 5) + [ANY] * 4 + [VM],
        [VM] * len(shapes),
        scratch,
        6,
    )


def routing(routes, pieces, piece_len):
    places = jnp.arange(pieces * piece_len)
    routed = jnp.any(routes[:, None, :] == places[None, :, None], axis=-1)
    routed = routed.reshape(-1, pieces, piece_len)
    before = jnp.arange(piece_len)[:, None] < jnp.arange(piece_len)[None, :]
    rank = jnp.einsum(
        "skp,pq->skq", routed.astype(BF), before.astype(BF), preferred_element_type=F32
    )
    slots = jnp.arange(CAP, dtype=F32)
    hot = routed[:, :, None, :] & (rank[:, :, None, :] == slots[None, None, :, None])
    filled = jnp.any(hot, axis=-1)
    spots = jnp.sum(jnp.where(hot, places.reshape(1, pieces, 1, piece_len), 0), axis=-1)
    return hot, jnp.where(filled, spots, -1)


def local(
    layer_input,
    teacher,
    lengths,
    dealing,
    attn_routes,
    ffn_routes,
    ffn_scores,
    gain_attn,
    gain_ffn,
    light_qkv,
    light_out,
    heavy_qkv,
    heavy_out,
    light_in,
    light_down,
    heavy_in,
    heavy_down,
):
    dp = lax.axis_size("dp")
    pieces = lax.axis_size("fsdp")
    data_index = lax.axis_index("dp")
    piece = lax.axis_index("fsdp")
    nz = dp // 2
    n = dp * pieces
    seqs = dealing.shape[0]
    group = seqs // dp
    gain_len = gain_attn.shape[0]
    hidden_units = heavy_in.shape[1] // 2 // n
    xin = deal_rows(dealing, layer_input[:, 0])
    mine = data_index * pieces + piece
    owned = jnp.arange(D)[None, :] // gain_len == mine
    spread_out = jnp.broadcast_to(
        jnp.stack([gain_attn, gain_ffn])[:, None, :], (2, D // gain_len, gain_len)
    ).reshape(2, D)
    gains = jnp.pad(jnp.where(owned, spread_out, 0.0).astype(BF), ((0, 6), (0, 0)))
    matrices = (light_qkv, heavy_qkv, light_out, heavy_out, light_in, light_down)
    hin_rows = heavy_in.shape[0]
    hin_src = (
        heavy_in.reshape(hin_rows, 2, nz, 8, hidden_units)
        .transpose(3, 0, 1, 2, 4)
        .reshape(8, hin_rows, 2 * nz * hidden_units)
    )
    if hin_rows % 8:
        hin_src = hin_src.reshape(8, -1, 128)
    tokens = layer_input.shape[2] * dp
    chosen = lax.dynamic_slice_in_dim(dealing, data_index * group, group)
    one = (chosen[:, None] == jnp.arange(seqs)[None, :])
    seq_lengths = jnp.sum(jnp.where(one, lengths[None, :], 0), axis=1)
    attn_pick = jnp.sum(jnp.where(one[:, :, None], attn_routes[None], 0), axis=1)
    ffn_pick = jnp.sum(jnp.where(one[:, :, None], ffn_routes[None], 0), axis=1)
    score_pick = jnp.sum(jnp.where(one[:, :, None], ffn_scores[None], 0.0), axis=1)
    token_count = jnp.sum(lengths).astype(F32)
    positions = piece * tokens + jnp.arange(tokens)
    valid_mask = positions[None, :] < seq_lengths[:, None]
    a_hot, a_spots = routing(attn_pick, pieces, tokens)
    f_hot, f_spots = routing(ffn_pick, pieces, tokens)
    a_select = lax.dynamic_index_in_dim(a_hot, piece, 1, False).astype(BF)
    f_select = lax.dynamic_index_in_dim(f_hot, piece, 1, False).astype(BF)
    a_spot = lax.dynamic_index_in_dim(a_spots, piece, 1, False)
    f_spot = lax.dynamic_index_in_dim(f_spots, piece, 1, False)
    slot_score = jnp.sum(
        jnp.where(f_spot[:, :, None] == ffn_pick[:, None, :], score_pick[:, None, :], 0.0), axis=-1
    )
    key_pos = piece * tokens - WIN + jnp.arange(tokens + 2 * WIN)
    live_key = (key_pos >= 0)[None, :] & (key_pos[None, :] < seq_lengths[:, None])
    key_line = jnp.where(live_key, 0.0, MASKED)
    key_bias = jnp.stack(
        [key_line[:, b : b + 3 * WIN] for b in range(0, tokens, WIN)], axis=1
    ).reshape(-1, 1, 3 * WIN)
    all_spots = a_spots.reshape(group, pieces * CAP)
    heavy_allowed = ((all_spots >= 0) & (all_spots < seq_lengths[:, None]))[:, None, :] | (
        a_spot[:, :, None] == all_spots[:, None, :]
    )
    heavy_bias = jnp.where(heavy_allowed, 0.0, MASKED)
    masks = (a_select, a_select.swapaxes(1, 2), key_bias, heavy_bias)
    sources = (xin, [gains] + [packed(m) for m in matrices], hin_src, heavy_down)
    merged = layer_input.shape[2] % 16 == 0 and all(
        m.shape[0] % 8 == 0 and m.shape[1] % 256 == 0 for m in (*matrices, heavy_in, heavy_down)
    )
    if merged:
        got = gather_attend(dp, *sources, masks)
    else:
        got = gather_all(dp, *sources)
    flat_x = got[0].reshape(-1, D)
    w_lqkv, w_hqkv, w_lout, w_hout, w_lin, w_ldown = (
        unpacked(full, *m.shape) for full, m in zip(got[2:8], matrices)
    )
    w_hin = unpacked(got[8], hin_rows, 2 * nz * hidden_units)
    w_hdown = got[9].reshape(-1, D)
    attn_weights = (w_lqkv, w_hqkv, w_lout, w_hout)
    if merged:
        gain, hidden, *saved = got[10:]
    else:
        gain = jnp.sum(got[1].reshape(n, 8, D).astype(F32), axis=0)
        hidden, *saved = attend(flat_x, gain, *masks, *attn_weights)
    weight_mask = valid_mask.reshape(-1, 1).astype(F32)
    grad_lin, grad_ldown, grad_hin, grad_hdown, d_hidden, ffn_stats = feed_forward(
        hidden,
        f_select,
        f_select.swapaxes(1, 2),
        slot_score.reshape(-1, 1),
        gain,
        teacher.reshape(-1, D),
        weight_mask,
        2.0 * weight_mask / (D * token_count),
        w_lin,
        w_ldown,
        w_hin,
        w_hdown,
    )
    rows = tokens // dp
    shards = (light_in, light_down, heavy_out, light_out, heavy_qkv, light_qkv)
    hin_part = grad_hin.reshape((nz, 8) + hin_src.shape[1:])
    hdn_part = grad_hdown.reshape(nz, -1, D)
    if merged:
        done = back_scatter(
            dp,
            rows,
            d_hidden,
            flat_x,
            gain,
            masks,
            attn_weights,
            saved,
            (grad_lin, grad_ldown),
            ffn_stats,
            tuple(shard.shape for shard in shards),
            hin_part,
            hdn_part,
        )
    else:
        grad_lqkv, grad_hqkv, grad_lout, grad_hout, d_inputs, attn_stats = attend_back(
            d_hidden, flat_x, gain, *masks, attn_weights, saved
        )
        stats = jnp.concatenate(
            [
                attn_stats[0].reshape(-1, 128),
                ffn_stats[0].reshape(-1, 128),
                jnp.broadcast_to(jnp.sum(ffn_stats[1]), (4, 128)),
            ]
        )
        grads = (grad_lin, grad_ldown, grad_hout, grad_lout, grad_hqkv, grad_lqkv)
        sent = [packed_full(grad, shard.shape, nz) for grad, shard in zip(grads, shards)]
        done = scatter_all(
            dp, d_inputs.reshape(group, dp, rows, D), stats, sent, hin_part, hdn_part
        )
    d_layer = undeal_rows(dealing, done[0].reshape(seqs, rows, D))[:, None]
    summed = done[1]
    loss_value = summed[12, 0] / (D * token_count)
    own_one = lax.dynamic_slice_in_dim(summed[:6].reshape(-1), mine * gain_len, gain_len)
    own_two = lax.dynamic_slice_in_dim(summed[6:12].reshape(-1), mine * gain_len, gain_len)
    g_lin, g_ldown, g_hout, g_lout, g_hqkv, g_lqkv = (
        full.reshape(shard.shape) for full, shard in zip(done[2:8], shards)
    )
    g_hin = (
        done[8]
        .astype(F32)
        .reshape(8, hin_rows, 2, nz, hidden_units)
        .transpose(1, 2, 3, 0, 4)
        .reshape(heavy_in.shape)
    )
    return (
        loss_value,
        d_layer,
        own_one,
        own_two,
        g_lqkv,
        g_lout,
        g_hqkv,
        g_hout,
        g_lin,
        g_ldown,
        g_hin,
        done[9].reshape(heavy_down.shape),
    )


def packed_full(grad, shard_shape, nz):
    rows, columns = shard_shape
    if rows % 8 == 0:
        return grad.reshape(nz, 2, 2, 2, rows, columns)
    return grad.reshape(nz, 2, 2, 2, rows * columns // 128, 128)


def solution(mesh):
    split = P(("dp", "fsdp"))
    matrix = P(("dp", "fsdp"), None)
    placed = (
        P(None, "fsdp", "dp", None),
        P("dp", "fsdp", None, None),
        P(),
        P(),
        P(),
        P(),
        P(),
        split,
        split,
    ) + (matrix,) * 8
    return jax.shard_map(
        local,
        mesh=mesh,
        in_specs=placed,
        out_specs=(P(), P(None, "fsdp", "dp", None), split, split) + (matrix,) * 8,
        check_vma=False,
    )
```

```python
import functools
import jax
import jax.numpy as jnp
from jax import lax
from jax.experimental import pallas as pl
from jax.experimental.pallas import tpu as pltpu
from jax.sharding import PartitionSpec as P

D = 768
HL = 8
HH = 12
DH = 64
FL = 1024
FH = 4096
WIN = 128
CAP = 64

EPSILON = 1e-06
MASKED = -1000000000.0
SCORE_SCALE = 0.125
MESH = pl.DeviceIdType.MESH
BF = jnp.bfloat16
F32 = jnp.float32
ANY = pl.BlockSpec(memory_space=pl.ANY)
VM = pl.BlockSpec(memory_space=pltpu.VMEM)
DMA = pltpu.SemaphoreType.DMA
VMEM_BYTES = 60 * 1024 * 1024


def place():
    d = lax.axis_index("dp")
    f = lax.axis_index("fsdp")
    return d // 2, d % 2, f // 2, f % 2


def at(hi, lo, x, c):
    return (hi * 2 + lo, x * 2 + c)


def meet(peers):
    barrier = pltpu.get_barrier_semaphore()
    for peer in peers:
        pl.semaphore_signal(barrier, inc=1, device_id=peer, device_id_type=MESH)
    pl.semaphore_wait(barrier, len(peers))


def send(src, dst, send_sem, recv_sem, peer):
    copy = pltpu.make_async_remote_copy(
        src_ref=src,
        dst_ref=dst,
        send_sem=send_sem,
        recv_sem=recv_sem,
        device_id=peer,
        device_id_type=MESH,
    )
    copy.start()
    return copy


def keep(src, dst, sem):
    copy = pltpu.make_async_copy(src, dst, sem)
    copy.start()
    return copy


def quad_peers():
    hi, lo, x, c = place()
    return [(lo, 1 - x), (1 - lo, x), (1 - lo, 1 - x)]


def call(kernel, out_shape, operands, in_specs, out_specs, scratch, collective_id):
    return pl.pallas_call(
        kernel,
        out_shape=out_shape,
        in_specs=in_specs,
        out_specs=out_specs,
        scratch_shapes=scratch,
        compiler_params=pltpu.CompilerParams(
            collective_id=collective_id, has_side_effects=True, vmem_limit_bytes=VMEM_BYTES
        ),
    )(*operands)


def deal_kernel(deal_ref, x_ref, o_ref):
    def body(i, carry):
        o_ref[i] = x_ref[deal_ref[i]]
        return carry

    lax.fori_loop(0, o_ref.shape[0], body, 0)


def deal_rows(dealing, rows):
    return pl.pallas_call(
        deal_kernel,
        out_shape=jax.ShapeDtypeStruct(rows.shape, rows.dtype),
        in_specs=[pl.BlockSpec(memory_space=pltpu.SMEM), VM],
        out_specs=VM,
        compiler_params=pltpu.CompilerParams(vmem_limit_bytes=VMEM_BYTES),
    )(dealing, rows)


def undeal_kernel(deal_ref, x_ref, o_ref):
    def body(i, carry):
        o_ref[deal_ref[i]] = x_ref[i].astype(F32)
        return carry

    lax.fori_loop(0, x_ref.shape[0], body, 0)


def undeal_rows(dealing, rows):
    return pl.pallas_call(
        undeal_kernel,
        out_shape=jax.ShapeDtypeStruct(rows.shape, F32),
        in_specs=[pl.BlockSpec(memory_space=pltpu.SMEM), VM],
        out_specs=VM,
        compiler_params=pltpu.CompilerParams(vmem_limit_bytes=VMEM_BYTES),
    )(dealing, rows)


def prepare_kernel(deal_ref, x_ref, heavy_ref, one_ref, two_ref, xin, hin, gains):
    def body(i, carry):
        xin[i] = x_ref[deal_ref[i]]
        return carry

    lax.fori_loop(0, xin.shape[0], body, 0)
    count = one_ref.shape[1]
    units = D // count
    step = heavy_ref.shape[1] // 2 // units
    for j in range(8):
        for k in range(units // 8):
            for g in (0, 1):
                start = g * heavy_ref.shape[1] // 2 + (k * 8 + j) * step
                spot = (g * (units // 8) + k) * step
                hin[j, :, spot : spot + step] = heavy_ref[:, start : start + step]
    mine = lax.axis_index("dp") * 4 + lax.axis_index("fsdp")
    row = lax.broadcasted_iota(jnp.int32, (count, D), 0)
    lane = lax.broadcasted_iota(jnp.int32, (count, D), 1)
    hot = jnp.where(lane == row + mine * count, 1.0, 0.0).astype(BF)
    lines = [jnp.broadcast_to(ref[...], (8, count)) for ref in (one_ref, two_ref)]
    one, two = (jnp.dot(line, hot, preferred_element_type=F32) for line in lines)
    kind = lax.broadcasted_iota(jnp.int32, (8, D), 0)
    gains[...] = jnp.where(kind == 0, one, jnp.where(kind == 1, two, 0.0)).astype(BF)


def prepare(dealing, rows, heavy_in, gain_one, gain_two):
    count = gain_one.shape[0]
    columns = heavy_in.shape[1] // 8
    return pl.pallas_call(
        prepare_kernel,
        out_shape=[
            jax.ShapeDtypeStruct(rows.shape, BF),
            jax.ShapeDtypeStruct((8, heavy_in.shape[0], columns), BF),
            jax.ShapeDtypeStruct((8, D), BF),
        ],
        in_specs=[pl.BlockSpec(memory_space=pltpu.SMEM), VM, VM, VM, VM],
        out_specs=[VM] * 3,
        compiler_params=pltpu.CompilerParams(vmem_limit_bytes=VMEM_BYTES),
    )(dealing, rows, heavy_in, gain_one.reshape(1, count), gain_two.reshape(1, count))


def finish_kernel(units, deal_ref, x_ref, hin, *refs):
    count = (len(refs) - 2) // 2
    ins, (rows, heavy), outs = refs[:count], refs[count : count + 2], refs[count + 2 :]

    def body(i, carry):
        rows[deal_ref[i]] = x_ref[i].astype(F32)
        return carry

    lax.fori_loop(0, x_ref.shape[0], body, 0)
    step = heavy.shape[1] // 2 // units
    for j in range(8):
        for k in range(units // 8):
            for g in (0, 1):
                start = g * heavy.shape[1] // 2 + (k * 8 + j) * step
                spot = (g * (units // 8) + k) * step
                heavy[:, start : start + step] = hin[j, :, spot : spot + step].astype(F32)
    for source, out in zip(ins, outs):
        out[...] = source[...]


def finish_all(units, dealing, rows, hin, grads, heavy_shape):
    shapes = [jax.ShapeDtypeStruct(rows.shape, F32), jax.ShapeDtypeStruct(heavy_shape, F32)]
    shapes += [jax.ShapeDtypeStruct(g.shape, F32) for g in grads]
    return pl.pallas_call(
        functools.partial(finish_kernel, units),
        out_shape=shapes,
        in_specs=[pl.BlockSpec(memory_space=pltpu.SMEM)] + [VM] * (2 + len(grads)),
        out_specs=[VM] * len(shapes),
        compiler_params=pltpu.CompilerParams(vmem_limit_bytes=VMEM_BYTES),
    )(dealing, rows, hin, *grads)


def packed(matrix):
    rows, columns = matrix.shape
    if rows % 8 == 0:
        return matrix
    return matrix.reshape(rows * columns // 128, 128)


def unpacked(gathered, rows, columns):
    return gathered.reshape(-1, rows, columns).reshape(-1, columns)


def plane_others():
    hi, lo, x, c = place()
    others = []
    for a in (0, 1):
        for b in (0, 1):
            for e in (0, 1):
                if a or b or e:
                    others.append(
                        (1 - lo if a else lo, 1 - x if b else x, 1 - c if e else c, b or e)
                    )
    return others


class Gather:
    def __init__(self, dp, xin, ws, hin, hdn, xo, wos, hin_o, hdn_o, sems, halves=None):
        self.dp, self.nz = dp, dp // 2
        self.xin, self.ws, self.hin, self.hdn = xin, ws, hin, hdn
        self.xo, self.wos, self.hin_o, self.hdn_o = xo, wos, hin_o, hdn_o
        self.loc, self.xs, self.xr, self.zs, self.zr = sems[:5]
        self.ps, self.pr, self.cs, self.cr, self.hs, self.hr = sems[5:]
        self.hi, self.lo, self.x, self.c = place()
        hi, lo, x, c = place()
        self.d = hi * 2 + lo
        self.home = (lo * 2 + x) * 2 + c
        self.rows_to = [(lax.rem(self.d + k, dp), x * 2 + c) for k in range(1, dp)]
        self.z_to = [at(lax.rem(hi + k, self.nz), lo, x, c) for k in range(1, self.nz)]
        self.others = plane_others()
        nw = len(ws)
        self.kept, self.z, self.p, self.f, self.k = ([None] * nw for _ in range(5))

        self.halves = halves

    def lanes(self, w, c):
        half = self.ws[w].shape[1] // 2
        return pl.ds(pl.multiple_of(c * half, 128), half)

    def shard(self, w, z, lo, x):
        if self.halves is None:
            return self.wos[w].at[z, lo, x, self.c]
        return self.wos[w].at[z, lo, x, :, self.lanes(w, self.c)]

    def swap(self, w):
        mine, mate, _, sems = self.halves
        partner = at(self.hi, self.lo, self.x, 1 - self.c)
        self.kept[w] = keep(self.ws[w].at[:, self.lanes(w, self.c)], mine[w], sems[0].at[w])
        out = self.ws[w].at[:, self.lanes(w, 1 - self.c)]
        self.z[w] = send(out, mate[w], sems[1].at[w], sems[2].at[w], partner)

    def join(self, w):
        mine, mate, base, _ = self.halves
        self.kept[w].wait()
        self.z[w].wait()
        a, b = mine[w][...].astype(F32), mate[w][...].astype(F32)
        first = self.c == 0
        rows = [jnp.where(first, a, b), jnp.where(first, b, a)]
        base[w][...] = jnp.concatenate(rows, axis=0).astype(BF)
        self.line(w)

    def meet(self):
        peers = self.rows_to + [at(self.hi, *q[:3]) for q in self.others if q[3]]
        meet(peers)

    def rows(self):
        group = self.xin.shape[0] // self.dp
        nw = len(self.ws)
        spot = self.xo.at[:, self.d]
        self.own = keep(self.xin.at[pl.ds(self.d * group, group)], spot, self.loc.at[nw])
        self.moved = [
            send(self.xin.at[pl.ds(to[0] * group, group)], spot, self.xs.at[k], self.xr.at[k], to)
            for k, to in enumerate(self.rows_to)
        ]

    def rows_ready(self):
        self.own.wait()
        for copy in self.moved:
            copy.wait()

    def line(self, w):
        spot = self.shard(w, self.hi, self.lo, self.x)
        own = self.ws[w] if self.halves is None else self.halves[2][w]
        self.kept[w] = keep(own, spot, self.loc.at[w])
        self.z[w] = [
            send(own, spot, self.zs.at[w, k], self.zr.at[w, k], to)
            for k, to in enumerate(self.z_to)
        ]

    def onward(self, part, w, k, to, sems):
        return send(part, part, sems[0].at[w, k], sems[1].at[w, k], to)

    def plane(self, w):
        self.kept[w].wait()
        for copy in self.z[w]:
            copy.wait()
        hi, lo, x, c = self.hi, self.lo, self.x, self.c
        column = self.shard(w, slice(None), lo, x)
        plane = (self.ps, self.pr)
        self.p[w] = [
            self.onward(column, w, 0, at(hi, lo, 1 - x, c), plane),
            self.onward(column, w, 1, at(hi, 1 - lo, x, c), plane),
        ]
        self.k[w] = [self.onward(column, w, 0, at(hi, lo, x, 1 - c), (self.cs, self.cr))]

    def cross(self, w):
        hi, lo, x, c = self.hi, self.lo, self.x, self.c
        plane, core, half = (self.ps, self.pr), (self.cs, self.cr), self.nz // 2
        partner = at(hi, lo, x, 1 - c)
        self.p[w][1].wait()
        part = self.shard(w, pl.ds(0, half), 1 - lo, x)
        first = self.onward(part, w, 2, at(hi, lo, 1 - x, c), plane)
        self.p[w][0].wait()
        part = self.shard(w, pl.ds(half, self.nz - half), lo, 1 - x)
        self.f[w] = [first, self.onward(part, w, 3, at(hi, 1 - lo, x, c), plane)]
        for k, part in ((1, (1 - lo, x)), (2, (lo, 1 - x))):
            self.k[w].append(
                self.onward(self.shard(w, slice(None), *part), w, k, partner, core)
            )

    def core(self, w):
        for copy in self.f[w]:
            copy.wait()
        part = self.shard(w, slice(None), 1 - self.lo, 1 - self.x)
        partner = at(self.hi, self.lo, self.x, 1 - self.c)
        self.k[w].append(self.onward(part, w, 3, partner, (self.cs, self.cr)))

    def ready(self, w):
        for copy in self.k[w]:
            copy.wait()

    def heavy_plane(self):
        nw, hi = len(self.ws), self.hi
        spot = self.hin_o.at[hi, self.home]
        self.h_own = [
            keep(self.hin.at[self.home], spot, self.loc.at[nw + 1]),
            keep(self.hdn, self.hdn_o.at[hi], self.loc.at[nw + 2]),
        ]
        self.h_near = [
            send(
                self.hin.at[(q[0] * 2 + q[1]) * 2 + q[2]],
                spot,
                self.hs.at[0, k],
                self.hr.at[0, k],
                at(hi, *q[:3]),
            )
            for k, q in enumerate(self.others)
        ]

    def heavy_line(self):
        for copy in self.h_own + self.h_near:
            copy.wait()
        part = self.hin_o.at[self.hi]
        self.h_far = []
        for k, to in enumerate(self.z_to):
            self.h_far.append(send(part, part, self.hs.at[1, k], self.hr.at[1, k], to))
            self.h_far.append(
                send(self.hdn, self.hdn_o.at[self.hi], self.hs.at[2, k], self.hr.at[2, k], to)
            )

    def heavy_ready(self):
        for copy in self.h_far:
            copy.wait()


def gather_sems(dp, nw):
    nz, most = dp // 2, max(7, dp // 2)
    return [
        DMA((nw + 3,)),
        DMA((dp,)),
        DMA((dp,)),
        DMA((nw, nz)),
        DMA((nw, nz)),
        DMA((nw, 4)),
        DMA((nw, 4)),
        DMA((nw, 4)),
        DMA((nw, 4)),
        DMA((3, most)),
        DMA((3, most)),
    ]


def gather_kernel(dp, nw, *refs):
    ins, outs, sems = refs[: 3 + nw], refs[3 + nw : 6 + 2 * nw], refs[6 + 2 * nw :]
    g = Gather(
        dp, ins[0], ins[1:-2], ins[-2], ins[-1], outs[0], outs[1:-2], outs[-2], outs[-1], sems
    )
    g.meet()
    g.rows()
    for w in range(nw):
        g.line(w)
    g.heavy_plane()
    for w in range(nw):
        g.plane(w)
        if w == 1:
            g.heavy_line()
        if w >= 1:
            g.cross(w - 1)
        if w >= 2:
            g.core(w - 2)
    g.cross(nw - 1)
    for w in range(nw - 2, nw):
        g.core(w)
    g.rows_ready()
    for w in range(nw):
        g.ready(w)
    g.heavy_ready()


def gather_shapes(dp, xin, weights, hin, hdn, paired):
    nz = dp // 2
    seqs, rows, _ = xin.shape
    shapes = [jax.ShapeDtypeStruct((seqs // dp, dp, rows, D), BF)]
    if paired:
        shapes += [jax.ShapeDtypeStruct((nz, 2, 2, 2 * w.shape[0], w.shape[1]), BF) for w in weights]
    else:
        shapes += [jax.ShapeDtypeStruct((nz, 2, 2, 2) + w.shape, BF) for w in weights]
    shapes.append(jax.ShapeDtypeStruct((nz,) + hin.shape, BF))
    shapes.append(jax.ShapeDtypeStruct((nz,) + hdn.shape, BF))
    return shapes


def gather_all(dp, xin, weights, hin, hdn):
    nw = len(weights)
    return call(
        functools.partial(gather_kernel, dp, nw),
        gather_shapes(dp, xin, weights, hin, hdn, False),
        [xin, *weights, hin, hdn],
        [ANY] * (3 + nw),
        [ANY] * (3 + nw),
        gather_sems(dp, nw),
        1,
    )


def rim_exchange(left, right, from_left, from_right, ls, lr, rs, rr):
    d = lax.axis_index("dp")
    f = lax.axis_index("fsdp")
    last = lax.axis_size("fsdp") - 1

    def down():
        return pltpu.make_async_remote_copy(
            src_ref=left,
            dst_ref=from_right,
            send_sem=ls,
            recv_sem=lr,
            device_id=(d, lax.max(f - 1, 0)),
            device_id_type=MESH,
        )

    def up():
        return pltpu.make_async_remote_copy(
            src_ref=right,
            dst_ref=from_left,
            send_sem=rs,
            recv_sem=rr,
            device_id=(d, lax.min(f + 1, last)),
            device_id_type=MESH,
        )

    @pl.when(f > 0)
    def _():
        down().start()

    @pl.when(f < last)
    def _():
        up().start()

    @pl.when(f == 0)
    def _():
        from_left[...] = jnp.zeros(from_left.shape, from_left.dtype)

    @pl.when(f == last)
    def _():
        from_right[...] = jnp.zeros(from_right.shape, from_right.dtype)

    def finish():
        @pl.when(f > 0)
        def _():
            down().wait_send()
            up().wait_recv()

        @pl.when(f < last)
        def _():
            up().wait_send()
            down().wait_recv()

    return finish


def line_peers():
    hi, lo, x, c = place()
    return [at(hi, lo, x, 1 - c), at(hi, lo, 1 - x, c), at(hi, lo, 1 - x, 1 - c)]


def dot(left, right):
    return jnp.dot(left, right, preferred_element_type=F32)


def dot_back(left, right):
    return lax.dot_general(left, right, (((1,), (1,)), ((), ())), preferred_element_type=F32)


def dot_grad(left, right):
    return lax.dot_general(left, right, (((0,), (0,)), ((), ())), preferred_element_type=F32)


def halves(value):
    high = value.astype(BF)
    return high, (value - high.astype(F32)).astype(BF)


def tiles(extent, step, body):
    def run(i, carry):
        body(pl.ds(pl.multiple_of(i * step, step), step))
        return carry

    lax.fori_loop(0, extent // step, run, 0)


GELU_A = 0.7978845608028654
GELU_B = 0.044715


def gelu_parts(v):
    square = v * v
    t = jnp.tanh(GELU_A * v * (1.0 + GELU_B * square))
    value = 0.5 * v * (1.0 + t)
    slope = 0.5 * (1.0 + t) + 0.5 * v * (1.0 - t * t) * GELU_A * (1.0 + 3.0 * GELU_B * square)
    return value, slope


def gelu_value(v):
    return 0.5 * v * (1.0 + jnp.tanh(GELU_A * v * (1.0 + GELU_B * v * v)))


def ffn_kernel(
    hidden,
    select,
    select_t,
    score,
    gain,
    teach,
    mask,
    scale,
    w_in,
    w_dn,
    w_hin,
    w_hdn,
    g_in,
    g_dn,
    g_hin,
    g_hdn,
    d_hidden,
    stats,
    hn,
    every,
    d_every,
    up_l,
    z,
    up_h,
    zh,
    part,
    near,
    far,
    near2,
    far2,
    out,
    dl,
    dup_l,
    dup_h,
    dhn,
    ps,
    pr,
    cs,
    cr,
    qs,
    qr,
    es,
    er,
):
    hi, lo, x, c = place()
    quad = quad_peers()
    partner = at(hi, lo, x, 1 - c)
    spots = [l2 * 2 + x2 for l2, x2 in quad]
    home = lo * 2 + x
    tokens = hidden.shape[0]
    group, cap, width = select.shape
    fl = z.shape[1]
    fh = zh.shape[2]
    rows_h = part.shape[1] * part.shape[2]
    meet([at(hi, l2, x2, c) for l2, x2 in quad] + [partner])

    def spread(buffer, i):
        spot = buffer.at[c, home]
        there = [
            send(spot, spot, ps.at[i, k], pr.at[i, k], at(hi, l2, x2, c))
            for k, (l2, x2) in enumerate(quad)
        ]
        return there, [send(spot, spot, cs.at[i, 3], cr.at[i, 3], partner)]

    def relay(buffer, i, there, back):
        for k, q in enumerate(spots):
            there[k].wait()
            other = buffer.at[c, q]
            back.append(send(other, other, cs.at[i, k], cr.at[i, k], partner))

    def fold(near_ref, far_ref, i, copy):
        copy.wait()
        there = []
        for k, q in enumerate(spots):
            near_ref[q] = (near_ref[q].astype(F32) + part[c, q].astype(F32)).astype(BF)
            l2, x2 = quad[k]
            there.append(
                send(near_ref.at[q], far_ref.at[k], qs.at[i, k], qr.at[i, k], at(hi, l2, x2, c))
            )
        return there

    def folded(near_ref, far_ref, there):
        for copy in there:
            copy.wait()
        return (
            near_ref[home].astype(F32)
            + part[c, home].astype(F32)
            + far_ref[0].astype(F32)
            + far_ref[1].astype(F32)
            + far_ref[2].astype(F32)
        )

    def norm(r):
        h = hidden[r, :]
        inv = lax.rsqrt(jnp.mean(h * h, axis=-1, keepdims=True) + EPSILON)
        hn[r, :] = (h * inv * gain[1:2, :]).astype(BF)

    tiles(tokens, 128, norm)
    for s in range(group):
        every[c, home, s * cap : (s + 1) * cap, :] = dot(
            select[s], hn[s * width : (s + 1) * width, :]
        ).astype(BF)
    there, back = spread(every, 0)

    def light_up(r):
        up_l[r, :] = dot(hn[r, :], w_in[...])
        z[r, :] = (gelu_value(up_l[r, :fl]) * up_l[r, fl:]).astype(BF)

    tiles(tokens, 256, light_up)

    def light_slopes(r):
        value, slope = gelu_parts(up_l[r, :fl])
        up_l[r, :fl] = up_l[r, fl:] * slope
        up_l[r, fl:] = value

    tiles(tokens, 64, light_slopes)
    relay(every, 0, there, back)

    def light_down(r):
        out[r, :] = hidden[r, :] + dot(z[r, :], w_dn[...])

    tiles(tokens, 256, light_down)
    for copy in back:
        copy.wait()

    def heavy(e):
        def up(i, carry):
            a = every[e, pl.ds(2 * i, 2)].reshape(2 * group * cap, D)
            r = pl.ds(pl.multiple_of(i * 256, 256), 256)
            up_h[e, r, :] = dot(a, w_hin[...])
            zh[e, r, :] = (gelu_value(up_h[e, r, :fh]) * up_h[e, r, fh:]).astype(BF)
            v = dot(zh[e, r, :], w_hdn[...]).astype(BF)
            part[e, pl.ds(2 * i, 2)] = v.reshape(2, group * cap, D)
            return carry

        lax.fori_loop(0, 2, up, 0)

    heavy(1 - c)
    first = send(part.at[1 - c], near, es.at[0], er.at[0], partner)
    heavy(c)
    there = fold(near, far, 0, first)
    for e in (0, 1):

        def heavy_slopes(r, e=e):
            value, slope = gelu_parts(up_h[e, r, :fh])
            up_h[e, r, :fh] = up_h[e, r, fh:] * slope
            up_h[e, r, fh:] = value

        tiles(rows_h, 128, heavy_slopes)
    hf = folded(near, far, there) * score[...]
    hf_high, hf_low = halves(hf)
    for s in range(group):
        r = slice(s * width, (s + 1) * width)
        q = slice(s * cap, (s + 1) * cap)
        out[r, :] += dot(select_t[s], hf_high[q]) + dot(select_t[s], hf_low[q])
    stats[...] = jnp.zeros(stats.shape, F32)

    def misfit(r):
        m = out[r, :] - teach[r, :].astype(F32)
        stats[1:2, :] += jnp.sum(mask[r, :] * m * m, axis=0, keepdims=True)
        d = scale[r, :] * m
        out[r, :] = d
        dl[r, :] = d.astype(BF)

    tiles(tokens, 128, misfit)
    for s in range(group):
        high, low = halves(out[s * width : (s + 1) * width, :])
        picked = dot(select[s], high) + dot(select[s], low)
        q = slice(s * cap, (s + 1) * cap)
        d_every[c, home, q, :] = (picked * score[q, :]).astype(BF)
    there, back = spread(d_every, 1)

    def light_back(r):
        dz = dot_back(dl[r, :], w_dn[...])
        dup_l[r, :fl] = (dz * up_l[r, :fl]).astype(BF)
        dup_l[r, fl:] = (dz * up_l[r, fl:]).astype(BF)

    tiles(tokens, 256, light_back)
    def light_in_back(r):
        dhn[r, :] = dot_back(dup_l[r, :], w_in[...])

    tiles(tokens, 256, light_in_back)
    relay(d_every, 1, there, back)

    def light_grad(j):
        g_dn[j, :] = dot_grad(z[:, j], dl[...]).astype(BF)

    tiles(fl, 512, light_grad)
    for copy in back:
        copy.wait()

    def heavy_back(e):
        def run(i, carry):
            d = d_every[e, pl.ds(2 * i, 2)].reshape(2 * group * cap, D)
            r = pl.ds(pl.multiple_of(i * 256, 256), 256)
            dz = dot_back(d, w_hdn[...])
            dup_h[e, r, :fh] = (dz * up_h[e, r, :fh]).astype(BF)
            dup_h[e, r, fh:] = (dz * up_h[e, r, fh:]).astype(BF)
            v = dot_back(dup_h[e, r, :], w_hin[...]).astype(BF)
            part[e, pl.ds(2 * i, 2)] = v.reshape(2, group * cap, D)
            return carry

        lax.fori_loop(0, 2, run, 0)

    heavy_back(1 - c)
    second = send(part.at[1 - c], near2, es.at[1], er.at[1], partner)
    heavy_back(c)
    there = fold(near2, far2, 1, second)

    def light_in_grad(j):
        g_in[:, j] = dot_grad(hn[...], dup_l[:, j]).astype(BF)

    tiles(2 * fl, 1024, light_in_grad)

    every_rows = every[...].reshape(2 * rows_h, D)

    def heavy_grad(j):
        g_hin[:, j] = dot_grad(every_rows, dup_h[:, :, j].reshape(2 * rows_h, 512)).astype(BF)

    tiles(2 * fh, 512, heavy_grad)
    d_rows = d_every[...].reshape(2 * rows_h, D)

    def heavy_down_grad(j):
        g_hdn[j, :] = dot_grad(zh[:, :, j].reshape(2 * rows_h, 512), d_rows).astype(BF)

    tiles(fh, 512, heavy_down_grad)
    d_high, d_low = halves(folded(near2, far2, there))
    for s in range(group):
        r = slice(s * width, (s + 1) * width)
        q = slice(s * cap, (s + 1) * cap)
        dhn[r, :] += dot(select_t[s], d_high[q]) + dot(select_t[s], d_low[q])

    def norm_back(r):
        h = hidden[r, :]
        inv = lax.rsqrt(jnp.mean(h * h, axis=-1, keepdims=True) + EPSILON)
        d = dhn[r, :]
        dh = d * h
        stats[0:1, :] += jnp.sum(dh * inv, axis=0, keepdims=True)
        mean = jnp.mean(gain[1:2, :] * dh, axis=-1, keepdims=True)
        d_hidden[r, :] = out[r, :] + inv * gain[1:2, :] * d - h * (inv * inv * inv * mean)

    tiles(tokens, 128, norm_back)


def feed_forward(hidden, select, select_t, score, gain, teach, mask, scale, w_in, w_dn, w_hin, w_hdn):
    tokens = hidden.shape[0]
    group, cap, _ = select.shape
    rows = group * cap
    fl, fh = w_dn.shape[0], w_hdn.shape[0]
    block = (2, 4, rows, D)
    operands = [hidden, select, select_t, score, gain, teach, mask, scale, w_in, w_dn, w_hin, w_hdn]
    return call(
        ffn_kernel,
        [
            jax.ShapeDtypeStruct((D, 2 * fl), BF),
            jax.ShapeDtypeStruct((fl, D), BF),
            jax.ShapeDtypeStruct((D, 2 * fh), BF),
            jax.ShapeDtypeStruct((fh, D), BF),
            jax.ShapeDtypeStruct((tokens, D), F32),
            jax.ShapeDtypeStruct((8, D), F32),
        ],
        operands,
        [VM] * len(operands),
        [VM] * 6,
        [
            pltpu.VMEM((tokens, D), BF),
            pltpu.VMEM(block, BF),
            pltpu.VMEM(block, BF),
            pltpu.VMEM((tokens, 2 * fl), F32),
            pltpu.VMEM((tokens, fl), BF),
            pltpu.VMEM((2, 4 * rows, 2 * fh), F32),
            pltpu.VMEM((2, 4 * rows, fh), BF),
            pltpu.VMEM(block, BF),
            pltpu.VMEM(block[1:], BF),
            pltpu.VMEM((3, rows, D), BF),
            pltpu.VMEM(block[1:], BF),
            pltpu.VMEM((3, rows, D), BF),
            pltpu.VMEM((tokens, D), F32),
            pltpu.VMEM((tokens, D), BF),
            pltpu.VMEM((tokens, 2 * fl), BF),
            pltpu.VMEM((2, 4 * rows, 2 * fh), BF),
            pltpu.VMEM((tokens, D), F32),
            DMA((2, 3)),
            DMA((2, 3)),
            DMA((2, 4)),
            DMA((2, 4)),
            DMA((2, 3)),
            DMA((2, 3)),
            DMA((2,)),
            DMA((2,)),
        ],
        5,
    )


def pair_masks(scale):
    lane = lax.broadcasted_iota(jnp.int32, (1, 2 * DH), 1)
    left = jnp.where(lane < DH, scale, 0.0).astype(BF)
    right = jnp.where(lane < DH, 0.0, scale).astype(BF)
    return left, right


def both(value, masks):
    return jnp.concatenate([value * masks[0], value * masks[1]], axis=0)


def side(stacked):
    rows = stacked.shape[0] // 2
    return jnp.concatenate([stacked[:rows], stacked[rows:]], axis=1)


def pair_forward(q, k, v, bias, ones, scaled):
    scores = dot_back(both(q, scaled), k) + bias
    top = jnp.max(scores, axis=-1, keepdims=True)
    shifted = jnp.exp(scores - top)
    total = jnp.sum(shifted, axis=-1, keepdims=True)
    prob = (shifted / total).astype(BF)
    return dot(side(prob), both(v, ones)).astype(BF), top + jnp.log(total)


def pair_backward(q, k, v, bias, lse, d_out, ones, scaled):
    q2 = both(q, scaled)
    d2 = both(d_out, ones)
    prob = jnp.exp(dot_back(q2, k) + bias - lse)
    d_prob = dot_back(d2, v)
    row = jnp.sum(prob * d_prob, axis=-1, keepdims=True)
    d_scores = (prob * (d_prob - row)).astype(BF)
    dq = dot(side(d_scores), both(k, scaled))
    return dq, dot_grad(d_scores, q2), dot_grad(prob.astype(BF), d2)


def reach_bias(key_bias):
    shape = (WIN, 3 * WIN)
    offset = lax.broadcasted_iota(jnp.int32, shape, 1) - lax.broadcasted_iota(jnp.int32, shape, 0) - WIN
    near = (offset >= -WIN) & (offset <= WIN)
    inner = jnp.where(offset == 0, 0.0, jnp.broadcast_to(key_bias, shape))
    bias = jnp.where(near, inner, MASKED)
    return jnp.concatenate([bias, bias], axis=0)


def put_lse(lse, pair, column):
    lane = lax.broadcasted_iota(jnp.int32, lse.shape, 1)
    rows = lse.shape[0]
    lse = jnp.where(lane == 2 * pair, column[:rows], lse)
    return jnp.where(lane == 2 * pair + 1, column[rows:], lse)


def get_lse(lse, pair):
    return jnp.concatenate([lse[:, 2 * pair : 2 * pair + 1], lse[:, 2 * pair + 1 : 2 * pair + 2]], axis=0)


def attend_body(
    stages,
    x,
    gain,
    select,
    select_t,
    key_bias,
    heavy_bias,
    w_lqkv,
    w_hqkv,
    w_lout,
    w_hout,
    hidden,
    xn,
    lq,
    rim,
    lo_out,
    l_lse,
    a_rows,
    hq,
    kvh,
    ho,
    h_lse,
    ls,
    lr,
    rs,
    rr,
    ss,
    sr,
):
    hi, lo, x_, c = place()
    f = x_ * 2 + c
    tokens = x.shape[0]
    group, cap, width = select.shape
    wl, wh = HL * DH, HH * DH
    ones, scaled = pair_masks(1.0), pair_masks(SCORE_SCALE)
    across, partner = at(hi, lo, 1 - x_, c), at(hi, lo, x_, 1 - c)

    def norm(r):
        h = x[r, :].astype(F32)
        inv = lax.rsqrt(jnp.mean(h * h, axis=-1, keepdims=True) + EPSILON)
        xn[r, :] = (h * inv * gain[0:1, :]).astype(BF)

    tiles(tokens, 128, norm)
    for s in range(group):
        rows = dot(select[s], xn[s * width : (s + 1) * width, :]).astype(BF)
        a_rows[s * cap : (s + 1) * cap, :] = rows
    stages[0]()
    kv = dot(a_rows[...], w_hqkv[:, wh:]).astype(BF)
    for s in range(group):
        kvh[s, f] = kv[s * cap : (s + 1) * cap]
    mine = kvh.at[:, f]
    first = send(mine, mine, ss.at[0], sr.at[0], across)
    beside = send(mine, mine, ss.at[1], sr.at[1], partner)
    stages[1]()
    for s in range(group):
        rows = xn[s * width : (s + 1) * width, :]
        rim[s, WIN : WIN + width, :] = dot(rows, w_lqkv[:, wl:]).astype(BF)
    finish = rim_exchange(
        rim.at[:, pl.ds(WIN, WIN)],
        rim.at[:, pl.ds(width, WIN)],
        rim.at[:, pl.ds(0, WIN)],
        rim.at[:, pl.ds(width + WIN, WIN)],
        ls,
        lr,
        rs,
        rr,
    )
    hq[...] = dot(a_rows[...], w_hqkv[:, :wh]).astype(BF)
    for s in range(group):
        rows = slice(s * width, (s + 1) * width)
        lq[rows, :] = dot(xn[rows, :], w_lqkv[:, :wl]).astype(BF)
    stages[2]()
    first.wait()
    other = kvh.at[:, (1 - x_) * 2 + c]
    relay = send(other, other, ss.at[2], sr.at[2], partner)
    finish()
    blocks = width // WIN

    def light(i, carry):
        s, b = i // blocks, i % blocks
        r = pl.ds(pl.multiple_of(i * WIN, WIN), WIN)
        keys = pl.ds(pl.multiple_of(b * WIN, WIN), 3 * WIN)
        bias = reach_bias(key_bias[i])
        lse = jnp.zeros((WIN, 128), F32)
        for pair in range(HL // 2):
            at_k = slice(pair * 128, (pair + 1) * 128)
            at_v = slice(wl + pair * 128, wl + (pair + 1) * 128)
            o, column = pair_forward(
                lq[r, at_k], rim[s, keys, at_k], rim[s, keys, at_v], bias, ones, scaled
            )
            lo_out[r, at_k] = o
            lse = put_lse(lse, pair, column)
        l_lse[r, :] = lse
        return carry

    lax.fori_loop(0, group * blocks // 2, light, 0)
    stages[3]()
    lax.fori_loop(group * blocks // 2, group * blocks, light, 0)
    stages[4]()
    beside.wait()
    relay.wait()
    heavy_kv = kvh.reshape(group, 4 * cap, 2 * wh)

    def heavy(s, carry):
        r = pl.ds(pl.multiple_of(s * cap, cap), cap)
        bias = heavy_bias[s]
        bias = jnp.concatenate([bias, bias], axis=0)
        lse = jnp.zeros((cap, 128), F32)
        for pair in range(HH // 2):
            at_k = slice(pair * 128, (pair + 1) * 128)
            at_v = slice(wh + pair * 128, wh + (pair + 1) * 128)
            o, column = pair_forward(
                hq[r, at_k], heavy_kv[s, :, at_k], heavy_kv[s, :, at_v], bias, ones, scaled
            )
            ho[r, at_k] = o
            lse = put_lse(lse, pair, column)
        h_lse[r, :] = lse
        return carry

    lax.fori_loop(0, group, heavy, 0)
    stages[5]()
    high, low = halves(dot(ho[...], w_hout[...]))
    for s in range(group):
        r = slice(s * width, (s + 1) * width)
        q = slice(s * cap, (s + 1) * cap)
        hidden[r, :] = (
            x[r, :].astype(F32)
            + dot(lo_out[r, :], w_lout[...])
            + (dot(select_t[s], high[q]) + dot(select_t[s], low[q]))
        )


def attend_kernel(*refs):
    meet(line_peers())
    attend_body([lambda: None] * 6, *refs)


def attend_shapes(tokens, select):
    group, cap, width = select.shape
    wl, wh = HL * DH, HH * DH
    rows = group * cap
    return [
        jax.ShapeDtypeStruct((tokens, D), F32),
        jax.ShapeDtypeStruct((tokens, D), BF),
        jax.ShapeDtypeStruct((tokens, wl), BF),
        jax.ShapeDtypeStruct((group, width + 2 * WIN, 2 * wl), BF),
        jax.ShapeDtypeStruct((tokens, wl), BF),
        jax.ShapeDtypeStruct((tokens, 128), F32),
        jax.ShapeDtypeStruct((rows, D), BF),
        jax.ShapeDtypeStruct((rows, wh), BF),
        jax.ShapeDtypeStruct((group, 4, cap, 2 * wh), BF),
        jax.ShapeDtypeStruct((rows, wh), BF),
        jax.ShapeDtypeStruct((rows, 128), F32),
    ]


ATTEND_SEMS = [DMA, DMA, DMA, DMA, DMA((3,)), DMA((3,))]


def attend(x, gain, select, select_t, key_bias, heavy_bias, w_lqkv, w_hqkv, w_lout, w_hout):
    operands = [x, gain, select, select_t, key_bias, heavy_bias, w_lqkv, w_hqkv, w_lout, w_hout]
    shapes = attend_shapes(x.shape[0], select)
    return call(
        attend_kernel,
        shapes,
        operands,
        [VM] * len(operands),
        [VM] * len(shapes),
        ATTEND_SEMS,
        2,
    )


def route_part(deal, lengths, routes_a, routes_f, scores, tables):
    sel_a, selt_a, key_bias, heavy_bias, sel_f, selt_f, score, mask, scale = tables
    hi, lo, x, c = place()
    group, cap, width = sel_a.shape
    seqs = deal.shape[1]
    here = ((x * 2 + c) * width).astype(F32)

    def line(shape, dim):
        return lax.broadcasted_iota(jnp.int32, shape, dim).astype(F32)

    lane = lax.broadcasted_iota(jnp.int32, (1, seqs), 1)
    before = jnp.where(line((width, width), 0) > line((width, width), 1), 1.0, 0.0).astype(BF)
    length_row = lengths[...].astype(F32)
    count = jnp.sum(length_row, axis=1, keepdims=True)
    column = line((width, 1), 0)
    row = line((1, width), 1)
    ones = jnp.ones((8, routes_a.shape[1]), BF)

    def columns_of(routes, base):
        held = jnp.where(routes == column + base, 1.0, 0.0)
        rank = jnp.sum(dot(before, held.astype(BF)), axis=1, keepdims=True)
        there = jnp.sum(held, axis=1, keepdims=True)
        hot_t = jnp.where(rank == line((width, cap), 1), 1.0, 0.0) * there
        return held, rank, hot_t

    def rows_of(held):
        there = dot_back(ones, held.astype(BF))
        rank = dot_back(there.astype(BF), before)
        return jnp.where(rank[:1] == line((cap, width), 0), 1.0, 0.0) * there[:1]

    for s in range(group):
        place_here = lane == (hi * 2 + lo) * group + s
        which = jnp.sum(jnp.where(place_here, deal[...].astype(F32), 0.0), axis=1, keepdims=True)
        one = line((seqs, 1), 0) == which
        length = jnp.sum(
            jnp.where(line((1, seqs), 1) == which, length_row, 0.0), axis=1, keepdims=True
        )
        ra, rf, sf = (
            jnp.sum(jnp.where(one, ref[...].astype(F32), 0.0), axis=0, keepdims=True)
            for ref in (routes_a, routes_f, scores)
        )
        held, rank, hot_t = columns_of(ra, here)
        hot = rows_of(held)
        sel_a[s] = hot.astype(BF)
        selt_a[s] = hot_t.astype(BF)
        own_spot = jnp.sum(hot * (row + here + 1.0), axis=1, keepdims=True) - 1.0
        for q in range(4):
            base = float(q * width)
            _, _, other_t = columns_of(ra, base)
            spot = jnp.sum(other_t * (column + base + 1.0), axis=0, keepdims=True) - 1.0
            live = jnp.where((spot >= 0.0) & (spot < length), 1.0, 0.0)
            same = jnp.where(own_spot == spot, 1.0, 0.0)
            heavy_bias[s, :, q * cap : (q + 1) * cap] = jnp.where(live + same > 0.0, 0.0, MASKED)
        for b in range(width // WIN):
            key = line((1, 3 * WIN), 1) + (here + float((b - 1) * WIN))
            live = (key >= 0.0) & (key < length)
            key_bias[s * (width // WIN) + b] = jnp.where(live, 0.0, MASKED)
        valid = jnp.where(column + here < length, 1.0, 0.0)
        mask[s * width : (s + 1) * width, :] = valid
        scale[s * width : (s + 1) * width, :] = 2.0 * valid / (D * count)
        held, rank, hot_t = columns_of(rf, here)
        sel_f[s] = rows_of(held).astype(BF)
        selt_f[s] = hot_t.astype(BF)
        slot = jnp.sum(held * rank, axis=0, keepdims=True)
        owned = jnp.sum(held, axis=0, keepdims=True)
        hits = jnp.where(slot == line((cap, slot.shape[1]), 0), 1.0, 0.0)
        score[s * cap : (s + 1) * cap, :] = jnp.sum(hits * (owned * sf), axis=1, keepdims=True)


def route_shapes(group, width, tokens):
    return [
        jax.ShapeDtypeStruct((group, CAP, width), BF),
        jax.ShapeDtypeStruct((group, width, CAP), BF),
        jax.ShapeDtypeStruct((tokens // WIN, 1, 3 * WIN), F32),
        jax.ShapeDtypeStruct((group, CAP, 4 * CAP), F32),
        jax.ShapeDtypeStruct((group, CAP, width), BF),
        jax.ShapeDtypeStruct((group, width, CAP), BF),
        jax.ShapeDtypeStruct((group * CAP, 1), F32),
        jax.ShapeDtypeStruct((tokens, 1), F32),
        jax.ShapeDtypeStruct((tokens, 1), F32),
    ]


def gather_attend_kernel(dp, nw, *refs):
    n_in, n_out = 8 + nw, 3 + nw + 21
    ins, outs, rest = refs[:n_in], refs[n_in : n_in + n_out], refs[n_in + n_out :]
    xin, ws, hin, hdn = ins[0], ins[1 : 1 + nw], ins[1 + nw], ins[2 + nw]
    integers = ins[3 + nw :]
    xo, wos, hin_o, hdn_o = outs[0], outs[1 : 1 + nw], outs[1 + nw], outs[2 + nw]
    gain, tables, saved = outs[3 + nw], outs[4 + nw : 13 + nw], outs[13 + nw :]
    parts, rest = rest[: 3 * nw + 3], rest[3 * nw + 3 :]
    halves = (parts[:nw], parts[nw : 2 * nw], parts[2 * nw : 3 * nw], parts[3 * nw :])
    g = Gather(dp, xin, ws, hin, hdn, xo, wos, hin_o, hdn_o, rest[:11], halves)
    g.meet()
    for w in range(nw):
        g.swap(w)
    for w in (0, 1, 2):
        g.join(w)
    for w in (0, 1, 2):
        g.plane(w)
    g.rows()
    for w in (3, 4, 5, 6):
        g.join(w)
    g.heavy_plane()
    route_part(*integers, tables)
    g.cross(0)
    g.core(0)
    g.cross(1)
    g.cross(2)
    g.heavy_line()
    g.plane(3)
    g.plane(4)
    g.ready(0)
    total = jnp.zeros(gain.shape, F32)
    for z in range(dp // 2):
        for l2, x2 in ((0, 0), (0, 1), (1, 0), (1, 1)):
            pair = wos[0][z, l2, x2].astype(F32)
            total += pair[:8] + pair[8:]
    gain[...] = total
    g.rows_ready()

    def heavy_projection():
        g.core(1)
        g.core(2)
        g.ready(2)

    def light_projection():
        g.plane(5)
        g.plane(6)
        g.ready(1)

    def keys_travel():
        g.cross(3)
        g.cross(4)

    def half_way():
        g.core(3)
        g.core(4)

    def light_done():
        g.cross(5)
        g.cross(6)

    def heavy_done():
        g.core(5)
        g.core(6)
        g.ready(3)
        g.ready(4)

    full = [wos[w].reshape(-1, wos[w].shape[-1]) for w in range(nw)]
    stages = [heavy_projection, light_projection, keys_travel, half_way, light_done, heavy_done]
    attend_body(
        stages,
        xo.reshape(-1, D),
        gain,
        *tables[:4],
        full[1],
        full[2],
        full[3],
        full[4],
        *saved,
        *rest[11:],
    )
    g.ready(5)
    g.ready(6)
    g.heavy_ready()


def gather_attend(dp, xin, weights, hin, hdn, integers):
    nw = len(weights)
    shapes = gather_shapes(dp, xin, weights, hin, hdn, True)
    group, width = shapes[0].shape[0], dp * xin.shape[1]
    tables = route_shapes(group, width, group * width)
    shapes.append(jax.ShapeDtypeStruct((8, D), F32))
    shapes += tables
    shapes += attend_shapes(group * width, tables[0])
    return call(
        functools.partial(gather_attend_kernel, dp, nw),
        shapes,
        [xin, *weights, hin, hdn, *integers],
        [ANY] * (3 + nw) + [VM] * 5,
        [VM] * 6 + [ANY] * 4 + [VM] * 21,
        [pltpu.VMEM((w.shape[0], w.shape[1] // 2), BF) for w in weights] * 2
        + [pltpu.VMEM((2 * w.shape[0], w.shape[1] // 2), BF) for w in weights]
        + [DMA((nw,))] * 3
        + gather_sems(dp, nw)
        + ATTEND_SEMS,
        1,
    )


def attend_back_body(
    stages,
    d_hidden,
    x,
    gain,
    select,
    select_t,
    key_bias,
    heavy_bias,
    w_lqkv,
    w_hqkv,
    w_lout,
    w_hout,
    xn,
    lq,
    rim,
    lo_out,
    l_lse,
    a_rows,
    hq,
    kvh,
    ho,
    h_lse,
    g_lqkv,
    g_hqkv,
    g_lout,
    g_hout,
    dx,
    stats,
    d_ho,
    d_hproj,
    part,
    got,
    far,
    d_la,
    d_lo,
    d_rim,
    edge,
    edge_in,
    d_lproj,
    ls,
    lr,
    rs,
    rr,
    ss,
    sr,
):
    hi, lo, x_, c = place()
    tokens = x.shape[0]
    group, cap, width = select.shape
    wl, wh = HL * DH, HH * DH
    ones, scaled = pair_masks(1.0), pair_masks(SCORE_SCALE)
    across, partner = at(hi, lo, 1 - x_, c), at(hi, lo, x_, 1 - c)
    picked = []
    for s in range(group):
        high, low = halves(d_hidden[s * width : (s + 1) * width, :])
        picked.append((dot(select[s], high) + dot(select[s], low)).astype(BF))
    d_ha = jnp.concatenate(picked, axis=0)
    d_ho[...] = dot_back(d_ha, w_hout[...]).astype(BF)
    heavy_kv = kvh.reshape(group, 4 * cap, 2 * wh)
    part_kv = part.reshape(group, 4 * cap, 2 * wh)

    def heavy(s, carry):
        r = pl.ds(pl.multiple_of(s * cap, cap), cap)
        bias = heavy_bias[s]
        bias = jnp.concatenate([bias, bias], axis=0)
        lse = h_lse[r, :]
        for pair in range(HH // 2):
            at_k = slice(pair * 128, (pair + 1) * 128)
            at_v = slice(wh + pair * 128, wh + (pair + 1) * 128)
            dq, dk, dv = pair_backward(
                hq[r, at_k],
                heavy_kv[s, :, at_k],
                heavy_kv[s, :, at_v],
                bias,
                get_lse(lse, pair),
                d_ho[r, at_k],
                ones,
                scaled,
            )
            d_hproj[r, at_k] = dq.astype(BF)
            part_kv[s, :, at_k] = dk.astype(BF)
            part_kv[s, :, at_v] = dv.astype(BF)
        return carry

    lax.fori_loop(0, group, heavy, 0)
    beside = [
        send(part.at[:, b * 2 + 1 - c], got.at[b], ss.at[b], sr.at[b], partner) for b in (0, 1)
    ]
    g_hout[...] = dot_grad(ho[...], d_ha).astype(BF)
    stages[0]()

    def light_out_back(r):
        d = d_hidden[r, :].astype(BF)
        d_la[r, :] = d
        d_lo[r, :] = dot_back(d, w_lout[...]).astype(BF)

    tiles(tokens, 256, light_out_back)
    g_lout[...] = dot_grad(lo_out[...], d_la[...]).astype(BF)
    stages[1]()
    for copy in beside:
        copy.wait()
    for b in (0, 1):
        got[b] = (got[b].astype(F32) + part[:, b * 2 + c].astype(F32)).astype(BF)
    third = send(got.at[1 - x_], far, ss.at[2], sr.at[2], across)
    stages[2]()
    d_rim[...] = jnp.zeros(d_rim.shape, F32)
    blocks = width // WIN

    def light(i, carry):
        s, b = i // blocks, i % blocks
        r = pl.ds(pl.multiple_of(i * WIN, WIN), WIN)
        keys = pl.ds(pl.multiple_of(b * WIN, WIN), 3 * WIN)
        bias = reach_bias(key_bias[i])
        lse = l_lse[r, :]
        for pair in range(HL // 2):
            at_k = slice(pair * 128, (pair + 1) * 128)
            at_v = slice(wl + pair * 128, wl + (pair + 1) * 128)
            dq, dk, dv = pair_backward(
                lq[r, at_k],
                rim[s, keys, at_k],
                rim[s, keys, at_v],
                bias,
                get_lse(lse, pair),
                d_lo[r, at_k],
                ones,
                scaled,
            )
            d_lproj[r, at_k] = dq.astype(BF)
            d_rim[s, keys, at_k] += dk
            d_rim[s, keys, at_v] += dv
        return carry

    lax.fori_loop(0, group * blocks // 2, light, 0)
    third.wait()
    total = (got[x_].astype(F32) + far[...].astype(F32)).astype(BF)
    for s in range(group):
        d_hproj[s * cap : (s + 1) * cap, wh:] = total[s]

    def heavy_grad(j):
        g_hqkv[:, j] = dot_grad(a_rows[...], d_hproj[:, j]).astype(BF)

    tiles(3 * wh, 768, heavy_grad)
    stages[3]()
    lax.fori_loop(group * blocks // 2, group * blocks, light, 0)
    edge[0] = d_rim[:, :WIN, :].astype(BF)
    edge[1] = d_rim[:, WIN + width :, :].astype(BF)
    finish = rim_exchange(
        edge.at[0], edge.at[1], edge_in.at[0], edge_in.at[1], ls, lr, rs, rr
    )
    stages[4]()
    d_high, d_low = halves(dot_back(d_hproj[...], w_hqkv[...]))
    finish()
    for s in range(group):
        d_rim[s, WIN : 2 * WIN, :] += edge_in[0, s].astype(F32)
        d_rim[s, width : width + WIN, :] += edge_in[1, s].astype(F32)
        d_lproj[s * width : (s + 1) * width, wl:] = d_rim[s, WIN : WIN + width, :].astype(BF)

    def light_grad(j):
        g_lqkv[:, j] = dot_grad(xn[...], d_lproj[:, j]).astype(BF)

    tiles(3 * wl, 768, light_grad)
    stages[5]()
    stats[...] = jnp.zeros(stats.shape, F32)
    for s in range(group):
        r = slice(s * width, (s + 1) * width)
        q = slice(s * cap, (s + 1) * cap)
        d = dot_back(d_lproj[r, :], w_lqkv[...]) + (
            dot(select_t[s], d_high[q]) + dot(select_t[s], d_low[q])
        )
        h = x[r, :].astype(F32)
        inv = lax.rsqrt(jnp.mean(h * h, axis=-1, keepdims=True) + EPSILON)
        dh = d * h
        stats[0:1, :] += jnp.sum(dh * inv, axis=0, keepdims=True)
        mean = jnp.mean(gain[0:1, :] * dh, axis=-1, keepdims=True)
        dx[r, :] = (
            d_hidden[r, :] + inv * gain[0:1, :] * d - h * (inv * inv * inv * mean)
        ).astype(BF)
    stages[6]()


def attend_back_kernel(*refs):
    meet(line_peers())
    attend_back_body([lambda: None] * 7, *refs)


def attend_back_scratch(tokens, select):
    group, cap, width = select.shape
    wl, wh = HL * DH, HH * DH
    rows = group * cap
    return [
        pltpu.VMEM((rows, wh), BF),
        pltpu.VMEM((rows, 3 * wh), BF),
        pltpu.VMEM((group, 4, cap, 2 * wh), BF),
        pltpu.VMEM((2, group, cap, 2 * wh), BF),
        pltpu.VMEM((group, cap, 2 * wh), BF),
        pltpu.VMEM((tokens, D), BF),
        pltpu.VMEM((tokens, wl), BF),
        pltpu.VMEM((group, width + 2 * WIN, 2 * wl), F32),
        pltpu.VMEM((2, group, WIN, 2 * wl), BF),
        pltpu.VMEM((2, group, WIN, 2 * wl), BF),
        pltpu.VMEM((tokens, 3 * wl), BF),
    ] + ATTEND_SEMS


def attend_back(d_hidden, x, gain, select, select_t, key_bias, heavy_bias, weights, saved):
    tokens = x.shape[0]
    wl, wh = HL * DH, HH * DH
    operands = [d_hidden, x, gain, select, select_t, key_bias, heavy_bias, *weights, *saved]
    shapes = [
        jax.ShapeDtypeStruct((D, 3 * wl), BF),
        jax.ShapeDtypeStruct((D, 3 * wh), BF),
        jax.ShapeDtypeStruct((wl, D), BF),
        jax.ShapeDtypeStruct((wh, D), BF),
        jax.ShapeDtypeStruct((tokens, D), BF),
        jax.ShapeDtypeStruct((8, D), F32),
    ]
    return call(
        attend_back_kernel,
        shapes,
        operands,
        [VM] * len(operands),
        [VM] * len(shapes),
        attend_back_scratch(tokens, select),
        3,
    )


def scatter_kernel(dp, nw, *refs):
    nz = dp // 2
    dx, stats, gs, hin, hdn = refs[0], refs[1], refs[2 : 2 + nw], refs[2 + nw], refs[3 + nw]
    outs = refs[4 + nw :]
    dxo, total, gos, hin_o, hdn_o = outs[0], outs[1], outs[2 : 2 + nw], outs[2 + nw], outs[3 + nw]
    scr = outs[4 + nw :]
    nears, fars, sums, ends = (scr[i * nw : (i + 1) * nw] for i in range(4))
    hin_r, hin_s, hdn_r, sc, sp, sz, acc, acc2 = scr[4 * nw : 4 * nw + 8]
    own, xs, xr, cs, cr, ps, pr, zs, zr, hs, hr, ts, tr = scr[4 * nw + 8 :]
    hi, lo, x, c = place()
    d = hi * 2 + lo
    f = x * 2 + c
    plane = (lo * 2 + x) * 2 + c
    dp_peers = [(lax.rem(d + k, dp), f) for k in range(1, dp)]
    rest = [(a, b, e) for a in (0, 1) for b in (0, 1) for e in (0, 1) if a or b or e]
    flat8 = []
    for a, b, e in rest:
        l2 = 1 - lo if a else lo
        x2 = 1 - x if b else x
        c2 = 1 - c if e else c
        flat8.append((l2, x2, c2))
    meet(dp_peers + [at(hi, *p) for (a, b, e), p in zip(rest, flat8) if b or e])
    partner = at(hi, lo, x, 1 - c)
    quad = quad_peers()
    z_index = [lax.rem(hi + k, nz) for k in range(1, nz)]
    z_peers = [at(z, lo, x, c) for z in z_index]
    c_sends = [
        send(gs[w].at[:, :, :, 1 - c], nears[w], cs.at[w], cr.at[w], partner) for w in range(nw)
    ]
    t_c = send(stats, sc, ts.at[0], tr.at[0], partner)
    mine = keep(dx.at[:, d], dxo.at[d], own)
    x_sends = [
        send(dx.at[:, peer[0]], dxo.at[d], xs.at[k], xr.at[k], peer)
        for k, peer in enumerate(dp_peers)
    ]
    h_sends = []
    for k, z in enumerate(z_index):
        h_sends.append(send(hin.at[z], hin_r.at[k], hs.at[1, k], hr.at[1, k], z_peers[k]))
        h_sends.append(send(hdn.at[z], hdn_r.at[k], hs.at[2, k], hr.at[2, k], z_peers[k]))
    p_sends, z_sends = [], []
    t_c.wait()
    acc[...] = stats[...] + sc[...]
    t_p = [
        send(acc, sp.at[k], ts.at[1 + k], tr.at[1 + k], at(hi, l2, x2, c))
        for k, (l2, x2) in enumerate(quad)
    ]

    def add_core(w):
        c_sends[w].wait()
        near, g = nears[w], gs[w]

        def body(i, carry):
            z, a, b = i // 4, (i // 2) % 2, i % 2
            near[z, a, b] = (near[z, a, b].astype(F32) + g[z, a, b, c].astype(F32)).astype(BF)
            return carry

        lax.fori_loop(0, nz * 4, body, 0)
        p_sends.append(
            [
                send(near.at[:, l2, x2], fars[w].at[k], ps.at[w, k], pr.at[w, k], at(hi, l2, x2, c))
                for k, (l2, x2) in enumerate(quad)
            ]
        )

    def add_plane(w):
        for copy in p_sends[w]:
            copy.wait()
        near, far, part = nears[w], fars[w], sums[w]

        def body(z, carry):
            part[z] = (
                near[z, lo, x].astype(F32)
                + far[0, z].astype(F32)
                + far[1, z].astype(F32)
                + far[2, z].astype(F32)
            ).astype(BF)
            return carry

        lax.fori_loop(0, nz, body, 0)
        z_sends.append(
            [
                send(part.at[z], ends[w].at[k], zs.at[w, k], zr.at[w, k], z_peers[k])
                for k, z in enumerate(z_index)
            ]
        )

    def add_line(w):
        for copy in z_sends[w]:
            copy.wait()
        gos[w][...] = sums[w][hi].astype(F32)
        for k in range(nz - 1):
            gos[w][...] += ends[w][k].astype(F32)

    for w in range(nw):
        add_core(w)
        if w >= 2:
            add_plane(w - 2)
    for copy in t_p:
        copy.wait()
    acc2[...] = acc[...] + sp[0] + sp[1] + sp[2]
    t_z = [send(acc2, sz.at[k], ts.at[4 + k], tr.at[4 + k], z_peers[k]) for k in range(nz - 1)]
    for copy in h_sends:
        copy.wait()

    def body(i, carry):
        value = hin[hi, i].astype(F32)
        for k in range(nz - 1):
            value += hin_r[k, i].astype(F32)
        hin_s[i] = value.astype(BF)
        return carry

    lax.fori_loop(0, 8, body, 0)
    hin_o[plane] = hin_s[plane]
    a_sends = [
        send(
            hin_s.at[(l2 * 2 + x2) * 2 + c2],
            hin_o.at[plane],
            hs.at[0, k],
            hr.at[0, k],
            at(hi, l2, x2, c2),
        )
        for k, (l2, x2, c2) in enumerate(flat8)
    ]
    hdn_o[...] = hdn[hi].astype(F32)
    for k in range(nz - 1):
        hdn_o[...] += hdn_r[k].astype(F32)
    for w in range(max(nw - 2, 0), nw):
        add_plane(w)
    for copy in t_z:
        copy.wait()
    total[...] = acc2[...]
    for k in range(nz - 1):
        total[...] += sz[k]
    for w in range(nw):
        add_line(w)
    mine.wait()
    for copy in x_sends + a_sends:
        copy.wait()


def scatter_all(dp, dx, stats, grads, hin, hdn):
    nz = dp // 2
    nw = len(grads)
    group, _, rows, _ = dx.shape
    tiles = [g.shape[4:] for g in grads]
    most = max(7, nz)
    scratch = [pltpu.VMEM((nz, 2, 2) + t, BF) for t in tiles]
    scratch += [pltpu.VMEM((3, nz) + t, BF) for t in tiles]
    scratch += [pltpu.VMEM((nz,) + t, BF) for t in tiles]
    scratch += [pltpu.VMEM((nz - 1,) + t, BF) for t in tiles]
    scratch += [
        pltpu.VMEM((nz - 1,) + hin.shape[1:], BF),
        pltpu.VMEM(hin.shape[1:], BF),
        pltpu.VMEM((nz - 1,) + hdn.shape[1:], BF),
        pltpu.VMEM(stats.shape, F32),
        pltpu.VMEM((3,) + stats.shape, F32),
        pltpu.VMEM((nz - 1,) + stats.shape, F32),
        pltpu.VMEM(stats.shape, F32),
        pltpu.VMEM(stats.shape, F32),
        DMA,
        DMA((dp,)),
        DMA((dp,)),
        DMA((nw,)),
        DMA((nw,)),
        DMA((nw, 3)),
        DMA((nw, 3)),
        DMA((nw, nz)),
        DMA((nw, nz)),
        DMA((3, most)),
        DMA((3, most)),
        DMA((4 + nz,)),
        DMA((4 + nz,)),
    ]
    shapes = [jax.ShapeDtypeStruct((dp, group, rows, D), BF), jax.ShapeDtypeStruct(stats.shape, F32)]
    shapes += [jax.ShapeDtypeStruct(t, F32) for t in tiles]
    shapes.append(jax.ShapeDtypeStruct(hin.shape[1:], BF))
    shapes.append(jax.ShapeDtypeStruct(hdn.shape[1:], F32))
    return call(
        functools.partial(scatter_kernel, dp, nw),
        shapes,
        [dx, stats, *grads, hin, hdn],
        [ANY] + [VM] * (3 + nw),
        [ANY] + [VM] * (3 + nw),
        scratch,
        4,
    )


class Scatter:
    def __init__(self, nz, shards, gs, near, one, two, end, sems):
        self.nz, self.shards, self.gs = nz, shards, gs
        self.near, self.one, self.two, self.end = near, one, two, end
        self.cs, self.cr, self.ps, self.pr, self.zs, self.zr = sems
        self.hi, self.lo, self.x, self.c = hi, lo, x, c = place()
        self.partner = at(hi, lo, x, 1 - c)
        self.by_x, self.by_y = at(hi, lo, 1 - x, c), at(hi, 1 - lo, x, c)
        self.z_index = [lax.rem(hi + k, nz) for k in range(1, nz)]
        self.copies = {}

    def lanes(self, w, c):
        half = self.shards[w][1] // 2
        return pl.ds(pl.multiple_of(c * half, 128), half)

    def core(self, w):
        out = self.gs[w].at[:, :, :, :, self.lanes(w, 1 - self.c)]
        self.copies[w, 0] = [send(out, self.near[w], self.cs.at[w], self.cr.at[w], self.partner)]

    def wait(self, w, stage):
        for copy in self.copies[w, stage]:
            copy.wait()

    def plane(self, w):
        g, own = self.gs[w], self.lanes(w, self.c)
        self.add_plane(w, lambda z, a, b: g[z, a, b, :, own])

    def own_plane(self, w, kept):
        self.add_plane(w, lambda z, a, b: kept[z, a, b])

    def add_plane(self, w, own):
        self.wait(w, 0)
        near = self.near[w]
        lo, x, half = self.lo, self.x, self.nz // 2

        def body(i, carry):
            z, a, b = i // 4, (i // 2) % 2, i % 2
            near[z, a, b] = (near[z, a, b].astype(F32) + own(z, a, b).astype(F32)).astype(BF)
            return carry

        lax.fori_loop(0, self.nz * 4, body, 0)
        low, high = pl.ds(0, half), pl.ds(half, self.nz - half)
        self.copies[w, 1] = [
            send(near.at[low, :, 1 - x], self.one[w].at[low], self.ps.at[w, 0], self.pr.at[w, 0], self.by_x),
            send(near.at[high, 1 - lo], self.one[w].at[high], self.ps.at[w, 1], self.pr.at[w, 1], self.by_y),
        ]

    def cross(self, w):
        self.wait(w, 1)
        near, one, lo, x, half = self.near[w], self.one[w], self.lo, self.x, self.nz // 2

        def low_body(i, carry):
            z, a = i // 2, i % 2
            near[z, a, x] = (near[z, a, x].astype(F32) + one[z, a].astype(F32)).astype(BF)
            return carry

        def high_body(i, carry):
            z, b = half + i // 2, i % 2
            near[z, lo, b] = (near[z, lo, b].astype(F32) + one[z, b].astype(F32)).astype(BF)
            return carry

        lax.fori_loop(0, half * 2, low_body, 0)
        lax.fori_loop(0, (self.nz - half) * 2, high_body, 0)
        low, high = pl.ds(0, half), pl.ds(half, self.nz - half)
        two = self.two[w]
        self.copies[w, 2] = [
            send(near.at[low, 1 - lo, x], two.at[low], self.ps.at[w, 2], self.pr.at[w, 2], self.by_y),
            send(near.at[high, lo, 1 - x], two.at[high], self.ps.at[w, 3], self.pr.at[w, 3], self.by_x),
        ]

    def line(self, w):
        self.wait(w, 2)
        near, part, lo, x = self.near[w], self.two[w], self.lo, self.x

        def body(z, carry):
            part[z] = (near[z, lo, x].astype(F32) + part[z].astype(F32)).astype(BF)
            return carry

        lax.fori_loop(0, self.nz, body, 0)
        self.copies[w, 3] = [
            send(
                part.at[z],
                self.end[w].at[k],
                self.zs.at[w, k],
                self.zr.at[w, k],
                at(z, lo, x, self.c),
            )
            for k, z in enumerate(self.z_index)
        ]

    def last(self, w, fin, out, sems):
        self.wait(w, 3)
        value = self.two[w][self.hi].astype(F32)
        for k in range(self.nz - 1):
            value += self.end[w][k].astype(F32)
        fin[...] = value
        count = self.shards[w][0]
        own = pl.ds(pl.multiple_of(self.c * count, 8), count)
        mate = pl.ds(pl.multiple_of((1 - self.c) * count, 8), count)
        spot = out.at[:, self.lanes(w, self.c)]
        return [
            keep(fin.at[own], spot, sems[0].at[w]),
            send(fin.at[mate], spot, sems[1].at[w], sems[2].at[w], self.partner),
        ]


def back_scatter_kernel(dp, shards, *refs):
    nz, nw = dp // 2, len(shards)
    n_ops = 7 + 4 + 10
    ops, (g_lin, g_ldn, hin, hdn, ffn_stats) = refs[:n_ops], refs[n_ops : n_ops + 5]
    outs, rest = refs[n_ops + 5 : n_ops + 9 + nw], refs[n_ops + 9 + nw :]
    dxo, total, gos, hin_o, hdn_o = outs[0], outs[1], outs[2 : 2 + nw], outs[2 + nw], outs[3 + nw]
    full, rest = rest[:4], rest[4:]
    own_lin, own_ldn, stats, rest = rest[0], rest[1], rest[2], rest[3:]
    back, rest = rest[:17], rest[17:]
    dx = back[5]
    near, one, two, end, fin = (rest[k * nw : (k + 1) * nw] for k in range(5))
    hin_own, hdn_own, hin_r, hdn_r, acc, sc, sp, sz, acc2 = rest[5 * nw : 5 * nw + 9]
    own, xs, xr, cs, cr, ps, pr, zs, zr, hs, hr, ts, tr, *fsem = rest[5 * nw + 9 :]
    hi, lo, x, c = place()
    d = hi * 2 + lo
    plane = (lo * 2 + x) * 2 + c
    others = plane_others()
    rows_to = [(lax.rem(d + k, dp), x * 2 + c) for k in range(1, dp)]
    z_index = [lax.rem(hi + k, nz) for k in range(1, nz)]
    z_to = [at(z, lo, x, c) for z in z_index]
    quad = quad_peers()
    g_views = [g_lin, g_ldn]
    for k, w in enumerate((2, 3, 4, 5)):
        rows, columns = shards[w]
        g_views.append(full[k].reshape(nz, 2, 2, 2 * rows, columns))
    t = Scatter(nz, shards, g_views, near, one, two, end, (cs, cr, ps, pr, zs, zr))
    meet(rows_to + [at(hi, *q[:3]) for q in others if q[3]])
    h_sends = []
    for k, z in enumerate(z_index):
        h_sends.append(send(hin.at[z], hin_r.at[k], hs.at[1, k], hr.at[1, k], z_to[k]))
        h_sends.append(send(hdn.at[z], hdn_r.at[k], hs.at[2, k], hr.at[2, k], z_to[k]))
    t.core(0)
    t.core(1)
    kept = [
        keep(g_lin.at[:, :, :, :, t.lanes(0, c)], own_lin, own.at[0]),
        keep(g_ldn.at[:, :, :, :, t.lanes(1, c)], own_ldn, own.at[1]),
        keep(hin.at[hi], hin_own, own.at[2]),
        keep(hdn.at[hi], hdn_own, own.at[3]),
    ]
    late = []

    def first_plane():
        kept[0].wait()
        kept[1].wait()
        t.own_plane(0, own_lin)
        t.own_plane(1, own_ldn)
        t.core(2)

    def out_core():
        t.core(3)

    def before_light():
        t.cross(0)
        t.cross(1)
        t.plane(2)

    def half_way():
        t.core(4)
        t.plane(3)
        t.line(0)
        t.line(1)

    def rims_left():
        t.plane(4)
        t.cross(2)
        t.cross(3)

    def light_grad_done():
        t.core(5)
        t.line(2)
        t.line(3)

    def rows_done():
        rows = dx.reshape(dxo.shape[1], dp, dxo.shape[2], D)
        late.append(keep(rows.at[:, d], dxo.at[d], own.at[4]))
        for k, to in enumerate(rows_to):
            late.append(send(rows.at[:, to[0]], dxo.at[d], xs.at[k], xr.at[k], to))

    stages = [
        first_plane,
        out_core,
        before_light,
        half_way,
        rims_left,
        light_grad_done,
        rows_done,
    ]
    attend_back_body(
        stages, *ops, full[3], full[2], full[1], full[0], dx, stats, *back
    )
    partner = at(hi, lo, x, 1 - c)
    for k in range(6):
        lanes = slice(k * 128, (k + 1) * 128)
        acc[k : k + 1, :] = stats[0:1, lanes]
        acc[6 + k : 7 + k, :] = ffn_stats[0:1, lanes]
    loss = jnp.sum(ffn_stats[1:2, :], axis=-1, keepdims=True)
    acc[12:16, :] = jnp.broadcast_to(loss, (4, 128))
    t_c = send(acc, sc, ts.at[0], tr.at[0], partner)
    t.plane(5)
    t.cross(4)
    t.line(4)
    t_c.wait()
    acc2[...] = acc[...] + sc[...]
    t_p = [
        send(acc2, sp.at[k], ts.at[1 + k], tr.at[1 + k], at(hi, l2, x2, c))
        for k, (l2, x2) in enumerate(quad)
    ]
    for copy in h_sends + kept[2:]:
        copy.wait()

    def body(i, carry):
        value = hin_own[i].astype(F32)
        for k in range(nz - 1):
            value += hin_r[k, i].astype(F32)
        hin_own[i] = value.astype(BF)
        return carry

    lax.fori_loop(0, 8, body, 0)
    hin_o[plane] = hin_own[plane]
    late += [
        send(
            hin_own.at[(q[0] * 2 + q[1]) * 2 + q[2]],
            hin_o.at[plane],
            hs.at[0, k],
            hr.at[0, k],
            at(hi, *q[:3]),
        )
        for k, q in enumerate(others)
    ]
    value = hdn_own[...].astype(F32)
    for k in range(nz - 1):
        value += hdn_r[k].astype(F32)
    hdn_o[...] = value
    t.cross(5)
    for copy in t_p:
        copy.wait()
    acc[...] = acc2[...] + sp[0] + sp[1] + sp[2]
    t_z = [send(acc, sz.at[k], ts.at[4 + k], tr.at[4 + k], z_to[k]) for k in range(nz - 1)]
    t.line(5)
    for w in range(nw):
        late += t.last(w, fin[w], gos[w], fsem)
    for copy in t_z:
        copy.wait()
    value = acc[...]
    for k in range(nz - 1):
        value += sz[k]
    total[...] = value
    for copy in late:
        copy.wait()


def back_scatter(dp, rows, d_hidden, x, gain, masks, weights, saved, ffn_grads, ffn_stats, shards, hin, hdn):
    nz, nw = dp // 2, len(shards)
    tokens = x.shape[0]
    group = masks[0].shape[0]
    most = max(7, nz)
    stat_shape = (16, 128)
    paired = [
        g.reshape(nz, 2, 2, 2 * s[0], s[1]) for g, s in zip(ffn_grads, shards)
    ]
    operands = [d_hidden, x, gain, *masks, *weights, *saved, *paired, hin, hdn, ffn_stats]
    shapes = [jax.ShapeDtypeStruct((dp, group, rows, D), BF), jax.ShapeDtypeStruct(stat_shape, F32)]
    shapes += [jax.ShapeDtypeStruct(s, F32) for s in shards]
    shapes.append(jax.ShapeDtypeStruct(hin.shape[1:], BF))
    shapes.append(jax.ShapeDtypeStruct(hdn.shape[1:], F32))
    scratch = [pltpu.VMEM((s[0] * 8 * nz, s[1]), BF) for s in shards[2:]]
    split = [(2 * s[0], s[1] // 2) for s in shards]
    scratch += [pltpu.VMEM((nz, 2, 2) + s, BF) for s in split[:2]]
    scratch += [pltpu.VMEM((8, D), F32)]
    scratch += attend_back_scratch(tokens, masks[0])
    scratch += [pltpu.VMEM((nz, 2, 2) + s, BF) for s in split]
    scratch += [pltpu.VMEM((nz, 2) + s, BF) for s in split]
    scratch += [pltpu.VMEM((nz,) + s, BF) for s in split]
    scratch += [pltpu.VMEM((nz - 1,) + s, BF) for s in split]
    scratch += [pltpu.VMEM(s, F32) for s in split]
    scratch += [
        pltpu.VMEM(hin.shape[1:], BF),
        pltpu.VMEM(hdn.shape[1:], BF),
        pltpu.VMEM((nz - 1,) + hin.shape[1:], BF),
        pltpu.VMEM((nz - 1,) + hdn.shape[1:], BF),
        pltpu.VMEM(stat_shape, F32),
        pltpu.VMEM(stat_shape, F32),
        pltpu.VMEM((3,) + stat_shape, F32),
        pltpu.VMEM((nz - 1,) + stat_shape, F32),
        pltpu.VMEM(stat_shape, F32),
        DMA((5,)),
        DMA((dp,)),
        DMA((dp,)),
        DMA((nw,)),
        DMA((nw,)),
        DMA((nw, 4)),
        DMA((nw, 4)),
        DMA((nw, nz)),
        DMA((nw, nz)),
        DMA((3, most)),
        DMA((3, most)),
        DMA((4 + nz,)),
        DMA((4 + nz,)),
        DMA((nw,)),
        DMA((nw,)),
        DMA((nw,)),
    ]
    return call(
        functools.partial(back_scatter_kernel, dp, shards),
        shapes,
        operands,
        [VM] * (len(operands) - 5) + [ANY] * 4 + [VM],
        [VM] * len(shapes),
        scratch,
        6,
    )


def routing(routes, pieces, piece_len):
    places = jnp.arange(pieces * piece_len)
    routed = jnp.any(routes[:, None, :] == places[None, :, None], axis=-1)
    routed = routed.reshape(-1, pieces, piece_len)
    before = jnp.arange(piece_len)[:, None] < jnp.arange(piece_len)[None, :]
    rank = jnp.einsum(
        "skp,pq->skq", routed.astype(BF), before.astype(BF), preferred_element_type=F32
    )
    slots = jnp.arange(CAP, dtype=F32)
    hot = routed[:, :, None, :] & (rank[:, :, None, :] == slots[None, None, :, None])
    filled = jnp.any(hot, axis=-1)
    spots = jnp.sum(jnp.where(hot, places.reshape(1, pieces, 1, piece_len), 0), axis=-1)
    return hot, jnp.where(filled, spots, -1)


def local(
    layer_input,
    teacher,
    lengths,
    dealing,
    attn_routes,
    ffn_routes,
    ffn_scores,
    gain_attn,
    gain_ffn,
    light_qkv,
    light_out,
    heavy_qkv,
    heavy_out,
    light_in,
    light_down,
    heavy_in,
    heavy_down,
):
    dp = lax.axis_size("dp")
    pieces = lax.axis_size("fsdp")
    data_index = lax.axis_index("dp")
    piece = lax.axis_index("fsdp")
    nz = dp // 2
    n = dp * pieces
    seqs = dealing.shape[0]
    group = seqs // dp
    gain_len = gain_attn.shape[0]
    hidden_units = heavy_in.shape[1] // 2 // n
    mine = data_index * pieces + piece
    tokens = layer_input.shape[2] * dp
    matrices = (light_qkv, heavy_qkv, light_out, heavy_out, light_in, light_down)
    hin_rows = heavy_in.shape[0]
    token_count = jnp.sum(lengths).astype(F32)
    merged = (
        layer_input.shape[2] % 16 == 0
        and hidden_units % 128 == 0
        and all(m.shape[0] % 8 == 0 and m.shape[1] % 256 == 0 for m in (*matrices, heavy_down))
    )
    if merged:
        xin, hin_src, gains = prepare(dealing, layer_input[:, 0], heavy_in, gain_attn, gain_ffn)
        integers = (dealing.reshape(1, -1), lengths.reshape(1, -1), attn_routes, ffn_routes, ffn_scores)
        got = gather_attend(dp, xin, [gains, *matrices], hin_src, heavy_down, integers)
    else:
        xin = deal_rows(dealing, layer_input[:, 0])
        owned = jnp.arange(D)[None, :] // gain_len == mine
        spread_out = jnp.broadcast_to(
            jnp.stack([gain_attn, gain_ffn])[:, None, :], (2, D // gain_len, gain_len)
        ).reshape(2, D)
        gains = jnp.pad(jnp.where(owned, spread_out, 0.0).astype(BF), ((0, 6), (0, 0)))
        hin_src = (
            heavy_in.reshape(hin_rows, 2, nz, 8, hidden_units)
            .transpose(3, 0, 1, 2, 4)
            .reshape(8, hin_rows, 2 * nz * hidden_units)
        )
        if hin_rows % 8:
            hin_src = hin_src.reshape(8, -1, 128)
        got = gather_all(dp, xin, [gains] + [packed(m) for m in matrices], hin_src, heavy_down)
    flat_x = got[0].reshape(-1, D)
    w_lqkv, w_hqkv, w_lout, w_hout, w_lin, w_ldown = (
        unpacked(full, *m.shape) for full, m in zip(got[2:8], matrices)
    )
    w_hin = unpacked(got[8], hin_rows, 2 * nz * hidden_units)
    w_hdown = got[9].reshape(-1, D)
    attn_weights = (w_lqkv, w_hqkv, w_lout, w_hout)
    if merged:
        gain, tables, (hidden, *saved) = got[10], got[11:20], got[20:]
        masks, ffn_masks = tables[:4], tables[4:]
    else:
        gain = jnp.sum(got[1].reshape(n, 8, D).astype(F32), axis=0)
        masks, ffn_masks = integer_tables(
            dealing, lengths, attn_routes, ffn_routes, ffn_scores, group, pieces, tokens
        )
        hidden, *saved = attend(flat_x, gain, *masks, *attn_weights)
    f_select, f_select_t, slot_score, weight_mask, weight_scale = ffn_masks
    grad_lin, grad_ldown, grad_hin, grad_hdown, d_hidden, ffn_stats = feed_forward(
        hidden,
        f_select,
        f_select_t,
        slot_score,
        gain,
        teacher.reshape(-1, D),
        weight_mask,
        weight_scale,
        w_lin,
        w_ldown,
        w_hin,
        w_hdown,
    )
    rows = tokens // dp
    shards = (light_in, light_down, heavy_out, light_out, heavy_qkv, light_qkv)
    hin_part = grad_hin.reshape((nz, 8) + hin_src.shape[1:])
    hdn_part = grad_hdown.reshape(nz, -1, D)
    if merged:
        done = back_scatter(
            dp,
            rows,
            d_hidden,
            flat_x,
            gain,
            masks,
            attn_weights,
            saved,
            (grad_lin, grad_ldown),
            ffn_stats,
            tuple(shard.shape for shard in shards),
            hin_part,
            hdn_part,
        )
    else:
        grad_lqkv, grad_hqkv, grad_lout, grad_hout, d_inputs, attn_stats = attend_back(
            d_hidden, flat_x, gain, *masks, attn_weights, saved
        )
        stats = jnp.concatenate(
            [
                attn_stats[0].reshape(-1, 128),
                ffn_stats[0].reshape(-1, 128),
                jnp.broadcast_to(jnp.sum(ffn_stats[1]), (4, 128)),
            ]
        )
        grads = (grad_lin, grad_ldown, grad_hout, grad_lout, grad_hqkv, grad_lqkv)
        sent = [packed_full(grad, shard.shape, nz) for grad, shard in zip(grads, shards)]
        done = scatter_all(
            dp, d_inputs.reshape(group, dp, rows, D), stats, sent, hin_part, hdn_part
        )
    summed = done[1]
    loss_value = summed[12, 0] / (D * token_count)
    own_one = lax.dynamic_slice_in_dim(summed[:6].reshape(-1), mine * gain_len, gain_len)
    own_two = lax.dynamic_slice_in_dim(summed[6:12].reshape(-1), mine * gain_len, gain_len)
    back_rows = done[0].reshape(seqs, rows, D)
    if merged:
        d_layer, g_hin, *owned = finish_all(
            n, dealing, back_rows, done[8], [*done[2:8], done[9]], heavy_in.shape
        )
    else:
        d_layer = undeal_rows(dealing, back_rows)
        owned = [full.reshape(shard.shape) for full, shard in zip(done[2:8], shards)]
        owned.append(done[9].reshape(heavy_down.shape))
        g_hin = (
            done[8]
            .astype(F32)
            .reshape(8, hin_rows, 2, nz, hidden_units)
            .transpose(1, 2, 3, 0, 4)
            .reshape(heavy_in.shape)
        )
    g_lin, g_ldown, g_hout, g_lout, g_hqkv, g_lqkv, g_hdown = owned
    return (
        loss_value,
        d_layer[:, None],
        own_one,
        own_two,
        g_lqkv,
        g_lout,
        g_hqkv,
        g_hout,
        g_lin,
        g_ldown,
        g_hin,
        g_hdown,
    )


def integer_tables(dealing, lengths, attn_routes, ffn_routes, ffn_scores, group, pieces, tokens):
    seqs = dealing.shape[0]
    data_index = lax.axis_index("dp")
    piece = lax.axis_index("fsdp")
    chosen = lax.dynamic_slice_in_dim(dealing, data_index * group, group)
    one = chosen[:, None] == jnp.arange(seqs)[None, :]
    seq_lengths = jnp.sum(jnp.where(one, lengths[None, :], 0), axis=1)
    attn_pick = jnp.sum(jnp.where(one[:, :, None], attn_routes[None], 0), axis=1)
    ffn_pick = jnp.sum(jnp.where(one[:, :, None], ffn_routes[None], 0), axis=1)
    score_pick = jnp.sum(jnp.where(one[:, :, None], ffn_scores[None], 0.0), axis=1)
    token_count = jnp.sum(lengths).astype(F32)
    positions = piece * tokens + jnp.arange(tokens)
    valid_mask = positions[None, :] < seq_lengths[:, None]
    a_hot, a_spots = routing(attn_pick, pieces, tokens)
    f_hot, f_spots = routing(ffn_pick, pieces, tokens)
    a_select = lax.dynamic_index_in_dim(a_hot, piece, 1, False).astype(BF)
    f_select = lax.dynamic_index_in_dim(f_hot, piece, 1, False).astype(BF)
    a_spot = lax.dynamic_index_in_dim(a_spots, piece, 1, False)
    f_spot = lax.dynamic_index_in_dim(f_spots, piece, 1, False)
    slot_score = jnp.sum(
        jnp.where(f_spot[:, :, None] == ffn_pick[:, None, :], score_pick[:, None, :], 0.0), axis=-1
    )
    key_pos = piece * tokens - WIN + jnp.arange(tokens + 2 * WIN)
    live_key = (key_pos >= 0)[None, :] & (key_pos[None, :] < seq_lengths[:, None])
    key_line = jnp.where(live_key, 0.0, MASKED)
    key_bias = jnp.stack(
        [key_line[:, b : b + 3 * WIN] for b in range(0, tokens, WIN)], axis=1
    ).reshape(-1, 1, 3 * WIN)
    all_spots = a_spots.reshape(group, pieces * CAP)
    heavy_allowed = ((all_spots >= 0) & (all_spots < seq_lengths[:, None]))[:, None, :] | (
        a_spot[:, :, None] == all_spots[:, None, :]
    )
    heavy_bias = jnp.where(heavy_allowed, 0.0, MASKED)
    weight_mask = valid_mask.reshape(-1, 1).astype(F32)
    masks = (a_select, a_select.swapaxes(1, 2), key_bias, heavy_bias)
    ffn_masks = (
        f_select,
        f_select.swapaxes(1, 2),
        slot_score.reshape(-1, 1),
        weight_mask,
        2.0 * weight_mask / (D * token_count),
    )
    return masks, ffn_masks


def packed_full(grad, shard_shape, nz):
    rows, columns = shard_shape
    if rows % 8 == 0:
        return grad.reshape(nz, 2, 2, 2, rows, columns)
    return grad.reshape(nz, 2, 2, 2, rows * columns // 128, 128)


def solution(mesh):
    split = P(("dp", "fsdp"))
    matrix = P(("dp", "fsdp"), None)
    placed = (
        P(None, "fsdp", "dp", None),
        P("dp", "fsdp", None, None),
        P(),
        P(),
        P(),
        P(),
        P(),
        split,
        split,
    ) + (matrix,) * 8
    return jax.shard_map(
        local,
        mesh=mesh,
        in_specs=placed,
        out_specs=(P(), P(None, "fsdp", "dp", None), split, split) + (matrix,) * 8,
        check_vma=False,
    )
```

```python
import functools
import jax
import jax.numpy as jnp
from jax import lax
from jax.experimental import pallas as pl
from jax.experimental.pallas import tpu as pltpu
from jax.sharding import PartitionSpec as P

D = 768
HL = 8
HH = 12
DH = 64
FL = 1024
FH = 4096
WIN = 128
CAP = 64

EPSILON = 1e-06
MASKED = -1000000000.0
SCORE_SCALE = 0.125
MESH = pl.DeviceIdType.MESH
BF = jnp.bfloat16
F32 = jnp.float32
ANY = pl.BlockSpec(memory_space=pl.ANY)
VM = pl.BlockSpec(memory_space=pltpu.VMEM)
DMA = pltpu.SemaphoreType.DMA
VMEM_BYTES = 60 * 1024 * 1024


def place():
    d = lax.axis_index("dp")
    f = lax.axis_index("fsdp")
    return d // 2, d % 2, f // 2, f % 2


def at(hi, lo, x, c):
    return (hi * 2 + lo, x * 2 + c)


def meet(peers):
    barrier = pltpu.get_barrier_semaphore()
    for peer in peers:
        pl.semaphore_signal(barrier, inc=1, device_id=peer, device_id_type=MESH)
    pl.semaphore_wait(barrier, len(peers))


def send(src, dst, send_sem, recv_sem, peer):
    copy = pltpu.make_async_remote_copy(
        src_ref=src,
        dst_ref=dst,
        send_sem=send_sem,
        recv_sem=recv_sem,
        device_id=peer,
        device_id_type=MESH,
    )
    copy.start()
    return copy


def keep(src, dst, sem):
    copy = pltpu.make_async_copy(src, dst, sem)
    copy.start()
    return copy


def quad_peers():
    hi, lo, x, c = place()
    return [(lo, 1 - x), (1 - lo, x), (1 - lo, 1 - x)]


def call(kernel, out_shape, operands, in_specs, out_specs, scratch, collective_id):
    return pl.pallas_call(
        kernel,
        out_shape=out_shape,
        in_specs=in_specs,
        out_specs=out_specs,
        scratch_shapes=scratch,
        compiler_params=pltpu.CompilerParams(
            collective_id=collective_id, has_side_effects=True, vmem_limit_bytes=VMEM_BYTES
        ),
    )(*operands)


def deal_kernel(deal_ref, x_ref, o_ref):
    def body(i, carry):
        o_ref[i] = x_ref[deal_ref[i]]
        return carry

    lax.fori_loop(0, o_ref.shape[0], body, 0)


def deal_rows(dealing, rows):
    return pl.pallas_call(
        deal_kernel,
        out_shape=jax.ShapeDtypeStruct(rows.shape, rows.dtype),
        in_specs=[pl.BlockSpec(memory_space=pltpu.SMEM), VM],
        out_specs=VM,
        compiler_params=pltpu.CompilerParams(vmem_limit_bytes=VMEM_BYTES),
    )(dealing, rows)


def undeal_kernel(deal_ref, x_ref, o_ref):
    def body(i, carry):
        o_ref[deal_ref[i]] = x_ref[i].astype(F32)
        return carry

    lax.fori_loop(0, x_ref.shape[0], body, 0)


def undeal_rows(dealing, rows):
    return pl.pallas_call(
        undeal_kernel,
        out_shape=jax.ShapeDtypeStruct(rows.shape, F32),
        in_specs=[pl.BlockSpec(memory_space=pltpu.SMEM), VM],
        out_specs=VM,
        compiler_params=pltpu.CompilerParams(vmem_limit_bytes=VMEM_BYTES),
    )(dealing, rows)


def prepare_kernel(deal_ref, x_ref, heavy_ref, one_ref, two_ref, xin, hin, gains):
    def body(i, carry):
        xin[i] = x_ref[deal_ref[i]]
        return carry

    lax.fori_loop(0, xin.shape[0], body, 0)
    count = one_ref.shape[1]
    units = D // count
    step = heavy_ref.shape[1] // 2 // units
    for j in range(8):
        for k in range(units // 8):
            for g in (0, 1):
                start = g * heavy_ref.shape[1] // 2 + (k * 8 + j) * step
                spot = (g * (units // 8) + k) * step
                hin[j, :, spot : spot + step] = heavy_ref[:, start : start + step]
    mine = lax.axis_index("dp") * 4 + lax.axis_index("fsdp")
    row = lax.broadcasted_iota(jnp.int32, (count, D), 0)
    lane = lax.broadcasted_iota(jnp.int32, (count, D), 1)
    hot = jnp.where(lane == row + mine * count, 1.0, 0.0).astype(BF)
    lines = [jnp.broadcast_to(ref[...], (8, count)) for ref in (one_ref, two_ref)]
    one, two = (jnp.dot(line, hot, preferred_element_type=F32) for line in lines)
    kind = lax.broadcasted_iota(jnp.int32, (8, D), 0)
    gains[...] = jnp.where(kind == 0, one, jnp.where(kind == 1, two, 0.0)).astype(BF)


def prepare(dealing, rows, heavy_in, gain_one, gain_two):
    count = gain_one.shape[0]
    columns = heavy_in.shape[1] // 8
    return pl.pallas_call(
        prepare_kernel,
        out_shape=[
            jax.ShapeDtypeStruct(rows.shape, BF),
            jax.ShapeDtypeStruct((8, heavy_in.shape[0], columns), BF),
            jax.ShapeDtypeStruct((8, D), BF),
        ],
        in_specs=[pl.BlockSpec(memory_space=pltpu.SMEM), VM, VM, VM, VM],
        out_specs=[VM] * 3,
        compiler_params=pltpu.CompilerParams(vmem_limit_bytes=VMEM_BYTES),
    )(dealing, rows, heavy_in, gain_one.reshape(1, count), gain_two.reshape(1, count))


def finish_kernel(units, deal_ref, x_ref, hin, *refs):
    count = (len(refs) - 2) // 2
    ins, (rows, heavy), outs = refs[:count], refs[count : count + 2], refs[count + 2 :]

    def body(i, carry):
        rows[deal_ref[i]] = x_ref[i].astype(F32)
        return carry

    lax.fori_loop(0, x_ref.shape[0], body, 0)
    step = heavy.shape[1] // 2 // units
    for j in range(8):
        for k in range(units // 8):
            for g in (0, 1):
                start = g * heavy.shape[1] // 2 + (k * 8 + j) * step
                spot = (g * (units // 8) + k) * step
                heavy[:, start : start + step] = hin[j, :, spot : spot + step].astype(F32)
    for source, out in zip(ins, outs):
        out[...] = source[...]


def finish_all(units, dealing, rows, hin, grads, heavy_shape):
    shapes = [jax.ShapeDtypeStruct(rows.shape, F32), jax.ShapeDtypeStruct(heavy_shape, F32)]
    shapes += [jax.ShapeDtypeStruct(g.shape, F32) for g in grads]
    return pl.pallas_call(
        functools.partial(finish_kernel, units),
        out_shape=shapes,
        in_specs=[pl.BlockSpec(memory_space=pltpu.SMEM)] + [VM] * (2 + len(grads)),
        out_specs=[VM] * len(shapes),
        compiler_params=pltpu.CompilerParams(vmem_limit_bytes=VMEM_BYTES),
    )(dealing, rows, hin, *grads)


def packed(matrix):
    rows, columns = matrix.shape
    if rows % 8 == 0:
        return matrix
    return matrix.reshape(rows * columns // 128, 128)


def unpacked(gathered, rows, columns):
    return gathered.reshape(-1, rows, columns).reshape(-1, columns)


def plane_others():
    hi, lo, x, c = place()
    others = []
    for a in (0, 1):
        for b in (0, 1):
            for e in (0, 1):
                if a or b or e:
                    others.append(
                        (1 - lo if a else lo, 1 - x if b else x, 1 - c if e else c, b or e)
                    )
    return others


class Gather:
    def __init__(self, dp, xin, ws, hin, xo, wos, hin_o, sems, halves=None):
        self.dp, self.nz = dp, dp // 2
        self.xin, self.ws, self.hin = xin, ws, hin
        self.xo, self.wos, self.hin_o = xo, wos, hin_o
        self.loc, self.xs, self.xr, self.zs, self.zr = sems[:5]
        self.ps, self.pr, self.cs, self.cr, self.hs, self.hr = sems[5:]
        self.hi, self.lo, self.x, self.c = place()
        hi, lo, x, c = place()
        self.d = hi * 2 + lo
        self.home = (lo * 2 + x) * 2 + c
        self.rows_to = [(lax.rem(self.d + k, dp), x * 2 + c) for k in range(1, dp)]
        self.z_to = [at(lax.rem(hi + k, self.nz), lo, x, c) for k in range(1, self.nz)]
        self.others = plane_others()
        nw = len(ws)
        self.kept, self.z, self.p, self.f, self.k = ([None] * nw for _ in range(5))

        self.halves = halves

    def lanes(self, w, c):
        half = self.ws[w].shape[1] // 2
        return pl.ds(pl.multiple_of(c * half, 128), half)

    def shard(self, w, z, lo, x):
        if self.halves is None:
            return self.wos[w].at[z, lo, x, self.c]
        return self.wos[w].at[z, lo, x, :, self.lanes(w, self.c)]

    def swap(self, w):
        mine, mate, _, sems = self.halves
        partner = at(self.hi, self.lo, self.x, 1 - self.c)
        self.kept[w] = keep(self.ws[w].at[:, self.lanes(w, self.c)], mine[w], sems[0].at[w])
        out = self.ws[w].at[:, self.lanes(w, 1 - self.c)]
        self.z[w] = send(out, mate[w], sems[1].at[w], sems[2].at[w], partner)

    def join(self, w):
        mine, mate, base, _ = self.halves
        self.kept[w].wait()
        self.z[w].wait()
        a, b = mine[w][...].astype(F32), mate[w][...].astype(F32)
        first = self.c == 0
        rows = [jnp.where(first, a, b), jnp.where(first, b, a)]
        base[w][...] = jnp.concatenate(rows, axis=0).astype(BF)
        self.line(w)

    def meet(self):
        peers = self.rows_to + [at(self.hi, *q[:3]) for q in self.others if q[3]]
        meet(peers)

    def rows(self):
        group = self.xin.shape[0] // self.dp
        nw = len(self.ws)
        spot = self.xo.at[:, self.d]
        self.own = keep(self.xin.at[pl.ds(self.d * group, group)], spot, self.loc.at[nw])
        self.moved = [
            send(self.xin.at[pl.ds(to[0] * group, group)], spot, self.xs.at[k], self.xr.at[k], to)
            for k, to in enumerate(self.rows_to)
        ]

    def rows_ready(self):
        self.own.wait()
        for copy in self.moved:
            copy.wait()

    def line(self, w):
        spot = self.shard(w, self.hi, self.lo, self.x)
        own = self.ws[w] if self.halves is None else self.halves[2][w]
        self.kept[w] = keep(own, spot, self.loc.at[w])
        self.z[w] = [
            send(own, spot, self.zs.at[w, k], self.zr.at[w, k], to)
            for k, to in enumerate(self.z_to)
        ]

    def onward(self, part, w, k, to, sems):
        return send(part, part, sems[0].at[w, k], sems[1].at[w, k], to)

    def plane(self, w):
        self.kept[w].wait()
        for copy in self.z[w]:
            copy.wait()
        hi, lo, x, c = self.hi, self.lo, self.x, self.c
        column = self.shard(w, slice(None), lo, x)
        plane = (self.ps, self.pr)
        self.p[w] = [
            self.onward(column, w, 0, at(hi, lo, 1 - x, c), plane),
            self.onward(column, w, 1, at(hi, 1 - lo, x, c), plane),
        ]
        self.k[w] = [self.onward(column, w, 0, at(hi, lo, x, 1 - c), (self.cs, self.cr))]

    def cross(self, w):
        hi, lo, x, c = self.hi, self.lo, self.x, self.c
        plane, core, half = (self.ps, self.pr), (self.cs, self.cr), self.nz // 2
        partner = at(hi, lo, x, 1 - c)
        self.p[w][1].wait()
        part = self.shard(w, pl.ds(0, half), 1 - lo, x)
        first = self.onward(part, w, 2, at(hi, lo, 1 - x, c), plane)
        self.p[w][0].wait()
        part = self.shard(w, pl.ds(half, self.nz - half), lo, 1 - x)
        self.f[w] = [first, self.onward(part, w, 3, at(hi, 1 - lo, x, c), plane)]
        for k, part in ((1, (1 - lo, x)), (2, (lo, 1 - x))):
            self.k[w].append(
                self.onward(self.shard(w, slice(None), *part), w, k, partner, core)
            )

    def core(self, w):
        for copy in self.f[w]:
            copy.wait()
        part = self.shard(w, slice(None), 1 - self.lo, 1 - self.x)
        partner = at(self.hi, self.lo, self.x, 1 - self.c)
        self.k[w].append(self.onward(part, w, 3, partner, (self.cs, self.cr)))

    def ready(self, w):
        for copy in self.k[w]:
            copy.wait()

    def heavy_plane(self):
        nw, hi = len(self.ws), self.hi
        spot = self.hin_o.at[hi, self.home]
        self.h_own = [
            keep(self.hin.at[self.home], spot, self.loc.at[nw + 1]),
        ]
        self.h_near = [
            send(
                self.hin.at[(q[0] * 2 + q[1]) * 2 + q[2]],
                spot,
                self.hs.at[0, k],
                self.hr.at[0, k],
                at(hi, *q[:3]),
            )
            for k, q in enumerate(self.others)
        ]

    def heavy_line(self):
        for copy in self.h_own + self.h_near:
            copy.wait()
        part = self.hin_o.at[self.hi]
        self.h_far = []
        for k, to in enumerate(self.z_to):
            self.h_far.append(send(part, part, self.hs.at[1, k], self.hr.at[1, k], to))

    def heavy_ready(self):
        for copy in self.h_far:
            copy.wait()


def gather_sems(dp, nw):
    nz, most = dp // 2, max(7, dp // 2)
    return [
        DMA((nw + 2,)),
        DMA((dp,)),
        DMA((dp,)),
        DMA((nw, nz)),
        DMA((nw, nz)),
        DMA((nw, 4)),
        DMA((nw, 4)),
        DMA((nw, 4)),
        DMA((nw, 4)),
        DMA((2, most)),
        DMA((2, most)),
    ]


def gather_kernel(dp, nw, *refs):
    ins, outs, sems = refs[: 2 + nw], refs[2 + nw : 4 + 2 * nw], refs[4 + 2 * nw :]
    g = Gather(dp, ins[0], ins[1:-1], ins[-1], outs[0], outs[1:-1], outs[-1], sems)
    g.meet()
    g.rows()
    for w in range(nw):
        g.line(w)
    g.heavy_plane()
    for w in range(nw):
        g.plane(w)
        if w == 1:
            g.heavy_line()
        if w >= 1:
            g.cross(w - 1)
        if w >= 2:
            g.core(w - 2)
    g.cross(nw - 1)
    for w in range(nw - 2, nw):
        g.core(w)
    g.rows_ready()
    for w in range(nw):
        g.ready(w)
    g.heavy_ready()


def gather_shapes(dp, xin, weights, hin, paired):
    nz = dp // 2
    seqs, rows, _ = xin.shape
    shapes = [jax.ShapeDtypeStruct((seqs // dp, dp, rows, D), BF)]
    if paired:
        shapes += [jax.ShapeDtypeStruct((nz, 2, 2, 2 * w.shape[0], w.shape[1]), BF) for w in weights]
    else:
        shapes += [jax.ShapeDtypeStruct((nz, 2, 2, 2) + w.shape, BF) for w in weights]
    shapes.append(jax.ShapeDtypeStruct((nz,) + hin.shape, BF))
    return shapes


def gather_all(dp, xin, weights, hin):
    nw = len(weights)
    return call(
        functools.partial(gather_kernel, dp, nw),
        gather_shapes(dp, xin, weights, hin, False),
        [xin, *weights, hin],
        [ANY] * (2 + nw),
        [ANY] * (2 + nw),
        gather_sems(dp, nw),
        1,
    )


def rim_exchange(left, right, from_left, from_right, ls, lr, rs, rr):
    d = lax.axis_index("dp")
    f = lax.axis_index("fsdp")
    last = lax.axis_size("fsdp") - 1

    def down():
        return pltpu.make_async_remote_copy(
            src_ref=left,
            dst_ref=from_right,
            send_sem=ls,
            recv_sem=lr,
            device_id=(d, lax.max(f - 1, 0)),
            device_id_type=MESH,
        )

    def up():
        return pltpu.make_async_remote_copy(
            src_ref=right,
            dst_ref=from_left,
            send_sem=rs,
            recv_sem=rr,
            device_id=(d, lax.min(f + 1, last)),
            device_id_type=MESH,
        )

    @pl.when(f > 0)
    def _():
        down().start()

    @pl.when(f < last)
    def _():
        up().start()

    @pl.when(f == 0)
    def _():
        from_left[...] = jnp.zeros(from_left.shape, from_left.dtype)

    @pl.when(f == last)
    def _():
        from_right[...] = jnp.zeros(from_right.shape, from_right.dtype)

    def finish():
        @pl.when(f > 0)
        def _():
            down().wait_send()
            up().wait_recv()

        @pl.when(f < last)
        def _():
            up().wait_send()
            down().wait_recv()

    return finish


def line_peers():
    hi, lo, x, c = place()
    return [at(hi, lo, x, 1 - c), at(hi, lo, 1 - x, c), at(hi, lo, 1 - x, 1 - c)]


def dot(left, right):
    return jnp.dot(left, right, preferred_element_type=F32)


def dot_back(left, right):
    return lax.dot_general(left, right, (((1,), (1,)), ((), ())), preferred_element_type=F32)


def dot_grad(left, right):
    return lax.dot_general(left, right, (((0,), (0,)), ((), ())), preferred_element_type=F32)


def halves(value):
    high = value.astype(BF)
    return high, (value - high.astype(F32)).astype(BF)


def tiles(extent, step, body):
    def run(i, carry):
        body(pl.ds(pl.multiple_of(i * step, step), step))
        return carry

    lax.fori_loop(0, extent // step, run, 0)


GELU_A = 0.7978845608028654
GELU_B = 0.044715


def gelu_parts(v):
    square = v * v
    t = jnp.tanh(GELU_A * v * (1.0 + GELU_B * square))
    value = 0.5 * v * (1.0 + t)
    slope = 0.5 * (1.0 + t) + 0.5 * v * (1.0 - t * t) * GELU_A * (1.0 + 3.0 * GELU_B * square)
    return value, slope


def gelu_value(v):
    return 0.5 * v * (1.0 + jnp.tanh(GELU_A * v * (1.0 + GELU_B * v * v)))


def ffn_kernel(
    nz,
    hidden,
    select,
    select_t,
    score,
    gain,
    teach,
    mask,
    scale,
    w_in,
    w_dn,
    w_hin,
    hdn,
    g_in,
    g_dn,
    g_hin,
    hdn_o,
    d_hidden,
    stats,
    w_line,
    g_line,
    g_in_line,
    hn,
    every,
    d_every,
    up_l,
    z,
    up_h,
    zh,
    part,
    near,
    far,
    out,
    dl,
    dup_l,
    dup_h,
    dhn,
    ps,
    pr,
    cs,
    cr,
    qs,
    qr,
    es,
    er,
    zs,
    zr,
    own,
):
    hi, lo, x, c = place()
    quad = quad_peers()
    partner = at(hi, lo, x, 1 - c)
    spots = [l2 * 2 + x2 for l2, x2 in quad]
    home = lo * 2 + x
    tokens = hidden.shape[0]
    group, cap, width = select.shape
    fl = z.shape[1]
    fh = zh.shape[3]
    block = 4 * cap
    z_index = [lax.rem(hi + k, nz) for k in range(1, nz)]
    z_to = [at(k, lo, x, c) for k in z_index]
    meet([at(hi, l2, x2, c) for l2, x2 in quad] + [partner] + z_to)
    hdn_own = keep(hdn, w_line.at[hi], own)
    hdn_far = [send(hdn, w_line.at[hi], zs.at[0, k], zr.at[0, k], to) for k, to in enumerate(z_to)]
    w_hdn = w_line.reshape(-1, D)

    def span(s):
        return slice(s * width, (s + 1) * width)

    def slots(s):
        return slice(s * cap, (s + 1) * cap)

    def spread(buffer, s, i):
        spot = buffer.at[s, c, home]
        there = [
            send(spot, spot, ps.at[i, k], pr.at[i, k], at(hi, l2, x2, c))
            for k, (l2, x2) in enumerate(quad)
        ]
        return there, [send(spot, spot, cs.at[i, 3], cr.at[i, 3], partner)]

    def relay(buffer, s, i, there, back):
        for k, q in enumerate(spots):
            there[k].wait()
            other = buffer.at[s, c, q]
            back.append(send(other, other, cs.at[i, k], cr.at[i, k], partner))

    def fold(s, i, copy):
        copy.wait()
        there = []
        for k, q in enumerate(spots):
            near[i, q] = (near[i, q].astype(F32) + part[s, c, q].astype(F32)).astype(BF)
            l2, x2 = quad[k]
            there.append(
                send(near.at[i, q], far.at[i, k], qs.at[i, k], qr.at[i, k], at(hi, l2, x2, c))
            )
        return there

    def folded(s, i, there):
        for copy in there:
            copy.wait()
        return (
            near[i, home].astype(F32)
            + part[s, c, home].astype(F32)
            + far[i, 0].astype(F32)
            + far[i, 1].astype(F32)
            + far[i, 2].astype(F32)
        )

    def norm(r):
        h = hidden[r, :]
        inv = lax.rsqrt(jnp.mean(h * h, axis=-1, keepdims=True) + EPSILON)
        hn[r, :] = (h * inv * gain[1:2, :]).astype(BF)

    seqs = range(group)
    moves = {}
    tiles(tokens, 128, norm)
    for s in seqs:
        every[s, c, home] = dot(select[s], hn[span(s), :]).astype(BF)
        moves[s] = spread(every, s, s)

    def light_up(r):
        up_l[r, :] = dot(hn[r, :], w_in[...])
        z[r, :] = (gelu_value(up_l[r, :fl]) * up_l[r, fl:]).astype(BF)

    tiles(tokens, width, light_up)
    for s in seqs:
        relay(every, s, s, *moves[s])

    def light_down(r):
        out[r, :] = hidden[r, :] + dot(z[r, :], w_dn[...])

    tiles(tokens, width, light_down)

    def light_slopes(r):
        value, slope = gelu_parts(up_l[r, :fl])
        up_l[r, :fl] = up_l[r, fl:] * slope
        up_l[r, fl:] = value

    def heavy(s, e):
        up_h[s, e] = dot(every[s, e].reshape(block, D), w_hin[...])
        zh[s, e] = (gelu_value(up_h[s, e, :, :fh]) * up_h[s, e, :, fh:]).astype(BF)
        part[s, e] = dot(zh[s, e], w_hdn[...]).astype(BF).reshape(4, cap, D)

    hdn_own.wait()
    for copy in hdn_far:
        copy.wait()
    sums = {}
    for s in seqs:
        for copy in moves[s][1]:
            copy.wait()
        heavy(s, 1 - c)
        first = send(part.at[s, 1 - c], near.at[s], es.at[s], er.at[s], partner)
        heavy(s, c)
        sums[s] = fold(s, s, first)
    tiles(tokens, 64, light_slopes)
    for s in seqs:
        for e in (0, 1):

            def heavy_slopes(r, s=s, e=e):
                value, slope = gelu_parts(up_h[s, e, r, :fh])
                up_h[s, e, r, :fh] = up_h[s, e, r, fh:] * slope
                up_h[s, e, r, fh:] = value

            if s == 0:
                tiles(block, 128, heavy_slopes)
    stats[...] = jnp.zeros(stats.shape, F32)

    def light_back(r):
        dz = dot_back(dl[r, :], w_dn[...])
        dup_l[r, :fl] = (dz * up_l[r, :fl]).astype(BF)
        dup_l[r, fl:] = (dz * up_l[r, fl:]).astype(BF)

    for s in seqs:
        r = span(s)
        high, low = halves(folded(s, s, sums[s]) * score[slots(s), :])
        total = out[r, :] + (dot(select_t[s], high) + dot(select_t[s], low))
        m = total - teach[r, :].astype(F32)
        stats[1:2, :] += jnp.sum(mask[r, :] * m * m, axis=0, keepdims=True)
        d = scale[r, :] * m
        out[r, :] = d
        dl[r, :] = d.astype(BF)
        high, low = halves(d)
        picked = dot(select[s], high) + dot(select[s], low)
        d_every[s, c, home] = (picked * score[slots(s), :]).astype(BF)
        moves[s] = spread(d_every, s, group + s)
        light_back(r)
        if s > 0:
            for e in (0, 1):

                def more_slopes(r, s=s, e=e):
                    value, slope = gelu_parts(up_h[s, e, r, :fh])
                    up_h[s, e, r, :fh] = up_h[s, e, r, fh:] * slope
                    up_h[s, e, r, fh:] = value

                tiles(block, 128, more_slopes)

    def heavy_back(s, e):
        dz = dot_back(d_every[s, e].reshape(block, D), w_hdn[...])
        dup_h[s, e, :, :fh] = (dz * up_h[s, e, :, :fh]).astype(BF)
        dup_h[s, e, :, fh:] = (dz * up_h[s, e, :, fh:]).astype(BF)
        v = dot_back(dup_h[s, e], w_hin[...]).astype(BF)
        part[s, e] = v.reshape(4, cap, D)

    for s in seqs:
        relay(d_every, s, group + s, *moves[s])
        dhn[span(s), :] = dot_back(dup_l[span(s), :], w_in[...])
    for s in seqs:
        for copy in moves[s][1]:
            copy.wait()
        heavy_back(s, 1 - c)
        i = group + s
        second = send(part.at[s, 1 - c], near.at[i], es.at[i], er.at[i], partner)
        heavy_back(s, c)
        sums[s] = fold(s, i, second)
    count = group * 2 * block
    d_rows = d_every[...].reshape(count, D)
    g_line[...] = dot_grad(zh[...].reshape(count, fh), d_rows).astype(BF)
    g_view = g_line.reshape(nz, -1, D)
    hdn_back = [
        send(g_view.at[k], g_in_line.at[n], zs.at[1, n], zr.at[1, n], z_to[n])
        for n, k in enumerate(z_index)
    ]

    def light_grad(j):
        g_dn[j, :] = dot_grad(z[:, j], dl[...]).astype(BF)

    tiles(fl, 512, light_grad)

    def light_in_grad(j):
        g_in[:, j] = dot_grad(hn[...], dup_l[:, j]).astype(BF)

    tiles(2 * fl, 1024, light_in_grad)
    every_rows = every[...].reshape(count, D)

    def heavy_grad(j):
        g_hin[:, j] = dot_grad(every_rows, dup_h[:, :, :, j].reshape(count, 512)).astype(BF)

    tiles(2 * fh, 512, heavy_grad)
    for s in seqs:
        r = span(s)
        high, low = halves(folded(s, group + s, sums[s]))
        d = dhn[r, :] + (dot(select_t[s], high) + dot(select_t[s], low))
        h = hidden[r, :]
        inv = lax.rsqrt(jnp.mean(h * h, axis=-1, keepdims=True) + EPSILON)
        dh = d * h
        stats[0:1, :] += jnp.sum(dh * inv, axis=0, keepdims=True)
        mean = jnp.mean(gain[1:2, :] * dh, axis=-1, keepdims=True)
        d_hidden[r, :] = out[r, :] + inv * gain[1:2, :] * d - h * (inv * inv * inv * mean)
    for copy in hdn_back:
        copy.wait()
    value = g_view[hi].astype(F32)
    for n in range(nz - 1):
        value += g_in_line[n].astype(F32)
    hdn_o[...] = value


def feed_forward(nz, hidden, select, select_t, score, gain, teach, mask, scale, w_in, w_dn, w_hin, hdn):
    tokens = hidden.shape[0]
    group, cap, _ = select.shape
    fl, fh = w_dn.shape[0], w_hin.shape[1] // 2
    block = (group, 2, 4, cap, D)
    line = (nz,) + hdn.shape
    operands = [hidden, select, select_t, score, gain, teach, mask, scale, w_in, w_dn, w_hin, hdn]
    return call(
        functools.partial(ffn_kernel, nz),
        [
            jax.ShapeDtypeStruct((D, 2 * fl), BF),
            jax.ShapeDtypeStruct((fl, D), BF),
            jax.ShapeDtypeStruct((D, 2 * fh), BF),
            jax.ShapeDtypeStruct(hdn.shape, F32),
            jax.ShapeDtypeStruct((tokens, D), F32),
            jax.ShapeDtypeStruct((8, D), F32),
        ],
        operands,
        [VM] * (len(operands) - 1) + [ANY],
        [VM] * 6,
        [
            pltpu.VMEM(line, BF),
            pltpu.VMEM((fh, D), BF),
            pltpu.VMEM((nz - 1,) + hdn.shape, BF),
            pltpu.VMEM((tokens, D), BF),
            pltpu.VMEM(block, BF),
            pltpu.VMEM(block, BF),
            pltpu.VMEM((tokens, 2 * fl), F32),
            pltpu.VMEM((tokens, fl), BF),
            pltpu.VMEM((group, 2, 4 * cap, 2 * fh), F32),
            pltpu.VMEM((group, 2, 4 * cap, fh), BF),
            pltpu.VMEM(block, BF),
            pltpu.VMEM((2 * group, 4, cap, D), BF),
            pltpu.VMEM((2 * group, 3, cap, D), BF),
            pltpu.VMEM((tokens, D), F32),
            pltpu.VMEM((tokens, D), BF),
            pltpu.VMEM((tokens, 2 * fl), BF),
            pltpu.VMEM((group, 2, 4 * cap, 2 * fh), BF),
            pltpu.VMEM((tokens, D), F32),
            DMA((2 * group, 3)),
            DMA((2 * group, 3)),
            DMA((2 * group, 4)),
            DMA((2 * group, 4)),
            DMA((2 * group, 3)),
            DMA((2 * group, 3)),
            DMA((2 * group,)),
            DMA((2 * group,)),
            DMA((2, nz)),
            DMA((2, nz)),
            DMA,
        ],
        5,
    )


def pair_masks(scale):
    lane = lax.broadcasted_iota(jnp.int32, (1, 2 * DH), 1)
    left = jnp.where(lane < DH, scale, 0.0).astype(BF)
    right = jnp.where(lane < DH, 0.0, scale).astype(BF)
    return left, right


def both(value, masks):
    return jnp.concatenate([value * masks[0], value * masks[1]], axis=0)


def side(stacked):
    rows = stacked.shape[0] // 2
    return jnp.concatenate([stacked[:rows], stacked[rows:]], axis=1)


def pair_forward(q, k, v, bias, ones, scaled):
    scores = dot_back(both(q, scaled), k) + bias
    top = jnp.max(scores, axis=-1, keepdims=True)
    shifted = jnp.exp(scores - top)
    total = jnp.sum(shifted, axis=-1, keepdims=True)
    prob = (shifted / total).astype(BF)
    return dot(side(prob), both(v, ones)).astype(BF), top + jnp.log(total)


def pair_backward(q, k, v, bias, lse, d_out, ones, scaled):
    q2 = both(q, scaled)
    d2 = both(d_out, ones)
    prob = jnp.exp(dot_back(q2, k) + bias - lse)
    d_prob = dot_back(d2, v)
    row = jnp.sum(prob * d_prob, axis=-1, keepdims=True)
    d_scores = (prob * (d_prob - row)).astype(BF)
    dq = dot(side(d_scores), both(k, scaled))
    return dq, dot_grad(d_scores, q2), dot_grad(prob.astype(BF), d2)


def reach_bias(key_bias):
    shape = (WIN, 3 * WIN)
    offset = lax.broadcasted_iota(jnp.int32, shape, 1) - lax.broadcasted_iota(jnp.int32, shape, 0) - WIN
    near = (offset >= -WIN) & (offset <= WIN)
    inner = jnp.where(offset == 0, 0.0, jnp.broadcast_to(key_bias, shape))
    bias = jnp.where(near, inner, MASKED)
    return jnp.concatenate([bias, bias], axis=0)


def put_lse(lse, pair, column):
    lane = lax.broadcasted_iota(jnp.int32, lse.shape, 1)
    rows = lse.shape[0]
    lse = jnp.where(lane == 2 * pair, column[:rows], lse)
    return jnp.where(lane == 2 * pair + 1, column[rows:], lse)


def get_lse(lse, pair):
    return jnp.concatenate([lse[:, 2 * pair : 2 * pair + 1], lse[:, 2 * pair + 1 : 2 * pair + 2]], axis=0)


def attend_body(
    stages,
    x,
    gain,
    select,
    select_t,
    key_bias,
    heavy_bias,
    w_lqkv,
    w_hqkv,
    w_lout,
    w_hout,
    hidden,
    xn,
    lq,
    rim,
    lo_out,
    l_lse,
    a_rows,
    hq,
    kvh,
    ho,
    h_lse,
    ls,
    lr,
    rs,
    rr,
    ss,
    sr,
):
    hi, lo, x_, c = place()
    f = x_ * 2 + c
    tokens = x.shape[0]
    group, cap, width = select.shape
    wl, wh = HL * DH, HH * DH
    ones, scaled = pair_masks(1.0), pair_masks(SCORE_SCALE)
    across, partner = at(hi, lo, 1 - x_, c), at(hi, lo, x_, 1 - c)

    def norm(r):
        h = x[r, :].astype(F32)
        inv = lax.rsqrt(jnp.mean(h * h, axis=-1, keepdims=True) + EPSILON)
        xn[r, :] = (h * inv * gain[0:1, :]).astype(BF)

    tiles(tokens, 128, norm)
    for s in range(group):
        rows = dot(select[s], xn[s * width : (s + 1) * width, :]).astype(BF)
        a_rows[s * cap : (s + 1) * cap, :] = rows
    stages[0]()
    kv = dot(a_rows[...], w_hqkv[:, wh:]).astype(BF)
    for s in range(group):
        kvh[s, f] = kv[s * cap : (s + 1) * cap]
    mine = kvh.at[:, f]
    first = send(mine, mine, ss.at[0], sr.at[0], across)
    beside = send(mine, mine, ss.at[1], sr.at[1], partner)
    stages[1]()
    for s in range(group):
        rows = xn[s * width : (s + 1) * width, :]
        rim[s, WIN : WIN + width, :] = dot(rows, w_lqkv[:, wl:]).astype(BF)
    finish = rim_exchange(
        rim.at[:, pl.ds(WIN, WIN)],
        rim.at[:, pl.ds(width, WIN)],
        rim.at[:, pl.ds(0, WIN)],
        rim.at[:, pl.ds(width + WIN, WIN)],
        ls,
        lr,
        rs,
        rr,
    )
    hq[...] = dot(a_rows[...], w_hqkv[:, :wh]).astype(BF)
    for s in range(group):
        rows = slice(s * width, (s + 1) * width)
        lq[rows, :] = dot(xn[rows, :], w_lqkv[:, :wl]).astype(BF)
    stages[2]()
    first.wait()
    other = kvh.at[:, (1 - x_) * 2 + c]
    relay = send(other, other, ss.at[2], sr.at[2], partner)
    finish()
    blocks = width // WIN

    def light(i, carry):
        s, b = i // blocks, i % blocks
        r = pl.ds(pl.multiple_of(i * WIN, WIN), WIN)
        keys = pl.ds(pl.multiple_of(b * WIN, WIN), 3 * WIN)
        bias = reach_bias(key_bias[i])
        lse = jnp.zeros((WIN, 128), F32)
        for pair in range(HL // 2):
            at_k = slice(pair * 128, (pair + 1) * 128)
            at_v = slice(wl + pair * 128, wl + (pair + 1) * 128)
            o, column = pair_forward(
                lq[r, at_k], rim[s, keys, at_k], rim[s, keys, at_v], bias, ones, scaled
            )
            lo_out[r, at_k] = o
            lse = put_lse(lse, pair, column)
        l_lse[r, :] = lse
        return carry

    lax.fori_loop(0, group * blocks // 2, light, 0)
    stages[3]()
    lax.fori_loop(group * blocks // 2, group * blocks, light, 0)
    stages[4]()
    beside.wait()
    relay.wait()
    heavy_kv = kvh.reshape(group, 4 * cap, 2 * wh)

    def heavy(s, carry):
        r = pl.ds(pl.multiple_of(s * cap, cap), cap)
        bias = heavy_bias[s]
        bias = jnp.concatenate([bias, bias], axis=0)
        lse = jnp.zeros((cap, 128), F32)
        for pair in range(HH // 2):
            at_k = slice(pair * 128, (pair + 1) * 128)
            at_v = slice(wh + pair * 128, wh + (pair + 1) * 128)
            o, column = pair_forward(
                hq[r, at_k], heavy_kv[s, :, at_k], heavy_kv[s, :, at_v], bias, ones, scaled
            )
            ho[r, at_k] = o
            lse = put_lse(lse, pair, column)
        h_lse[r, :] = lse
        return carry

    lax.fori_loop(0, group, heavy, 0)
    stages[5]()
    high, low = halves(dot(ho[...], w_hout[...]))
    for s in range(group):
        r = slice(s * width, (s + 1) * width)
        q = slice(s * cap, (s + 1) * cap)
        hidden[r, :] = (
            x[r, :].astype(F32)
            + dot(lo_out[r, :], w_lout[...])
            + (dot(select_t[s], high[q]) + dot(select_t[s], low[q]))
        )


def attend_kernel(*refs):
    meet(line_peers())
    attend_body([lambda: None] * 6, *refs)


def attend_shapes(tokens, select):
    group, cap, width = select.shape
    wl, wh = HL * DH, HH * DH
    rows = group * cap
    return [
        jax.ShapeDtypeStruct((tokens, D), F32),
        jax.ShapeDtypeStruct((tokens, D), BF),
        jax.ShapeDtypeStruct((tokens, wl), BF),
        jax.ShapeDtypeStruct((group, width + 2 * WIN, 2 * wl), BF),
        jax.ShapeDtypeStruct((tokens, wl), BF),
        jax.ShapeDtypeStruct((tokens, 128), F32),
        jax.ShapeDtypeStruct((rows, D), BF),
        jax.ShapeDtypeStruct((rows, wh), BF),
        jax.ShapeDtypeStruct((group, 4, cap, 2 * wh), BF),
        jax.ShapeDtypeStruct((rows, wh), BF),
        jax.ShapeDtypeStruct((rows, 128), F32),
    ]


ATTEND_SEMS = [DMA, DMA, DMA, DMA, DMA((3,)), DMA((3,))]


def attend(x, gain, select, select_t, key_bias, heavy_bias, w_lqkv, w_hqkv, w_lout, w_hout):
    operands = [x, gain, select, select_t, key_bias, heavy_bias, w_lqkv, w_hqkv, w_lout, w_hout]
    shapes = attend_shapes(x.shape[0], select)
    return call(
        attend_kernel,
        shapes,
        operands,
        [VM] * len(operands),
        [VM] * len(shapes),
        ATTEND_SEMS,
        2,
    )


def route_part(deal, lengths, routes_a, routes_f, scores, tables):
    sel_a, selt_a, key_bias, heavy_bias, sel_f, selt_f, score, mask, scale = tables
    hi, lo, x, c = place()
    group, cap, width = sel_a.shape
    seqs = deal.shape[1]
    here = ((x * 2 + c) * width).astype(F32)

    def line(shape, dim):
        return lax.broadcasted_iota(jnp.int32, shape, dim).astype(F32)

    lane = lax.broadcasted_iota(jnp.int32, (1, seqs), 1)
    before = jnp.where(line((width, width), 0) > line((width, width), 1), 1.0, 0.0).astype(BF)
    length_row = lengths[...].astype(F32)
    count = jnp.sum(length_row, axis=1, keepdims=True)
    column = line((width, 1), 0)
    row = line((1, width), 1)
    ones = jnp.ones((8, routes_a.shape[1]), BF)

    def columns_of(routes, base):
        held = jnp.where(routes == column + base, 1.0, 0.0)
        rank = jnp.sum(dot(before, held.astype(BF)), axis=1, keepdims=True)
        there = jnp.sum(held, axis=1, keepdims=True)
        hot_t = jnp.where(rank == line((width, cap), 1), 1.0, 0.0) * there
        return held, rank, hot_t

    def rows_of(held):
        there = dot_back(ones, held.astype(BF))
        rank = dot_back(there.astype(BF), before)
        return jnp.where(rank[:1] == line((cap, width), 0), 1.0, 0.0) * there[:1]

    for s in range(group):
        place_here = lane == (hi * 2 + lo) * group + s
        which = jnp.sum(jnp.where(place_here, deal[...].astype(F32), 0.0), axis=1, keepdims=True)
        one = line((seqs, 1), 0) == which
        length = jnp.sum(
            jnp.where(line((1, seqs), 1) == which, length_row, 0.0), axis=1, keepdims=True
        )
        ra, rf, sf = (
            jnp.sum(jnp.where(one, ref[...].astype(F32), 0.0), axis=0, keepdims=True)
            for ref in (routes_a, routes_f, scores)
        )
        held, rank, hot_t = columns_of(ra, here)
        hot = rows_of(held)
        sel_a[s] = hot.astype(BF)
        selt_a[s] = hot_t.astype(BF)
        own_spot = jnp.sum(hot * (row + here + 1.0), axis=1, keepdims=True) - 1.0
        for q in range(4):
            base = float(q * width)
            _, _, other_t = columns_of(ra, base)
            spot = jnp.sum(other_t * (column + base + 1.0), axis=0, keepdims=True) - 1.0
            live = jnp.where((spot >= 0.0) & (spot < length), 1.0, 0.0)
            same = jnp.where(own_spot == spot, 1.0, 0.0)
            heavy_bias[s, :, q * cap : (q + 1) * cap] = jnp.where(live + same > 0.0, 0.0, MASKED)
        for b in range(width // WIN):
            key = line((1, 3 * WIN), 1) + (here + float((b - 1) * WIN))
            live = (key >= 0.0) & (key < length)
            key_bias[s * (width // WIN) + b] = jnp.where(live, 0.0, MASKED)
        valid = jnp.where(column + here < length, 1.0, 0.0)
        mask[s * width : (s + 1) * width, :] = valid
        scale[s * width : (s + 1) * width, :] = 2.0 * valid / (D * count)
        held, rank, hot_t = columns_of(rf, here)
        sel_f[s] = rows_of(held).astype(BF)
        selt_f[s] = hot_t.astype(BF)
        slot = jnp.sum(held * rank, axis=0, keepdims=True)
        owned = jnp.sum(held, axis=0, keepdims=True)
        hits = jnp.where(slot == line((cap, slot.shape[1]), 0), 1.0, 0.0)
        score[s * cap : (s + 1) * cap, :] = jnp.sum(hits * (owned * sf), axis=1, keepdims=True)


def route_shapes(group, width, tokens):
    return [
        jax.ShapeDtypeStruct((group, CAP, width), BF),
        jax.ShapeDtypeStruct((group, width, CAP), BF),
        jax.ShapeDtypeStruct((tokens // WIN, 1, 3 * WIN), F32),
        jax.ShapeDtypeStruct((group, CAP, 4 * CAP), F32),
        jax.ShapeDtypeStruct((group, CAP, width), BF),
        jax.ShapeDtypeStruct((group, width, CAP), BF),
        jax.ShapeDtypeStruct((group * CAP, 1), F32),
        jax.ShapeDtypeStruct((tokens, 1), F32),
        jax.ShapeDtypeStruct((tokens, 1), F32),
    ]


def gather_attend_kernel(dp, nw, *refs):
    n_in, n_out = 7 + nw, 2 + nw + 21
    ins, outs, rest = refs[:n_in], refs[n_in : n_in + n_out], refs[n_in + n_out :]
    xin, ws, hin = ins[0], ins[1 : 1 + nw], ins[1 + nw]
    integers = ins[2 + nw :]
    xo, wos, hin_o = outs[0], outs[1 : 1 + nw], outs[1 + nw]
    gain, tables, saved = outs[2 + nw], outs[3 + nw : 12 + nw], outs[12 + nw :]
    parts, rest = rest[: 3 * nw + 3], rest[3 * nw + 3 :]
    halves = (parts[:nw], parts[nw : 2 * nw], parts[2 * nw : 3 * nw], parts[3 * nw :])
    g = Gather(dp, xin, ws, hin, xo, wos, hin_o, rest[:11], halves)
    g.meet()
    for w in range(nw):
        g.swap(w)
    for w in (0, 1, 2):
        g.join(w)
    for w in (0, 1, 2):
        g.plane(w)
    g.rows()
    for w in (3, 4, 5, 6):
        g.join(w)
    g.heavy_plane()
    route_part(*integers, tables)
    g.cross(0)
    g.core(0)
    g.cross(1)
    g.cross(2)
    g.heavy_line()
    g.plane(3)
    g.plane(4)
    g.ready(0)
    total = jnp.zeros(gain.shape, F32)
    for z in range(dp // 2):
        for l2, x2 in ((0, 0), (0, 1), (1, 0), (1, 1)):
            pair = wos[0][z, l2, x2].astype(F32)
            total += pair[:8] + pair[8:]
    gain[...] = total
    g.rows_ready()

    def heavy_projection():
        g.core(1)
        g.core(2)
        g.ready(2)

    def light_projection():
        g.plane(5)
        g.plane(6)
        g.ready(1)

    def keys_travel():
        g.cross(3)
        g.cross(4)

    def half_way():
        g.core(3)
        g.core(4)

    def light_done():
        g.cross(5)
        g.cross(6)

    def heavy_done():
        g.core(5)
        g.core(6)
        g.ready(3)
        g.ready(4)

    full = [wos[w].reshape(-1, wos[w].shape[-1]) for w in range(nw)]
    stages = [heavy_projection, light_projection, keys_travel, half_way, light_done, heavy_done]
    attend_body(
        stages,
        xo.reshape(-1, D),
        gain,
        *tables[:4],
        full[1],
        full[2],
        full[3],
        full[4],
        *saved,
        *rest[11:],
    )
    g.ready(5)
    g.ready(6)
    g.heavy_ready()


def gather_attend(dp, xin, weights, hin, integers):
    nw = len(weights)
    shapes = gather_shapes(dp, xin, weights, hin, True)
    group, width = shapes[0].shape[0], dp * xin.shape[1]
    tables = route_shapes(group, width, group * width)
    shapes.append(jax.ShapeDtypeStruct((8, D), F32))
    shapes += tables
    shapes += attend_shapes(group * width, tables[0])
    return call(
        functools.partial(gather_attend_kernel, dp, nw),
        shapes,
        [xin, *weights, hin, *integers],
        [ANY] * (2 + nw) + [VM] * 5,
        [VM] * 6 + [ANY] * 3 + [VM] * 21,
        [pltpu.VMEM((w.shape[0], w.shape[1] // 2), BF) for w in weights] * 2
        + [pltpu.VMEM((2 * w.shape[0], w.shape[1] // 2), BF) for w in weights]
        + [DMA((nw,))] * 3
        + gather_sems(dp, nw)
        + ATTEND_SEMS,
        1,
    )


def attend_back_body(
    stages,
    d_hidden,
    x,
    gain,
    select,
    select_t,
    key_bias,
    heavy_bias,
    w_lqkv,
    w_hqkv,
    w_lout,
    w_hout,
    xn,
    lq,
    rim,
    lo_out,
    l_lse,
    a_rows,
    hq,
    kvh,
    ho,
    h_lse,
    g_lqkv,
    g_hqkv,
    g_lout,
    g_hout,
    dx,
    stats,
    d_ho,
    d_hproj,
    part,
    got,
    far,
    d_la,
    d_lo,
    d_rim,
    edge,
    edge_in,
    d_lproj,
    ls,
    lr,
    rs,
    rr,
    ss,
    sr,
):
    hi, lo, x_, c = place()
    tokens = x.shape[0]
    group, cap, width = select.shape
    wl, wh = HL * DH, HH * DH
    ones, scaled = pair_masks(1.0), pair_masks(SCORE_SCALE)
    across, partner = at(hi, lo, 1 - x_, c), at(hi, lo, x_, 1 - c)
    picked = []
    for s in range(group):
        high, low = halves(d_hidden[s * width : (s + 1) * width, :])
        picked.append((dot(select[s], high) + dot(select[s], low)).astype(BF))
    d_ha = jnp.concatenate(picked, axis=0)
    d_ho[...] = dot_back(d_ha, w_hout[...]).astype(BF)
    heavy_kv = kvh.reshape(group, 4 * cap, 2 * wh)
    part_kv = part.reshape(group, 4 * cap, 2 * wh)

    def heavy(s, carry):
        r = pl.ds(pl.multiple_of(s * cap, cap), cap)
        bias = heavy_bias[s]
        bias = jnp.concatenate([bias, bias], axis=0)
        lse = h_lse[r, :]
        for pair in range(HH // 2):
            at_k = slice(pair * 128, (pair + 1) * 128)
            at_v = slice(wh + pair * 128, wh + (pair + 1) * 128)
            dq, dk, dv = pair_backward(
                hq[r, at_k],
                heavy_kv[s, :, at_k],
                heavy_kv[s, :, at_v],
                bias,
                get_lse(lse, pair),
                d_ho[r, at_k],
                ones,
                scaled,
            )
            d_hproj[r, at_k] = dq.astype(BF)
            part_kv[s, :, at_k] = dk.astype(BF)
            part_kv[s, :, at_v] = dv.astype(BF)
        return carry

    lax.fori_loop(0, group, heavy, 0)
    beside = [
        send(part.at[:, b * 2 + 1 - c], got.at[b], ss.at[b], sr.at[b], partner) for b in (0, 1)
    ]
    g_hout[...] = dot_grad(ho[...], d_ha).astype(BF)
    stages[0]()

    def light_out_back(r):
        d = d_hidden[r, :].astype(BF)
        d_la[r, :] = d
        d_lo[r, :] = dot_back(d, w_lout[...]).astype(BF)

    tiles(tokens, 256, light_out_back)
    g_lout[...] = dot_grad(lo_out[...], d_la[...]).astype(BF)
    stages[1]()
    for copy in beside:
        copy.wait()
    for b in (0, 1):
        got[b] = (got[b].astype(F32) + part[:, b * 2 + c].astype(F32)).astype(BF)
    third = send(got.at[1 - x_], far, ss.at[2], sr.at[2], across)
    stages[2]()
    d_rim[...] = jnp.zeros(d_rim.shape, F32)
    blocks = width // WIN

    def light(i, carry):
        s, b = i // blocks, i % blocks
        r = pl.ds(pl.multiple_of(i * WIN, WIN), WIN)
        keys = pl.ds(pl.multiple_of(b * WIN, WIN), 3 * WIN)
        bias = reach_bias(key_bias[i])
        lse = l_lse[r, :]
        for pair in range(HL // 2):
            at_k = slice(pair * 128, (pair + 1) * 128)
            at_v = slice(wl + pair * 128, wl + (pair + 1) * 128)
            dq, dk, dv = pair_backward(
                lq[r, at_k],
                rim[s, keys, at_k],
                rim[s, keys, at_v],
                bias,
                get_lse(lse, pair),
                d_lo[r, at_k],
                ones,
                scaled,
            )
            d_lproj[r, at_k] = dq.astype(BF)
            d_rim[s, keys, at_k] += dk
            d_rim[s, keys, at_v] += dv
        return carry

    lax.fori_loop(0, group * blocks // 2, light, 0)
    third.wait()
    total = (got[x_].astype(F32) + far[...].astype(F32)).astype(BF)
    for s in range(group):
        d_hproj[s * cap : (s + 1) * cap, wh:] = total[s]

    def heavy_grad(j):
        g_hqkv[:, j] = dot_grad(a_rows[...], d_hproj[:, j]).astype(BF)

    tiles(3 * wh, 768, heavy_grad)
    stages[3]()
    lax.fori_loop(group * blocks // 2, group * blocks, light, 0)
    edge[0] = d_rim[:, :WIN, :].astype(BF)
    edge[1] = d_rim[:, WIN + width :, :].astype(BF)
    finish = rim_exchange(
        edge.at[0], edge.at[1], edge_in.at[0], edge_in.at[1], ls, lr, rs, rr
    )
    stages[4]()
    d_high, d_low = halves(dot_back(d_hproj[...], w_hqkv[...]))
    finish()
    for s in range(group):
        d_rim[s, WIN : 2 * WIN, :] += edge_in[0, s].astype(F32)
        d_rim[s, width : width + WIN, :] += edge_in[1, s].astype(F32)
        d_lproj[s * width : (s + 1) * width, wl:] = d_rim[s, WIN : WIN + width, :].astype(BF)

    def light_grad(j):
        g_lqkv[:, j] = dot_grad(xn[...], d_lproj[:, j]).astype(BF)

    tiles(3 * wl, 768, light_grad)
    stages[5]()
    stats[...] = jnp.zeros(stats.shape, F32)
    for s in range(group):
        r = slice(s * width, (s + 1) * width)
        q = slice(s * cap, (s + 1) * cap)
        d = dot_back(d_lproj[r, :], w_lqkv[...]) + (
            dot(select_t[s], d_high[q]) + dot(select_t[s], d_low[q])
        )
        h = x[r, :].astype(F32)
        inv = lax.rsqrt(jnp.mean(h * h, axis=-1, keepdims=True) + EPSILON)
        dh = d * h
        stats[0:1, :] += jnp.sum(dh * inv, axis=0, keepdims=True)
        mean = jnp.mean(gain[0:1, :] * dh, axis=-1, keepdims=True)
        dx[r, :] = (
            d_hidden[r, :] + inv * gain[0:1, :] * d - h * (inv * inv * inv * mean)
        ).astype(BF)
    stages[6]()


def attend_back_kernel(*refs):
    meet(line_peers())
    attend_back_body([lambda: None] * 7, *refs)


def attend_back_scratch(tokens, select):
    group, cap, width = select.shape
    wl, wh = HL * DH, HH * DH
    rows = group * cap
    return [
        pltpu.VMEM((rows, wh), BF),
        pltpu.VMEM((rows, 3 * wh), BF),
        pltpu.VMEM((group, 4, cap, 2 * wh), BF),
        pltpu.VMEM((2, group, cap, 2 * wh), BF),
        pltpu.VMEM((group, cap, 2 * wh), BF),
        pltpu.VMEM((tokens, D), BF),
        pltpu.VMEM((tokens, wl), BF),
        pltpu.VMEM((group, width + 2 * WIN, 2 * wl), F32),
        pltpu.VMEM((2, group, WIN, 2 * wl), BF),
        pltpu.VMEM((2, group, WIN, 2 * wl), BF),
        pltpu.VMEM((tokens, 3 * wl), BF),
    ] + ATTEND_SEMS


def attend_back(d_hidden, x, gain, select, select_t, key_bias, heavy_bias, weights, saved):
    tokens = x.shape[0]
    wl, wh = HL * DH, HH * DH
    operands = [d_hidden, x, gain, select, select_t, key_bias, heavy_bias, *weights, *saved]
    shapes = [
        jax.ShapeDtypeStruct((D, 3 * wl), BF),
        jax.ShapeDtypeStruct((D, 3 * wh), BF),
        jax.ShapeDtypeStruct((wl, D), BF),
        jax.ShapeDtypeStruct((wh, D), BF),
        jax.ShapeDtypeStruct((tokens, D), BF),
        jax.ShapeDtypeStruct((8, D), F32),
    ]
    return call(
        attend_back_kernel,
        shapes,
        operands,
        [VM] * len(operands),
        [VM] * len(shapes),
        attend_back_scratch(tokens, select),
        3,
    )


def scatter_kernel(dp, nw, *refs):
    nz = dp // 2
    dx, stats, gs, hin = refs[0], refs[1], refs[2 : 2 + nw], refs[2 + nw]
    outs = refs[3 + nw :]
    dxo, total, gos, hin_o = outs[0], outs[1], outs[2 : 2 + nw], outs[2 + nw]
    scr = outs[3 + nw :]
    nears, fars, sums, ends = (scr[i * nw : (i + 1) * nw] for i in range(4))
    hin_r, hin_s, sc, sp, sz, acc, acc2 = scr[4 * nw : 4 * nw + 7]
    own, xs, xr, cs, cr, ps, pr, zs, zr, hs, hr, ts, tr = scr[4 * nw + 7 :]
    hi, lo, x, c = place()
    d = hi * 2 + lo
    f = x * 2 + c
    plane = (lo * 2 + x) * 2 + c
    dp_peers = [(lax.rem(d + k, dp), f) for k in range(1, dp)]
    rest = [(a, b, e) for a in (0, 1) for b in (0, 1) for e in (0, 1) if a or b or e]
    flat8 = []
    for a, b, e in rest:
        l2 = 1 - lo if a else lo
        x2 = 1 - x if b else x
        c2 = 1 - c if e else c
        flat8.append((l2, x2, c2))
    meet(dp_peers + [at(hi, *p) for (a, b, e), p in zip(rest, flat8) if b or e])
    partner = at(hi, lo, x, 1 - c)
    quad = quad_peers()
    z_index = [lax.rem(hi + k, nz) for k in range(1, nz)]
    z_peers = [at(z, lo, x, c) for z in z_index]
    c_sends = [
        send(gs[w].at[:, :, :, 1 - c], nears[w], cs.at[w], cr.at[w], partner) for w in range(nw)
    ]
    t_c = send(stats, sc, ts.at[0], tr.at[0], partner)
    mine = keep(dx.at[:, d], dxo.at[d], own)
    x_sends = [
        send(dx.at[:, peer[0]], dxo.at[d], xs.at[k], xr.at[k], peer)
        for k, peer in enumerate(dp_peers)
    ]
    h_sends = []
    for k, z in enumerate(z_index):
        h_sends.append(send(hin.at[z], hin_r.at[k], hs.at[1, k], hr.at[1, k], z_peers[k]))
    p_sends, z_sends = [], []
    t_c.wait()
    acc[...] = stats[...] + sc[...]
    t_p = [
        send(acc, sp.at[k], ts.at[1 + k], tr.at[1 + k], at(hi, l2, x2, c))
        for k, (l2, x2) in enumerate(quad)
    ]

    def add_core(w):
        c_sends[w].wait()
        near, g = nears[w], gs[w]

        def body(i, carry):
            z, a, b = i // 4, (i // 2) % 2, i % 2
            near[z, a, b] = (near[z, a, b].astype(F32) + g[z, a, b, c].astype(F32)).astype(BF)
            return carry

        lax.fori_loop(0, nz * 4, body, 0)
        p_sends.append(
            [
                send(near.at[:, l2, x2], fars[w].at[k], ps.at[w, k], pr.at[w, k], at(hi, l2, x2, c))
                for k, (l2, x2) in enumerate(quad)
            ]
        )

    def add_plane(w):
        for copy in p_sends[w]:
            copy.wait()
        near, far, part = nears[w], fars[w], sums[w]

        def body(z, carry):
            part[z] = (
                near[z, lo, x].astype(F32)
                + far[0, z].astype(F32)
                + far[1, z].astype(F32)
                + far[2, z].astype(F32)
            ).astype(BF)
            return carry

        lax.fori_loop(0, nz, body, 0)
        z_sends.append(
            [
                send(part.at[z], ends[w].at[k], zs.at[w, k], zr.at[w, k], z_peers[k])
                for k, z in enumerate(z_index)
            ]
        )

    def add_line(w):
        for copy in z_sends[w]:
            copy.wait()
        gos[w][...] = sums[w][hi].astype(F32)
        for k in range(nz - 1):
            gos[w][...] += ends[w][k].astype(F32)

    for w in range(nw):
        add_core(w)
        if w >= 2:
            add_plane(w - 2)
    for copy in t_p:
        copy.wait()
    acc2[...] = acc[...] + sp[0] + sp[1] + sp[2]
    t_z = [send(acc2, sz.at[k], ts.at[4 + k], tr.at[4 + k], z_peers[k]) for k in range(nz - 1)]
    for copy in h_sends:
        copy.wait()

    def body(i, carry):
        value = hin[hi, i].astype(F32)
        for k in range(nz - 1):
            value += hin_r[k, i].astype(F32)
        hin_s[i] = value.astype(BF)
        return carry

    lax.fori_loop(0, 8, body, 0)
    hin_o[plane] = hin_s[plane]
    a_sends = [
        send(
            hin_s.at[(l2 * 2 + x2) * 2 + c2],
            hin_o.at[plane],
            hs.at[0, k],
            hr.at[0, k],
            at(hi, l2, x2, c2),
        )
        for k, (l2, x2, c2) in enumerate(flat8)
    ]
    for w in range(max(nw - 2, 0), nw):
        add_plane(w)
    for copy in t_z:
        copy.wait()
    total[...] = acc2[...]
    for k in range(nz - 1):
        total[...] += sz[k]
    for w in range(nw):
        add_line(w)
    mine.wait()
    for copy in x_sends + a_sends:
        copy.wait()


def scatter_all(dp, dx, stats, grads, hin):
    nz = dp // 2
    nw = len(grads)
    group, _, rows, _ = dx.shape
    tiles = [g.shape[4:] for g in grads]
    most = max(7, nz)
    scratch = [pltpu.VMEM((nz, 2, 2) + t, BF) for t in tiles]
    scratch += [pltpu.VMEM((3, nz) + t, BF) for t in tiles]
    scratch += [pltpu.VMEM((nz,) + t, BF) for t in tiles]
    scratch += [pltpu.VMEM((nz - 1,) + t, BF) for t in tiles]
    scratch += [
        pltpu.VMEM((nz - 1,) + hin.shape[1:], BF),
        pltpu.VMEM(hin.shape[1:], BF),
        pltpu.VMEM(stats.shape, F32),
        pltpu.VMEM((3,) + stats.shape, F32),
        pltpu.VMEM((nz - 1,) + stats.shape, F32),
        pltpu.VMEM(stats.shape, F32),
        pltpu.VMEM(stats.shape, F32),
        DMA,
        DMA((dp,)),
        DMA((dp,)),
        DMA((nw,)),
        DMA((nw,)),
        DMA((nw, 3)),
        DMA((nw, 3)),
        DMA((nw, nz)),
        DMA((nw, nz)),
        DMA((3, most)),
        DMA((3, most)),
        DMA((4 + nz,)),
        DMA((4 + nz,)),
    ]
    shapes = [jax.ShapeDtypeStruct((dp, group, rows, D), BF), jax.ShapeDtypeStruct(stats.shape, F32)]
    shapes += [jax.ShapeDtypeStruct(t, F32) for t in tiles]
    shapes.append(jax.ShapeDtypeStruct(hin.shape[1:], BF))
    return call(
        functools.partial(scatter_kernel, dp, nw),
        shapes,
        [dx, stats, *grads, hin],
        [ANY] + [VM] * (2 + nw),
        [ANY] + [VM] * (2 + nw),
        scratch,
        4,
    )


class Scatter:
    def __init__(self, nz, shards, gs, near, one, two, end, sems):
        self.nz, self.shards, self.gs = nz, shards, gs
        self.near, self.one, self.two, self.end = near, one, two, end
        self.cs, self.cr, self.ps, self.pr, self.zs, self.zr = sems
        self.hi, self.lo, self.x, self.c = hi, lo, x, c = place()
        self.partner = at(hi, lo, x, 1 - c)
        self.by_x, self.by_y = at(hi, lo, 1 - x, c), at(hi, 1 - lo, x, c)
        self.z_index = [lax.rem(hi + k, nz) for k in range(1, nz)]
        self.copies = {}

    def lanes(self, w, c):
        half = self.shards[w][1] // 2
        return pl.ds(pl.multiple_of(c * half, 128), half)

    def core(self, w):
        out = self.gs[w].at[:, :, :, :, self.lanes(w, 1 - self.c)]
        self.copies[w, 0] = [send(out, self.near[w], self.cs.at[w], self.cr.at[w], self.partner)]

    def wait(self, w, stage):
        for copy in self.copies[w, stage]:
            copy.wait()

    def plane(self, w):
        g, own = self.gs[w], self.lanes(w, self.c)
        self.add_plane(w, lambda z, a, b: g[z, a, b, :, own])

    def own_plane(self, w, kept):
        self.add_plane(w, lambda z, a, b: kept[z, a, b])

    def add_plane(self, w, own):
        self.wait(w, 0)
        near = self.near[w]
        lo, x, half = self.lo, self.x, self.nz // 2

        def body(i, carry):
            z, a, b = i // 4, (i // 2) % 2, i % 2
            near[z, a, b] = (near[z, a, b].astype(F32) + own(z, a, b).astype(F32)).astype(BF)
            return carry

        lax.fori_loop(0, self.nz * 4, body, 0)
        low, high = pl.ds(0, half), pl.ds(half, self.nz - half)
        self.copies[w, 1] = [
            send(near.at[low, :, 1 - x], self.one[w].at[low], self.ps.at[w, 0], self.pr.at[w, 0], self.by_x),
            send(near.at[high, 1 - lo], self.one[w].at[high], self.ps.at[w, 1], self.pr.at[w, 1], self.by_y),
        ]

    def cross(self, w):
        self.wait(w, 1)
        near, one, lo, x, half = self.near[w], self.one[w], self.lo, self.x, self.nz // 2

        def low_body(i, carry):
            z, a = i // 2, i % 2
            near[z, a, x] = (near[z, a, x].astype(F32) + one[z, a].astype(F32)).astype(BF)
            return carry

        def high_body(i, carry):
            z, b = half + i // 2, i % 2
            near[z, lo, b] = (near[z, lo, b].astype(F32) + one[z, b].astype(F32)).astype(BF)
            return carry

        lax.fori_loop(0, half * 2, low_body, 0)
        lax.fori_loop(0, (self.nz - half) * 2, high_body, 0)
        low, high = pl.ds(0, half), pl.ds(half, self.nz - half)
        two = self.two[w]
        self.copies[w, 2] = [
            send(near.at[low, 1 - lo, x], two.at[low], self.ps.at[w, 2], self.pr.at[w, 2], self.by_y),
            send(near.at[high, lo, 1 - x], two.at[high], self.ps.at[w, 3], self.pr.at[w, 3], self.by_x),
        ]

    def line(self, w):
        self.wait(w, 2)
        near, part, lo, x = self.near[w], self.two[w], self.lo, self.x

        def body(z, carry):
            part[z] = (near[z, lo, x].astype(F32) + part[z].astype(F32)).astype(BF)
            return carry

        lax.fori_loop(0, self.nz, body, 0)
        self.copies[w, 3] = [
            send(
                part.at[z],
                self.end[w].at[k],
                self.zs.at[w, k],
                self.zr.at[w, k],
                at(z, lo, x, self.c),
            )
            for k, z in enumerate(self.z_index)
        ]

    def last(self, w, fin, out, sems):
        self.wait(w, 3)
        value = self.two[w][self.hi].astype(F32)
        for k in range(self.nz - 1):
            value += self.end[w][k].astype(F32)
        fin[...] = value
        count = self.shards[w][0]
        own = pl.ds(pl.multiple_of(self.c * count, 8), count)
        mate = pl.ds(pl.multiple_of((1 - self.c) * count, 8), count)
        spot = out.at[:, self.lanes(w, self.c)]
        return [
            keep(fin.at[own], spot, sems[0].at[w]),
            send(fin.at[mate], spot, sems[1].at[w], sems[2].at[w], self.partner),
        ]


def back_scatter_kernel(dp, shards, *refs):
    nz, nw = dp // 2, len(shards)
    n_ops = 7 + 4 + 10
    ops, (g_lin, g_ldn, hin, ffn_stats) = refs[:n_ops], refs[n_ops : n_ops + 4]
    outs, rest = refs[n_ops + 4 : n_ops + 7 + nw], refs[n_ops + 7 + nw :]
    dxo, total, gos, hin_o = outs[0], outs[1], outs[2 : 2 + nw], outs[2 + nw]
    full, rest = rest[:4], rest[4:]
    own_lin, own_ldn, stats, rest = rest[0], rest[1], rest[2], rest[3:]
    back, rest = rest[:17], rest[17:]
    dx = back[5]
    near, one, two, end, fin = (rest[k * nw : (k + 1) * nw] for k in range(5))
    hin_own, hin_r, acc, sc, sp, sz, acc2 = rest[5 * nw : 5 * nw + 7]
    own, xs, xr, cs, cr, ps, pr, zs, zr, hs, hr, ts, tr, *fsem = rest[5 * nw + 7 :]
    hi, lo, x, c = place()
    d = hi * 2 + lo
    plane = (lo * 2 + x) * 2 + c
    others = plane_others()
    rows_to = [(lax.rem(d + k, dp), x * 2 + c) for k in range(1, dp)]
    z_index = [lax.rem(hi + k, nz) for k in range(1, nz)]
    z_to = [at(z, lo, x, c) for z in z_index]
    quad = quad_peers()
    g_views = [g_lin, g_ldn]
    for k, w in enumerate((2, 3, 4, 5)):
        rows, columns = shards[w]
        g_views.append(full[k].reshape(nz, 2, 2, 2 * rows, columns))
    t = Scatter(nz, shards, g_views, near, one, two, end, (cs, cr, ps, pr, zs, zr))
    meet(rows_to + [at(hi, *q[:3]) for q in others if q[3]])
    h_sends = []
    for k, z in enumerate(z_index):
        h_sends.append(send(hin.at[z], hin_r.at[k], hs.at[1, k], hr.at[1, k], z_to[k]))
    t.core(0)
    t.core(1)
    kept = [
        keep(g_lin.at[:, :, :, :, t.lanes(0, c)], own_lin, own.at[0]),
        keep(g_ldn.at[:, :, :, :, t.lanes(1, c)], own_ldn, own.at[1]),
        keep(hin.at[hi], hin_own, own.at[2]),
    ]
    late = []

    def first_plane():
        kept[0].wait()
        kept[1].wait()
        t.own_plane(0, own_lin)
        t.own_plane(1, own_ldn)
        t.core(2)

    def out_core():
        t.core(3)

    def before_light():
        t.cross(0)
        t.cross(1)
        t.plane(2)

    def half_way():
        t.core(4)
        t.plane(3)
        t.line(0)
        t.line(1)

    def rims_left():
        t.plane(4)
        t.cross(2)
        t.cross(3)

    def light_grad_done():
        t.core(5)
        t.line(2)
        t.line(3)

    def rows_done():
        rows = dx.reshape(dxo.shape[1], dp, dxo.shape[2], D)
        late.append(keep(rows.at[:, d], dxo.at[d], own.at[4]))
        for k, to in enumerate(rows_to):
            late.append(send(rows.at[:, to[0]], dxo.at[d], xs.at[k], xr.at[k], to))

    stages = [
        first_plane,
        out_core,
        before_light,
        half_way,
        rims_left,
        light_grad_done,
        rows_done,
    ]
    attend_back_body(
        stages, *ops, full[3], full[2], full[1], full[0], dx, stats, *back
    )
    partner = at(hi, lo, x, 1 - c)
    for k in range(6):
        lanes = slice(k * 128, (k + 1) * 128)
        acc[k : k + 1, :] = stats[0:1, lanes]
        acc[6 + k : 7 + k, :] = ffn_stats[0:1, lanes]
    loss = jnp.sum(ffn_stats[1:2, :], axis=-1, keepdims=True)
    acc[12:16, :] = jnp.broadcast_to(loss, (4, 128))
    t_c = send(acc, sc, ts.at[0], tr.at[0], partner)
    t.plane(5)
    t.cross(4)
    t.line(4)
    t_c.wait()
    acc2[...] = acc[...] + sc[...]
    t_p = [
        send(acc2, sp.at[k], ts.at[1 + k], tr.at[1 + k], at(hi, l2, x2, c))
        for k, (l2, x2) in enumerate(quad)
    ]
    for copy in h_sends + kept[2:]:
        copy.wait()

    def body(i, carry):
        value = hin_own[i].astype(F32)
        for k in range(nz - 1):
            value += hin_r[k, i].astype(F32)
        hin_own[i] = value.astype(BF)
        return carry

    lax.fori_loop(0, 8, body, 0)
    hin_o[plane] = hin_own[plane]
    late += [
        send(
            hin_own.at[(q[0] * 2 + q[1]) * 2 + q[2]],
            hin_o.at[plane],
            hs.at[0, k],
            hr.at[0, k],
            at(hi, *q[:3]),
        )
        for k, q in enumerate(others)
    ]
    t.cross(5)
    for copy in t_p:
        copy.wait()
    acc[...] = acc2[...] + sp[0] + sp[1] + sp[2]
    t_z = [send(acc, sz.at[k], ts.at[4 + k], tr.at[4 + k], z_to[k]) for k in range(nz - 1)]
    t.line(5)
    for w in range(nw):
        late += t.last(w, fin[w], gos[w], fsem)
    for copy in t_z:
        copy.wait()
    value = acc[...]
    for k in range(nz - 1):
        value += sz[k]
    total[...] = value
    for copy in late:
        copy.wait()


def back_scatter(dp, rows, d_hidden, x, gain, masks, weights, saved, ffn_grads, ffn_stats, shards, hin):
    nz, nw = dp // 2, len(shards)
    tokens = x.shape[0]
    group = masks[0].shape[0]
    most = max(7, nz)
    stat_shape = (16, 128)
    paired = [
        g.reshape(nz, 2, 2, 2 * s[0], s[1]) for g, s in zip(ffn_grads, shards)
    ]
    operands = [d_hidden, x, gain, *masks, *weights, *saved, *paired, hin, ffn_stats]
    shapes = [jax.ShapeDtypeStruct((dp, group, rows, D), BF), jax.ShapeDtypeStruct(stat_shape, F32)]
    shapes += [jax.ShapeDtypeStruct(s, F32) for s in shards]
    shapes.append(jax.ShapeDtypeStruct(hin.shape[1:], BF))
    scratch = [pltpu.VMEM((s[0] * 8 * nz, s[1]), BF) for s in shards[2:]]
    split = [(2 * s[0], s[1] // 2) for s in shards]
    scratch += [pltpu.VMEM((nz, 2, 2) + s, BF) for s in split[:2]]
    scratch += [pltpu.VMEM((8, D), F32)]
    scratch += attend_back_scratch(tokens, masks[0])
    scratch += [pltpu.VMEM((nz, 2, 2) + s, BF) for s in split]
    scratch += [pltpu.VMEM((nz, 2) + s, BF) for s in split]
    scratch += [pltpu.VMEM((nz,) + s, BF) for s in split]
    scratch += [pltpu.VMEM((nz - 1,) + s, BF) for s in split]
    scratch += [pltpu.VMEM(s, F32) for s in split]
    scratch += [
        pltpu.VMEM(hin.shape[1:], BF),
        pltpu.VMEM((nz - 1,) + hin.shape[1:], BF),
        pltpu.VMEM(stat_shape, F32),
        pltpu.VMEM(stat_shape, F32),
        pltpu.VMEM((3,) + stat_shape, F32),
        pltpu.VMEM((nz - 1,) + stat_shape, F32),
        pltpu.VMEM(stat_shape, F32),
        DMA((5,)),
        DMA((dp,)),
        DMA((dp,)),
        DMA((nw,)),
        DMA((nw,)),
        DMA((nw, 4)),
        DMA((nw, 4)),
        DMA((nw, nz)),
        DMA((nw, nz)),
        DMA((3, most)),
        DMA((3, most)),
        DMA((4 + nz,)),
        DMA((4 + nz,)),
        DMA((nw,)),
        DMA((nw,)),
        DMA((nw,)),
    ]
    return call(
        functools.partial(back_scatter_kernel, dp, shards),
        shapes,
        operands,
        [VM] * (len(operands) - 4) + [ANY] * 3 + [VM],
        [VM] * len(shapes),
        scratch,
        6,
    )


def routing(routes, pieces, piece_len):
    places = jnp.arange(pieces * piece_len)
    routed = jnp.any(routes[:, None, :] == places[None, :, None], axis=-1)
    routed = routed.reshape(-1, pieces, piece_len)
    before = jnp.arange(piece_len)[:, None] < jnp.arange(piece_len)[None, :]
    rank = jnp.einsum(
        "skp,pq->skq", routed.astype(BF), before.astype(BF), preferred_element_type=F32
    )
    slots = jnp.arange(CAP, dtype=F32)
    hot = routed[:, :, None, :] & (rank[:, :, None, :] == slots[None, None, :, None])
    filled = jnp.any(hot, axis=-1)
    spots = jnp.sum(jnp.where(hot, places.reshape(1, pieces, 1, piece_len), 0), axis=-1)
    return hot, jnp.where(filled, spots, -1)


def local(
    layer_input,
    teacher,
    lengths,
    dealing,
    attn_routes,
    ffn_routes,
    ffn_scores,
    gain_attn,
    gain_ffn,
    light_qkv,
    light_out,
    heavy_qkv,
    heavy_out,
    light_in,
    light_down,
    heavy_in,
    heavy_down,
):
    dp = lax.axis_size("dp")
    pieces = lax.axis_size("fsdp")
    data_index = lax.axis_index("dp")
    piece = lax.axis_index("fsdp")
    nz = dp // 2
    n = dp * pieces
    seqs = dealing.shape[0]
    group = seqs // dp
    gain_len = gain_attn.shape[0]
    hidden_units = heavy_in.shape[1] // 2 // n
    mine = data_index * pieces + piece
    tokens = layer_input.shape[2] * dp
    matrices = (light_qkv, heavy_qkv, light_out, heavy_out, light_in, light_down)
    hin_rows = heavy_in.shape[0]
    token_count = jnp.sum(lengths).astype(F32)
    merged = (
        layer_input.shape[2] % 16 == 0
        and hidden_units % 128 == 0
        and all(m.shape[0] % 8 == 0 and m.shape[1] % 256 == 0 for m in (*matrices, heavy_down))
    )
    if merged:
        xin, hin_src, gains = prepare(dealing, layer_input[:, 0], heavy_in, gain_attn, gain_ffn)
        integers = (dealing.reshape(1, -1), lengths.reshape(1, -1), attn_routes, ffn_routes, ffn_scores)
        got = gather_attend(dp, xin, [gains, *matrices], hin_src, integers)
    else:
        xin = deal_rows(dealing, layer_input[:, 0])
        owned = jnp.arange(D)[None, :] // gain_len == mine
        spread_out = jnp.broadcast_to(
            jnp.stack([gain_attn, gain_ffn])[:, None, :], (2, D // gain_len, gain_len)
        ).reshape(2, D)
        gains = jnp.pad(jnp.where(owned, spread_out, 0.0).astype(BF), ((0, 6), (0, 0)))
        hin_src = (
            heavy_in.reshape(hin_rows, 2, nz, 8, hidden_units)
            .transpose(3, 0, 1, 2, 4)
            .reshape(8, hin_rows, 2 * nz * hidden_units)
        )
        if hin_rows % 8:
            hin_src = hin_src.reshape(8, -1, 128)
        got = gather_all(dp, xin, [gains] + [packed(m) for m in matrices], hin_src)
    flat_x = got[0].reshape(-1, D)
    w_lqkv, w_hqkv, w_lout, w_hout, w_lin, w_ldown = (
        unpacked(full, *m.shape) for full, m in zip(got[2:8], matrices)
    )
    w_hin = unpacked(got[8], hin_rows, 2 * nz * hidden_units)
    attn_weights = (w_lqkv, w_hqkv, w_lout, w_hout)
    if merged:
        gain, tables, (hidden, *saved) = got[9], got[10:19], got[19:]
        masks, ffn_masks = tables[:4], tables[4:]
    else:
        gain = jnp.sum(got[1].reshape(n, 8, D).astype(F32), axis=0)
        masks, ffn_masks = integer_tables(
            dealing, lengths, attn_routes, ffn_routes, ffn_scores, group, pieces, tokens
        )
        hidden, *saved = attend(flat_x, gain, *masks, *attn_weights)
    f_select, f_select_t, slot_score, weight_mask, weight_scale = ffn_masks
    grad_lin, grad_ldown, grad_hin, g_hdown, d_hidden, ffn_stats = feed_forward(
        nz,
        hidden,
        f_select,
        f_select_t,
        slot_score,
        gain,
        teacher.reshape(-1, D),
        weight_mask,
        weight_scale,
        w_lin,
        w_ldown,
        w_hin,
        heavy_down,
    )
    rows = tokens // dp
    shards = (light_in, light_down, heavy_out, light_out, heavy_qkv, light_qkv)
    hin_part = grad_hin.reshape((nz, 8) + hin_src.shape[1:])
    if merged:
        done = back_scatter(
            dp,
            rows,
            d_hidden,
            flat_x,
            gain,
            masks,
            attn_weights,
            saved,
            (grad_lin, grad_ldown),
            ffn_stats,
            tuple(shard.shape for shard in shards),
            hin_part,
        )
    else:
        grad_lqkv, grad_hqkv, grad_lout, grad_hout, d_inputs, attn_stats = attend_back(
            d_hidden, flat_x, gain, *masks, attn_weights, saved
        )
        stats = jnp.concatenate(
            [
                attn_stats[0].reshape(-1, 128),
                ffn_stats[0].reshape(-1, 128),
                jnp.broadcast_to(jnp.sum(ffn_stats[1]), (4, 128)),
            ]
        )
        grads = (grad_lin, grad_ldown, grad_hout, grad_lout, grad_hqkv, grad_lqkv)
        sent = [packed_full(grad, shard.shape, nz) for grad, shard in zip(grads, shards)]
        done = scatter_all(
            dp, d_inputs.reshape(group, dp, rows, D), stats, sent, hin_part
        )
    summed = done[1]
    loss_value = summed[12, 0] / (D * token_count)
    own_one = lax.dynamic_slice_in_dim(summed[:6].reshape(-1), mine * gain_len, gain_len)
    own_two = lax.dynamic_slice_in_dim(summed[6:12].reshape(-1), mine * gain_len, gain_len)
    back_rows = done[0].reshape(seqs, rows, D)
    if merged:
        d_layer, g_hin, *owned = finish_all(
            n, dealing, back_rows, done[8], [*done[2:8], g_hdown], heavy_in.shape
        )
    else:
        d_layer = undeal_rows(dealing, back_rows)
        owned = [full.reshape(shard.shape) for full, shard in zip(done[2:8], shards)]
        owned.append(g_hdown)
        g_hin = (
            done[8]
            .astype(F32)
            .reshape(8, hin_rows, 2, nz, hidden_units)
            .transpose(1, 2, 3, 0, 4)
            .reshape(heavy_in.shape)
        )
    g_lin, g_ldown, g_hout, g_lout, g_hqkv, g_lqkv, g_hdown = owned
    return (
        loss_value,
        d_layer[:, None],
        own_one,
        own_two,
        g_lqkv,
        g_lout,
        g_hqkv,
        g_hout,
        g_lin,
        g_ldown,
        g_hin,
        g_hdown,
    )


def integer_tables(dealing, lengths, attn_routes, ffn_routes, ffn_scores, group, pieces, tokens):
    seqs = dealing.shape[0]
    data_index = lax.axis_index("dp")
    piece = lax.axis_index("fsdp")
    chosen = lax.dynamic_slice_in_dim(dealing, data_index * group, group)
    one = chosen[:, None] == jnp.arange(seqs)[None, :]
    seq_lengths = jnp.sum(jnp.where(one, lengths[None, :], 0), axis=1)
    attn_pick = jnp.sum(jnp.where(one[:, :, None], attn_routes[None], 0), axis=1)
    ffn_pick = jnp.sum(jnp.where(one[:, :, None], ffn_routes[None], 0), axis=1)
    score_pick = jnp.sum(jnp.where(one[:, :, None], ffn_scores[None], 0.0), axis=1)
    token_count = jnp.sum(lengths).astype(F32)
    positions = piece * tokens + jnp.arange(tokens)
    valid_mask = positions[None, :] < seq_lengths[:, None]
    a_hot, a_spots = routing(attn_pick, pieces, tokens)
    f_hot, f_spots = routing(ffn_pick, pieces, tokens)
    a_select = lax.dynamic_index_in_dim(a_hot, piece, 1, False).astype(BF)
    f_select = lax.dynamic_index_in_dim(f_hot, piece, 1, False).astype(BF)
    a_spot = lax.dynamic_index_in_dim(a_spots, piece, 1, False)
    f_spot = lax.dynamic_index_in_dim(f_spots, piece, 1, False)
    slot_score = jnp.sum(
        jnp.where(f_spot[:, :, None] == ffn_pick[:, None, :], score_pick[:, None, :], 0.0), axis=-1
    )
    key_pos = piece * tokens - WIN + jnp.arange(tokens + 2 * WIN)
    live_key = (key_pos >= 0)[None, :] & (key_pos[None, :] < seq_lengths[:, None])
    key_line = jnp.where(live_key, 0.0, MASKED)
    key_bias = jnp.stack(
        [key_line[:, b : b + 3 * WIN] for b in range(0, tokens, WIN)], axis=1
    ).reshape(-1, 1, 3 * WIN)
    all_spots = a_spots.reshape(group, pieces * CAP)
    heavy_allowed = ((all_spots >= 0) & (all_spots < seq_lengths[:, None]))[:, None, :] | (
        a_spot[:, :, None] == all_spots[:, None, :]
    )
    heavy_bias = jnp.where(heavy_allowed, 0.0, MASKED)
    weight_mask = valid_mask.reshape(-1, 1).astype(F32)
    masks = (a_select, a_select.swapaxes(1, 2), key_bias, heavy_bias)
    ffn_masks = (
        f_select,
        f_select.swapaxes(1, 2),
        slot_score.reshape(-1, 1),
        weight_mask,
        2.0 * weight_mask / (D * token_count),
    )
    return masks, ffn_masks


def packed_full(grad, shard_shape, nz):
    rows, columns = shard_shape
    if rows % 8 == 0:
        return grad.reshape(nz, 2, 2, 2, rows, columns)
    return grad.reshape(nz, 2, 2, 2, rows * columns // 128, 128)


def solution(mesh):
    split = P(("dp", "fsdp"))
    matrix = P(("dp", "fsdp"), None)
    placed = (
        P(None, "fsdp", "dp", None),
        P("dp", "fsdp", None, None),
        P(),
        P(),
        P(),
        P(),
        P(),
        split,
        split,
    ) + (matrix,) * 8
    return jax.shard_map(
        local,
        mesh=mesh,
        in_specs=placed,
        out_specs=(P(), P(None, "fsdp", "dp", None), split, split) + (matrix,) * 8,
        check_vma=False,
    )
```

```python
import functools
import jax
import jax.numpy as jnp
from jax import lax
from jax.experimental import pallas as pl
from jax.experimental.pallas import tpu as pltpu
from jax.sharding import PartitionSpec as P

D = 768
HL = 8
HH = 12
DH = 64
FL = 1024
FH = 4096
WIN = 128
CAP = 64

EPSILON = 1e-06
MASKED = -1000000000.0
SCORE_SCALE = 0.125
MESH = pl.DeviceIdType.MESH
BF = jnp.bfloat16
F32 = jnp.float32
ANY = pl.BlockSpec(memory_space=pl.ANY)
VM = pl.BlockSpec(memory_space=pltpu.VMEM)
DMA = pltpu.SemaphoreType.DMA
VMEM_BYTES = 60 * 1024 * 1024


def place():
    d = lax.axis_index("dp")
    f = lax.axis_index("fsdp")
    return d // 2, d % 2, f // 2, f % 2


def at(hi, lo, x, c):
    return (hi * 2 + lo, x * 2 + c)


def meet(peers):
    barrier = pltpu.get_barrier_semaphore()
    for peer in peers:
        pl.semaphore_signal(barrier, inc=1, device_id=peer, device_id_type=MESH)
    pl.semaphore_wait(barrier, len(peers))


def send(src, dst, send_sem, recv_sem, peer):
    copy = pltpu.make_async_remote_copy(
        src_ref=src,
        dst_ref=dst,
        send_sem=send_sem,
        recv_sem=recv_sem,
        device_id=peer,
        device_id_type=MESH,
    )
    copy.start()
    return copy


def keep(src, dst, sem):
    copy = pltpu.make_async_copy(src, dst, sem)
    copy.start()
    return copy


def quad_peers():
    hi, lo, x, c = place()
    return [(lo, 1 - x), (1 - lo, x), (1 - lo, 1 - x)]


def call(kernel, out_shape, operands, in_specs, out_specs, scratch, collective_id):
    return pl.pallas_call(
        kernel,
        out_shape=out_shape,
        in_specs=in_specs,
        out_specs=out_specs,
        scratch_shapes=scratch,
        compiler_params=pltpu.CompilerParams(
            collective_id=collective_id, has_side_effects=True, vmem_limit_bytes=VMEM_BYTES
        ),
    )(*operands)


def deal_kernel(deal_ref, x_ref, o_ref):
    def body(i, carry):
        o_ref[i] = x_ref[deal_ref[i]]
        return carry

    lax.fori_loop(0, o_ref.shape[0], body, 0)


def deal_rows(dealing, rows):
    return pl.pallas_call(
        deal_kernel,
        out_shape=jax.ShapeDtypeStruct(rows.shape, rows.dtype),
        in_specs=[pl.BlockSpec(memory_space=pltpu.SMEM), VM],
        out_specs=VM,
        compiler_params=pltpu.CompilerParams(vmem_limit_bytes=VMEM_BYTES),
    )(dealing, rows)


def undeal_kernel(deal_ref, x_ref, o_ref):
    def body(i, carry):
        o_ref[deal_ref[i]] = x_ref[i].astype(F32)
        return carry

    lax.fori_loop(0, x_ref.shape[0], body, 0)


def undeal_rows(dealing, rows):
    return pl.pallas_call(
        undeal_kernel,
        out_shape=jax.ShapeDtypeStruct(rows.shape, F32),
        in_specs=[pl.BlockSpec(memory_space=pltpu.SMEM), VM],
        out_specs=VM,
        compiler_params=pltpu.CompilerParams(vmem_limit_bytes=VMEM_BYTES),
    )(dealing, rows)


def prepare_kernel(deal_ref, x_ref, heavy_ref, one_ref, two_ref, xin, hin, gains):
    def body(i, carry):
        xin[i] = x_ref[deal_ref[i]]
        return carry

    lax.fori_loop(0, xin.shape[0], body, 0)
    count = one_ref.shape[1]
    units = D // count
    step = heavy_ref.shape[1] // 2 // units
    for j in range(8):
        for k in range(units // 8):
            for g in (0, 1):
                start = g * heavy_ref.shape[1] // 2 + (k * 8 + j) * step
                spot = (g * (units // 8) + k) * step
                hin[j, :, spot : spot + step] = heavy_ref[:, start : start + step]
    mine = lax.axis_index("dp") * 4 + lax.axis_index("fsdp")
    row = lax.broadcasted_iota(jnp.int32, (count, D), 0)
    lane = lax.broadcasted_iota(jnp.int32, (count, D), 1)
    hot = jnp.where(lane == row + mine * count, 1.0, 0.0).astype(BF)
    lines = [jnp.broadcast_to(ref[...], (8, count)) for ref in (one_ref, two_ref)]
    one, two = (jnp.dot(line, hot, preferred_element_type=F32) for line in lines)
    kind = lax.broadcasted_iota(jnp.int32, (8, D), 0)
    gains[...] = jnp.where(kind == 0, one, jnp.where(kind == 1, two, 0.0)).astype(BF)


def prepare(dealing, rows, heavy_in, gain_one, gain_two):
    count = gain_one.shape[0]
    columns = heavy_in.shape[1] // 8
    return pl.pallas_call(
        prepare_kernel,
        out_shape=[
            jax.ShapeDtypeStruct(rows.shape, BF),
            jax.ShapeDtypeStruct((8, heavy_in.shape[0], columns), BF),
            jax.ShapeDtypeStruct((8, D), BF),
        ],
        in_specs=[pl.BlockSpec(memory_space=pltpu.SMEM), VM, VM, VM, VM],
        out_specs=[VM] * 3,
        compiler_params=pltpu.CompilerParams(vmem_limit_bytes=VMEM_BYTES),
    )(dealing, rows, heavy_in, gain_one.reshape(1, count), gain_two.reshape(1, count))


def finish_kernel(units, deal_ref, x_ref, hin, *refs):
    count = (len(refs) - 2) // 2
    ins, (rows, heavy), outs = refs[:count], refs[count : count + 2], refs[count + 2 :]

    def body(i, carry):
        rows[deal_ref[i]] = x_ref[i].astype(F32)
        return carry

    lax.fori_loop(0, x_ref.shape[0], body, 0)
    step = heavy.shape[1] // 2 // units
    for j in range(8):
        for k in range(units // 8):
            for g in (0, 1):
                start = g * heavy.shape[1] // 2 + (k * 8 + j) * step
                spot = (g * (units // 8) + k) * step
                heavy[:, start : start + step] = hin[j, :, spot : spot + step].astype(F32)
    for source, out in zip(ins, outs):
        out[...] = source[...]


def finish_all(units, dealing, rows, hin, grads, heavy_shape):
    shapes = [jax.ShapeDtypeStruct(rows.shape, F32), jax.ShapeDtypeStruct(heavy_shape, F32)]
    shapes += [jax.ShapeDtypeStruct(g.shape, F32) for g in grads]
    return pl.pallas_call(
        functools.partial(finish_kernel, units),
        out_shape=shapes,
        in_specs=[pl.BlockSpec(memory_space=pltpu.SMEM)] + [VM] * (2 + len(grads)),
        out_specs=[VM] * len(shapes),
        compiler_params=pltpu.CompilerParams(vmem_limit_bytes=VMEM_BYTES),
    )(dealing, rows, hin, *grads)


def packed(matrix):
    rows, columns = matrix.shape
    if rows % 8 == 0:
        return matrix
    return matrix.reshape(rows * columns // 128, 128)


def unpacked(gathered, rows, columns):
    return gathered.reshape(-1, rows, columns).reshape(-1, columns)


def plane_others():
    hi, lo, x, c = place()
    others = []
    for a in (0, 1):
        for b in (0, 1):
            for e in (0, 1):
                if a or b or e:
                    others.append(
                        (1 - lo if a else lo, 1 - x if b else x, 1 - c if e else c, b or e)
                    )
    return others


class Gather:
    def __init__(self, dp, xin, ws, hin, xo, wos, hin_o, sems, halves=None):
        self.dp, self.nz = dp, dp // 2
        self.xin, self.ws, self.hin = xin, ws, hin
        self.xo, self.wos, self.hin_o = xo, wos, hin_o
        self.loc, self.xs, self.xr, self.zs, self.zr = sems[:5]
        self.ps, self.pr, self.cs, self.cr, self.hs, self.hr = sems[5:]
        self.hi, self.lo, self.x, self.c = place()
        hi, lo, x, c = place()
        self.d = hi * 2 + lo
        self.home = (lo * 2 + x) * 2 + c
        self.rows_to = [(lax.rem(self.d + k, dp), x * 2 + c) for k in range(1, dp)]
        self.z_to = [at(lax.rem(hi + k, self.nz), lo, x, c) for k in range(1, self.nz)]
        self.others = plane_others()
        nw = len(ws)
        self.kept, self.z, self.p, self.f, self.k = ([None] * nw for _ in range(5))

        self.halves = halves

    def lanes(self, w, c):
        half = self.ws[w].shape[1] // 2
        return pl.ds(pl.multiple_of(c * half, 128), half)

    def shard(self, w, z, lo, x):
        if self.halves is None:
            return self.wos[w].at[z, lo, x, self.c]
        return self.wos[w].at[z, lo, x, :, self.lanes(w, self.c)]

    def swap(self, w):
        mine, mate, _, sems = self.halves
        partner = at(self.hi, self.lo, self.x, 1 - self.c)
        self.kept[w] = keep(self.ws[w].at[:, self.lanes(w, self.c)], mine[w], sems[0].at[w])
        out = self.ws[w].at[:, self.lanes(w, 1 - self.c)]
        self.z[w] = send(out, mate[w], sems[1].at[w], sems[2].at[w], partner)

    def join(self, w):
        mine, mate, base, _ = self.halves
        self.kept[w].wait()
        self.z[w].wait()
        a, b = mine[w][...].astype(F32), mate[w][...].astype(F32)
        first = self.c == 0
        rows = [jnp.where(first, a, b), jnp.where(first, b, a)]
        base[w][...] = jnp.concatenate(rows, axis=0).astype(BF)
        self.line(w)

    def meet(self):
        peers = self.rows_to + [at(self.hi, *q[:3]) for q in self.others if q[3]]
        meet(peers)

    def rows(self):
        group = self.xin.shape[0] // self.dp
        nw = len(self.ws)
        spot = self.xo.at[:, self.d]
        self.own = keep(self.xin.at[pl.ds(self.d * group, group)], spot, self.loc.at[nw])
        self.moved = [
            send(self.xin.at[pl.ds(to[0] * group, group)], spot, self.xs.at[k], self.xr.at[k], to)
            for k, to in enumerate(self.rows_to)
        ]

    def rows_ready(self):
        self.own.wait()
        for copy in self.moved:
            copy.wait()

    def line(self, w):
        spot = self.shard(w, self.hi, self.lo, self.x)
        own = self.ws[w] if self.halves is None else self.halves[2][w]
        self.kept[w] = keep(own, spot, self.loc.at[w])
        self.z[w] = [
            send(own, spot, self.zs.at[w, k], self.zr.at[w, k], to)
            for k, to in enumerate(self.z_to)
        ]

    def onward(self, part, w, k, to, sems):
        return send(part, part, sems[0].at[w, k], sems[1].at[w, k], to)

    def plane(self, w):
        self.kept[w].wait()
        for copy in self.z[w]:
            copy.wait()
        hi, lo, x, c = self.hi, self.lo, self.x, self.c
        column = self.shard(w, slice(None), lo, x)
        plane = (self.ps, self.pr)
        self.p[w] = [
            self.onward(column, w, 0, at(hi, lo, 1 - x, c), plane),
            self.onward(column, w, 1, at(hi, 1 - lo, x, c), plane),
        ]
        self.k[w] = [self.onward(column, w, 0, at(hi, lo, x, 1 - c), (self.cs, self.cr))]

    def cross(self, w):
        hi, lo, x, c = self.hi, self.lo, self.x, self.c
        plane, core, half = (self.ps, self.pr), (self.cs, self.cr), self.nz // 2
        partner = at(hi, lo, x, 1 - c)
        self.p[w][1].wait()
        part = self.shard(w, pl.ds(0, half), 1 - lo, x)
        first = self.onward(part, w, 2, at(hi, lo, 1 - x, c), plane)
        self.p[w][0].wait()
        part = self.shard(w, pl.ds(half, self.nz - half), lo, 1 - x)
        self.f[w] = [first, self.onward(part, w, 3, at(hi, 1 - lo, x, c), plane)]
        for k, part in ((1, (1 - lo, x)), (2, (lo, 1 - x))):
            self.k[w].append(
                self.onward(self.shard(w, slice(None), *part), w, k, partner, core)
            )

    def core(self, w):
        for copy in self.f[w]:
            copy.wait()
        part = self.shard(w, slice(None), 1 - self.lo, 1 - self.x)
        partner = at(self.hi, self.lo, self.x, 1 - self.c)
        self.k[w].append(self.onward(part, w, 3, partner, (self.cs, self.cr)))

    def ready(self, w):
        for copy in self.k[w]:
            copy.wait()

    def heavy_plane(self):
        nw, hi = len(self.ws), self.hi
        spot = self.hin_o.at[hi, self.home]
        self.h_own = [
            keep(self.hin.at[self.home], spot, self.loc.at[nw + 1]),
        ]
        self.h_near = [
            send(
                self.hin.at[(q[0] * 2 + q[1]) * 2 + q[2]],
                spot,
                self.hs.at[0, k],
                self.hr.at[0, k],
                at(hi, *q[:3]),
            )
            for k, q in enumerate(self.others)
        ]

    def heavy_line(self):
        for copy in self.h_own + self.h_near:
            copy.wait()
        part = self.hin_o.at[self.hi]
        self.h_far = []
        for k, to in enumerate(self.z_to):
            self.h_far.append(send(part, part, self.hs.at[1, k], self.hr.at[1, k], to))

    def heavy_ready(self):
        for copy in self.h_far:
            copy.wait()


def gather_sems(dp, nw):
    nz, most = dp // 2, max(7, dp // 2)
    return [
        DMA((nw + 2,)),
        DMA((dp,)),
        DMA((dp,)),
        DMA((nw, nz)),
        DMA((nw, nz)),
        DMA((nw, 4)),
        DMA((nw, 4)),
        DMA((nw, 4)),
        DMA((nw, 4)),
        DMA((2, most)),
        DMA((2, most)),
    ]


def gather_kernel(dp, nw, *refs):
    ins, outs, sems = refs[: 2 + nw], refs[2 + nw : 4 + 2 * nw], refs[4 + 2 * nw :]
    g = Gather(dp, ins[0], ins[1:-1], ins[-1], outs[0], outs[1:-1], outs[-1], sems)
    g.meet()
    g.rows()
    for w in range(nw):
        g.line(w)
    g.heavy_plane()
    for w in range(nw):
        g.plane(w)
        if w == 1:
            g.heavy_line()
        if w >= 1:
            g.cross(w - 1)
        if w >= 2:
            g.core(w - 2)
    g.cross(nw - 1)
    for w in range(nw - 2, nw):
        g.core(w)
    g.rows_ready()
    for w in range(nw):
        g.ready(w)
    g.heavy_ready()


def gather_shapes(dp, xin, weights, hin, paired):
    nz = dp // 2
    seqs, rows, _ = xin.shape
    shapes = [jax.ShapeDtypeStruct((seqs // dp, dp, rows, D), BF)]
    if paired:
        shapes += [jax.ShapeDtypeStruct((nz, 2, 2, 2 * w.shape[0], w.shape[1]), BF) for w in weights]
    else:
        shapes += [jax.ShapeDtypeStruct((nz, 2, 2, 2) + w.shape, BF) for w in weights]
    shapes.append(jax.ShapeDtypeStruct((nz,) + hin.shape, BF))
    return shapes


def gather_all(dp, xin, weights, hin):
    nw = len(weights)
    return call(
        functools.partial(gather_kernel, dp, nw),
        gather_shapes(dp, xin, weights, hin, False),
        [xin, *weights, hin],
        [ANY] * (2 + nw),
        [ANY] * (2 + nw),
        gather_sems(dp, nw),
        1,
    )


def rim_exchange(left, right, from_left, from_right, ls, lr, rs, rr):
    d = lax.axis_index("dp")
    f = lax.axis_index("fsdp")
    last = lax.axis_size("fsdp") - 1

    def down():
        return pltpu.make_async_remote_copy(
            src_ref=left,
            dst_ref=from_right,
            send_sem=ls,
            recv_sem=lr,
            device_id=(d, lax.max(f - 1, 0)),
            device_id_type=MESH,
        )

    def up():
        return pltpu.make_async_remote_copy(
            src_ref=right,
            dst_ref=from_left,
            send_sem=rs,
            recv_sem=rr,
            device_id=(d, lax.min(f + 1, last)),
            device_id_type=MESH,
        )

    @pl.when(f > 0)
    def _():
        down().start()

    @pl.when(f < last)
    def _():
        up().start()

    @pl.when(f == 0)
    def _():
        from_left[...] = jnp.zeros(from_left.shape, from_left.dtype)

    @pl.when(f == last)
    def _():
        from_right[...] = jnp.zeros(from_right.shape, from_right.dtype)

    def finish():
        @pl.when(f > 0)
        def _():
            down().wait_send()
            up().wait_recv()

        @pl.when(f < last)
        def _():
            up().wait_send()
            down().wait_recv()

    return finish


def line_peers():
    hi, lo, x, c = place()
    return [at(hi, lo, x, 1 - c), at(hi, lo, 1 - x, c), at(hi, lo, 1 - x, 1 - c)]


def dot(left, right):
    return jnp.dot(left, right, preferred_element_type=F32)


def dot_back(left, right):
    return lax.dot_general(left, right, (((1,), (1,)), ((), ())), preferred_element_type=F32)


def dot_grad(left, right):
    return lax.dot_general(left, right, (((0,), (0,)), ((), ())), preferred_element_type=F32)


def halves(value):
    high = value.astype(BF)
    return high, (value - high.astype(F32)).astype(BF)


def tiles(extent, step, body):
    def run(i, carry):
        body(pl.ds(pl.multiple_of(i * step, step), step))
        return carry

    lax.fori_loop(0, extent // step, run, 0)


GELU_A = 0.7978845608028654
GELU_B = 0.044715


def gelu_parts(v):
    square = v * v
    t = jnp.tanh(GELU_A * v * (1.0 + GELU_B * square))
    value = 0.5 * v * (1.0 + t)
    slope = 0.5 * (1.0 + t) + 0.5 * v * (1.0 - t * t) * GELU_A * (1.0 + 3.0 * GELU_B * square)
    return value, slope


def gelu_value(v):
    return 0.5 * v * (1.0 + jnp.tanh(GELU_A * v * (1.0 + GELU_B * v * v)))


def ffn_kernel(
    nz,
    hidden,
    select,
    select_t,
    score,
    gain,
    teach_hbm,
    mask,
    scale,
    w_in_hbm,
    w_dn_hbm,
    w_hin_hbm,
    hdn,
    g_in_hbm,
    g_dn_hbm,
    g_hin_hbm,
    hdn_o,
    d_hidden,
    stats,
    teach,
    w_in,
    w_dn,
    w_hin,
    g_in,
    g_dn,
    g_hin,
    moves_sem,
    w_line,
    g_line,
    g_in_line,
    hn,
    every,
    d_every,
    up_l,
    z,
    up_h,
    zh,
    part,
    near,
    far,
    out,
    dl,
    dup_l,
    dup_h,
    dhn,
    ps,
    pr,
    cs,
    cr,
    qs,
    qr,
    es,
    er,
    zs,
    zr,
    own,
):
    hi, lo, x, c = place()
    quad = quad_peers()
    partner = at(hi, lo, x, 1 - c)
    spots = [l2 * 2 + x2 for l2, x2 in quad]
    home = lo * 2 + x
    tokens = hidden.shape[0]
    group, cap, width = select.shape
    fl = z.shape[1]
    fh = zh.shape[3]
    block = 4 * cap
    z_index = [lax.rem(hi + k, nz) for k in range(1, nz)]
    z_to = [at(k, lo, x, c) for k in z_index]
    meet([at(hi, l2, x2, c) for l2, x2 in quad] + [partner] + z_to)
    pairs = ((w_in_hbm, w_in), (w_dn_hbm, w_dn), (w_hin_hbm, w_hin), (teach_hbm, teach))
    fetched = [keep(source, ref, moves_sem.at[k]) for k, (source, ref) in enumerate(pairs)]
    hdn_own = keep(hdn, w_line.at[hi], own)
    hdn_far = [send(hdn, w_line.at[hi], zs.at[0, k], zr.at[0, k], to) for k, to in enumerate(z_to)]
    w_hdn = w_line.reshape(-1, D)

    def span(s):
        return slice(s * width, (s + 1) * width)

    def slots(s):
        return slice(s * cap, (s + 1) * cap)

    def spread(buffer, s, i):
        spot = buffer.at[s, c, home]
        there = [
            send(spot, spot, ps.at[i, k], pr.at[i, k], at(hi, l2, x2, c))
            for k, (l2, x2) in enumerate(quad)
        ]
        return there, [send(spot, spot, cs.at[i, 3], cr.at[i, 3], partner)]

    def relay(buffer, s, i, there, back):
        for k, q in enumerate(spots):
            there[k].wait()
            other = buffer.at[s, c, q]
            back.append(send(other, other, cs.at[i, k], cr.at[i, k], partner))

    def fold(s, i, copy):
        copy.wait()
        there = []
        for k, q in enumerate(spots):
            near[i, q] = (near[i, q].astype(F32) + part[s, c, q].astype(F32)).astype(BF)
            l2, x2 = quad[k]
            there.append(
                send(near.at[i, q], far.at[i, k], qs.at[i, k], qr.at[i, k], at(hi, l2, x2, c))
            )
        return there

    def folded(s, i, there):
        for copy in there:
            copy.wait()
        return (
            near[i, home].astype(F32)
            + part[s, c, home].astype(F32)
            + far[i, 0].astype(F32)
            + far[i, 1].astype(F32)
            + far[i, 2].astype(F32)
        )

    def norm(r):
        h = hidden[r, :]
        inv = lax.rsqrt(jnp.mean(h * h, axis=-1, keepdims=True) + EPSILON)
        hn[r, :] = (h * inv * gain[1:2, :]).astype(BF)

    seqs = range(group)
    moves = {}
    tiles(tokens, 128, norm)
    for s in seqs:
        every[s, c, home] = dot(select[s], hn[span(s), :]).astype(BF)
        moves[s] = spread(every, s, s)

    def light_up(r):
        up_l[r, :] = dot(hn[r, :], w_in[...])
        z[r, :] = (gelu_value(up_l[r, :fl]) * up_l[r, fl:]).astype(BF)

    fetched[0].wait()
    tiles(tokens, width, light_up)
    for s in seqs:
        relay(every, s, s, *moves[s])

    def light_down(r):
        out[r, :] = hidden[r, :] + dot(z[r, :], w_dn[...])

    fetched[1].wait()
    tiles(tokens, width, light_down)

    def light_slopes(r):
        value, slope = gelu_parts(up_l[r, :fl])
        up_l[r, :fl] = up_l[r, fl:] * slope
        up_l[r, fl:] = value

    def heavy_up(s, e):
        up_h[s, e] = dot(every[s, e].reshape(block, D), w_hin[...])
        zh[s, e] = (gelu_value(up_h[s, e, :, :fh]) * up_h[s, e, :, fh:]).astype(BF)

    def heavy_down(s, e):
        part[s, e] = dot(zh[s, e], w_hdn[...]).astype(BF).reshape(4, cap, D)

    fetched[2].wait()
    sums = {}
    for s in seqs:
        for copy in moves[s][1]:
            copy.wait()
        heavy_up(s, 1 - c)
        heavy_up(s, c)
    tiles(tokens, 64, light_slopes)
    hdn_own.wait()
    for copy in hdn_far:
        copy.wait()
    for s in seqs:
        heavy_down(s, 1 - c)
        first = send(part.at[s, 1 - c], near.at[s], es.at[s], er.at[s], partner)
        heavy_down(s, c)
        sums[s] = fold(s, s, first)
    for s in seqs:
        for e in (0, 1):

            def heavy_slopes(r, s=s, e=e):
                value, slope = gelu_parts(up_h[s, e, r, :fh])
                up_h[s, e, r, :fh] = up_h[s, e, r, fh:] * slope
                up_h[s, e, r, fh:] = value

            if s == 0:
                tiles(block, 128, heavy_slopes)
    stats[...] = jnp.zeros(stats.shape, F32)
    fetched[3].wait()

    def light_back(r):
        dz = dot_back(dl[r, :], w_dn[...])
        dup_l[r, :fl] = (dz * up_l[r, :fl]).astype(BF)
        dup_l[r, fl:] = (dz * up_l[r, fl:]).astype(BF)

    for s in seqs:
        r = span(s)
        high, low = halves(folded(s, s, sums[s]) * score[slots(s), :])
        total = out[r, :] + (dot(select_t[s], high) + dot(select_t[s], low))
        m = total - teach[r, :].astype(F32)
        stats[1:2, :] += jnp.sum(mask[r, :] * m * m, axis=0, keepdims=True)
        d = scale[r, :] * m
        out[r, :] = d
        dl[r, :] = d.astype(BF)
        high, low = halves(d)
        picked = dot(select[s], high) + dot(select[s], low)
        d_every[s, c, home] = (picked * score[slots(s), :]).astype(BF)
        moves[s] = spread(d_every, s, group + s)
        light_back(r)
        if s > 0:
            for e in (0, 1):

                def more_slopes(r, s=s, e=e):
                    value, slope = gelu_parts(up_h[s, e, r, :fh])
                    up_h[s, e, r, :fh] = up_h[s, e, r, fh:] * slope
                    up_h[s, e, r, fh:] = value

                tiles(block, 128, more_slopes)

    def heavy_back(s, e):
        dz = dot_back(d_every[s, e].reshape(block, D), w_hdn[...])
        dup_h[s, e, :, :fh] = (dz * up_h[s, e, :, :fh]).astype(BF)
        dup_h[s, e, :, fh:] = (dz * up_h[s, e, :, fh:]).astype(BF)
        v = dot_back(dup_h[s, e], w_hin[...]).astype(BF)
        part[s, e] = v.reshape(4, cap, D)

    for s in seqs:
        relay(d_every, s, group + s, *moves[s])
        dhn[span(s), :] = dot_back(dup_l[span(s), :], w_in[...])
    for s in seqs:
        for copy in moves[s][1]:
            copy.wait()
        heavy_back(s, 1 - c)
        i = group + s
        second = send(part.at[s, 1 - c], near.at[i], es.at[i], er.at[i], partner)
        heavy_back(s, c)
        sums[s] = fold(s, i, second)
    count = group * 2 * block
    d_rows = d_every[...].reshape(count, D)
    g_line[...] = dot_grad(zh[...].reshape(count, fh), d_rows).astype(BF)
    g_view = g_line.reshape(nz, -1, D)
    hdn_back = [
        send(g_view.at[k], g_in_line.at[n], zs.at[1, n], zr.at[1, n], z_to[n])
        for n, k in enumerate(z_index)
    ]

    def light_grad(j):
        g_dn[j, :] = dot_grad(z[:, j], dl[...]).astype(BF)

    tiles(fl, 512, light_grad)
    flushed = [keep(g_dn, g_dn_hbm, moves_sem.at[4])]

    def light_in_grad(j):
        g_in[:, j] = dot_grad(hn[...], dup_l[:, j]).astype(BF)

    tiles(2 * fl, 1024, light_in_grad)
    flushed.append(keep(g_in, g_in_hbm, moves_sem.at[5]))
    every_rows = every[...].reshape(count, D)

    def heavy_grad(j):
        g_hin[:, j] = dot_grad(every_rows, dup_h[:, :, :, j].reshape(count, 512)).astype(BF)

    tiles(2 * fh, 512, heavy_grad)
    flushed.append(keep(g_hin, g_hin_hbm, moves_sem.at[6]))
    for s in seqs:
        r = span(s)
        high, low = halves(folded(s, group + s, sums[s]))
        d = dhn[r, :] + (dot(select_t[s], high) + dot(select_t[s], low))
        h = hidden[r, :]
        inv = lax.rsqrt(jnp.mean(h * h, axis=-1, keepdims=True) + EPSILON)
        dh = d * h
        stats[0:1, :] += jnp.sum(dh * inv, axis=0, keepdims=True)
        mean = jnp.mean(gain[1:2, :] * dh, axis=-1, keepdims=True)
        d_hidden[r, :] = out[r, :] + inv * gain[1:2, :] * d - h * (inv * inv * inv * mean)
    for copy in hdn_back + flushed:
        copy.wait()
    value = g_view[hi].astype(F32)
    for n in range(nz - 1):
        value += g_in_line[n].astype(F32)
    hdn_o[...] = value


def feed_forward(nz, hidden, select, select_t, score, gain, teach, mask, scale, w_in, w_dn, w_hin, hdn):
    tokens = hidden.shape[0]
    group, cap, _ = select.shape
    fl, fh = w_dn.shape[0], w_hin.shape[1] // 2
    block = (group, 2, 4, cap, D)
    line = (nz,) + hdn.shape
    operands = [hidden, select, select_t, score, gain, teach, mask, scale, w_in, w_dn, w_hin, hdn]
    return call(
        functools.partial(ffn_kernel, nz),
        [
            jax.ShapeDtypeStruct((D, 2 * fl), BF),
            jax.ShapeDtypeStruct((fl, D), BF),
            jax.ShapeDtypeStruct((D, 2 * fh), BF),
            jax.ShapeDtypeStruct(hdn.shape, F32),
            jax.ShapeDtypeStruct((tokens, D), F32),
            jax.ShapeDtypeStruct((8, D), F32),
        ],
        operands,
        [VM] * 5 + [ANY] + [VM] * 2 + [ANY] * 4,
        [ANY] * 3 + [VM] * 3,
        [
            pltpu.VMEM((tokens, D), BF),
            pltpu.VMEM((D, 2 * fl), BF),
            pltpu.VMEM((fl, D), BF),
            pltpu.VMEM((D, 2 * fh), BF),
            pltpu.VMEM((D, 2 * fl), BF),
            pltpu.VMEM((fl, D), BF),
            pltpu.VMEM((D, 2 * fh), BF),
            DMA((7,)),
            pltpu.VMEM(line, BF),
            pltpu.VMEM((fh, D), BF),
            pltpu.VMEM((nz - 1,) + hdn.shape, BF),
            pltpu.VMEM((tokens, D), BF),
            pltpu.VMEM(block, BF),
            pltpu.VMEM(block, BF),
            pltpu.VMEM((tokens, 2 * fl), F32),
            pltpu.VMEM((tokens, fl), BF),
            pltpu.VMEM((group, 2, 4 * cap, 2 * fh), F32),
            pltpu.VMEM((group, 2, 4 * cap, fh), BF),
            pltpu.VMEM(block, BF),
            pltpu.VMEM((2 * group, 4, cap, D), BF),
            pltpu.VMEM((2 * group, 3, cap, D), BF),
            pltpu.VMEM((tokens, D), F32),
            pltpu.VMEM((tokens, D), BF),
            pltpu.VMEM((tokens, 2 * fl), BF),
            pltpu.VMEM((group, 2, 4 * cap, 2 * fh), BF),
            pltpu.VMEM((tokens, D), F32),
            DMA((2 * group, 3)),
            DMA((2 * group, 3)),
            DMA((2 * group, 4)),
            DMA((2 * group, 4)),
            DMA((2 * group, 3)),
            DMA((2 * group, 3)),
            DMA((2 * group,)),
            DMA((2 * group,)),
            DMA((2, nz)),
            DMA((2, nz)),
            DMA,
        ],
        5,
    )


def pair_masks(scale):
    lane = lax.broadcasted_iota(jnp.int32, (1, 2 * DH), 1)
    left = jnp.where(lane < DH, scale, 0.0).astype(BF)
    right = jnp.where(lane < DH, 0.0, scale).astype(BF)
    return left, right


def both(value, masks):
    return jnp.concatenate([value * masks[0], value * masks[1]], axis=0)


def side(stacked):
    rows = stacked.shape[0] // 2
    return jnp.concatenate([stacked[:rows], stacked[rows:]], axis=1)


def pair_forward(q, k, v, bias, ones, scaled):
    scores = dot_back(both(q, scaled), k) + bias
    top = jnp.max(scores, axis=-1, keepdims=True)
    shifted = jnp.exp(scores - top)
    total = jnp.sum(shifted, axis=-1, keepdims=True)
    prob = (shifted / total).astype(BF)
    return dot(side(prob), both(v, ones)).astype(BF), top + jnp.log(total)


def pair_backward(q, k, v, bias, lse, d_out, ones, scaled):
    q2 = both(q, scaled)
    d2 = both(d_out, ones)
    prob = jnp.exp(dot_back(q2, k) + bias - lse)
    d_prob = dot_back(d2, v)
    row = jnp.sum(prob * d_prob, axis=-1, keepdims=True)
    d_scores = (prob * (d_prob - row)).astype(BF)
    dq = dot(side(d_scores), both(k, scaled))
    return dq, dot_grad(d_scores, q2), dot_grad(prob.astype(BF), d2)


def reach_bias(key_bias):
    shape = (WIN, 3 * WIN)
    offset = lax.broadcasted_iota(jnp.int32, shape, 1) - lax.broadcasted_iota(jnp.int32, shape, 0) - WIN
    near = (offset >= -WIN) & (offset <= WIN)
    inner = jnp.where(offset == 0, 0.0, jnp.broadcast_to(key_bias, shape))
    bias = jnp.where(near, inner, MASKED)
    return jnp.concatenate([bias, bias], axis=0)


def put_lse(lse, pair, column):
    lane = lax.broadcasted_iota(jnp.int32, lse.shape, 1)
    rows = lse.shape[0]
    lse = jnp.where(lane == 2 * pair, column[:rows], lse)
    return jnp.where(lane == 2 * pair + 1, column[rows:], lse)


def get_lse(lse, pair):
    return jnp.concatenate([lse[:, 2 * pair : 2 * pair + 1], lse[:, 2 * pair + 1 : 2 * pair + 2]], axis=0)


def attend_body(
    stages,
    x,
    gain,
    select,
    select_t,
    key_bias,
    heavy_bias,
    w_lqkv,
    w_hqkv,
    w_lout,
    w_hout,
    hidden,
    xn,
    lq,
    rim,
    lo_out,
    l_lse,
    a_rows,
    hq,
    kvh,
    ho,
    h_lse,
    ls,
    lr,
    rs,
    rr,
    ss,
    sr,
):
    hi, lo, x_, c = place()
    f = x_ * 2 + c
    tokens = x.shape[0]
    group, cap, width = select.shape
    wl, wh = HL * DH, HH * DH
    ones, scaled = pair_masks(1.0), pair_masks(SCORE_SCALE)
    across, partner = at(hi, lo, 1 - x_, c), at(hi, lo, x_, 1 - c)

    def norm(r):
        h = x[r, :].astype(F32)
        inv = lax.rsqrt(jnp.mean(h * h, axis=-1, keepdims=True) + EPSILON)
        xn[r, :] = (h * inv * gain[0:1, :]).astype(BF)

    tiles(tokens, 128, norm)
    for s in range(group):
        rows = dot(select[s], xn[s * width : (s + 1) * width, :]).astype(BF)
        a_rows[s * cap : (s + 1) * cap, :] = rows
    stages[0]()
    kv = dot(a_rows[...], w_hqkv[:, wh:]).astype(BF)
    for s in range(group):
        kvh[s, f] = kv[s * cap : (s + 1) * cap]
    mine = kvh.at[:, f]
    first = send(mine, mine, ss.at[0], sr.at[0], across)
    beside = send(mine, mine, ss.at[1], sr.at[1], partner)
    stages[1]()
    for s in range(group):
        rows = xn[s * width : (s + 1) * width, :]
        rim[s, WIN : WIN + width, :] = dot(rows, w_lqkv[:, wl:]).astype(BF)
    finish = rim_exchange(
        rim.at[:, pl.ds(WIN, WIN)],
        rim.at[:, pl.ds(width, WIN)],
        rim.at[:, pl.ds(0, WIN)],
        rim.at[:, pl.ds(width + WIN, WIN)],
        ls,
        lr,
        rs,
        rr,
    )
    hq[...] = dot(a_rows[...], w_hqkv[:, :wh]).astype(BF)
    for s in range(group):
        rows = slice(s * width, (s + 1) * width)
        lq[rows, :] = dot(xn[rows, :], w_lqkv[:, :wl]).astype(BF)
    stages[2]()
    first.wait()
    other = kvh.at[:, (1 - x_) * 2 + c]
    relay = send(other, other, ss.at[2], sr.at[2], partner)
    finish()
    stages[3]()
    blocks = width // WIN

    def light(i, carry):
        s, b = i // blocks, i % blocks
        r = pl.ds(pl.multiple_of(i * WIN, WIN), WIN)
        keys = pl.ds(pl.multiple_of(b * WIN, WIN), 3 * WIN)
        bias = reach_bias(key_bias[i])
        lse = jnp.zeros((WIN, 128), F32)
        for pair in range(HL // 2):
            at_k = slice(pair * 128, (pair + 1) * 128)
            at_v = slice(wl + pair * 128, wl + (pair + 1) * 128)
            o, column = pair_forward(
                lq[r, at_k], rim[s, keys, at_k], rim[s, keys, at_v], bias, ones, scaled
            )
            lo_out[r, at_k] = o
            lse = put_lse(lse, pair, column)
        l_lse[r, :] = lse
        return carry

    lax.fori_loop(0, group * blocks // 2, light, 0)
    stages[4]()
    lax.fori_loop(group * blocks // 2, group * blocks, light, 0)
    stages[5]()
    beside.wait()
    relay.wait()
    heavy_kv = kvh.reshape(group, 4 * cap, 2 * wh)

    def heavy(s, carry):
        r = pl.ds(pl.multiple_of(s * cap, cap), cap)
        bias = heavy_bias[s]
        bias = jnp.concatenate([bias, bias], axis=0)
        lse = jnp.zeros((cap, 128), F32)
        for pair in range(HH // 2):
            at_k = slice(pair * 128, (pair + 1) * 128)
            at_v = slice(wh + pair * 128, wh + (pair + 1) * 128)
            o, column = pair_forward(
                hq[r, at_k], heavy_kv[s, :, at_k], heavy_kv[s, :, at_v], bias, ones, scaled
            )
            ho[r, at_k] = o
            lse = put_lse(lse, pair, column)
        h_lse[r, :] = lse
        return carry

    lax.fori_loop(0, group, heavy, 0)
    stages[6]()
    high, low = halves(dot(ho[...], w_hout[...]))
    for s in range(group):
        r = slice(s * width, (s + 1) * width)
        q = slice(s * cap, (s + 1) * cap)
        hidden[r, :] = (
            x[r, :].astype(F32)
            + dot(lo_out[r, :], w_lout[...])
            + (dot(select_t[s], high[q]) + dot(select_t[s], low[q]))
        )


def attend_kernel(*refs):
    meet(line_peers())
    attend_body([lambda: None] * 7, *refs)


def attend_shapes(tokens, select):
    group, cap, width = select.shape
    wl, wh = HL * DH, HH * DH
    rows = group * cap
    return [
        jax.ShapeDtypeStruct((tokens, D), F32),
        jax.ShapeDtypeStruct((tokens, D), BF),
        jax.ShapeDtypeStruct((tokens, wl), BF),
        jax.ShapeDtypeStruct((group, width + 2 * WIN, 2 * wl), BF),
        jax.ShapeDtypeStruct((tokens, wl), BF),
        jax.ShapeDtypeStruct((tokens, 128), F32),
        jax.ShapeDtypeStruct((rows, D), BF),
        jax.ShapeDtypeStruct((rows, wh), BF),
        jax.ShapeDtypeStruct((group, 4, cap, 2 * wh), BF),
        jax.ShapeDtypeStruct((rows, wh), BF),
        jax.ShapeDtypeStruct((rows, 128), F32),
    ]


ATTEND_SEMS = [DMA, DMA, DMA, DMA, DMA((3,)), DMA((3,))]


def attend(x, gain, select, select_t, key_bias, heavy_bias, w_lqkv, w_hqkv, w_lout, w_hout):
    operands = [x, gain, select, select_t, key_bias, heavy_bias, w_lqkv, w_hqkv, w_lout, w_hout]
    shapes = attend_shapes(x.shape[0], select)
    return call(
        attend_kernel,
        shapes,
        operands,
        [VM] * len(operands),
        [VM] * len(shapes),
        ATTEND_SEMS,
        2,
    )


def route_part(deal, lengths, routes_a, routes_f, scores, tables):
    sel_a, selt_a, key_bias, heavy_bias, sel_f, selt_f, score, mask, scale = tables
    hi, lo, x, c = place()
    group, cap, width = sel_a.shape
    seqs = deal.shape[1]
    here = ((x * 2 + c) * width).astype(F32)

    def line(shape, dim):
        return lax.broadcasted_iota(jnp.int32, shape, dim).astype(F32)

    lane = lax.broadcasted_iota(jnp.int32, (1, seqs), 1)
    before = jnp.where(line((width, width), 0) > line((width, width), 1), 1.0, 0.0).astype(BF)
    length_row = lengths[...].astype(F32)
    count = jnp.sum(length_row, axis=1, keepdims=True)
    column = line((width, 1), 0)
    row = line((1, width), 1)
    ones = jnp.ones((8, routes_a.shape[1]), BF)

    def columns_of(routes, base):
        held = jnp.where(routes == column + base, 1.0, 0.0)
        rank = jnp.sum(dot(before, held.astype(BF)), axis=1, keepdims=True)
        there = jnp.sum(held, axis=1, keepdims=True)
        hot_t = jnp.where(rank == line((width, cap), 1), 1.0, 0.0) * there
        return held, rank, hot_t

    def rows_of(held):
        there = dot_back(ones, held.astype(BF))
        rank = dot_back(there.astype(BF), before)
        return jnp.where(rank[:1] == line((cap, width), 0), 1.0, 0.0) * there[:1]

    for s in range(group):
        place_here = lane == (hi * 2 + lo) * group + s
        which = jnp.sum(jnp.where(place_here, deal[...].astype(F32), 0.0), axis=1, keepdims=True)
        one = line((seqs, 1), 0) == which
        length = jnp.sum(
            jnp.where(line((1, seqs), 1) == which, length_row, 0.0), axis=1, keepdims=True
        )
        ra, rf, sf = (
            jnp.sum(jnp.where(one, ref[...].astype(F32), 0.0), axis=0, keepdims=True)
            for ref in (routes_a, routes_f, scores)
        )
        held, rank, hot_t = columns_of(ra, here)
        hot = rows_of(held)
        sel_a[s] = hot.astype(BF)
        selt_a[s] = hot_t.astype(BF)
        own_spot = jnp.sum(hot * (row + here + 1.0), axis=1, keepdims=True) - 1.0
        for q in range(4):
            base = float(q * width)
            _, _, other_t = columns_of(ra, base)
            spot = jnp.sum(other_t * (column + base + 1.0), axis=0, keepdims=True) - 1.0
            live = jnp.where((spot >= 0.0) & (spot < length), 1.0, 0.0)
            same = jnp.where(own_spot == spot, 1.0, 0.0)
            heavy_bias[s, :, q * cap : (q + 1) * cap] = jnp.where(live + same > 0.0, 0.0, MASKED)
        for b in range(width // WIN):
            key = line((1, 3 * WIN), 1) + (here + float((b - 1) * WIN))
            live = (key >= 0.0) & (key < length)
            key_bias[s * (width // WIN) + b] = jnp.where(live, 0.0, MASKED)
        valid = jnp.where(column + here < length, 1.0, 0.0)
        mask[s * width : (s + 1) * width, :] = valid
        scale[s * width : (s + 1) * width, :] = 2.0 * valid / (D * count)
        held, rank, hot_t = columns_of(rf, here)
        sel_f[s] = rows_of(held).astype(BF)
        selt_f[s] = hot_t.astype(BF)
        slot = jnp.sum(held * rank, axis=0, keepdims=True)
        owned = jnp.sum(held, axis=0, keepdims=True)
        hits = jnp.where(slot == line((cap, slot.shape[1]), 0), 1.0, 0.0)
        score[s * cap : (s + 1) * cap, :] = jnp.sum(hits * (owned * sf), axis=1, keepdims=True)


def route_shapes(group, width, tokens):
    return [
        jax.ShapeDtypeStruct((group, CAP, width), BF),
        jax.ShapeDtypeStruct((group, width, CAP), BF),
        jax.ShapeDtypeStruct((tokens // WIN, 1, 3 * WIN), F32),
        jax.ShapeDtypeStruct((group, CAP, 4 * CAP), F32),
        jax.ShapeDtypeStruct((group, CAP, width), BF),
        jax.ShapeDtypeStruct((group, width, CAP), BF),
        jax.ShapeDtypeStruct((group * CAP, 1), F32),
        jax.ShapeDtypeStruct((tokens, 1), F32),
        jax.ShapeDtypeStruct((tokens, 1), F32),
    ]


def gather_attend_kernel(dp, nw, *refs):
    n_in, n_out = 7 + nw, 2 + nw + 21
    ins, outs, rest = refs[:n_in], list(refs[n_in : n_in + n_out]), refs[n_in + n_out :]
    count = len(STAGED)
    held, flush_sem, rest = rest[:count], rest[count], rest[count + 1 :]
    final = [outs[k] for k in STAGED]
    for k, ref in zip(STAGED, held):
        outs[k] = ref
    flushed = []

    def flush(*which):
        for k in which:
            n = STAGED.index(k)
            flushed.append(keep(held[n], final[n], flush_sem.at[n]))

    xin, ws, hin = ins[0], ins[1 : 1 + nw], ins[1 + nw]
    integers = ins[2 + nw :]
    xo, wos, hin_o = outs[0], outs[1 : 1 + nw], outs[1 + nw]
    gain, tables, saved = outs[2 + nw], outs[3 + nw : 12 + nw], outs[12 + nw :]
    parts, rest = rest[: 3 * nw + 3], rest[3 * nw + 3 :]
    halves = (parts[:nw], parts[nw : 2 * nw], parts[2 * nw : 3 * nw], parts[3 * nw :])
    g = Gather(dp, xin, ws, hin, xo, wos, hin_o, rest[:11], halves)
    g.meet()
    for w in range(nw):
        g.swap(w)
    g.join(0)
    g.join(2)
    g.plane(0)
    g.plane(2)
    g.join(1)
    g.rows()
    route_part(*integers, tables)
    g.cross(0)
    g.cross(2)
    g.core(0)
    g.plane(1)
    g.core(2)
    g.ready(0)
    total = jnp.zeros(gain.shape, F32)
    for z in range(dp // 2):
        for l2, x2 in ((0, 0), (0, 1), (1, 0), (1, 1)):
            pair = wos[0][z, l2, x2].astype(F32)
            total += pair[:8] + pair[8:]
    gain[...] = total
    g.rows_ready()
    for w in (4, 3, 5, 6):
        g.join(w)
    g.heavy_plane()
    flush(0)

    def heavy_projection():
        g.cross(1)
        g.ready(2)
        flush(20, 3)

    def light_projection():
        g.core(1)
        g.ready(1)
        flush(2)

    def keys_travel():
        g.plane(4)
        g.plane(3)
        flush(21)

    def keys_there():
        g.plane(5)
        g.plane(6)
        g.heavy_line()
        flush(22)

    def half_way():
        g.cross(4)
        g.cross(3)

    def light_done():
        g.core(4)
        g.core(3)
        flush(23)

    def heavy_done():
        g.cross(5)
        g.cross(6)
        g.ready(4)
        g.ready(3)
        flush(27, 4, 5)

    full = [wos[w].reshape(-1, wos[w].shape[-1]) for w in range(nw)]
    stages = [
        heavy_projection,
        light_projection,
        keys_travel,
        keys_there,
        half_way,
        light_done,
        heavy_done,
    ]
    attend_body(
        stages,
        xo.reshape(-1, D),
        gain,
        *tables[:4],
        full[1],
        full[2],
        full[3],
        full[4],
        *saved,
        *rest[11:],
    )
    g.core(5)
    g.core(6)
    g.ready(5)
    g.ready(6)
    g.heavy_ready()
    for copy in flushed:
        copy.wait()


STAGED = (0, 2, 3, 4, 5, 20, 21, 22, 23, 27)


def gather_attend(dp, xin, weights, hin, integers):
    nw = len(weights)
    shapes = gather_shapes(dp, xin, weights, hin, True)
    group, width = shapes[0].shape[0], dp * xin.shape[1]
    tables = route_shapes(group, width, group * width)
    shapes.append(jax.ShapeDtypeStruct((8, D), F32))
    shapes += tables
    shapes += attend_shapes(group * width, tables[0])
    return call(
        functools.partial(gather_attend_kernel, dp, nw),
        shapes,
        [xin, *weights, hin, *integers],
        [ANY] * (2 + nw) + [VM] * 5,
        [ANY if k in STAGED + (6, 7, 8) else VM for k in range(len(shapes))],
        [pltpu.VMEM(shapes[k].shape, BF) for k in STAGED]
        + [DMA((len(STAGED),))]
        + [pltpu.VMEM((w.shape[0], w.shape[1] // 2), BF) for w in weights] * 2
        + [pltpu.VMEM((2 * w.shape[0], w.shape[1] // 2), BF) for w in weights]
        + [DMA((nw,))] * 3
        + gather_sems(dp, nw)
        + ATTEND_SEMS,
        1,
    )


def attend_back_body(
    stages,
    d_hidden,
    x,
    gain,
    select,
    select_t,
    key_bias,
    heavy_bias,
    w_lqkv,
    w_hqkv,
    w_lout,
    w_hout,
    xn,
    lq,
    rim,
    lo_out,
    l_lse,
    a_rows,
    hq,
    kvh,
    ho,
    h_lse,
    g_lqkv,
    g_hqkv,
    g_lout,
    g_hout,
    dx,
    stats,
    d_ho,
    d_hproj,
    part,
    got,
    far,
    d_la,
    d_lo,
    d_rim,
    edge,
    edge_in,
    d_lproj,
    ls,
    lr,
    rs,
    rr,
    ss,
    sr,
):
    hi, lo, x_, c = place()
    tokens = x.shape[0]
    group, cap, width = select.shape
    wl, wh = HL * DH, HH * DH
    ones, scaled = pair_masks(1.0), pair_masks(SCORE_SCALE)
    across, partner = at(hi, lo, 1 - x_, c), at(hi, lo, x_, 1 - c)
    picked = []
    for s in range(group):
        high, low = halves(d_hidden[s * width : (s + 1) * width, :])
        picked.append((dot(select[s], high) + dot(select[s], low)).astype(BF))
    d_ha = jnp.concatenate(picked, axis=0)
    d_ho[...] = dot_back(d_ha, w_hout[...]).astype(BF)
    heavy_kv = kvh.reshape(group, 4 * cap, 2 * wh)
    part_kv = part.reshape(group, 4 * cap, 2 * wh)

    def heavy(s, carry):
        r = pl.ds(pl.multiple_of(s * cap, cap), cap)
        bias = heavy_bias[s]
        bias = jnp.concatenate([bias, bias], axis=0)
        lse = h_lse[r, :]
        for pair in range(HH // 2):
            at_k = slice(pair * 128, (pair + 1) * 128)
            at_v = slice(wh + pair * 128, wh + (pair + 1) * 128)
            dq, dk, dv = pair_backward(
                hq[r, at_k],
                heavy_kv[s, :, at_k],
                heavy_kv[s, :, at_v],
                bias,
                get_lse(lse, pair),
                d_ho[r, at_k],
                ones,
                scaled,
            )
            d_hproj[r, at_k] = dq.astype(BF)
            part_kv[s, :, at_k] = dk.astype(BF)
            part_kv[s, :, at_v] = dv.astype(BF)
        return carry

    lax.fori_loop(0, group, heavy, 0)
    beside = [
        send(part.at[:, b * 2 + 1 - c], got.at[b], ss.at[b], sr.at[b], partner) for b in (0, 1)
    ]
    g_hout[...] = dot_grad(ho[...], d_ha).astype(BF)
    stages[0]()

    def light_out_back(r):
        d = d_hidden[r, :].astype(BF)
        d_la[r, :] = d
        d_lo[r, :] = dot_back(d, w_lout[...]).astype(BF)

    tiles(tokens, 256, light_out_back)
    g_lout[...] = dot_grad(lo_out[...], d_la[...]).astype(BF)
    stages[1]()
    for copy in beside:
        copy.wait()
    for b in (0, 1):
        got[b] = (got[b].astype(F32) + part[:, b * 2 + c].astype(F32)).astype(BF)
    third = send(got.at[1 - x_], far, ss.at[2], sr.at[2], across)
    stages[2]()
    d_rim[...] = jnp.zeros(d_rim.shape, F32)
    blocks = width // WIN

    def light(i, carry):
        s, b = i // blocks, i % blocks
        r = pl.ds(pl.multiple_of(i * WIN, WIN), WIN)
        keys = pl.ds(pl.multiple_of(b * WIN, WIN), 3 * WIN)
        bias = reach_bias(key_bias[i])
        lse = l_lse[r, :]
        for pair in range(HL // 2):
            at_k = slice(pair * 128, (pair + 1) * 128)
            at_v = slice(wl + pair * 128, wl + (pair + 1) * 128)
            dq, dk, dv = pair_backward(
                lq[r, at_k],
                rim[s, keys, at_k],
                rim[s, keys, at_v],
                bias,
                get_lse(lse, pair),
                d_lo[r, at_k],
                ones,
                scaled,
            )
            d_lproj[r, at_k] = dq.astype(BF)
            d_rim[s, keys, at_k] += dk
            d_rim[s, keys, at_v] += dv
        return carry

    lax.fori_loop(0, group * blocks // 2, light, 0)
    third.wait()
    total = (got[x_].astype(F32) + far[...].astype(F32)).astype(BF)
    for s in range(group):
        d_hproj[s * cap : (s + 1) * cap, wh:] = total[s]

    def heavy_grad(j):
        g_hqkv[:, j] = dot_grad(a_rows[...], d_hproj[:, j]).astype(BF)

    tiles(3 * wh, 768, heavy_grad)
    stages[3]()
    lax.fori_loop(group * blocks // 2, group * blocks, light, 0)
    edge[0] = d_rim[:, :WIN, :].astype(BF)
    edge[1] = d_rim[:, WIN + width :, :].astype(BF)
    finish = rim_exchange(
        edge.at[0], edge.at[1], edge_in.at[0], edge_in.at[1], ls, lr, rs, rr
    )
    stages[4]()
    d_high, d_low = halves(dot_back(d_hproj[...], w_hqkv[...]))
    finish()
    for s in range(group):
        d_rim[s, WIN : 2 * WIN, :] += edge_in[0, s].astype(F32)
        d_rim[s, width : width + WIN, :] += edge_in[1, s].astype(F32)
        d_lproj[s * width : (s + 1) * width, wl:] = d_rim[s, WIN : WIN + width, :].astype(BF)

    def light_grad(j):
        g_lqkv[:, j] = dot_grad(xn[...], d_lproj[:, j]).astype(BF)

    tiles(3 * wl, 768, light_grad)
    stages[5]()
    stats[...] = jnp.zeros(stats.shape, F32)
    for s in range(group):
        r = slice(s * width, (s + 1) * width)
        q = slice(s * cap, (s + 1) * cap)
        d = dot_back(d_lproj[r, :], w_lqkv[...]) + (
            dot(select_t[s], d_high[q]) + dot(select_t[s], d_low[q])
        )
        h = x[r, :].astype(F32)
        inv = lax.rsqrt(jnp.mean(h * h, axis=-1, keepdims=True) + EPSILON)
        dh = d * h
        stats[0:1, :] += jnp.sum(dh * inv, axis=0, keepdims=True)
        mean = jnp.mean(gain[0:1, :] * dh, axis=-1, keepdims=True)
        dx[r, :] = (
            d_hidden[r, :] + inv * gain[0:1, :] * d - h * (inv * inv * inv * mean)
        ).astype(BF)
    stages[6]()


def attend_back_kernel(*refs):
    meet(line_peers())
    attend_back_body([lambda: None] * 7, *refs)


def attend_back_scratch(tokens, select):
    group, cap, width = select.shape
    wl, wh = HL * DH, HH * DH
    rows = group * cap
    return [
        pltpu.VMEM((rows, wh), BF),
        pltpu.VMEM((rows, 3 * wh), BF),
        pltpu.VMEM((group, 4, cap, 2 * wh), BF),
        pltpu.VMEM((2, group, cap, 2 * wh), BF),
        pltpu.VMEM((group, cap, 2 * wh), BF),
        pltpu.VMEM((tokens, D), BF),
        pltpu.VMEM((tokens, wl), BF),
        pltpu.VMEM((group, width + 2 * WIN, 2 * wl), F32),
        pltpu.VMEM((2, group, WIN, 2 * wl), BF),
        pltpu.VMEM((2, group, WIN, 2 * wl), BF),
        pltpu.VMEM((tokens, 3 * wl), BF),
    ] + ATTEND_SEMS


def attend_back(d_hidden, x, gain, select, select_t, key_bias, heavy_bias, weights, saved):
    tokens = x.shape[0]
    wl, wh = HL * DH, HH * DH
    operands = [d_hidden, x, gain, select, select_t, key_bias, heavy_bias, *weights, *saved]
    shapes = [
        jax.ShapeDtypeStruct((D, 3 * wl), BF),
        jax.ShapeDtypeStruct((D, 3 * wh), BF),
        jax.ShapeDtypeStruct((wl, D), BF),
        jax.ShapeDtypeStruct((wh, D), BF),
        jax.ShapeDtypeStruct((tokens, D), BF),
        jax.ShapeDtypeStruct((8, D), F32),
    ]
    return call(
        attend_back_kernel,
        shapes,
        operands,
        [VM] * len(operands),
        [VM] * len(shapes),
        attend_back_scratch(tokens, select),
        3,
    )


def scatter_kernel(dp, nw, *refs):
    nz = dp // 2
    dx, stats, gs, hin = refs[0], refs[1], refs[2 : 2 + nw], refs[2 + nw]
    outs = refs[3 + nw :]
    dxo, total, gos, hin_o = outs[0], outs[1], outs[2 : 2 + nw], outs[2 + nw]
    scr = outs[3 + nw :]
    nears, fars, sums, ends = (scr[i * nw : (i + 1) * nw] for i in range(4))
    hin_r, hin_s, sc, sp, sz, acc, acc2 = scr[4 * nw : 4 * nw + 7]
    own, xs, xr, cs, cr, ps, pr, zs, zr, hs, hr, ts, tr = scr[4 * nw + 7 :]
    hi, lo, x, c = place()
    d = hi * 2 + lo
    f = x * 2 + c
    plane = (lo * 2 + x) * 2 + c
    dp_peers = [(lax.rem(d + k, dp), f) for k in range(1, dp)]
    rest = [(a, b, e) for a in (0, 1) for b in (0, 1) for e in (0, 1) if a or b or e]
    flat8 = []
    for a, b, e in rest:
        l2 = 1 - lo if a else lo
        x2 = 1 - x if b else x
        c2 = 1 - c if e else c
        flat8.append((l2, x2, c2))
    meet(dp_peers + [at(hi, *p) for (a, b, e), p in zip(rest, flat8) if b or e])
    partner = at(hi, lo, x, 1 - c)
    quad = quad_peers()
    z_index = [lax.rem(hi + k, nz) for k in range(1, nz)]
    z_peers = [at(z, lo, x, c) for z in z_index]
    c_sends = [
        send(gs[w].at[:, :, :, 1 - c], nears[w], cs.at[w], cr.at[w], partner) for w in range(nw)
    ]
    t_c = send(stats, sc, ts.at[0], tr.at[0], partner)
    mine = keep(dx.at[:, d], dxo.at[d], own)
    x_sends = [
        send(dx.at[:, peer[0]], dxo.at[d], xs.at[k], xr.at[k], peer)
        for k, peer in enumerate(dp_peers)
    ]
    h_sends = []
    for k, z in enumerate(z_index):
        h_sends.append(send(hin.at[z], hin_r.at[k], hs.at[1, k], hr.at[1, k], z_peers[k]))
    p_sends, z_sends = [], []
    t_c.wait()
    acc[...] = stats[...] + sc[...]
    t_p = [
        send(acc, sp.at[k], ts.at[1 + k], tr.at[1 + k], at(hi, l2, x2, c))
        for k, (l2, x2) in enumerate(quad)
    ]

    def add_core(w):
        c_sends[w].wait()
        near, g = nears[w], gs[w]

        def body(i, carry):
            z, a, b = i // 4, (i // 2) % 2, i % 2
            near[z, a, b] = (near[z, a, b].astype(F32) + g[z, a, b, c].astype(F32)).astype(BF)
            return carry

        lax.fori_loop(0, nz * 4, body, 0)
        p_sends.append(
            [
                send(near.at[:, l2, x2], fars[w].at[k], ps.at[w, k], pr.at[w, k], at(hi, l2, x2, c))
                for k, (l2, x2) in enumerate(quad)
            ]
        )

    def add_plane(w):
        for copy in p_sends[w]:
            copy.wait()
        near, far, part = nears[w], fars[w], sums[w]

        def body(z, carry):
            part[z] = (
                near[z, lo, x].astype(F32)
                + far[0, z].astype(F32)
                + far[1, z].astype(F32)
                + far[2, z].astype(F32)
            ).astype(BF)
            return carry

        lax.fori_loop(0, nz, body, 0)
        z_sends.append(
            [
                send(part.at[z], ends[w].at[k], zs.at[w, k], zr.at[w, k], z_peers[k])
                for k, z in enumerate(z_index)
            ]
        )

    def add_line(w):
        for copy in z_sends[w]:
            copy.wait()
        gos[w][...] = sums[w][hi].astype(F32)
        for k in range(nz - 1):
            gos[w][...] += ends[w][k].astype(F32)

    for w in range(nw):
        add_core(w)
        if w >= 2:
            add_plane(w - 2)
    for copy in t_p:
        copy.wait()
    acc2[...] = acc[...] + sp[0] + sp[1] + sp[2]
    t_z = [send(acc2, sz.at[k], ts.at[4 + k], tr.at[4 + k], z_peers[k]) for k in range(nz - 1)]
    for copy in h_sends:
        copy.wait()

    def body(i, carry):
        value = hin[hi, i].astype(F32)
        for k in range(nz - 1):
            value += hin_r[k, i].astype(F32)
        hin_s[i] = value.astype(BF)
        return carry

    lax.fori_loop(0, 8, body, 0)
    hin_o[plane] = hin_s[plane]
    a_sends = [
        send(
            hin_s.at[(l2 * 2 + x2) * 2 + c2],
            hin_o.at[plane],
            hs.at[0, k],
            hr.at[0, k],
            at(hi, l2, x2, c2),
        )
        for k, (l2, x2, c2) in enumerate(flat8)
    ]
    for w in range(max(nw - 2, 0), nw):
        add_plane(w)
    for copy in t_z:
        copy.wait()
    total[...] = acc2[...]
    for k in range(nz - 1):
        total[...] += sz[k]
    for w in range(nw):
        add_line(w)
    mine.wait()
    for copy in x_sends + a_sends:
        copy.wait()


def scatter_all(dp, dx, stats, grads, hin):
    nz = dp // 2
    nw = len(grads)
    group, _, rows, _ = dx.shape
    tiles = [g.shape[4:] for g in grads]
    most = max(7, nz)
    scratch = [pltpu.VMEM((nz, 2, 2) + t, BF) for t in tiles]
    scratch += [pltpu.VMEM((3, nz) + t, BF) for t in tiles]
    scratch += [pltpu.VMEM((nz,) + t, BF) for t in tiles]
    scratch += [pltpu.VMEM((nz - 1,) + t, BF) for t in tiles]
    scratch += [
        pltpu.VMEM((nz - 1,) + hin.shape[1:], BF),
        pltpu.VMEM(hin.shape[1:], BF),
        pltpu.VMEM(stats.shape, F32),
        pltpu.VMEM((3,) + stats.shape, F32),
        pltpu.VMEM((nz - 1,) + stats.shape, F32),
        pltpu.VMEM(stats.shape, F32),
        pltpu.VMEM(stats.shape, F32),
        DMA,
        DMA((dp,)),
        DMA((dp,)),
        DMA((nw,)),
        DMA((nw,)),
        DMA((nw, 3)),
        DMA((nw, 3)),
        DMA((nw, nz)),
        DMA((nw, nz)),
        DMA((3, most)),
        DMA((3, most)),
        DMA((4 + nz,)),
        DMA((4 + nz,)),
    ]
    shapes = [jax.ShapeDtypeStruct((dp, group, rows, D), BF), jax.ShapeDtypeStruct(stats.shape, F32)]
    shapes += [jax.ShapeDtypeStruct(t, F32) for t in tiles]
    shapes.append(jax.ShapeDtypeStruct(hin.shape[1:], BF))
    return call(
        functools.partial(scatter_kernel, dp, nw),
        shapes,
        [dx, stats, *grads, hin],
        [ANY] + [VM] * (2 + nw),
        [ANY] + [VM] * (2 + nw),
        scratch,
        4,
    )


class Scatter:
    def __init__(self, nz, shards, gs, near, one, two, end, sems):
        self.nz, self.shards, self.gs = nz, shards, gs
        self.near, self.one, self.two, self.end = near, one, two, end
        self.cs, self.cr, self.ps, self.pr, self.zs, self.zr = sems
        self.hi, self.lo, self.x, self.c = hi, lo, x, c = place()
        self.partner = at(hi, lo, x, 1 - c)
        self.by_x, self.by_y = at(hi, lo, 1 - x, c), at(hi, 1 - lo, x, c)
        self.z_index = [lax.rem(hi + k, nz) for k in range(1, nz)]
        self.copies = {}

    def lanes(self, w, c):
        half = self.shards[w][1] // 2
        return pl.ds(pl.multiple_of(c * half, 128), half)

    def core(self, w):
        out = self.gs[w].at[:, :, :, :, self.lanes(w, 1 - self.c)]
        self.copies[w, 0] = [send(out, self.near[w], self.cs.at[w], self.cr.at[w], self.partner)]

    def wait(self, w, stage):
        for copy in self.copies[w, stage]:
            copy.wait()

    def plane(self, w):
        g, own = self.gs[w], self.lanes(w, self.c)
        self.add_plane(w, lambda z, a, b: g[z, a, b, :, own])

    def own_plane(self, w, kept):
        self.add_plane(w, lambda z, a, b: kept[z, a, b])

    def add_plane(self, w, own):
        self.wait(w, 0)
        near = self.near[w]
        lo, x, half = self.lo, self.x, self.nz // 2

        def body(i, carry):
            z, a, b = i // 4, (i // 2) % 2, i % 2
            near[z, a, b] = (near[z, a, b].astype(F32) + own(z, a, b).astype(F32)).astype(BF)
            return carry

        lax.fori_loop(0, self.nz * 4, body, 0)
        low, high = pl.ds(0, half), pl.ds(half, self.nz - half)
        self.copies[w, 1] = [
            send(near.at[low, :, 1 - x], self.one[w].at[low], self.ps.at[w, 0], self.pr.at[w, 0], self.by_x),
            send(near.at[high, 1 - lo], self.one[w].at[high], self.ps.at[w, 1], self.pr.at[w, 1], self.by_y),
        ]

    def cross(self, w):
        self.wait(w, 1)
        near, one, lo, x, half = self.near[w], self.one[w], self.lo, self.x, self.nz // 2

        def low_body(i, carry):
            z, a = i // 2, i % 2
            near[z, a, x] = (near[z, a, x].astype(F32) + one[z, a].astype(F32)).astype(BF)
            return carry

        def high_body(i, carry):
            z, b = half + i // 2, i % 2
            near[z, lo, b] = (near[z, lo, b].astype(F32) + one[z, b].astype(F32)).astype(BF)
            return carry

        lax.fori_loop(0, half * 2, low_body, 0)
        lax.fori_loop(0, (self.nz - half) * 2, high_body, 0)
        low, high = pl.ds(0, half), pl.ds(half, self.nz - half)
        two = self.two[w]
        self.copies[w, 2] = [
            send(near.at[low, 1 - lo, x], two.at[low], self.ps.at[w, 2], self.pr.at[w, 2], self.by_y),
            send(near.at[high, lo, 1 - x], two.at[high], self.ps.at[w, 3], self.pr.at[w, 3], self.by_x),
        ]

    def line(self, w):
        self.wait(w, 2)
        near, part, lo, x = self.near[w], self.two[w], self.lo, self.x

        def body(z, carry):
            part[z] = (near[z, lo, x].astype(F32) + part[z].astype(F32)).astype(BF)
            return carry

        lax.fori_loop(0, self.nz, body, 0)
        self.copies[w, 3] = [
            send(
                part.at[z],
                self.end[w].at[k],
                self.zs.at[w, k],
                self.zr.at[w, k],
                at(z, lo, x, self.c),
            )
            for k, z in enumerate(self.z_index)
        ]

    def last(self, w, fin, out, sems):
        self.wait(w, 3)
        value = self.two[w][self.hi].astype(F32)
        for k in range(self.nz - 1):
            value += self.end[w][k].astype(F32)
        fin[...] = value
        count = self.shards[w][0]
        own = pl.ds(pl.multiple_of(self.c * count, 8), count)
        mate = pl.ds(pl.multiple_of((1 - self.c) * count, 8), count)
        spot = out.at[:, self.lanes(w, self.c)]
        return [
            keep(fin.at[own], spot, sems[0].at[w]),
            send(fin.at[mate], spot, sems[1].at[w], sems[2].at[w], self.partner),
        ]


def back_scatter_kernel(dp, shards, *refs):
    nz, nw = dp // 2, len(shards)
    n_ops = 7 + 4 + 10
    ops, (g_lin, g_ldn, hin, ffn_stats) = refs[:n_ops], refs[n_ops : n_ops + 4]
    outs, rest = refs[n_ops + 4 : n_ops + 7 + nw], refs[n_ops + 7 + nw :]
    dxo, total, gos, hin_o = outs[0], outs[1], outs[2 : 2 + nw], outs[2 + nw]
    count = len(FETCHED)
    held, fetch_sem, rest = rest[:count], rest[count], rest[count + 1 :]
    sources, ops = [ops[k] for k in FETCHED], list(ops)
    for k, ref in zip(FETCHED, held):
        ops[k] = ref
    full, rest = rest[:4], rest[4:]
    own_lin, own_ldn, stats, rest = rest[0], rest[1], rest[2], rest[3:]
    back, rest = rest[:17], rest[17:]
    dx = back[5]
    near, one, two, end, fin = (rest[k * nw : (k + 1) * nw] for k in range(5))
    hin_own, hin_r, acc, sc, sp, sz, acc2 = rest[5 * nw : 5 * nw + 7]
    own, xs, xr, cs, cr, ps, pr, zs, zr, hs, hr, ts, tr, *fsem = rest[5 * nw + 7 :]
    hi, lo, x, c = place()
    d = hi * 2 + lo
    plane = (lo * 2 + x) * 2 + c
    others = plane_others()
    rows_to = [(lax.rem(d + k, dp), x * 2 + c) for k in range(1, dp)]
    z_index = [lax.rem(hi + k, nz) for k in range(1, nz)]
    z_to = [at(z, lo, x, c) for z in z_index]
    quad = quad_peers()
    g_views = [g_lin, g_ldn]
    for k, w in enumerate((2, 3, 4, 5)):
        rows, columns = shards[w]
        g_views.append(full[k].reshape(nz, 2, 2, 2 * rows, columns))
    t = Scatter(nz, shards, g_views, near, one, two, end, (cs, cr, ps, pr, zs, zr))
    meet(rows_to + [at(hi, *q[:3]) for q in others if q[3]])
    fetched = {
        k: keep(source, ref, fetch_sem.at[n])
        for n, (k, source, ref) in enumerate(zip(FETCHED, sources, held))
    }

    def fetch(*which):
        for k in which:
            fetched[k].wait()

    h_sends = []
    for k, z in enumerate(z_index):
        h_sends.append(send(hin.at[z], hin_r.at[k], hs.at[1, k], hr.at[1, k], z_to[k]))
    t.core(0)
    t.core(1)
    kept = [
        keep(g_lin.at[:, :, :, :, t.lanes(0, c)], own_lin, own.at[0]),
        keep(g_ldn.at[:, :, :, :, t.lanes(1, c)], own_ldn, own.at[1]),
        keep(hin.at[hi], hin_own, own.at[2]),
    ]
    late = []

    def first_plane():
        fetch(9, 14)
        kept[0].wait()
        kept[1].wait()
        t.own_plane(0, own_lin)
        t.own_plane(1, own_ldn)
        t.core(2)

    def out_core():
        t.core(3)

    def before_light():
        fetch(12, 13)

    def half_way():
        t.core(4)
        t.cross(0)
        t.cross(1)
        t.plane(2)
        t.plane(3)

    def rims_left():
        fetch(8, 11)
        t.plane(4)
        t.line(0)
        t.line(1)
        t.cross(2)
        t.cross(3)

    def light_grad_done():
        t.core(5)
        fetch(7, 1)

    def rows_done():
        rows = dx.reshape(dxo.shape[1], dp, dxo.shape[2], D)
        late.append(keep(rows.at[:, d], dxo.at[d], own.at[4]))
        for k, to in enumerate(rows_to):
            late.append(send(rows.at[:, to[0]], dxo.at[d], xs.at[k], xr.at[k], to))

    stages = [
        first_plane,
        out_core,
        before_light,
        half_way,
        rims_left,
        light_grad_done,
        rows_done,
    ]
    attend_back_body(
        stages, *ops, full[3], full[2], full[1], full[0], dx, stats, *back
    )
    partner = at(hi, lo, x, 1 - c)
    for k in range(6):
        lanes = slice(k * 128, (k + 1) * 128)
        acc[k : k + 1, :] = stats[0:1, lanes]
        acc[6 + k : 7 + k, :] = ffn_stats[0:1, lanes]
    loss = jnp.sum(ffn_stats[1:2, :], axis=-1, keepdims=True)
    acc[12:16, :] = jnp.broadcast_to(loss, (4, 128))
    t_c = send(acc, sc, ts.at[0], tr.at[0], partner)
    t.plane(5)
    t.line(2)
    t.line(3)
    t.cross(4)
    t_c.wait()
    acc2[...] = acc[...] + sc[...]
    t_p = [
        send(acc2, sp.at[k], ts.at[1 + k], tr.at[1 + k], at(hi, l2, x2, c))
        for k, (l2, x2) in enumerate(quad)
    ]
    t.line(4)
    for copy in h_sends + kept[2:]:
        copy.wait()

    def body(i, carry):
        value = hin_own[i].astype(F32)
        for k in range(nz - 1):
            value += hin_r[k, i].astype(F32)
        hin_own[i] = value.astype(BF)
        return carry

    lax.fori_loop(0, 8, body, 0)
    hin_o[plane] = hin_own[plane]
    late += [
        send(
            hin_own.at[(q[0] * 2 + q[1]) * 2 + q[2]],
            hin_o.at[plane],
            hs.at[0, k],
            hr.at[0, k],
            at(hi, *q[:3]),
        )
        for k, q in enumerate(others)
    ]
    t.cross(5)
    for copy in t_p:
        copy.wait()
    acc[...] = acc2[...] + sp[0] + sp[1] + sp[2]
    t_z = [send(acc, sz.at[k], ts.at[4 + k], tr.at[4 + k], z_to[k]) for k in range(nz - 1)]
    t.line(5)
    for w in range(nw):
        late += t.last(w, fin[w], gos[w], fsem)
    for copy in t_z:
        copy.wait()
    value = acc[...]
    for k in range(nz - 1):
        value += sz[k]
    total[...] = value
    for copy in late:
        copy.wait()


FETCHED = (9, 14, 12, 13, 8, 11, 7, 1)


def back_scatter(dp, rows, d_hidden, x, gain, masks, weights, saved, ffn_grads, ffn_stats, shards, hin):
    nz, nw = dp // 2, len(shards)
    tokens = x.shape[0]
    group = masks[0].shape[0]
    most = max(7, nz)
    stat_shape = (16, 128)
    paired = [
        g.reshape(nz, 2, 2, 2 * s[0], s[1]) for g, s in zip(ffn_grads, shards)
    ]
    operands = [d_hidden, x, gain, *masks, *weights, *saved, *paired, hin, ffn_stats]
    shapes = [jax.ShapeDtypeStruct((dp, group, rows, D), BF), jax.ShapeDtypeStruct(stat_shape, F32)]
    shapes += [jax.ShapeDtypeStruct(s, F32) for s in shards]
    shapes.append(jax.ShapeDtypeStruct(hin.shape[1:], BF))
    scratch = [pltpu.VMEM(operands[k].shape, operands[k].dtype) for k in FETCHED]
    scratch.append(DMA((len(FETCHED),)))
    scratch += [pltpu.VMEM((s[0] * 8 * nz, s[1]), BF) for s in shards[2:]]
    split = [(2 * s[0], s[1] // 2) for s in shards]
    scratch += [pltpu.VMEM((nz, 2, 2) + s, BF) for s in split[:2]]
    scratch += [pltpu.VMEM((8, D), F32)]
    scratch += attend_back_scratch(tokens, masks[0])
    scratch += [pltpu.VMEM((nz, 2, 2) + s, BF) for s in split]
    scratch += [pltpu.VMEM((nz, 2) + s, BF) for s in split]
    scratch += [pltpu.VMEM((nz,) + s, BF) for s in split]
    scratch += [pltpu.VMEM((nz - 1,) + s, BF) for s in split]
    scratch += [pltpu.VMEM(s, F32) for s in split]
    scratch += [
        pltpu.VMEM(hin.shape[1:], BF),
        pltpu.VMEM((nz - 1,) + hin.shape[1:], BF),
        pltpu.VMEM(stat_shape, F32),
        pltpu.VMEM(stat_shape, F32),
        pltpu.VMEM((3,) + stat_shape, F32),
        pltpu.VMEM((nz - 1,) + stat_shape, F32),
        pltpu.VMEM(stat_shape, F32),
        DMA((5,)),
        DMA((dp,)),
        DMA((dp,)),
        DMA((nw,)),
        DMA((nw,)),
        DMA((nw, 4)),
        DMA((nw, 4)),
        DMA((nw, nz)),
        DMA((nw, nz)),
        DMA((3, most)),
        DMA((3, most)),
        DMA((4 + nz,)),
        DMA((4 + nz,)),
        DMA((nw,)),
        DMA((nw,)),
        DMA((nw,)),
    ]
    return call(
        functools.partial(back_scatter_kernel, dp, shards),
        shapes,
        operands,
        [ANY if k in FETCHED else VM for k in range(len(operands) - 4)] + [ANY] * 3 + [VM],
        [VM] * len(shapes),
        scratch,
        6,
    )


def routing(routes, pieces, piece_len):
    places = jnp.arange(pieces * piece_len)
    routed = jnp.any(routes[:, None, :] == places[None, :, None], axis=-1)
    routed = routed.reshape(-1, pieces, piece_len)
    before = jnp.arange(piece_len)[:, None] < jnp.arange(piece_len)[None, :]
    rank = jnp.einsum(
        "skp,pq->skq", routed.astype(BF), before.astype(BF), preferred_element_type=F32
    )
    slots = jnp.arange(CAP, dtype=F32)
    hot = routed[:, :, None, :] & (rank[:, :, None, :] == slots[None, None, :, None])
    filled = jnp.any(hot, axis=-1)
    spots = jnp.sum(jnp.where(hot, places.reshape(1, pieces, 1, piece_len), 0), axis=-1)
    return hot, jnp.where(filled, spots, -1)


def local(
    layer_input,
    teacher,
    lengths,
    dealing,
    attn_routes,
    ffn_routes,
    ffn_scores,
    gain_attn,
    gain_ffn,
    light_qkv,
    light_out,
    heavy_qkv,
    heavy_out,
    light_in,
    light_down,
    heavy_in,
    heavy_down,
):
    dp = lax.axis_size("dp")
    pieces = lax.axis_size("fsdp")
    data_index = lax.axis_index("dp")
    piece = lax.axis_index("fsdp")
    nz = dp // 2
    n = dp * pieces
    seqs = dealing.shape[0]
    group = seqs // dp
    gain_len = gain_attn.shape[0]
    hidden_units = heavy_in.shape[1] // 2 // n
    mine = data_index * pieces + piece
    tokens = layer_input.shape[2] * dp
    matrices = (light_qkv, heavy_qkv, light_out, heavy_out, light_in, light_down)
    hin_rows = heavy_in.shape[0]
    token_count = jnp.sum(lengths).astype(F32)
    merged = (
        layer_input.shape[2] % 16 == 0
        and hidden_units % 128 == 0
        and all(m.shape[0] % 8 == 0 and m.shape[1] % 256 == 0 for m in (*matrices, heavy_down))
    )
    if merged:
        xin, hin_src, gains = prepare(dealing, layer_input[:, 0], heavy_in, gain_attn, gain_ffn)
        integers = (dealing.reshape(1, -1), lengths.reshape(1, -1), attn_routes, ffn_routes, ffn_scores)
        got = gather_attend(dp, xin, [gains, *matrices], hin_src, integers)
    else:
        xin = deal_rows(dealing, layer_input[:, 0])
        owned = jnp.arange(D)[None, :] // gain_len == mine
        spread_out = jnp.broadcast_to(
            jnp.stack([gain_attn, gain_ffn])[:, None, :], (2, D // gain_len, gain_len)
        ).reshape(2, D)
        gains = jnp.pad(jnp.where(owned, spread_out, 0.0).astype(BF), ((0, 6), (0, 0)))
        hin_src = (
            heavy_in.reshape(hin_rows, 2, nz, 8, hidden_units)
            .transpose(3, 0, 1, 2, 4)
            .reshape(8, hin_rows, 2 * nz * hidden_units)
        )
        if hin_rows % 8:
            hin_src = hin_src.reshape(8, -1, 128)
        got = gather_all(dp, xin, [gains] + [packed(m) for m in matrices], hin_src)
    flat_x = got[0].reshape(-1, D)
    w_lqkv, w_hqkv, w_lout, w_hout, w_lin, w_ldown = (
        unpacked(full, *m.shape) for full, m in zip(got[2:8], matrices)
    )
    w_hin = unpacked(got[8], hin_rows, 2 * nz * hidden_units)
    attn_weights = (w_lqkv, w_hqkv, w_lout, w_hout)
    if merged:
        gain, tables, (hidden, *saved) = got[9], got[10:19], got[19:]
        masks, ffn_masks = tables[:4], tables[4:]
    else:
        gain = jnp.sum(got[1].reshape(n, 8, D).astype(F32), axis=0)
        masks, ffn_masks = integer_tables(
            dealing, lengths, attn_routes, ffn_routes, ffn_scores, group, pieces, tokens
        )
        hidden, *saved = attend(flat_x, gain, *masks, *attn_weights)
    f_select, f_select_t, slot_score, weight_mask, weight_scale = ffn_masks
    grad_lin, grad_ldown, grad_hin, g_hdown, d_hidden, ffn_stats = feed_forward(
        nz,
        hidden,
        f_select,
        f_select_t,
        slot_score,
        gain,
        teacher.reshape(-1, D),
        weight_mask,
        weight_scale,
        w_lin,
        w_ldown,
        w_hin,
        heavy_down,
    )
    rows = tokens // dp
    shards = (light_in, light_down, heavy_out, light_out, heavy_qkv, light_qkv)
    hin_part = grad_hin.reshape((nz, 8) + hin_src.shape[1:])
    if merged:
        done = back_scatter(
            dp,
            rows,
            d_hidden,
            flat_x,
            gain,
            masks,
            attn_weights,
            saved,
            (grad_lin, grad_ldown),
            ffn_stats,
            tuple(shard.shape for shard in shards),
            hin_part,
        )
    else:
        grad_lqkv, grad_hqkv, grad_lout, grad_hout, d_inputs, attn_stats = attend_back(
            d_hidden, flat_x, gain, *masks, attn_weights, saved
        )
        stats = jnp.concatenate(
            [
                attn_stats[0].reshape(-1, 128),
                ffn_stats[0].reshape(-1, 128),
                jnp.broadcast_to(jnp.sum(ffn_stats[1]), (4, 128)),
            ]
        )
        grads = (grad_lin, grad_ldown, grad_hout, grad_lout, grad_hqkv, grad_lqkv)
        sent = [packed_full(grad, shard.shape, nz) for grad, shard in zip(grads, shards)]
        done = scatter_all(
            dp, d_inputs.reshape(group, dp, rows, D), stats, sent, hin_part
        )
    summed = done[1]
    loss_value = summed[12, 0] / (D * token_count)
    own_one = lax.dynamic_slice_in_dim(summed[:6].reshape(-1), mine * gain_len, gain_len)
    own_two = lax.dynamic_slice_in_dim(summed[6:12].reshape(-1), mine * gain_len, gain_len)
    back_rows = done[0].reshape(seqs, rows, D)
    if merged:
        d_layer, g_hin, *owned = finish_all(
            n, dealing, back_rows, done[8], [*done[2:8], g_hdown], heavy_in.shape
        )
    else:
        d_layer = undeal_rows(dealing, back_rows)
        owned = [full.reshape(shard.shape) for full, shard in zip(done[2:8], shards)]
        owned.append(g_hdown)
        g_hin = (
            done[8]
            .astype(F32)
            .reshape(8, hin_rows, 2, nz, hidden_units)
            .transpose(1, 2, 3, 0, 4)
            .reshape(heavy_in.shape)
        )
    g_lin, g_ldown, g_hout, g_lout, g_hqkv, g_lqkv, g_hdown = owned
    return (
        loss_value,
        d_layer[:, None],
        own_one,
        own_two,
        g_lqkv,
        g_lout,
        g_hqkv,
        g_hout,
        g_lin,
        g_ldown,
        g_hin,
        g_hdown,
    )


def integer_tables(dealing, lengths, attn_routes, ffn_routes, ffn_scores, group, pieces, tokens):
    seqs = dealing.shape[0]
    data_index = lax.axis_index("dp")
    piece = lax.axis_index("fsdp")
    chosen = lax.dynamic_slice_in_dim(dealing, data_index * group, group)
    one = chosen[:, None] == jnp.arange(seqs)[None, :]
    seq_lengths = jnp.sum(jnp.where(one, lengths[None, :], 0), axis=1)
    attn_pick = jnp.sum(jnp.where(one[:, :, None], attn_routes[None], 0), axis=1)
    ffn_pick = jnp.sum(jnp.where(one[:, :, None], ffn_routes[None], 0), axis=1)
    score_pick = jnp.sum(jnp.where(one[:, :, None], ffn_scores[None], 0.0), axis=1)
    token_count = jnp.sum(lengths).astype(F32)
    positions = piece * tokens + jnp.arange(tokens)
    valid_mask = positions[None, :] < seq_lengths[:, None]
    a_hot, a_spots = routing(attn_pick, pieces, tokens)
    f_hot, f_spots = routing(ffn_pick, pieces, tokens)
    a_select = lax.dynamic_index_in_dim(a_hot, piece, 1, False).astype(BF)
    f_select = lax.dynamic_index_in_dim(f_hot, piece, 1, False).astype(BF)
    a_spot = lax.dynamic_index_in_dim(a_spots, piece, 1, False)
    f_spot = lax.dynamic_index_in_dim(f_spots, piece, 1, False)
    slot_score = jnp.sum(
        jnp.where(f_spot[:, :, None] == ffn_pick[:, None, :], score_pick[:, None, :], 0.0), axis=-1
    )
    key_pos = piece * tokens - WIN + jnp.arange(tokens + 2 * WIN)
    live_key = (key_pos >= 0)[None, :] & (key_pos[None, :] < seq_lengths[:, None])
    key_line = jnp.where(live_key, 0.0, MASKED)
    key_bias = jnp.stack(
        [key_line[:, b : b + 3 * WIN] for b in range(0, tokens, WIN)], axis=1
    ).reshape(-1, 1, 3 * WIN)
    all_spots = a_spots.reshape(group, pieces * CAP)
    heavy_allowed = ((all_spots >= 0) & (all_spots < seq_lengths[:, None]))[:, None, :] | (
        a_spot[:, :, None] == all_spots[:, None, :]
    )
    heavy_bias = jnp.where(heavy_allowed, 0.0, MASKED)
    weight_mask = valid_mask.reshape(-1, 1).astype(F32)
    masks = (a_select, a_select.swapaxes(1, 2), key_bias, heavy_bias)
    ffn_masks = (
        f_select,
        f_select.swapaxes(1, 2),
        slot_score.reshape(-1, 1),
        weight_mask,
        2.0 * weight_mask / (D * token_count),
    )
    return masks, ffn_masks


def packed_full(grad, shard_shape, nz):
    rows, columns = shard_shape
    if rows % 8 == 0:
        return grad.reshape(nz, 2, 2, 2, rows, columns)
    return grad.reshape(nz, 2, 2, 2, rows * columns // 128, 128)


def solution(mesh):
    split = P(("dp", "fsdp"))
    matrix = P(("dp", "fsdp"), None)
    placed = (
        P(None, "fsdp", "dp", None),
        P("dp", "fsdp", None, None),
        P(),
        P(),
        P(),
        P(),
        P(),
        split,
        split,
    ) + (matrix,) * 8
    return jax.shard_map(
        local,
        mesh=mesh,
        in_specs=placed,
        out_specs=(P(), P(None, "fsdp", "dp", None), split, split) + (matrix,) * 8,
        check_vma=False,
    )
```

```python
import functools
import jax
import jax.numpy as jnp
from jax import lax
from jax.experimental import pallas as pl
from jax.experimental.pallas import tpu as pltpu
from jax.sharding import PartitionSpec as P

D = 768
HL = 8
HH = 12
DH = 64
FL = 1024
FH = 4096
WIN = 128
CAP = 64

EPSILON = 1e-06
MASKED = -1000000000.0
SCORE_SCALE = 0.125
MESH = pl.DeviceIdType.MESH
BF = jnp.bfloat16
F32 = jnp.float32
ANY = pl.BlockSpec(memory_space=pl.ANY)
VM = pl.BlockSpec(memory_space=pltpu.VMEM)
DMA = pltpu.SemaphoreType.DMA
VMEM_BYTES = 60 * 1024 * 1024


def place():
    d = lax.axis_index("dp")
    f = lax.axis_index("fsdp")
    return d // 2, d % 2, f // 2, f % 2


def at(hi, lo, x, c):
    return (hi * 2 + lo, x * 2 + c)


def meet(peers):
    barrier = pltpu.get_barrier_semaphore()
    for peer in peers:
        pl.semaphore_signal(barrier, inc=1, device_id=peer, device_id_type=MESH)
    pl.semaphore_wait(barrier, len(peers))


def send(src, dst, send_sem, recv_sem, peer):
    copy = pltpu.make_async_remote_copy(
        src_ref=src,
        dst_ref=dst,
        send_sem=send_sem,
        recv_sem=recv_sem,
        device_id=peer,
        device_id_type=MESH,
    )
    copy.start()
    return copy


def keep(src, dst, sem):
    copy = pltpu.make_async_copy(src, dst, sem)
    copy.start()
    return copy


def quad_peers():
    hi, lo, x, c = place()
    return [(lo, 1 - x), (1 - lo, x), (1 - lo, 1 - x)]


def call(kernel, out_shape, operands, in_specs, out_specs, scratch, collective_id):
    return pl.pallas_call(
        kernel,
        out_shape=out_shape,
        in_specs=in_specs,
        out_specs=out_specs,
        scratch_shapes=scratch,
        compiler_params=pltpu.CompilerParams(
            collective_id=collective_id, has_side_effects=True, vmem_limit_bytes=VMEM_BYTES
        ),
    )(*operands)


def deal_kernel(deal_ref, x_ref, o_ref):
    def body(i, carry):
        o_ref[i] = x_ref[deal_ref[i]]
        return carry

    lax.fori_loop(0, o_ref.shape[0], body, 0)


def deal_rows(dealing, rows):
    return pl.pallas_call(
        deal_kernel,
        out_shape=jax.ShapeDtypeStruct(rows.shape, rows.dtype),
        in_specs=[pl.BlockSpec(memory_space=pltpu.SMEM), VM],
        out_specs=VM,
        compiler_params=pltpu.CompilerParams(vmem_limit_bytes=VMEM_BYTES),
    )(dealing, rows)


def undeal_kernel(deal_ref, x_ref, o_ref):
    def body(i, carry):
        o_ref[deal_ref[i]] = x_ref[i].astype(F32)
        return carry

    lax.fori_loop(0, x_ref.shape[0], body, 0)


def undeal_rows(dealing, rows):
    return pl.pallas_call(
        undeal_kernel,
        out_shape=jax.ShapeDtypeStruct(rows.shape, F32),
        in_specs=[pl.BlockSpec(memory_space=pltpu.SMEM), VM],
        out_specs=VM,
        compiler_params=pltpu.CompilerParams(vmem_limit_bytes=VMEM_BYTES),
    )(dealing, rows)


def prepare_kernel(deal_ref, x_ref, heavy_ref, one_ref, two_ref, xin, hin, gains):
    def body(i, carry):
        xin[i] = x_ref[deal_ref[i]]
        return carry

    lax.fori_loop(0, xin.shape[0], body, 0)
    count = one_ref.shape[1]
    units = D // count
    step = heavy_ref.shape[1] // 2 // units
    for j in range(8):
        for k in range(units // 8):
            for g in (0, 1):
                start = g * heavy_ref.shape[1] // 2 + (k * 8 + j) * step
                spot = (g * (units // 8) + k) * step
                hin[j, :, spot : spot + step] = heavy_ref[:, start : start + step]
    mine = lax.axis_index("dp") * 4 + lax.axis_index("fsdp")
    row = lax.broadcasted_iota(jnp.int32, (count, D), 0)
    lane = lax.broadcasted_iota(jnp.int32, (count, D), 1)
    hot = jnp.where(lane == row + mine * count, 1.0, 0.0).astype(BF)
    lines = [jnp.broadcast_to(ref[...], (8, count)) for ref in (one_ref, two_ref)]
    one, two = (jnp.dot(line, hot, preferred_element_type=F32) for line in lines)
    kind = lax.broadcasted_iota(jnp.int32, (8, D), 0)
    gains[...] = jnp.where(kind == 0, one, jnp.where(kind == 1, two, 0.0)).astype(BF)


def prepare(dealing, rows, heavy_in, gain_one, gain_two):
    count = gain_one.shape[0]
    columns = heavy_in.shape[1] // 8
    return pl.pallas_call(
        prepare_kernel,
        out_shape=[
            jax.ShapeDtypeStruct(rows.shape, BF),
            jax.ShapeDtypeStruct((8, heavy_in.shape[0], columns), BF),
            jax.ShapeDtypeStruct((8, D), BF),
        ],
        in_specs=[pl.BlockSpec(memory_space=pltpu.SMEM), VM, VM, VM, VM],
        out_specs=[VM] * 3,
        compiler_params=pltpu.CompilerParams(vmem_limit_bytes=VMEM_BYTES),
    )(dealing, rows, heavy_in, gain_one.reshape(1, count), gain_two.reshape(1, count))


def finish_kernel(units, deal_ref, x_ref, hin, *refs):
    count = (len(refs) - 2) // 2
    ins, (rows, heavy), outs = refs[:count], refs[count : count + 2], refs[count + 2 :]

    def body(i, carry):
        rows[deal_ref[i]] = x_ref[i].astype(F32)
        return carry

    lax.fori_loop(0, x_ref.shape[0], body, 0)
    step = heavy.shape[1] // 2 // units
    for j in range(8):
        for k in range(units // 8):
            for g in (0, 1):
                start = g * heavy.shape[1] // 2 + (k * 8 + j) * step
                spot = (g * (units // 8) + k) * step
                heavy[:, start : start + step] = hin[j, :, spot : spot + step].astype(F32)
    for source, out in zip(ins, outs):
        out[...] = source[...]


def finish_all(units, dealing, rows, hin, grads, heavy_shape):
    shapes = [jax.ShapeDtypeStruct(rows.shape, F32), jax.ShapeDtypeStruct(heavy_shape, F32)]
    shapes += [jax.ShapeDtypeStruct(g.shape, F32) for g in grads]
    return pl.pallas_call(
        functools.partial(finish_kernel, units),
        out_shape=shapes,
        in_specs=[pl.BlockSpec(memory_space=pltpu.SMEM)] + [VM] * (2 + len(grads)),
        out_specs=[VM] * len(shapes),
        compiler_params=pltpu.CompilerParams(vmem_limit_bytes=VMEM_BYTES),
    )(dealing, rows, hin, *grads)


def packed(matrix):
    rows, columns = matrix.shape
    if rows % 8 == 0:
        return matrix
    return matrix.reshape(rows * columns // 128, 128)


def unpacked(gathered, rows, columns):
    return gathered.reshape(-1, rows, columns).reshape(-1, columns)


def plane_others():
    hi, lo, x, c = place()
    others = []
    for a in (0, 1):
        for b in (0, 1):
            for e in (0, 1):
                if a or b or e:
                    others.append(
                        (1 - lo if a else lo, 1 - x if b else x, 1 - c if e else c, b or e)
                    )
    return others


class Gather:
    def __init__(self, dp, xin, ws, hin, xo, wos, hin_o, sems, halves=None):
        self.dp, self.nz = dp, dp // 2
        self.xin, self.ws, self.hin = xin, ws, hin
        self.xo, self.wos, self.hin_o = xo, wos, hin_o
        self.loc, self.xs, self.xr, self.zs, self.zr = sems[:5]
        self.ps, self.pr, self.cs, self.cr, self.hs, self.hr = sems[5:]
        self.hi, self.lo, self.x, self.c = place()
        hi, lo, x, c = place()
        self.d = hi * 2 + lo
        self.home = (lo * 2 + x) * 2 + c
        self.rows_to = [(lax.rem(self.d + k, dp), x * 2 + c) for k in range(1, dp)]
        self.z_to = [at(lax.rem(hi + k, self.nz), lo, x, c) for k in range(1, self.nz)]
        self.others = plane_others()
        nw = len(ws)
        self.kept, self.z, self.p, self.f, self.k = ([None] * nw for _ in range(5))

        self.halves = halves

    def lanes(self, w, c):
        half = self.ws[w].shape[1] // 2
        return pl.ds(pl.multiple_of(c * half, 128), half)

    def shard(self, w, z, lo, x):
        if self.halves is None:
            return self.wos[w].at[z, lo, x, self.c]
        return self.wos[w].at[z, lo, x, :, self.lanes(w, self.c)]

    def swap(self, w):
        mine, mate, _, sems = self.halves
        partner = at(self.hi, self.lo, self.x, 1 - self.c)
        self.kept[w] = keep(self.ws[w].at[:, self.lanes(w, self.c)], mine[w], sems[0].at[w])
        out = self.ws[w].at[:, self.lanes(w, 1 - self.c)]
        self.z[w] = send(out, mate[w], sems[1].at[w], sems[2].at[w], partner)

    def join(self, w):
        mine, mate, base, _ = self.halves
        self.kept[w].wait()
        self.z[w].wait()
        a, b = mine[w][...].astype(F32), mate[w][...].astype(F32)
        first = self.c == 0
        rows = [jnp.where(first, a, b), jnp.where(first, b, a)]
        base[w][...] = jnp.concatenate(rows, axis=0).astype(BF)
        self.line(w)

    def meet(self):
        peers = self.rows_to + [at(self.hi, *q[:3]) for q in self.others if q[3]]
        meet(peers)

    def rows(self):
        group = self.xin.shape[0] // self.dp
        nw = len(self.ws)
        spot = self.xo.at[:, self.d]
        self.own = keep(self.xin.at[pl.ds(self.d * group, group)], spot, self.loc.at[nw])
        self.moved = [
            send(self.xin.at[pl.ds(to[0] * group, group)], spot, self.xs.at[k], self.xr.at[k], to)
            for k, to in enumerate(self.rows_to)
        ]

    def rows_ready(self):
        self.own.wait()
        for copy in self.moved:
            copy.wait()

    def line(self, w):
        spot = self.shard(w, self.hi, self.lo, self.x)
        own = self.ws[w] if self.halves is None else self.halves[2][w]
        self.kept[w] = keep(own, spot, self.loc.at[w])
        self.z[w] = [
            send(own, spot, self.zs.at[w, k], self.zr.at[w, k], to)
            for k, to in enumerate(self.z_to)
        ]

    def onward(self, part, w, k, to, sems):
        return send(part, part, sems[0].at[w, k], sems[1].at[w, k], to)

    def plane(self, w):
        self.kept[w].wait()
        for copy in self.z[w]:
            copy.wait()
        hi, lo, x, c = self.hi, self.lo, self.x, self.c
        column = self.shard(w, slice(None), lo, x)
        plane = (self.ps, self.pr)
        self.p[w] = [
            self.onward(column, w, 0, at(hi, lo, 1 - x, c), plane),
            self.onward(column, w, 1, at(hi, 1 - lo, x, c), plane),
        ]
        self.k[w] = [self.onward(column, w, 0, at(hi, lo, x, 1 - c), (self.cs, self.cr))]

    def cross(self, w):
        hi, lo, x, c = self.hi, self.lo, self.x, self.c
        plane, core, half = (self.ps, self.pr), (self.cs, self.cr), self.nz // 2
        partner = at(hi, lo, x, 1 - c)
        self.p[w][1].wait()
        part = self.shard(w, pl.ds(0, half), 1 - lo, x)
        first = self.onward(part, w, 2, at(hi, lo, 1 - x, c), plane)
        self.p[w][0].wait()
        part = self.shard(w, pl.ds(half, self.nz - half), lo, 1 - x)
        self.f[w] = [first, self.onward(part, w, 3, at(hi, 1 - lo, x, c), plane)]
        for k, part in ((1, (1 - lo, x)), (2, (lo, 1 - x))):
            self.k[w].append(
                self.onward(self.shard(w, slice(None), *part), w, k, partner, core)
            )

    def core(self, w):
        for copy in self.f[w]:
            copy.wait()
        part = self.shard(w, slice(None), 1 - self.lo, 1 - self.x)
        partner = at(self.hi, self.lo, self.x, 1 - self.c)
        self.k[w].append(self.onward(part, w, 3, partner, (self.cs, self.cr)))

    def ready(self, w):
        for copy in self.k[w]:
            copy.wait()

    def heavy_plane(self):
        nw, hi = len(self.ws), self.hi
        spot = self.hin_o.at[hi, self.home]
        self.h_own = [
            keep(self.hin.at[self.home], spot, self.loc.at[nw + 1]),
        ]
        self.h_near = [
            send(
                self.hin.at[(q[0] * 2 + q[1]) * 2 + q[2]],
                spot,
                self.hs.at[0, k],
                self.hr.at[0, k],
                at(hi, *q[:3]),
            )
            for k, q in enumerate(self.others)
        ]

    def heavy_line(self):
        for copy in self.h_own + self.h_near:
            copy.wait()
        part = self.hin_o.at[self.hi]
        self.h_far = []
        for k, to in enumerate(self.z_to):
            self.h_far.append(send(part, part, self.hs.at[1, k], self.hr.at[1, k], to))

    def heavy_ready(self):
        for copy in self.h_far:
            copy.wait()


def gather_sems(dp, nw):
    nz, most = dp // 2, max(7, dp // 2)
    return [
        DMA((nw + 2,)),
        DMA((dp,)),
        DMA((dp,)),
        DMA((nw, nz)),
        DMA((nw, nz)),
        DMA((nw, 4)),
        DMA((nw, 4)),
        DMA((nw, 4)),
        DMA((nw, 4)),
        DMA((2, most)),
        DMA((2, most)),
    ]


def gather_kernel(dp, nw, *refs):
    ins, outs, sems = refs[: 2 + nw], refs[2 + nw : 4 + 2 * nw], refs[4 + 2 * nw :]
    g = Gather(dp, ins[0], ins[1:-1], ins[-1], outs[0], outs[1:-1], outs[-1], sems)
    g.meet()
    g.rows()
    for w in range(nw):
        g.line(w)
    g.heavy_plane()
    for w in range(nw):
        g.plane(w)
        if w == 1:
            g.heavy_line()
        if w >= 1:
            g.cross(w - 1)
        if w >= 2:
            g.core(w - 2)
    g.cross(nw - 1)
    for w in range(nw - 2, nw):
        g.core(w)
    g.rows_ready()
    for w in range(nw):
        g.ready(w)
    g.heavy_ready()


def gather_shapes(dp, xin, weights, hin, paired):
    nz = dp // 2
    seqs, rows, _ = xin.shape
    shapes = [jax.ShapeDtypeStruct((seqs // dp, dp, rows, D), BF)]
    if paired:
        shapes += [jax.ShapeDtypeStruct((nz, 2, 2, 2 * w.shape[0], w.shape[1]), BF) for w in weights]
    else:
        shapes += [jax.ShapeDtypeStruct((nz, 2, 2, 2) + w.shape, BF) for w in weights]
    shapes.append(jax.ShapeDtypeStruct((nz,) + hin.shape, BF))
    return shapes


def gather_all(dp, xin, weights, hin):
    nw = len(weights)
    return call(
        functools.partial(gather_kernel, dp, nw),
        gather_shapes(dp, xin, weights, hin, False),
        [xin, *weights, hin],
        [ANY] * (2 + nw),
        [ANY] * (2 + nw),
        gather_sems(dp, nw),
        1,
    )


def rim_exchange(left, right, from_left, from_right, ls, lr, rs, rr):
    d = lax.axis_index("dp")
    f = lax.axis_index("fsdp")
    last = lax.axis_size("fsdp") - 1

    def down():
        return pltpu.make_async_remote_copy(
            src_ref=left,
            dst_ref=from_right,
            send_sem=ls,
            recv_sem=lr,
            device_id=(d, lax.max(f - 1, 0)),
            device_id_type=MESH,
        )

    def up():
        return pltpu.make_async_remote_copy(
            src_ref=right,
            dst_ref=from_left,
            send_sem=rs,
            recv_sem=rr,
            device_id=(d, lax.min(f + 1, last)),
            device_id_type=MESH,
        )

    @pl.when(f > 0)
    def _():
        down().start()

    @pl.when(f < last)
    def _():
        up().start()

    @pl.when(f == 0)
    def _():
        from_left[...] = jnp.zeros(from_left.shape, from_left.dtype)

    @pl.when(f == last)
    def _():
        from_right[...] = jnp.zeros(from_right.shape, from_right.dtype)

    def finish():
        @pl.when(f > 0)
        def _():
            down().wait_send()
            up().wait_recv()

        @pl.when(f < last)
        def _():
            up().wait_send()
            down().wait_recv()

    return finish


def line_peers():
    hi, lo, x, c = place()
    return [at(hi, lo, x, 1 - c), at(hi, lo, 1 - x, c), at(hi, lo, 1 - x, 1 - c)]


def dot(left, right):
    return jnp.dot(left, right, preferred_element_type=F32)


def dot_back(left, right):
    return lax.dot_general(left, right, (((1,), (1,)), ((), ())), preferred_element_type=F32)


def dot_grad(left, right):
    return lax.dot_general(left, right, (((0,), (0,)), ((), ())), preferred_element_type=F32)


def halves(value):
    high = value.astype(BF)
    return high, (value - high.astype(F32)).astype(BF)


def tiles(extent, step, body):
    def run(i, carry):
        body(pl.ds(pl.multiple_of(i * step, step), step))
        return carry

    lax.fori_loop(0, extent // step, run, 0)


GELU_A = 0.7978845608028654
GELU_B = 0.044715


def gelu_parts(v):
    square = v * v
    t = jnp.tanh(GELU_A * v * (1.0 + GELU_B * square))
    value = 0.5 * v * (1.0 + t)
    slope = 0.5 * (1.0 + t) + 0.5 * v * (1.0 - t * t) * GELU_A * (1.0 + 3.0 * GELU_B * square)
    return value, slope


def gelu_value(v):
    return 0.5 * v * (1.0 + jnp.tanh(GELU_A * v * (1.0 + GELU_B * v * v)))


def ffn_kernel(
    nz,
    hidden,
    select,
    select_t,
    score,
    gain,
    teach_hbm,
    mask,
    scale,
    w_in_hbm,
    w_dn_hbm,
    w_hin_hbm,
    hdn,
    g_in_hbm,
    g_dn_hbm,
    g_hin_hbm,
    hdn_o,
    d_hidden,
    stats,
    teach,
    w_in,
    w_dn,
    w_hin,
    g_in,
    g_dn,
    g_hin,
    moves_sem,
    w_line,
    g_line,
    g_in_line,
    hn,
    every,
    d_every,
    up_l,
    z,
    up_h,
    zh,
    part,
    near,
    far,
    out,
    dl,
    dup_l,
    dup_h,
    dhn,
    ps,
    pr,
    cs,
    cr,
    qs,
    qr,
    es,
    er,
    zs,
    zr,
    own,
):
    hi, lo, x, c = place()
    quad = quad_peers()
    partner = at(hi, lo, x, 1 - c)
    spots = [l2 * 2 + x2 for l2, x2 in quad]
    home = lo * 2 + x
    tokens = hidden.shape[0]
    group, cap, width = select.shape
    fl = z.shape[1]
    fh = zh.shape[3]
    block = 4 * cap
    z_index = [lax.rem(hi + k, nz) for k in range(1, nz)]
    z_to = [at(k, lo, x, c) for k in z_index]
    meet([at(hi, l2, x2, c) for l2, x2 in quad] + [partner] + z_to)
    pairs = ((w_in_hbm, w_in), (w_dn_hbm, w_dn), (w_hin_hbm, w_hin), (teach_hbm, teach))
    fetched = [keep(source, ref, moves_sem.at[k]) for k, (source, ref) in enumerate(pairs)]
    hdn_own = keep(hdn, w_line.at[hi], own)
    hdn_far = [send(hdn, w_line.at[hi], zs.at[0, k], zr.at[0, k], to) for k, to in enumerate(z_to)]
    w_hdn = w_line.reshape(-1, D)

    def span(s):
        return slice(s * width, (s + 1) * width)

    def slots(s):
        return slice(s * cap, (s + 1) * cap)

    def spread(buffer, s, i):
        spot = buffer.at[s, c, home]
        there = [
            send(spot, spot, ps.at[i, k], pr.at[i, k], at(hi, l2, x2, c))
            for k, (l2, x2) in enumerate(quad)
        ]
        return there, [send(spot, spot, cs.at[i, 3], cr.at[i, 3], partner)]

    def relay(buffer, s, i, there, back):
        for k, q in enumerate(spots):
            there[k].wait()
            other = buffer.at[s, c, q]
            back.append(send(other, other, cs.at[i, k], cr.at[i, k], partner))

    def fold(s, i, copy):
        copy.wait()
        there = []
        for k, q in enumerate(spots):
            near[i, q] = (near[i, q].astype(F32) + part[s, c, q].astype(F32)).astype(BF)
            l2, x2 = quad[k]
            there.append(
                send(near.at[i, q], far.at[i, k], qs.at[i, k], qr.at[i, k], at(hi, l2, x2, c))
            )
        return there

    def folded(s, i, there):
        for copy in there:
            copy.wait()
        return (
            near[i, home].astype(F32)
            + part[s, c, home].astype(F32)
            + far[i, 0].astype(F32)
            + far[i, 1].astype(F32)
            + far[i, 2].astype(F32)
        )

    def norm(r):
        h = hidden[r, :]
        inv = lax.rsqrt(jnp.mean(h * h, axis=-1, keepdims=True) + EPSILON)
        hn[r, :] = (h * inv * gain[1:2, :]).astype(BF)

    seqs = range(group)
    moves = {}
    tiles(tokens, 128, norm)
    for s in seqs:
        every[s, c, home] = dot(select[s], hn[span(s), :]).astype(BF)
        moves[s] = spread(every, s, s)

    def light_up(r):
        up_l[r, :] = dot(hn[r, :], w_in[...])
        z[r, :] = (gelu_value(up_l[r, :fl]) * up_l[r, fl:]).astype(BF)

    fetched[0].wait()
    tiles(tokens, width, light_up)
    for s in seqs:
        relay(every, s, s, *moves[s])

    def light_down(r):
        out[r, :] = hidden[r, :] + dot(z[r, :], w_dn[...])

    fetched[1].wait()
    tiles(tokens, width, light_down)

    def light_slopes(r):
        value, slope = gelu_parts(up_l[r, :fl])
        up_l[r, :fl] = up_l[r, fl:] * slope
        up_l[r, fl:] = value

    def heavy_up(s, e):
        up_h[s, e] = dot(every[s, e].reshape(block, D), w_hin[...])
        zh[s, e] = (gelu_value(up_h[s, e, :, :fh]) * up_h[s, e, :, fh:]).astype(BF)

    def heavy_down(s, e):
        part[s, e] = dot(zh[s, e], w_hdn[...]).astype(BF).reshape(4, cap, D)

    fetched[2].wait()
    sums = {}
    for s in seqs:
        for copy in moves[s][1]:
            copy.wait()
        heavy_up(s, 1 - c)
        heavy_up(s, c)
    tiles(tokens, 64, light_slopes)
    hdn_own.wait()
    for copy in hdn_far:
        copy.wait()
    first = {}
    for s in seqs:
        heavy_down(s, 1 - c)
        first[s] = send(part.at[s, 1 - c], near.at[s], es.at[s], er.at[s], partner)
        if s > 0:
            sums[s - 1] = fold(s - 1, s - 1, first[s - 1])
        heavy_down(s, c)
    sums[group - 1] = fold(group - 1, group - 1, first[group - 1])
    for s in seqs:
        for e in (0, 1):

            def heavy_slopes(r, s=s, e=e):
                value, slope = gelu_parts(up_h[s, e, r, :fh])
                up_h[s, e, r, :fh] = up_h[s, e, r, fh:] * slope
                up_h[s, e, r, fh:] = value

            if s == 0:
                tiles(block, 128, heavy_slopes)
    stats[...] = jnp.zeros(stats.shape, F32)
    fetched[3].wait()

    def light_back(r):
        dz = dot_back(dl[r, :], w_dn[...])
        dup_l[r, :fl] = (dz * up_l[r, :fl]).astype(BF)
        dup_l[r, fl:] = (dz * up_l[r, fl:]).astype(BF)

    for s in seqs:
        r = span(s)
        high, low = halves(folded(s, s, sums[s]) * score[slots(s), :])
        total = out[r, :] + (dot(select_t[s], high) + dot(select_t[s], low))
        m = total - teach[r, :].astype(F32)
        stats[1:2, :] += jnp.sum(mask[r, :] * m * m, axis=0, keepdims=True)
        d = scale[r, :] * m
        out[r, :] = d
        dl[r, :] = d.astype(BF)
        high, low = halves(d)
        picked = dot(select[s], high) + dot(select[s], low)
        d_every[s, c, home] = (picked * score[slots(s), :]).astype(BF)
        moves[s] = spread(d_every, s, group + s)
        light_back(r)
        if s > 0:
            for e in (0, 1):

                def more_slopes(r, s=s, e=e):
                    value, slope = gelu_parts(up_h[s, e, r, :fh])
                    up_h[s, e, r, :fh] = up_h[s, e, r, fh:] * slope
                    up_h[s, e, r, fh:] = value

                tiles(block, 128, more_slopes)

    def heavy_back(s, e):
        dz = dot_back(d_every[s, e].reshape(block, D), w_hdn[...])
        dup_h[s, e, :, :fh] = (dz * up_h[s, e, :, :fh]).astype(BF)
        dup_h[s, e, :, fh:] = (dz * up_h[s, e, :, fh:]).astype(BF)
        v = dot_back(dup_h[s, e], w_hin[...]).astype(BF)
        part[s, e] = v.reshape(4, cap, D)

    for s in seqs:
        relay(d_every, s, group + s, *moves[s])
        dhn[span(s), :] = dot_back(dup_l[span(s), :], w_in[...])
    for s in seqs:
        for copy in moves[s][1]:
            copy.wait()
    count = group * 2 * block
    d_rows = d_every[...].reshape(count, D)
    g_line[...] = dot_grad(zh[...].reshape(count, fh), d_rows).astype(BF)
    g_view = g_line.reshape(nz, -1, D)
    hdn_back = [
        send(g_view.at[k], g_in_line.at[n], zs.at[1, n], zr.at[1, n], z_to[n])
        for n, k in enumerate(z_index)
    ]
    for s in seqs:
        i = group + s
        heavy_back(s, 1 - c)
        first[s] = send(part.at[s, 1 - c], near.at[i], es.at[i], er.at[i], partner)
        if s > 0:
            sums[s - 1] = fold(s - 1, i - 1, first[s - 1])
        heavy_back(s, c)
    sums[group - 1] = fold(group - 1, 2 * group - 1, first[group - 1])

    def light_grad(j):
        g_dn[j, :] = dot_grad(z[:, j], dl[...]).astype(BF)

    tiles(fl, 512, light_grad)
    flushed = [keep(g_dn, g_dn_hbm, moves_sem.at[4])]

    def light_in_grad(j):
        g_in[:, j] = dot_grad(hn[...], dup_l[:, j]).astype(BF)

    tiles(2 * fl, 1024, light_in_grad)
    flushed.append(keep(g_in, g_in_hbm, moves_sem.at[5]))
    every_rows = every[...].reshape(count, D)

    def heavy_grad(j):
        g_hin[:, j] = dot_grad(every_rows, dup_h[:, :, :, j].reshape(count, 512)).astype(BF)

    tiles(2 * fh, 512, heavy_grad)
    flushed.append(keep(g_hin, g_hin_hbm, moves_sem.at[6]))
    for s in seqs:
        r = span(s)
        high, low = halves(folded(s, group + s, sums[s]))
        d = dhn[r, :] + (dot(select_t[s], high) + dot(select_t[s], low))
        h = hidden[r, :]
        inv = lax.rsqrt(jnp.mean(h * h, axis=-1, keepdims=True) + EPSILON)
        dh = d * h
        stats[0:1, :] += jnp.sum(dh * inv, axis=0, keepdims=True)
        mean = jnp.mean(gain[1:2, :] * dh, axis=-1, keepdims=True)
        d_hidden[r, :] = out[r, :] + inv * gain[1:2, :] * d - h * (inv * inv * inv * mean)
    for copy in hdn_back + flushed:
        copy.wait()
    value = g_view[hi].astype(F32)
    for n in range(nz - 1):
        value += g_in_line[n].astype(F32)
    hdn_o[...] = value


def feed_forward(nz, hidden, select, select_t, score, gain, teach, mask, scale, w_in, w_dn, w_hin, hdn):
    tokens = hidden.shape[0]
    group, cap, _ = select.shape
    fl, fh = w_dn.shape[0], w_hin.shape[1] // 2
    block = (group, 2, 4, cap, D)
    line = (nz,) + hdn.shape
    operands = [hidden, select, select_t, score, gain, teach, mask, scale, w_in, w_dn, w_hin, hdn]
    return call(
        functools.partial(ffn_kernel, nz),
        [
            jax.ShapeDtypeStruct((D, 2 * fl), BF),
            jax.ShapeDtypeStruct((fl, D), BF),
            jax.ShapeDtypeStruct((D, 2 * fh), BF),
            jax.ShapeDtypeStruct(hdn.shape, F32),
            jax.ShapeDtypeStruct((tokens, D), F32),
            jax.ShapeDtypeStruct((8, D), F32),
        ],
        operands,
        [VM] * 5 + [ANY] + [VM] * 2 + [ANY] * 4,
        [ANY] * 3 + [VM] * 3,
        [
            pltpu.VMEM((tokens, D), BF),
            pltpu.VMEM((D, 2 * fl), BF),
            pltpu.VMEM((fl, D), BF),
            pltpu.VMEM((D, 2 * fh), BF),
            pltpu.VMEM((D, 2 * fl), BF),
            pltpu.VMEM((fl, D), BF),
            pltpu.VMEM((D, 2 * fh), BF),
            DMA((7,)),
            pltpu.VMEM(line, BF),
            pltpu.VMEM((fh, D), BF),
            pltpu.VMEM((nz - 1,) + hdn.shape, BF),
            pltpu.VMEM((tokens, D), BF),
            pltpu.VMEM(block, BF),
            pltpu.VMEM(block, BF),
            pltpu.VMEM((tokens, 2 * fl), F32),
            pltpu.VMEM((tokens, fl), BF),
            pltpu.VMEM((group, 2, 4 * cap, 2 * fh), F32),
            pltpu.VMEM((group, 2, 4 * cap, fh), BF),
            pltpu.VMEM(block, BF),
            pltpu.VMEM((2 * group, 4, cap, D), BF),
            pltpu.VMEM((2 * group, 3, cap, D), BF),
            pltpu.VMEM((tokens, D), F32),
            pltpu.VMEM((tokens, D), BF),
            pltpu.VMEM((tokens, 2 * fl), BF),
            pltpu.VMEM((group, 2, 4 * cap, 2 * fh), BF),
            pltpu.VMEM((tokens, D), F32),
            DMA((2 * group, 3)),
            DMA((2 * group, 3)),
            DMA((2 * group, 4)),
            DMA((2 * group, 4)),
            DMA((2 * group, 3)),
            DMA((2 * group, 3)),
            DMA((2 * group,)),
            DMA((2 * group,)),
            DMA((2, nz)),
            DMA((2, nz)),
            DMA,
        ],
        5,
    )


def pair_masks(scale):
    lane = lax.broadcasted_iota(jnp.int32, (1, 2 * DH), 1)
    left = jnp.where(lane < DH, scale, 0.0).astype(BF)
    right = jnp.where(lane < DH, 0.0, scale).astype(BF)
    return left, right


def both(value, masks):
    return jnp.concatenate([value * masks[0], value * masks[1]], axis=0)


def side(stacked):
    rows = stacked.shape[0] // 2
    return jnp.concatenate([stacked[:rows], stacked[rows:]], axis=1)


def pair_forward(q, k, v, bias, ones, scaled):
    scores = dot_back(both(q, scaled), k) + bias
    top = jnp.max(scores, axis=-1, keepdims=True)
    shifted = jnp.exp(scores - top)
    total = jnp.sum(shifted, axis=-1, keepdims=True)
    prob = (shifted / total).astype(BF)
    return dot(side(prob), both(v, ones)).astype(BF), top + jnp.log(total)


def pair_backward(q, k, v, bias, lse, d_out, ones, scaled):
    q2 = both(q, scaled)
    d2 = both(d_out, ones)
    prob = jnp.exp(dot_back(q2, k) + bias - lse)
    d_prob = dot_back(d2, v)
    row = jnp.sum(prob * d_prob, axis=-1, keepdims=True)
    d_scores = (prob * (d_prob - row)).astype(BF)
    dq = dot(side(d_scores), both(k, scaled))
    return dq, dot_grad(d_scores, q2), dot_grad(prob.astype(BF), d2)


def reach_bias(key_bias):
    shape = (WIN, 3 * WIN)
    offset = lax.broadcasted_iota(jnp.int32, shape, 1) - lax.broadcasted_iota(jnp.int32, shape, 0) - WIN
    near = (offset >= -WIN) & (offset <= WIN)
    inner = jnp.where(offset == 0, 0.0, jnp.broadcast_to(key_bias, shape))
    bias = jnp.where(near, inner, MASKED)
    return jnp.concatenate([bias, bias], axis=0)


def put_lse(lse, pair, column):
    lane = lax.broadcasted_iota(jnp.int32, lse.shape, 1)
    rows = lse.shape[0]
    lse = jnp.where(lane == 2 * pair, column[:rows], lse)
    return jnp.where(lane == 2 * pair + 1, column[rows:], lse)


def get_lse(lse, pair):
    return jnp.concatenate([lse[:, 2 * pair : 2 * pair + 1], lse[:, 2 * pair + 1 : 2 * pair + 2]], axis=0)


def attend_body(
    stages,
    x,
    gain,
    select,
    select_t,
    key_bias,
    heavy_bias,
    w_lqkv,
    w_hqkv,
    w_lout,
    w_hout,
    hidden,
    xn,
    lq,
    rim,
    lo_out,
    l_lse,
    a_rows,
    hq,
    kvh,
    ho,
    h_lse,
    ls,
    lr,
    rs,
    rr,
    ss,
    sr,
):
    hi, lo, x_, c = place()
    f = x_ * 2 + c
    tokens = x.shape[0]
    group, cap, width = select.shape
    wl, wh = HL * DH, HH * DH
    ones, scaled = pair_masks(1.0), pair_masks(SCORE_SCALE)
    across, partner = at(hi, lo, 1 - x_, c), at(hi, lo, x_, 1 - c)

    def norm(r):
        h = x[r, :].astype(F32)
        inv = lax.rsqrt(jnp.mean(h * h, axis=-1, keepdims=True) + EPSILON)
        xn[r, :] = (h * inv * gain[0:1, :]).astype(BF)

    tiles(tokens, 128, norm)
    for s in range(group):
        rows = dot(select[s], xn[s * width : (s + 1) * width, :]).astype(BF)
        a_rows[s * cap : (s + 1) * cap, :] = rows
    stages[0]()
    kv = dot(a_rows[...], w_hqkv[:, wh:]).astype(BF)
    for s in range(group):
        kvh[s, f] = kv[s * cap : (s + 1) * cap]
    mine = kvh.at[:, f]
    first = send(mine, mine, ss.at[0], sr.at[0], across)
    beside = send(mine, mine, ss.at[1], sr.at[1], partner)
    stages[1]()
    for s in range(group):
        rows = xn[s * width : (s + 1) * width, :]
        rim[s, WIN : WIN + width, :] = dot(rows, w_lqkv[:, wl:]).astype(BF)
    finish = rim_exchange(
        rim.at[:, pl.ds(WIN, WIN)],
        rim.at[:, pl.ds(width, WIN)],
        rim.at[:, pl.ds(0, WIN)],
        rim.at[:, pl.ds(width + WIN, WIN)],
        ls,
        lr,
        rs,
        rr,
    )
    hq[...] = dot(a_rows[...], w_hqkv[:, :wh]).astype(BF)
    for s in range(group):
        rows = slice(s * width, (s + 1) * width)
        lq[rows, :] = dot(xn[rows, :], w_lqkv[:, :wl]).astype(BF)
    stages[2]()
    first.wait()
    other = kvh.at[:, (1 - x_) * 2 + c]
    relay = send(other, other, ss.at[2], sr.at[2], partner)
    finish()
    stages[3]()
    blocks = width // WIN

    def light(i, carry):
        s, b = i // blocks, i % blocks
        r = pl.ds(pl.multiple_of(i * WIN, WIN), WIN)
        keys = pl.ds(pl.multiple_of(b * WIN, WIN), 3 * WIN)
        bias = reach_bias(key_bias[i])
        lse = jnp.zeros((WIN, 128), F32)
        for pair in range(HL // 2):
            at_k = slice(pair * 128, (pair + 1) * 128)
            at_v = slice(wl + pair * 128, wl + (pair + 1) * 128)
            o, column = pair_forward(
                lq[r, at_k], rim[s, keys, at_k], rim[s, keys, at_v], bias, ones, scaled
            )
            lo_out[r, at_k] = o
            lse = put_lse(lse, pair, column)
        l_lse[r, :] = lse
        return carry

    lax.fori_loop(0, group * blocks // 2, light, 0)
    stages[4]()
    lax.fori_loop(group * blocks // 2, group * blocks, light, 0)
    stages[5]()
    beside.wait()
    relay.wait()
    heavy_kv = kvh.reshape(group, 4 * cap, 2 * wh)

    def heavy(s, carry):
        r = pl.ds(pl.multiple_of(s * cap, cap), cap)
        bias = heavy_bias[s]
        bias = jnp.concatenate([bias, bias], axis=0)
        lse = jnp.zeros((cap, 128), F32)
        for pair in range(HH // 2):
            at_k = slice(pair * 128, (pair + 1) * 128)
            at_v = slice(wh + pair * 128, wh + (pair + 1) * 128)
            o, column = pair_forward(
                hq[r, at_k], heavy_kv[s, :, at_k], heavy_kv[s, :, at_v], bias, ones, scaled
            )
            ho[r, at_k] = o
            lse = put_lse(lse, pair, column)
        h_lse[r, :] = lse
        return carry

    lax.fori_loop(0, group, heavy, 0)
    stages[6]()
    high, low = halves(dot(ho[...], w_hout[...]))
    for s in range(group):
        r = slice(s * width, (s + 1) * width)
        q = slice(s * cap, (s + 1) * cap)
        hidden[r, :] = (
            x[r, :].astype(F32)
            + dot(lo_out[r, :], w_lout[...])
            + (dot(select_t[s], high[q]) + dot(select_t[s], low[q]))
        )


def attend_kernel(*refs):
    meet(line_peers())
    attend_body([lambda: None] * 7, *refs)


def attend_shapes(tokens, select):
    group, cap, width = select.shape
    wl, wh = HL * DH, HH * DH
    rows = group * cap
    return [
        jax.ShapeDtypeStruct((tokens, D), F32),
        jax.ShapeDtypeStruct((tokens, D), BF),
        jax.ShapeDtypeStruct((tokens, wl), BF),
        jax.ShapeDtypeStruct((group, width + 2 * WIN, 2 * wl), BF),
        jax.ShapeDtypeStruct((tokens, wl), BF),
        jax.ShapeDtypeStruct((tokens, 128), F32),
        jax.ShapeDtypeStruct((rows, D), BF),
        jax.ShapeDtypeStruct((rows, wh), BF),
        jax.ShapeDtypeStruct((group, 4, cap, 2 * wh), BF),
        jax.ShapeDtypeStruct((rows, wh), BF),
        jax.ShapeDtypeStruct((rows, 128), F32),
    ]


ATTEND_SEMS = [DMA, DMA, DMA, DMA, DMA((3,)), DMA((3,))]


def attend(x, gain, select, select_t, key_bias, heavy_bias, w_lqkv, w_hqkv, w_lout, w_hout):
    operands = [x, gain, select, select_t, key_bias, heavy_bias, w_lqkv, w_hqkv, w_lout, w_hout]
    shapes = attend_shapes(x.shape[0], select)
    return call(
        attend_kernel,
        shapes,
        operands,
        [VM] * len(operands),
        [VM] * len(shapes),
        ATTEND_SEMS,
        2,
    )


def route_part(deal, lengths, routes_a, routes_f, scores, tables):
    sel_a, selt_a, key_bias, heavy_bias, sel_f, selt_f, score, mask, scale = tables
    hi, lo, x, c = place()
    group, cap, width = sel_a.shape
    seqs = deal.shape[1]
    here = ((x * 2 + c) * width).astype(F32)

    def line(shape, dim):
        return lax.broadcasted_iota(jnp.int32, shape, dim).astype(F32)

    lane = lax.broadcasted_iota(jnp.int32, (1, seqs), 1)
    before = jnp.where(line((width, width), 0) > line((width, width), 1), 1.0, 0.0).astype(BF)
    length_row = lengths[...].astype(F32)
    count = jnp.sum(length_row, axis=1, keepdims=True)
    column = line((width, 1), 0)
    row = line((1, width), 1)
    ones = jnp.ones((8, routes_a.shape[1]), BF)

    def columns_of(routes, base):
        held = jnp.where(routes == column + base, 1.0, 0.0)
        rank = jnp.sum(dot(before, held.astype(BF)), axis=1, keepdims=True)
        there = jnp.sum(held, axis=1, keepdims=True)
        hot_t = jnp.where(rank == line((width, cap), 1), 1.0, 0.0) * there
        return held, rank, hot_t

    def rows_of(held):
        there = dot_back(ones, held.astype(BF))
        rank = dot_back(there.astype(BF), before)
        return jnp.where(rank[:1] == line((cap, width), 0), 1.0, 0.0) * there[:1]

    for s in range(group):
        place_here = lane == (hi * 2 + lo) * group + s
        which = jnp.sum(jnp.where(place_here, deal[...].astype(F32), 0.0), axis=1, keepdims=True)
        one = line((seqs, 1), 0) == which
        length = jnp.sum(
            jnp.where(line((1, seqs), 1) == which, length_row, 0.0), axis=1, keepdims=True
        )
        ra, rf, sf = (
            jnp.sum(jnp.where(one, ref[...].astype(F32), 0.0), axis=0, keepdims=True)
            for ref in (routes_a, routes_f, scores)
        )
        held, rank, hot_t = columns_of(ra, here)
        hot = rows_of(held)
        sel_a[s] = hot.astype(BF)
        selt_a[s] = hot_t.astype(BF)
        own_spot = jnp.sum(hot * (row + here + 1.0), axis=1, keepdims=True) - 1.0
        for q in range(4):
            base = float(q * width)
            _, _, other_t = columns_of(ra, base)
            spot = jnp.sum(other_t * (column + base + 1.0), axis=0, keepdims=True) - 1.0
            live = jnp.where((spot >= 0.0) & (spot < length), 1.0, 0.0)
            same = jnp.where(own_spot == spot, 1.0, 0.0)
            heavy_bias[s, :, q * cap : (q + 1) * cap] = jnp.where(live + same > 0.0, 0.0, MASKED)
        for b in range(width // WIN):
            key = line((1, 3 * WIN), 1) + (here + float((b - 1) * WIN))
            live = (key >= 0.0) & (key < length)
            key_bias[s * (width // WIN) + b] = jnp.where(live, 0.0, MASKED)
        valid = jnp.where(column + here < length, 1.0, 0.0)
        mask[s * width : (s + 1) * width, :] = valid
        scale[s * width : (s + 1) * width, :] = 2.0 * valid / (D * count)
        held, rank, hot_t = columns_of(rf, here)
        sel_f[s] = rows_of(held).astype(BF)
        selt_f[s] = hot_t.astype(BF)
        slot = jnp.sum(held * rank, axis=0, keepdims=True)
        owned = jnp.sum(held, axis=0, keepdims=True)
        hits = jnp.where(slot == line((cap, slot.shape[1]), 0), 1.0, 0.0)
        score[s * cap : (s + 1) * cap, :] = jnp.sum(hits * (owned * sf), axis=1, keepdims=True)


def route_shapes(group, width, tokens):
    return [
        jax.ShapeDtypeStruct((group, CAP, width), BF),
        jax.ShapeDtypeStruct((group, width, CAP), BF),
        jax.ShapeDtypeStruct((tokens // WIN, 1, 3 * WIN), F32),
        jax.ShapeDtypeStruct((group, CAP, 4 * CAP), F32),
        jax.ShapeDtypeStruct((group, CAP, width), BF),
        jax.ShapeDtypeStruct((group, width, CAP), BF),
        jax.ShapeDtypeStruct((group * CAP, 1), F32),
        jax.ShapeDtypeStruct((tokens, 1), F32),
        jax.ShapeDtypeStruct((tokens, 1), F32),
    ]


def gather_attend_kernel(dp, nw, *refs):
    n_in, n_out = 7 + nw, 2 + nw + 21
    ins, outs, rest = refs[:n_in], list(refs[n_in : n_in + n_out]), refs[n_in + n_out :]
    count = len(STAGED)
    held, flush_sem, rest = rest[:count], rest[count], rest[count + 1 :]
    final = [outs[k] for k in STAGED]
    for k, ref in zip(STAGED, held):
        outs[k] = ref
    flushed = []

    def flush(*which):
        for k in which:
            n = STAGED.index(k)
            flushed.append(keep(held[n], final[n], flush_sem.at[n]))

    xin, ws, hin = ins[0], ins[1 : 1 + nw], ins[1 + nw]
    integers = ins[2 + nw :]
    xo, wos, hin_o = outs[0], outs[1 : 1 + nw], outs[1 + nw]
    gain, tables, saved = outs[2 + nw], outs[3 + nw : 12 + nw], outs[12 + nw :]
    parts, rest = rest[: 3 * nw + 3], rest[3 * nw + 3 :]
    halves = (parts[:nw], parts[nw : 2 * nw], parts[2 * nw : 3 * nw], parts[3 * nw :])
    g = Gather(dp, xin, ws, hin, xo, wos, hin_o, rest[:11], halves)
    g.meet()
    for w in range(nw):
        g.swap(w)
    g.join(0)
    g.join(2)
    g.plane(0)
    g.plane(2)
    g.join(1)
    g.rows()
    route_part(*integers, tables)
    g.cross(0)
    g.cross(2)
    g.core(0)
    g.plane(1)
    g.core(2)
    g.ready(0)
    total = jnp.zeros(gain.shape, F32)
    for z in range(dp // 2):
        for l2, x2 in ((0, 0), (0, 1), (1, 0), (1, 1)):
            pair = wos[0][z, l2, x2].astype(F32)
            total += pair[:8] + pair[8:]
    gain[...] = total
    g.rows_ready()
    for w in (4, 3, 5, 6):
        g.join(w)
    g.heavy_plane()
    flush(0)

    def heavy_projection():
        g.cross(1)
        g.ready(2)
        flush(20, 3)

    def light_projection():
        g.core(1)
        g.ready(1)
        flush(2)

    def keys_travel():
        g.plane(4)
        g.plane(3)
        g.heavy_line()
        flush(21)

    def keys_there():
        g.plane(5)
        g.plane(6)
        flush(22)

    def half_way():
        g.cross(4)
        g.cross(3)

    def light_done():
        g.core(4)
        g.core(3)
        g.cross(5)
        g.cross(6)
        flush(23)

    def heavy_done():
        g.ready(4)
        g.ready(3)
        flush(27, 4, 5)

    full = [wos[w].reshape(-1, wos[w].shape[-1]) for w in range(nw)]
    stages = [
        heavy_projection,
        light_projection,
        keys_travel,
        keys_there,
        half_way,
        light_done,
        heavy_done,
    ]
    attend_body(
        stages,
        xo.reshape(-1, D),
        gain,
        *tables[:4],
        full[1],
        full[2],
        full[3],
        full[4],
        *saved,
        *rest[11:],
    )
    g.core(5)
    g.core(6)
    g.ready(5)
    g.ready(6)
    g.heavy_ready()
    for copy in flushed:
        copy.wait()


STAGED = (0, 2, 3, 4, 5, 20, 21, 22, 23, 27)


def gather_attend(dp, xin, weights, hin, integers):
    nw = len(weights)
    shapes = gather_shapes(dp, xin, weights, hin, True)
    group, width = shapes[0].shape[0], dp * xin.shape[1]
    tables = route_shapes(group, width, group * width)
    shapes.append(jax.ShapeDtypeStruct((8, D), F32))
    shapes += tables
    shapes += attend_shapes(group * width, tables[0])
    return call(
        functools.partial(gather_attend_kernel, dp, nw),
        shapes,
        [xin, *weights, hin, *integers],
        [ANY] * (2 + nw) + [VM] * 5,
        [ANY if k in STAGED + (6, 7, 8) else VM for k in range(len(shapes))],
        [pltpu.VMEM(shapes[k].shape, BF) for k in STAGED]
        + [DMA((len(STAGED),))]
        + [pltpu.VMEM((w.shape[0], w.shape[1] // 2), BF) for w in weights] * 2
        + [pltpu.VMEM((2 * w.shape[0], w.shape[1] // 2), BF) for w in weights]
        + [DMA((nw,))] * 3
        + gather_sems(dp, nw)
        + ATTEND_SEMS,
        1,
    )


def attend_back_body(
    stages,
    d_hidden,
    x,
    gain,
    select,
    select_t,
    key_bias,
    heavy_bias,
    w_lqkv,
    w_hqkv,
    w_lout,
    w_hout,
    xn,
    lq,
    rim,
    lo_out,
    l_lse,
    a_rows,
    hq,
    kvh,
    ho,
    h_lse,
    g_lqkv,
    g_hqkv,
    g_lout,
    g_hout,
    dx,
    stats,
    d_ho,
    d_hproj,
    part,
    got,
    far,
    d_la,
    d_lo,
    d_rim,
    edge,
    edge_in,
    d_lproj,
    ls,
    lr,
    rs,
    rr,
    ss,
    sr,
):
    hi, lo, x_, c = place()
    tokens = x.shape[0]
    group, cap, width = select.shape
    wl, wh = HL * DH, HH * DH
    ones, scaled = pair_masks(1.0), pair_masks(SCORE_SCALE)
    across, partner = at(hi, lo, 1 - x_, c), at(hi, lo, x_, 1 - c)
    picked = []
    for s in range(group):
        high, low = halves(d_hidden[s * width : (s + 1) * width, :])
        picked.append((dot(select[s], high) + dot(select[s], low)).astype(BF))
    d_ha = jnp.concatenate(picked, axis=0)
    d_ho[...] = dot_back(d_ha, w_hout[...]).astype(BF)
    heavy_kv = kvh.reshape(group, 4 * cap, 2 * wh)
    part_kv = part.reshape(group, 4 * cap, 2 * wh)

    def heavy(s, carry):
        r = pl.ds(pl.multiple_of(s * cap, cap), cap)
        bias = heavy_bias[s]
        bias = jnp.concatenate([bias, bias], axis=0)
        lse = h_lse[r, :]
        for pair in range(HH // 2):
            at_k = slice(pair * 128, (pair + 1) * 128)
            at_v = slice(wh + pair * 128, wh + (pair + 1) * 128)
            dq, dk, dv = pair_backward(
                hq[r, at_k],
                heavy_kv[s, :, at_k],
                heavy_kv[s, :, at_v],
                bias,
                get_lse(lse, pair),
                d_ho[r, at_k],
                ones,
                scaled,
            )
            d_hproj[r, at_k] = dq.astype(BF)
            part_kv[s, :, at_k] = dk.astype(BF)
            part_kv[s, :, at_v] = dv.astype(BF)
        return carry

    lax.fori_loop(0, group, heavy, 0)
    beside = [
        send(part.at[:, b * 2 + 1 - c], got.at[b], ss.at[b], sr.at[b], partner) for b in (0, 1)
    ]
    g_hout[...] = dot_grad(ho[...], d_ha).astype(BF)
    stages[0]()

    def light_out_back(r):
        d = d_hidden[r, :].astype(BF)
        d_la[r, :] = d
        d_lo[r, :] = dot_back(d, w_lout[...]).astype(BF)

    tiles(tokens, 256, light_out_back)
    g_lout[...] = dot_grad(lo_out[...], d_la[...]).astype(BF)
    stages[1]()
    for copy in beside:
        copy.wait()
    for b in (0, 1):
        got[b] = (got[b].astype(F32) + part[:, b * 2 + c].astype(F32)).astype(BF)
    third = send(got.at[1 - x_], far, ss.at[2], sr.at[2], across)
    stages[2]()
    d_rim[...] = jnp.zeros(d_rim.shape, F32)
    blocks = width // WIN

    def light(i, carry):
        s, b = i // blocks, i % blocks
        r = pl.ds(pl.multiple_of(i * WIN, WIN), WIN)
        keys = pl.ds(pl.multiple_of(b * WIN, WIN), 3 * WIN)
        bias = reach_bias(key_bias[i])
        lse = l_lse[r, :]
        for pair in range(HL // 2):
            at_k = slice(pair * 128, (pair + 1) * 128)
            at_v = slice(wl + pair * 128, wl + (pair + 1) * 128)
            dq, dk, dv = pair_backward(
                lq[r, at_k],
                rim[s, keys, at_k],
                rim[s, keys, at_v],
                bias,
                get_lse(lse, pair),
                d_lo[r, at_k],
                ones,
                scaled,
            )
            d_lproj[r, at_k] = dq.astype(BF)
            d_rim[s, keys, at_k] += dk
            d_rim[s, keys, at_v] += dv
        return carry

    lax.fori_loop(0, group * blocks // 2, light, 0)
    third.wait()
    total = (got[x_].astype(F32) + far[...].astype(F32)).astype(BF)
    for s in range(group):
        d_hproj[s * cap : (s + 1) * cap, wh:] = total[s]

    def heavy_grad(j):
        g_hqkv[:, j] = dot_grad(a_rows[...], d_hproj[:, j]).astype(BF)

    tiles(3 * wh, 768, heavy_grad)
    stages[3]()
    lax.fori_loop(group * blocks // 2, group * blocks, light, 0)
    edge[0] = d_rim[:, :WIN, :].astype(BF)
    edge[1] = d_rim[:, WIN + width :, :].astype(BF)
    finish = rim_exchange(
        edge.at[0], edge.at[1], edge_in.at[0], edge_in.at[1], ls, lr, rs, rr
    )
    stages[4]()
    d_high, d_low = halves(dot_back(d_hproj[...], w_hqkv[...]))
    finish()
    for s in range(group):
        d_rim[s, WIN : 2 * WIN, :] += edge_in[0, s].astype(F32)
        d_rim[s, width : width + WIN, :] += edge_in[1, s].astype(F32)
        d_lproj[s * width : (s + 1) * width, wl:] = d_rim[s, WIN : WIN + width, :].astype(BF)

    def light_grad(j):
        g_lqkv[:, j] = dot_grad(xn[...], d_lproj[:, j]).astype(BF)

    tiles(3 * wl, 768, light_grad)
    stages[5]()
    stats[...] = jnp.zeros(stats.shape, F32)
    for s in range(group):
        r = slice(s * width, (s + 1) * width)
        q = slice(s * cap, (s + 1) * cap)
        d = dot_back(d_lproj[r, :], w_lqkv[...]) + (
            dot(select_t[s], d_high[q]) + dot(select_t[s], d_low[q])
        )
        h = x[r, :].astype(F32)
        inv = lax.rsqrt(jnp.mean(h * h, axis=-1, keepdims=True) + EPSILON)
        dh = d * h
        stats[0:1, :] += jnp.sum(dh * inv, axis=0, keepdims=True)
        mean = jnp.mean(gain[0:1, :] * dh, axis=-1, keepdims=True)
        dx[r, :] = (
            d_hidden[r, :] + inv * gain[0:1, :] * d - h * (inv * inv * inv * mean)
        ).astype(BF)
    stages[6]()


def attend_back_kernel(*refs):
    meet(line_peers())
    attend_back_body([lambda: None] * 7, *refs)


def attend_back_scratch(tokens, select):
    group, cap, width = select.shape
    wl, wh = HL * DH, HH * DH
    rows = group * cap
    return [
        pltpu.VMEM((rows, wh), BF),
        pltpu.VMEM((rows, 3 * wh), BF),
        pltpu.VMEM((group, 4, cap, 2 * wh), BF),
        pltpu.VMEM((2, group, cap, 2 * wh), BF),
        pltpu.VMEM((group, cap, 2 * wh), BF),
        pltpu.VMEM((tokens, D), BF),
        pltpu.VMEM((tokens, wl), BF),
        pltpu.VMEM((group, width + 2 * WIN, 2 * wl), F32),
        pltpu.VMEM((2, group, WIN, 2 * wl), BF),
        pltpu.VMEM((2, group, WIN, 2 * wl), BF),
        pltpu.VMEM((tokens, 3 * wl), BF),
    ] + ATTEND_SEMS


def attend_back(d_hidden, x, gain, select, select_t, key_bias, heavy_bias, weights, saved):
    tokens = x.shape[0]
    wl, wh = HL * DH, HH * DH
    operands = [d_hidden, x, gain, select, select_t, key_bias, heavy_bias, *weights, *saved]
    shapes = [
        jax.ShapeDtypeStruct((D, 3 * wl), BF),
        jax.ShapeDtypeStruct((D, 3 * wh), BF),
        jax.ShapeDtypeStruct((wl, D), BF),
        jax.ShapeDtypeStruct((wh, D), BF),
        jax.ShapeDtypeStruct((tokens, D), BF),
        jax.ShapeDtypeStruct((8, D), F32),
    ]
    return call(
        attend_back_kernel,
        shapes,
        operands,
        [VM] * len(operands),
        [VM] * len(shapes),
        attend_back_scratch(tokens, select),
        3,
    )


def scatter_kernel(dp, nw, *refs):
    nz = dp // 2
    dx, stats, gs, hin = refs[0], refs[1], refs[2 : 2 + nw], refs[2 + nw]
    outs = refs[3 + nw :]
    dxo, total, gos, hin_o = outs[0], outs[1], outs[2 : 2 + nw], outs[2 + nw]
    scr = outs[3 + nw :]
    nears, fars, sums, ends = (scr[i * nw : (i + 1) * nw] for i in range(4))
    hin_r, hin_s, sc, sp, sz, acc, acc2 = scr[4 * nw : 4 * nw + 7]
    own, xs, xr, cs, cr, ps, pr, zs, zr, hs, hr, ts, tr = scr[4 * nw + 7 :]
    hi, lo, x, c = place()
    d = hi * 2 + lo
    f = x * 2 + c
    plane = (lo * 2 + x) * 2 + c
    dp_peers = [(lax.rem(d + k, dp), f) for k in range(1, dp)]
    rest = [(a, b, e) for a in (0, 1) for b in (0, 1) for e in (0, 1) if a or b or e]
    flat8 = []
    for a, b, e in rest:
        l2 = 1 - lo if a else lo
        x2 = 1 - x if b else x
        c2 = 1 - c if e else c
        flat8.append((l2, x2, c2))
    meet(dp_peers + [at(hi, *p) for (a, b, e), p in zip(rest, flat8) if b or e])
    partner = at(hi, lo, x, 1 - c)
    quad = quad_peers()
    z_index = [lax.rem(hi + k, nz) for k in range(1, nz)]
    z_peers = [at(z, lo, x, c) for z in z_index]
    c_sends = [
        send(gs[w].at[:, :, :, 1 - c], nears[w], cs.at[w], cr.at[w], partner) for w in range(nw)
    ]
    t_c = send(stats, sc, ts.at[0], tr.at[0], partner)
    mine = keep(dx.at[:, d], dxo.at[d], own)
    x_sends = [
        send(dx.at[:, peer[0]], dxo.at[d], xs.at[k], xr.at[k], peer)
        for k, peer in enumerate(dp_peers)
    ]
    h_sends = []
    for k, z in enumerate(z_index):
        h_sends.append(send(hin.at[z], hin_r.at[k], hs.at[1, k], hr.at[1, k], z_peers[k]))
    p_sends, z_sends = [], []
    t_c.wait()
    acc[...] = stats[...] + sc[...]
    t_p = [
        send(acc, sp.at[k], ts.at[1 + k], tr.at[1 + k], at(hi, l2, x2, c))
        for k, (l2, x2) in enumerate(quad)
    ]

    def add_core(w):
        c_sends[w].wait()
        near, g = nears[w], gs[w]

        def body(i, carry):
            z, a, b = i // 4, (i // 2) % 2, i % 2
            near[z, a, b] = (near[z, a, b].astype(F32) + g[z, a, b, c].astype(F32)).astype(BF)
            return carry

        lax.fori_loop(0, nz * 4, body, 0)
        p_sends.append(
            [
                send(near.at[:, l2, x2], fars[w].at[k], ps.at[w, k], pr.at[w, k], at(hi, l2, x2, c))
                for k, (l2, x2) in enumerate(quad)
            ]
        )

    def add_plane(w):
        for copy in p_sends[w]:
            copy.wait()
        near, far, part = nears[w], fars[w], sums[w]

        def body(z, carry):
            part[z] = (
                near[z, lo, x].astype(F32)
                + far[0, z].astype(F32)
                + far[1, z].astype(F32)
                + far[2, z].astype(F32)
            ).astype(BF)
            return carry

        lax.fori_loop(0, nz, body, 0)
        z_sends.append(
            [
                send(part.at[z], ends[w].at[k], zs.at[w, k], zr.at[w, k], z_peers[k])
                for k, z in enumerate(z_index)
            ]
        )

    def add_line(w):
        for copy in z_sends[w]:
            copy.wait()
        gos[w][...] = sums[w][hi].astype(F32)
        for k in range(nz - 1):
            gos[w][...] += ends[w][k].astype(F32)

    for w in range(nw):
        add_core(w)
        if w >= 2:
            add_plane(w - 2)
    for copy in t_p:
        copy.wait()
    acc2[...] = acc[...] + sp[0] + sp[1] + sp[2]
    t_z = [send(acc2, sz.at[k], ts.at[4 + k], tr.at[4 + k], z_peers[k]) for k in range(nz - 1)]
    for copy in h_sends:
        copy.wait()

    def body(i, carry):
        value = hin[hi, i].astype(F32)
        for k in range(nz - 1):
            value += hin_r[k, i].astype(F32)
        hin_s[i] = value.astype(BF)
        return carry

    lax.fori_loop(0, 8, body, 0)
    hin_o[plane] = hin_s[plane]
    a_sends = [
        send(
            hin_s.at[(l2 * 2 + x2) * 2 + c2],
            hin_o.at[plane],
            hs.at[0, k],
            hr.at[0, k],
            at(hi, l2, x2, c2),
        )
        for k, (l2, x2, c2) in enumerate(flat8)
    ]
    for w in range(max(nw - 2, 0), nw):
        add_plane(w)
    for copy in t_z:
        copy.wait()
    total[...] = acc2[...]
    for k in range(nz - 1):
        total[...] += sz[k]
    for w in range(nw):
        add_line(w)
    mine.wait()
    for copy in x_sends + a_sends:
        copy.wait()


def scatter_all(dp, dx, stats, grads, hin):
    nz = dp // 2
    nw = len(grads)
    group, _, rows, _ = dx.shape
    tiles = [g.shape[4:] for g in grads]
    most = max(7, nz)
    scratch = [pltpu.VMEM((nz, 2, 2) + t, BF) for t in tiles]
    scratch += [pltpu.VMEM((3, nz) + t, BF) for t in tiles]
    scratch += [pltpu.VMEM((nz,) + t, BF) for t in tiles]
    scratch += [pltpu.VMEM((nz - 1,) + t, BF) for t in tiles]
    scratch += [
        pltpu.VMEM((nz - 1,) + hin.shape[1:], BF),
        pltpu.VMEM(hin.shape[1:], BF),
        pltpu.VMEM(stats.shape, F32),
        pltpu.VMEM((3,) + stats.shape, F32),
        pltpu.VMEM((nz - 1,) + stats.shape, F32),
        pltpu.VMEM(stats.shape, F32),
        pltpu.VMEM(stats.shape, F32),
        DMA,
        DMA((dp,)),
        DMA((dp,)),
        DMA((nw,)),
        DMA((nw,)),
        DMA((nw, 3)),
        DMA((nw, 3)),
        DMA((nw, nz)),
        DMA((nw, nz)),
        DMA((3, most)),
        DMA((3, most)),
        DMA((4 + nz,)),
        DMA((4 + nz,)),
    ]
    shapes = [jax.ShapeDtypeStruct((dp, group, rows, D), BF), jax.ShapeDtypeStruct(stats.shape, F32)]
    shapes += [jax.ShapeDtypeStruct(t, F32) for t in tiles]
    shapes.append(jax.ShapeDtypeStruct(hin.shape[1:], BF))
    return call(
        functools.partial(scatter_kernel, dp, nw),
        shapes,
        [dx, stats, *grads, hin],
        [ANY] + [VM] * (2 + nw),
        [ANY] + [VM] * (2 + nw),
        scratch,
        4,
    )


class Scatter:
    def __init__(self, nz, shards, gs, near, one, two, end, sems):
        self.nz, self.shards, self.gs = nz, shards, gs
        self.near, self.one, self.two, self.end = near, one, two, end
        self.cs, self.cr, self.ps, self.pr, self.zs, self.zr = sems
        self.hi, self.lo, self.x, self.c = hi, lo, x, c = place()
        self.partner = at(hi, lo, x, 1 - c)
        self.by_x, self.by_y = at(hi, lo, 1 - x, c), at(hi, 1 - lo, x, c)
        self.z_index = [lax.rem(hi + k, nz) for k in range(1, nz)]
        self.copies = {}

    def lanes(self, w, c):
        half = self.shards[w][1] // 2
        return pl.ds(pl.multiple_of(c * half, 128), half)

    def core(self, w):
        out = self.gs[w].at[:, :, :, :, self.lanes(w, 1 - self.c)]
        self.copies[w, 0] = [send(out, self.near[w], self.cs.at[w], self.cr.at[w], self.partner)]

    def wait(self, w, stage):
        for copy in self.copies[w, stage]:
            copy.wait()

    def plane(self, w):
        g, own = self.gs[w], self.lanes(w, self.c)
        self.add_plane(w, lambda z, a, b: g[z, a, b, :, own])

    def own_plane(self, w, kept):
        self.add_plane(w, lambda z, a, b: kept[z, a, b])

    def add_plane(self, w, own):
        self.wait(w, 0)
        near = self.near[w]
        lo, x, half = self.lo, self.x, self.nz // 2

        def body(i, carry):
            z, a, b = i // 4, (i // 2) % 2, i % 2
            near[z, a, b] = (near[z, a, b].astype(F32) + own(z, a, b).astype(F32)).astype(BF)
            return carry

        lax.fori_loop(0, self.nz * 4, body, 0)
        low, high = pl.ds(0, half), pl.ds(half, self.nz - half)
        self.copies[w, 1] = [
            send(near.at[low, :, 1 - x], self.one[w].at[low], self.ps.at[w, 0], self.pr.at[w, 0], self.by_x),
            send(near.at[high, 1 - lo], self.one[w].at[high], self.ps.at[w, 1], self.pr.at[w, 1], self.by_y),
        ]

    def cross(self, w):
        self.wait(w, 1)
        near, one, lo, x, half = self.near[w], self.one[w], self.lo, self.x, self.nz // 2

        def low_body(i, carry):
            z, a = i // 2, i % 2
            near[z, a, x] = (near[z, a, x].astype(F32) + one[z, a].astype(F32)).astype(BF)
            return carry

        def high_body(i, carry):
            z, b = half + i // 2, i % 2
            near[z, lo, b] = (near[z, lo, b].astype(F32) + one[z, b].astype(F32)).astype(BF)
            return carry

        lax.fori_loop(0, half * 2, low_body, 0)
        lax.fori_loop(0, (self.nz - half) * 2, high_body, 0)
        low, high = pl.ds(0, half), pl.ds(half, self.nz - half)
        two = self.two[w]
        self.copies[w, 2] = [
            send(near.at[low, 1 - lo, x], two.at[low], self.ps.at[w, 2], self.pr.at[w, 2], self.by_y),
            send(near.at[high, lo, 1 - x], two.at[high], self.ps.at[w, 3], self.pr.at[w, 3], self.by_x),
        ]

    def line(self, w):
        self.wait(w, 2)
        near, part, lo, x = self.near[w], self.two[w], self.lo, self.x

        def body(z, carry):
            part[z] = (near[z, lo, x].astype(F32) + part[z].astype(F32)).astype(BF)
            return carry

        lax.fori_loop(0, self.nz, body, 0)
        self.copies[w, 3] = [
            send(
                part.at[z],
                self.end[w].at[k],
                self.zs.at[w, k],
                self.zr.at[w, k],
                at(z, lo, x, self.c),
            )
            for k, z in enumerate(self.z_index)
        ]

    def last(self, w, fin, out, sems):
        self.wait(w, 3)
        value = self.two[w][self.hi].astype(F32)
        for k in range(self.nz - 1):
            value += self.end[w][k].astype(F32)
        fin[...] = value
        count = self.shards[w][0]
        own = pl.ds(pl.multiple_of(self.c * count, 8), count)
        mate = pl.ds(pl.multiple_of((1 - self.c) * count, 8), count)
        spot = out.at[:, self.lanes(w, self.c)]
        return [
            keep(fin.at[own], spot, sems[0].at[w]),
            send(fin.at[mate], spot, sems[1].at[w], sems[2].at[w], self.partner),
        ]


def back_scatter_kernel(dp, shards, *refs):
    nz, nw = dp // 2, len(shards)
    n_ops = 7 + 4 + 10
    ops, (g_lin, g_ldn, hin, ffn_stats) = refs[:n_ops], refs[n_ops : n_ops + 4]
    outs, rest = refs[n_ops + 4 : n_ops + 7 + nw], refs[n_ops + 7 + nw :]
    dxo, total, gos, hin_o = outs[0], outs[1], outs[2 : 2 + nw], outs[2 + nw]
    count = len(FETCHED)
    held, fetch_sem, rest = rest[:count], rest[count], rest[count + 1 :]
    sources, ops = [ops[k] for k in FETCHED], list(ops)
    for k, ref in zip(FETCHED, held):
        ops[k] = ref
    full, rest = rest[:4], rest[4:]
    own_lin, own_ldn, stats, rest = rest[0], rest[1], rest[2], rest[3:]
    back, rest = rest[:17], rest[17:]
    dx = back[5]
    near, one, two, end, fin = (rest[k * nw : (k + 1) * nw] for k in range(5))
    hin_own, hin_r, acc, sc, sp, sz, acc2 = rest[5 * nw : 5 * nw + 7]
    own, xs, xr, cs, cr, ps, pr, zs, zr, hs, hr, ts, tr, *fsem = rest[5 * nw + 7 :]
    hi, lo, x, c = place()
    d = hi * 2 + lo
    plane = (lo * 2 + x) * 2 + c
    others = plane_others()
    rows_to = [(lax.rem(d + k, dp), x * 2 + c) for k in range(1, dp)]
    z_index = [lax.rem(hi + k, nz) for k in range(1, nz)]
    z_to = [at(z, lo, x, c) for z in z_index]
    quad = quad_peers()
    g_views = [g_lin, g_ldn]
    for k, w in enumerate((2, 3, 4, 5)):
        rows, columns = shards[w]
        g_views.append(full[k].reshape(nz, 2, 2, 2 * rows, columns))
    t = Scatter(nz, shards, g_views, near, one, two, end, (cs, cr, ps, pr, zs, zr))
    meet(rows_to + [at(hi, *q[:3]) for q in others if q[3]])
    fetched = {
        k: keep(source, ref, fetch_sem.at[n])
        for n, (k, source, ref) in enumerate(zip(FETCHED, sources, held))
    }

    def fetch(*which):
        for k in which:
            fetched[k].wait()

    h_sends = []
    for k, z in enumerate(z_index):
        h_sends.append(send(hin.at[z], hin_r.at[k], hs.at[1, k], hr.at[1, k], z_to[k]))
    t.core(0)
    t.core(1)
    kept = [
        keep(g_lin.at[:, :, :, :, t.lanes(0, c)], own_lin, own.at[0]),
        keep(g_ldn.at[:, :, :, :, t.lanes(1, c)], own_ldn, own.at[1]),
        keep(hin.at[hi], hin_own, own.at[2]),
    ]
    late = []

    def first_plane():
        fetch(9, 14)
        kept[0].wait()
        kept[1].wait()
        t.own_plane(0, own_lin)
        t.own_plane(1, own_ldn)
        t.core(2)

    def out_core():
        t.core(3)

    def before_light():
        fetch(12, 13)

    def half_way():
        t.core(4)
        t.cross(0)
        t.cross(1)
        t.plane(2)
        t.plane(3)

    def rims_left():
        fetch(8, 11)
        t.plane(4)
        t.line(0)
        t.line(1)
        t.cross(2)
        t.cross(3)

    def light_grad_done():
        t.core(5)
        fetch(7, 1)

    def rows_done():
        rows = dx.reshape(dxo.shape[1], dp, dxo.shape[2], D)
        late.append(keep(rows.at[:, d], dxo.at[d], own.at[4]))
        for k, to in enumerate(rows_to):
            late.append(send(rows.at[:, to[0]], dxo.at[d], xs.at[k], xr.at[k], to))

    stages = [
        first_plane,
        out_core,
        before_light,
        half_way,
        rims_left,
        light_grad_done,
        rows_done,
    ]
    attend_back_body(
        stages, *ops, full[3], full[2], full[1], full[0], dx, stats, *back
    )
    partner = at(hi, lo, x, 1 - c)
    for k in range(6):
        lanes = slice(k * 128, (k + 1) * 128)
        acc[k : k + 1, :] = stats[0:1, lanes]
        acc[6 + k : 7 + k, :] = ffn_stats[0:1, lanes]
    loss = jnp.sum(ffn_stats[1:2, :], axis=-1, keepdims=True)
    acc[12:16, :] = jnp.broadcast_to(loss, (4, 128))
    t_c = send(acc, sc, ts.at[0], tr.at[0], partner)
    t.plane(5)
    t.line(2)
    t.line(3)
    t.cross(4)
    t_c.wait()
    acc2[...] = acc[...] + sc[...]
    t_p = [
        send(acc2, sp.at[k], ts.at[1 + k], tr.at[1 + k], at(hi, l2, x2, c))
        for k, (l2, x2) in enumerate(quad)
    ]
    t.line(4)
    for copy in h_sends + kept[2:]:
        copy.wait()

    def body(i, carry):
        value = hin_own[i].astype(F32)
        for k in range(nz - 1):
            value += hin_r[k, i].astype(F32)
        hin_own[i] = value.astype(BF)
        return carry

    lax.fori_loop(0, 8, body, 0)
    hin_o[plane] = hin_own[plane]
    late += [
        send(
            hin_own.at[(q[0] * 2 + q[1]) * 2 + q[2]],
            hin_o.at[plane],
            hs.at[0, k],
            hr.at[0, k],
            at(hi, *q[:3]),
        )
        for k, q in enumerate(others)
    ]
    t.cross(5)
    for copy in t_p:
        copy.wait()
    acc[...] = acc2[...] + sp[0] + sp[1] + sp[2]
    t_z = [send(acc, sz.at[k], ts.at[4 + k], tr.at[4 + k], z_to[k]) for k in range(nz - 1)]
    t.line(5)
    for w in range(nw):
        late += t.last(w, fin[w], gos[w], fsem)
    for copy in t_z:
        copy.wait()
    value = acc[...]
    for k in range(nz - 1):
        value += sz[k]
    total[...] = value
    for copy in late:
        copy.wait()


FETCHED = (9, 14, 12, 13, 8, 11, 7, 1)


def back_scatter(dp, rows, d_hidden, x, gain, masks, weights, saved, ffn_grads, ffn_stats, shards, hin):
    nz, nw = dp // 2, len(shards)
    tokens = x.shape[0]
    group = masks[0].shape[0]
    most = max(7, nz)
    stat_shape = (16, 128)
    paired = [
        g.reshape(nz, 2, 2, 2 * s[0], s[1]) for g, s in zip(ffn_grads, shards)
    ]
    operands = [d_hidden, x, gain, *masks, *weights, *saved, *paired, hin, ffn_stats]
    shapes = [jax.ShapeDtypeStruct((dp, group, rows, D), BF), jax.ShapeDtypeStruct(stat_shape, F32)]
    shapes += [jax.ShapeDtypeStruct(s, F32) for s in shards]
    shapes.append(jax.ShapeDtypeStruct(hin.shape[1:], BF))
    scratch = [pltpu.VMEM(operands[k].shape, operands[k].dtype) for k in FETCHED]
    scratch.append(DMA((len(FETCHED),)))
    scratch += [pltpu.VMEM((s[0] * 8 * nz, s[1]), BF) for s in shards[2:]]
    split = [(2 * s[0], s[1] // 2) for s in shards]
    scratch += [pltpu.VMEM((nz, 2, 2) + s, BF) for s in split[:2]]
    scratch += [pltpu.VMEM((8, D), F32)]
    scratch += attend_back_scratch(tokens, masks[0])
    scratch += [pltpu.VMEM((nz, 2, 2) + s, BF) for s in split]
    scratch += [pltpu.VMEM((nz, 2) + s, BF) for s in split]
    scratch += [pltpu.VMEM((nz,) + s, BF) for s in split]
    scratch += [pltpu.VMEM((nz - 1,) + s, BF) for s in split]
    scratch += [pltpu.VMEM(s, F32) for s in split]
    scratch += [
        pltpu.VMEM(hin.shape[1:], BF),
        pltpu.VMEM((nz - 1,) + hin.shape[1:], BF),
        pltpu.VMEM(stat_shape, F32),
        pltpu.VMEM(stat_shape, F32),
        pltpu.VMEM((3,) + stat_shape, F32),
        pltpu.VMEM((nz - 1,) + stat_shape, F32),
        pltpu.VMEM(stat_shape, F32),
        DMA((5,)),
        DMA((dp,)),
        DMA((dp,)),
        DMA((nw,)),
        DMA((nw,)),
        DMA((nw, 4)),
        DMA((nw, 4)),
        DMA((nw, nz)),
        DMA((nw, nz)),
        DMA((3, most)),
        DMA((3, most)),
        DMA((4 + nz,)),
        DMA((4 + nz,)),
        DMA((nw,)),
        DMA((nw,)),
        DMA((nw,)),
    ]
    return call(
        functools.partial(back_scatter_kernel, dp, shards),
        shapes,
        operands,
        [ANY if k in FETCHED else VM for k in range(len(operands) - 4)] + [ANY] * 3 + [VM],
        [VM] * len(shapes),
        scratch,
        6,
    )


def routing(routes, pieces, piece_len):
    places = jnp.arange(pieces * piece_len)
    routed = jnp.any(routes[:, None, :] == places[None, :, None], axis=-1)
    routed = routed.reshape(-1, pieces, piece_len)
    before = jnp.arange(piece_len)[:, None] < jnp.arange(piece_len)[None, :]
    rank = jnp.einsum(
        "skp,pq->skq", routed.astype(BF), before.astype(BF), preferred_element_type=F32
    )
    slots = jnp.arange(CAP, dtype=F32)
    hot = routed[:, :, None, :] & (rank[:, :, None, :] == slots[None, None, :, None])
    filled = jnp.any(hot, axis=-1)
    spots = jnp.sum(jnp.where(hot, places.reshape(1, pieces, 1, piece_len), 0), axis=-1)
    return hot, jnp.where(filled, spots, -1)


def local(
    layer_input,
    teacher,
    lengths,
    dealing,
    attn_routes,
    ffn_routes,
    ffn_scores,
    gain_attn,
    gain_ffn,
    light_qkv,
    light_out,
    heavy_qkv,
    heavy_out,
    light_in,
    light_down,
    heavy_in,
    heavy_down,
):
    dp = lax.axis_size("dp")
    pieces = lax.axis_size("fsdp")
    data_index = lax.axis_index("dp")
    piece = lax.axis_index("fsdp")
    nz = dp // 2
    n = dp * pieces
    seqs = dealing.shape[0]
    group = seqs // dp
    gain_len = gain_attn.shape[0]
    hidden_units = heavy_in.shape[1] // 2 // n
    mine = data_index * pieces + piece
    tokens = layer_input.shape[2] * dp
    matrices = (light_qkv, heavy_qkv, light_out, heavy_out, light_in, light_down)
    hin_rows = heavy_in.shape[0]
    token_count = jnp.sum(lengths).astype(F32)
    merged = (
        layer_input.shape[2] % 16 == 0
        and hidden_units % 128 == 0
        and all(m.shape[0] % 8 == 0 and m.shape[1] % 256 == 0 for m in (*matrices, heavy_down))
    )
    if merged:
        xin, hin_src, gains = prepare(dealing, layer_input[:, 0], heavy_in, gain_attn, gain_ffn)
        integers = (dealing.reshape(1, -1), lengths.reshape(1, -1), attn_routes, ffn_routes, ffn_scores)
        got = gather_attend(dp, xin, [gains, *matrices], hin_src, integers)
    else:
        xin = deal_rows(dealing, layer_input[:, 0])
        owned = jnp.arange(D)[None, :] // gain_len == mine
        spread_out = jnp.broadcast_to(
            jnp.stack([gain_attn, gain_ffn])[:, None, :], (2, D // gain_len, gain_len)
        ).reshape(2, D)
        gains = jnp.pad(jnp.where(owned, spread_out, 0.0).astype(BF), ((0, 6), (0, 0)))
        hin_src = (
            heavy_in.reshape(hin_rows, 2, nz, 8, hidden_units)
            .transpose(3, 0, 1, 2, 4)
            .reshape(8, hin_rows, 2 * nz * hidden_units)
        )
        if hin_rows % 8:
            hin_src = hin_src.reshape(8, -1, 128)
        got = gather_all(dp, xin, [gains] + [packed(m) for m in matrices], hin_src)
    flat_x = got[0].reshape(-1, D)
    w_lqkv, w_hqkv, w_lout, w_hout, w_lin, w_ldown = (
        unpacked(full, *m.shape) for full, m in zip(got[2:8], matrices)
    )
    w_hin = unpacked(got[8], hin_rows, 2 * nz * hidden_units)
    attn_weights = (w_lqkv, w_hqkv, w_lout, w_hout)
    if merged:
        gain, tables, (hidden, *saved) = got[9], got[10:19], got[19:]
        masks, ffn_masks = tables[:4], tables[4:]
    else:
        gain = jnp.sum(got[1].reshape(n, 8, D).astype(F32), axis=0)
        masks, ffn_masks = integer_tables(
            dealing, lengths, attn_routes, ffn_routes, ffn_scores, group, pieces, tokens
        )
        hidden, *saved = attend(flat_x, gain, *masks, *attn_weights)
    f_select, f_select_t, slot_score, weight_mask, weight_scale = ffn_masks
    grad_lin, grad_ldown, grad_hin, g_hdown, d_hidden, ffn_stats = feed_forward(
        nz,
        hidden,
        f_select,
        f_select_t,
        slot_score,
        gain,
        teacher.reshape(-1, D),
        weight_mask,
        weight_scale,
        w_lin,
        w_ldown,
        w_hin,
        heavy_down,
    )
    rows = tokens // dp
    shards = (light_in, light_down, heavy_out, light_out, heavy_qkv, light_qkv)
    hin_part = grad_hin.reshape((nz, 8) + hin_src.shape[1:])
    if merged:
        done = back_scatter(
            dp,
            rows,
            d_hidden,
            flat_x,
            gain,
            masks,
            attn_weights,
            saved,
            (grad_lin, grad_ldown),
            ffn_stats,
            tuple(shard.shape for shard in shards),
            hin_part,
        )
    else:
        grad_lqkv, grad_hqkv, grad_lout, grad_hout, d_inputs, attn_stats = attend_back(
            d_hidden, flat_x, gain, *masks, attn_weights, saved
        )
        stats = jnp.concatenate(
            [
                attn_stats[0].reshape(-1, 128),
                ffn_stats[0].reshape(-1, 128),
                jnp.broadcast_to(jnp.sum(ffn_stats[1]), (4, 128)),
            ]
        )
        grads = (grad_lin, grad_ldown, grad_hout, grad_lout, grad_hqkv, grad_lqkv)
        sent = [packed_full(grad, shard.shape, nz) for grad, shard in zip(grads, shards)]
        done = scatter_all(
            dp, d_inputs.reshape(group, dp, rows, D), stats, sent, hin_part
        )
    summed = done[1]
    loss_value = summed[12, 0] / (D * token_count)
    own_one = lax.dynamic_slice_in_dim(summed[:6].reshape(-1), mine * gain_len, gain_len)
    own_two = lax.dynamic_slice_in_dim(summed[6:12].reshape(-1), mine * gain_len, gain_len)
    back_rows = done[0].reshape(seqs, rows, D)
    if merged:
        d_layer, g_hin, *owned = finish_all(
            n, dealing, back_rows, done[8], [*done[2:8], g_hdown], heavy_in.shape
        )
    else:
        d_layer = undeal_rows(dealing, back_rows)
        owned = [full.reshape(shard.shape) for full, shard in zip(done[2:8], shards)]
        owned.append(g_hdown)
        g_hin = (
            done[8]
            .astype(F32)
            .reshape(8, hin_rows, 2, nz, hidden_units)
            .transpose(1, 2, 3, 0, 4)
            .reshape(heavy_in.shape)
        )
    g_lin, g_ldown, g_hout, g_lout, g_hqkv, g_lqkv, g_hdown = owned
    return (
        loss_value,
        d_layer[:, None],
        own_one,
        own_two,
        g_lqkv,
        g_lout,
        g_hqkv,
        g_hout,
        g_lin,
        g_ldown,
        g_hin,
        g_hdown,
    )


def integer_tables(dealing, lengths, attn_routes, ffn_routes, ffn_scores, group, pieces, tokens):
    seqs = dealing.shape[0]
    data_index = lax.axis_index("dp")
    piece = lax.axis_index("fsdp")
    chosen = lax.dynamic_slice_in_dim(dealing, data_index * group, group)
    one = chosen[:, None] == jnp.arange(seqs)[None, :]
    seq_lengths = jnp.sum(jnp.where(one, lengths[None, :], 0), axis=1)
    attn_pick = jnp.sum(jnp.where(one[:, :, None], attn_routes[None], 0), axis=1)
    ffn_pick = jnp.sum(jnp.where(one[:, :, None], ffn_routes[None], 0), axis=1)
    score_pick = jnp.sum(jnp.where(one[:, :, None], ffn_scores[None], 0.0), axis=1)
    token_count = jnp.sum(lengths).astype(F32)
    positions = piece * tokens + jnp.arange(tokens)
    valid_mask = positions[None, :] < seq_lengths[:, None]
    a_hot, a_spots = routing(attn_pick, pieces, tokens)
    f_hot, f_spots = routing(ffn_pick, pieces, tokens)
    a_select = lax.dynamic_index_in_dim(a_hot, piece, 1, False).astype(BF)
    f_select = lax.dynamic_index_in_dim(f_hot, piece, 1, False).astype(BF)
    a_spot = lax.dynamic_index_in_dim(a_spots, piece, 1, False)
    f_spot = lax.dynamic_index_in_dim(f_spots, piece, 1, False)
    slot_score = jnp.sum(
        jnp.where(f_spot[:, :, None] == ffn_pick[:, None, :], score_pick[:, None, :], 0.0), axis=-1
    )
    key_pos = piece * tokens - WIN + jnp.arange(tokens + 2 * WIN)
    live_key = (key_pos >= 0)[None, :] & (key_pos[None, :] < seq_lengths[:, None])
    key_line = jnp.where(live_key, 0.0, MASKED)
    key_bias = jnp.stack(
        [key_line[:, b : b + 3 * WIN] for b in range(0, tokens, WIN)], axis=1
    ).reshape(-1, 1, 3 * WIN)
    all_spots = a_spots.reshape(group, pieces * CAP)
    heavy_allowed = ((all_spots >= 0) & (all_spots < seq_lengths[:, None]))[:, None, :] | (
        a_spot[:, :, None] == all_spots[:, None, :]
    )
    heavy_bias = jnp.where(heavy_allowed, 0.0, MASKED)
    weight_mask = valid_mask.reshape(-1, 1).astype(F32)
    masks = (a_select, a_select.swapaxes(1, 2), key_bias, heavy_bias)
    ffn_masks = (
        f_select,
        f_select.swapaxes(1, 2),
        slot_score.reshape(-1, 1),
        weight_mask,
        2.0 * weight_mask / (D * token_count),
    )
    return masks, ffn_masks


def packed_full(grad, shard_shape, nz):
    rows, columns = shard_shape
    if rows % 8 == 0:
        return grad.reshape(nz, 2, 2, 2, rows, columns)
    return grad.reshape(nz, 2, 2, 2, rows * columns // 128, 128)


def solution(mesh):
    split = P(("dp", "fsdp"))
    matrix = P(("dp", "fsdp"), None)
    placed = (
        P(None, "fsdp", "dp", None),
        P("dp", "fsdp", None, None),
        P(),
        P(),
        P(),
        P(),
        P(),
        split,
        split,
    ) + (matrix,) * 8
    return jax.shard_map(
        local,
        mesh=mesh,
        in_specs=placed,
        out_specs=(P(), P(None, "fsdp", "dp", None), split, split) + (matrix,) * 8,
        check_vma=False,
    )
```

```python
import functools
import jax
import jax.numpy as jnp
from jax import lax
from jax.experimental import pallas as pl
from jax.experimental.pallas import tpu as pltpu
from jax.sharding import PartitionSpec as P

D = 768
HL = 8
HH = 12
DH = 64
FL = 1024
FH = 4096
WIN = 128
CAP = 64

EPSILON = 1e-06
MASKED = -1000000000.0
SCORE_SCALE = 0.125
MESH = pl.DeviceIdType.MESH
BF = jnp.bfloat16
F32 = jnp.float32
ANY = pl.BlockSpec(memory_space=pl.ANY)
VM = pl.BlockSpec(memory_space=pltpu.VMEM)
DMA = pltpu.SemaphoreType.DMA
VMEM_BYTES = 60 * 1024 * 1024


def place():
    d = lax.axis_index("dp")
    f = lax.axis_index("fsdp")
    return d // 2, d % 2, f // 2, f % 2


def at(hi, lo, x, c):
    return (hi * 2 + lo, x * 2 + c)


def meet(peers):
    barrier = pltpu.get_barrier_semaphore()
    for peer in peers:
        pl.semaphore_signal(barrier, inc=1, device_id=peer, device_id_type=MESH)
    pl.semaphore_wait(barrier, len(peers))


def send(src, dst, send_sem, recv_sem, peer):
    copy = pltpu.make_async_remote_copy(
        src_ref=src,
        dst_ref=dst,
        send_sem=send_sem,
        recv_sem=recv_sem,
        device_id=peer,
        device_id_type=MESH,
    )
    copy.start()
    return copy


def keep(src, dst, sem):
    copy = pltpu.make_async_copy(src, dst, sem)
    copy.start()
    return copy


def quad_peers():
    hi, lo, x, c = place()
    return [(lo, 1 - x), (1 - lo, x), (1 - lo, 1 - x)]


def call(kernel, out_shape, operands, in_specs, out_specs, scratch, collective_id):
    return pl.pallas_call(
        kernel,
        out_shape=out_shape,
        in_specs=in_specs,
        out_specs=out_specs,
        scratch_shapes=scratch,
        compiler_params=pltpu.CompilerParams(
            collective_id=collective_id, has_side_effects=True, vmem_limit_bytes=VMEM_BYTES
        ),
    )(*operands)


def deal_kernel(deal_ref, x_ref, o_ref):
    def body(i, carry):
        o_ref[i] = x_ref[deal_ref[i]]
        return carry

    lax.fori_loop(0, o_ref.shape[0], body, 0)


def deal_rows(dealing, rows):
    return pl.pallas_call(
        deal_kernel,
        out_shape=jax.ShapeDtypeStruct(rows.shape, rows.dtype),
        in_specs=[pl.BlockSpec(memory_space=pltpu.SMEM), VM],
        out_specs=VM,
        compiler_params=pltpu.CompilerParams(vmem_limit_bytes=VMEM_BYTES),
    )(dealing, rows)


def undeal_kernel(deal_ref, x_ref, o_ref):
    def body(i, carry):
        o_ref[deal_ref[i]] = x_ref[i].astype(F32)
        return carry

    lax.fori_loop(0, x_ref.shape[0], body, 0)


def undeal_rows(dealing, rows):
    return pl.pallas_call(
        undeal_kernel,
        out_shape=jax.ShapeDtypeStruct(rows.shape, F32),
        in_specs=[pl.BlockSpec(memory_space=pltpu.SMEM), VM],
        out_specs=VM,
        compiler_params=pltpu.CompilerParams(vmem_limit_bytes=VMEM_BYTES),
    )(dealing, rows)


def prepare_kernel(deal_ref, x_ref, heavy_ref, one_ref, two_ref, xin, hin, gains):
    def body(i, carry):
        xin[i] = x_ref[deal_ref[i]]
        return carry

    lax.fori_loop(0, xin.shape[0], body, 0)
    count = one_ref.shape[1]
    units = D // count
    step = heavy_ref.shape[1] // 2 // units
    for j in range(8):
        for k in range(units // 8):
            for g in (0, 1):
                start = g * heavy_ref.shape[1] // 2 + (k * 8 + j) * step
                spot = (g * (units // 8) + k) * step
                hin[j, :, spot : spot + step] = heavy_ref[:, start : start + step]
    mine = lax.axis_index("dp") * 4 + lax.axis_index("fsdp")
    row = lax.broadcasted_iota(jnp.int32, (count, D), 0)
    lane = lax.broadcasted_iota(jnp.int32, (count, D), 1)
    hot = jnp.where(lane == row + mine * count, 1.0, 0.0).astype(BF)
    lines = [jnp.broadcast_to(ref[...], (8, count)) for ref in (one_ref, two_ref)]
    one, two = (jnp.dot(line, hot, preferred_element_type=F32) for line in lines)
    kind = lax.broadcasted_iota(jnp.int32, (8, D), 0)
    gains[...] = jnp.where(kind == 0, one, jnp.where(kind == 1, two, 0.0)).astype(BF)


def prepare(dealing, rows, heavy_in, gain_one, gain_two):
    count = gain_one.shape[0]
    columns = heavy_in.shape[1] // 8
    return pl.pallas_call(
        prepare_kernel,
        out_shape=[
            jax.ShapeDtypeStruct(rows.shape, BF),
            jax.ShapeDtypeStruct((8, heavy_in.shape[0], columns), BF),
            jax.ShapeDtypeStruct((8, D), BF),
        ],
        in_specs=[pl.BlockSpec(memory_space=pltpu.SMEM), VM, VM, VM, VM],
        out_specs=[VM] * 3,
        compiler_params=pltpu.CompilerParams(vmem_limit_bytes=VMEM_BYTES),
    )(dealing, rows, heavy_in, gain_one.reshape(1, count), gain_two.reshape(1, count))


def finish_kernel(units, deal_ref, x_ref, hin, *refs):
    count = (len(refs) - 2) // 2
    ins, (rows, heavy), outs = refs[:count], refs[count : count + 2], refs[count + 2 :]

    def body(i, carry):
        rows[deal_ref[i]] = x_ref[i].astype(F32)
        return carry

    lax.fori_loop(0, x_ref.shape[0], body, 0)
    step = heavy.shape[1] // 2 // units
    for j in range(8):
        for k in range(units // 8):
            for g in (0, 1):
                start = g * heavy.shape[1] // 2 + (k * 8 + j) * step
                spot = (g * (units // 8) + k) * step
                heavy[:, start : start + step] = hin[j, :, spot : spot + step].astype(F32)
    for source, out in zip(ins, outs):
        out[...] = source[...]


def finish_all(units, dealing, rows, hin, grads, heavy_shape):
    shapes = [jax.ShapeDtypeStruct(rows.shape, F32), jax.ShapeDtypeStruct(heavy_shape, F32)]
    shapes += [jax.ShapeDtypeStruct(g.shape, F32) for g in grads]
    return pl.pallas_call(
        functools.partial(finish_kernel, units),
        out_shape=shapes,
        in_specs=[pl.BlockSpec(memory_space=pltpu.SMEM)] + [VM] * (2 + len(grads)),
        out_specs=[VM] * len(shapes),
        compiler_params=pltpu.CompilerParams(vmem_limit_bytes=VMEM_BYTES),
    )(dealing, rows, hin, *grads)


def packed(matrix):
    rows, columns = matrix.shape
    if rows % 8 == 0:
        return matrix
    return matrix.reshape(rows * columns // 128, 128)


def unpacked(gathered, rows, columns):
    return gathered.reshape(-1, rows, columns).reshape(-1, columns)


def plane_others():
    hi, lo, x, c = place()
    others = []
    for a in (0, 1):
        for b in (0, 1):
            for e in (0, 1):
                if a or b or e:
                    others.append(
                        (1 - lo if a else lo, 1 - x if b else x, 1 - c if e else c, b or e)
                    )
    return others


class Gather:
    def __init__(self, dp, xin, ws, hin, xo, wos, hin_o, sems, halves=None):
        self.dp, self.nz = dp, dp // 2
        self.xin, self.ws, self.hin = xin, ws, hin
        self.xo, self.wos, self.hin_o = xo, wos, hin_o
        self.loc, self.xs, self.xr, self.zs, self.zr = sems[:5]
        self.ps, self.pr, self.cs, self.cr, self.hs, self.hr = sems[5:]
        self.hi, self.lo, self.x, self.c = place()
        hi, lo, x, c = place()
        self.d = hi * 2 + lo
        self.home = (lo * 2 + x) * 2 + c
        self.rows_to = [(lax.rem(self.d + k, dp), x * 2 + c) for k in range(1, dp)]
        self.z_to = [at(lax.rem(hi + k, self.nz), lo, x, c) for k in range(1, self.nz)]
        self.others = plane_others()
        nw = len(ws)
        self.kept, self.z, self.p, self.f, self.k = ([None] * nw for _ in range(5))

        self.halves = halves

    def lanes(self, w, c):
        half = self.ws[w].shape[1] // 2
        return pl.ds(pl.multiple_of(c * half, 128), half)

    def shard(self, w, z, lo, x):
        if self.halves is None:
            return self.wos[w].at[z, lo, x, self.c]
        return self.wos[w].at[z, lo, x, :, self.lanes(w, self.c)]

    def swap(self, w):
        mine, mate, _, sems = self.halves
        partner = at(self.hi, self.lo, self.x, 1 - self.c)
        self.kept[w] = keep(self.ws[w].at[:, self.lanes(w, self.c)], mine[w], sems[0].at[w])
        out = self.ws[w].at[:, self.lanes(w, 1 - self.c)]
        self.z[w] = send(out, mate[w], sems[1].at[w], sems[2].at[w], partner)

    def join(self, w):
        mine, mate, base, _ = self.halves
        self.kept[w].wait()
        self.z[w].wait()
        a, b = mine[w][...].astype(F32), mate[w][...].astype(F32)
        first = self.c == 0
        rows = [jnp.where(first, a, b), jnp.where(first, b, a)]
        base[w][...] = jnp.concatenate(rows, axis=0).astype(BF)
        self.line(w)

    def meet(self):
        peers = self.rows_to + [at(self.hi, *q[:3]) for q in self.others if q[3]]
        meet(peers)

    def rows(self):
        group = self.xin.shape[0] // self.dp
        nw = len(self.ws)
        spot = self.xo.at[:, self.d]
        self.own = keep(self.xin.at[pl.ds(self.d * group, group)], spot, self.loc.at[nw])
        self.moved = [
            send(self.xin.at[pl.ds(to[0] * group, group)], spot, self.xs.at[k], self.xr.at[k], to)
            for k, to in enumerate(self.rows_to)
        ]

    def rows_ready(self):
        self.own.wait()
        for copy in self.moved:
            copy.wait()

    def line(self, w):
        spot = self.shard(w, self.hi, self.lo, self.x)
        own = self.ws[w] if self.halves is None else self.halves[2][w]
        self.kept[w] = keep(own, spot, self.loc.at[w])
        self.z[w] = [
            send(own, spot, self.zs.at[w, k], self.zr.at[w, k], to)
            for k, to in enumerate(self.z_to)
        ]

    def onward(self, part, w, k, to, sems):
        return send(part, part, sems[0].at[w, k], sems[1].at[w, k], to)

    def plane(self, w):
        self.kept[w].wait()
        for copy in self.z[w]:
            copy.wait()
        hi, lo, x, c = self.hi, self.lo, self.x, self.c
        column = self.shard(w, slice(None), lo, x)
        plane = (self.ps, self.pr)
        self.p[w] = [
            self.onward(column, w, 0, at(hi, lo, 1 - x, c), plane),
            self.onward(column, w, 1, at(hi, 1 - lo, x, c), plane),
        ]
        self.k[w] = [self.onward(column, w, 0, at(hi, lo, x, 1 - c), (self.cs, self.cr))]

    def cross(self, w):
        hi, lo, x, c = self.hi, self.lo, self.x, self.c
        plane, core, half = (self.ps, self.pr), (self.cs, self.cr), self.nz // 2
        partner = at(hi, lo, x, 1 - c)
        self.p[w][1].wait()
        part = self.shard(w, pl.ds(0, half), 1 - lo, x)
        first = self.onward(part, w, 2, at(hi, lo, 1 - x, c), plane)
        self.p[w][0].wait()
        part = self.shard(w, pl.ds(half, self.nz - half), lo, 1 - x)
        self.f[w] = [first, self.onward(part, w, 3, at(hi, 1 - lo, x, c), plane)]
        for k, part in ((1, (1 - lo, x)), (2, (lo, 1 - x))):
            self.k[w].append(
                self.onward(self.shard(w, slice(None), *part), w, k, partner, core)
            )

    def core(self, w):
        for copy in self.f[w]:
            copy.wait()
        part = self.shard(w, slice(None), 1 - self.lo, 1 - self.x)
        partner = at(self.hi, self.lo, self.x, 1 - self.c)
        self.k[w].append(self.onward(part, w, 3, partner, (self.cs, self.cr)))

    def ready(self, w):
        for copy in self.k[w]:
            copy.wait()

    def heavy_plane(self):
        nw, hi = len(self.ws), self.hi
        spot = self.hin_o.at[hi, self.home]
        self.h_own = [
            keep(self.hin.at[self.home], spot, self.loc.at[nw + 1]),
        ]
        self.h_near = [
            send(
                self.hin.at[(q[0] * 2 + q[1]) * 2 + q[2]],
                spot,
                self.hs.at[0, k],
                self.hr.at[0, k],
                at(hi, *q[:3]),
            )
            for k, q in enumerate(self.others)
        ]

    def heavy_line(self):
        for copy in self.h_own + self.h_near:
            copy.wait()
        part = self.hin_o.at[self.hi]
        self.h_far = []
        for k, to in enumerate(self.z_to):
            self.h_far.append(send(part, part, self.hs.at[1, k], self.hr.at[1, k], to))

    def heavy_ready(self):
        for copy in self.h_far:
            copy.wait()


def gather_sems(dp, nw):
    nz, most = dp // 2, max(7, dp // 2)
    return [
        DMA((nw + 2,)),
        DMA((dp,)),
        DMA((dp,)),
        DMA((nw, nz)),
        DMA((nw, nz)),
        DMA((nw, 4)),
        DMA((nw, 4)),
        DMA((nw, 4)),
        DMA((nw, 4)),
        DMA((2, most)),
        DMA((2, most)),
    ]


def gather_kernel(dp, nw, *refs):
    ins, outs, sems = refs[: 2 + nw], refs[2 + nw : 4 + 2 * nw], refs[4 + 2 * nw :]
    g = Gather(dp, ins[0], ins[1:-1], ins[-1], outs[0], outs[1:-1], outs[-1], sems)
    g.meet()
    g.rows()
    for w in range(nw):
        g.line(w)
    g.heavy_plane()
    for w in range(nw):
        g.plane(w)
        if w == 1:
            g.heavy_line()
        if w >= 1:
            g.cross(w - 1)
        if w >= 2:
            g.core(w - 2)
    g.cross(nw - 1)
    for w in range(nw - 2, nw):
        g.core(w)
    g.rows_ready()
    for w in range(nw):
        g.ready(w)
    g.heavy_ready()


def gather_shapes(dp, xin, weights, hin, paired):
    nz = dp // 2
    seqs, rows, _ = xin.shape
    shapes = [jax.ShapeDtypeStruct((seqs // dp, dp, rows, D), BF)]
    if paired:
        shapes += [jax.ShapeDtypeStruct((nz, 2, 2, 2 * w.shape[0], w.shape[1]), BF) for w in weights]
    else:
        shapes += [jax.ShapeDtypeStruct((nz, 2, 2, 2) + w.shape, BF) for w in weights]
    shapes.append(jax.ShapeDtypeStruct((nz,) + hin.shape, BF))
    return shapes


def gather_all(dp, xin, weights, hin):
    nw = len(weights)
    return call(
        functools.partial(gather_kernel, dp, nw),
        gather_shapes(dp, xin, weights, hin, False),
        [xin, *weights, hin],
        [ANY] * (2 + nw),
        [ANY] * (2 + nw),
        gather_sems(dp, nw),
        1,
    )


def rim_exchange(left, right, from_left, from_right, ls, lr, rs, rr):
    d = lax.axis_index("dp")
    f = lax.axis_index("fsdp")
    last = lax.axis_size("fsdp") - 1

    def down():
        return pltpu.make_async_remote_copy(
            src_ref=left,
            dst_ref=from_right,
            send_sem=ls,
            recv_sem=lr,
            device_id=(d, lax.max(f - 1, 0)),
            device_id_type=MESH,
        )

    def up():
        return pltpu.make_async_remote_copy(
            src_ref=right,
            dst_ref=from_left,
            send_sem=rs,
            recv_sem=rr,
            device_id=(d, lax.min(f + 1, last)),
            device_id_type=MESH,
        )

    @pl.when(f > 0)
    def _():
        down().start()

    @pl.when(f < last)
    def _():
        up().start()

    @pl.when(f == 0)
    def _():
        from_left[...] = jnp.zeros(from_left.shape, from_left.dtype)

    @pl.when(f == last)
    def _():
        from_right[...] = jnp.zeros(from_right.shape, from_right.dtype)

    def finish():
        @pl.when(f > 0)
        def _():
            down().wait_send()
            up().wait_recv()

        @pl.when(f < last)
        def _():
            up().wait_send()
            down().wait_recv()

    return finish


def line_peers():
    hi, lo, x, c = place()
    return [at(hi, lo, x, 1 - c), at(hi, lo, 1 - x, c), at(hi, lo, 1 - x, 1 - c)]


def dot(left, right):
    return jnp.dot(left, right, preferred_element_type=F32)


def dot_back(left, right):
    return lax.dot_general(left, right, (((1,), (1,)), ((), ())), preferred_element_type=F32)


def dot_grad(left, right):
    return lax.dot_general(left, right, (((0,), (0,)), ((), ())), preferred_element_type=F32)


def halves(value):
    high = value.astype(BF)
    return high, (value - high.astype(F32)).astype(BF)


def tiles(extent, step, body):
    def run(i, carry):
        body(pl.ds(pl.multiple_of(i * step, step), step))
        return carry

    lax.fori_loop(0, extent // step, run, 0)


GELU_A = 0.7978845608028654
GELU_B = 0.044715


def gelu_parts(v):
    square = v * v
    t = jnp.tanh(GELU_A * v * (1.0 + GELU_B * square))
    value = 0.5 * v * (1.0 + t)
    slope = 0.5 * (1.0 + t) + 0.5 * v * (1.0 - t * t) * GELU_A * (1.0 + 3.0 * GELU_B * square)
    return value, slope


def gelu_value(v):
    return 0.5 * v * (1.0 + jnp.tanh(GELU_A * v * (1.0 + GELU_B * v * v)))


def ffn_kernel(
    nz,
    swapped,
    hidden,
    select,
    select_t,
    score,
    gain,
    teach_hbm,
    mask,
    scale,
    w_in_hbm,
    w_dn_hbm,
    w_hin_hbm,
    hdn,
    g_in_hbm,
    g_dn_hbm,
    g_hin_hbm,
    hdn_o,
    d_hidden,
    stats,
    teach,
    w_in,
    w_dn,
    w_hin,
    g_in,
    g_dn,
    g_hin,
    moves_sem,
    w_line,
    g_line,
    g_in_line,
    hn,
    every,
    d_every,
    up_l,
    z,
    up_h,
    zh,
    part,
    near,
    far,
    out,
    dl,
    dup_l,
    dup_h,
    dhn,
    ps,
    pr,
    cs,
    cr,
    qs,
    qr,
    es,
    er,
    zs,
    zr,
    own,
    *mates,
):
    hi, lo, x, c = place()
    quad = quad_peers()
    partner = at(hi, lo, x, 1 - c)
    spots = [l2 * 2 + x2 for l2, x2 in quad]
    home = lo * 2 + x
    tokens = hidden.shape[0]
    group, cap, width = select.shape
    fl = z.shape[1]
    fh = zh.shape[3]
    block = 4 * cap
    z_index = [lax.rem(hi + k, nz) for k in range(1, nz)]
    z_to = [at(k, lo, x, c) for k in z_index]
    meet([at(hi, l2, x2, c) for l2, x2 in quad] + [partner] + z_to)
    pairs = ((w_in_hbm, w_in), (w_dn_hbm, w_dn), (w_hin_hbm, w_hin), (teach_hbm, teach))
    fetched = [keep(source, ref, moves_sem.at[k]) for k, (source, ref) in enumerate(pairs)]
    hdn_own = keep(hdn, w_line.at[hi], own)
    hdn_far = [send(hdn, w_line.at[hi], zs.at[0, k], zr.at[0, k], to) for k, to in enumerate(z_to)]
    w_hdn = w_line.reshape(-1, D)

    def span(s):
        return slice(s * width, (s + 1) * width)

    def slots(s):
        return slice(s * cap, (s + 1) * cap)

    def spread(buffer, s, i):
        spot = buffer.at[s, c, home]
        there = [
            send(spot, spot, ps.at[i, k], pr.at[i, k], at(hi, l2, x2, c))
            for k, (l2, x2) in enumerate(quad)
        ]
        return there, [send(spot, spot, cs.at[i, 3], cr.at[i, 3], partner)]

    def relay(buffer, s, i, there, back):
        for k, q in enumerate(spots):
            there[k].wait()
            other = buffer.at[s, c, q]
            back.append(send(other, other, cs.at[i, k], cr.at[i, k], partner))

    def fold(s, i, copy):
        copy.wait()
        there = []
        for k, q in enumerate(spots):
            near[i, q] = (near[i, q].astype(F32) + part[s, c, q].astype(F32)).astype(BF)
            l2, x2 = quad[k]
            there.append(
                send(near.at[i, q], far.at[i, k], qs.at[i, k], qr.at[i, k], at(hi, l2, x2, c))
            )
        return there

    def folded(s, i, there):
        for copy in there:
            copy.wait()
        return (
            near[i, home].astype(F32)
            + part[s, c, home].astype(F32)
            + far[i, 0].astype(F32)
            + far[i, 1].astype(F32)
            + far[i, 2].astype(F32)
        )

    def norm(r):
        h = hidden[r, :]
        inv = lax.rsqrt(jnp.mean(h * h, axis=-1, keepdims=True) + EPSILON)
        hn[r, :] = (h * inv * gain[1:2, :]).astype(BF)

    seqs = range(group)
    moves = {}
    tiles(tokens, 128, norm)
    for s in seqs:
        every[s, c, home] = dot(select[s], hn[span(s), :]).astype(BF)
        moves[s] = spread(every, s, s)

    def light_up(r):
        up_l[r, :] = dot(hn[r, :], w_in[...])
        z[r, :] = (gelu_value(up_l[r, :fl]) * up_l[r, fl:]).astype(BF)

    fetched[0].wait()
    tiles(tokens, width, light_up)
    for s in seqs:
        relay(every, s, s, *moves[s])

    def light_down(r):
        out[r, :] = hidden[r, :] + dot(z[r, :], w_dn[...])

    fetched[1].wait()
    tiles(tokens, width, light_down)

    def light_slopes(r):
        value, slope = gelu_parts(up_l[r, :fl])
        up_l[r, :fl] = up_l[r, fl:] * slope
        up_l[r, fl:] = value

    def heavy_up(s, e):
        up_h[s, e] = dot(every[s, e].reshape(block, D), w_hin[...])
        zh[s, e] = (gelu_value(up_h[s, e, :, :fh]) * up_h[s, e, :, fh:]).astype(BF)

    def heavy_down(s, e):
        part[s, e] = dot(zh[s, e], w_hdn[...]).astype(BF).reshape(4, cap, D)

    fetched[2].wait()
    sums = {}
    for s in seqs:
        for copy in moves[s][1]:
            copy.wait()
        heavy_up(s, 1 - c)
        heavy_up(s, c)
    tiles(tokens, 64, light_slopes)
    hdn_own.wait()
    for copy in hdn_far:
        copy.wait()
    first = {}
    for s in seqs:
        heavy_down(s, 1 - c)
        first[s] = send(part.at[s, 1 - c], near.at[s], es.at[s], er.at[s], partner)
        if s > 0:
            sums[s - 1] = fold(s - 1, s - 1, first[s - 1])
        heavy_down(s, c)
    sums[group - 1] = fold(group - 1, group - 1, first[group - 1])
    for s in seqs:
        for e in (0, 1):

            def heavy_slopes(r, s=s, e=e):
                value, slope = gelu_parts(up_h[s, e, r, :fh])
                up_h[s, e, r, :fh] = up_h[s, e, r, fh:] * slope
                up_h[s, e, r, fh:] = value

            if s == 0:
                tiles(block, 128, heavy_slopes)
    stats[...] = jnp.zeros(stats.shape, F32)
    fetched[3].wait()

    def light_back(r):
        dz = dot_back(dl[r, :], w_dn[...])
        dup_l[r, :fl] = (dz * up_l[r, :fl]).astype(BF)
        dup_l[r, fl:] = (dz * up_l[r, fl:]).astype(BF)

    for s in seqs:
        r = span(s)
        high, low = halves(folded(s, s, sums[s]) * score[slots(s), :])
        total = out[r, :] + (dot(select_t[s], high) + dot(select_t[s], low))
        m = total - teach[r, :].astype(F32)
        stats[1:2, :] += jnp.sum(mask[r, :] * m * m, axis=0, keepdims=True)
        d = scale[r, :] * m
        out[r, :] = d
        dl[r, :] = d.astype(BF)
        high, low = halves(d)
        picked = dot(select[s], high) + dot(select[s], low)
        d_every[s, c, home] = (picked * score[slots(s), :]).astype(BF)
        moves[s] = spread(d_every, s, group + s)
        light_back(r)
        if s > 0:
            for e in (0, 1):

                def more_slopes(r, s=s, e=e):
                    value, slope = gelu_parts(up_h[s, e, r, :fh])
                    up_h[s, e, r, :fh] = up_h[s, e, r, fh:] * slope
                    up_h[s, e, r, fh:] = value

                tiles(block, 128, more_slopes)

    def heavy_back(s, e):
        dz = dot_back(d_every[s, e].reshape(block, D), w_hdn[...])
        dup_h[s, e, :, :fh] = (dz * up_h[s, e, :, :fh]).astype(BF)
        dup_h[s, e, :, fh:] = (dz * up_h[s, e, :, fh:]).astype(BF)
        v = dot_back(dup_h[s, e], w_hin[...]).astype(BF)
        part[s, e] = v.reshape(4, cap, D)

    for s in seqs:
        relay(d_every, s, group + s, *moves[s])
        dhn[span(s), :] = dot_back(dup_l[span(s), :], w_in[...])
    for s in seqs:
        for copy in moves[s][1]:
            copy.wait()
    count = group * 2 * block
    d_rows = d_every[...].reshape(count, D)
    g_line[...] = dot_grad(zh[...].reshape(count, fh), d_rows).astype(BF)
    g_view = g_line.reshape(nz, -1, D)
    hdn_back = [
        send(g_view.at[k], g_in_line.at[n], zs.at[1, n], zr.at[1, n], z_to[n])
        for n, k in enumerate(z_index)
    ]
    for s in seqs:
        i = group + s
        heavy_back(s, 1 - c)
        first[s] = send(part.at[s, 1 - c], near.at[i], es.at[i], er.at[i], partner)
        if s > 0:
            sums[s - 1] = fold(s - 1, i - 1, first[s - 1])
        heavy_back(s, c)
    sums[group - 1] = fold(group - 1, 2 * group - 1, first[group - 1])

    def light_grad(j):
        g_dn[j, :] = dot_grad(z[:, j], dl[...]).astype(BF)

    tiles(fl, 512, light_grad)
    halved = []

    def swap(k, grad):
        rows, lanes = mates[k].shape[3:]
        view = grad.reshape(nz, 2, 2, rows, 2 * lanes)
        other = pl.ds(pl.multiple_of((1 - c) * lanes, 128), lanes)
        halved.append(view)
        sem = mates[2:]
        return send(view.at[:, :, :, :, other], mates[k], sem[0].at[k], sem[1].at[k], partner)

    def join(k):
        near_k, view, lanes = mates[k], halved[k], mates[k].shape[4]
        own_lanes = pl.ds(pl.multiple_of(c * lanes, 128), lanes)

        def add(n, carry):
            a, b, e = n // 4, (n // 2) % 2, n % 2
            value = near_k[a, b, e].astype(F32) + view[a, b, e, :, own_lanes].astype(F32)
            near_k[a, b, e] = value.astype(BF)
            return carry

        lax.fori_loop(0, nz * 4, add, 0)

    flushed, swaps = [], []
    if swapped:
        swaps.append(swap(0, g_dn))
    else:
        flushed.append(keep(g_dn, g_dn_hbm, moves_sem.at[4]))

    def light_in_grad(j):
        g_in[:, j] = dot_grad(hn[...], dup_l[:, j]).astype(BF)

    tiles(2 * fl, 1024, light_in_grad)
    if swapped:
        swaps.append(swap(1, g_in))
    else:
        flushed.append(keep(g_in, g_in_hbm, moves_sem.at[5]))
    every_rows = every[...].reshape(count, D)

    def heavy_grad(j):
        g_hin[:, j] = dot_grad(every_rows, dup_h[:, :, :, j].reshape(count, 512)).astype(BF)

    tiles(2 * fh, 512, heavy_grad)
    flushed.append(keep(g_hin, g_hin_hbm, moves_sem.at[6]))
    if swapped:
        for k, target in enumerate((g_dn_hbm, g_in_hbm)):
            swaps[k].wait()
            join(k)
            flushed.append(keep(mates[k], target, moves_sem.at[4 + k]))
    for s in seqs:
        r = span(s)
        high, low = halves(folded(s, group + s, sums[s]))
        d = dhn[r, :] + (dot(select_t[s], high) + dot(select_t[s], low))
        h = hidden[r, :]
        inv = lax.rsqrt(jnp.mean(h * h, axis=-1, keepdims=True) + EPSILON)
        dh = d * h
        stats[0:1, :] += jnp.sum(dh * inv, axis=0, keepdims=True)
        mean = jnp.mean(gain[1:2, :] * dh, axis=-1, keepdims=True)
        d_hidden[r, :] = out[r, :] + inv * gain[1:2, :] * d - h * (inv * inv * inv * mean)
    for copy in hdn_back + flushed:
        copy.wait()
    value = g_view[hi].astype(F32)
    for n in range(nz - 1):
        value += g_in_line[n].astype(F32)
    hdn_o[...] = value


def feed_forward(nz, swapped, hidden, select, select_t, score, gain, teach, mask, scale, w_in, w_dn, w_hin, hdn):
    tokens = hidden.shape[0]
    group, cap, _ = select.shape
    fl, fh = w_dn.shape[0], w_hin.shape[1] // 2
    block = (group, 2, 4, cap, D)
    line = (nz,) + hdn.shape
    half_in = (nz, 2, 2, D // (nz * 4), fl)
    half_dn = (nz, 2, 2, fl // (nz * 4), D // 2)
    extra = [pltpu.VMEM(half_dn, BF), pltpu.VMEM(half_in, BF), DMA((2,)), DMA((2,))]
    operands = [hidden, select, select_t, score, gain, teach, mask, scale, w_in, w_dn, w_hin, hdn]
    return call(
        functools.partial(ffn_kernel, nz, swapped),
        [
            jax.ShapeDtypeStruct(half_in if swapped else (D, 2 * fl), BF),
            jax.ShapeDtypeStruct(half_dn if swapped else (fl, D), BF),
            jax.ShapeDtypeStruct((D, 2 * fh), BF),
            jax.ShapeDtypeStruct(hdn.shape, F32),
            jax.ShapeDtypeStruct((tokens, D), F32),
            jax.ShapeDtypeStruct((8, D), F32),
        ],
        operands,
        [VM] * 5 + [ANY] + [VM] * 2 + [ANY] * 4,
        [ANY] * 3 + [VM] * 3,
        [
            pltpu.VMEM((tokens, D), BF),
            pltpu.VMEM((D, 2 * fl), BF),
            pltpu.VMEM((fl, D), BF),
            pltpu.VMEM((D, 2 * fh), BF),
            pltpu.VMEM((D, 2 * fl), BF),
            pltpu.VMEM((fl, D), BF),
            pltpu.VMEM((D, 2 * fh), BF),
            DMA((7,)),
            pltpu.VMEM(line, BF),
            pltpu.VMEM((fh, D), BF),
            pltpu.VMEM((nz - 1,) + hdn.shape, BF),
            pltpu.VMEM((tokens, D), BF),
            pltpu.VMEM(block, BF),
            pltpu.VMEM(block, BF),
            pltpu.VMEM((tokens, 2 * fl), F32),
            pltpu.VMEM((tokens, fl), BF),
            pltpu.VMEM((group, 2, 4 * cap, 2 * fh), F32),
            pltpu.VMEM((group, 2, 4 * cap, fh), BF),
            pltpu.VMEM(block, BF),
            pltpu.VMEM((2 * group, 4, cap, D), BF),
            pltpu.VMEM((2 * group, 3, cap, D), BF),
            pltpu.VMEM((tokens, D), F32),
            pltpu.VMEM((tokens, D), BF),
            pltpu.VMEM((tokens, 2 * fl), BF),
            pltpu.VMEM((group, 2, 4 * cap, 2 * fh), BF),
            pltpu.VMEM((tokens, D), F32),
            DMA((2 * group, 3)),
            DMA((2 * group, 3)),
            DMA((2 * group, 4)),
            DMA((2 * group, 4)),
            DMA((2 * group, 3)),
            DMA((2 * group, 3)),
            DMA((2 * group,)),
            DMA((2 * group,)),
            DMA((2, nz)),
            DMA((2, nz)),
            DMA,
        ]
        + (extra if swapped else []),
        5,
    )


def pair_masks(scale):
    lane = lax.broadcasted_iota(jnp.int32, (1, 2 * DH), 1)
    left = jnp.where(lane < DH, scale, 0.0).astype(BF)
    right = jnp.where(lane < DH, 0.0, scale).astype(BF)
    return left, right


def both(value, masks):
    return jnp.concatenate([value * masks[0], value * masks[1]], axis=0)


def side(stacked):
    rows = stacked.shape[0] // 2
    return jnp.concatenate([stacked[:rows], stacked[rows:]], axis=1)


def pair_forward(q, k, v, bias, ones, scaled):
    scores = dot_back(both(q, scaled), k) + bias
    top = jnp.max(scores, axis=-1, keepdims=True)
    shifted = jnp.exp(scores - top)
    total = jnp.sum(shifted, axis=-1, keepdims=True)
    prob = (shifted / total).astype(BF)
    return dot(side(prob), both(v, ones)).astype(BF), top + jnp.log(total)


def pair_backward(q, k, v, bias, lse, d_out, ones, scaled):
    q2 = both(q, scaled)
    d2 = both(d_out, ones)
    prob = jnp.exp(dot_back(q2, k) + bias - lse)
    d_prob = dot_back(d2, v)
    row = jnp.sum(prob * d_prob, axis=-1, keepdims=True)
    d_scores = (prob * (d_prob - row)).astype(BF)
    dq = dot(side(d_scores), both(k, scaled))
    return dq, dot_grad(d_scores, q2), dot_grad(prob.astype(BF), d2)


def reach_bias(key_bias):
    shape = (WIN, 3 * WIN)
    offset = lax.broadcasted_iota(jnp.int32, shape, 1) - lax.broadcasted_iota(jnp.int32, shape, 0) - WIN
    near = (offset >= -WIN) & (offset <= WIN)
    inner = jnp.where(offset == 0, 0.0, jnp.broadcast_to(key_bias, shape))
    bias = jnp.where(near, inner, MASKED)
    return jnp.concatenate([bias, bias], axis=0)


def put_lse(lse, pair, column):
    lane = lax.broadcasted_iota(jnp.int32, lse.shape, 1)
    rows = lse.shape[0]
    lse = jnp.where(lane == 2 * pair, column[:rows], lse)
    return jnp.where(lane == 2 * pair + 1, column[rows:], lse)


def get_lse(lse, pair):
    return jnp.concatenate([lse[:, 2 * pair : 2 * pair + 1], lse[:, 2 * pair + 1 : 2 * pair + 2]], axis=0)


def attend_body(
    stages,
    x,
    gain,
    select,
    select_t,
    key_bias,
    heavy_bias,
    w_lqkv,
    w_hqkv,
    w_lout,
    w_hout,
    hidden,
    xn,
    lq,
    rim,
    lo_out,
    l_lse,
    a_rows,
    hq,
    kvh,
    ho,
    h_lse,
    ls,
    lr,
    rs,
    rr,
    ss,
    sr,
):
    hi, lo, x_, c = place()
    f = x_ * 2 + c
    tokens = x.shape[0]
    group, cap, width = select.shape
    wl, wh = HL * DH, HH * DH
    ones, scaled = pair_masks(1.0), pair_masks(SCORE_SCALE)
    across, partner = at(hi, lo, 1 - x_, c), at(hi, lo, x_, 1 - c)

    def norm(r):
        h = x[r, :].astype(F32)
        inv = lax.rsqrt(jnp.mean(h * h, axis=-1, keepdims=True) + EPSILON)
        xn[r, :] = (h * inv * gain[0:1, :]).astype(BF)

    tiles(tokens, 128, norm)
    for s in range(group):
        rows = dot(select[s], xn[s * width : (s + 1) * width, :]).astype(BF)
        a_rows[s * cap : (s + 1) * cap, :] = rows
    stages[0]()
    kv = dot(a_rows[...], w_hqkv[:, wh:]).astype(BF)
    for s in range(group):
        kvh[s, f] = kv[s * cap : (s + 1) * cap]
    mine = kvh.at[:, f]
    first = send(mine, mine, ss.at[0], sr.at[0], across)
    beside = send(mine, mine, ss.at[1], sr.at[1], partner)
    stages[1]()
    for s in range(group):
        rows = xn[s * width : (s + 1) * width, :]
        rim[s, WIN : WIN + width, :] = dot(rows, w_lqkv[:, wl:]).astype(BF)
    finish = rim_exchange(
        rim.at[:, pl.ds(WIN, WIN)],
        rim.at[:, pl.ds(width, WIN)],
        rim.at[:, pl.ds(0, WIN)],
        rim.at[:, pl.ds(width + WIN, WIN)],
        ls,
        lr,
        rs,
        rr,
    )
    hq[...] = dot(a_rows[...], w_hqkv[:, :wh]).astype(BF)
    for s in range(group):
        rows = slice(s * width, (s + 1) * width)
        lq[rows, :] = dot(xn[rows, :], w_lqkv[:, :wl]).astype(BF)
    stages[2]()
    first.wait()
    other = kvh.at[:, (1 - x_) * 2 + c]
    relay = send(other, other, ss.at[2], sr.at[2], partner)
    finish()
    stages[3]()
    blocks = width // WIN

    def light(i, carry):
        s, b = i // blocks, i % blocks
        r = pl.ds(pl.multiple_of(i * WIN, WIN), WIN)
        keys = pl.ds(pl.multiple_of(b * WIN, WIN), 3 * WIN)
        bias = reach_bias(key_bias[i])
        lse = jnp.zeros((WIN, 128), F32)
        for pair in range(HL // 2):
            at_k = slice(pair * 128, (pair + 1) * 128)
            at_v = slice(wl + pair * 128, wl + (pair + 1) * 128)
            o, column = pair_forward(
                lq[r, at_k], rim[s, keys, at_k], rim[s, keys, at_v], bias, ones, scaled
            )
            lo_out[r, at_k] = o
            lse = put_lse(lse, pair, column)
        l_lse[r, :] = lse
        return carry

    lax.fori_loop(0, group * blocks // 2, light, 0)
    stages[4]()
    lax.fori_loop(group * blocks // 2, group * blocks, light, 0)
    stages[5]()
    beside.wait()
    relay.wait()
    heavy_kv = kvh.reshape(group, 4 * cap, 2 * wh)

    def heavy(s, carry):
        r = pl.ds(pl.multiple_of(s * cap, cap), cap)
        bias = heavy_bias[s]
        bias = jnp.concatenate([bias, bias], axis=0)
        lse = jnp.zeros((cap, 128), F32)
        for pair in range(HH // 2):
            at_k = slice(pair * 128, (pair + 1) * 128)
            at_v = slice(wh + pair * 128, wh + (pair + 1) * 128)
            o, column = pair_forward(
                hq[r, at_k], heavy_kv[s, :, at_k], heavy_kv[s, :, at_v], bias, ones, scaled
            )
            ho[r, at_k] = o
            lse = put_lse(lse, pair, column)
        h_lse[r, :] = lse
        return carry

    lax.fori_loop(0, group, heavy, 0)
    stages[6]()
    high, low = halves(dot(ho[...], w_hout[...]))
    for s in range(group):
        r = slice(s * width, (s + 1) * width)
        q = slice(s * cap, (s + 1) * cap)
        hidden[r, :] = (
            x[r, :].astype(F32)
            + dot(lo_out[r, :], w_lout[...])
            + (dot(select_t[s], high[q]) + dot(select_t[s], low[q]))
        )


def attend_kernel(*refs):
    meet(line_peers())
    attend_body([lambda: None] * 7, *refs)


def attend_shapes(tokens, select):
    group, cap, width = select.shape
    wl, wh = HL * DH, HH * DH
    rows = group * cap
    return [
        jax.ShapeDtypeStruct((tokens, D), F32),
        jax.ShapeDtypeStruct((tokens, D), BF),
        jax.ShapeDtypeStruct((tokens, wl), BF),
        jax.ShapeDtypeStruct((group, width + 2 * WIN, 2 * wl), BF),
        jax.ShapeDtypeStruct((tokens, wl), BF),
        jax.ShapeDtypeStruct((tokens, 128), F32),
        jax.ShapeDtypeStruct((rows, D), BF),
        jax.ShapeDtypeStruct((rows, wh), BF),
        jax.ShapeDtypeStruct((group, 4, cap, 2 * wh), BF),
        jax.ShapeDtypeStruct((rows, wh), BF),
        jax.ShapeDtypeStruct((rows, 128), F32),
    ]


ATTEND_SEMS = [DMA, DMA, DMA, DMA, DMA((3,)), DMA((3,))]


def attend(x, gain, select, select_t, key_bias, heavy_bias, w_lqkv, w_hqkv, w_lout, w_hout):
    operands = [x, gain, select, select_t, key_bias, heavy_bias, w_lqkv, w_hqkv, w_lout, w_hout]
    shapes = attend_shapes(x.shape[0], select)
    return call(
        attend_kernel,
        shapes,
        operands,
        [VM] * len(operands),
        [VM] * len(shapes),
        ATTEND_SEMS,
        2,
    )


def route_part(deal, lengths, routes_a, routes_f, scores, tables):
    sel_a, selt_a, key_bias, heavy_bias, sel_f, selt_f, score, mask, scale = tables
    hi, lo, x, c = place()
    group, cap, width = sel_a.shape
    seqs = deal.shape[1]
    here = ((x * 2 + c) * width).astype(F32)

    def line(shape, dim):
        return lax.broadcasted_iota(jnp.int32, shape, dim).astype(F32)

    lane = lax.broadcasted_iota(jnp.int32, (1, seqs), 1)
    before = jnp.where(line((width, width), 0) > line((width, width), 1), 1.0, 0.0).astype(BF)
    length_row = lengths[...].astype(F32)
    count = jnp.sum(length_row, axis=1, keepdims=True)
    column = line((width, 1), 0)
    row = line((1, width), 1)
    ones = jnp.ones((8, routes_a.shape[1]), BF)

    def columns_of(routes, base):
        held = jnp.where(routes == column + base, 1.0, 0.0)
        rank = jnp.sum(dot(before, held.astype(BF)), axis=1, keepdims=True)
        there = jnp.sum(held, axis=1, keepdims=True)
        hot_t = jnp.where(rank == line((width, cap), 1), 1.0, 0.0) * there
        return held, rank, hot_t

    def rows_of(held):
        there = dot_back(ones, held.astype(BF))
        rank = dot_back(there.astype(BF), before)
        return jnp.where(rank[:1] == line((cap, width), 0), 1.0, 0.0) * there[:1]

    for s in range(group):
        place_here = lane == (hi * 2 + lo) * group + s
        which = jnp.sum(jnp.where(place_here, deal[...].astype(F32), 0.0), axis=1, keepdims=True)
        one = line((seqs, 1), 0) == which
        length = jnp.sum(
            jnp.where(line((1, seqs), 1) == which, length_row, 0.0), axis=1, keepdims=True
        )
        ra, rf, sf = (
            jnp.sum(jnp.where(one, ref[...].astype(F32), 0.0), axis=0, keepdims=True)
            for ref in (routes_a, routes_f, scores)
        )
        held, rank, hot_t = columns_of(ra, here)
        hot = rows_of(held)
        sel_a[s] = hot.astype(BF)
        selt_a[s] = hot_t.astype(BF)
        own_spot = jnp.sum(hot * (row + here + 1.0), axis=1, keepdims=True) - 1.0
        for q in range(4):
            base = float(q * width)
            _, _, other_t = columns_of(ra, base)
            spot = jnp.sum(other_t * (column + base + 1.0), axis=0, keepdims=True) - 1.0
            live = jnp.where((spot >= 0.0) & (spot < length), 1.0, 0.0)
            same = jnp.where(own_spot == spot, 1.0, 0.0)
            heavy_bias[s, :, q * cap : (q + 1) * cap] = jnp.where(live + same > 0.0, 0.0, MASKED)
        for b in range(width // WIN):
            key = line((1, 3 * WIN), 1) + (here + float((b - 1) * WIN))
            live = (key >= 0.0) & (key < length)
            key_bias[s * (width // WIN) + b] = jnp.where(live, 0.0, MASKED)
        valid = jnp.where(column + here < length, 1.0, 0.0)
        mask[s * width : (s + 1) * width, :] = valid
        scale[s * width : (s + 1) * width, :] = 2.0 * valid / (D * count)
        held, rank, hot_t = columns_of(rf, here)
        sel_f[s] = rows_of(held).astype(BF)
        selt_f[s] = hot_t.astype(BF)
        slot = jnp.sum(held * rank, axis=0, keepdims=True)
        owned = jnp.sum(held, axis=0, keepdims=True)
        hits = jnp.where(slot == line((cap, slot.shape[1]), 0), 1.0, 0.0)
        score[s * cap : (s + 1) * cap, :] = jnp.sum(hits * (owned * sf), axis=1, keepdims=True)


def route_shapes(group, width, tokens):
    return [
        jax.ShapeDtypeStruct((group, CAP, width), BF),
        jax.ShapeDtypeStruct((group, width, CAP), BF),
        jax.ShapeDtypeStruct((tokens // WIN, 1, 3 * WIN), F32),
        jax.ShapeDtypeStruct((group, CAP, 4 * CAP), F32),
        jax.ShapeDtypeStruct((group, CAP, width), BF),
        jax.ShapeDtypeStruct((group, width, CAP), BF),
        jax.ShapeDtypeStruct((group * CAP, 1), F32),
        jax.ShapeDtypeStruct((tokens, 1), F32),
        jax.ShapeDtypeStruct((tokens, 1), F32),
    ]


def gather_attend_kernel(dp, nw, *refs):
    n_in, n_out = 7 + nw, 2 + nw + 21
    ins, outs, rest = refs[:n_in], list(refs[n_in : n_in + n_out]), refs[n_in + n_out :]
    count = len(STAGED)
    held, flush_sem, rest = rest[:count], rest[count], rest[count + 1 :]
    final = [outs[k] for k in STAGED]
    for k, ref in zip(STAGED, held):
        outs[k] = ref
    flushed = []

    def flush(*which):
        for k in which:
            n = STAGED.index(k)
            flushed.append(keep(held[n], final[n], flush_sem.at[n]))

    xin, ws, hin = ins[0], ins[1 : 1 + nw], ins[1 + nw]
    integers = ins[2 + nw :]
    xo, wos, hin_o = outs[0], outs[1 : 1 + nw], outs[1 + nw]
    gain, tables, saved = outs[2 + nw], outs[3 + nw : 12 + nw], outs[12 + nw :]
    parts, rest = rest[: 3 * nw + 3], rest[3 * nw + 3 :]
    halves = (parts[:nw], parts[nw : 2 * nw], parts[2 * nw : 3 * nw], parts[3 * nw :])
    g = Gather(dp, xin, ws, hin, xo, wos, hin_o, rest[:11], halves)
    g.meet()
    for w in range(nw):
        g.swap(w)
    g.join(0)
    g.join(2)
    g.plane(0)
    g.plane(2)
    g.join(1)
    g.rows()
    route_part(*integers, tables)
    g.cross(0)
    g.cross(2)
    g.core(0)
    g.plane(1)
    g.core(2)
    g.ready(0)
    total = jnp.zeros(gain.shape, F32)
    for z in range(dp // 2):
        for l2, x2 in ((0, 0), (0, 1), (1, 0), (1, 1)):
            pair = wos[0][z, l2, x2].astype(F32)
            total += pair[:8] + pair[8:]
    gain[...] = total
    g.rows_ready()
    for w in (4, 3, 5, 6):
        g.join(w)
    g.heavy_plane()
    flush(0)

    def heavy_projection():
        g.cross(1)
        g.ready(2)
        flush(20, 3)

    def light_projection():
        g.core(1)
        g.ready(1)
        flush(2)

    def keys_travel():
        g.plane(4)
        g.plane(3)
        g.heavy_line()
        flush(21)

    def keys_there():
        g.plane(5)
        g.plane(6)
        flush(22)

    def half_way():
        g.cross(4)
        g.cross(3)

    def light_done():
        g.core(4)
        g.core(3)
        g.cross(5)
        g.cross(6)
        flush(23)

    def heavy_done():
        g.ready(4)
        g.ready(3)
        flush(27, 4, 5)

    full = [wos[w].reshape(-1, wos[w].shape[-1]) for w in range(nw)]
    stages = [
        heavy_projection,
        light_projection,
        keys_travel,
        keys_there,
        half_way,
        light_done,
        heavy_done,
    ]
    attend_body(
        stages,
        xo.reshape(-1, D),
        gain,
        *tables[:4],
        full[1],
        full[2],
        full[3],
        full[4],
        *saved,
        *rest[11:],
    )
    g.core(5)
    g.core(6)
    g.ready(5)
    g.ready(6)
    g.heavy_ready()
    for copy in flushed:
        copy.wait()


STAGED = (0, 2, 3, 4, 5, 20, 21, 22, 23, 27)


def gather_attend(dp, xin, weights, hin, integers):
    nw = len(weights)
    shapes = gather_shapes(dp, xin, weights, hin, True)
    group, width = shapes[0].shape[0], dp * xin.shape[1]
    tables = route_shapes(group, width, group * width)
    shapes.append(jax.ShapeDtypeStruct((8, D), F32))
    shapes += tables
    shapes += attend_shapes(group * width, tables[0])
    return call(
        functools.partial(gather_attend_kernel, dp, nw),
        shapes,
        [xin, *weights, hin, *integers],
        [ANY] * (2 + nw) + [VM] * 5,
        [ANY if k in STAGED + (6, 7, 8) else VM for k in range(len(shapes))],
        [pltpu.VMEM(shapes[k].shape, BF) for k in STAGED]
        + [DMA((len(STAGED),))]
        + [pltpu.VMEM((w.shape[0], w.shape[1] // 2), BF) for w in weights] * 2
        + [pltpu.VMEM((2 * w.shape[0], w.shape[1] // 2), BF) for w in weights]
        + [DMA((nw,))] * 3
        + gather_sems(dp, nw)
        + ATTEND_SEMS,
        1,
    )


def attend_back_body(
    stages,
    d_hidden,
    x,
    gain,
    select,
    select_t,
    key_bias,
    heavy_bias,
    w_lqkv,
    w_hqkv,
    w_lout,
    w_hout,
    xn,
    lq,
    rim,
    lo_out,
    l_lse,
    a_rows,
    hq,
    kvh,
    ho,
    h_lse,
    g_lqkv,
    g_hqkv,
    g_lout,
    g_hout,
    dx,
    stats,
    d_ho,
    d_hproj,
    part,
    got,
    far,
    d_la,
    d_lo,
    d_rim,
    edge,
    edge_in,
    d_lproj,
    ls,
    lr,
    rs,
    rr,
    ss,
    sr,
):
    hi, lo, x_, c = place()
    tokens = x.shape[0]
    group, cap, width = select.shape
    wl, wh = HL * DH, HH * DH
    ones, scaled = pair_masks(1.0), pair_masks(SCORE_SCALE)
    across, partner = at(hi, lo, 1 - x_, c), at(hi, lo, x_, 1 - c)
    picked = []
    for s in range(group):
        high, low = halves(d_hidden[s * width : (s + 1) * width, :])
        picked.append((dot(select[s], high) + dot(select[s], low)).astype(BF))
    d_ha = jnp.concatenate(picked, axis=0)
    d_ho[...] = dot_back(d_ha, w_hout[...]).astype(BF)
    heavy_kv = kvh.reshape(group, 4 * cap, 2 * wh)
    part_kv = part.reshape(group, 4 * cap, 2 * wh)

    def heavy(s, carry):
        r = pl.ds(pl.multiple_of(s * cap, cap), cap)
        bias = heavy_bias[s]
        bias = jnp.concatenate([bias, bias], axis=0)
        lse = h_lse[r, :]
        for pair in range(HH // 2):
            at_k = slice(pair * 128, (pair + 1) * 128)
            at_v = slice(wh + pair * 128, wh + (pair + 1) * 128)
            dq, dk, dv = pair_backward(
                hq[r, at_k],
                heavy_kv[s, :, at_k],
                heavy_kv[s, :, at_v],
                bias,
                get_lse(lse, pair),
                d_ho[r, at_k],
                ones,
                scaled,
            )
            d_hproj[r, at_k] = dq.astype(BF)
            part_kv[s, :, at_k] = dk.astype(BF)
            part_kv[s, :, at_v] = dv.astype(BF)
        return carry

    lax.fori_loop(0, group, heavy, 0)
    beside = [
        send(part.at[:, b * 2 + 1 - c], got.at[b], ss.at[b], sr.at[b], partner) for b in (0, 1)
    ]
    g_hout[...] = dot_grad(ho[...], d_ha).astype(BF)
    stages[0]()

    def light_out_back(r):
        d = d_hidden[r, :].astype(BF)
        d_la[r, :] = d
        d_lo[r, :] = dot_back(d, w_lout[...]).astype(BF)

    tiles(tokens, 256, light_out_back)
    g_lout[...] = dot_grad(lo_out[...], d_la[...]).astype(BF)
    stages[1]()
    for copy in beside:
        copy.wait()
    for b in (0, 1):
        got[b] = (got[b].astype(F32) + part[:, b * 2 + c].astype(F32)).astype(BF)
    third = send(got.at[1 - x_], far, ss.at[2], sr.at[2], across)
    stages[2]()
    d_rim[...] = jnp.zeros(d_rim.shape, F32)
    blocks = width // WIN

    def light(i, carry):
        s, b = i // blocks, i % blocks
        r = pl.ds(pl.multiple_of(i * WIN, WIN), WIN)
        keys = pl.ds(pl.multiple_of(b * WIN, WIN), 3 * WIN)
        bias = reach_bias(key_bias[i])
        lse = l_lse[r, :]
        for pair in range(HL // 2):
            at_k = slice(pair * 128, (pair + 1) * 128)
            at_v = slice(wl + pair * 128, wl + (pair + 1) * 128)
            dq, dk, dv = pair_backward(
                lq[r, at_k],
                rim[s, keys, at_k],
                rim[s, keys, at_v],
                bias,
                get_lse(lse, pair),
                d_lo[r, at_k],
                ones,
                scaled,
            )
            d_lproj[r, at_k] = dq.astype(BF)
            d_rim[s, keys, at_k] += dk
            d_rim[s, keys, at_v] += dv
        return carry

    lax.fori_loop(0, group * blocks // 2, light, 0)
    third.wait()
    total = (got[x_].astype(F32) + far[...].astype(F32)).astype(BF)
    for s in range(group):
        d_hproj[s * cap : (s + 1) * cap, wh:] = total[s]

    def heavy_grad(j):
        g_hqkv[:, j] = dot_grad(a_rows[...], d_hproj[:, j]).astype(BF)

    tiles(3 * wh, 768, heavy_grad)
    stages[3]()
    lax.fori_loop(group * blocks // 2, group * blocks, light, 0)
    edge[0] = d_rim[:, :WIN, :].astype(BF)
    edge[1] = d_rim[:, WIN + width :, :].astype(BF)
    finish = rim_exchange(
        edge.at[0], edge.at[1], edge_in.at[0], edge_in.at[1], ls, lr, rs, rr
    )
    stages[4]()
    d_high, d_low = halves(dot_back(d_hproj[...], w_hqkv[...]))
    finish()
    for s in range(group):
        d_rim[s, WIN : 2 * WIN, :] += edge_in[0, s].astype(F32)
        d_rim[s, width : width + WIN, :] += edge_in[1, s].astype(F32)
        d_lproj[s * width : (s + 1) * width, wl:] = d_rim[s, WIN : WIN + width, :].astype(BF)

    def light_grad(j):
        g_lqkv[:, j] = dot_grad(xn[...], d_lproj[:, j]).astype(BF)

    tiles(3 * wl, 768, light_grad)
    stages[5]()
    stats[...] = jnp.zeros(stats.shape, F32)
    for s in range(group):
        r = slice(s * width, (s + 1) * width)
        q = slice(s * cap, (s + 1) * cap)
        d = dot_back(d_lproj[r, :], w_lqkv[...]) + (
            dot(select_t[s], d_high[q]) + dot(select_t[s], d_low[q])
        )
        h = x[r, :].astype(F32)
        inv = lax.rsqrt(jnp.mean(h * h, axis=-1, keepdims=True) + EPSILON)
        dh = d * h
        stats[0:1, :] += jnp.sum(dh * inv, axis=0, keepdims=True)
        mean = jnp.mean(gain[0:1, :] * dh, axis=-1, keepdims=True)
        dx[r, :] = (
            d_hidden[r, :] + inv * gain[0:1, :] * d - h * (inv * inv * inv * mean)
        ).astype(BF)
    stages[6]()


def attend_back_kernel(*refs):
    meet(line_peers())
    attend_back_body([lambda: None] * 7, *refs)


def attend_back_scratch(tokens, select):
    group, cap, width = select.shape
    wl, wh = HL * DH, HH * DH
    rows = group * cap
    return [
        pltpu.VMEM((rows, wh), BF),
        pltpu.VMEM((rows, 3 * wh), BF),
        pltpu.VMEM((group, 4, cap, 2 * wh), BF),
        pltpu.VMEM((2, group, cap, 2 * wh), BF),
        pltpu.VMEM((group, cap, 2 * wh), BF),
        pltpu.VMEM((tokens, D), BF),
        pltpu.VMEM((tokens, wl), BF),
        pltpu.VMEM((group, width + 2 * WIN, 2 * wl), F32),
        pltpu.VMEM((2, group, WIN, 2 * wl), BF),
        pltpu.VMEM((2, group, WIN, 2 * wl), BF),
        pltpu.VMEM((tokens, 3 * wl), BF),
    ] + ATTEND_SEMS


def attend_back(d_hidden, x, gain, select, select_t, key_bias, heavy_bias, weights, saved):
    tokens = x.shape[0]
    wl, wh = HL * DH, HH * DH
    operands = [d_hidden, x, gain, select, select_t, key_bias, heavy_bias, *weights, *saved]
    shapes = [
        jax.ShapeDtypeStruct((D, 3 * wl), BF),
        jax.ShapeDtypeStruct((D, 3 * wh), BF),
        jax.ShapeDtypeStruct((wl, D), BF),
        jax.ShapeDtypeStruct((wh, D), BF),
        jax.ShapeDtypeStruct((tokens, D), BF),
        jax.ShapeDtypeStruct((8, D), F32),
    ]
    return call(
        attend_back_kernel,
        shapes,
        operands,
        [VM] * len(operands),
        [VM] * len(shapes),
        attend_back_scratch(tokens, select),
        3,
    )


def scatter_kernel(dp, nw, *refs):
    nz = dp // 2
    dx, stats, gs, hin = refs[0], refs[1], refs[2 : 2 + nw], refs[2 + nw]
    outs = refs[3 + nw :]
    dxo, total, gos, hin_o = outs[0], outs[1], outs[2 : 2 + nw], outs[2 + nw]
    scr = outs[3 + nw :]
    nears, fars, sums, ends = (scr[i * nw : (i + 1) * nw] for i in range(4))
    hin_r, hin_s, sc, sp, sz, acc, acc2 = scr[4 * nw : 4 * nw + 7]
    own, xs, xr, cs, cr, ps, pr, zs, zr, hs, hr, ts, tr = scr[4 * nw + 7 :]
    hi, lo, x, c = place()
    d = hi * 2 + lo
    f = x * 2 + c
    plane = (lo * 2 + x) * 2 + c
    dp_peers = [(lax.rem(d + k, dp), f) for k in range(1, dp)]
    rest = [(a, b, e) for a in (0, 1) for b in (0, 1) for e in (0, 1) if a or b or e]
    flat8 = []
    for a, b, e in rest:
        l2 = 1 - lo if a else lo
        x2 = 1 - x if b else x
        c2 = 1 - c if e else c
        flat8.append((l2, x2, c2))
    meet(dp_peers + [at(hi, *p) for (a, b, e), p in zip(rest, flat8) if b or e])
    partner = at(hi, lo, x, 1 - c)
    quad = quad_peers()
    z_index = [lax.rem(hi + k, nz) for k in range(1, nz)]
    z_peers = [at(z, lo, x, c) for z in z_index]
    c_sends = [
        send(gs[w].at[:, :, :, 1 - c], nears[w], cs.at[w], cr.at[w], partner) for w in range(nw)
    ]
    t_c = send(stats, sc, ts.at[0], tr.at[0], partner)
    mine = keep(dx.at[:, d], dxo.at[d], own)
    x_sends = [
        send(dx.at[:, peer[0]], dxo.at[d], xs.at[k], xr.at[k], peer)
        for k, peer in enumerate(dp_peers)
    ]
    h_sends = []
    for k, z in enumerate(z_index):
        h_sends.append(send(hin.at[z], hin_r.at[k], hs.at[1, k], hr.at[1, k], z_peers[k]))
    p_sends, z_sends = [], []
    t_c.wait()
    acc[...] = stats[...] + sc[...]
    t_p = [
        send(acc, sp.at[k], ts.at[1 + k], tr.at[1 + k], at(hi, l2, x2, c))
        for k, (l2, x2) in enumerate(quad)
    ]

    def add_core(w):
        c_sends[w].wait()
        near, g = nears[w], gs[w]

        def body(i, carry):
            z, a, b = i // 4, (i // 2) % 2, i % 2
            near[z, a, b] = (near[z, a, b].astype(F32) + g[z, a, b, c].astype(F32)).astype(BF)
            return carry

        lax.fori_loop(0, nz * 4, body, 0)
        p_sends.append(
            [
                send(near.at[:, l2, x2], fars[w].at[k], ps.at[w, k], pr.at[w, k], at(hi, l2, x2, c))
                for k, (l2, x2) in enumerate(quad)
            ]
        )

    def add_plane(w):
        for copy in p_sends[w]:
            copy.wait()
        near, far, part = nears[w], fars[w], sums[w]

        def body(z, carry):
            part[z] = (
                near[z, lo, x].astype(F32)
                + far[0, z].astype(F32)
                + far[1, z].astype(F32)
                + far[2, z].astype(F32)
            ).astype(BF)
            return carry

        lax.fori_loop(0, nz, body, 0)
        z_sends.append(
            [
                send(part.at[z], ends[w].at[k], zs.at[w, k], zr.at[w, k], z_peers[k])
                for k, z in enumerate(z_index)
            ]
        )

    def add_line(w):
        for copy in z_sends[w]:
            copy.wait()
        gos[w][...] = sums[w][hi].astype(F32)
        for k in range(nz - 1):
            gos[w][...] += ends[w][k].astype(F32)

    for w in range(nw):
        add_core(w)
        if w >= 2:
            add_plane(w - 2)
    for copy in t_p:
        copy.wait()
    acc2[...] = acc[...] + sp[0] + sp[1] + sp[2]
    t_z = [send(acc2, sz.at[k], ts.at[4 + k], tr.at[4 + k], z_peers[k]) for k in range(nz - 1)]
    for copy in h_sends:
        copy.wait()

    def body(i, carry):
        value = hin[hi, i].astype(F32)
        for k in range(nz - 1):
            value += hin_r[k, i].astype(F32)
        hin_s[i] = value.astype(BF)
        return carry

    lax.fori_loop(0, 8, body, 0)
    hin_o[plane] = hin_s[plane]
    a_sends = [
        send(
            hin_s.at[(l2 * 2 + x2) * 2 + c2],
            hin_o.at[plane],
            hs.at[0, k],
            hr.at[0, k],
            at(hi, l2, x2, c2),
        )
        for k, (l2, x2, c2) in enumerate(flat8)
    ]
    for w in range(max(nw - 2, 0), nw):
        add_plane(w)
    for copy in t_z:
        copy.wait()
    total[...] = acc2[...]
    for k in range(nz - 1):
        total[...] += sz[k]
    for w in range(nw):
        add_line(w)
    mine.wait()
    for copy in x_sends + a_sends:
        copy.wait()


def scatter_all(dp, dx, stats, grads, hin):
    nz = dp // 2
    nw = len(grads)
    group, _, rows, _ = dx.shape
    tiles = [g.shape[4:] for g in grads]
    most = max(7, nz)
    scratch = [pltpu.VMEM((nz, 2, 2) + t, BF) for t in tiles]
    scratch += [pltpu.VMEM((3, nz) + t, BF) for t in tiles]
    scratch += [pltpu.VMEM((nz,) + t, BF) for t in tiles]
    scratch += [pltpu.VMEM((nz - 1,) + t, BF) for t in tiles]
    scratch += [
        pltpu.VMEM((nz - 1,) + hin.shape[1:], BF),
        pltpu.VMEM(hin.shape[1:], BF),
        pltpu.VMEM(stats.shape, F32),
        pltpu.VMEM((3,) + stats.shape, F32),
        pltpu.VMEM((nz - 1,) + stats.shape, F32),
        pltpu.VMEM(stats.shape, F32),
        pltpu.VMEM(stats.shape, F32),
        DMA,
        DMA((dp,)),
        DMA((dp,)),
        DMA((nw,)),
        DMA((nw,)),
        DMA((nw, 3)),
        DMA((nw, 3)),
        DMA((nw, nz)),
        DMA((nw, nz)),
        DMA((3, most)),
        DMA((3, most)),
        DMA((4 + nz,)),
        DMA((4 + nz,)),
    ]
    shapes = [jax.ShapeDtypeStruct((dp, group, rows, D), BF), jax.ShapeDtypeStruct(stats.shape, F32)]
    shapes += [jax.ShapeDtypeStruct(t, F32) for t in tiles]
    shapes.append(jax.ShapeDtypeStruct(hin.shape[1:], BF))
    return call(
        functools.partial(scatter_kernel, dp, nw),
        shapes,
        [dx, stats, *grads, hin],
        [ANY] + [VM] * (2 + nw),
        [ANY] + [VM] * (2 + nw),
        scratch,
        4,
    )


class Scatter:
    def __init__(self, nz, shards, gs, near, one, two, end, sems):
        self.nz, self.shards, self.gs = nz, shards, gs
        self.near, self.one, self.two, self.end = near, one, two, end
        self.cs, self.cr, self.ps, self.pr, self.zs, self.zr = sems
        self.hi, self.lo, self.x, self.c = hi, lo, x, c = place()
        self.partner = at(hi, lo, x, 1 - c)
        self.by_x, self.by_y = at(hi, lo, 1 - x, c), at(hi, 1 - lo, x, c)
        self.z_index = [lax.rem(hi + k, nz) for k in range(1, nz)]
        self.copies = {}

    def lanes(self, w, c):
        half = self.shards[w][1] // 2
        return pl.ds(pl.multiple_of(c * half, 128), half)

    def core(self, w):
        out = self.gs[w].at[:, :, :, :, self.lanes(w, 1 - self.c)]
        self.copies[w, 0] = [send(out, self.near[w], self.cs.at[w], self.cr.at[w], self.partner)]

    def wait(self, w, stage):
        for copy in self.copies[w, stage]:
            copy.wait()

    def plane(self, w):
        g, own = self.gs[w], self.lanes(w, self.c)
        self.add_plane(w, lambda z, a, b: g[z, a, b, :, own])

    def add_plane(self, w, own):
        self.wait(w, 0)
        near = self.near[w]
        lo, x, half = self.lo, self.x, self.nz // 2

        def body(i, carry):
            z, a, b = i // 4, (i // 2) % 2, i % 2
            near[z, a, b] = (near[z, a, b].astype(F32) + own(z, a, b).astype(F32)).astype(BF)
            return carry

        lax.fori_loop(0, self.nz * 4, body, 0)
        low, high = pl.ds(0, half), pl.ds(half, self.nz - half)
        self.copies[w, 1] = [
            send(near.at[low, :, 1 - x], self.one[w].at[low], self.ps.at[w, 0], self.pr.at[w, 0], self.by_x),
            send(near.at[high, 1 - lo], self.one[w].at[high], self.ps.at[w, 1], self.pr.at[w, 1], self.by_y),
        ]

    def begin(self, w, source, sem):
        near, lo, x, half = self.near[w], self.lo, self.x, self.nz // 2
        low, high = pl.ds(0, half), pl.ds(half, self.nz - half)
        self.copies[w, 1] = [
            keep(source, near, sem),
            send(source.at[low, :, 1 - x], self.one[w].at[low], self.ps.at[w, 0], self.pr.at[w, 0], self.by_x),
            send(source.at[high, 1 - lo], self.one[w].at[high], self.ps.at[w, 1], self.pr.at[w, 1], self.by_y),
        ]

    def cross(self, w):
        self.wait(w, 1)
        near, one, lo, x, half = self.near[w], self.one[w], self.lo, self.x, self.nz // 2

        def low_body(i, carry):
            z, a = i // 2, i % 2
            near[z, a, x] = (near[z, a, x].astype(F32) + one[z, a].astype(F32)).astype(BF)
            return carry

        def high_body(i, carry):
            z, b = half + i // 2, i % 2
            near[z, lo, b] = (near[z, lo, b].astype(F32) + one[z, b].astype(F32)).astype(BF)
            return carry

        lax.fori_loop(0, half * 2, low_body, 0)
        lax.fori_loop(0, (self.nz - half) * 2, high_body, 0)
        low, high = pl.ds(0, half), pl.ds(half, self.nz - half)
        two = self.two[w]
        self.copies[w, 2] = [
            send(near.at[low, 1 - lo, x], two.at[low], self.ps.at[w, 2], self.pr.at[w, 2], self.by_y),
            send(near.at[high, lo, 1 - x], two.at[high], self.ps.at[w, 3], self.pr.at[w, 3], self.by_x),
        ]

    def line(self, w):
        self.wait(w, 2)
        near, part, lo, x = self.near[w], self.two[w], self.lo, self.x

        def body(z, carry):
            part[z] = (near[z, lo, x].astype(F32) + part[z].astype(F32)).astype(BF)
            return carry

        lax.fori_loop(0, self.nz, body, 0)
        self.copies[w, 3] = [
            send(
                part.at[z],
                self.end[w].at[k],
                self.zs.at[w, k],
                self.zr.at[w, k],
                at(z, lo, x, self.c),
            )
            for k, z in enumerate(self.z_index)
        ]

    def last(self, w, fin, out, sems):
        self.wait(w, 3)
        value = self.two[w][self.hi].astype(F32)
        for k in range(self.nz - 1):
            value += self.end[w][k].astype(F32)
        fin[...] = value
        count = self.shards[w][0]
        own = pl.ds(pl.multiple_of(self.c * count, 8), count)
        mate = pl.ds(pl.multiple_of((1 - self.c) * count, 8), count)
        spot = out.at[:, self.lanes(w, self.c)]
        return [
            keep(fin.at[own], spot, sems[0].at[w]),
            send(fin.at[mate], spot, sems[1].at[w], sems[2].at[w], self.partner),
        ]


def back_scatter_kernel(dp, shards, *refs):
    nz, nw = dp // 2, len(shards)
    n_ops = 7 + 4 + 10
    ops, (g_lin, g_ldn, hin, ffn_stats) = refs[:n_ops], refs[n_ops : n_ops + 4]
    outs, rest = refs[n_ops + 4 : n_ops + 7 + nw], refs[n_ops + 7 + nw :]
    dxo, total, gos, hin_o = outs[0], outs[1], outs[2 : 2 + nw], outs[2 + nw]
    count = len(FETCHED)
    held, fetch_sem, rest = rest[:count], rest[count], rest[count + 1 :]
    sources, ops = [ops[k] for k in FETCHED], list(ops)
    for k, ref in zip(FETCHED, held):
        ops[k] = ref
    full, rest = rest[:4], rest[4:]
    stats, rest = rest[0], rest[1:]
    back, rest = rest[:17], rest[17:]
    dx = back[5]
    near, one, two, end, fin = (rest[k * nw : (k + 1) * nw] for k in range(5))
    hin_own, hin_r, acc, sc, sp, sz, acc2 = rest[5 * nw : 5 * nw + 7]
    own, xs, xr, cs, cr, ps, pr, zs, zr, hs, hr, ts, tr, *fsem = rest[5 * nw + 7 :]
    hi, lo, x, c = place()
    d = hi * 2 + lo
    plane = (lo * 2 + x) * 2 + c
    others = plane_others()
    rows_to = [(lax.rem(d + k, dp), x * 2 + c) for k in range(1, dp)]
    z_index = [lax.rem(hi + k, nz) for k in range(1, nz)]
    z_to = [at(z, lo, x, c) for z in z_index]
    quad = quad_peers()
    g_views = [None, None]
    for k, w in enumerate((2, 3, 4, 5)):
        rows, columns = shards[w]
        g_views.append(full[k].reshape(nz, 2, 2, 2 * rows, columns))
    t = Scatter(nz, shards, g_views, near, one, two, end, (cs, cr, ps, pr, zs, zr))
    meet(rows_to + [at(hi, *q[:3]) for q in others if q[3]])
    fetched = {
        k: keep(source, ref, fetch_sem.at[n])
        for n, (k, source, ref) in enumerate(zip(FETCHED, sources, held))
    }

    def fetch(*which):
        for k in which:
            fetched[k].wait()

    h_sends = []
    for k, z in enumerate(z_index):
        h_sends.append(send(hin.at[z], hin_r.at[k], hs.at[1, k], hr.at[1, k], z_to[k]))
    t.begin(0, g_lin, own.at[0])
    t.begin(1, g_ldn, own.at[1])
    kept = [keep(hin.at[hi], hin_own, own.at[2])]
    late = []

    def first_plane():
        fetch(9, 14)
        t.core(2)

    def out_core():
        t.core(3)

    def before_light():
        fetch(12, 13)

    def half_way():
        t.core(4)
        t.cross(0)
        t.cross(1)
        t.plane(2)
        t.plane(3)

    def rims_left():
        fetch(8, 11)
        t.plane(4)
        t.line(0)
        t.line(1)
        t.cross(2)
        t.cross(3)

    def light_grad_done():
        t.core(5)
        fetch(7, 1)

    def rows_done():
        rows = dx.reshape(dxo.shape[1], dp, dxo.shape[2], D)
        late.append(keep(rows.at[:, d], dxo.at[d], own.at[4]))
        for k, to in enumerate(rows_to):
            late.append(send(rows.at[:, to[0]], dxo.at[d], xs.at[k], xr.at[k], to))

    stages = [
        first_plane,
        out_core,
        before_light,
        half_way,
        rims_left,
        light_grad_done,
        rows_done,
    ]
    attend_back_body(
        stages, *ops, full[3], full[2], full[1], full[0], dx, stats, *back
    )
    partner = at(hi, lo, x, 1 - c)
    for k in range(6):
        lanes = slice(k * 128, (k + 1) * 128)
        acc[k : k + 1, :] = stats[0:1, lanes]
        acc[6 + k : 7 + k, :] = ffn_stats[0:1, lanes]
    loss = jnp.sum(ffn_stats[1:2, :], axis=-1, keepdims=True)
    acc[12:16, :] = jnp.broadcast_to(loss, (4, 128))
    t_c = send(acc, sc, ts.at[0], tr.at[0], partner)
    t.plane(5)
    t.line(2)
    t.line(3)
    t.cross(4)
    t_c.wait()
    acc2[...] = acc[...] + sc[...]
    t_p = [
        send(acc2, sp.at[k], ts.at[1 + k], tr.at[1 + k], at(hi, l2, x2, c))
        for k, (l2, x2) in enumerate(quad)
    ]
    t.line(4)
    for copy in h_sends + kept:
        copy.wait()

    def body(i, carry):
        value = hin_own[i].astype(F32)
        for k in range(nz - 1):
            value += hin_r[k, i].astype(F32)
        hin_own[i] = value.astype(BF)
        return carry

    lax.fori_loop(0, 8, body, 0)
    hin_o[plane] = hin_own[plane]
    late += [
        send(
            hin_own.at[(q[0] * 2 + q[1]) * 2 + q[2]],
            hin_o.at[plane],
            hs.at[0, k],
            hr.at[0, k],
            at(hi, *q[:3]),
        )
        for k, q in enumerate(others)
    ]
    t.cross(5)
    for copy in t_p:
        copy.wait()
    acc[...] = acc2[...] + sp[0] + sp[1] + sp[2]
    t_z = [send(acc, sz.at[k], ts.at[4 + k], tr.at[4 + k], z_to[k]) for k in range(nz - 1)]
    t.line(5)
    for w in range(nw):
        late += t.last(w, fin[w], gos[w], fsem)
    for copy in t_z:
        copy.wait()
    value = acc[...]
    for k in range(nz - 1):
        value += sz[k]
    total[...] = value
    for copy in late:
        copy.wait()


FETCHED = (9, 14, 12, 13, 8, 11, 7, 1)


def back_scatter(dp, rows, d_hidden, x, gain, masks, weights, saved, ffn_grads, ffn_stats, shards, hin):
    nz, nw = dp // 2, len(shards)
    tokens = x.shape[0]
    group = masks[0].shape[0]
    most = max(7, nz)
    stat_shape = (16, 128)
    operands = [d_hidden, x, gain, *masks, *weights, *saved, *ffn_grads, hin, ffn_stats]
    shapes = [jax.ShapeDtypeStruct((dp, group, rows, D), BF), jax.ShapeDtypeStruct(stat_shape, F32)]
    shapes += [jax.ShapeDtypeStruct(s, F32) for s in shards]
    shapes.append(jax.ShapeDtypeStruct(hin.shape[1:], BF))
    scratch = [pltpu.VMEM(operands[k].shape, operands[k].dtype) for k in FETCHED]
    scratch.append(DMA((len(FETCHED),)))
    scratch += [pltpu.VMEM((s[0] * 8 * nz, s[1]), BF) for s in shards[2:]]
    split = [(2 * s[0], s[1] // 2) for s in shards]
    scratch += [pltpu.VMEM((8, D), F32)]
    scratch += attend_back_scratch(tokens, masks[0])
    scratch += [pltpu.VMEM((nz, 2, 2) + s, BF) for s in split]
    scratch += [pltpu.VMEM((nz, 2) + s, BF) for s in split]
    scratch += [pltpu.VMEM((nz,) + s, BF) for s in split]
    scratch += [pltpu.VMEM((nz - 1,) + s, BF) for s in split]
    scratch += [pltpu.VMEM(s, F32) for s in split]
    scratch += [
        pltpu.VMEM(hin.shape[1:], BF),
        pltpu.VMEM((nz - 1,) + hin.shape[1:], BF),
        pltpu.VMEM(stat_shape, F32),
        pltpu.VMEM(stat_shape, F32),
        pltpu.VMEM((3,) + stat_shape, F32),
        pltpu.VMEM((nz - 1,) + stat_shape, F32),
        pltpu.VMEM(stat_shape, F32),
        DMA((5,)),
        DMA((dp,)),
        DMA((dp,)),
        DMA((nw,)),
        DMA((nw,)),
        DMA((nw, 4)),
        DMA((nw, 4)),
        DMA((nw, nz)),
        DMA((nw, nz)),
        DMA((3, most)),
        DMA((3, most)),
        DMA((4 + nz,)),
        DMA((4 + nz,)),
        DMA((nw,)),
        DMA((nw,)),
        DMA((nw,)),
    ]
    return call(
        functools.partial(back_scatter_kernel, dp, shards),
        shapes,
        operands,
        [ANY if k in FETCHED else VM for k in range(len(operands) - 4)] + [ANY] * 3 + [VM],
        [VM] * len(shapes),
        scratch,
        6,
    )


def routing(routes, pieces, piece_len):
    places = jnp.arange(pieces * piece_len)
    routed = jnp.any(routes[:, None, :] == places[None, :, None], axis=-1)
    routed = routed.reshape(-1, pieces, piece_len)
    before = jnp.arange(piece_len)[:, None] < jnp.arange(piece_len)[None, :]
    rank = jnp.einsum(
        "skp,pq->skq", routed.astype(BF), before.astype(BF), preferred_element_type=F32
    )
    slots = jnp.arange(CAP, dtype=F32)
    hot = routed[:, :, None, :] & (rank[:, :, None, :] == slots[None, None, :, None])
    filled = jnp.any(hot, axis=-1)
    spots = jnp.sum(jnp.where(hot, places.reshape(1, pieces, 1, piece_len), 0), axis=-1)
    return hot, jnp.where(filled, spots, -1)


def local(
    layer_input,
    teacher,
    lengths,
    dealing,
    attn_routes,
    ffn_routes,
    ffn_scores,
    gain_attn,
    gain_ffn,
    light_qkv,
    light_out,
    heavy_qkv,
    heavy_out,
    light_in,
    light_down,
    heavy_in,
    heavy_down,
):
    dp = lax.axis_size("dp")
    pieces = lax.axis_size("fsdp")
    data_index = lax.axis_index("dp")
    piece = lax.axis_index("fsdp")
    nz = dp // 2
    n = dp * pieces
    seqs = dealing.shape[0]
    group = seqs // dp
    gain_len = gain_attn.shape[0]
    hidden_units = heavy_in.shape[1] // 2 // n
    mine = data_index * pieces + piece
    tokens = layer_input.shape[2] * dp
    matrices = (light_qkv, heavy_qkv, light_out, heavy_out, light_in, light_down)
    hin_rows = heavy_in.shape[0]
    token_count = jnp.sum(lengths).astype(F32)
    merged = (
        layer_input.shape[2] % 16 == 0
        and hidden_units % 128 == 0
        and all(m.shape[0] % 8 == 0 and m.shape[1] % 256 == 0 for m in (*matrices, heavy_down))
    )
    if merged:
        xin, hin_src, gains = prepare(dealing, layer_input[:, 0], heavy_in, gain_attn, gain_ffn)
        integers = (dealing.reshape(1, -1), lengths.reshape(1, -1), attn_routes, ffn_routes, ffn_scores)
        got = gather_attend(dp, xin, [gains, *matrices], hin_src, integers)
    else:
        xin = deal_rows(dealing, layer_input[:, 0])
        owned = jnp.arange(D)[None, :] // gain_len == mine
        spread_out = jnp.broadcast_to(
            jnp.stack([gain_attn, gain_ffn])[:, None, :], (2, D // gain_len, gain_len)
        ).reshape(2, D)
        gains = jnp.pad(jnp.where(owned, spread_out, 0.0).astype(BF), ((0, 6), (0, 0)))
        hin_src = (
            heavy_in.reshape(hin_rows, 2, nz, 8, hidden_units)
            .transpose(3, 0, 1, 2, 4)
            .reshape(8, hin_rows, 2 * nz * hidden_units)
        )
        if hin_rows % 8:
            hin_src = hin_src.reshape(8, -1, 128)
        got = gather_all(dp, xin, [gains] + [packed(m) for m in matrices], hin_src)
    flat_x = got[0].reshape(-1, D)
    w_lqkv, w_hqkv, w_lout, w_hout, w_lin, w_ldown = (
        unpacked(full, *m.shape) for full, m in zip(got[2:8], matrices)
    )
    w_hin = unpacked(got[8], hin_rows, 2 * nz * hidden_units)
    attn_weights = (w_lqkv, w_hqkv, w_lout, w_hout)
    if merged:
        gain, tables, (hidden, *saved) = got[9], got[10:19], got[19:]
        masks, ffn_masks = tables[:4], tables[4:]
    else:
        gain = jnp.sum(got[1].reshape(n, 8, D).astype(F32), axis=0)
        masks, ffn_masks = integer_tables(
            dealing, lengths, attn_routes, ffn_routes, ffn_scores, group, pieces, tokens
        )
        hidden, *saved = attend(flat_x, gain, *masks, *attn_weights)
    f_select, f_select_t, slot_score, weight_mask, weight_scale = ffn_masks
    grad_lin, grad_ldown, grad_hin, g_hdown, d_hidden, ffn_stats = feed_forward(
        nz,
        merged,
        hidden,
        f_select,
        f_select_t,
        slot_score,
        gain,
        teacher.reshape(-1, D),
        weight_mask,
        weight_scale,
        w_lin,
        w_ldown,
        w_hin,
        heavy_down,
    )
    rows = tokens // dp
    shards = (light_in, light_down, heavy_out, light_out, heavy_qkv, light_qkv)
    hin_part = grad_hin.reshape((nz, 8) + hin_src.shape[1:])
    if merged:
        done = back_scatter(
            dp,
            rows,
            d_hidden,
            flat_x,
            gain,
            masks,
            attn_weights,
            saved,
            (grad_lin, grad_ldown),
            ffn_stats,
            tuple(shard.shape for shard in shards),
            hin_part,
        )
    else:
        grad_lqkv, grad_hqkv, grad_lout, grad_hout, d_inputs, attn_stats = attend_back(
            d_hidden, flat_x, gain, *masks, attn_weights, saved
        )
        stats = jnp.concatenate(
            [
                attn_stats[0].reshape(-1, 128),
                ffn_stats[0].reshape(-1, 128),
                jnp.broadcast_to(jnp.sum(ffn_stats[1]), (4, 128)),
            ]
        )
        grads = (grad_lin, grad_ldown, grad_hout, grad_lout, grad_hqkv, grad_lqkv)
        sent = [packed_full(grad, shard.shape, nz) for grad, shard in zip(grads, shards)]
        done = scatter_all(
            dp, d_inputs.reshape(group, dp, rows, D), stats, sent, hin_part
        )
    summed = done[1]
    loss_value = summed[12, 0] / (D * token_count)
    own_one = lax.dynamic_slice_in_dim(summed[:6].reshape(-1), mine * gain_len, gain_len)
    own_two = lax.dynamic_slice_in_dim(summed[6:12].reshape(-1), mine * gain_len, gain_len)
    back_rows = done[0].reshape(seqs, rows, D)
    if merged:
        d_layer, g_hin, *owned = finish_all(
            n, dealing, back_rows, done[8], [*done[2:8], g_hdown], heavy_in.shape
        )
    else:
        d_layer = undeal_rows(dealing, back_rows)
        owned = [full.reshape(shard.shape) for full, shard in zip(done[2:8], shards)]
        owned.append(g_hdown)
        g_hin = (
            done[8]
            .astype(F32)
            .reshape(8, hin_rows, 2, nz, hidden_units)
            .transpose(1, 2, 3, 0, 4)
            .reshape(heavy_in.shape)
        )
    g_lin, g_ldown, g_hout, g_lout, g_hqkv, g_lqkv, g_hdown = owned
    return (
        loss_value,
        d_layer[:, None],
        own_one,
        own_two,
        g_lqkv,
        g_lout,
        g_hqkv,
        g_hout,
        g_lin,
        g_ldown,
        g_hin,
        g_hdown,
    )


def integer_tables(dealing, lengths, attn_routes, ffn_routes, ffn_scores, group, pieces, tokens):
    seqs = dealing.shape[0]
    data_index = lax.axis_index("dp")
    piece = lax.axis_index("fsdp")
    chosen = lax.dynamic_slice_in_dim(dealing, data_index * group, group)
    one = chosen[:, None] == jnp.arange(seqs)[None, :]
    seq_lengths = jnp.sum(jnp.where(one, lengths[None, :], 0), axis=1)
    attn_pick = jnp.sum(jnp.where(one[:, :, None], attn_routes[None], 0), axis=1)
    ffn_pick = jnp.sum(jnp.where(one[:, :, None], ffn_routes[None], 0), axis=1)
    score_pick = jnp.sum(jnp.where(one[:, :, None], ffn_scores[None], 0.0), axis=1)
    token_count = jnp.sum(lengths).astype(F32)
    positions = piece * tokens + jnp.arange(tokens)
    valid_mask = positions[None, :] < seq_lengths[:, None]
    a_hot, a_spots = routing(attn_pick, pieces, tokens)
    f_hot, f_spots = routing(ffn_pick, pieces, tokens)
    a_select = lax.dynamic_index_in_dim(a_hot, piece, 1, False).astype(BF)
    f_select = lax.dynamic_index_in_dim(f_hot, piece, 1, False).astype(BF)
    a_spot = lax.dynamic_index_in_dim(a_spots, piece, 1, False)
    f_spot = lax.dynamic_index_in_dim(f_spots, piece, 1, False)
    slot_score = jnp.sum(
        jnp.where(f_spot[:, :, None] == ffn_pick[:, None, :], score_pick[:, None, :], 0.0), axis=-1
    )
    key_pos = piece * tokens - WIN + jnp.arange(tokens + 2 * WIN)
    live_key = (key_pos >= 0)[None, :] & (key_pos[None, :] < seq_lengths[:, None])
    key_line = jnp.where(live_key, 0.0, MASKED)
    key_bias = jnp.stack(
        [key_line[:, b : b + 3 * WIN] for b in range(0, tokens, WIN)], axis=1
    ).reshape(-1, 1, 3 * WIN)
    all_spots = a_spots.reshape(group, pieces * CAP)
    heavy_allowed = ((all_spots >= 0) & (all_spots < seq_lengths[:, None]))[:, None, :] | (
        a_spot[:, :, None] == all_spots[:, None, :]
    )
    heavy_bias = jnp.where(heavy_allowed, 0.0, MASKED)
    weight_mask = valid_mask.reshape(-1, 1).astype(F32)
    masks = (a_select, a_select.swapaxes(1, 2), key_bias, heavy_bias)
    ffn_masks = (
        f_select,
        f_select.swapaxes(1, 2),
        slot_score.reshape(-1, 1),
        weight_mask,
        2.0 * weight_mask / (D * token_count),
    )
    return masks, ffn_masks


def packed_full(grad, shard_shape, nz):
    rows, columns = shard_shape
    if rows % 8 == 0:
        return grad.reshape(nz, 2, 2, 2, rows, columns)
    return grad.reshape(nz, 2, 2, 2, rows * columns // 128, 128)


def solution(mesh):
    split = P(("dp", "fsdp"))
    matrix = P(("dp", "fsdp"), None)
    placed = (
        P(None, "fsdp", "dp", None),
        P("dp", "fsdp", None, None),
        P(),
        P(),
        P(),
        P(),
        P(),
        split,
        split,
    ) + (matrix,) * 8
    return jax.shard_map(
        local,
        mesh=mesh,
        in_specs=placed,
        out_specs=(P(), P(None, "fsdp", "dp", None), split, split) + (matrix,) * 8,
        check_vma=False,
    )
```

```python
import functools
import jax
import jax.numpy as jnp
from jax import lax
from jax.experimental import pallas as pl
from jax.experimental.pallas import tpu as pltpu
from jax.sharding import PartitionSpec as P

D = 768
HL = 8
HH = 12
DH = 64
FL = 1024
FH = 4096
WIN = 128
CAP = 64

EPSILON = 1e-06
MASKED = -1000000000.0
SCORE_SCALE = 0.125
MESH = pl.DeviceIdType.MESH
BF = jnp.bfloat16
F32 = jnp.float32
ANY = pl.BlockSpec(memory_space=pl.ANY)
VM = pl.BlockSpec(memory_space=pltpu.VMEM)
DMA = pltpu.SemaphoreType.DMA
VMEM_BYTES = 60 * 1024 * 1024


def place():
    d = lax.axis_index("dp")
    f = lax.axis_index("fsdp")
    return d // 2, d % 2, f // 2, f % 2


def at(hi, lo, x, c):
    return (hi * 2 + lo, x * 2 + c)


def meet(peers):
    barrier = pltpu.get_barrier_semaphore()
    for peer in peers:
        pl.semaphore_signal(barrier, inc=1, device_id=peer, device_id_type=MESH)
    pl.semaphore_wait(barrier, len(peers))


def send(src, dst, send_sem, recv_sem, peer):
    copy = pltpu.make_async_remote_copy(
        src_ref=src,
        dst_ref=dst,
        send_sem=send_sem,
        recv_sem=recv_sem,
        device_id=peer,
        device_id_type=MESH,
    )
    copy.start()
    return copy


def keep(src, dst, sem):
    copy = pltpu.make_async_copy(src, dst, sem)
    copy.start()
    return copy


def quad_peers():
    hi, lo, x, c = place()
    return [(lo, 1 - x), (1 - lo, x), (1 - lo, 1 - x)]


def call(kernel, out_shape, operands, in_specs, out_specs, scratch, collective_id):
    return pl.pallas_call(
        kernel,
        out_shape=out_shape,
        in_specs=in_specs,
        out_specs=out_specs,
        scratch_shapes=scratch,
        compiler_params=pltpu.CompilerParams(
            collective_id=collective_id, has_side_effects=True, vmem_limit_bytes=VMEM_BYTES
        ),
    )(*operands)


def deal_kernel(deal_ref, x_ref, o_ref):
    def body(i, carry):
        o_ref[i] = x_ref[deal_ref[i]]
        return carry

    lax.fori_loop(0, o_ref.shape[0], body, 0)


def deal_rows(dealing, rows):
    return pl.pallas_call(
        deal_kernel,
        out_shape=jax.ShapeDtypeStruct(rows.shape, rows.dtype),
        in_specs=[pl.BlockSpec(memory_space=pltpu.SMEM), VM],
        out_specs=VM,
        compiler_params=pltpu.CompilerParams(vmem_limit_bytes=VMEM_BYTES),
    )(dealing, rows)


def undeal_kernel(deal_ref, x_ref, o_ref):
    def body(i, carry):
        o_ref[deal_ref[i]] = x_ref[i].astype(F32)
        return carry

    lax.fori_loop(0, x_ref.shape[0], body, 0)


def undeal_rows(dealing, rows):
    return pl.pallas_call(
        undeal_kernel,
        out_shape=jax.ShapeDtypeStruct(rows.shape, F32),
        in_specs=[pl.BlockSpec(memory_space=pltpu.SMEM), VM],
        out_specs=VM,
        compiler_params=pltpu.CompilerParams(vmem_limit_bytes=VMEM_BYTES),
    )(dealing, rows)


def prepare_kernel(deal_ref, x_ref, heavy_ref, one_ref, two_ref, xin, hin, gains):
    def body(i, carry):
        xin[i] = x_ref[deal_ref[i]]
        return carry

    lax.fori_loop(0, xin.shape[0], body, 0)
    count = one_ref.shape[1]
    units = D // count
    step = heavy_ref.shape[1] // 2 // units
    for j in range(8):
        for k in range(units // 8):
            for g in (0, 1):
                start = g * heavy_ref.shape[1] // 2 + (k * 8 + j) * step
                spot = (g * (units // 8) + k) * step
                hin[j, :, spot : spot + step] = heavy_ref[:, start : start + step]
    mine = lax.axis_index("dp") * 4 + lax.axis_index("fsdp")
    row = lax.broadcasted_iota(jnp.int32, (count, D), 0)
    lane = lax.broadcasted_iota(jnp.int32, (count, D), 1)
    hot = jnp.where(lane == row + mine * count, 1.0, 0.0).astype(BF)
    lines = [jnp.broadcast_to(ref[...], (8, count)) for ref in (one_ref, two_ref)]
    one, two = (jnp.dot(line, hot, preferred_element_type=F32) for line in lines)
    kind = lax.broadcasted_iota(jnp.int32, (8, D), 0)
    gains[...] = jnp.where(kind == 0, one, jnp.where(kind == 1, two, 0.0)).astype(BF)


def prepare(dealing, rows, heavy_in, gain_one, gain_two):
    count = gain_one.shape[0]
    columns = heavy_in.shape[1] // 8
    return pl.pallas_call(
        prepare_kernel,
        out_shape=[
            jax.ShapeDtypeStruct(rows.shape, BF),
            jax.ShapeDtypeStruct((8, heavy_in.shape[0], columns), BF),
            jax.ShapeDtypeStruct((8, D), BF),
        ],
        in_specs=[pl.BlockSpec(memory_space=pltpu.SMEM), VM, VM, VM, VM],
        out_specs=[VM] * 3,
        compiler_params=pltpu.CompilerParams(vmem_limit_bytes=VMEM_BYTES),
    )(dealing, rows, heavy_in, gain_one.reshape(1, count), gain_two.reshape(1, count))


def finish_kernel(units, deal_ref, x_ref, hin, summed, lengths, *refs):
    count = (len(refs) - 5) // 2
    ins, (rows, heavy, loss, one, two), outs = refs[:count], refs[count : count + 5], refs[count + 5 :]
    tokens = jnp.sum(lengths[...].astype(F32), axis=1, keepdims=True)
    loss[...] = summed[12:13, 0:1] / (D * tokens)
    owned = one.shape[1]
    mine = lax.axis_index("dp") * 4 + lax.axis_index("fsdp")
    row = lax.broadcasted_iota(jnp.int32, (128, owned), 0)
    lane = lax.broadcasted_iota(jnp.int32, (128, owned), 1)
    gains = [jnp.zeros((1, owned), F32)] * 2
    for k in range(D // 128):
        hot = jnp.where(row + k * 128 == lane + mine * owned, 1.0, 0.0)
        part = jnp.dot(summed[...], hot, precision=lax.Precision.HIGHEST, preferred_element_type=F32)
        gains = [gains[0] + part[k : k + 1], gains[1] + part[6 + k : 7 + k]]
    one[...] = gains[0]
    two[...] = gains[1]

    def body(i, carry):
        rows[deal_ref[i]] = x_ref[i].astype(F32)
        return carry

    lax.fori_loop(0, x_ref.shape[0], body, 0)
    step = heavy.shape[1] // 2 // units
    for j in range(8):
        for k in range(units // 8):
            for g in (0, 1):
                start = g * heavy.shape[1] // 2 + (k * 8 + j) * step
                spot = (g * (units // 8) + k) * step
                heavy[:, start : start + step] = hin[j, :, spot : spot + step].astype(F32)
    for source, out in zip(ins, outs):
        out[...] = source[...]


def finish_all(units, dealing, rows, hin, summed, lengths, grads, heavy_shape, owned):
    shapes = [jax.ShapeDtypeStruct(rows.shape, F32), jax.ShapeDtypeStruct(heavy_shape, F32)]
    shapes += [jax.ShapeDtypeStruct(shape, F32) for shape in ((1, 1), (1, owned), (1, owned))]
    shapes += [jax.ShapeDtypeStruct(g.shape, F32) for g in grads]
    return pl.pallas_call(
        functools.partial(finish_kernel, units),
        out_shape=shapes,
        in_specs=[pl.BlockSpec(memory_space=pltpu.SMEM)] + [VM] * (4 + len(grads)),
        out_specs=[VM] * len(shapes),
        compiler_params=pltpu.CompilerParams(vmem_limit_bytes=VMEM_BYTES),
    )(dealing, rows, hin, summed, lengths, *grads)


def packed(matrix):
    rows, columns = matrix.shape
    if rows % 8 == 0:
        return matrix
    return matrix.reshape(rows * columns // 128, 128)


def unpacked(gathered, rows, columns):
    return gathered.reshape(-1, rows, columns).reshape(-1, columns)


def plane_others():
    hi, lo, x, c = place()
    others = []
    for a in (0, 1):
        for b in (0, 1):
            for e in (0, 1):
                if a or b or e:
                    others.append(
                        (1 - lo if a else lo, 1 - x if b else x, 1 - c if e else c, b or e)
                    )
    return others


class Gather:
    def __init__(self, dp, xin, ws, hin, xo, wos, hin_o, sems, halves=None):
        self.dp, self.nz = dp, dp // 2
        self.xin, self.ws, self.hin = xin, ws, hin
        self.xo, self.wos, self.hin_o = xo, wos, hin_o
        self.loc, self.xs, self.xr, self.zs, self.zr = sems[:5]
        self.ps, self.pr, self.cs, self.cr, self.hs, self.hr = sems[5:]
        self.hi, self.lo, self.x, self.c = place()
        hi, lo, x, c = place()
        self.d = hi * 2 + lo
        self.home = (lo * 2 + x) * 2 + c
        self.rows_to = [(lax.rem(self.d + k, dp), x * 2 + c) for k in range(1, dp)]
        self.z_to = [at(lax.rem(hi + k, self.nz), lo, x, c) for k in range(1, self.nz)]
        self.others = plane_others()
        nw = len(ws)
        self.kept, self.z, self.p, self.f, self.k = ([None] * nw for _ in range(5))

        self.halves = halves

    def lanes(self, w, c):
        half = self.ws[w].shape[1] // 2
        return pl.ds(pl.multiple_of(c * half, 128), half)

    def shard(self, w, z, lo, x):
        if self.halves is None:
            return self.wos[w].at[z, lo, x, self.c]
        return self.wos[w].at[z, lo, x, :, self.lanes(w, self.c)]

    def swap(self, w):
        mine, mate, _, sems = self.halves
        partner = at(self.hi, self.lo, self.x, 1 - self.c)
        self.kept[w] = keep(self.ws[w].at[:, self.lanes(w, self.c)], mine[w], sems[0].at[w])
        out = self.ws[w].at[:, self.lanes(w, 1 - self.c)]
        self.z[w] = send(out, mate[w], sems[1].at[w], sems[2].at[w], partner)

    def join(self, w):
        mine, mate, base, _ = self.halves
        self.kept[w].wait()
        self.z[w].wait()
        a, b = mine[w][...].astype(F32), mate[w][...].astype(F32)
        first = self.c == 0
        rows = [jnp.where(first, a, b), jnp.where(first, b, a)]
        base[w][...] = jnp.concatenate(rows, axis=0).astype(BF)
        self.line(w)

    def meet(self):
        peers = self.rows_to + [at(self.hi, *q[:3]) for q in self.others if q[3]]
        meet(peers)

    def rows(self):
        group = self.xin.shape[0] // self.dp
        nw = len(self.ws)
        spot = self.xo.at[:, self.d]
        self.own = keep(self.xin.at[pl.ds(self.d * group, group)], spot, self.loc.at[nw])
        self.moved = [
            send(self.xin.at[pl.ds(to[0] * group, group)], spot, self.xs.at[k], self.xr.at[k], to)
            for k, to in enumerate(self.rows_to)
        ]

    def rows_ready(self):
        self.own.wait()
        for copy in self.moved:
            copy.wait()

    def line(self, w):
        spot = self.shard(w, self.hi, self.lo, self.x)
        own = self.ws[w] if self.halves is None else self.halves[2][w]
        self.kept[w] = keep(own, spot, self.loc.at[w])
        self.z[w] = [
            send(own, spot, self.zs.at[w, k], self.zr.at[w, k], to)
            for k, to in enumerate(self.z_to)
        ]

    def onward(self, part, w, k, to, sems):
        return send(part, part, sems[0].at[w, k], sems[1].at[w, k], to)

    def plane(self, w):
        self.kept[w].wait()
        for copy in self.z[w]:
            copy.wait()
        hi, lo, x, c = self.hi, self.lo, self.x, self.c
        column = self.shard(w, slice(None), lo, x)
        plane = (self.ps, self.pr)
        self.p[w] = [
            self.onward(column, w, 0, at(hi, lo, 1 - x, c), plane),
            self.onward(column, w, 1, at(hi, 1 - lo, x, c), plane),
        ]
        self.k[w] = [self.onward(column, w, 0, at(hi, lo, x, 1 - c), (self.cs, self.cr))]

    def cross(self, w):
        hi, lo, x, c = self.hi, self.lo, self.x, self.c
        plane, core, half = (self.ps, self.pr), (self.cs, self.cr), self.nz // 2
        partner = at(hi, lo, x, 1 - c)
        self.p[w][1].wait()
        part = self.shard(w, pl.ds(0, half), 1 - lo, x)
        first = self.onward(part, w, 2, at(hi, lo, 1 - x, c), plane)
        self.p[w][0].wait()
        part = self.shard(w, pl.ds(half, self.nz - half), lo, 1 - x)
        self.f[w] = [first, self.onward(part, w, 3, at(hi, 1 - lo, x, c), plane)]
        for k, part in ((1, (1 - lo, x)), (2, (lo, 1 - x))):
            self.k[w].append(
                self.onward(self.shard(w, slice(None), *part), w, k, partner, core)
            )

    def core(self, w):
        for copy in self.f[w]:
            copy.wait()
        part = self.shard(w, slice(None), 1 - self.lo, 1 - self.x)
        partner = at(self.hi, self.lo, self.x, 1 - self.c)
        self.k[w].append(self.onward(part, w, 3, partner, (self.cs, self.cr)))

    def ready(self, w):
        for copy in self.k[w]:
            copy.wait()

    def heavy_plane(self):
        nw, hi = len(self.ws), self.hi
        spot = self.hin_o.at[hi, self.home]
        self.h_own = [
            keep(self.hin.at[self.home], spot, self.loc.at[nw + 1]),
        ]
        self.h_near = [
            send(
                self.hin.at[(q[0] * 2 + q[1]) * 2 + q[2]],
                spot,
                self.hs.at[0, k],
                self.hr.at[0, k],
                at(hi, *q[:3]),
            )
            for k, q in enumerate(self.others)
        ]

    def heavy_line(self):
        for copy in self.h_own + self.h_near:
            copy.wait()
        part = self.hin_o.at[self.hi]
        self.h_far = []
        for k, to in enumerate(self.z_to):
            self.h_far.append(send(part, part, self.hs.at[1, k], self.hr.at[1, k], to))

    def heavy_ready(self):
        for copy in self.h_far:
            copy.wait()


def gather_sems(dp, nw):
    nz, most = dp // 2, max(7, dp // 2)
    return [
        DMA((nw + 2,)),
        DMA((dp,)),
        DMA((dp,)),
        DMA((nw, nz)),
        DMA((nw, nz)),
        DMA((nw, 4)),
        DMA((nw, 4)),
        DMA((nw, 4)),
        DMA((nw, 4)),
        DMA((2, most)),
        DMA((2, most)),
    ]


def gather_kernel(dp, nw, *refs):
    ins, outs, sems = refs[: 2 + nw], refs[2 + nw : 4 + 2 * nw], refs[4 + 2 * nw :]
    g = Gather(dp, ins[0], ins[1:-1], ins[-1], outs[0], outs[1:-1], outs[-1], sems)
    g.meet()
    g.rows()
    for w in range(nw):
        g.line(w)
    g.heavy_plane()
    for w in range(nw):
        g.plane(w)
        if w == 1:
            g.heavy_line()
        if w >= 1:
            g.cross(w - 1)
        if w >= 2:
            g.core(w - 2)
    g.cross(nw - 1)
    for w in range(nw - 2, nw):
        g.core(w)
    g.rows_ready()
    for w in range(nw):
        g.ready(w)
    g.heavy_ready()


def gather_shapes(dp, xin, weights, hin, paired):
    nz = dp // 2
    seqs, rows, _ = xin.shape
    shapes = [jax.ShapeDtypeStruct((seqs // dp, dp, rows, D), BF)]
    if paired:
        shapes += [jax.ShapeDtypeStruct((nz, 2, 2, 2 * w.shape[0], w.shape[1]), BF) for w in weights]
    else:
        shapes += [jax.ShapeDtypeStruct((nz, 2, 2, 2) + w.shape, BF) for w in weights]
    shapes.append(jax.ShapeDtypeStruct((nz,) + hin.shape, BF))
    return shapes


def gather_all(dp, xin, weights, hin):
    nw = len(weights)
    return call(
        functools.partial(gather_kernel, dp, nw),
        gather_shapes(dp, xin, weights, hin, False),
        [xin, *weights, hin],
        [ANY] * (2 + nw),
        [ANY] * (2 + nw),
        gather_sems(dp, nw),
        1,
    )


def rim_exchange(left, right, from_left, from_right, ls, lr, rs, rr):
    d = lax.axis_index("dp")
    f = lax.axis_index("fsdp")
    last = lax.axis_size("fsdp") - 1

    def down():
        return pltpu.make_async_remote_copy(
            src_ref=left,
            dst_ref=from_right,
            send_sem=ls,
            recv_sem=lr,
            device_id=(d, lax.max(f - 1, 0)),
            device_id_type=MESH,
        )

    def up():
        return pltpu.make_async_remote_copy(
            src_ref=right,
            dst_ref=from_left,
            send_sem=rs,
            recv_sem=rr,
            device_id=(d, lax.min(f + 1, last)),
            device_id_type=MESH,
        )

    @pl.when(f > 0)
    def _():
        down().start()

    @pl.when(f < last)
    def _():
        up().start()

    @pl.when(f == 0)
    def _():
        from_left[...] = jnp.zeros(from_left.shape, from_left.dtype)

    @pl.when(f == last)
    def _():
        from_right[...] = jnp.zeros(from_right.shape, from_right.dtype)

    def finish():
        @pl.when(f > 0)
        def _():
            down().wait_send()
            up().wait_recv()

        @pl.when(f < last)
        def _():
            up().wait_send()
            down().wait_recv()

    return finish


def line_peers():
    hi, lo, x, c = place()
    return [at(hi, lo, x, 1 - c), at(hi, lo, 1 - x, c), at(hi, lo, 1 - x, 1 - c)]


def dot(left, right):
    return jnp.dot(left, right, preferred_element_type=F32)


def dot_back(left, right):
    return lax.dot_general(left, right, (((1,), (1,)), ((), ())), preferred_element_type=F32)


def dot_grad(left, right):
    return lax.dot_general(left, right, (((0,), (0,)), ((), ())), preferred_element_type=F32)


def halves(value):
    high = value.astype(BF)
    return high, (value - high.astype(F32)).astype(BF)


def tiles(extent, step, body):
    def run(i, carry):
        body(pl.ds(pl.multiple_of(i * step, step), step))
        return carry

    lax.fori_loop(0, extent // step, run, 0)


GELU_A = 0.7978845608028654
GELU_B = 0.044715


def gelu_parts(v):
    square = v * v
    t = jnp.tanh(GELU_A * v * (1.0 + GELU_B * square))
    value = 0.5 * v * (1.0 + t)
    slope = 0.5 * (1.0 + t) + 0.5 * v * (1.0 - t * t) * GELU_A * (1.0 + 3.0 * GELU_B * square)
    return value, slope


def gelu_value(v):
    return 0.5 * v * (1.0 + jnp.tanh(GELU_A * v * (1.0 + GELU_B * v * v)))


def ffn_kernel(
    nz,
    swapped,
    hidden,
    select,
    select_t,
    score,
    gain,
    teach_hbm,
    mask,
    scale,
    w_in_hbm,
    w_dn_hbm,
    w_hin_hbm,
    hdn,
    g_in_hbm,
    g_dn_hbm,
    g_hin_hbm,
    hdn_o,
    d_hidden,
    stats,
    teach,
    w_in,
    w_dn,
    w_hin,
    g_in,
    g_dn,
    g_hin,
    moves_sem,
    w_line,
    g_line,
    g_in_line,
    hn,
    every,
    d_every,
    up_l,
    z,
    up_h,
    zh,
    part,
    near,
    far,
    out,
    dl,
    dup_l,
    dup_h,
    dhn,
    ps,
    pr,
    cs,
    cr,
    qs,
    qr,
    es,
    er,
    zs,
    zr,
    own,
    *mates,
):
    hi, lo, x, c = place()
    quad = quad_peers()
    partner = at(hi, lo, x, 1 - c)
    spots = [l2 * 2 + x2 for l2, x2 in quad]
    home = lo * 2 + x
    tokens = hidden.shape[0]
    group, cap, width = select.shape
    fl = z.shape[1]
    fh = zh.shape[3]
    block = 4 * cap
    z_index = [lax.rem(hi + k, nz) for k in range(1, nz)]
    z_to = [at(k, lo, x, c) for k in z_index]
    meet([at(hi, l2, x2, c) for l2, x2 in quad] + [partner] + z_to)
    pairs = ((w_in_hbm, w_in), (w_dn_hbm, w_dn), (w_hin_hbm, w_hin), (teach_hbm, teach))
    fetched = [keep(source, ref, moves_sem.at[k]) for k, (source, ref) in enumerate(pairs)]
    hdn_own = keep(hdn, w_line.at[hi], own)
    hdn_far = [send(hdn, w_line.at[hi], zs.at[0, k], zr.at[0, k], to) for k, to in enumerate(z_to)]
    w_hdn = w_line.reshape(-1, D)

    def span(s):
        return slice(s * width, (s + 1) * width)

    def slots(s):
        return slice(s * cap, (s + 1) * cap)

    def spread(buffer, s, i):
        spot = buffer.at[s, c, home]
        there = [
            send(spot, spot, ps.at[i, k], pr.at[i, k], at(hi, l2, x2, c))
            for k, (l2, x2) in enumerate(quad)
        ]
        return there, [send(spot, spot, cs.at[i, 3], cr.at[i, 3], partner)]

    def relay(buffer, s, i, there, back):
        for k, q in enumerate(spots):
            there[k].wait()
            other = buffer.at[s, c, q]
            back.append(send(other, other, cs.at[i, k], cr.at[i, k], partner))

    def fold(s, i, copy):
        copy.wait()
        there = []
        for k, q in enumerate(spots):
            near[i, q] = (near[i, q].astype(F32) + part[s, c, q].astype(F32)).astype(BF)
            l2, x2 = quad[k]
            there.append(
                send(near.at[i, q], far.at[i, k], qs.at[i, k], qr.at[i, k], at(hi, l2, x2, c))
            )
        return there

    def folded(s, i, there):
        for copy in there:
            copy.wait()
        return (
            near[i, home].astype(F32)
            + part[s, c, home].astype(F32)
            + far[i, 0].astype(F32)
            + far[i, 1].astype(F32)
            + far[i, 2].astype(F32)
        )

    def norm(r):
        h = hidden[r, :]
        inv = lax.rsqrt(jnp.mean(h * h, axis=-1, keepdims=True) + EPSILON)
        hn[r, :] = (h * inv * gain[1:2, :]).astype(BF)

    seqs = range(group)
    moves = {}
    tiles(tokens, 128, norm)
    for s in seqs:
        every[s, c, home] = dot(select[s], hn[span(s), :]).astype(BF)
        moves[s] = spread(every, s, s)

    def light_up(r):
        up_l[r, :] = dot(hn[r, :], w_in[...])
        z[r, :] = (gelu_value(up_l[r, :fl]) * up_l[r, fl:]).astype(BF)

    fetched[0].wait()
    tiles(tokens, width, light_up)
    for s in seqs:
        relay(every, s, s, *moves[s])

    def light_down(r):
        out[r, :] = hidden[r, :] + dot(z[r, :], w_dn[...])

    fetched[1].wait()
    tiles(tokens, width, light_down)

    def light_slopes(r):
        value, slope = gelu_parts(up_l[r, :fl])
        up_l[r, :fl] = up_l[r, fl:] * slope
        up_l[r, fl:] = value

    def heavy_up(s, e):
        up_h[s, e] = dot(every[s, e].reshape(block, D), w_hin[...])
        zh[s, e] = (gelu_value(up_h[s, e, :, :fh]) * up_h[s, e, :, fh:]).astype(BF)

    def heavy_down(s, e):
        part[s, e] = dot(zh[s, e], w_hdn[...]).astype(BF).reshape(4, cap, D)

    fetched[2].wait()
    sums = {}
    for s in seqs:
        for copy in moves[s][1]:
            copy.wait()
        heavy_up(s, 1 - c)
        heavy_up(s, c)
    tiles(tokens, 64, light_slopes)
    hdn_own.wait()
    for copy in hdn_far:
        copy.wait()
    first = {}
    for s in seqs:
        heavy_down(s, 1 - c)
        first[s] = send(part.at[s, 1 - c], near.at[s], es.at[s], er.at[s], partner)
        if s > 0:
            sums[s - 1] = fold(s - 1, s - 1, first[s - 1])
        heavy_down(s, c)
    sums[group - 1] = fold(group - 1, group - 1, first[group - 1])
    for s in seqs:
        for e in (0, 1):

            def heavy_slopes(r, s=s, e=e):
                value, slope = gelu_parts(up_h[s, e, r, :fh])
                up_h[s, e, r, :fh] = up_h[s, e, r, fh:] * slope
                up_h[s, e, r, fh:] = value

            if s == 0:
                tiles(block, 128, heavy_slopes)
    stats[...] = jnp.zeros(stats.shape, F32)
    fetched[3].wait()

    def light_back(r):
        dz = dot_back(dl[r, :], w_dn[...])
        dup_l[r, :fl] = (dz * up_l[r, :fl]).astype(BF)
        dup_l[r, fl:] = (dz * up_l[r, fl:]).astype(BF)

    for s in seqs:
        r = span(s)
        high, low = halves(folded(s, s, sums[s]) * score[slots(s), :])
        total = out[r, :] + (dot(select_t[s], high) + dot(select_t[s], low))
        m = total - teach[r, :].astype(F32)
        stats[1:2, :] += jnp.sum(mask[r, :] * m * m, axis=0, keepdims=True)
        d = scale[r, :] * m
        out[r, :] = d
        dl[r, :] = d.astype(BF)
        high, low = halves(d)
        picked = dot(select[s], high) + dot(select[s], low)
        d_every[s, c, home] = (picked * score[slots(s), :]).astype(BF)
        moves[s] = spread(d_every, s, group + s)
        light_back(r)
        if s > 0:
            for e in (0, 1):

                def more_slopes(r, s=s, e=e):
                    value, slope = gelu_parts(up_h[s, e, r, :fh])
                    up_h[s, e, r, :fh] = up_h[s, e, r, fh:] * slope
                    up_h[s, e, r, fh:] = value

                tiles(block, 128, more_slopes)

    def heavy_back(s, e):
        dz = dot_back(d_every[s, e].reshape(block, D), w_hdn[...])
        dup_h[s, e, :, :fh] = (dz * up_h[s, e, :, :fh]).astype(BF)
        dup_h[s, e, :, fh:] = (dz * up_h[s, e, :, fh:]).astype(BF)
        v = dot_back(dup_h[s, e], w_hin[...]).astype(BF)
        part[s, e] = v.reshape(4, cap, D)

    for s in seqs:
        relay(d_every, s, group + s, *moves[s])
        dhn[span(s), :] = dot_back(dup_l[span(s), :], w_in[...])
    for s in seqs:
        for copy in moves[s][1]:
            copy.wait()
    count = group * 2 * block
    d_rows = d_every[...].reshape(count, D)
    g_line[...] = dot_grad(zh[...].reshape(count, fh), d_rows).astype(BF)
    g_view = g_line.reshape(nz, -1, D)
    hdn_back = [
        send(g_view.at[k], g_in_line.at[n], zs.at[1, n], zr.at[1, n], z_to[n])
        for n, k in enumerate(z_index)
    ]
    for s in seqs:
        i = group + s
        heavy_back(s, 1 - c)
        first[s] = send(part.at[s, 1 - c], near.at[i], es.at[i], er.at[i], partner)
        if s > 0:
            sums[s - 1] = fold(s - 1, i - 1, first[s - 1])
        heavy_back(s, c)
    sums[group - 1] = fold(group - 1, 2 * group - 1, first[group - 1])

    def light_grad(j):
        g_dn[j, :] = dot_grad(z[:, j], dl[...]).astype(BF)

    tiles(fl, 512, light_grad)
    halved = []

    def swap(k, grad):
        rows, lanes = mates[k].shape[3:]
        view = grad.reshape(nz, 2, 2, rows, 2 * lanes)
        other = pl.ds(pl.multiple_of((1 - c) * lanes, 128), lanes)
        halved.append(view)
        sem = mates[2:]
        return send(view.at[:, :, :, :, other], mates[k], sem[0].at[k], sem[1].at[k], partner)

    def join(k):
        near_k, view, lanes = mates[k], halved[k], mates[k].shape[4]
        own_lanes = pl.ds(pl.multiple_of(c * lanes, 128), lanes)

        def add(n, carry):
            a, b, e = n // 4, (n // 2) % 2, n % 2
            value = near_k[a, b, e].astype(F32) + view[a, b, e, :, own_lanes].astype(F32)
            near_k[a, b, e] = value.astype(BF)
            return carry

        lax.fori_loop(0, nz * 4, add, 0)

    flushed, swaps = [], []
    if swapped:
        swaps.append(swap(0, g_dn))
    else:
        flushed.append(keep(g_dn, g_dn_hbm, moves_sem.at[4]))

    def light_in_grad(j):
        g_in[:, j] = dot_grad(hn[...], dup_l[:, j]).astype(BF)

    tiles(2 * fl, 1024, light_in_grad)
    if swapped:
        swaps.append(swap(1, g_in))
    else:
        flushed.append(keep(g_in, g_in_hbm, moves_sem.at[5]))
    every_rows = every[...].reshape(count, D)

    def heavy_grad(j):
        g_hin[:, j] = dot_grad(every_rows, dup_h[:, :, :, j].reshape(count, 512)).astype(BF)

    tiles(2 * fh, 512, heavy_grad)
    flushed.append(keep(g_hin, g_hin_hbm, moves_sem.at[6]))
    if swapped:
        for k, target in enumerate((g_dn_hbm, g_in_hbm)):
            swaps[k].wait()
            join(k)
            flushed.append(keep(mates[k], target, moves_sem.at[4 + k]))
    for s in seqs:
        r = span(s)
        high, low = halves(folded(s, group + s, sums[s]))
        d = dhn[r, :] + (dot(select_t[s], high) + dot(select_t[s], low))
        h = hidden[r, :]
        inv = lax.rsqrt(jnp.mean(h * h, axis=-1, keepdims=True) + EPSILON)
        dh = d * h
        stats[0:1, :] += jnp.sum(dh * inv, axis=0, keepdims=True)
        mean = jnp.mean(gain[1:2, :] * dh, axis=-1, keepdims=True)
        d_hidden[r, :] = out[r, :] + inv * gain[1:2, :] * d - h * (inv * inv * inv * mean)
    for copy in hdn_back + flushed:
        copy.wait()
    value = g_view[hi].astype(F32)
    for n in range(nz - 1):
        value += g_in_line[n].astype(F32)
    hdn_o[...] = value


def feed_forward(nz, swapped, hidden, select, select_t, score, gain, teach, mask, scale, w_in, w_dn, w_hin, hdn):
    tokens = hidden.shape[0]
    group, cap, _ = select.shape
    fl, fh = w_dn.shape[0], w_hin.shape[1] // 2
    block = (group, 2, 4, cap, D)
    line = (nz,) + hdn.shape
    half_in = (nz, 2, 2, D // (nz * 4), fl)
    half_dn = (nz, 2, 2, fl // (nz * 4), D // 2)
    extra = [pltpu.VMEM(half_dn, BF), pltpu.VMEM(half_in, BF), DMA((2,)), DMA((2,))]
    operands = [hidden, select, select_t, score, gain, teach, mask, scale, w_in, w_dn, w_hin, hdn]
    return call(
        functools.partial(ffn_kernel, nz, swapped),
        [
            jax.ShapeDtypeStruct(half_in if swapped else (D, 2 * fl), BF),
            jax.ShapeDtypeStruct(half_dn if swapped else (fl, D), BF),
            jax.ShapeDtypeStruct((D, 2 * fh), BF),
            jax.ShapeDtypeStruct(hdn.shape, F32),
            jax.ShapeDtypeStruct((tokens, D), F32),
            jax.ShapeDtypeStruct((8, D), F32),
        ],
        operands,
        [VM] * 5 + [ANY] + [VM] * 2 + [ANY] * 4,
        [ANY] * 3 + [VM] * 3,
        [
            pltpu.VMEM((tokens, D), BF),
            pltpu.VMEM((D, 2 * fl), BF),
            pltpu.VMEM((fl, D), BF),
            pltpu.VMEM((D, 2 * fh), BF),
            pltpu.VMEM((D, 2 * fl), BF),
            pltpu.VMEM((fl, D), BF),
            pltpu.VMEM((D, 2 * fh), BF),
            DMA((7,)),
            pltpu.VMEM(line, BF),
            pltpu.VMEM((fh, D), BF),
            pltpu.VMEM((nz - 1,) + hdn.shape, BF),
            pltpu.VMEM((tokens, D), BF),
            pltpu.VMEM(block, BF),
            pltpu.VMEM(block, BF),
            pltpu.VMEM((tokens, 2 * fl), F32),
            pltpu.VMEM((tokens, fl), BF),
            pltpu.VMEM((group, 2, 4 * cap, 2 * fh), F32),
            pltpu.VMEM((group, 2, 4 * cap, fh), BF),
            pltpu.VMEM(block, BF),
            pltpu.VMEM((2 * group, 4, cap, D), BF),
            pltpu.VMEM((2 * group, 3, cap, D), BF),
            pltpu.VMEM((tokens, D), F32),
            pltpu.VMEM((tokens, D), BF),
            pltpu.VMEM((tokens, 2 * fl), BF),
            pltpu.VMEM((group, 2, 4 * cap, 2 * fh), BF),
            pltpu.VMEM((tokens, D), F32),
            DMA((2 * group, 3)),
            DMA((2 * group, 3)),
            DMA((2 * group, 4)),
            DMA((2 * group, 4)),
            DMA((2 * group, 3)),
            DMA((2 * group, 3)),
            DMA((2 * group,)),
            DMA((2 * group,)),
            DMA((2, nz)),
            DMA((2, nz)),
            DMA,
        ]
        + (extra if swapped else []),
        5,
    )


def pair_masks(scale):
    lane = lax.broadcasted_iota(jnp.int32, (1, 2 * DH), 1)
    left = jnp.where(lane < DH, scale, 0.0).astype(BF)
    right = jnp.where(lane < DH, 0.0, scale).astype(BF)
    return left, right


def both(value, masks):
    return jnp.concatenate([value * masks[0], value * masks[1]], axis=0)


def side(stacked):
    rows = stacked.shape[0] // 2
    return jnp.concatenate([stacked[:rows], stacked[rows:]], axis=1)


def pair_forward(q, k, v, bias, ones, scaled):
    scores = dot_back(both(q, scaled), k) + bias
    top = jnp.max(scores, axis=-1, keepdims=True)
    shifted = jnp.exp(scores - top)
    total = jnp.sum(shifted, axis=-1, keepdims=True)
    prob = (shifted / total).astype(BF)
    return dot(side(prob), both(v, ones)).astype(BF), top + jnp.log(total)


def pair_backward(q, k, v, bias, lse, d_out, ones, scaled):
    q2 = both(q, scaled)
    d2 = both(d_out, ones)
    prob = jnp.exp(dot_back(q2, k) + bias - lse)
    d_prob = dot_back(d2, v)
    row = jnp.sum(prob * d_prob, axis=-1, keepdims=True)
    d_scores = (prob * (d_prob - row)).astype(BF)
    dq = dot(side(d_scores), both(k, scaled))
    return dq, dot_grad(d_scores, q2), dot_grad(prob.astype(BF), d2)


def reach_bias(key_bias):
    shape = (WIN, 3 * WIN)
    offset = lax.broadcasted_iota(jnp.int32, shape, 1) - lax.broadcasted_iota(jnp.int32, shape, 0) - WIN
    near = (offset >= -WIN) & (offset <= WIN)
    inner = jnp.where(offset == 0, 0.0, jnp.broadcast_to(key_bias, shape))
    bias = jnp.where(near, inner, MASKED)
    return jnp.concatenate([bias, bias], axis=0)


def put_lse(lse, pair, column):
    lane = lax.broadcasted_iota(jnp.int32, lse.shape, 1)
    rows = lse.shape[0]
    lse = jnp.where(lane == 2 * pair, column[:rows], lse)
    return jnp.where(lane == 2 * pair + 1, column[rows:], lse)


def get_lse(lse, pair):
    return jnp.concatenate([lse[:, 2 * pair : 2 * pair + 1], lse[:, 2 * pair + 1 : 2 * pair + 2]], axis=0)


def attend_body(
    stages,
    x,
    gain,
    select,
    select_t,
    key_bias,
    heavy_bias,
    w_lqkv,
    w_hqkv,
    w_lout,
    w_hout,
    hidden,
    xn,
    lq,
    rim,
    lo_out,
    l_lse,
    a_rows,
    hq,
    kvh,
    ho,
    h_lse,
    ls,
    lr,
    rs,
    rr,
    ss,
    sr,
):
    hi, lo, x_, c = place()
    f = x_ * 2 + c
    tokens = x.shape[0]
    group, cap, width = select.shape
    wl, wh = HL * DH, HH * DH
    ones, scaled = pair_masks(1.0), pair_masks(SCORE_SCALE)
    across, partner = at(hi, lo, 1 - x_, c), at(hi, lo, x_, 1 - c)

    def norm(r):
        h = x[r, :].astype(F32)
        inv = lax.rsqrt(jnp.mean(h * h, axis=-1, keepdims=True) + EPSILON)
        xn[r, :] = (h * inv * gain[0:1, :]).astype(BF)

    tiles(tokens, 128, norm)
    for s in range(group):
        rows = dot(select[s], xn[s * width : (s + 1) * width, :]).astype(BF)
        a_rows[s * cap : (s + 1) * cap, :] = rows
    stages[0]()
    kv = dot(a_rows[...], w_hqkv[:, wh:]).astype(BF)
    for s in range(group):
        kvh[s, f] = kv[s * cap : (s + 1) * cap]
    mine = kvh.at[:, f]
    first = send(mine, mine, ss.at[0], sr.at[0], across)
    beside = send(mine, mine, ss.at[1], sr.at[1], partner)
    stages[1]()
    for s in range(group):
        rows = xn[s * width : (s + 1) * width, :]
        rim[s, WIN : WIN + width, :] = dot(rows, w_lqkv[:, wl:]).astype(BF)
    finish = rim_exchange(
        rim.at[:, pl.ds(WIN, WIN)],
        rim.at[:, pl.ds(width, WIN)],
        rim.at[:, pl.ds(0, WIN)],
        rim.at[:, pl.ds(width + WIN, WIN)],
        ls,
        lr,
        rs,
        rr,
    )
    hq[...] = dot(a_rows[...], w_hqkv[:, :wh]).astype(BF)
    for s in range(group):
        rows = slice(s * width, (s + 1) * width)
        lq[rows, :] = dot(xn[rows, :], w_lqkv[:, :wl]).astype(BF)
    stages[2]()
    first.wait()
    other = kvh.at[:, (1 - x_) * 2 + c]
    relay = send(other, other, ss.at[2], sr.at[2], partner)
    finish()
    stages[3]()
    blocks = width // WIN

    def light(i, carry):
        s, b = i // blocks, i % blocks
        r = pl.ds(pl.multiple_of(i * WIN, WIN), WIN)
        keys = pl.ds(pl.multiple_of(b * WIN, WIN), 3 * WIN)
        bias = reach_bias(key_bias[i])
        lse = jnp.zeros((WIN, 128), F32)
        for pair in range(HL // 2):
            at_k = slice(pair * 128, (pair + 1) * 128)
            at_v = slice(wl + pair * 128, wl + (pair + 1) * 128)
            o, column = pair_forward(
                lq[r, at_k], rim[s, keys, at_k], rim[s, keys, at_v], bias, ones, scaled
            )
            lo_out[r, at_k] = o
            lse = put_lse(lse, pair, column)
        l_lse[r, :] = lse
        return carry

    lax.fori_loop(0, group * blocks // 2, light, 0)
    stages[4]()
    lax.fori_loop(group * blocks // 2, group * blocks, light, 0)
    stages[5]()
    beside.wait()
    relay.wait()
    heavy_kv = kvh.reshape(group, 4 * cap, 2 * wh)

    def heavy(s, carry):
        r = pl.ds(pl.multiple_of(s * cap, cap), cap)
        bias = heavy_bias[s]
        bias = jnp.concatenate([bias, bias], axis=0)
        lse = jnp.zeros((cap, 128), F32)
        for pair in range(HH // 2):
            at_k = slice(pair * 128, (pair + 1) * 128)
            at_v = slice(wh + pair * 128, wh + (pair + 1) * 128)
            o, column = pair_forward(
                hq[r, at_k], heavy_kv[s, :, at_k], heavy_kv[s, :, at_v], bias, ones, scaled
            )
            ho[r, at_k] = o
            lse = put_lse(lse, pair, column)
        h_lse[r, :] = lse
        return carry

    lax.fori_loop(0, group, heavy, 0)
    stages[6]()
    high, low = halves(dot(ho[...], w_hout[...]))
    for s in range(group):
        r = slice(s * width, (s + 1) * width)
        q = slice(s * cap, (s + 1) * cap)
        hidden[r, :] = (
            x[r, :].astype(F32)
            + dot(lo_out[r, :], w_lout[...])
            + (dot(select_t[s], high[q]) + dot(select_t[s], low[q]))
        )


def attend_kernel(*refs):
    meet(line_peers())
    attend_body([lambda: None] * 7, *refs)


def attend_shapes(tokens, select):
    group, cap, width = select.shape
    wl, wh = HL * DH, HH * DH
    rows = group * cap
    return [
        jax.ShapeDtypeStruct((tokens, D), F32),
        jax.ShapeDtypeStruct((tokens, D), BF),
        jax.ShapeDtypeStruct((tokens, wl), BF),
        jax.ShapeDtypeStruct((group, width + 2 * WIN, 2 * wl), BF),
        jax.ShapeDtypeStruct((tokens, wl), BF),
        jax.ShapeDtypeStruct((tokens, 128), F32),
        jax.ShapeDtypeStruct((rows, D), BF),
        jax.ShapeDtypeStruct((rows, wh), BF),
        jax.ShapeDtypeStruct((group, 4, cap, 2 * wh), BF),
        jax.ShapeDtypeStruct((rows, wh), BF),
        jax.ShapeDtypeStruct((rows, 128), F32),
    ]


ATTEND_SEMS = [DMA, DMA, DMA, DMA, DMA((3,)), DMA((3,))]


def attend(x, gain, select, select_t, key_bias, heavy_bias, w_lqkv, w_hqkv, w_lout, w_hout):
    operands = [x, gain, select, select_t, key_bias, heavy_bias, w_lqkv, w_hqkv, w_lout, w_hout]
    shapes = attend_shapes(x.shape[0], select)
    return call(
        attend_kernel,
        shapes,
        operands,
        [VM] * len(operands),
        [VM] * len(shapes),
        ATTEND_SEMS,
        2,
    )


def route_part(deal, lengths, routes_a, routes_f, scores, tables):
    sel_a, selt_a, key_bias, heavy_bias, sel_f, selt_f, score, mask, scale = tables
    hi, lo, x, c = place()
    group, cap, width = sel_a.shape
    seqs = deal.shape[1]
    here = ((x * 2 + c) * width).astype(F32)

    def line(shape, dim):
        return lax.broadcasted_iota(jnp.int32, shape, dim).astype(F32)

    lane = lax.broadcasted_iota(jnp.int32, (1, seqs), 1)
    before = jnp.where(line((width, width), 0) > line((width, width), 1), 1.0, 0.0).astype(BF)
    length_row = lengths[...].astype(F32)
    count = jnp.sum(length_row, axis=1, keepdims=True)
    column = line((width, 1), 0)
    row = line((1, width), 1)
    ones = jnp.ones((8, routes_a.shape[1]), BF)

    def columns_of(routes, base):
        held = jnp.where(routes == column + base, 1.0, 0.0)
        rank = jnp.sum(dot(before, held.astype(BF)), axis=1, keepdims=True)
        there = jnp.sum(held, axis=1, keepdims=True)
        hot_t = jnp.where(rank == line((width, cap), 1), 1.0, 0.0) * there
        return held, rank, hot_t

    def rows_of(held):
        there = dot_back(ones, held.astype(BF))
        rank = dot_back(there.astype(BF), before)
        return jnp.where(rank[:1] == line((cap, width), 0), 1.0, 0.0) * there[:1]

    for s in range(group):
        place_here = lane == (hi * 2 + lo) * group + s
        which = jnp.sum(jnp.where(place_here, deal[...].astype(F32), 0.0), axis=1, keepdims=True)
        one = line((seqs, 1), 0) == which
        length = jnp.sum(
            jnp.where(line((1, seqs), 1) == which, length_row, 0.0), axis=1, keepdims=True
        )
        ra, rf, sf = (
            jnp.sum(jnp.where(one, ref[...].astype(F32), 0.0), axis=0, keepdims=True)
            for ref in (routes_a, routes_f, scores)
        )
        held, rank, hot_t = columns_of(ra, here)
        hot = rows_of(held)
        sel_a[s] = hot.astype(BF)
        selt_a[s] = hot_t.astype(BF)
        own_spot = jnp.sum(hot * (row + here + 1.0), axis=1, keepdims=True) - 1.0
        for q in range(4):
            base = float(q * width)
            _, _, other_t = columns_of(ra, base)
            spot = jnp.sum(other_t * (column + base + 1.0), axis=0, keepdims=True) - 1.0
            live = jnp.where((spot >= 0.0) & (spot < length), 1.0, 0.0)
            same = jnp.where(own_spot == spot, 1.0, 0.0)
            heavy_bias[s, :, q * cap : (q + 1) * cap] = jnp.where(live + same > 0.0, 0.0, MASKED)
        for b in range(width // WIN):
            key = line((1, 3 * WIN), 1) + (here + float((b - 1) * WIN))
            live = (key >= 0.0) & (key < length)
            key_bias[s * (width // WIN) + b] = jnp.where(live, 0.0, MASKED)
        valid = jnp.where(column + here < length, 1.0, 0.0)
        mask[s * width : (s + 1) * width, :] = valid
        scale[s * width : (s + 1) * width, :] = 2.0 * valid / (D * count)
        held, rank, hot_t = columns_of(rf, here)
        sel_f[s] = rows_of(held).astype(BF)
        selt_f[s] = hot_t.astype(BF)
        slot = jnp.sum(held * rank, axis=0, keepdims=True)
        owned = jnp.sum(held, axis=0, keepdims=True)
        hits = jnp.where(slot == line((cap, slot.shape[1]), 0), 1.0, 0.0)
        score[s * cap : (s + 1) * cap, :] = jnp.sum(hits * (owned * sf), axis=1, keepdims=True)


def route_shapes(group, width, tokens):
    return [
        jax.ShapeDtypeStruct((group, CAP, width), BF),
        jax.ShapeDtypeStruct((group, width, CAP), BF),
        jax.ShapeDtypeStruct((tokens // WIN, 1, 3 * WIN), F32),
        jax.ShapeDtypeStruct((group, CAP, 4 * CAP), F32),
        jax.ShapeDtypeStruct((group, CAP, width), BF),
        jax.ShapeDtypeStruct((group, width, CAP), BF),
        jax.ShapeDtypeStruct((group * CAP, 1), F32),
        jax.ShapeDtypeStruct((tokens, 1), F32),
        jax.ShapeDtypeStruct((tokens, 1), F32),
    ]


def gather_attend_kernel(dp, nw, *refs):
    n_in, n_out = 7 + nw, 2 + nw + 21
    ins, outs, rest = refs[:n_in], list(refs[n_in : n_in + n_out]), refs[n_in + n_out :]
    count = len(STAGED)
    held, flush_sem, rest = rest[:count], rest[count], rest[count + 1 :]
    final = [outs[k] for k in STAGED]
    for k, ref in zip(STAGED, held):
        outs[k] = ref
    flushed = []

    def flush(*which):
        for k in which:
            n = STAGED.index(k)
            flushed.append(keep(held[n], final[n], flush_sem.at[n]))

    xin, ws, hin = ins[0], ins[1 : 1 + nw], ins[1 + nw]
    integers = ins[2 + nw :]
    xo, wos, hin_o = outs[0], outs[1 : 1 + nw], outs[1 + nw]
    gain, tables, saved = outs[2 + nw], outs[3 + nw : 12 + nw], outs[12 + nw :]
    parts, rest = rest[: 3 * nw + 3], rest[3 * nw + 3 :]
    halves = (parts[:nw], parts[nw : 2 * nw], parts[2 * nw : 3 * nw], parts[3 * nw :])
    g = Gather(dp, xin, ws, hin, xo, wos, hin_o, rest[:11], halves)
    g.meet()
    for w in range(nw):
        g.swap(w)
    g.join(0)
    g.join(2)
    g.plane(0)
    g.plane(2)
    g.join(1)
    g.rows()
    route_part(*integers, tables)
    g.cross(0)
    g.cross(2)
    g.core(0)
    g.plane(1)
    g.core(2)
    g.ready(0)
    total = jnp.zeros(gain.shape, F32)
    for z in range(dp // 2):
        for l2, x2 in ((0, 0), (0, 1), (1, 0), (1, 1)):
            pair = wos[0][z, l2, x2].astype(F32)
            total += pair[:8] + pair[8:]
    gain[...] = total
    g.rows_ready()
    for w in (4, 3, 5, 6):
        g.join(w)
    g.heavy_plane()
    flush(0)

    def heavy_projection():
        g.cross(1)
        g.ready(2)
        flush(20, 3)

    def light_projection():
        g.core(1)
        g.ready(1)
        flush(2)

    def keys_travel():
        g.plane(4)
        g.plane(3)
        g.heavy_line()
        flush(21)

    def keys_there():
        g.plane(5)
        g.plane(6)
        flush(22)

    def half_way():
        g.cross(4)
        g.cross(3)

    def light_done():
        g.core(4)
        g.core(3)
        g.cross(5)
        g.cross(6)
        flush(23)

    def heavy_done():
        g.ready(4)
        g.ready(3)
        flush(27, 4, 5)

    full = [wos[w].reshape(-1, wos[w].shape[-1]) for w in range(nw)]
    stages = [
        heavy_projection,
        light_projection,
        keys_travel,
        keys_there,
        half_way,
        light_done,
        heavy_done,
    ]
    attend_body(
        stages,
        xo.reshape(-1, D),
        gain,
        *tables[:4],
        full[1],
        full[2],
        full[3],
        full[4],
        *saved,
        *rest[11:],
    )
    g.core(5)
    g.core(6)
    g.ready(5)
    g.ready(6)
    g.heavy_ready()
    for copy in flushed:
        copy.wait()


STAGED = (0, 2, 3, 4, 5, 20, 21, 22, 23, 27)


def gather_attend(dp, xin, weights, hin, integers):
    nw = len(weights)
    shapes = gather_shapes(dp, xin, weights, hin, True)
    group, width = shapes[0].shape[0], dp * xin.shape[1]
    tables = route_shapes(group, width, group * width)
    shapes.append(jax.ShapeDtypeStruct((8, D), F32))
    shapes += tables
    shapes += attend_shapes(group * width, tables[0])
    return call(
        functools.partial(gather_attend_kernel, dp, nw),
        shapes,
        [xin, *weights, hin, *integers],
        [ANY] * (2 + nw) + [VM] * 5,
        [ANY if k in STAGED + (6, 7, 8) else VM for k in range(len(shapes))],
        [pltpu.VMEM(shapes[k].shape, BF) for k in STAGED]
        + [DMA((len(STAGED),))]
        + [pltpu.VMEM((w.shape[0], w.shape[1] // 2), BF) for w in weights] * 2
        + [pltpu.VMEM((2 * w.shape[0], w.shape[1] // 2), BF) for w in weights]
        + [DMA((nw,))] * 3
        + gather_sems(dp, nw)
        + ATTEND_SEMS,
        1,
    )


def attend_back_body(
    stages,
    d_hidden,
    x,
    gain,
    select,
    select_t,
    key_bias,
    heavy_bias,
    w_lqkv,
    w_hqkv,
    w_lout,
    w_hout,
    xn,
    lq,
    rim,
    lo_out,
    l_lse,
    a_rows,
    hq,
    kvh,
    ho,
    h_lse,
    g_lqkv,
    g_hqkv,
    g_lout,
    g_hout,
    dx,
    stats,
    d_ho,
    d_hproj,
    part,
    got,
    far,
    d_la,
    d_lo,
    d_rim,
    edge,
    edge_in,
    d_lproj,
    ls,
    lr,
    rs,
    rr,
    ss,
    sr,
):
    hi, lo, x_, c = place()
    tokens = x.shape[0]
    group, cap, width = select.shape
    wl, wh = HL * DH, HH * DH
    ones, scaled = pair_masks(1.0), pair_masks(SCORE_SCALE)
    across, partner = at(hi, lo, 1 - x_, c), at(hi, lo, x_, 1 - c)
    picked = []
    for s in range(group):
        high, low = halves(d_hidden[s * width : (s + 1) * width, :])
        picked.append((dot(select[s], high) + dot(select[s], low)).astype(BF))
    d_ha = jnp.concatenate(picked, axis=0)
    d_ho[...] = dot_back(d_ha, w_hout[...]).astype(BF)
    heavy_kv = kvh.reshape(group, 4 * cap, 2 * wh)
    part_kv = part.reshape(group, 4 * cap, 2 * wh)

    def heavy(s, carry):
        r = pl.ds(pl.multiple_of(s * cap, cap), cap)
        bias = heavy_bias[s]
        bias = jnp.concatenate([bias, bias], axis=0)
        lse = h_lse[r, :]
        for pair in range(HH // 2):
            at_k = slice(pair * 128, (pair + 1) * 128)
            at_v = slice(wh + pair * 128, wh + (pair + 1) * 128)
            dq, dk, dv = pair_backward(
                hq[r, at_k],
                heavy_kv[s, :, at_k],
                heavy_kv[s, :, at_v],
                bias,
                get_lse(lse, pair),
                d_ho[r, at_k],
                ones,
                scaled,
            )
            d_hproj[r, at_k] = dq.astype(BF)
            part_kv[s, :, at_k] = dk.astype(BF)
            part_kv[s, :, at_v] = dv.astype(BF)
        return carry

    lax.fori_loop(0, group, heavy, 0)
    beside = [
        send(part.at[:, b * 2 + 1 - c], got.at[b], ss.at[b], sr.at[b], partner) for b in (0, 1)
    ]
    g_hout[...] = dot_grad(ho[...], d_ha).astype(BF)
    stages[0]()

    def light_out_back(r):
        d = d_hidden[r, :].astype(BF)
        d_la[r, :] = d
        d_lo[r, :] = dot_back(d, w_lout[...]).astype(BF)

    tiles(tokens, 256, light_out_back)
    g_lout[...] = dot_grad(lo_out[...], d_la[...]).astype(BF)
    stages[1]()
    for copy in beside:
        copy.wait()
    for b in (0, 1):
        got[b] = (got[b].astype(F32) + part[:, b * 2 + c].astype(F32)).astype(BF)
    third = send(got.at[1 - x_], far, ss.at[2], sr.at[2], across)
    stages[2]()
    d_rim[...] = jnp.zeros(d_rim.shape, F32)
    blocks = width // WIN

    def light(i, carry):
        s, b = i // blocks, i % blocks
        r = pl.ds(pl.multiple_of(i * WIN, WIN), WIN)
        keys = pl.ds(pl.multiple_of(b * WIN, WIN), 3 * WIN)
        bias = reach_bias(key_bias[i])
        lse = l_lse[r, :]
        for pair in range(HL // 2):
            at_k = slice(pair * 128, (pair + 1) * 128)
            at_v = slice(wl + pair * 128, wl + (pair + 1) * 128)
            dq, dk, dv = pair_backward(
                lq[r, at_k],
                rim[s, keys, at_k],
                rim[s, keys, at_v],
                bias,
                get_lse(lse, pair),
                d_lo[r, at_k],
                ones,
                scaled,
            )
            d_lproj[r, at_k] = dq.astype(BF)
            d_rim[s, keys, at_k] += dk
            d_rim[s, keys, at_v] += dv
        return carry

    lax.fori_loop(0, group * blocks // 2, light, 0)
    third.wait()
    total = (got[x_].astype(F32) + far[...].astype(F32)).astype(BF)
    for s in range(group):
        d_hproj[s * cap : (s + 1) * cap, wh:] = total[s]

    def heavy_grad(j):
        g_hqkv[:, j] = dot_grad(a_rows[...], d_hproj[:, j]).astype(BF)

    tiles(3 * wh, 768, heavy_grad)
    stages[3]()
    lax.fori_loop(group * blocks // 2, group * blocks, light, 0)
    edge[0] = d_rim[:, :WIN, :].astype(BF)
    edge[1] = d_rim[:, WIN + width :, :].astype(BF)
    finish = rim_exchange(
        edge.at[0], edge.at[1], edge_in.at[0], edge_in.at[1], ls, lr, rs, rr
    )
    stages[4]()
    d_high, d_low = halves(dot_back(d_hproj[...], w_hqkv[...]))
    finish()
    for s in range(group):
        d_rim[s, WIN : 2 * WIN, :] += edge_in[0, s].astype(F32)
        d_rim[s, width : width + WIN, :] += edge_in[1, s].astype(F32)
        d_lproj[s * width : (s + 1) * width, wl:] = d_rim[s, WIN : WIN + width, :].astype(BF)

    def light_grad(j):
        g_lqkv[:, j] = dot_grad(xn[...], d_lproj[:, j]).astype(BF)

    tiles(3 * wl, 768, light_grad)
    stages[5]()
    stats[...] = jnp.zeros(stats.shape, F32)
    for s in range(group):
        r = slice(s * width, (s + 1) * width)
        q = slice(s * cap, (s + 1) * cap)
        d = dot_back(d_lproj[r, :], w_lqkv[...]) + (
            dot(select_t[s], d_high[q]) + dot(select_t[s], d_low[q])
        )
        h = x[r, :].astype(F32)
        inv = lax.rsqrt(jnp.mean(h * h, axis=-1, keepdims=True) + EPSILON)
        dh = d * h
        stats[0:1, :] += jnp.sum(dh * inv, axis=0, keepdims=True)
        mean = jnp.mean(gain[0:1, :] * dh, axis=-1, keepdims=True)
        dx[r, :] = (
            d_hidden[r, :] + inv * gain[0:1, :] * d - h * (inv * inv * inv * mean)
        ).astype(BF)
    stages[6]()


def attend_back_kernel(*refs):
    meet(line_peers())
    attend_back_body([lambda: None] * 7, *refs)


def attend_back_scratch(tokens, select):
    group, cap, width = select.shape
    wl, wh = HL * DH, HH * DH
    rows = group * cap
    return [
        pltpu.VMEM((rows, wh), BF),
        pltpu.VMEM((rows, 3 * wh), BF),
        pltpu.VMEM((group, 4, cap, 2 * wh), BF),
        pltpu.VMEM((2, group, cap, 2 * wh), BF),
        pltpu.VMEM((group, cap, 2 * wh), BF),
        pltpu.VMEM((tokens, D), BF),
        pltpu.VMEM((tokens, wl), BF),
        pltpu.VMEM((group, width + 2 * WIN, 2 * wl), F32),
        pltpu.VMEM((2, group, WIN, 2 * wl), BF),
        pltpu.VMEM((2, group, WIN, 2 * wl), BF),
        pltpu.VMEM((tokens, 3 * wl), BF),
    ] + ATTEND_SEMS


def attend_back(d_hidden, x, gain, select, select_t, key_bias, heavy_bias, weights, saved):
    tokens = x.shape[0]
    wl, wh = HL * DH, HH * DH
    operands = [d_hidden, x, gain, select, select_t, key_bias, heavy_bias, *weights, *saved]
    shapes = [
        jax.ShapeDtypeStruct((D, 3 * wl), BF),
        jax.ShapeDtypeStruct((D, 3 * wh), BF),
        jax.ShapeDtypeStruct((wl, D), BF),
        jax.ShapeDtypeStruct((wh, D), BF),
        jax.ShapeDtypeStruct((tokens, D), BF),
        jax.ShapeDtypeStruct((8, D), F32),
    ]
    return call(
        attend_back_kernel,
        shapes,
        operands,
        [VM] * len(operands),
        [VM] * len(shapes),
        attend_back_scratch(tokens, select),
        3,
    )


def scatter_kernel(dp, nw, *refs):
    nz = dp // 2
    dx, stats, gs, hin = refs[0], refs[1], refs[2 : 2 + nw], refs[2 + nw]
    outs = refs[3 + nw :]
    dxo, total, gos, hin_o = outs[0], outs[1], outs[2 : 2 + nw], outs[2 + nw]
    scr = outs[3 + nw :]
    nears, fars, sums, ends = (scr[i * nw : (i + 1) * nw] for i in range(4))
    hin_r, hin_s, sc, sp, sz, acc, acc2 = scr[4 * nw : 4 * nw + 7]
    own, xs, xr, cs, cr, ps, pr, zs, zr, hs, hr, ts, tr = scr[4 * nw + 7 :]
    hi, lo, x, c = place()
    d = hi * 2 + lo
    f = x * 2 + c
    plane = (lo * 2 + x) * 2 + c
    dp_peers = [(lax.rem(d + k, dp), f) for k in range(1, dp)]
    rest = [(a, b, e) for a in (0, 1) for b in (0, 1) for e in (0, 1) if a or b or e]
    flat8 = []
    for a, b, e in rest:
        l2 = 1 - lo if a else lo
        x2 = 1 - x if b else x
        c2 = 1 - c if e else c
        flat8.append((l2, x2, c2))
    meet(dp_peers + [at(hi, *p) for (a, b, e), p in zip(rest, flat8) if b or e])
    partner = at(hi, lo, x, 1 - c)
    quad = quad_peers()
    z_index = [lax.rem(hi + k, nz) for k in range(1, nz)]
    z_peers = [at(z, lo, x, c) for z in z_index]
    c_sends = [
        send(gs[w].at[:, :, :, 1 - c], nears[w], cs.at[w], cr.at[w], partner) for w in range(nw)
    ]
    t_c = send(stats, sc, ts.at[0], tr.at[0], partner)
    mine = keep(dx.at[:, d], dxo.at[d], own)
    x_sends = [
        send(dx.at[:, peer[0]], dxo.at[d], xs.at[k], xr.at[k], peer)
        for k, peer in enumerate(dp_peers)
    ]
    h_sends = []
    for k, z in enumerate(z_index):
        h_sends.append(send(hin.at[z], hin_r.at[k], hs.at[1, k], hr.at[1, k], z_peers[k]))
    p_sends, z_sends = [], []
    t_c.wait()
    acc[...] = stats[...] + sc[...]
    t_p = [
        send(acc, sp.at[k], ts.at[1 + k], tr.at[1 + k], at(hi, l2, x2, c))
        for k, (l2, x2) in enumerate(quad)
    ]

    def add_core(w):
        c_sends[w].wait()
        near, g = nears[w], gs[w]

        def body(i, carry):
            z, a, b = i // 4, (i // 2) % 2, i % 2
            near[z, a, b] = (near[z, a, b].astype(F32) + g[z, a, b, c].astype(F32)).astype(BF)
            return carry

        lax.fori_loop(0, nz * 4, body, 0)
        p_sends.append(
            [
                send(near.at[:, l2, x2], fars[w].at[k], ps.at[w, k], pr.at[w, k], at(hi, l2, x2, c))
                for k, (l2, x2) in enumerate(quad)
            ]
        )

    def add_plane(w):
        for copy in p_sends[w]:
            copy.wait()
        near, far, part = nears[w], fars[w], sums[w]

        def body(z, carry):
            part[z] = (
                near[z, lo, x].astype(F32)
                + far[0, z].astype(F32)
                + far[1, z].astype(F32)
                + far[2, z].astype(F32)
            ).astype(BF)
            return carry

        lax.fori_loop(0, nz, body, 0)
        z_sends.append(
            [
                send(part.at[z], ends[w].at[k], zs.at[w, k], zr.at[w, k], z_peers[k])
                for k, z in enumerate(z_index)
            ]
        )

    def add_line(w):
        for copy in z_sends[w]:
            copy.wait()
        gos[w][...] = sums[w][hi].astype(F32)
        for k in range(nz - 1):
            gos[w][...] += ends[w][k].astype(F32)

    for w in range(nw):
        add_core(w)
        if w >= 2:
            add_plane(w - 2)
    for copy in t_p:
        copy.wait()
    acc2[...] = acc[...] + sp[0] + sp[1] + sp[2]
    t_z = [send(acc2, sz.at[k], ts.at[4 + k], tr.at[4 + k], z_peers[k]) for k in range(nz - 1)]
    for copy in h_sends:
        copy.wait()

    def body(i, carry):
        value = hin[hi, i].astype(F32)
        for k in range(nz - 1):
            value += hin_r[k, i].astype(F32)
        hin_s[i] = value.astype(BF)
        return carry

    lax.fori_loop(0, 8, body, 0)
    hin_o[plane] = hin_s[plane]
    a_sends = [
        send(
            hin_s.at[(l2 * 2 + x2) * 2 + c2],
            hin_o.at[plane],
            hs.at[0, k],
            hr.at[0, k],
            at(hi, l2, x2, c2),
        )
        for k, (l2, x2, c2) in enumerate(flat8)
    ]
    for w in range(max(nw - 2, 0), nw):
        add_plane(w)
    for copy in t_z:
        copy.wait()
    total[...] = acc2[...]
    for k in range(nz - 1):
        total[...] += sz[k]
    for w in range(nw):
        add_line(w)
    mine.wait()
    for copy in x_sends + a_sends:
        copy.wait()


def scatter_all(dp, dx, stats, grads, hin):
    nz = dp // 2
    nw = len(grads)
    group, _, rows, _ = dx.shape
    tiles = [g.shape[4:] for g in grads]
    most = max(7, nz)
    scratch = [pltpu.VMEM((nz, 2, 2) + t, BF) for t in tiles]
    scratch += [pltpu.VMEM((3, nz) + t, BF) for t in tiles]
    scratch += [pltpu.VMEM((nz,) + t, BF) for t in tiles]
    scratch += [pltpu.VMEM((nz - 1,) + t, BF) for t in tiles]
    scratch += [
        pltpu.VMEM((nz - 1,) + hin.shape[1:], BF),
        pltpu.VMEM(hin.shape[1:], BF),
        pltpu.VMEM(stats.shape, F32),
        pltpu.VMEM((3,) + stats.shape, F32),
        pltpu.VMEM((nz - 1,) + stats.shape, F32),
        pltpu.VMEM(stats.shape, F32),
        pltpu.VMEM(stats.shape, F32),
        DMA,
        DMA((dp,)),
        DMA((dp,)),
        DMA((nw,)),
        DMA((nw,)),
        DMA((nw, 3)),
        DMA((nw, 3)),
        DMA((nw, nz)),
        DMA((nw, nz)),
        DMA((3, most)),
        DMA((3, most)),
        DMA((4 + nz,)),
        DMA((4 + nz,)),
    ]
    shapes = [jax.ShapeDtypeStruct((dp, group, rows, D), BF), jax.ShapeDtypeStruct(stats.shape, F32)]
    shapes += [jax.ShapeDtypeStruct(t, F32) for t in tiles]
    shapes.append(jax.ShapeDtypeStruct(hin.shape[1:], BF))
    return call(
        functools.partial(scatter_kernel, dp, nw),
        shapes,
        [dx, stats, *grads, hin],
        [ANY] + [VM] * (2 + nw),
        [ANY] + [VM] * (2 + nw),
        scratch,
        4,
    )


class Scatter:
    def __init__(self, nz, shards, gs, near, one, two, end, sems):
        self.nz, self.shards, self.gs = nz, shards, gs
        self.near, self.one, self.two, self.end = near, one, two, end
        self.cs, self.cr, self.ps, self.pr, self.zs, self.zr = sems
        self.hi, self.lo, self.x, self.c = hi, lo, x, c = place()
        self.partner = at(hi, lo, x, 1 - c)
        self.by_x, self.by_y = at(hi, lo, 1 - x, c), at(hi, 1 - lo, x, c)
        self.z_index = [lax.rem(hi + k, nz) for k in range(1, nz)]
        self.copies = {}

    def lanes(self, w, c):
        half = self.shards[w][1] // 2
        return pl.ds(pl.multiple_of(c * half, 128), half)

    def core(self, w):
        out = self.gs[w].at[:, :, :, :, self.lanes(w, 1 - self.c)]
        self.copies[w, 0] = [send(out, self.near[w], self.cs.at[w], self.cr.at[w], self.partner)]

    def wait(self, w, stage):
        for copy in self.copies[w, stage]:
            copy.wait()

    def plane(self, w):
        g, own = self.gs[w], self.lanes(w, self.c)
        self.add_plane(w, lambda z, a, b: g[z, a, b, :, own])

    def add_plane(self, w, own):
        self.wait(w, 0)
        near = self.near[w]
        lo, x, half = self.lo, self.x, self.nz // 2

        def body(i, carry):
            z, a, b = i // 4, (i // 2) % 2, i % 2
            near[z, a, b] = (near[z, a, b].astype(F32) + own(z, a, b).astype(F32)).astype(BF)
            return carry

        lax.fori_loop(0, self.nz * 4, body, 0)
        low, high = pl.ds(0, half), pl.ds(half, self.nz - half)
        self.copies[w, 1] = [
            send(near.at[low, :, 1 - x], self.one[w].at[low], self.ps.at[w, 0], self.pr.at[w, 0], self.by_x),
            send(near.at[high, 1 - lo], self.one[w].at[high], self.ps.at[w, 1], self.pr.at[w, 1], self.by_y),
        ]

    def begin(self, w, source, sem):
        near, lo, x, half = self.near[w], self.lo, self.x, self.nz // 2
        low, high = pl.ds(0, half), pl.ds(half, self.nz - half)
        self.copies[w, 1] = [
            keep(source, near, sem),
            send(source.at[low, :, 1 - x], self.one[w].at[low], self.ps.at[w, 0], self.pr.at[w, 0], self.by_x),
            send(source.at[high, 1 - lo], self.one[w].at[high], self.ps.at[w, 1], self.pr.at[w, 1], self.by_y),
        ]

    def cross(self, w):
        self.wait(w, 1)
        near, one, lo, x, half = self.near[w], self.one[w], self.lo, self.x, self.nz // 2

        def low_body(i, carry):
            z, a = i // 2, i % 2
            near[z, a, x] = (near[z, a, x].astype(F32) + one[z, a].astype(F32)).astype(BF)
            return carry

        def high_body(i, carry):
            z, b = half + i // 2, i % 2
            near[z, lo, b] = (near[z, lo, b].astype(F32) + one[z, b].astype(F32)).astype(BF)
            return carry

        lax.fori_loop(0, half * 2, low_body, 0)
        lax.fori_loop(0, (self.nz - half) * 2, high_body, 0)
        low, high = pl.ds(0, half), pl.ds(half, self.nz - half)
        two = self.two[w]
        self.copies[w, 2] = [
            send(near.at[low, 1 - lo, x], two.at[low], self.ps.at[w, 2], self.pr.at[w, 2], self.by_y),
            send(near.at[high, lo, 1 - x], two.at[high], self.ps.at[w, 3], self.pr.at[w, 3], self.by_x),
        ]

    def line(self, w):
        self.wait(w, 2)
        near, part, lo, x = self.near[w], self.two[w], self.lo, self.x

        def body(z, carry):
            part[z] = (near[z, lo, x].astype(F32) + part[z].astype(F32)).astype(BF)
            return carry

        lax.fori_loop(0, self.nz, body, 0)
        self.copies[w, 3] = [
            send(
                part.at[z],
                self.end[w].at[k],
                self.zs.at[w, k],
                self.zr.at[w, k],
                at(z, lo, x, self.c),
            )
            for k, z in enumerate(self.z_index)
        ]

    def last(self, w, fin, out, sems):
        self.wait(w, 3)
        value = self.two[w][self.hi].astype(F32)
        for k in range(self.nz - 1):
            value += self.end[w][k].astype(F32)
        fin[...] = value
        count = self.shards[w][0]
        own = pl.ds(pl.multiple_of(self.c * count, 8), count)
        mate = pl.ds(pl.multiple_of((1 - self.c) * count, 8), count)
        spot = out.at[:, self.lanes(w, self.c)]
        return [
            keep(fin.at[own], spot, sems[0].at[w]),
            send(fin.at[mate], spot, sems[1].at[w], sems[2].at[w], self.partner),
        ]


def back_scatter_kernel(dp, shards, *refs):
    nz, nw = dp // 2, len(shards)
    n_ops = 7 + 4 + 10
    ops, (g_lin, g_ldn, hin, ffn_stats) = refs[:n_ops], refs[n_ops : n_ops + 4]
    outs, rest = refs[n_ops + 4 : n_ops + 7 + nw], refs[n_ops + 7 + nw :]
    dxo, total, gos, hin_o = outs[0], outs[1], outs[2 : 2 + nw], outs[2 + nw]
    count = len(FETCHED)
    held, fetch_sem, rest = rest[:count], rest[count], rest[count + 1 :]
    sources, ops = [ops[k] for k in FETCHED], list(ops)
    for k, ref in zip(FETCHED, held):
        ops[k] = ref
    full, rest = rest[:4], rest[4:]
    stats, rest = rest[0], rest[1:]
    back, rest = rest[:17], rest[17:]
    dx = back[5]
    near, one, two, end, fin = (rest[k * nw : (k + 1) * nw] for k in range(5))
    hin_own, hin_r, acc, sc, sp, sz, acc2 = rest[5 * nw : 5 * nw + 7]
    own, xs, xr, cs, cr, ps, pr, zs, zr, hs, hr, ts, tr, *fsem = rest[5 * nw + 7 :]
    hi, lo, x, c = place()
    d = hi * 2 + lo
    plane = (lo * 2 + x) * 2 + c
    others = plane_others()
    rows_to = [(lax.rem(d + k, dp), x * 2 + c) for k in range(1, dp)]
    z_index = [lax.rem(hi + k, nz) for k in range(1, nz)]
    z_to = [at(z, lo, x, c) for z in z_index]
    quad = quad_peers()
    g_views = [None, None]
    for k, w in enumerate((2, 3, 4, 5)):
        rows, columns = shards[w]
        g_views.append(full[k].reshape(nz, 2, 2, 2 * rows, columns))
    t = Scatter(nz, shards, g_views, near, one, two, end, (cs, cr, ps, pr, zs, zr))
    meet(rows_to + [at(hi, *q[:3]) for q in others if q[3]])
    fetched = {
        k: keep(source, ref, fetch_sem.at[n])
        for n, (k, source, ref) in enumerate(zip(FETCHED, sources, held))
    }

    def fetch(*which):
        for k in which:
            fetched[k].wait()

    h_sends = []
    for k, z in enumerate(z_index):
        h_sends.append(send(hin.at[z], hin_r.at[k], hs.at[1, k], hr.at[1, k], z_to[k]))
    t.begin(0, g_lin, own.at[0])
    t.begin(1, g_ldn, own.at[1])
    kept = [keep(hin.at[hi], hin_own, own.at[2])]
    late = []

    def first_plane():
        fetch(9, 14)
        t.core(2)

    def out_core():
        t.core(3)

    def before_light():
        fetch(12, 13)

    def half_way():
        t.core(4)
        t.cross(0)
        t.cross(1)
        t.plane(2)
        t.plane(3)

    def rims_left():
        fetch(8, 11)
        t.plane(4)
        t.line(0)
        t.line(1)
        t.cross(2)
        t.cross(3)

    def light_grad_done():
        t.core(5)
        fetch(7, 1)

    def rows_done():
        rows = dx.reshape(dxo.shape[1], dp, dxo.shape[2], D)
        late.append(keep(rows.at[:, d], dxo.at[d], own.at[4]))
        for k, to in enumerate(rows_to):
            late.append(send(rows.at[:, to[0]], dxo.at[d], xs.at[k], xr.at[k], to))

    stages = [
        first_plane,
        out_core,
        before_light,
        half_way,
        rims_left,
        light_grad_done,
        rows_done,
    ]
    attend_back_body(
        stages, *ops, full[3], full[2], full[1], full[0], dx, stats, *back
    )
    partner = at(hi, lo, x, 1 - c)
    for k in range(6):
        lanes = slice(k * 128, (k + 1) * 128)
        acc[k : k + 1, :] = stats[0:1, lanes]
        acc[6 + k : 7 + k, :] = ffn_stats[0:1, lanes]
    loss = jnp.sum(ffn_stats[1:2, :], axis=-1, keepdims=True)
    acc[12:16, :] = jnp.broadcast_to(loss, (4, 128))
    t_c = send(acc, sc, ts.at[0], tr.at[0], partner)
    t.plane(5)
    t.line(2)
    t.line(3)
    t.cross(4)
    t_c.wait()
    acc2[...] = acc[...] + sc[...]
    t_p = [
        send(acc2, sp.at[k], ts.at[1 + k], tr.at[1 + k], at(hi, l2, x2, c))
        for k, (l2, x2) in enumerate(quad)
    ]
    t.line(4)
    for copy in h_sends + kept:
        copy.wait()

    def body(i, carry):
        value = hin_own[i].astype(F32)
        for k in range(nz - 1):
            value += hin_r[k, i].astype(F32)
        hin_own[i] = value.astype(BF)
        return carry

    lax.fori_loop(0, 8, body, 0)
    hin_o[plane] = hin_own[plane]
    late += [
        send(
            hin_own.at[(q[0] * 2 + q[1]) * 2 + q[2]],
            hin_o.at[plane],
            hs.at[0, k],
            hr.at[0, k],
            at(hi, *q[:3]),
        )
        for k, q in enumerate(others)
    ]
    t.cross(5)
    for copy in t_p:
        copy.wait()
    acc[...] = acc2[...] + sp[0] + sp[1] + sp[2]
    t_z = [send(acc, sz.at[k], ts.at[4 + k], tr.at[4 + k], z_to[k]) for k in range(nz - 1)]
    t.line(5)
    for w in range(nw):
        late += t.last(w, fin[w], gos[w], fsem)
    for copy in t_z:
        copy.wait()
    value = acc[...]
    for k in range(nz - 1):
        value += sz[k]
    total[...] = value
    for copy in late:
        copy.wait()


FETCHED = (9, 14, 12, 13, 8, 11, 7, 1)


def back_scatter(dp, rows, d_hidden, x, gain, masks, weights, saved, ffn_grads, ffn_stats, shards, hin):
    nz, nw = dp // 2, len(shards)
    tokens = x.shape[0]
    group = masks[0].shape[0]
    most = max(7, nz)
    stat_shape = (16, 128)
    operands = [d_hidden, x, gain, *masks, *weights, *saved, *ffn_grads, hin, ffn_stats]
    shapes = [jax.ShapeDtypeStruct((dp, group, rows, D), BF), jax.ShapeDtypeStruct(stat_shape, F32)]
    shapes += [jax.ShapeDtypeStruct(s, F32) for s in shards]
    shapes.append(jax.ShapeDtypeStruct(hin.shape[1:], BF))
    scratch = [pltpu.VMEM(operands[k].shape, operands[k].dtype) for k in FETCHED]
    scratch.append(DMA((len(FETCHED),)))
    scratch += [pltpu.VMEM((s[0] * 8 * nz, s[1]), BF) for s in shards[2:]]
    split = [(2 * s[0], s[1] // 2) for s in shards]
    scratch += [pltpu.VMEM((8, D), F32)]
    scratch += attend_back_scratch(tokens, masks[0])
    scratch += [pltpu.VMEM((nz, 2, 2) + s, BF) for s in split]
    scratch += [pltpu.VMEM((nz, 2) + s, BF) for s in split]
    scratch += [pltpu.VMEM((nz,) + s, BF) for s in split]
    scratch += [pltpu.VMEM((nz - 1,) + s, BF) for s in split]
    scratch += [pltpu.VMEM(s, F32) for s in split]
    scratch += [
        pltpu.VMEM(hin.shape[1:], BF),
        pltpu.VMEM((nz - 1,) + hin.shape[1:], BF),
        pltpu.VMEM(stat_shape, F32),
        pltpu.VMEM(stat_shape, F32),
        pltpu.VMEM((3,) + stat_shape, F32),
        pltpu.VMEM((nz - 1,) + stat_shape, F32),
        pltpu.VMEM(stat_shape, F32),
        DMA((5,)),
        DMA((dp,)),
        DMA((dp,)),
        DMA((nw,)),
        DMA((nw,)),
        DMA((nw, 4)),
        DMA((nw, 4)),
        DMA((nw, nz)),
        DMA((nw, nz)),
        DMA((3, most)),
        DMA((3, most)),
        DMA((4 + nz,)),
        DMA((4 + nz,)),
        DMA((nw,)),
        DMA((nw,)),
        DMA((nw,)),
    ]
    return call(
        functools.partial(back_scatter_kernel, dp, shards),
        shapes,
        operands,
        [ANY if k in FETCHED else VM for k in range(len(operands) - 4)] + [ANY] * 3 + [VM],
        [VM] * len(shapes),
        scratch,
        6,
    )


def routing(routes, pieces, piece_len):
    places = jnp.arange(pieces * piece_len)
    routed = jnp.any(routes[:, None, :] == places[None, :, None], axis=-1)
    routed = routed.reshape(-1, pieces, piece_len)
    before = jnp.arange(piece_len)[:, None] < jnp.arange(piece_len)[None, :]
    rank = jnp.einsum(
        "skp,pq->skq", routed.astype(BF), before.astype(BF), preferred_element_type=F32
    )
    slots = jnp.arange(CAP, dtype=F32)
    hot = routed[:, :, None, :] & (rank[:, :, None, :] == slots[None, None, :, None])
    filled = jnp.any(hot, axis=-1)
    spots = jnp.sum(jnp.where(hot, places.reshape(1, pieces, 1, piece_len), 0), axis=-1)
    return hot, jnp.where(filled, spots, -1)


def local(
    layer_input,
    teacher,
    lengths,
    dealing,
    attn_routes,
    ffn_routes,
    ffn_scores,
    gain_attn,
    gain_ffn,
    light_qkv,
    light_out,
    heavy_qkv,
    heavy_out,
    light_in,
    light_down,
    heavy_in,
    heavy_down,
):
    dp = lax.axis_size("dp")
    pieces = lax.axis_size("fsdp")
    data_index = lax.axis_index("dp")
    piece = lax.axis_index("fsdp")
    nz = dp // 2
    n = dp * pieces
    seqs = dealing.shape[0]
    group = seqs // dp
    gain_len = gain_attn.shape[0]
    hidden_units = heavy_in.shape[1] // 2 // n
    mine = data_index * pieces + piece
    tokens = layer_input.shape[2] * dp
    matrices = (light_qkv, heavy_qkv, light_out, heavy_out, light_in, light_down)
    hin_rows = heavy_in.shape[0]
    token_count = jnp.sum(lengths).astype(F32)
    merged = (
        layer_input.shape[2] % 16 == 0
        and hidden_units % 128 == 0
        and all(m.shape[0] % 8 == 0 and m.shape[1] % 256 == 0 for m in (*matrices, heavy_down))
    )
    if merged:
        xin, hin_src, gains = prepare(dealing, layer_input[:, 0], heavy_in, gain_attn, gain_ffn)
        integers = (dealing.reshape(1, -1), lengths.reshape(1, -1), attn_routes, ffn_routes, ffn_scores)
        got = gather_attend(dp, xin, [gains, *matrices], hin_src, integers)
    else:
        xin = deal_rows(dealing, layer_input[:, 0])
        owned = jnp.arange(D)[None, :] // gain_len == mine
        spread_out = jnp.broadcast_to(
            jnp.stack([gain_attn, gain_ffn])[:, None, :], (2, D // gain_len, gain_len)
        ).reshape(2, D)
        gains = jnp.pad(jnp.where(owned, spread_out, 0.0).astype(BF), ((0, 6), (0, 0)))
        hin_src = (
            heavy_in.reshape(hin_rows, 2, nz, 8, hidden_units)
            .transpose(3, 0, 1, 2, 4)
            .reshape(8, hin_rows, 2 * nz * hidden_units)
        )
        if hin_rows % 8:
            hin_src = hin_src.reshape(8, -1, 128)
        got = gather_all(dp, xin, [gains] + [packed(m) for m in matrices], hin_src)
    flat_x = got[0].reshape(-1, D)
    w_lqkv, w_hqkv, w_lout, w_hout, w_lin, w_ldown = (
        unpacked(full, *m.shape) for full, m in zip(got[2:8], matrices)
    )
    w_hin = unpacked(got[8], hin_rows, 2 * nz * hidden_units)
    attn_weights = (w_lqkv, w_hqkv, w_lout, w_hout)
    if merged:
        gain, tables, (hidden, *saved) = got[9], got[10:19], got[19:]
        masks, ffn_masks = tables[:4], tables[4:]
    else:
        gain = jnp.sum(got[1].reshape(n, 8, D).astype(F32), axis=0)
        masks, ffn_masks = integer_tables(
            dealing, lengths, attn_routes, ffn_routes, ffn_scores, group, pieces, tokens
        )
        hidden, *saved = attend(flat_x, gain, *masks, *attn_weights)
    f_select, f_select_t, slot_score, weight_mask, weight_scale = ffn_masks
    grad_lin, grad_ldown, grad_hin, g_hdown, d_hidden, ffn_stats = feed_forward(
        nz,
        merged,
        hidden,
        f_select,
        f_select_t,
        slot_score,
        gain,
        teacher.reshape(-1, D),
        weight_mask,
        weight_scale,
        w_lin,
        w_ldown,
        w_hin,
        heavy_down,
    )
    rows = tokens // dp
    shards = (light_in, light_down, heavy_out, light_out, heavy_qkv, light_qkv)
    hin_part = grad_hin.reshape((nz, 8) + hin_src.shape[1:])
    if merged:
        done = back_scatter(
            dp,
            rows,
            d_hidden,
            flat_x,
            gain,
            masks,
            attn_weights,
            saved,
            (grad_lin, grad_ldown),
            ffn_stats,
            tuple(shard.shape for shard in shards),
            hin_part,
        )
    else:
        grad_lqkv, grad_hqkv, grad_lout, grad_hout, d_inputs, attn_stats = attend_back(
            d_hidden, flat_x, gain, *masks, attn_weights, saved
        )
        stats = jnp.concatenate(
            [
                attn_stats[0].reshape(-1, 128),
                ffn_stats[0].reshape(-1, 128),
                jnp.broadcast_to(jnp.sum(ffn_stats[1]), (4, 128)),
            ]
        )
        grads = (grad_lin, grad_ldown, grad_hout, grad_lout, grad_hqkv, grad_lqkv)
        sent = [packed_full(grad, shard.shape, nz) for grad, shard in zip(grads, shards)]
        done = scatter_all(
            dp, d_inputs.reshape(group, dp, rows, D), stats, sent, hin_part
        )
    summed = done[1]
    back_rows = done[0].reshape(seqs, rows, D)
    if merged:
        d_layer, g_hin, loss_value, own_one, own_two, *owned = finish_all(
            n,
            dealing,
            back_rows,
            done[8],
            summed,
            integers[1],
            [*done[2:8], g_hdown],
            heavy_in.shape,
            gain_len,
        )
        loss_value, own_one, own_two = (
            loss_value.reshape(()),
            own_one.reshape(gain_len),
            own_two.reshape(gain_len),
        )
    else:
        loss_value = summed[12, 0] / (D * token_count)
        own_one = lax.dynamic_slice_in_dim(summed[:6].reshape(-1), mine * gain_len, gain_len)
        own_two = lax.dynamic_slice_in_dim(summed[6:12].reshape(-1), mine * gain_len, gain_len)
        d_layer = undeal_rows(dealing, back_rows)
        owned = [full.reshape(shard.shape) for full, shard in zip(done[2:8], shards)]
        owned.append(g_hdown)
        g_hin = (
            done[8]
            .astype(F32)
            .reshape(8, hin_rows, 2, nz, hidden_units)
            .transpose(1, 2, 3, 0, 4)
            .reshape(heavy_in.shape)
        )
    g_lin, g_ldown, g_hout, g_lout, g_hqkv, g_lqkv, g_hdown = owned
    return (
        loss_value,
        d_layer[:, None],
        own_one,
        own_two,
        g_lqkv,
        g_lout,
        g_hqkv,
        g_hout,
        g_lin,
        g_ldown,
        g_hin,
        g_hdown,
    )


def integer_tables(dealing, lengths, attn_routes, ffn_routes, ffn_scores, group, pieces, tokens):
    seqs = dealing.shape[0]
    data_index = lax.axis_index("dp")
    piece = lax.axis_index("fsdp")
    chosen = lax.dynamic_slice_in_dim(dealing, data_index * group, group)
    one = chosen[:, None] == jnp.arange(seqs)[None, :]
    seq_lengths = jnp.sum(jnp.where(one, lengths[None, :], 0), axis=1)
    attn_pick = jnp.sum(jnp.where(one[:, :, None], attn_routes[None], 0), axis=1)
    ffn_pick = jnp.sum(jnp.where(one[:, :, None], ffn_routes[None], 0), axis=1)
    score_pick = jnp.sum(jnp.where(one[:, :, None], ffn_scores[None], 0.0), axis=1)
    token_count = jnp.sum(lengths).astype(F32)
    positions = piece * tokens + jnp.arange(tokens)
    valid_mask = positions[None, :] < seq_lengths[:, None]
    a_hot, a_spots = routing(attn_pick, pieces, tokens)
    f_hot, f_spots = routing(ffn_pick, pieces, tokens)
    a_select = lax.dynamic_index_in_dim(a_hot, piece, 1, False).astype(BF)
    f_select = lax.dynamic_index_in_dim(f_hot, piece, 1, False).astype(BF)
    a_spot = lax.dynamic_index_in_dim(a_spots, piece, 1, False)
    f_spot = lax.dynamic_index_in_dim(f_spots, piece, 1, False)
    slot_score = jnp.sum(
        jnp.where(f_spot[:, :, None] == ffn_pick[:, None, :], score_pick[:, None, :], 0.0), axis=-1
    )
    key_pos = piece * tokens - WIN + jnp.arange(tokens + 2 * WIN)
    live_key = (key_pos >= 0)[None, :] & (key_pos[None, :] < seq_lengths[:, None])
    key_line = jnp.where(live_key, 0.0, MASKED)
    key_bias = jnp.stack(
        [key_line[:, b : b + 3 * WIN] for b in range(0, tokens, WIN)], axis=1
    ).reshape(-1, 1, 3 * WIN)
    all_spots = a_spots.reshape(group, pieces * CAP)
    heavy_allowed = ((all_spots >= 0) & (all_spots < seq_lengths[:, None]))[:, None, :] | (
        a_spot[:, :, None] == all_spots[:, None, :]
    )
    heavy_bias = jnp.where(heavy_allowed, 0.0, MASKED)
    weight_mask = valid_mask.reshape(-1, 1).astype(F32)
    masks = (a_select, a_select.swapaxes(1, 2), key_bias, heavy_bias)
    ffn_masks = (
        f_select,
        f_select.swapaxes(1, 2),
        slot_score.reshape(-1, 1),
        weight_mask,
        2.0 * weight_mask / (D * token_count),
    )
    return masks, ffn_masks


def packed_full(grad, shard_shape, nz):
    rows, columns = shard_shape
    if rows % 8 == 0:
        return grad.reshape(nz, 2, 2, 2, rows, columns)
    return grad.reshape(nz, 2, 2, 2, rows * columns // 128, 128)


def solution(mesh):
    split = P(("dp", "fsdp"))
    matrix = P(("dp", "fsdp"), None)
    placed = (
        P(None, "fsdp", "dp", None),
        P("dp", "fsdp", None, None),
        P(),
        P(),
        P(),
        P(),
        P(),
        split,
        split,
    ) + (matrix,) * 8
    return jax.shard_map(
        local,
        mesh=mesh,
        in_specs=placed,
        out_specs=(P(), P(None, "fsdp", "dp", None), split, split) + (matrix,) * 8,
        check_vma=False,
    )
```
